32 devices in a mesh: dp: 8 (over z, y), cls: 4 (over x, core).
Axes of the slice: x: 2, y: 2, z: 4, core: 2. Of those that a mesh axis runs over, the one named last changes fastest.
Arguments:
- patches: bfloat16 [32768, 768], P(('dp', 'cls')), may hold values from -6 to 6
- image_ids: int32 [32, 1024], P(('dp', 'cls')), may hold values from 0 to 7, never falling along the last dimension, each value on 1 to 196 neighbouring positions
- keep: int32 [32, 1024], P(('dp', 'cls')), may hold values 0 or 1
- labels: int32 [256, 2], P('dp'), may hold values from 0 to 21842
- owner: int32 [52], replicated, may hold values from 0 to 55, as said below
- step: int32 [], replicated, may hold values from 2 to 20
- enc_weights: float32 [13, 768, 768], P(None, 'dp')
- stats_left: float32 [13, 768, 768], P(None, 'dp')
- stats_right: float32 [13, 768, 768], P(None, 'dp')
- root_left: float32 [13, 768, 768], P(None, 'dp')
- root_right: float32 [13, 768, 768], P(None, 'dp')
- head_weights: float32 [768, 21848], P('dp', 'cls'), may hold values from -0.21875 to 0.21875
- head_m: float32 [768, 21848], P('dp', 'cls'), may hold values from -0.0001 to 0.0001
- head_v: float32 [768, 21848], P('dp', 'cls'), may hold values from 6e-11 to 2.4e-10
- vectors: float32 [15, 768], P(None, 'dp')
- vec_m: float32 [15, 768], P(None, 'dp'), may hold values from -0.0005 to 0.0005
- vec_v: float32 [15, 768], P(None, 'dp'), may hold values from 1e-09 to 4e-09
Outputs:
- loss: float32 [], replicated
- grad_norm: float32 [], replicated
- new_enc_weights: float32 [13, 768, 768], P(None, 'dp')
- enc_grad: float32 [13, 768, 768], P(None, 'dp')
- new_stats_left: float32 [13, 768, 768], P(None, 'dp')
- new_stats_right: float32 [13, 768, 768], P(None, 'dp')
- new_vectors: float32 [15, 768], P(None, 'dp')
- new_vec_m: float32 [15, 768], P(None, 'dp')
- new_vec_v: float32 [15, 768], P(None, 'dp')
- new_head: float32 [768, 21848], P('dp', 'cls')
- new_head_m: float32 [768, 21848], P('dp', 'cls')
- new_head_v: float32 [768, 21848], P('dp', 'cls')
The draws below stay inside these ranges and needn't reach their ends.
Inputs may be any that keep to these rules, and one draw needn't show every extreme that they name: `owner`: distinct slot numbers; the block with slot s is owned by index s // 7 of dp, so no index owns more than 7 blocks; one block has slot 0 and one has the last slot.
All inputs are finite; a program needn't handle non-finite values. No bound on the sum of `keep` on one device may be relied on, other than what follows from the above.
Results may differ from the reference program's by a relative error of at most 0.0008.
The reference program's roundings to bfloat16 on the way count: a program that leaves them out, or rounds other values in their place, can miss the bound.
Values may be sent and summed in bfloat16 or wider, within the bound.
A program may use at most 320 MiB of HBM per device.

```python
import math
import jax
import jax.numpy as jnp
import numpy as np
from jax import lax

D = 768
HEADS = 12
HEAD = 64
MLP = 3072
PATCH = 768
LABELS_REAL = 21843
CLASSES = 21848
LEN = 1024
IMG_PACK = 8
PATCHES_IMG = 196
NLAB = 2
NBLK = 13
SB = 384
NPRE = 52
NVEC = 15
SLOTS = 7
PACKS = 32
IMAGES = 256
N_DP = 8


def spd_blocks(key, low_end, high_end):
    key_level, key_along, key_noise = jax.random.split(key, 3)
    level = jax.random.uniform(key_level, (NPRE, 1, 1), jnp.float32, low_end, high_end)
    along = jax.random.uniform(key_along, (NPRE, SB), jnp.float32, 0.7, 1.3)
    noise = jax.random.normal(key_noise, (NPRE, SB, SB), jnp.float32)
    symmetric = (noise + jnp.swapaxes(noise, 1, 2)) * (0.2 / (2.0 * SB) ** 0.5)
    identity = jnp.eye(SB, dtype=jnp.float32)
    quads = level * (identity[None] * along[:, :, None] + symmetric)
    return jnp.transpose(quads.reshape(NBLK, 2, 2, SB, SB), (0, 1, 3, 2, 4)).reshape(NBLK, D, D)


def stats_level():
    return D / (NBLK * D * D + D * CLASSES)


def draw_stats_left(key, part):
    return spd_blocks(jax.random.fold_in(key, 11), 0.02 * stats_level(), 0.1 * stats_level())


def draw_stats_right(key, part):
    return spd_blocks(jax.random.fold_in(key, 12), 0.02 * stats_level(), 0.1 * stats_level())


def draw_root_left(key, part):
    return spd_blocks(jax.random.fold_in(key, 13), 8.0, 20.0)


def draw_root_right(key, part):
    return spd_blocks(jax.random.fold_in(key, 14), 8.0, 20.0)


def draw_enc_weights(key, part):
    noise = jax.random.normal(jax.random.fold_in(key, 15), (NBLK, D, D), jnp.float32)
    index = jnp.arange(NBLK)[:, None, None]
    spread = jnp.where(index == 4, (LEN // IMG_PACK) ** 0.5 / D ** 0.5, 1.0 / D ** 0.5)
    spread = jnp.where(index >= 5 + MLP // D, 1.0 / MLP ** 0.5, spread)
    return noise * spread


def draw_vectors(key, part):
    noise = jax.random.normal(jax.random.fold_in(key, 16), (NVEC, D), jnp.float32)
    row_index = jnp.arange(NVEC)[:, None]
    gains = (row_index == 1) | (row_index == 6) | (row_index == 9 + MLP // D)
    return jnp.where(gains, 1.0 + 0.1 * noise, 0.1 * noise)


def draw_owner(key, part):
    total = N_DP * SLOTS
    key_middle = jax.random.fold_in(key, 17)
    key_order = jax.random.fold_in(key, 18)
    middle = 1 + jax.random.permutation(key_middle, total - 2)[:NPRE - 2]
    values = jnp.concatenate([jnp.array([0, total - 1], jnp.int32), middle.astype(jnp.int32)])
    order = jax.random.permutation(key_order, NPRE)
    return values[order].astype(jnp.int32)


def plant(drawn, rng, low, largest):
    place = [jax.random.randint(jax.random.fold_in(rng, axis), (), 0, length) for axis, length in enumerate(drawn.shape)]
    longest = drawn.shape.index(max(drawn.shape))
    neighbour = place[:longest] + [(place[longest] + 1) % drawn.shape[longest]] + place[longest + 1:]
    return drawn.at[tuple(place)].set(low).at[tuple(neighbour)].set(largest)


def block_levels(stream_key, extent, pieces, least, high):
    loudness = 1.0
    for axis_at, shards_of in pieces:
        steps = jax.random.uniform(jax.random.fold_in(jax.random.fold_in(stream_key, 6), axis_at), (shards_of,), jnp.float32, least / len(pieces), high / len(pieces))
        loudness = loudness * jnp.repeat(jnp.exp(steps), extent[axis_at] // shards_of).reshape((-1,) + (1,) * (len(extent) - 1 - axis_at))
    return loudness


def profile(amount, total, bound, lean):
    portions = [(1 << 20) // math.isqrt(standing ** lean) + 1 for standing in range(2, amount + 1)]
    rest, counts = total - bound - (amount - 1), [1] * (amount - 1)
    while rest > 0:
        candidates = [i for i in range(amount - 1) if counts[i] < bound]
        pool, budget = sum([portions[i] for i in candidates]), rest
        for i in candidates:
            extra = min(bound - counts[i], max(1, budget * portions[i] // pool), rest)
            counts[i] = counts[i] + extra
            rest = rest - extra
    return np.array([bound] + counts)


def ragged(stream_key, amount, total, reach, lean):
    if amount == 2:
        one = jax.random.randint(stream_key, (), max(1, total - reach), min(reach, total - 1) + 1)
        return jnp.stack([one, total - one])
    lengths = jnp.asarray(profile(amount, total, reach, lean), jnp.int32)
    pairs = (amount - 1) // 2
    giver, taker = lengths[1:1 + 2 * pairs:2], lengths[2:2 + 2 * pairs:2]
    room = jnp.minimum(giver - 1, reach - taker)
    passed = jax.random.randint(jax.random.fold_in(stream_key, 1), (pairs,), 0, 1 << 20) % (room + 1)
    lengths = lengths.at[1:1 + 2 * pairs:2].set(giver - passed).at[2:2 + 2 * pairs:2].set(taker + passed)
    return lengths[jax.random.permutation(jax.random.fold_in(stream_key, 2), amount)]


def scatter_about(stream_key, shape, scale, limit, cuts=(), held_as=jnp.bfloat16):
    result = jax.random.normal(stream_key, shape, jnp.float32) * scale
    if len(cuts) > 0:
        result = block_levels(stream_key, shape, cuts, -0.22, 0.18) * result
    return jnp.clip(result, min=-limit, max=limit).astype(held_as)


def setup_inputs(seed: int = 0) -> dict:
    keys = jax.random.split(jax.random.key(seed), 18)
    patches = scatter_about(keys[0], (PACKS * LEN, PATCH), 1.0, 6.0, ((0, 32),))
    image_ids = jax.vmap(lambda own: jnp.searchsorted(jnp.cumsum(ragged(own, IMG_PACK, LEN, PATCHES_IMG, 1)), jnp.arange(LEN), side="right"))(jax.random.split(keys[1], PACKS)).reshape((PACKS, LEN)).astype(jnp.int32)
    keep = plant((jax.random.randint(keys[2], (PACKS, LEN), 0, 4) < 3).astype(jnp.int32), jax.random.fold_in(keys[2], 1), 0, 1)
    labels = plant(jax.random.randint(keys[3], (IMAGES, NLAB), 0, LABELS_REAL), jax.random.fold_in(keys[3], 1), 0, LABELS_REAL - 1).astype(jnp.int32)
    owner = draw_owner(jax.random.fold_in(keys[17], 71), 0)
    step = jax.random.randint(keys[5], (), 2, 21).astype(jnp.int32)
    enc_weights = draw_enc_weights(jax.random.fold_in(keys[17], 71), 0)
    stats_left = draw_stats_left(jax.random.fold_in(keys[17], 71), 0)
    stats_right = draw_stats_right(jax.random.fold_in(keys[17], 71), 0)
    root_left = draw_root_left(jax.random.fold_in(keys[17], 71), 0)
    root_right = draw_root_right(jax.random.fold_in(keys[17], 71), 0)
    head_weights = scatter_about(keys[11], (D, CLASSES), D ** -0.5, 0.21875, ((0, 8), (1, 4)), jnp.float32)
    head_m = scatter_about(keys[12], (D, CLASSES), 0.000027, 0.0001, ((0, 8), (1, 4)), jnp.float32)
    head_v = jnp.clip(jnp.exp(math.log(2.399999921021134e-10) - 1.3862944 * jax.random.uniform(keys[13], (D, CLASSES), jnp.float32) ** block_levels(keys[13], (D, CLASSES), ((0, 8), (1, 4)), -0.2, 0.2)), 5.999999802552836e-11, 2.399999921021134e-10)
    vectors = draw_vectors(jax.random.fold_in(keys[17], 71), 0)
    vec_m = scatter_about(keys[15], (NVEC, D), 0.0001, 0.0005, ((1, 8),), jnp.float32)
    vec_v = jnp.clip(jnp.exp(math.log(3.999999886872274e-09) - 1.3862944 * jax.random.uniform(keys[16], (NVEC, D), jnp.float32) ** block_levels(keys[16], (NVEC, D), ((1, 8),), -0.2, 0.2)), 9.999999717180685e-10, 3.999999886872274e-09)
    return {"patches": patches, "image_ids": image_ids, "keep": keep, "labels": labels, "owner": owner, "step": step, "enc_weights": enc_weights, "stats_left": stats_left, "stats_right": stats_right, "root_left": root_left, "root_right": root_right, "head_weights": head_weights, "head_m": head_m, "head_v": head_v, "vectors": vectors, "vec_m": vec_m, "vec_v": vec_v}


FULL_PRECISION = lax.Precision.HIGHEST
NORM_EPS = 1e-06
CLIP_NORM = 1.0
ADAM_RATE = 0.02
SHAMPOO_RATE = 0.01
BETA_FIRST = 0.9
BETA_SECOND = 0.999
ADAM_EPS = 1e-08
WEIGHT_DECAY = 0.1
ROOT_EPS = 1e-06

@jax.custom_vjp
def low(v):
    return lax.optimization_barrier(v.astype(jnp.bfloat16)).astype(jnp.float32)

@jax.custom_vjp
def low_back(v):
    return v

def low_keep(v):
    return (low(v), None)

def low_pass(kept, grad):
    return (grad,)

def back_keep(v):
    return (v, None)

def back_low(kept, grad):
    return (low(grad),)
low.defvjp(low_keep, low_pass)
low_back.defvjp(back_keep, back_low)

def norm_rows(values, gain, shift):
    centred = values - lax.optimization_barrier(jnp.mean(values, -1, keepdims=True))
    spread = lax.optimization_barrier(jnp.mean(centred * centred, -1, keepdims=True))
    return centred * lax.rsqrt(spread + NORM_EPS) * gain + shift

def matmul(left, right):
    return jnp.dot(left, right, precision=FULL_PRECISION)

def encode(blocks, vec_all, patch, pack_ids, pack_keep):
    up_count = MLP // D
    embedded = low_back(matmul(patch, blocks[0]) + vec_all[0])
    normed_one = low(norm_rows(embedded, vec_all[1], vec_all[2]))
    queries = low(low_back(matmul(normed_one, blocks[1]) + vec_all[3])).reshape(LEN, HEADS, HEAD)
    keys_all = low(low_back(matmul(normed_one, blocks[2]))).reshape(LEN, HEADS, HEAD)
    values_all = low(low_back(matmul(normed_one, blocks[3]) + vec_all[4])).reshape(LEN, HEADS, HEAD)
    positions = jnp.arange(LEN)
    allowed = (pack_ids[:, None] == pack_ids[None, :]) & ((pack_keep[None, :] == 1) | (positions[:, None] == positions[None, :]))
    scores = low_back(HEAD ** (-0.5) * jnp.einsum('qhd,khd->hqk', queries, keys_all, precision=FULL_PRECISION))
    scores = jnp.where(allowed[None], scores, -1e+30)
    row_top = lax.optimization_barrier(jnp.max(scores, -1, keepdims=True))
    exp_scores = jnp.exp(scores - row_top)
    probs = exp_scores / lax.optimization_barrier(jnp.sum(exp_scores, -1, keepdims=True))
    attended = jnp.einsum('hqk,khd->qhd', low(probs), values_all, precision=FULL_PRECISION).reshape(LEN, D)
    attended = low(low_back(attended))
    hidden = embedded + low_back(matmul(attended, blocks[4]) + vec_all[5])
    normed_two = low(norm_rows(hidden, vec_all[6], vec_all[7]))
    up_matrix = jnp.transpose(blocks[5:5 + up_count], (1, 0, 2)).reshape(D, MLP)
    pre_act = low_back(matmul(normed_two, up_matrix) + vec_all[8:8 + up_count].reshape(MLP))
    units = low(jax.nn.gelu(pre_act, approximate=False))
    output = hidden + low_back(matmul(units, blocks[5 + up_count:].reshape(MLP, D)) + vec_all[8 + up_count])
    final = norm_rows(output, vec_all[9 + up_count], vec_all[10 + up_count])
    member = ((pack_ids[None, :] == jnp.arange(IMG_PACK)[:, None]) & (pack_keep[None, :] == 1)).astype(jnp.float32)
    counted = jnp.maximum(lax.optimization_barrier(jnp.sum(member, 1)), 1.0)
    return matmul(member, final) / counted[:, None]

def total_loss(enc_weights, vectors, head_weights, patch_all, image_ids, keep, labels):
    blocks = low(enc_weights)
    vec_all = low(vectors)
    head_low = low(head_weights)

    def one_pack(inputs):
        return encode(blocks, vec_all, inputs[0], inputs[1], inputs[2])
    pooled = lax.map(jax.checkpoint(one_pack), (patch_all.reshape(PACKS, LEN, PATCH), image_ids, keep))
    pooled = low(pooled.reshape(IMAGES, D))
    logits = low_back(matmul(pooled, head_low))
    class_ids = jnp.arange(CLASSES)
    target = jnp.any(labels[:, :, None] == class_ids[None, None, :], 1).astype(jnp.float32)
    valid = class_ids[None, :] < LABELS_REAL
    terms = jax.nn.softplus(logits) - target * logits
    return jnp.sum(jnp.where(valid, terms, 0.0)) / IMAGES

def adam_step(weight, grad, first, second, count):
    first = BETA_FIRST * first + (1.0 - BETA_FIRST) * grad
    second = BETA_SECOND * second + (1.0 - BETA_SECOND) * grad * grad
    fix_first = 1.0 - jnp.power(BETA_FIRST, count)
    fix_second = 1.0 - jnp.power(BETA_SECOND, count)
    update = first / fix_first / (jnp.sqrt(second / fix_second) + ADAM_EPS) + WEIGHT_DECAY * weight
    return (weight - ADAM_RATE * update, first, second)

def to_quads(values):
    return jnp.transpose(values.reshape(NBLK, 2, SB, 2, SB), (0, 1, 3, 2, 4)).reshape(NPRE, SB, SB)

def from_quads(values):
    return jnp.transpose(values.reshape(NBLK, 2, 2, SB, SB), (0, 1, 3, 2, 4)).reshape(NBLK, D, D)

def reference(patches, image_ids, keep, labels, owner, step, enc_weights, stats_left, stats_right, root_left, root_right, head_weights, head_m, head_v, vectors, vec_m, vec_v):
    patch_all = patches.astype(jnp.float32)

    def loss_of(blocks, vec_all, head_all):
        return total_loss(blocks, vec_all, head_all, patch_all, image_ids, keep, labels)
    loss, pull_back = jax.vjp(loss_of, enc_weights, vectors, head_weights)
    grad_blocks, grad_vec, grad_head = pull_back(jnp.ones((), jnp.float32))
    squares = jnp.sum(grad_blocks * grad_blocks) + jnp.sum(grad_vec * grad_vec) + jnp.sum(grad_head * grad_head)
    grad_norm = jnp.sqrt(squares)
    factor = CLIP_NORM / jnp.maximum(grad_norm, CLIP_NORM)
    grad_blocks = grad_blocks * factor
    grad_vec = grad_vec * factor
    grad_head = grad_head * factor
    grad_quads = to_quads(grad_blocks)
    new_left = 0.5 * to_quads(stats_left) + 0.5 * jnp.einsum('bij,blj->bil', grad_quads, grad_quads, precision=FULL_PRECISION)
    new_right = 0.5 * to_quads(stats_right) + 0.5 * jnp.einsum('bji,bjl->bil', grad_quads, grad_quads, precision=FULL_PRECISION)
    direction = jnp.einsum('bij,bjl->bil', to_quads(root_left), grad_quads, precision=FULL_PRECISION)
    direction = jnp.einsum('bij,bjl->bil', direction, to_quads(root_right), precision=FULL_PRECISION)
    direction = direction * lax.rsqrt(lax.optimization_barrier(jnp.mean(direction * direction, (1, 2), keepdims=True)) + ROOT_EPS)
    new_blocks = enc_weights - SHAMPOO_RATE * from_quads(direction)
    count = step.astype(jnp.float32)
    new_vec, new_vec_m, new_vec_v = adam_step(vectors, grad_vec, vec_m, vec_v, count)
    new_head, new_head_m, new_head_v = adam_step(head_weights, grad_head, head_m, head_v, count)
    return (loss, grad_norm, new_blocks, grad_blocks, from_quads(new_left), from_quads(new_right), new_vec, new_vec_m, new_vec_v, new_head, new_head_m, new_head_v)
```

```python
import jax
import jax.numpy as jnp
from jax import lax
from jax.sharding import PartitionSpec as P

HEADS = 12
HEAD = 64
LABELS_REAL = 21843
LEN = 1024
QBLOCK = 512
IMG_PACK = 8


FULL_PRECISION = lax.Precision.HIGHEST
NORM_EPS = 1e-06
CLIP_NORM = 1.0
ADAM_RATE = 0.02
SHAMPOO_RATE = 0.01
BETA_FIRST = 0.9
BETA_SECOND = 0.999
ADAM_EPS = 1e-08
WEIGHT_DECAY = 0.1
ROOT_EPS = 1e-06


def norm_rows(values, gain, shift):
    centred = values - jnp.mean(values, -1, keepdims=True)
    spread = jnp.mean(centred * centred, -1, keepdims=True)
    return centred * lax.rsqrt(spread + NORM_EPS) * gain + shift


def gelu_exact(values):
    return jax.nn.gelu(values, approximate=False)


def pool_rows(output, gain, shift, pack_ids, pack_keep):
    final = norm_rows(output, gain, shift)
    member = (
        (pack_ids[None, :] == jnp.arange(IMG_PACK)[:, None]) & (pack_keep[None, :] == 1)
    ).astype(jnp.float32)
    counted = jnp.maximum(jnp.sum(member, 1), 1.0)
    return jnp.dot(member, final, precision=FULL_PRECISION) / counted[:, None]


def masked_scores(qkv_rows, pack_ids, pack_keep, row_start):
    length = qkv_rows.shape[1]
    queries = lax.dynamic_slice_in_dim(qkv_rows[0], row_start, QBLOCK, 0).reshape(
        QBLOCK, HEADS, HEAD
    )
    keys_all = qkv_rows[1].reshape(length, HEADS, HEAD)
    scores = jnp.einsum(
        "qhd,khd->hqk", queries, keys_all, preferred_element_type=jnp.float32
    ) * HEAD ** (-0.5)
    query_ids = lax.dynamic_slice_in_dim(pack_ids, row_start, QBLOCK, 0)
    key_pos = jnp.arange(length)
    query_pos = row_start + jnp.arange(QBLOCK)
    allowed = (query_ids[:, None] == pack_ids[None, :]) & (
        (pack_keep[None, :] == 1) | (query_pos[:, None] == key_pos[None, :])
    )
    return (jnp.where(allowed[None], scores, -1e30), queries, keys_all)


def attention_forward(qkv_rows, pack_ids, pack_keep):
    length = qkv_rows.shape[1]
    values_all = qkv_rows[2].reshape(length, HEADS, HEAD)

    def block_out(row_start):
        scores, queries, keys_all = masked_scores(qkv_rows, pack_ids, pack_keep, row_start)
        row_top = jnp.max(scores, -1, keepdims=True)
        exp_scores = jnp.exp(scores - row_top)
        totals = jnp.sum(exp_scores, -1, keepdims=True)
        probs = (exp_scores / totals).astype(jnp.bfloat16)
        attended = jnp.einsum("hqk,khd->qhd", probs, values_all, preferred_element_type=jnp.float32)
        return (
            attended.reshape(QBLOCK, HEADS * HEAD).astype(jnp.bfloat16),
            (row_top + jnp.log(totals))[..., 0],
        )

    attended, log_totals = lax.map(block_out, jnp.arange(length // QBLOCK) * QBLOCK)
    return (attended.reshape(length, HEADS * HEAD), log_totals)


def attention_backward(qkv_rows, pack_ids, pack_keep, log_totals, grad_attended):
    length = qkv_rows.shape[1]
    values_all = qkv_rows[2].reshape(length, HEADS, HEAD)
    scale = HEAD ** (-0.5)

    def block_back(carried, inputs):
        row_start, block_lse = inputs
        scores, queries, keys_all = masked_scores(qkv_rows, pack_ids, pack_keep, row_start)
        probs = jnp.exp(scores - block_lse[:, :, None])
        grad_rows = lax.dynamic_slice_in_dim(grad_attended, row_start, QBLOCK, 0).reshape(
            QBLOCK, HEADS, HEAD
        )
        grad_probs = jnp.einsum(
            "qhd,khd->hqk", grad_rows, values_all, preferred_element_type=jnp.float32
        )
        grad_scores = (
            probs * (grad_probs - jnp.sum(probs * grad_probs, -1, keepdims=True))
        ).astype(jnp.bfloat16)
        grad_queries = (
            jnp.einsum("hqk,khd->qhd", grad_scores, keys_all, preferred_element_type=jnp.float32)
            * scale
        )
        grad_keys = (
            carried[0]
            + jnp.einsum("hqk,qhd->khd", grad_scores, queries, preferred_element_type=jnp.float32)
            * scale
        )
        grad_values = carried[1] + jnp.einsum(
            "hqk,qhd->khd",
            probs.astype(jnp.bfloat16),
            grad_rows,
            preferred_element_type=jnp.float32,
        )
        return ((grad_keys, grad_values), grad_queries)

    zeros_kv = jnp.zeros((length, HEADS, HEAD), jnp.float32)
    starts = jnp.arange(length // QBLOCK) * QBLOCK
    (grad_keys, grad_values), grad_queries = lax.scan(
        block_back, (zeros_kv, zeros_kv), (starts, log_totals)
    )
    return jnp.stack(
        [
            grad_queries.reshape(length, HEADS * HEAD),
            grad_keys.reshape(length, HEADS * HEAD),
            grad_values.reshape(length, HEADS * HEAD),
        ]
    )


def layer_forward(blocks, vec_all, patch, pack_ids, pack_keep):
    length, feature_dim = patch.shape
    up_count = (blocks.shape[0] - 5) // 2
    embedded = jnp.dot(patch, blocks[0], preferred_element_type=jnp.float32) + vec_all[0]
    normed_one = norm_rows(embedded, vec_all[1], vec_all[2]).astype(jnp.bfloat16)
    qkv_rows = jnp.einsum(
        "td,kde->kte", normed_one, blocks[1:4], preferred_element_type=jnp.float32
    )
    qkv_bias = jnp.stack([vec_all[3], jnp.zeros_like(vec_all[3]), vec_all[4]])
    qkv_rows = (qkv_rows + qkv_bias[:, None, :]).astype(jnp.bfloat16)
    attended, log_totals = attention_forward(qkv_rows, pack_ids, pack_keep)
    hidden = (
        embedded + jnp.dot(attended, blocks[4], preferred_element_type=jnp.float32) + vec_all[5]
    )
    normed_two = norm_rows(hidden, vec_all[6], vec_all[7]).astype(jnp.bfloat16)
    pre_act = jnp.einsum(
        "td,jde->tje", normed_two, blocks[5 : 5 + up_count], preferred_element_type=jnp.float32
    )
    pre_act = pre_act.reshape(length, up_count * feature_dim) + vec_all[8 : 8 + up_count].reshape(
        -1
    )
    units = gelu_exact(pre_act).astype(jnp.bfloat16)
    down_matrix = blocks[5 + up_count :].reshape(up_count * feature_dim, feature_dim)
    output = (
        hidden
        + jnp.dot(units, down_matrix, preferred_element_type=jnp.float32)
        + vec_all[8 + up_count]
    )
    return (
        output,
        (embedded, normed_one, qkv_rows, attended, log_totals, hidden, normed_two, pre_act, units),
    )


def layer_backward(
    blocks, vec_all, patch, saved, pack_ids, pack_keep, grad_output, grad_gain, grad_shift
):
    embedded, normed_one, qkv_rows, attended, log_totals, hidden, normed_two, pre_act, units = saved
    length, feature_dim = patch.shape
    up_count = (blocks.shape[0] - 5) // 2
    down_matrix = blocks[5 + up_count :].reshape(up_count * feature_dim, feature_dim)
    grad_branch = grad_output.astype(jnp.bfloat16)
    grad_down = jnp.einsum("tf,td->fd", units, grad_branch, preferred_element_type=jnp.float32)
    grad_units = jnp.einsum(
        "td,fd->tf", grad_branch, down_matrix, preferred_element_type=jnp.float32
    )
    gelu_back = jax.vjp(gelu_exact, pre_act)[1]
    grad_pre = gelu_back(grad_units)[0].astype(jnp.bfloat16)
    grad_pre_blocks = grad_pre.reshape(length, up_count, feature_dim)
    grad_up = jnp.einsum(
        "td,tje->jde", normed_two, grad_pre_blocks, preferred_element_type=jnp.float32
    )
    grad_normed_two = jnp.einsum(
        "tje,jde->td", grad_pre_blocks, blocks[5 : 5 + up_count], preferred_element_type=jnp.float32
    )
    norm_two_back = jax.vjp(norm_rows, hidden, vec_all[6], vec_all[7])[1]
    grad_hidden_norm, grad_gain_two, grad_shift_two = norm_two_back(grad_normed_two)
    grad_hidden = grad_output + grad_hidden_norm
    grad_attn_out = grad_hidden.astype(jnp.bfloat16)
    grad_out_proj = jnp.einsum(
        "te,td->ed", attended, grad_attn_out, preferred_element_type=jnp.float32
    )
    grad_attended = jnp.einsum(
        "td,ed->te", grad_attn_out, blocks[4], preferred_element_type=jnp.float32
    ).astype(jnp.bfloat16)
    grad_qkv = attention_backward(qkv_rows, pack_ids, pack_keep, log_totals, grad_attended).astype(
        jnp.bfloat16
    )
    grad_qkv_proj = jnp.einsum(
        "td,kte->kde", normed_one, grad_qkv, preferred_element_type=jnp.float32
    )
    grad_normed_one = jnp.einsum(
        "kte,kde->td", grad_qkv, blocks[1:4], preferred_element_type=jnp.float32
    )
    norm_one_back = jax.vjp(norm_rows, embedded, vec_all[1], vec_all[2])[1]
    grad_embed_norm, grad_gain_one, grad_shift_one = norm_one_back(grad_normed_one)
    grad_embedded = (grad_hidden + grad_embed_norm).astype(jnp.bfloat16)
    grad_patch = jnp.einsum("tp,td->pd", patch, grad_embedded, preferred_element_type=jnp.float32)
    grad_first = jnp.concatenate([grad_patch[None], grad_qkv_proj, grad_out_proj[None]], 0)
    grad_mlp = jnp.concatenate(
        [grad_up, grad_down.reshape(up_count, feature_dim, feature_dim)], 0
    )
    bias_sums = jnp.stack(
        [
            jnp.sum(grad_embedded.astype(jnp.float32), 0),
            grad_gain_one,
            grad_shift_one,
            jnp.sum(grad_qkv[0].astype(jnp.float32), 0),
            jnp.sum(grad_qkv[2].astype(jnp.float32), 0),
            jnp.sum(grad_attn_out.astype(jnp.float32), 0),
            grad_gain_two,
            grad_shift_two,
        ]
    )
    up_sums = jnp.sum(grad_pre.astype(jnp.float32), 0).reshape(up_count, feature_dim)
    tail_sums = jnp.stack([jnp.sum(grad_branch.astype(jnp.float32), 0), grad_gain, grad_shift])
    return (grad_first, grad_mlp, jnp.concatenate([bias_sums, up_sums, tail_sums], 0))


def adam_step(weight, grad, first, second, count):
    first = BETA_FIRST * first + (1.0 - BETA_FIRST) * grad
    second = BETA_SECOND * second + (1.0 - BETA_SECOND) * grad * grad
    fix_first = 1.0 - jnp.power(BETA_FIRST, count)
    fix_second = 1.0 - jnp.power(BETA_SECOND, count)
    update = first / fix_first / (jnp.sqrt(second / fix_second) + ADAM_EPS) + WEIGHT_DECAY * weight
    return (weight - ADAM_RATE * update, first, second)


def split_halves(values, half_size):
    block_count, row_count, feature_dim = values.shape
    return values.reshape(block_count, row_count, 2, half_size)


def on_device(
    patches,
    image_ids,
    keep,
    labels,
    owner,
    step,
    enc_weights,
    stats_left,
    stats_right,
    root_left,
    root_right,
    head_weights,
    head_m,
    head_v,
    vectors,
    vec_m,
    vec_v,
):
    dp_count = lax.axis_size("dp")
    cls_count = lax.axis_size("cls")
    dp_index = lax.axis_index("dp")
    cls_index = lax.axis_index("cls")
    block_count, row_count, feature_dim = enc_weights.shape
    up_count = (block_count - 5) // 2
    half_size = feature_dim // 2
    part_rows = row_count // cls_count
    half_dp = dp_count // 2
    half_group = half_dp * cls_count
    half_groups = [
        list(range(half_group)),
        list(range(half_group, 2 * half_group)),
    ]

    def my_part(values):
        return lax.dynamic_slice_in_dim(values, cls_index * part_rows, part_rows, 1)

    blocks = lax.all_gather(
        my_part(enc_weights.astype(jnp.bfloat16)), ("dp", "cls"), axis=1, tiled=True
    )
    vec_low = lax.all_gather(vectors.astype(jnp.bfloat16), "dp", axis=1, tiled=True)
    vec_all = vec_low.astype(jnp.float32)
    head_low = lax.all_gather(head_weights.astype(jnp.bfloat16), "dp", axis=0, tiled=True)
    right_half = lax.all_gather(
        my_part(root_right), ("dp", "cls"), axis=1, tiled=True, axis_index_groups=half_groups
    )
    final_gain = vec_all[9 + up_count]
    final_shift = vec_all[10 + up_count]
    pack_ids, pack_keep = image_ids[0], keep[0]

    output, saved = layer_forward(blocks, vec_all, patches, pack_ids, pack_keep)
    pooled = pool_rows(output, final_gain, final_shift, pack_ids, pack_keep)
    group = lax.all_gather(pooled.astype(jnp.bfloat16), "cls", axis=0, tiled=True)
    pooled_all = lax.all_gather(group, "dp", axis=0, tiled=True)
    logits = jnp.dot(group, head_low, preferred_element_type=jnp.float32)
    class_dev = head_low.shape[1]
    class_ids = cls_index * class_dev + jnp.arange(class_dev)
    valid = class_ids[None, :] < LABELS_REAL
    target = jnp.any(labels[:, :, None] == class_ids[None, None, :], 1).astype(jnp.float32)
    image_total = labels.shape[0] * dp_count
    loss_part = (
        jnp.sum(jnp.where(valid, jax.nn.softplus(logits) - target * logits, 0.0)) / image_total
    )
    grad_logits = (jnp.where(valid, jax.nn.sigmoid(logits) - target, 0.0) / image_total).astype(
        jnp.bfloat16
    )
    group_grad = jnp.einsum("gc,dc->gd", grad_logits, head_low, preferred_element_type=jnp.float32)
    grad_pooled = lax.psum_scatter(group_grad, "cls", scatter_dimension=0, tiled=True)
    grad_logits_all = lax.all_gather(grad_logits, "dp", axis=0, tiled=True)
    pooled_mine = lax.dynamic_slice_in_dim(pooled_all, dp_index * row_count, row_count, 1)
    head_grad = jnp.einsum(
        "gr,gc->rc", pooled_mine, grad_logits_all, preferred_element_type=jnp.float32
    )

    def pool_local(rows_in, gain, shift):
        return pool_rows(rows_in, gain, shift, pack_ids, pack_keep)

    pool_back = jax.vjp(pool_local, output, final_gain, final_shift)[1]
    grad_output, grad_gain, grad_shift = pool_back(grad_pooled)
    grad_first, grad_mlp, grad_vectors = layer_backward(
        blocks,
        vec_all,
        patches,
        saved,
        pack_ids,
        pack_keep,
        grad_output,
        grad_gain,
        grad_shift,
    )

    def reduced_half(values):
        part = lax.psum_scatter(values, ("dp", "cls"), scatter_dimension=1, tiled=True)
        return lax.all_gather(
            part, ("dp", "cls"), axis=1, tiled=True, axis_index_groups=half_groups
        )

    grad_half = jnp.concatenate([reduced_half(grad_first), reduced_half(grad_mlp)], 0)
    own_start = (dp_index % half_dp) * row_count
    block_rows = lax.dynamic_slice_in_dim(grad_half, own_start, row_count, 1)
    vector_sum = lax.psum(grad_vectors, ("dp", "cls"))
    vector_rows = lax.dynamic_slice_in_dim(vector_sum, dp_index * row_count, row_count, 1)

    precise = lax.Precision.HIGHEST
    grad_quads = split_halves(grad_half, half_size)
    rows_quads = split_halves(block_rows, half_size)
    cols_quads = lax.dynamic_slice_in_dim(grad_quads, own_start, row_count, 3)
    left_add = jnp.einsum("brjk,bljk->brjl", rows_quads, grad_quads, precision=precise)
    right_add = jnp.einsum("bkja,bkjm->bajm", cols_quads, grad_quads, precision=precise)
    direction = jnp.einsum(
        "brjk,bkjm->brjm", split_halves(root_left, half_size), grad_quads, precision=precise
    )
    direction = jnp.einsum(
        "brjk,bkjm->brjm", direction, split_halves(right_half, half_size), precision=precise
    )
    block_squares = jnp.sum(direction * direction, (1, 3))
    in_top = (dp_index < half_dp).astype(jnp.float32)
    once = (cls_index == 0).astype(jnp.float32)
    layer_squares = once * jnp.sum(block_rows * block_rows)
    vector_squares = once * jnp.sum(vector_rows * vector_rows)
    packed = jnp.concatenate(
        [
            (once * in_top * block_squares).reshape(-1),
            (once * (1.0 - in_top) * block_squares).reshape(-1),
            jnp.stack([layer_squares + vector_squares + jnp.sum(head_grad * head_grad), loss_part]),
        ]
    )
    packed = lax.psum(packed, ("dp", "cls"))
    loss = packed[4 * block_count + 1]
    grad_norm = jnp.sqrt(packed[4 * block_count])
    factor = CLIP_NORM / jnp.maximum(grad_norm, CLIP_NORM)
    sums = packed[: 4 * block_count].reshape(2, block_count, 2)
    mean_squares = jnp.where(dp_index < half_dp, sums[0], sums[1]) / (half_size * half_size)
    mean_squares = mean_squares * factor * factor
    scale = factor * lax.rsqrt(mean_squares + ROOT_EPS)
    flat = (block_count, row_count, feature_dim)
    new_blocks = enc_weights - SHAMPOO_RATE * (direction * scale[:, None, :, None]).reshape(flat)
    square_factor = 0.5 * factor * factor
    new_left = 0.5 * stats_left + square_factor * left_add.reshape(flat)
    new_right = 0.5 * stats_right + square_factor * right_add.reshape(flat)
    count = step.astype(jnp.float32)
    new_vec, new_vec_m, new_vec_v = adam_step(vectors, vector_rows * factor, vec_m, vec_v, count)
    new_head, new_head_m, new_head_v = adam_step(
        head_weights, head_grad * factor, head_m, head_v, count
    )
    return (
        loss,
        grad_norm,
        new_blocks,
        block_rows * factor,
        new_left,
        new_right,
        new_vec,
        new_vec_m,
        new_vec_v,
        new_head,
        new_head_m,
        new_head_v,
    )


def solution(mesh):
    return jax.shard_map(
        on_device,
        mesh=mesh,
        in_specs=(
            P(("dp", "cls"), None),
            P(("dp", "cls"), None),
            P(("dp", "cls"), None),
            P("dp", None),
            P(),
            P(),
            P(None, "dp", None),
            P(None, "dp", None),
            P(None, "dp", None),
            P(None, "dp", None),
            P(None, "dp", None),
            P("dp", "cls"),
            P("dp", "cls"),
            P("dp", "cls"),
            P(None, "dp"),
            P(None, "dp"),
            P(None, "dp"),
        ),
        out_specs=(
            P(),
            P(),
            P(None, "dp", None),
            P(None, "dp", None),
            P(None, "dp", None),
            P(None, "dp", None),
            P(None, "dp"),
            P(None, "dp"),
            P(None, "dp"),
            P("dp", "cls"),
            P("dp", "cls"),
            P("dp", "cls"),
        ),
        check_vma=False,
    )
```

```python
import jax
import jax.numpy as jnp
from jax import lax
from jax.experimental import pallas as pl
from jax.experimental.pallas import tpu as pltpu
from jax.sharding import PartitionSpec as P

HEADS = 12
HEAD = 64
LABELS_REAL = 21843
IMAGE_MAX = 196
QTILE = 256
PAIR = 2 * HEAD
ROWS = 256
HIDDEN_TILE = 384
IMG_PACK = 8


FULL_PRECISION = lax.Precision.HIGHEST
NORM_EPS = 1e-06
CLIP_NORM = 1.0
ADAM_RATE = 0.02
SHAMPOO_RATE = 0.01
BETA_FIRST = 0.9
BETA_SECOND = 0.999
ADAM_EPS = 1e-08
WEIGHT_DECAY = 0.1
ROOT_EPS = 1e-06


def norm_rows(values, gain, shift):
    centred = values - jnp.mean(values, -1, keepdims=True)
    spread = jnp.mean(centred * centred, -1, keepdims=True)
    return centred * lax.rsqrt(spread + NORM_EPS) * gain + shift


def pool_rows(output, gain, shift, pack_ids, pack_keep):
    final = norm_rows(output, gain, shift)
    member = (
        (pack_ids[None, :] == jnp.arange(IMG_PACK)[:, None]) & (pack_keep[None, :] == 1)
    ).astype(jnp.float32)
    counted = jnp.maximum(jnp.sum(member, 1), 1.0)
    return jnp.dot(member, final, precision=FULL_PRECISION) / counted[:, None]


def key_window(tile, length):
    reach = -(-(IMAGE_MAX - 1) // 128) * 128
    low = max(0, tile * QTILE - reach)
    high = min(length, (tile + 1) * QTILE + reach)
    return low, high


def attention_forward_kernel(qids_ref, kcodes_ref, q_ref, k_ref, v_ref, out_ref, bias_ref):
    length = q_ref.shape[0]
    lane = lax.broadcasted_iota(jnp.int32, (QTILE, PAIR), 1)

    @pl.when(pl.program_id(0) == 0)
    def _():
        for tile in range(length // QTILE):
            low, high = key_window(tile, length)
            shape = (QTILE, high - low)
            rows = lax.broadcasted_iota(jnp.int32, shape, 0) + tile * QTILE
            cols = lax.broadcasted_iota(jnp.int32, shape, 1) + low
            same = qids_ref[tile * QTILE : (tile + 1) * QTILE, :] == kcodes_ref[:, low:high]
            bias_ref[tile, :, : high - low] = jnp.where(same | (rows == cols), 0.0, -1e30)

    for tile in range(length // QTILE):
        low, high = key_window(tile, length)
        rows = pl.ds(tile * QTILE, QTILE)
        queries = q_ref[rows, :] * jnp.bfloat16(HEAD ** (-0.5))
        keys = k_ref[low:high, :]
        values = v_ref[low:high, :]
        halves = []
        for head in range(2):
            mine = (lane >= head * HEAD) & (lane < (head + 1) * HEAD)
            picked = jnp.where(mine, queries, jnp.zeros_like(queries))
            scores = lax.dot_general(
                picked, keys, (((1,), (1,)), ((), ())), preferred_element_type=jnp.float32
            )
            scores = scores + bias_ref[tile, :, : high - low]
            top = jnp.max(scores, -1, keepdims=True)
            weights = jnp.exp(scores - top)
            probs = weights * (1.0 / jnp.sum(weights, -1, keepdims=True))
            halves.append(
                jnp.dot(probs.astype(jnp.bfloat16), values, preferred_element_type=jnp.float32)
            )
        out_ref[rows, :] = jnp.where(lane < HEAD, halves[0], halves[1]).astype(jnp.bfloat16)


def attention_backward_kernel(
    qids_ref, kcodes_ref, q_ref, k_ref, v_ref, do_ref, out_ref, bias_ref, dk_ref, dv_ref
):
    length = q_ref.shape[0]
    lane = lax.broadcasted_iota(jnp.int32, (QTILE, PAIR), 1)
    scale = jnp.bfloat16(HEAD ** (-0.5))

    @pl.when(pl.program_id(0) == 0)
    def _():
        for tile in range(length // QTILE):
            low, high = key_window(tile, length)
            shape = (high - low, QTILE)
            rows = lax.broadcasted_iota(jnp.int32, shape, 0) + low
            cols = lax.broadcasted_iota(jnp.int32, shape, 1) + tile * QTILE
            same = kcodes_ref[low:high, :] == qids_ref[:, tile * QTILE : (tile + 1) * QTILE]
            bias_ref[tile, : high - low, :] = jnp.where(same | (rows == cols), 0.0, -1e30)

    dk_ref[...] = jnp.zeros_like(dk_ref)
    dv_ref[...] = jnp.zeros_like(dv_ref)
    for tile in range(length // QTILE):
        low, high = key_window(tile, length)
        rows = pl.ds(tile * QTILE, QTILE)
        window = pl.ds(low, high - low)
        queries = q_ref[rows, :] * scale
        keys = k_ref[window, :]
        values = v_ref[window, :]
        grads = do_ref[rows, :]
        halves = []
        for head in range(2):
            mine = (lane >= head * HEAD) & (lane < (head + 1) * HEAD)
            picked = jnp.where(mine, queries, jnp.zeros_like(queries))
            picked_grads = jnp.where(mine, grads, jnp.zeros_like(grads))
            scores = lax.dot_general(
                keys, picked, (((1,), (1,)), ((), ())), preferred_element_type=jnp.float32
            )
            scores = scores + bias_ref[tile, : high - low, :]
            top = jnp.max(scores, 0, keepdims=True)
            weights = jnp.exp(scores - top)
            probs = weights * (1.0 / jnp.sum(weights, 0, keepdims=True))
            grad_probs = lax.dot_general(
                values, picked_grads, (((1,), (1,)), ((), ())), preferred_element_type=jnp.float32
            )
            inner = jnp.sum(probs * grad_probs, 0, keepdims=True)
            grad_scores = (probs * (grad_probs - inner)).astype(jnp.bfloat16)
            dv_ref[window, :] += jnp.dot(
                probs.astype(jnp.bfloat16), picked_grads, preferred_element_type=jnp.float32
            )
            dk_ref[window, :] += jnp.dot(
                grad_scores, picked, preferred_element_type=jnp.float32
            )
            halves.append(
                lax.dot_general(
                    grad_scores,
                    keys,
                    (((0,), (0,)), ((), ())),
                    preferred_element_type=jnp.float32,
                )
            )
        grad_queries = jnp.where(lane < HEAD, halves[0], halves[1]) * HEAD ** (-0.5)
        out_ref[0, rows, :] = grad_queries.astype(jnp.bfloat16)
    out_ref[1] = dk_ref[...].astype(jnp.bfloat16)
    out_ref[2] = dv_ref[...].astype(jnp.bfloat16)


def pair_spec(length, part=None):
    if part is None:
        return pl.BlockSpec((length, PAIR), lambda pair: (0, pair))
    return pl.BlockSpec((None, length, PAIR), lambda pair: (part, 0, pair))


def whole_spec(shape):
    return pl.BlockSpec(shape, lambda pair: (0,) * len(shape))


def attention_forward(qkv_rows, pack_ids, key_codes):
    _, length, width = qkv_rows.shape
    tiles = length // QTILE
    window = max(high - low for low, high in (key_window(t, length) for t in range(tiles)))
    return pl.pallas_call(
        attention_forward_kernel,
        grid=(width // PAIR,),
        out_shape=jax.ShapeDtypeStruct((length, width), jnp.bfloat16),
        in_specs=[whole_spec((length, 1)), whole_spec((1, length))]
        + [pair_spec(length, part) for part in range(3)],
        out_specs=pair_spec(length),
        scratch_shapes=[pltpu.VMEM((tiles, QTILE, window), jnp.float32)],
        compiler_params=pltpu.CompilerParams(vmem_limit_bytes=40 << 20),
        name="attention_forward",
    )(pack_ids[:, None], key_codes[None, :], qkv_rows, qkv_rows, qkv_rows)


def attention_backward(qkv_rows, pack_ids, key_codes, grad_attended):
    _, length, width = qkv_rows.shape
    tiles = length // QTILE
    window = max(high - low for low, high in (key_window(t, length) for t in range(tiles)))
    return pl.pallas_call(
        attention_backward_kernel,
        grid=(width // PAIR,),
        out_shape=jax.ShapeDtypeStruct((3, length, width), jnp.bfloat16),
        in_specs=[whole_spec((1, length)), whole_spec((length, 1))]
        + [pair_spec(length, part) for part in range(3)]
        + [pair_spec(length)],
        out_specs=pl.BlockSpec((3, length, PAIR), lambda pair: (0, 0, pair)),
        scratch_shapes=[
            pltpu.VMEM((tiles, window, QTILE), jnp.float32),
            pltpu.VMEM((length, PAIR), jnp.float32),
            pltpu.VMEM((length, PAIR), jnp.float32),
        ],
        compiler_params=pltpu.CompilerParams(vmem_limit_bytes=40 << 20),
        name="attention_backward",
    )(pack_ids[None, :], key_codes[:, None], qkv_rows, qkv_rows, qkv_rows, grad_attended)


def mlp_forward_kernel(x_ref, up_ref, bias_ref, down_ref, units_ref, slope_ref, out_ref):
    first = pl.program_id(0) == 0

    @pl.when(first)
    def _():
        out_ref[...] = jnp.zeros_like(out_ref)

    for start in range(0, x_ref.shape[0], ROWS):
        rows = pl.ds(start, ROWS)
        pre = jnp.dot(x_ref[rows, :], up_ref[...], preferred_element_type=jnp.float32)
        pre = pre + bias_ref[...]
        half = 0.5 + 0.5 * lax.erf(pre * 0.7071067811865476)
        bell = jnp.exp(-0.5 * pre * pre) * 0.3989422804014327
        units = (pre * half).astype(jnp.bfloat16)
        units_ref[rows, :] = units
        slope_ref[rows, :] = half + pre * bell
        out_ref[rows, :] += jnp.dot(units, down_ref[...], preferred_element_type=jnp.float32)


def mlp_backward_kernel(
    x_ref, dm_ref, up_ref, down_ref, units_ref, slope_ref,
    grad_up_ref, grad_down_ref, bias_ref, dx_ref, dpre_ref
):
    @pl.when(pl.program_id(0) == 0)
    def _():
        dx_ref[...] = jnp.zeros_like(dx_ref)

    total = jnp.zeros((1, HIDDEN_TILE), jnp.float32)
    for start in range(0, x_ref.shape[0], ROWS):
        rows = pl.ds(start, ROWS)
        units_back = lax.dot_general(
            dm_ref[rows, :], down_ref[...], (((1,), (1,)), ((), ())),
            preferred_element_type=jnp.float32,
        )
        grad_pre = (units_back * slope_ref[rows, :]).astype(jnp.bfloat16)
        dpre_ref[rows, :] = grad_pre
        total = total + jnp.sum(grad_pre.astype(jnp.float32), 0, keepdims=True)
        dx_ref[rows, :] += lax.dot_general(
            grad_pre, up_ref[...], (((1,), (1,)), ((), ())), preferred_element_type=jnp.float32
        )
    bias_ref[...] = total
    over_rows = (((0,), (0,)), ((), ()))
    grad_down_ref[...] = lax.dot_general(
        units_ref[...], dm_ref[...], over_rows, preferred_element_type=jnp.float32
    )
    grad_up_ref[...] = lax.dot_general(
        x_ref[...], dpre_ref[...], over_rows, preferred_element_type=jnp.float32
    )


def mlp_specs(length, width, up_count):
    split = width // HIDDEN_TILE
    resident = pl.BlockSpec((length, width), lambda t: (0, 0))
    up = pl.BlockSpec((None, width, HIDDEN_TILE), lambda t: (5 + t // split, 0, t % split))
    down = pl.BlockSpec(
        (None, HIDDEN_TILE, width), lambda t: (5 + up_count + t // split, t % split, 0)
    )
    hidden = pl.BlockSpec((length, HIDDEN_TILE), lambda t: (0, t))
    bias = pl.BlockSpec((1, HIDDEN_TILE), lambda t: (0, t))
    return split, resident, up, down, hidden, bias


def mlp_forward(rows, blocks, up_bias):
    length, width = rows.shape
    up_count = (blocks.shape[0] - 5) // 2
    split, resident, up, down, hidden, bias = mlp_specs(length, width, up_count)
    hidden_size = up_count * width
    return pl.pallas_call(
        mlp_forward_kernel,
        grid=(up_count * split,),
        out_shape=(
            jax.ShapeDtypeStruct((length, hidden_size), jnp.bfloat16),
            jax.ShapeDtypeStruct((length, hidden_size), jnp.float32),
            jax.ShapeDtypeStruct((length, width), jnp.float32),
        ),
        in_specs=[resident, up, bias, down],
        out_specs=(hidden, hidden, resident),
        compiler_params=pltpu.CompilerParams(vmem_limit_bytes=48 << 20),
        name="mlp_forward",
    )(rows, blocks, up_bias.reshape(1, hidden_size), blocks)


def mlp_backward(rows, grad_branch, blocks, units, slopes):
    length, width = rows.shape
    up_count = (blocks.shape[0] - 5) // 2
    split, resident, up, down, hidden, bias = mlp_specs(length, width, up_count)
    hidden_size = up_count * width
    return pl.pallas_call(
        mlp_backward_kernel,
        grid=(up_count * split,),
        out_shape=(
            jax.ShapeDtypeStruct((up_count, width, width), jnp.float32),
            jax.ShapeDtypeStruct((up_count, width, width), jnp.float32),
            jax.ShapeDtypeStruct((1, hidden_size), jnp.float32),
            jax.ShapeDtypeStruct((length, width), jnp.float32),
        ),
        in_specs=[resident, resident, up, down, hidden, hidden],
        out_specs=(
            pl.BlockSpec((None, width, HIDDEN_TILE), lambda t: (t // split, 0, t % split)),
            pl.BlockSpec((None, HIDDEN_TILE, width), lambda t: (t // split, t % split, 0)),
            bias,
            resident,
        ),
        scratch_shapes=[pltpu.VMEM((length, HIDDEN_TILE), jnp.bfloat16)],
        compiler_params=pltpu.CompilerParams(vmem_limit_bytes=48 << 20),
        name="mlp_backward",
    )(rows, grad_branch, blocks, blocks, units, slopes)


def layer_forward(blocks, vec_all, patch, pack_ids, key_codes):
    up_count = (blocks.shape[0] - 5) // 2
    embedded = jnp.dot(patch, blocks[0], preferred_element_type=jnp.float32) + vec_all[0]
    normed_one = norm_rows(embedded, vec_all[1], vec_all[2]).astype(jnp.bfloat16)
    qkv_rows = jnp.einsum(
        "td,kde->kte", normed_one, blocks[1:4], preferred_element_type=jnp.float32
    )
    qkv_bias = jnp.stack([vec_all[3], jnp.zeros_like(vec_all[3]), vec_all[4]])
    qkv_rows = (qkv_rows + qkv_bias[:, None, :]).astype(jnp.bfloat16)
    attended = attention_forward(qkv_rows, pack_ids, key_codes)
    hidden = (
        embedded + jnp.dot(attended, blocks[4], preferred_element_type=jnp.float32) + vec_all[5]
    )
    normed_two = norm_rows(hidden, vec_all[6], vec_all[7]).astype(jnp.bfloat16)
    units, slopes, branch = mlp_forward(normed_two, blocks, vec_all[8 : 8 + up_count])
    output = hidden + branch + vec_all[8 + up_count]
    return (
        output,
        (embedded, normed_one, qkv_rows, attended, hidden, normed_two, slopes, units),
    )


def layer_backward(
    blocks, vec_all, patch, saved, pack_ids, key_codes, grad_output, grad_gain, grad_shift
):
    embedded, normed_one, qkv_rows, attended, hidden, normed_two, slopes, units = saved
    feature_dim = patch.shape[1]
    up_count = (blocks.shape[0] - 5) // 2
    grad_branch = grad_output.astype(jnp.bfloat16)
    grad_up, grad_down, up_sums, grad_normed_two = mlp_backward(
        normed_two, grad_branch, blocks, units, slopes
    )
    norm_two_back = jax.vjp(norm_rows, hidden, vec_all[6], vec_all[7])[1]
    grad_hidden_norm, grad_gain_two, grad_shift_two = norm_two_back(grad_normed_two)
    grad_hidden = grad_output + grad_hidden_norm
    grad_attn_out = grad_hidden.astype(jnp.bfloat16)
    grad_out_proj = jnp.einsum(
        "te,td->ed", attended, grad_attn_out, preferred_element_type=jnp.float32
    )
    grad_attended = jnp.einsum(
        "td,ed->te", grad_attn_out, blocks[4], preferred_element_type=jnp.float32
    ).astype(jnp.bfloat16)
    grad_qkv = attention_backward(qkv_rows, pack_ids, key_codes, grad_attended)
    grad_qkv_proj = jnp.einsum(
        "td,kte->kde", normed_one, grad_qkv, preferred_element_type=jnp.float32
    )
    grad_normed_one = jnp.einsum(
        "kte,kde->td", grad_qkv, blocks[1:4], preferred_element_type=jnp.float32
    )
    norm_one_back = jax.vjp(norm_rows, embedded, vec_all[1], vec_all[2])[1]
    grad_embed_norm, grad_gain_one, grad_shift_one = norm_one_back(grad_normed_one)
    grad_embedded = (grad_hidden + grad_embed_norm).astype(jnp.bfloat16)
    grad_patch = jnp.einsum("tp,td->pd", patch, grad_embedded, preferred_element_type=jnp.float32)
    grad_first = jnp.concatenate([grad_patch[None], grad_qkv_proj, grad_out_proj[None]], 0)
    grad_mlp = jnp.concatenate([grad_up, grad_down], 0)
    bias_sums = jnp.stack(
        [
            jnp.sum(grad_embedded.astype(jnp.float32), 0),
            grad_gain_one,
            grad_shift_one,
            jnp.sum(grad_qkv[0].astype(jnp.float32), 0),
            jnp.sum(grad_qkv[2].astype(jnp.float32), 0),
            jnp.sum(grad_attn_out.astype(jnp.float32), 0),
            grad_gain_two,
            grad_shift_two,
        ]
    )
    up_sums = up_sums.reshape(up_count, feature_dim)
    tail_sums = jnp.stack([jnp.sum(grad_branch.astype(jnp.float32), 0), grad_gain, grad_shift])
    return (grad_first, grad_mlp, jnp.concatenate([bias_sums, up_sums, tail_sums], 0))


def adam_step(weight, grad, first, second, count):
    first = BETA_FIRST * first + (1.0 - BETA_FIRST) * grad
    second = BETA_SECOND * second + (1.0 - BETA_SECOND) * grad * grad
    fix_first = 1.0 - jnp.power(BETA_FIRST, count)
    fix_second = 1.0 - jnp.power(BETA_SECOND, count)
    update = first / fix_first / (jnp.sqrt(second / fix_second) + ADAM_EPS) + WEIGHT_DECAY * weight
    return (weight - ADAM_RATE * update, first, second)


def split_halves(values, half_size):
    block_count, row_count, feature_dim = values.shape
    return values.reshape(block_count, row_count, 2, half_size)


def on_device(
    patches,
    image_ids,
    keep,
    labels,
    owner,
    step,
    enc_weights,
    stats_left,
    stats_right,
    root_left,
    root_right,
    head_weights,
    head_m,
    head_v,
    vectors,
    vec_m,
    vec_v,
):
    dp_count = lax.axis_size("dp")
    cls_count = lax.axis_size("cls")
    dp_index = lax.axis_index("dp")
    cls_index = lax.axis_index("cls")
    block_count, row_count, feature_dim = enc_weights.shape
    up_count = (block_count - 5) // 2
    half_size = feature_dim // 2
    part_rows = row_count // cls_count
    half_dp = dp_count // 2
    half_group = half_dp * cls_count
    half_groups = [
        list(range(half_group)),
        list(range(half_group, 2 * half_group)),
    ]

    def my_part(values):
        return lax.dynamic_slice_in_dim(values, cls_index * part_rows, part_rows, 1)

    blocks = lax.all_gather(
        my_part(enc_weights.astype(jnp.bfloat16)), ("dp", "cls"), axis=1, tiled=True
    )
    vec_low = lax.all_gather(vectors.astype(jnp.bfloat16), "dp", axis=1, tiled=True)
    vec_all = vec_low.astype(jnp.float32)
    head_low = lax.all_gather(head_weights.astype(jnp.bfloat16), "dp", axis=0, tiled=True)
    right_half = lax.all_gather(
        my_part(root_right), ("dp", "cls"), axis=1, tiled=True, axis_index_groups=half_groups
    )
    final_gain = vec_all[9 + up_count]
    final_shift = vec_all[10 + up_count]
    pack_ids, pack_keep = image_ids[0], keep[0]
    key_codes = jnp.where(pack_keep == 1, pack_ids, -1)

    output, saved = layer_forward(blocks, vec_all, patches, pack_ids, key_codes)
    pooled = pool_rows(output, final_gain, final_shift, pack_ids, pack_keep)
    group = lax.all_gather(pooled.astype(jnp.bfloat16), "cls", axis=0, tiled=True)
    pooled_all = lax.all_gather(group, "dp", axis=0, tiled=True)
    logits = jnp.dot(group, head_low, preferred_element_type=jnp.float32)
    class_dev = head_low.shape[1]
    class_ids = cls_index * class_dev + jnp.arange(class_dev)
    valid = class_ids[None, :] < LABELS_REAL
    target = jnp.any(labels[:, :, None] == class_ids[None, None, :], 1).astype(jnp.float32)
    image_total = labels.shape[0] * dp_count
    loss_part = (
        jnp.sum(jnp.where(valid, jax.nn.softplus(logits) - target * logits, 0.0)) / image_total
    )
    grad_logits = (jnp.where(valid, jax.nn.sigmoid(logits) - target, 0.0) / image_total).astype(
        jnp.bfloat16
    )
    group_grad = jnp.einsum("gc,dc->gd", grad_logits, head_low, preferred_element_type=jnp.float32)
    grad_pooled = lax.psum_scatter(group_grad, "cls", scatter_dimension=0, tiled=True)
    grad_logits_all = lax.all_gather(grad_logits, "dp", axis=0, tiled=True)
    pooled_mine = lax.dynamic_slice_in_dim(pooled_all, dp_index * row_count, row_count, 1)
    head_grad = jnp.einsum(
        "gr,gc->rc", pooled_mine, grad_logits_all, preferred_element_type=jnp.float32
    )

    def pool_local(rows_in, gain, shift):
        return pool_rows(rows_in, gain, shift, pack_ids, pack_keep)

    pool_back = jax.vjp(pool_local, output, final_gain, final_shift)[1]
    grad_output, grad_gain, grad_shift = pool_back(grad_pooled)
    grad_first, grad_mlp, grad_vectors = layer_backward(
        blocks,
        vec_all,
        patches,
        saved,
        pack_ids,
        key_codes,
        grad_output,
        grad_gain,
        grad_shift,
    )

    def reduced_half(values):
        part = lax.psum_scatter(values, ("dp", "cls"), scatter_dimension=1, tiled=True)
        return lax.all_gather(
            part, ("dp", "cls"), axis=1, tiled=True, axis_index_groups=half_groups
        )

    grad_half = jnp.concatenate([reduced_half(grad_first), reduced_half(grad_mlp)], 0)
    own_start = (dp_index % half_dp) * row_count
    block_rows = lax.dynamic_slice_in_dim(grad_half, own_start, row_count, 1)
    vector_sum = lax.psum(grad_vectors, ("dp", "cls"))
    vector_rows = lax.dynamic_slice_in_dim(vector_sum, dp_index * row_count, row_count, 1)

    precise = lax.Precision.HIGHEST
    grad_quads = split_halves(grad_half, half_size)
    rows_quads = split_halves(block_rows, half_size)
    cols_quads = lax.dynamic_slice_in_dim(grad_quads, own_start, row_count, 3)
    left_add = jnp.einsum("brjk,bljk->brjl", rows_quads, grad_quads, precision=precise)
    right_add = jnp.einsum("bkja,bkjm->bajm", cols_quads, grad_quads, precision=precise)
    direction = jnp.einsum(
        "brjk,bkjm->brjm", split_halves(root_left, half_size), grad_quads, precision=precise
    )
    direction = jnp.einsum(
        "brjk,bkjm->brjm", direction, split_halves(right_half, half_size), precision=precise
    )
    block_squares = jnp.sum(direction * direction, (1, 3))
    in_top = (dp_index < half_dp).astype(jnp.float32)
    once = (cls_index == 0).astype(jnp.float32)
    layer_squares = once * jnp.sum(block_rows * block_rows)
    vector_squares = once * jnp.sum(vector_rows * vector_rows)
    packed = jnp.concatenate(
        [
            (once * in_top * block_squares).reshape(-1),
            (once * (1.0 - in_top) * block_squares).reshape(-1),
            jnp.stack([layer_squares + vector_squares + jnp.sum(head_grad * head_grad), loss_part]),
        ]
    )
    packed = lax.psum(packed, ("dp", "cls"))
    loss = packed[4 * block_count + 1]
    grad_norm = jnp.sqrt(packed[4 * block_count])
    factor = CLIP_NORM / jnp.maximum(grad_norm, CLIP_NORM)
    sums = packed[: 4 * block_count].reshape(2, block_count, 2)
    mean_squares = jnp.where(dp_index < half_dp, sums[0], sums[1]) / (half_size * half_size)
    mean_squares = mean_squares * factor * factor
    scale = factor * lax.rsqrt(mean_squares + ROOT_EPS)
    flat = (block_count, row_count, feature_dim)
    new_blocks = enc_weights - SHAMPOO_RATE * (direction * scale[:, None, :, None]).reshape(flat)
    square_factor = 0.5 * factor * factor
    new_left = 0.5 * stats_left + square_factor * left_add.reshape(flat)
    new_right = 0.5 * stats_right + square_factor * right_add.reshape(flat)
    count = step.astype(jnp.float32)
    new_vec, new_vec_m, new_vec_v = adam_step(vectors, vector_rows * factor, vec_m, vec_v, count)
    new_head, new_head_m, new_head_v = adam_step(
        head_weights, head_grad * factor, head_m, head_v, count
    )
    return (
        loss,
        grad_norm,
        new_blocks,
        block_rows * factor,
        new_left,
        new_right,
        new_vec,
        new_vec_m,
        new_vec_v,
        new_head,
        new_head_m,
        new_head_v,
    )


def solution(mesh):
    return jax.shard_map(
        on_device,
        mesh=mesh,
        in_specs=(
            P(("dp", "cls"), None),
            P(("dp", "cls"), None),
            P(("dp", "cls"), None),
            P("dp", None),
            P(),
            P(),
            P(None, "dp", None),
            P(None, "dp", None),
            P(None, "dp", None),
            P(None, "dp", None),
            P(None, "dp", None),
            P("dp", "cls"),
            P("dp", "cls"),
            P("dp", "cls"),
            P(None, "dp"),
            P(None, "dp"),
            P(None, "dp"),
        ),
        out_specs=(
            P(),
            P(),
            P(None, "dp", None),
            P(None, "dp", None),
            P(None, "dp", None),
            P(None, "dp", None),
            P(None, "dp"),
            P(None, "dp"),
            P(None, "dp"),
            P("dp", "cls"),
            P("dp", "cls"),
            P("dp", "cls"),
        ),
        check_vma=False,
    )
```

```python
import functools

import jax
import jax.numpy as jnp
from jax import lax
from jax.experimental import pallas as pl
from jax.experimental.pallas import tpu as pltpu
from jax.sharding import PartitionSpec as P

HEADS = 12
HEAD = 64
LABELS_REAL = 21843
IMAGE_MAX = 196
QTILE = 256
PAIR = 2 * HEAD
ROWS = 256
HIDDEN_TILE = 384
MESH = pl.DeviceIdType.MESH
CODE_TOP = 32766.0
CODE_FLOOR = 1e-33
PIECE = 48
IMG_PACK = 8


FULL_PRECISION = lax.Precision.HIGHEST
NORM_EPS = 1e-06
CLIP_NORM = 1.0
ADAM_RATE = 0.02
SHAMPOO_RATE = 0.01
BETA_FIRST = 0.9
BETA_SECOND = 0.999
ADAM_EPS = 1e-08
WEIGHT_DECAY = 0.1
ROOT_EPS = 1e-06


def norm_rows(values, gain, shift):
    centred = values - jnp.mean(values, -1, keepdims=True)
    spread = jnp.mean(centred * centred, -1, keepdims=True)
    return centred * lax.rsqrt(spread + NORM_EPS) * gain + shift


def pool_rows(output, gain, shift, pack_ids, pack_keep):
    final = norm_rows(output, gain, shift)
    member = (
        (pack_ids[None, :] == jnp.arange(IMG_PACK)[:, None]) & (pack_keep[None, :] == 1)
    ).astype(jnp.float32)
    counted = jnp.maximum(jnp.sum(member, 1), 1.0)
    return jnp.dot(member, final, precision=FULL_PRECISION) / counted[:, None]


def key_window(tile, length):
    reach = -(-(IMAGE_MAX - 1) // 128) * 128
    low = max(0, tile * QTILE - reach)
    high = min(length, (tile + 1) * QTILE + reach)
    return low, high


def attention_forward_kernel(qids_ref, kcodes_ref, q_ref, k_ref, v_ref, out_ref, bias_ref):
    length = q_ref.shape[0]
    lane = lax.broadcasted_iota(jnp.int32, (QTILE, PAIR), 1)

    @pl.when(pl.program_id(0) == 0)
    def _():
        for tile in range(length // QTILE):
            low, high = key_window(tile, length)
            shape = (QTILE, high - low)
            rows = lax.broadcasted_iota(jnp.int32, shape, 0) + tile * QTILE
            cols = lax.broadcasted_iota(jnp.int32, shape, 1) + low
            same = qids_ref[tile * QTILE : (tile + 1) * QTILE, :] == kcodes_ref[:, low:high]
            bias_ref[tile, :, : high - low] = jnp.where(same | (rows == cols), 0.0, -1e30)

    for tile in range(length // QTILE):
        low, high = key_window(tile, length)
        rows = pl.ds(tile * QTILE, QTILE)
        queries = q_ref[rows, :] * jnp.bfloat16(HEAD ** (-0.5))
        keys = k_ref[low:high, :]
        values = v_ref[low:high, :]
        halves = []
        for head in range(2):
            mine = (lane >= head * HEAD) & (lane < (head + 1) * HEAD)
            picked = jnp.where(mine, queries, jnp.zeros_like(queries))
            scores = lax.dot_general(
                picked, keys, (((1,), (1,)), ((), ())), preferred_element_type=jnp.float32
            )
            scores = scores + bias_ref[tile, :, : high - low]
            top = jnp.max(scores, -1, keepdims=True)
            weights = jnp.exp(scores - top)
            probs = weights * (1.0 / jnp.sum(weights, -1, keepdims=True))
            halves.append(
                jnp.dot(probs.astype(jnp.bfloat16), values, preferred_element_type=jnp.float32)
            )
        out_ref[rows, :] = jnp.where(lane < HEAD, halves[0], halves[1]).astype(jnp.bfloat16)


def attention_backward_kernel(
    qids_ref, kcodes_ref, q_ref, k_ref, v_ref, do_ref, out_ref, bias_ref, dk_ref, dv_ref
):
    length = q_ref.shape[0]
    lane = lax.broadcasted_iota(jnp.int32, (QTILE, PAIR), 1)
    scale = jnp.bfloat16(HEAD ** (-0.5))

    @pl.when(pl.program_id(0) == 0)
    def _():
        for tile in range(length // QTILE):
            low, high = key_window(tile, length)
            shape = (high - low, QTILE)
            rows = lax.broadcasted_iota(jnp.int32, shape, 0) + low
            cols = lax.broadcasted_iota(jnp.int32, shape, 1) + tile * QTILE
            same = kcodes_ref[low:high, :] == qids_ref[:, tile * QTILE : (tile + 1) * QTILE]
            bias_ref[tile, : high - low, :] = jnp.where(same | (rows == cols), 0.0, -1e30)

    dk_ref[...] = jnp.zeros_like(dk_ref)
    dv_ref[...] = jnp.zeros_like(dv_ref)
    for tile in range(length // QTILE):
        low, high = key_window(tile, length)
        rows = pl.ds(tile * QTILE, QTILE)
        window = pl.ds(low, high - low)
        queries = q_ref[rows, :] * scale
        keys = k_ref[window, :]
        values = v_ref[window, :]
        grads = do_ref[rows, :]
        halves = []
        for head in range(2):
            mine = (lane >= head * HEAD) & (lane < (head + 1) * HEAD)
            picked = jnp.where(mine, queries, jnp.zeros_like(queries))
            picked_grads = jnp.where(mine, grads, jnp.zeros_like(grads))
            scores = lax.dot_general(
                keys, picked, (((1,), (1,)), ((), ())), preferred_element_type=jnp.float32
            )
            scores = scores + bias_ref[tile, : high - low, :]
            top = jnp.max(scores, 0, keepdims=True)
            weights = jnp.exp(scores - top)
            probs = weights * (1.0 / jnp.sum(weights, 0, keepdims=True))
            grad_probs = lax.dot_general(
                values, picked_grads, (((1,), (1,)), ((), ())), preferred_element_type=jnp.float32
            )
            inner = jnp.sum(probs * grad_probs, 0, keepdims=True)
            grad_scores = (probs * (grad_probs - inner)).astype(jnp.bfloat16)
            dv_ref[window, :] += jnp.dot(
                probs.astype(jnp.bfloat16), picked_grads, preferred_element_type=jnp.float32
            )
            dk_ref[window, :] += jnp.dot(
                grad_scores, picked, preferred_element_type=jnp.float32
            )
            halves.append(
                lax.dot_general(
                    grad_scores,
                    keys,
                    (((0,), (0,)), ((), ())),
                    preferred_element_type=jnp.float32,
                )
            )
        grad_queries = jnp.where(lane < HEAD, halves[0], halves[1]) * HEAD ** (-0.5)
        out_ref[0, rows, :] = grad_queries.astype(jnp.bfloat16)
    out_ref[1] = dk_ref[...].astype(jnp.bfloat16)
    out_ref[2] = dv_ref[...].astype(jnp.bfloat16)


def pair_spec(length, part=None):
    if part is None:
        return pl.BlockSpec((length, PAIR), lambda pair: (0, pair))
    return pl.BlockSpec((None, length, PAIR), lambda pair: (part, 0, pair))


def whole_spec(shape):
    return pl.BlockSpec(shape, lambda pair: (0,) * len(shape))


def attention_forward(qkv_rows, pack_ids, key_codes):
    _, length, width = qkv_rows.shape
    tiles = length // QTILE
    window = max(high - low for low, high in (key_window(t, length) for t in range(tiles)))
    return pl.pallas_call(
        attention_forward_kernel,
        grid=(width // PAIR,),
        out_shape=jax.ShapeDtypeStruct((length, width), jnp.bfloat16),
        in_specs=[whole_spec((length, 1)), whole_spec((1, length))]
        + [pair_spec(length, part) for part in range(3)],
        out_specs=pair_spec(length),
        scratch_shapes=[pltpu.VMEM((tiles, QTILE, window), jnp.float32)],
        compiler_params=pltpu.CompilerParams(vmem_limit_bytes=40 << 20),
        name="attention_forward",
    )(pack_ids[:, None], key_codes[None, :], qkv_rows, qkv_rows, qkv_rows)


def attention_backward(qkv_rows, pack_ids, key_codes, grad_attended):
    _, length, width = qkv_rows.shape
    tiles = length // QTILE
    window = max(high - low for low, high in (key_window(t, length) for t in range(tiles)))
    return pl.pallas_call(
        attention_backward_kernel,
        grid=(width // PAIR,),
        out_shape=jax.ShapeDtypeStruct((3, length, width), jnp.bfloat16),
        in_specs=[whole_spec((1, length)), whole_spec((length, 1))]
        + [pair_spec(length, part) for part in range(3)]
        + [pair_spec(length)],
        out_specs=pl.BlockSpec((3, length, PAIR), lambda pair: (0, 0, pair)),
        scratch_shapes=[
            pltpu.VMEM((tiles, window, QTILE), jnp.float32),
            pltpu.VMEM((length, PAIR), jnp.float32),
            pltpu.VMEM((length, PAIR), jnp.float32),
        ],
        compiler_params=pltpu.CompilerParams(vmem_limit_bytes=40 << 20),
        name="attention_backward",
    )(pack_ids[None, :], key_codes[:, None], qkv_rows, qkv_rows, qkv_rows, grad_attended)


def mlp_forward_kernel(x_ref, up_ref, bias_ref, down_ref, units_ref, slope_ref, out_ref):
    first = pl.program_id(0) == 0

    @pl.when(first)
    def _():
        out_ref[...] = jnp.zeros_like(out_ref)

    for start in range(0, x_ref.shape[0], ROWS):
        rows = pl.ds(start, ROWS)
        pre = jnp.dot(x_ref[rows, :], up_ref[...], preferred_element_type=jnp.float32)
        pre = pre + bias_ref[...]
        half = 0.5 + 0.5 * lax.erf(pre * 0.7071067811865476)
        bell = jnp.exp(-0.5 * pre * pre) * 0.3989422804014327
        units = (pre * half).astype(jnp.bfloat16)
        units_ref[rows, :] = units
        slope_ref[rows, :] = half + pre * bell
        out_ref[rows, :] += jnp.dot(units, down_ref[...], preferred_element_type=jnp.float32)


def mlp_backward_kernel(
    x_ref, dm_ref, up_ref, down_ref, units_ref, slope_ref,
    grad_up_ref, grad_down_ref, bias_ref, dx_ref, dpre_ref
):
    @pl.when(pl.program_id(0) == 0)
    def _():
        dx_ref[...] = jnp.zeros_like(dx_ref)

    total = jnp.zeros((1, HIDDEN_TILE), jnp.float32)
    for start in range(0, x_ref.shape[0], ROWS):
        rows = pl.ds(start, ROWS)
        units_back = lax.dot_general(
            dm_ref[rows, :], down_ref[...], (((1,), (1,)), ((), ())),
            preferred_element_type=jnp.float32,
        )
        grad_pre = (units_back * slope_ref[rows, :]).astype(jnp.bfloat16)
        dpre_ref[rows, :] = grad_pre
        total = total + jnp.sum(grad_pre.astype(jnp.float32), 0, keepdims=True)
        dx_ref[rows, :] += lax.dot_general(
            grad_pre, up_ref[...], (((1,), (1,)), ((), ())), preferred_element_type=jnp.float32
        )
    bias_ref[...] = total
    over_rows = (((0,), (0,)), ((), ()))
    grad_down_ref[...] = lax.dot_general(
        units_ref[...], dm_ref[...], over_rows, preferred_element_type=jnp.float32
    )
    grad_up_ref[...] = lax.dot_general(
        x_ref[...], dpre_ref[...], over_rows, preferred_element_type=jnp.float32
    )


def mlp_specs(length, width, up_count):
    split = width // HIDDEN_TILE
    resident = pl.BlockSpec((length, width), lambda t: (0, 0))
    up = pl.BlockSpec((None, width, HIDDEN_TILE), lambda t: (5 + t // split, 0, t % split))
    down = pl.BlockSpec(
        (None, HIDDEN_TILE, width), lambda t: (5 + up_count + t // split, t % split, 0)
    )
    hidden = pl.BlockSpec((length, HIDDEN_TILE), lambda t: (0, t))
    bias = pl.BlockSpec((1, HIDDEN_TILE), lambda t: (0, t))
    return split, resident, up, down, hidden, bias


def mlp_forward(rows, blocks, up_bias):
    length, width = rows.shape
    up_count = (blocks.shape[0] - 5) // 2
    split, resident, up, down, hidden, bias = mlp_specs(length, width, up_count)
    hidden_size = up_count * width
    return pl.pallas_call(
        mlp_forward_kernel,
        grid=(up_count * split,),
        out_shape=(
            jax.ShapeDtypeStruct((length, hidden_size), jnp.bfloat16),
            jax.ShapeDtypeStruct((length, hidden_size), jnp.float32),
            jax.ShapeDtypeStruct((length, width), jnp.float32),
        ),
        in_specs=[resident, up, bias, down],
        out_specs=(hidden, hidden, resident),
        compiler_params=pltpu.CompilerParams(vmem_limit_bytes=48 << 20),
        name="mlp_forward",
    )(rows, blocks, up_bias.reshape(1, hidden_size), blocks)


def mlp_backward(rows, grad_branch, blocks, units, slopes):
    length, width = rows.shape
    up_count = (blocks.shape[0] - 5) // 2
    split, resident, up, down, hidden, bias = mlp_specs(length, width, up_count)
    hidden_size = up_count * width
    return pl.pallas_call(
        mlp_backward_kernel,
        grid=(up_count * split,),
        out_shape=(
            jax.ShapeDtypeStruct((up_count, width, width), jnp.float32),
            jax.ShapeDtypeStruct((up_count, width, width), jnp.float32),
            jax.ShapeDtypeStruct((1, hidden_size), jnp.float32),
            jax.ShapeDtypeStruct((length, width), jnp.float32),
        ),
        in_specs=[resident, resident, up, down, hidden, hidden],
        out_specs=(
            pl.BlockSpec((None, width, HIDDEN_TILE), lambda t: (t // split, 0, t % split)),
            pl.BlockSpec((None, HIDDEN_TILE, width), lambda t: (t // split, t % split, 0)),
            bias,
            resident,
        ),
        scratch_shapes=[pltpu.VMEM((length, HIDDEN_TILE), jnp.bfloat16)],
        compiler_params=pltpu.CompilerParams(vmem_limit_bytes=48 << 20),
        name="mlp_backward",
    )(rows, grad_branch, blocks, blocks, units, slopes)


def layer_forward(blocks, vec_all, patch, pack_ids, key_codes):
    up_count = (blocks.shape[0] - 5) // 2
    embedded = jnp.dot(patch, blocks[0], preferred_element_type=jnp.float32) + vec_all[0]
    normed_one = norm_rows(embedded, vec_all[1], vec_all[2]).astype(jnp.bfloat16)
    qkv_rows = jnp.einsum(
        "td,kde->kte", normed_one, blocks[1:4], preferred_element_type=jnp.float32
    )
    qkv_bias = jnp.stack([vec_all[3], jnp.zeros_like(vec_all[3]), vec_all[4]])
    qkv_rows = (qkv_rows + qkv_bias[:, None, :]).astype(jnp.bfloat16)
    attended = attention_forward(qkv_rows, pack_ids, key_codes)
    hidden = (
        embedded + jnp.dot(attended, blocks[4], preferred_element_type=jnp.float32) + vec_all[5]
    )
    normed_two = norm_rows(hidden, vec_all[6], vec_all[7]).astype(jnp.bfloat16)
    units, slopes, branch = mlp_forward(normed_two, blocks, vec_all[8 : 8 + up_count])
    output = hidden + branch + vec_all[8 + up_count]
    return (
        output,
        (embedded, normed_one, qkv_rows, attended, hidden, normed_two, slopes, units),
    )


def layer_backward(
    blocks, vec_all, patch, saved, pack_ids, key_codes, grad_output, grad_gain, grad_shift
):
    embedded, normed_one, qkv_rows, attended, hidden, normed_two, slopes, units = saved
    feature_dim = patch.shape[1]
    up_count = (blocks.shape[0] - 5) // 2
    grad_branch = grad_output.astype(jnp.bfloat16)
    grad_up, grad_down, up_sums, grad_normed_two = mlp_backward(
        normed_two, grad_branch, blocks, units, slopes
    )
    norm_two_back = jax.vjp(norm_rows, hidden, vec_all[6], vec_all[7])[1]
    grad_hidden_norm, grad_gain_two, grad_shift_two = norm_two_back(grad_normed_two)
    grad_hidden = grad_output + grad_hidden_norm
    grad_attn_out = grad_hidden.astype(jnp.bfloat16)
    grad_out_proj = jnp.einsum(
        "te,td->ed", attended, grad_attn_out, preferred_element_type=jnp.float32
    )
    grad_attended = jnp.einsum(
        "td,ed->te", grad_attn_out, blocks[4], preferred_element_type=jnp.float32
    ).astype(jnp.bfloat16)
    grad_qkv = attention_backward(qkv_rows, pack_ids, key_codes, grad_attended)
    grad_qkv_proj = jnp.einsum(
        "td,kte->kde", normed_one, grad_qkv, preferred_element_type=jnp.float32
    )
    grad_normed_one = jnp.einsum(
        "kte,kde->td", grad_qkv, blocks[1:4], preferred_element_type=jnp.float32
    )
    norm_one_back = jax.vjp(norm_rows, embedded, vec_all[1], vec_all[2])[1]
    grad_embed_norm, grad_gain_one, grad_shift_one = norm_one_back(grad_normed_one)
    grad_embedded = (grad_hidden + grad_embed_norm).astype(jnp.bfloat16)
    grad_patch = jnp.einsum("tp,td->pd", patch, grad_embedded, preferred_element_type=jnp.float32)
    grad_arrays = (grad_patch[None], grad_qkv_proj, grad_out_proj[None], grad_up, grad_down)
    bias_sums = jnp.stack(
        [
            jnp.sum(grad_embedded.astype(jnp.float32), 0),
            grad_gain_one,
            grad_shift_one,
            jnp.sum(grad_qkv[0].astype(jnp.float32), 0),
            jnp.sum(grad_qkv[2].astype(jnp.float32), 0),
            jnp.sum(grad_attn_out.astype(jnp.float32), 0),
            grad_gain_two,
            grad_shift_two,
        ]
    )
    up_sums = up_sums.reshape(up_count, feature_dim)
    tail_sums = jnp.stack([jnp.sum(grad_branch.astype(jnp.float32), 0), grad_gain, grad_shift])
    return (grad_arrays, jnp.concatenate([bias_sums, up_sums, tail_sums], 0))


def torus_place():
    dp, cls = lax.axis_index("dp"), lax.axis_index("cls")
    return dp // 2, dp % 2, cls // 2, cls % 2


def torus_device(z, y, x, core):
    return (z * 2 + y, x * 2 + core)


def encode(pieces, code_refs, scale_ref):
    top = None
    for piece in pieces:
        peak = jnp.max(jnp.abs(piece()), 0, keepdims=True)
        top = peak if top is None else jnp.maximum(top, peak)
    top = jnp.maximum(top, CODE_FLOOR)
    inverse = CODE_TOP / top
    for piece, code_ref in zip(pieces, code_refs):
        code_ref[...] = jnp.round(piece() * inverse).astype(jnp.int32).astype(jnp.int16)
    scale_ref[...] = top * (1.0 / CODE_TOP)


def decode(code, scale):
    return code.astype(jnp.int32).astype(jnp.float32) * scale


def reduce_kernel(counts, *refs):
    sources, refs = refs[: len(counts)], refs[len(counts) :]
    (vec_ref, codes_hbm, scales_hbm, vec_out_ref,
     acc, spare, kept, sent0, got0, sent1, got1, sent2, got2, sent3, got3, sent4, got4,
     ss0, gs0, ss1, gs1, ss2, gs2, ss3, gs3, ss4, gs4, codes, scales, vec_got,
     load_sem, out_sem, send_sem, recv_sem, send_scale_sem, recv_scale_sem,
     vec_send_sem, vec_recv_sem) = refs
    total = sum(counts)
    half, width = codes.shape[1], codes.shape[2]
    cols = width // 2
    z, y, x, core = torus_place()
    upper = z // 2
    inner = (z % 2) != upper
    mate_core = torus_device(z, y, x, 1 - core)
    mate_x = torus_device(z, y, 1 - x, core)
    mate_y = torus_device(z, 1 - y, x, core)
    mate_z = torus_device(z + 1 - 2 * (z % 2), y, x, core)
    mate_mid = torus_device(3 - z, y, x, core)
    mate_far = torus_device((z + 2) % 4, y, x, core)

    barrier = pltpu.get_barrier_semaphore()
    mates = (mate_core, mate_x, mate_y, mate_z, mate_mid, mate_far)
    for mate in mates:
        pl.semaphore_signal(barrier, inc=1, device_id=mate, device_id_type=MESH)
    pl.semaphore_wait(barrier, len(mates))

    own_cols = pl.ds(pl.multiple_of(core * cols, 128), cols)
    other_cols = pl.ds(pl.multiple_of((1 - core) * cols, 128), cols)

    def rows_at(start, size):
        return pl.ds(pl.multiple_of(start, PIECE), size)

    def loads(m, body):
        start = 0
        for source, count in zip(sources, counts):
            def one(source=source, start=start):
                pair = (
                    pltpu.make_async_copy(
                        source.at[m - start, :, own_cols], acc.at[m % 5], load_sem.at[m % 2, 0]
                    ),
                    pltpu.make_async_copy(
                        source.at[m - start, :, other_cols], spare.at[m % 2], load_sem.at[m % 2, 1]
                    ),
                )
                for copy in pair:
                    body(copy)

            pl.when((m >= start) & (m < start + count))(one)
            start += count

    def message(stage, m, source, scale_source, target, scale_target, mate):
        return (
            pltpu.make_async_remote_copy(
                src_ref=source, dst_ref=target,
                send_sem=send_sem.at[stage, m % 2], recv_sem=recv_sem.at[stage, m],
                device_id=mate, device_id_type=MESH,
            ),
            pltpu.make_async_remote_copy(
                src_ref=scale_source, dst_ref=scale_target,
                send_sem=send_scale_sem.at[stage, m % 2], recv_sem=recv_scale_sem.at[stage, m],
                device_id=mate, device_id_type=MESH,
            ),
        )

    def first(m):
        return message(0, m, sent0.at[m % 2], ss0.at[m % 2], got0.at[m], gs0.at[m], mate_core)

    def second(m, b):
        return message(
            1 + b, m, sent1.at[m % 2, b], ss1.at[m % 2, b], got1.at[m, b], gs1.at[m, b],
            mate_y if b else mate_x,
        )

    def third(m, b):
        return message(
            3 + b, m, sent2.at[m % 2, b], ss2.at[m % 2, b], got2.at[m, b], gs2.at[m, b],
            mate_x if b else mate_y,
        )

    def fourth(m):
        return message(5, m, sent3.at[m % 2], ss3.at[m % 2], got3.at[m], gs3.at[m], mate_z)

    def fifth(m):
        return message(6, m, sent4.at[m % 2], ss4.at[m % 2], got4.at[m], gs4.at[m], mate_mid)

    piece_a = 2 * x + y
    piece_b = 4 + 2 * y + x

    def spread(stage, m, piece, count, mate, columns=own_cols):
        rows = pl.ds(pl.multiple_of(piece * PIECE, PIECE), count * PIECE)
        block = codes.at[m, rows, columns]
        scale = scales.at[m, pl.ds(piece, count), :, columns]
        return message(stage, m, block, scale, block, scale, mate)

    def start(copies):
        for copy in copies:
            copy.start()

    def wait_send(copies):
        for copy in copies:
            copy.wait_send()

    def wait_recv(copies):
        for copy in copies:
            copy.wait_recv()

    def vec_copy(step, mate):
        return pltpu.make_async_remote_copy(
            src_ref=vec_got.at[step, 0], dst_ref=vec_got.at[step, 1],
            send_sem=vec_send_sem.at[step], recv_sem=vec_recv_sem.at[step],
            device_id=mate, device_id_type=MESH,
        )

    vec_mates = (mate_core, mate_x, mate_y, mate_z, mate_far)

    loads(jnp.int32(0), lambda copy: copy.start())
    vec_got[0, 0] = vec_ref[...]
    vec_copy(0, vec_mates[0]).start()

    def step(t, carry):
        for n in range(1, 6):
            @pl.when(t == n)
            def _(n=n):
                vec_copy(n - 1, vec_mates[n - 1]).wait()
                value = vec_got[n - 1, 0] + vec_got[n - 1, 1]
                if n < 5:
                    vec_got[n, 0] = value
                    vec_copy(n, vec_mates[n]).start()
                else:
                    vec_out_ref[...] = value

        @pl.when(t < total)
        def _():
            m = t
            loads(m, lambda copy: copy.wait())

            @pl.when(m + 1 < total)
            def _():
                loads(m + 1, lambda copy: copy.start())

            span = 2 * PIECE
            encode(
                [lambda r=r: spare[m % 2, r : r + span, :] for r in range(0, 2 * half, span)],
                [sent0.at[m % 2, r : r + span, :] for r in range(0, 2 * half, span)],
                ss0.at[m % 2],
            )
            start(first(m))

        @pl.when((t >= 1) & (t < total + 1))
        def _():
            m = t - 1
            copies = first(m)
            wait_send(copies)
            wait_recv(copies)
            slot = m % 5
            span = 2 * PIECE
            for r in range(0, 2 * half, span):
                acc[slot, r : r + span, :] += decode(got0[m, r : r + span, :], gs0[m])
            for b in range(2):
                other = (1 - y) if b else (1 - x)
                begins = [h * half + b * 4 * PIECE + other * span for h in range(2)]
                encode(
                    [lambda s=s: acc[slot, rows_at(s, span), :] for s in begins],
                    [sent1.at[m % 2, b, h] for h in range(2)],
                    ss1.at[m % 2, b],
                )
                start(second(m, b))

        @pl.when((t >= 2) & (t < total + 2))
        def _():
            m = t - 2
            slot = m % 5
            span = 2 * PIECE
            for b in range(2):
                copies = second(m, b)
                wait_send(copies)
                wait_recv(copies)
                mine = y if b else x
                other = (1 - x) if b else (1 - y)
                begins = [h * half + b * 4 * PIECE + mine * span for h in range(2)]
                for h, s in enumerate(begins):
                    acc[slot, rows_at(s, span), :] += decode(got1[m, b, h], gs1[m, b])
                encode(
                    [lambda s=s: acc[slot, rows_at(s + other * PIECE, PIECE), :] for s in begins],
                    [sent2.at[m % 2, b, h] for h in range(2)],
                    ss2.at[m % 2, b],
                )
                start(third(m, b))

        @pl.when((t >= 3) & (t < total + 3))
        def _():
            m = t - 3
            slot = m % 5
            for b in range(2):
                copies = third(m, b)
                wait_send(copies)
                wait_recv(copies)
                place = piece_b if b else piece_a
                for h in range(2):
                    kept[m % 3, h, b] = acc[
                        slot, rows_at(h * half + place * PIECE, PIECE), :
                    ] + decode(got2[m, b, h], gs2[m, b])

            @pl.when(jnp.logical_not(inner))
            def _():
                pairs = [(h, b) for h in range(2) for b in range(2)]
                encode(
                    [lambda h=h, b=b: kept[m % 3, h, b] for h, b in pairs],
                    [sent3.at[m % 2, h, b] for h, b in pairs],
                    ss3.at[m % 2],
                )
                start(fourth(m))

        @pl.when((t >= 4) & (t < total + 4))
        def _():
            m = t - 4
            copies = fourth(m)

            @pl.when(jnp.logical_not(inner))
            def _():
                wait_send(copies)

            @pl.when(inner)
            def _():
                wait_recv(copies)
                for h in range(2):
                    for b in range(2):
                        kept[m % 3, h, b] += decode(got3[m, h, b], gs3[m])
                encode(
                    [lambda b=b: kept[m % 3, 1 - upper, b] for b in range(2)],
                    [sent4.at[m % 2, b] for b in range(2)],
                    ss4.at[m % 2],
                )
                start(fifth(m))

        @pl.when((t >= 5) & (t < total + 5))
        def _():
            m = t - 5

            @pl.when(inner)
            def _():
                copies = fifth(m)
                wait_send(copies)
                wait_recv(copies)
                for b in range(2):
                    place = piece_b if b else piece_a
                    value = kept[m % 3, upper, b] + decode(got4[m, b], gs4[m])
                    encode(
                        [lambda value=value: value],
                        [codes.at[m, rows_at(place * PIECE, PIECE), own_cols]],
                        scales.at[m, place, :, own_cols],
                    )
                    start(spread(7 + b, m, place, 1, mate_z))

        @pl.when((t >= 6) & (t < total + 6))
        def _():
            m = t - 6
            for b in range(2):
                place = piece_b if b else piece_a
                copies = spread(7 + b, m, place, 1, mate_z)

                @pl.when(inner)
                def _(copies=copies):
                    wait_send(copies)

                @pl.when(jnp.logical_not(inner))
                def _(copies=copies):
                    wait_recv(copies)

                start(spread(9 + b, m, place, 1, mate_x if b else mate_y))

        @pl.when((t >= 7) & (t < total + 7))
        def _():
            m = t - 7
            for b in range(2):
                place = piece_b if b else piece_a
                theirs = (4 + 2 * y + 1 - x) if b else (2 * x + 1 - y)
                wait_send(spread(9 + b, m, place, 1, mate_x if b else mate_y))
                wait_recv(spread(9 + b, m, theirs, 1, mate_x if b else mate_y))
                begin = (4 + 2 * y) if b else 2 * x
                start(spread(11 + b, m, begin, 2, mate_y if b else mate_x))

        @pl.when((t >= 8) & (t < total + 8))
        def _():
            m = t - 8
            for b in range(2):
                begin = (4 + 2 * y) if b else 2 * x
                theirs = (4 + 2 * (1 - y)) if b else 2 * (1 - x)
                wait_send(spread(11 + b, m, begin, 2, mate_y if b else mate_x))
                wait_recv(spread(11 + b, m, theirs, 2, mate_y if b else mate_x))
            start(spread(13, m, 0, 8, mate_core))

        def outs(m):
            return (
                pltpu.make_async_copy(codes.at[m], codes_hbm.at[m], out_sem.at[m % 2, 0]),
                pltpu.make_async_copy(scales.at[m], scales_hbm.at[m], out_sem.at[m % 2, 1]),
            )

        @pl.when((t >= 9) & (t < total + 9))
        def _():
            m = t - 9
            wait_send(spread(13, m, 0, 8, mate_core))
            wait_recv(spread(13, m, 0, 8, mate_core, other_cols))
            start(outs(m))

        @pl.when((t >= 10) & (t < total + 10))
        def _():
            for copy in outs(t - 10):
                copy.wait()

        return carry

    lax.fori_loop(0, total + 10, step, 0)


def reduce_gradients(arrays, vec_sums):
    counts = tuple(array.shape[0] for array in arrays)
    total = sum(counts)
    width = arrays[0].shape[1]
    half, cols = width // 2, width // 2
    f32, i16 = jnp.float32, jnp.int16

    def pair(*shape):
        return [pltpu.VMEM((2,) + shape, i16), pltpu.VMEM((total,) + shape, i16)]

    def scale_pair(*shape):
        return [
            pltpu.VMEM((2,) + shape + (1, cols), f32),
            pltpu.VMEM((total,) + shape + (1, cols), f32),
        ]

    hbm = pl.BlockSpec(memory_space=pl.ANY)
    vmem = pl.BlockSpec(memory_space=pltpu.VMEM)
    return pl.pallas_call(
        functools.partial(reduce_kernel, counts),
        out_shape=(
            jax.ShapeDtypeStruct((total, half, width), i16),
            jax.ShapeDtypeStruct((total, half // PIECE, 1, width), f32),
            jax.ShapeDtypeStruct(vec_sums.shape, f32),
        ),
        in_specs=[hbm] * len(arrays) + [vmem],
        out_specs=(hbm, hbm, vmem),
        scratch_shapes=[
            pltpu.VMEM((5, width, cols), f32),
            pltpu.VMEM((2, width, cols), f32),
            pltpu.VMEM((3, 2, 2, PIECE, cols), f32),
        ]
        + pair(width, cols)
        + pair(2, 2, 2 * PIECE, cols)
        + pair(2, 2, PIECE, cols)
        + pair(2, 2, PIECE, cols)
        + pair(2, PIECE, cols)
        + scale_pair()
        + scale_pair(2)
        + scale_pair(2)
        + scale_pair()
        + scale_pair()
        + [
            pltpu.VMEM((total, half, width), i16),
            pltpu.VMEM((total, half // PIECE, 1, width), f32),
            pltpu.VMEM((5, 2) + vec_sums.shape, f32),
            pltpu.SemaphoreType.DMA((2, 2)),
            pltpu.SemaphoreType.DMA((2, 2)),
            pltpu.SemaphoreType.DMA((14, 2)),
            pltpu.SemaphoreType.DMA((14, total)),
            pltpu.SemaphoreType.DMA((14, 2)),
            pltpu.SemaphoreType.DMA((14, total)),
            pltpu.SemaphoreType.DMA((5,)),
            pltpu.SemaphoreType.DMA((5,)),
        ],
        compiler_params=pltpu.CompilerParams(
            collective_id=1, has_side_effects=True, vmem_limit_bytes=60 << 20
        ),
        name="reduce_gradients",
    )(*arrays, vec_sums)


def split_float(values):
    high = values.astype(jnp.bfloat16)
    return high, (values - high.astype(jnp.float32)).astype(jnp.bfloat16)


def stacked_dot(lefts, right, contract_last):
    rows = lefts[0].shape[0]
    left = jnp.concatenate(lefts, 0) if len(lefts) > 1 else lefts[0]
    dims = (((1,), (1 if contract_last else 0,)), ((), ()))
    out = lax.dot_general(left, right, dims, preferred_element_type=jnp.float32)
    return [out[n * rows : (n + 1) * rows] for n in range(len(lefts))]


def precondition_kernel(
    own_count, codes_ref, scales_ref, left_ref, right_ref,
    left_out, right_out, step_out, own_out, squares_ref, high_ref, low_ref
):
    half, width = codes_ref.shape
    rows = left_ref.shape[0]
    own = lax.rem(lax.axis_index("dp"), own_count) * rows
    own_rows = pl.ds(pl.multiple_of(own, PIECE), rows)
    for piece in range(half // PIECE):
        part = slice(piece * PIECE, (piece + 1) * PIECE)
        value = codes_ref[part, :].astype(jnp.int32).astype(jnp.float32) * scales_ref[piece]
        high_ref[part, :], low_ref[part, :] = split_float(value)
    own_value = high_ref[own_rows, :].astype(jnp.float32) + low_ref[own_rows, :].astype(jnp.float32)
    own_out[...] = own_value
    squares_ref[0:1, :] = jnp.sum(own_value * own_value, 0, keepdims=True)
    picks = (
        lax.broadcasted_iota(jnp.int32, (rows, half), 1)
        == lax.broadcasted_iota(jnp.int32, (rows, half), 0) + own
    ).astype(jnp.float32).astype(jnp.bfloat16)
    for quad in range(2):
        cols = slice(quad * half, (quad + 1) * half)
        high, low = high_ref[:, cols], low_ref[:, cols]
        mine_high, mine_low = high_ref[own_rows, cols], low_ref[own_rows, cols]
        hh, lh, turned_high = stacked_dot([mine_high, mine_low, picks], high, True)
        hl, turned_low = stacked_dot([mine_high, picks], low, True)
        left_out[:, cols] = hh + (lh + hl)
        turned_high = turned_high.astype(jnp.bfloat16)
        turned_low = turned_low.astype(jnp.bfloat16)
        root_high, root_low = split_float(left_ref[:, cols])
        thh, tlh, rhh, rlh = stacked_dot([turned_high, turned_low, root_high, root_low], high, False)
        thl, rhl = stacked_dot([turned_high, root_high], low, False)
        right_out[:, cols] = thh + (tlh + thl)
        half_step = rhh + (rlh + rhl)
        step_high, step_low = split_float(half_step)
        right_high, right_low = split_float(right_ref[:, cols])
        shh, slh = stacked_dot([step_high, step_low], right_high, False)
        (shl,) = stacked_dot([step_high], right_low, False)
        direction = shh + (slh + shl)
        step_out[:, cols] = direction
        squares_ref[1:2, cols] = jnp.sum(direction * direction, 0, keepdims=True)


def precondition(codes, scales, root_left, right_half, own_count):
    count, half, width = codes.shape
    rows = root_left.shape[1]

    def spec(*shape):
        return pl.BlockSpec((None,) + shape, lambda b: (b,) + (0,) * len(shape))

    mine = jax.ShapeDtypeStruct((count, rows, width), jnp.float32)
    return pl.pallas_call(
        functools.partial(precondition_kernel, own_count),
        grid=(count,),
        out_shape=(mine, mine, mine, mine, jax.ShapeDtypeStruct((count, 2, width), jnp.float32)),
        in_specs=[
            spec(half, width),
            spec(half // PIECE, 1, width),
            spec(rows, width),
            spec(half, width),
        ],
        out_specs=(spec(rows, width),) * 4 + (spec(2, width),),
        scratch_shapes=[
            pltpu.VMEM((half, width), jnp.bfloat16),
            pltpu.VMEM((half, width), jnp.bfloat16),
        ],
        compiler_params=pltpu.CompilerParams(vmem_limit_bytes=32 << 20),
        name="precondition",
    )(codes, scales, root_left, right_half)


def sum_kernel(dp_count, cls_count, in_ref, out_ref, slots, send_sem, recv_sem):
    dp, cls = lax.axis_index("dp"), lax.axis_index("cls")
    total = dp_count * cls_count
    me = dp * cls_count + cls
    barrier = pltpu.get_barrier_semaphore()

    def mate(n):
        other = lax.rem(me + n, total)
        return (other // cls_count, lax.rem(other, cls_count))

    for n in range(1, total):
        pl.semaphore_signal(barrier, inc=1, device_id=mate(n), device_id_type=MESH)
    pl.semaphore_wait(barrier, total - 1)

    def copy(n):
        return pltpu.make_async_remote_copy(
            src_ref=in_ref, dst_ref=slots.at[me],
            send_sem=send_sem.at[n], recv_sem=recv_sem.at[me],
            device_id=mate(n), device_id_type=MESH,
        )

    def arrival(n):
        source = lax.rem(me + n, total)
        return pltpu.make_async_remote_copy(
            src_ref=in_ref, dst_ref=slots.at[source],
            send_sem=send_sem.at[n], recv_sem=recv_sem.at[source],
            device_id=mate(n), device_id_type=MESH,
        )

    for n in range(1, total):
        copy(n).start()
    slots[me] = in_ref[...]
    for n in range(1, total):
        copy(n).wait_send()
        arrival(n).wait_recv()
    value = slots[0]
    for n in range(1, total):
        value = value + slots[n]
    out_ref[...] = value


def sum_everywhere(values, dp_count, cls_count):
    total = dp_count * cls_count
    vmem = pl.BlockSpec(memory_space=pltpu.VMEM)
    return pl.pallas_call(
        functools.partial(sum_kernel, dp_count, cls_count),
        out_shape=jax.ShapeDtypeStruct(values.shape, jnp.float32),
        in_specs=[vmem],
        out_specs=vmem,
        scratch_shapes=[
            pltpu.VMEM((total,) + values.shape, jnp.float32),
            pltpu.SemaphoreType.DMA((total,)),
            pltpu.SemaphoreType.DMA((total,)),
        ],
        compiler_params=pltpu.CompilerParams(collective_id=2, has_side_effects=True),
        name="sum_everywhere",
    )(values)


def adam_step(weight, grad, first, second, count):
    first = BETA_FIRST * first + (1.0 - BETA_FIRST) * grad
    second = BETA_SECOND * second + (1.0 - BETA_SECOND) * grad * grad
    fix_first = 1.0 - jnp.power(BETA_FIRST, count)
    fix_second = 1.0 - jnp.power(BETA_SECOND, count)
    update = first / fix_first / (jnp.sqrt(second / fix_second) + ADAM_EPS) + WEIGHT_DECAY * weight
    return (weight - ADAM_RATE * update, first, second)


def split_halves(values, half_size):
    block_count, row_count, feature_dim = values.shape
    return values.reshape(block_count, row_count, 2, half_size)


def reduced_half(values, half_groups):
    part = lax.psum_scatter(values, ("dp", "cls"), scatter_dimension=1, tiled=True)
    return lax.all_gather(part, ("dp", "cls"), axis=1, tiled=True, axis_index_groups=half_groups)


def preconditioned_rows(grad_half, root_left, right_half, own_start):
    count, row_count, width = root_left.shape
    half_size = width // 2
    block_rows = lax.dynamic_slice_in_dim(grad_half, own_start, row_count, 1)
    grad_quads = split_halves(grad_half, half_size)
    rows_quads = split_halves(block_rows, half_size)
    cols_quads = lax.dynamic_slice_in_dim(grad_quads, own_start, row_count, 3)
    precise = FULL_PRECISION
    left_add = jnp.einsum("brjk,bljk->brjl", rows_quads, grad_quads, precision=precise)
    right_add = jnp.einsum("bkja,bkjm->bajm", cols_quads, grad_quads, precision=precise)
    direction = jnp.einsum(
        "brjk,bkjm->brjm", split_halves(root_left, half_size), grad_quads, precision=precise
    )
    direction = jnp.einsum(
        "brjk,bkjm->brjm", direction, split_halves(right_half, half_size), precision=precise
    )
    flat = (count, row_count, width)
    return left_add.reshape(flat), right_add.reshape(flat), direction.reshape(flat), block_rows


def on_device(
    patches,
    image_ids,
    keep,
    labels,
    owner,
    step,
    enc_weights,
    stats_left,
    stats_right,
    root_left,
    root_right,
    head_weights,
    head_m,
    head_v,
    vectors,
    vec_m,
    vec_v,
):
    dp_count = lax.axis_size("dp")
    cls_count = lax.axis_size("cls")
    dp_index = lax.axis_index("dp")
    cls_index = lax.axis_index("cls")
    block_count, row_count, feature_dim = enc_weights.shape
    up_count = (block_count - 5) // 2
    half_size = feature_dim // 2
    part_rows = row_count // cls_count
    half_dp = dp_count // 2
    half_group = half_dp * cls_count
    half_groups = [
        list(range(half_group)),
        list(range(half_group, 2 * half_group)),
    ]

    def my_part(values):
        return lax.dynamic_slice_in_dim(values, cls_index * part_rows, part_rows, 1)

    blocks = lax.all_gather(
        my_part(enc_weights.astype(jnp.bfloat16)), ("dp", "cls"), axis=1, tiled=True
    )
    vec_low = lax.all_gather(vectors.astype(jnp.bfloat16), "dp", axis=1, tiled=True)
    vec_all = vec_low.astype(jnp.float32)
    head_low = lax.all_gather(head_weights.astype(jnp.bfloat16), "dp", axis=0, tiled=True)
    right_half = lax.all_gather(
        my_part(root_right), ("dp", "cls"), axis=1, tiled=True, axis_index_groups=half_groups
    )
    final_gain = vec_all[9 + up_count]
    final_shift = vec_all[10 + up_count]
    pack_ids, pack_keep = image_ids[0], keep[0]
    key_codes = jnp.where(pack_keep == 1, pack_ids, -1)

    output, saved = layer_forward(blocks, vec_all, patches, pack_ids, key_codes)
    pooled = pool_rows(output, final_gain, final_shift, pack_ids, pack_keep)
    group = lax.all_gather(pooled.astype(jnp.bfloat16), "cls", axis=0, tiled=True)
    pooled_all = lax.all_gather(group, "dp", axis=0, tiled=True)
    logits = jnp.dot(group, head_low, preferred_element_type=jnp.float32)
    class_dev = head_low.shape[1]
    class_ids = cls_index * class_dev + jnp.arange(class_dev)
    valid = class_ids[None, :] < LABELS_REAL
    target = jnp.any(labels[:, :, None] == class_ids[None, None, :], 1).astype(jnp.float32)
    image_total = labels.shape[0] * dp_count
    loss_part = (
        jnp.sum(jnp.where(valid, jax.nn.softplus(logits) - target * logits, 0.0)) / image_total
    )
    grad_logits = (jnp.where(valid, jax.nn.sigmoid(logits) - target, 0.0) / image_total).astype(
        jnp.bfloat16
    )
    group_grad = jnp.einsum("gc,dc->gd", grad_logits, head_low, preferred_element_type=jnp.float32)
    grad_pooled = lax.psum_scatter(group_grad, "cls", scatter_dimension=0, tiled=True)
    grad_logits_all = lax.all_gather(grad_logits, "dp", axis=0, tiled=True)
    pooled_mine = lax.dynamic_slice_in_dim(pooled_all, dp_index * row_count, row_count, 1)
    head_grad = jnp.einsum(
        "gr,gc->rc", pooled_mine, grad_logits_all, preferred_element_type=jnp.float32
    )

    def pool_local(rows_in, gain, shift):
        return pool_rows(rows_in, gain, shift, pack_ids, pack_keep)

    pool_back = jax.vjp(pool_local, output, final_gain, final_shift)[1]
    grad_output, grad_gain, grad_shift = pool_back(grad_pooled)
    grad_arrays, grad_vectors = layer_backward(
        blocks,
        vec_all,
        patches,
        saved,
        pack_ids,
        key_codes,
        grad_output,
        grad_gain,
        grad_shift,
    )

    on_torus = dp_count == 8 and cls_count == 4
    if on_torus:
        padded = jnp.pad(grad_vectors, ((0, -grad_vectors.shape[0] % 8), (0, 0)))
        codes, scales, vector_sum = reduce_gradients(grad_arrays, padded)
        vector_sum = vector_sum[: grad_vectors.shape[0]]
        left_add, right_add, direction, block_rows, squares = precondition(
            codes, scales, root_left, right_half, half_dp
        )
        layer_squares = jnp.sum(squares[:, 0])
        block_squares = jnp.sum(squares[:, 1].reshape(block_count, 2, half_size), -1)
    else:
        grad_half = reduced_half(jnp.concatenate(grad_arrays, 0), half_groups)
        vector_sum = lax.psum(grad_vectors, ("dp", "cls"))
        left_add, right_add, direction, block_rows = preconditioned_rows(
            grad_half, root_left, right_half, (dp_index % half_dp) * row_count
        )
        layer_squares = jnp.sum(block_rows * block_rows)
        block_squares = jnp.sum(split_halves(direction * direction, half_size), (1, 3))
    vector_rows = lax.dynamic_slice_in_dim(vector_sum, dp_index * row_count, row_count, 1)
    in_top = (dp_index < half_dp).astype(jnp.float32)
    once = (cls_index == 0).astype(jnp.float32)
    own_squares = once * (layer_squares + jnp.sum(vector_rows * vector_rows))
    packed = jnp.concatenate(
        [
            (once * in_top * block_squares).reshape(-1),
            (once * (1.0 - in_top) * block_squares).reshape(-1),
            jnp.stack([own_squares + jnp.sum(head_grad * head_grad), loss_part]),
        ]
    )
    if on_torus:
        spare = -packed.shape[0] % 1024
        packed = sum_everywhere(
            jnp.pad(packed, (0, spare)).reshape(8, 128), dp_count, cls_count
        ).reshape(-1)
    else:
        packed = lax.psum(packed, ("dp", "cls"))
    loss = packed[4 * block_count + 1]
    grad_norm = jnp.sqrt(packed[4 * block_count])
    factor = CLIP_NORM / jnp.maximum(grad_norm, CLIP_NORM)
    sums = packed[: 4 * block_count].reshape(2, block_count, 2)
    mean_squares = jnp.where(dp_index < half_dp, sums[0], sums[1]) / (half_size * half_size)
    mean_squares = mean_squares * factor * factor
    scale = factor * lax.rsqrt(mean_squares + ROOT_EPS)
    wide_scale = jnp.repeat(SHAMPOO_RATE * scale, half_size, axis=1)
    new_blocks = enc_weights - direction * wide_scale[:, None, :]
    square_factor = 0.5 * factor * factor
    new_left = 0.5 * stats_left + square_factor * left_add
    new_right = 0.5 * stats_right + square_factor * right_add
    count = step.astype(jnp.float32)
    new_vec, new_vec_m, new_vec_v = adam_step(vectors, vector_rows * factor, vec_m, vec_v, count)
    new_head, new_head_m, new_head_v = adam_step(
        head_weights, head_grad * factor, head_m, head_v, count
    )
    return (
        loss,
        grad_norm,
        new_blocks,
        block_rows * factor,
        new_left,
        new_right,
        new_vec,
        new_vec_m,
        new_vec_v,
        new_head,
        new_head_m,
        new_head_v,
    )


def solution(mesh):
    return jax.shard_map(
        on_device,
        mesh=mesh,
        in_specs=(
            P(("dp", "cls"), None),
            P(("dp", "cls"), None),
            P(("dp", "cls"), None),
            P("dp", None),
            P(),
            P(),
            P(None, "dp", None),
            P(None, "dp", None),
            P(None, "dp", None),
            P(None, "dp", None),
            P(None, "dp", None),
            P("dp", "cls"),
            P("dp", "cls"),
            P("dp", "cls"),
            P(None, "dp"),
            P(None, "dp"),
            P(None, "dp"),
        ),
        out_specs=(
            P(),
            P(),
            P(None, "dp", None),
            P(None, "dp", None),
            P(None, "dp", None),
            P(None, "dp", None),
            P(None, "dp"),
            P(None, "dp"),
            P(None, "dp"),
            P("dp", "cls"),
            P("dp", "cls"),
            P("dp", "cls"),
        ),
        check_vma=False,
    )
```

```python
import functools

import jax
import jax.numpy as jnp
from jax import lax
from jax.experimental import pallas as pl
from jax.experimental.pallas import tpu as pltpu
from jax.sharding import PartitionSpec as P

HEADS = 12
HEAD = 64
LABELS_REAL = 21843
IMAGE_MAX = 196
QTILE = 256
PAIR = 2 * HEAD
ROWS = 256
HIDDEN_TILE = 384
MESH = pl.DeviceIdType.MESH
CODE_TOP = 32766.0
CODE_FLOOR = 1e-33
PIECE = 48
SPAN = 48
SHARES = 8
IMG_PACK = 8


FULL_PRECISION = lax.Precision.HIGHEST
NORM_EPS = 1e-06
CLIP_NORM = 1.0
ADAM_RATE = 0.02
SHAMPOO_RATE = 0.01
BETA_FIRST = 0.9
BETA_SECOND = 0.999
ADAM_EPS = 1e-08
WEIGHT_DECAY = 0.1
ROOT_EPS = 1e-06


def norm_rows(values, gain, shift):
    centred = values - jnp.mean(values, -1, keepdims=True)
    spread = jnp.mean(centred * centred, -1, keepdims=True)
    return centred * lax.rsqrt(spread + NORM_EPS) * gain + shift


def pool_rows(output, gain, shift, pack_ids, pack_keep):
    final = norm_rows(output, gain, shift)
    member = (
        (pack_ids[None, :] == jnp.arange(IMG_PACK)[:, None]) & (pack_keep[None, :] == 1)
    ).astype(jnp.float32)
    counted = jnp.maximum(jnp.sum(member, 1), 1.0)
    return jnp.dot(member, final, precision=FULL_PRECISION) / counted[:, None]


def key_window(tile, length):
    reach = -(-(IMAGE_MAX - 1) // 128) * 128
    low = max(0, tile * QTILE - reach)
    high = min(length, (tile + 1) * QTILE + reach)
    return low, high


def attention_forward_kernel(qids_ref, kcodes_ref, q_ref, k_ref, v_ref, out_ref, bias_ref):
    length = q_ref.shape[0]
    lane = lax.broadcasted_iota(jnp.int32, (QTILE, PAIR), 1)

    @pl.when(pl.program_id(0) == 0)
    def _():
        for tile in range(length // QTILE):
            low, high = key_window(tile, length)
            shape = (QTILE, high - low)
            rows = lax.broadcasted_iota(jnp.int32, shape, 0) + tile * QTILE
            cols = lax.broadcasted_iota(jnp.int32, shape, 1) + low
            same = qids_ref[tile * QTILE : (tile + 1) * QTILE, :] == kcodes_ref[:, low:high]
            bias_ref[tile, :, : high - low] = jnp.where(same | (rows == cols), 0.0, -1e30)

    for tile in range(length // QTILE):
        low, high = key_window(tile, length)
        rows = pl.ds(tile * QTILE, QTILE)
        queries = q_ref[rows, :] * jnp.bfloat16(HEAD ** (-0.5))
        keys = k_ref[low:high, :]
        values = v_ref[low:high, :]
        halves = []
        for head in range(2):
            mine = (lane >= head * HEAD) & (lane < (head + 1) * HEAD)
            picked = jnp.where(mine, queries, jnp.zeros_like(queries))
            scores = lax.dot_general(
                picked, keys, (((1,), (1,)), ((), ())), preferred_element_type=jnp.float32
            )
            scores = scores + bias_ref[tile, :, : high - low]
            top = jnp.max(scores, -1, keepdims=True)
            weights = jnp.exp(scores - top)
            probs = weights * (1.0 / jnp.sum(weights, -1, keepdims=True))
            halves.append(
                jnp.dot(probs.astype(jnp.bfloat16), values, preferred_element_type=jnp.float32)
            )
        out_ref[rows, :] = jnp.where(lane < HEAD, halves[0], halves[1]).astype(jnp.bfloat16)


def attention_backward_kernel(
    qids_ref, kcodes_ref, q_ref, k_ref, v_ref, do_ref, out_ref, bias_ref, dk_ref, dv_ref
):
    length = q_ref.shape[0]
    lane = lax.broadcasted_iota(jnp.int32, (QTILE, PAIR), 1)
    scale = jnp.bfloat16(HEAD ** (-0.5))

    @pl.when(pl.program_id(0) == 0)
    def _():
        for tile in range(length // QTILE):
            low, high = key_window(tile, length)
            shape = (high - low, QTILE)
            rows = lax.broadcasted_iota(jnp.int32, shape, 0) + low
            cols = lax.broadcasted_iota(jnp.int32, shape, 1) + tile * QTILE
            same = kcodes_ref[low:high, :] == qids_ref[:, tile * QTILE : (tile + 1) * QTILE]
            bias_ref[tile, : high - low, :] = jnp.where(same | (rows == cols), 0.0, -1e30)

    dk_ref[...] = jnp.zeros_like(dk_ref)
    dv_ref[...] = jnp.zeros_like(dv_ref)
    for tile in range(length // QTILE):
        low, high = key_window(tile, length)
        rows = pl.ds(tile * QTILE, QTILE)
        window = pl.ds(low, high - low)
        queries = q_ref[rows, :] * scale
        keys = k_ref[window, :]
        values = v_ref[window, :]
        grads = do_ref[rows, :]
        halves = []
        for head in range(2):
            mine = (lane >= head * HEAD) & (lane < (head + 1) * HEAD)
            picked = jnp.where(mine, queries, jnp.zeros_like(queries))
            picked_grads = jnp.where(mine, grads, jnp.zeros_like(grads))
            scores = lax.dot_general(
                keys, picked, (((1,), (1,)), ((), ())), preferred_element_type=jnp.float32
            )
            scores = scores + bias_ref[tile, : high - low, :]
            top = jnp.max(scores, 0, keepdims=True)
            weights = jnp.exp(scores - top)
            probs = weights * (1.0 / jnp.sum(weights, 0, keepdims=True))
            grad_probs = lax.dot_general(
                values, picked_grads, (((1,), (1,)), ((), ())), preferred_element_type=jnp.float32
            )
            inner = jnp.sum(probs * grad_probs, 0, keepdims=True)
            grad_scores = (probs * (grad_probs - inner)).astype(jnp.bfloat16)
            dv_ref[window, :] += jnp.dot(
                probs.astype(jnp.bfloat16), picked_grads, preferred_element_type=jnp.float32
            )
            dk_ref[window, :] += jnp.dot(
                grad_scores, picked, preferred_element_type=jnp.float32
            )
            halves.append(
                lax.dot_general(
                    grad_scores,
                    keys,
                    (((0,), (0,)), ((), ())),
                    preferred_element_type=jnp.float32,
                )
            )
        grad_queries = jnp.where(lane < HEAD, halves[0], halves[1]) * HEAD ** (-0.5)
        out_ref[0, rows, :] = grad_queries.astype(jnp.bfloat16)
    out_ref[1] = dk_ref[...].astype(jnp.bfloat16)
    out_ref[2] = dv_ref[...].astype(jnp.bfloat16)


def pair_spec(length, part=None):
    if part is None:
        return pl.BlockSpec((length, PAIR), lambda pair: (0, pair))
    return pl.BlockSpec((None, length, PAIR), lambda pair: (part, 0, pair))


def whole_spec(shape):
    return pl.BlockSpec(shape, lambda pair: (0,) * len(shape))


def attention_forward(qkv_rows, pack_ids, key_codes):
    _, length, width = qkv_rows.shape
    tiles = length // QTILE
    window = max(high - low for low, high in (key_window(t, length) for t in range(tiles)))
    return pl.pallas_call(
        attention_forward_kernel,
        grid=(width // PAIR,),
        out_shape=jax.ShapeDtypeStruct((length, width), jnp.bfloat16),
        in_specs=[whole_spec((length, 1)), whole_spec((1, length))]
        + [pair_spec(length, part) for part in range(3)],
        out_specs=pair_spec(length),
        scratch_shapes=[pltpu.VMEM((tiles, QTILE, window), jnp.float32)],
        compiler_params=pltpu.CompilerParams(vmem_limit_bytes=40 << 20),
        name="attention_forward",
    )(pack_ids[:, None], key_codes[None, :], qkv_rows, qkv_rows, qkv_rows)


def attention_backward(qkv_rows, pack_ids, key_codes, grad_attended):
    _, length, width = qkv_rows.shape
    tiles = length // QTILE
    window = max(high - low for low, high in (key_window(t, length) for t in range(tiles)))
    return pl.pallas_call(
        attention_backward_kernel,
        grid=(width // PAIR,),
        out_shape=jax.ShapeDtypeStruct((3, length, width), jnp.bfloat16),
        in_specs=[whole_spec((1, length)), whole_spec((length, 1))]
        + [pair_spec(length, part) for part in range(3)]
        + [pair_spec(length)],
        out_specs=pl.BlockSpec((3, length, PAIR), lambda pair: (0, 0, pair)),
        scratch_shapes=[
            pltpu.VMEM((tiles, window, QTILE), jnp.float32),
            pltpu.VMEM((length, PAIR), jnp.float32),
            pltpu.VMEM((length, PAIR), jnp.float32),
        ],
        compiler_params=pltpu.CompilerParams(vmem_limit_bytes=40 << 20),
        name="attention_backward",
    )(pack_ids[None, :], key_codes[:, None], qkv_rows, qkv_rows, qkv_rows, grad_attended)


def mlp_forward_kernel(x_ref, up_ref, bias_ref, down_ref, units_ref, slope_ref, out_ref):
    first = pl.program_id(0) == 0

    @pl.when(first)
    def _():
        out_ref[...] = jnp.zeros_like(out_ref)

    for start in range(0, x_ref.shape[0], ROWS):
        rows = pl.ds(start, ROWS)
        pre = jnp.dot(x_ref[rows, :], up_ref[...], preferred_element_type=jnp.float32)
        pre = pre + bias_ref[...]
        half = 0.5 + 0.5 * lax.erf(pre * 0.7071067811865476)
        bell = jnp.exp(-0.5 * pre * pre) * 0.3989422804014327
        units = (pre * half).astype(jnp.bfloat16)
        units_ref[rows, :] = units
        slope_ref[rows, :] = half + pre * bell
        out_ref[rows, :] += jnp.dot(units, down_ref[...], preferred_element_type=jnp.float32)


def mlp_backward_kernel(
    x_ref, dm_ref, up_ref, down_ref, units_ref, slope_ref,
    grad_up_ref, grad_down_ref, bias_ref, dx_ref, dpre_ref
):
    @pl.when(pl.program_id(0) == 0)
    def _():
        dx_ref[...] = jnp.zeros_like(dx_ref)

    total = jnp.zeros((1, HIDDEN_TILE), jnp.float32)
    for start in range(0, x_ref.shape[0], ROWS):
        rows = pl.ds(start, ROWS)
        units_back = lax.dot_general(
            dm_ref[rows, :], down_ref[...], (((1,), (1,)), ((), ())),
            preferred_element_type=jnp.float32,
        )
        grad_pre = (units_back * slope_ref[rows, :]).astype(jnp.bfloat16)
        dpre_ref[rows, :] = grad_pre
        total = total + jnp.sum(grad_pre.astype(jnp.float32), 0, keepdims=True)
        dx_ref[rows, :] += lax.dot_general(
            grad_pre, up_ref[...], (((1,), (1,)), ((), ())), preferred_element_type=jnp.float32
        )
    bias_ref[...] = total
    over_rows = (((0,), (0,)), ((), ()))
    grad_down_ref[...] = lax.dot_general(
        units_ref[...], dm_ref[...], over_rows, preferred_element_type=jnp.float32
    )
    grad_up_ref[...] = lax.dot_general(
        x_ref[...], dpre_ref[...], over_rows, preferred_element_type=jnp.float32
    )


def mlp_specs(length, width, up_count):
    split = width // HIDDEN_TILE
    resident = pl.BlockSpec((length, width), lambda t: (0, 0))
    up = pl.BlockSpec((None, width, HIDDEN_TILE), lambda t: (5 + t // split, 0, t % split))
    down = pl.BlockSpec(
        (None, HIDDEN_TILE, width), lambda t: (5 + up_count + t // split, t % split, 0)
    )
    hidden = pl.BlockSpec((length, HIDDEN_TILE), lambda t: (0, t))
    bias = pl.BlockSpec((1, HIDDEN_TILE), lambda t: (0, t))
    return split, resident, up, down, hidden, bias


def mlp_forward(rows, blocks, up_bias):
    length, width = rows.shape
    up_count = (blocks.shape[0] - 5) // 2
    split, resident, up, down, hidden, bias = mlp_specs(length, width, up_count)
    hidden_size = up_count * width
    return pl.pallas_call(
        mlp_forward_kernel,
        grid=(up_count * split,),
        out_shape=(
            jax.ShapeDtypeStruct((length, hidden_size), jnp.bfloat16),
            jax.ShapeDtypeStruct((length, hidden_size), jnp.float32),
            jax.ShapeDtypeStruct((length, width), jnp.float32),
        ),
        in_specs=[resident, up, bias, down],
        out_specs=(hidden, hidden, resident),
        compiler_params=pltpu.CompilerParams(vmem_limit_bytes=48 << 20),
        name="mlp_forward",
    )(rows, blocks, up_bias.reshape(1, hidden_size), blocks)


def mlp_backward(rows, grad_branch, blocks, units, slopes):
    length, width = rows.shape
    up_count = (blocks.shape[0] - 5) // 2
    split, resident, up, down, hidden, bias = mlp_specs(length, width, up_count)
    hidden_size = up_count * width
    return pl.pallas_call(
        mlp_backward_kernel,
        grid=(up_count * split,),
        out_shape=(
            jax.ShapeDtypeStruct((up_count, width, width), jnp.float32),
            jax.ShapeDtypeStruct((up_count, width, width), jnp.float32),
            jax.ShapeDtypeStruct((1, hidden_size), jnp.float32),
            jax.ShapeDtypeStruct((length, width), jnp.float32),
        ),
        in_specs=[resident, resident, up, down, hidden, hidden],
        out_specs=(
            pl.BlockSpec((None, width, HIDDEN_TILE), lambda t: (t // split, 0, t % split)),
            pl.BlockSpec((None, HIDDEN_TILE, width), lambda t: (t // split, t % split, 0)),
            bias,
            resident,
        ),
        scratch_shapes=[pltpu.VMEM((length, HIDDEN_TILE), jnp.bfloat16)],
        compiler_params=pltpu.CompilerParams(vmem_limit_bytes=48 << 20),
        name="mlp_backward",
    )(rows, grad_branch, blocks, blocks, units, slopes)


def layer_forward(blocks, vec_all, patch, pack_ids, key_codes):
    up_count = (blocks.shape[0] - 5) // 2
    embedded = jnp.dot(patch, blocks[0], preferred_element_type=jnp.float32) + vec_all[0]
    normed_one = norm_rows(embedded, vec_all[1], vec_all[2]).astype(jnp.bfloat16)
    qkv_rows = jnp.einsum(
        "td,kde->kte", normed_one, blocks[1:4], preferred_element_type=jnp.float32
    )
    qkv_bias = jnp.stack([vec_all[3], jnp.zeros_like(vec_all[3]), vec_all[4]])
    qkv_rows = (qkv_rows + qkv_bias[:, None, :]).astype(jnp.bfloat16)
    attended = attention_forward(qkv_rows, pack_ids, key_codes)
    hidden = (
        embedded + jnp.dot(attended, blocks[4], preferred_element_type=jnp.float32) + vec_all[5]
    )
    normed_two = norm_rows(hidden, vec_all[6], vec_all[7]).astype(jnp.bfloat16)
    units, slopes, branch = mlp_forward(normed_two, blocks, vec_all[8 : 8 + up_count])
    output = hidden + branch + vec_all[8 + up_count]
    return (
        output,
        (embedded, normed_one, qkv_rows, attended, hidden, normed_two, slopes, units),
    )


def layer_backward(
    blocks, vec_all, patch, saved, pack_ids, key_codes, grad_output, grad_gain, grad_shift
):
    embedded, normed_one, qkv_rows, attended, hidden, normed_two, slopes, units = saved
    feature_dim = patch.shape[1]
    up_count = (blocks.shape[0] - 5) // 2
    grad_branch = grad_output.astype(jnp.bfloat16)
    grad_up, grad_down, up_sums, grad_normed_two = mlp_backward(
        normed_two, grad_branch, blocks, units, slopes
    )
    norm_two_back = jax.vjp(norm_rows, hidden, vec_all[6], vec_all[7])[1]
    grad_hidden_norm, grad_gain_two, grad_shift_two = norm_two_back(grad_normed_two)
    grad_hidden = grad_output + grad_hidden_norm
    grad_attn_out = grad_hidden.astype(jnp.bfloat16)
    grad_out_proj = jnp.einsum(
        "te,td->ed", attended, grad_attn_out, preferred_element_type=jnp.float32
    )
    grad_attended = jnp.einsum(
        "td,ed->te", grad_attn_out, blocks[4], preferred_element_type=jnp.float32
    ).astype(jnp.bfloat16)
    grad_qkv = attention_backward(qkv_rows, pack_ids, key_codes, grad_attended)
    grad_qkv_proj = jnp.einsum(
        "td,kte->kde", normed_one, grad_qkv, preferred_element_type=jnp.float32
    )
    grad_normed_one = jnp.einsum(
        "kte,kde->td", grad_qkv, blocks[1:4], preferred_element_type=jnp.float32
    )
    norm_one_back = jax.vjp(norm_rows, embedded, vec_all[1], vec_all[2])[1]
    grad_embed_norm, grad_gain_one, grad_shift_one = norm_one_back(grad_normed_one)
    grad_embedded = (grad_hidden + grad_embed_norm).astype(jnp.bfloat16)
    grad_patch = jnp.einsum("tp,td->pd", patch, grad_embedded, preferred_element_type=jnp.float32)
    grad_arrays = (grad_patch[None], grad_qkv_proj, grad_out_proj[None], grad_up, grad_down)
    bias_sums = jnp.stack(
        [
            jnp.sum(grad_embedded.astype(jnp.float32), 0),
            grad_gain_one,
            grad_shift_one,
            jnp.sum(grad_qkv[0].astype(jnp.float32), 0),
            jnp.sum(grad_qkv[2].astype(jnp.float32), 0),
            jnp.sum(grad_attn_out.astype(jnp.float32), 0),
            grad_gain_two,
            grad_shift_two,
        ]
    )
    up_sums = up_sums.reshape(up_count, feature_dim)
    tail_sums = jnp.stack([jnp.sum(grad_branch.astype(jnp.float32), 0), grad_gain, grad_shift])
    return (grad_arrays, jnp.concatenate([bias_sums, up_sums, tail_sums], 0))


def torus_place():
    dp, cls = lax.axis_index("dp"), lax.axis_index("cls")
    return dp // 2, dp % 2, cls // 2, cls % 2


def torus_device(z, y, x, core):
    return (z * 2 + y, x * 2 + core)


def encode(pieces, code_refs, scale_ref):
    top = None
    for piece in pieces:
        peak = jnp.max(jnp.abs(piece()), 0, keepdims=True)
        top = peak if top is None else jnp.maximum(top, peak)
    top = jnp.maximum(top, CODE_FLOOR)
    inverse = CODE_TOP / top
    for piece, code_ref in zip(pieces, code_refs):
        code_ref[...] = jnp.round(piece() * inverse).astype(jnp.int32).astype(jnp.int16)
    scale_ref[...] = top * (1.0 / CODE_TOP)


def decode(code, scale):
    return code.astype(jnp.int32).astype(jnp.float32) * scale


def reduce_kernel(counts, *refs):
    sources, refs = refs[: len(counts)], refs[len(counts) :]
    (vec_ref, codes_hbm, scales_hbm, vec_out_ref,
     acc, spare, kept, sent0, got0, sent1, got1, sent2, got2, sent3, got3, sent4, got4,
     ss0, gs0, ss1, gs1, ss2, gs2, ss3, gs3, ss4, gs4, codes, scales, vec_got,
     load_sem, out_sem, send_sem, recv_sem, send_scale_sem, recv_scale_sem,
     vec_send_sem, vec_recv_sem) = refs
    total = sum(counts)
    half, width = codes.shape[1], codes.shape[2]
    cols = width // 2
    z, y, x, core = torus_place()
    upper = z // 2
    inner = (z % 2) != upper
    mate_core = torus_device(z, y, x, 1 - core)
    mate_x = torus_device(z, y, 1 - x, core)
    mate_y = torus_device(z, 1 - y, x, core)
    mate_z = torus_device(z + 1 - 2 * (z % 2), y, x, core)
    mate_mid = torus_device(3 - z, y, x, core)
    mate_far = torus_device((z + 2) % 4, y, x, core)

    barrier = pltpu.get_barrier_semaphore()
    mates = (mate_core, mate_x, mate_y, mate_z, mate_mid, mate_far)
    for mate in mates:
        pl.semaphore_signal(barrier, inc=1, device_id=mate, device_id_type=MESH)
    pl.semaphore_wait(barrier, len(mates))

    own_cols = pl.ds(pl.multiple_of(core * cols, 128), cols)
    other_cols = pl.ds(pl.multiple_of((1 - core) * cols, 128), cols)

    def rows_at(start, size):
        return pl.ds(pl.multiple_of(start, PIECE), size)

    def loads(m, body):
        start = 0
        for source, count in zip(sources, counts):
            def one(source=source, start=start):
                pair = (
                    pltpu.make_async_copy(
                        source.at[m - start, :, own_cols], acc.at[m % 5], load_sem.at[m % 2, 0]
                    ),
                    pltpu.make_async_copy(
                        source.at[m - start, :, other_cols], spare.at[m % 2], load_sem.at[m % 2, 1]
                    ),
                )
                for copy in pair:
                    body(copy)

            pl.when((m >= start) & (m < start + count))(one)
            start += count

    def message(stage, m, source, scale_source, target, scale_target, mate):
        return (
            pltpu.make_async_remote_copy(
                src_ref=source, dst_ref=target,
                send_sem=send_sem.at[stage, m % 2], recv_sem=recv_sem.at[stage, m],
                device_id=mate, device_id_type=MESH,
            ),
            pltpu.make_async_remote_copy(
                src_ref=scale_source, dst_ref=scale_target,
                send_sem=send_scale_sem.at[stage, m % 2], recv_sem=recv_scale_sem.at[stage, m],
                device_id=mate, device_id_type=MESH,
            ),
        )

    def first(m):
        return message(0, m, sent0.at[m % 2], ss0.at[m % 2], got0.at[m], gs0.at[m], mate_core)

    def second(m, b):
        return message(
            1 + b, m, sent1.at[m % 2, b], ss1.at[m % 2, b], got1.at[m, b], gs1.at[m, b],
            mate_y if b else mate_x,
        )

    def third(m, b):
        return message(
            3 + b, m, sent2.at[m % 2, b], ss2.at[m % 2, b], got2.at[m, b], gs2.at[m, b],
            mate_x if b else mate_y,
        )

    def fourth(m):
        return message(5, m, sent3.at[m % 2], ss3.at[m % 2], got3.at[m], gs3.at[m], mate_z)

    def fifth(m):
        return message(6, m, sent4.at[m % 2], ss4.at[m % 2], got4.at[m], gs4.at[m], mate_mid)

    piece_a = 2 * x + y
    piece_b = 4 + 2 * y + x

    def spread(stage, m, piece, count, mate, columns=own_cols):
        rows = pl.ds(pl.multiple_of(piece * PIECE, PIECE), count * PIECE)
        block = codes.at[m, rows, columns]
        scale = scales.at[m, pl.ds(piece, count), :, columns]
        return message(stage, m, block, scale, block, scale, mate)

    def start(copies):
        for copy in copies:
            copy.start()

    def wait_send(copies):
        for copy in copies:
            copy.wait_send()

    def wait_recv(copies):
        for copy in copies:
            copy.wait_recv()

    def vec_copy(step, mate):
        return pltpu.make_async_remote_copy(
            src_ref=vec_got.at[step, 0], dst_ref=vec_got.at[step, 1],
            send_sem=vec_send_sem.at[step], recv_sem=vec_recv_sem.at[step],
            device_id=mate, device_id_type=MESH,
        )

    vec_mates = (mate_core, mate_x, mate_y, mate_z, mate_far)

    loads(jnp.int32(0), lambda copy: copy.start())
    vec_got[0, 0] = vec_ref[...]
    vec_copy(0, vec_mates[0]).start()

    def step(t, carry):
        for n in range(1, 6):
            @pl.when(t == n)
            def _(n=n):
                vec_copy(n - 1, vec_mates[n - 1]).wait()
                value = vec_got[n - 1, 0] + vec_got[n - 1, 1]
                if n < 5:
                    vec_got[n, 0] = value
                    vec_copy(n, vec_mates[n]).start()
                else:
                    vec_out_ref[...] = value

        @pl.when(t < total)
        def _():
            m = t
            loads(m, lambda copy: copy.wait())

            @pl.when(m + 1 < total)
            def _():
                loads(m + 1, lambda copy: copy.start())

            span = 2 * PIECE
            encode(
                [lambda r=r: spare[m % 2, r : r + span, :] for r in range(0, 2 * half, span)],
                [sent0.at[m % 2, r : r + span, :] for r in range(0, 2 * half, span)],
                ss0.at[m % 2],
            )
            start(first(m))

        @pl.when((t >= 1) & (t < total + 1))
        def _():
            m = t - 1
            copies = first(m)
            wait_send(copies)
            wait_recv(copies)
            slot = m % 5
            span = 2 * PIECE
            for r in range(0, 2 * half, span):
                acc[slot, r : r + span, :] += decode(got0[m, r : r + span, :], gs0[m])
            for b in range(2):
                other = (1 - y) if b else (1 - x)
                begins = [h * half + b * 4 * PIECE + other * span for h in range(2)]
                encode(
                    [lambda s=s: acc[slot, rows_at(s, span), :] for s in begins],
                    [sent1.at[m % 2, b, h] for h in range(2)],
                    ss1.at[m % 2, b],
                )
                start(second(m, b))

        @pl.when((t >= 2) & (t < total + 2))
        def _():
            m = t - 2
            slot = m % 5
            span = 2 * PIECE
            for b in range(2):
                copies = second(m, b)
                wait_send(copies)
                wait_recv(copies)
                mine = y if b else x
                other = (1 - x) if b else (1 - y)
                begins = [h * half + b * 4 * PIECE + mine * span for h in range(2)]
                for h, s in enumerate(begins):
                    acc[slot, rows_at(s, span), :] += decode(got1[m, b, h], gs1[m, b])
                encode(
                    [lambda s=s: acc[slot, rows_at(s + other * PIECE, PIECE), :] for s in begins],
                    [sent2.at[m % 2, b, h] for h in range(2)],
                    ss2.at[m % 2, b],
                )
                start(third(m, b))

        @pl.when((t >= 3) & (t < total + 3))
        def _():
            m = t - 3
            slot = m % 5
            for b in range(2):
                copies = third(m, b)
                wait_send(copies)
                wait_recv(copies)
                place = piece_b if b else piece_a
                for h in range(2):
                    kept[m % 3, h, b] = acc[
                        slot, rows_at(h * half + place * PIECE, PIECE), :
                    ] + decode(got2[m, b, h], gs2[m, b])

            @pl.when(jnp.logical_not(inner))
            def _():
                pairs = [(h, b) for h in range(2) for b in range(2)]
                encode(
                    [lambda h=h, b=b: kept[m % 3, h, b] for h, b in pairs],
                    [sent3.at[m % 2, h, b] for h, b in pairs],
                    ss3.at[m % 2],
                )
                start(fourth(m))

        @pl.when((t >= 4) & (t < total + 4))
        def _():
            m = t - 4
            copies = fourth(m)

            @pl.when(jnp.logical_not(inner))
            def _():
                wait_send(copies)

            @pl.when(inner)
            def _():
                wait_recv(copies)
                for h in range(2):
                    for b in range(2):
                        kept[m % 3, h, b] += decode(got3[m, h, b], gs3[m])
                encode(
                    [lambda b=b: kept[m % 3, 1 - upper, b] for b in range(2)],
                    [sent4.at[m % 2, b] for b in range(2)],
                    ss4.at[m % 2],
                )
                start(fifth(m))

        @pl.when((t >= 5) & (t < total + 5))
        def _():
            m = t - 5

            @pl.when(inner)
            def _():
                copies = fifth(m)
                wait_send(copies)
                wait_recv(copies)
                for b in range(2):
                    place = piece_b if b else piece_a
                    value = kept[m % 3, upper, b] + decode(got4[m, b], gs4[m])
                    encode(
                        [lambda value=value: value],
                        [codes.at[m, rows_at(place * PIECE, PIECE), own_cols]],
                        scales.at[m, place, :, own_cols],
                    )
                    start(spread(7 + b, m, place, 1, mate_z))

        @pl.when((t >= 6) & (t < total + 6))
        def _():
            m = t - 6
            for b in range(2):
                place = piece_b if b else piece_a
                copies = spread(7 + b, m, place, 1, mate_z)

                @pl.when(inner)
                def _(copies=copies):
                    wait_send(copies)

                @pl.when(jnp.logical_not(inner))
                def _(copies=copies):
                    wait_recv(copies)

                start(spread(9 + b, m, place, 1, mate_x if b else mate_y))

        @pl.when((t >= 7) & (t < total + 7))
        def _():
            m = t - 7
            for b in range(2):
                place = piece_b if b else piece_a
                theirs = (4 + 2 * y + 1 - x) if b else (2 * x + 1 - y)
                wait_send(spread(9 + b, m, place, 1, mate_x if b else mate_y))
                wait_recv(spread(9 + b, m, theirs, 1, mate_x if b else mate_y))
                begin = (4 + 2 * y) if b else 2 * x
                start(spread(11 + b, m, begin, 2, mate_y if b else mate_x))

        @pl.when((t >= 8) & (t < total + 8))
        def _():
            m = t - 8
            for b in range(2):
                begin = (4 + 2 * y) if b else 2 * x
                theirs = (4 + 2 * (1 - y)) if b else 2 * (1 - x)
                wait_send(spread(11 + b, m, begin, 2, mate_y if b else mate_x))
                wait_recv(spread(11 + b, m, theirs, 2, mate_y if b else mate_x))
            start(spread(13, m, 0, 8, mate_core))

        def outs(m):
            return (
                pltpu.make_async_copy(codes.at[m], codes_hbm.at[m], out_sem.at[m % 2, 0]),
                pltpu.make_async_copy(scales.at[m], scales_hbm.at[m], out_sem.at[m % 2, 1]),
            )

        @pl.when((t >= 9) & (t < total + 9))
        def _():
            m = t - 9
            wait_send(spread(13, m, 0, 8, mate_core))
            wait_recv(spread(13, m, 0, 8, mate_core, other_cols))
            start(outs(m))

        @pl.when((t >= 10) & (t < total + 10))
        def _():
            for copy in outs(t - 10):
                copy.wait()

        return carry

    lax.fori_loop(0, total + 10, step, 0)


def reduce_gradients(arrays, vec_sums):
    counts = tuple(array.shape[0] for array in arrays)
    total = sum(counts)
    width = arrays[0].shape[1]
    half, cols = width // 2, width // 2
    f32, i16 = jnp.float32, jnp.int16

    def pair(*shape):
        return [pltpu.VMEM((2,) + shape, i16), pltpu.VMEM((total,) + shape, i16)]

    def scale_pair(*shape):
        return [
            pltpu.VMEM((2,) + shape + (1, cols), f32),
            pltpu.VMEM((total,) + shape + (1, cols), f32),
        ]

    hbm = pl.BlockSpec(memory_space=pl.ANY)
    vmem = pl.BlockSpec(memory_space=pltpu.VMEM)
    return pl.pallas_call(
        functools.partial(reduce_kernel, counts),
        out_shape=(
            jax.ShapeDtypeStruct((total, half, width), i16),
            jax.ShapeDtypeStruct((total, half // PIECE, 1, width), f32),
            jax.ShapeDtypeStruct(vec_sums.shape, f32),
        ),
        in_specs=[hbm] * len(arrays) + [vmem],
        out_specs=(hbm, hbm, vmem),
        scratch_shapes=[
            pltpu.VMEM((5, width, cols), f32),
            pltpu.VMEM((2, width, cols), f32),
            pltpu.VMEM((3, 2, 2, PIECE, cols), f32),
        ]
        + pair(width, cols)
        + pair(2, 2, 2 * PIECE, cols)
        + pair(2, 2, PIECE, cols)
        + pair(2, 2, PIECE, cols)
        + pair(2, PIECE, cols)
        + scale_pair()
        + scale_pair(2)
        + scale_pair(2)
        + scale_pair()
        + scale_pair()
        + [
            pltpu.VMEM((total, half, width), i16),
            pltpu.VMEM((total, half // PIECE, 1, width), f32),
            pltpu.VMEM((5, 2) + vec_sums.shape, f32),
            pltpu.SemaphoreType.DMA((2, 2)),
            pltpu.SemaphoreType.DMA((2, 2)),
            pltpu.SemaphoreType.DMA((14, 2)),
            pltpu.SemaphoreType.DMA((14, total)),
            pltpu.SemaphoreType.DMA((14, 2)),
            pltpu.SemaphoreType.DMA((14, total)),
            pltpu.SemaphoreType.DMA((5,)),
            pltpu.SemaphoreType.DMA((5,)),
        ],
        compiler_params=pltpu.CompilerParams(
            collective_id=1, has_side_effects=True, vmem_limit_bytes=60 << 20
        ),
        name="reduce_gradients",
    )(*arrays, vec_sums)


def split_float(values):
    high = values.astype(jnp.bfloat16)
    return high, (values - high.astype(jnp.float32)).astype(jnp.bfloat16)


def stacked_dot(lefts, right, contract_last):
    rows = lefts[0].shape[0]
    left = jnp.concatenate(lefts, 0) if len(lefts) > 1 else lefts[0]
    dims = (((1,), (1 if contract_last else 0,)), ((), ()))
    out = lax.dot_general(left, right, dims, preferred_element_type=jnp.float32)
    return [out[n * rows : (n + 1) * rows] for n in range(len(lefts))]


def precondition_kernel(
    own_count, codes_ref, scales_ref, left_ref, right_ref,
    left_out, right_out, step_out, own_out, squares_ref, high_ref, low_ref
):
    half, width = codes_ref.shape
    rows = left_ref.shape[0]
    own = lax.rem(lax.axis_index("dp"), own_count) * rows
    own_rows = pl.ds(pl.multiple_of(own, PIECE), rows)
    for piece in range(half // PIECE):
        part = slice(piece * PIECE, (piece + 1) * PIECE)
        value = codes_ref[part, :].astype(jnp.int32).astype(jnp.float32) * scales_ref[piece]
        high_ref[part, :], low_ref[part, :] = split_float(value)
    own_value = high_ref[own_rows, :].astype(jnp.float32) + low_ref[own_rows, :].astype(jnp.float32)
    own_out[...] = own_value
    squares_ref[0:1, :] = jnp.sum(own_value * own_value, 0, keepdims=True)
    picks = (
        lax.broadcasted_iota(jnp.int32, (rows, half), 1)
        == lax.broadcasted_iota(jnp.int32, (rows, half), 0) + own
    ).astype(jnp.float32).astype(jnp.bfloat16)
    for quad in range(2):
        cols = slice(quad * half, (quad + 1) * half)
        high, low = high_ref[:, cols], low_ref[:, cols]
        mine_high, mine_low = high_ref[own_rows, cols], low_ref[own_rows, cols]
        hh, lh, turned_high = stacked_dot([mine_high, mine_low, picks], high, True)
        hl, turned_low = stacked_dot([mine_high, picks], low, True)
        left_out[:, cols] = hh + (lh + hl)
        turned_high = turned_high.astype(jnp.bfloat16)
        turned_low = turned_low.astype(jnp.bfloat16)
        root_high, root_low = split_float(left_ref[:, cols])
        thh, tlh, rhh, rlh = stacked_dot([turned_high, turned_low, root_high, root_low], high, False)
        thl, rhl = stacked_dot([turned_high, root_high], low, False)
        right_out[:, cols] = thh + (tlh + thl)
        half_step = rhh + (rlh + rhl)
        step_high, step_low = split_float(half_step)
        right_high, right_low = split_float(right_ref[:, cols])
        shh, slh = stacked_dot([step_high, step_low], right_high, False)
        (shl,) = stacked_dot([step_high], right_low, False)
        direction = shh + (slh + shl)
        step_out[:, cols] = direction
        squares_ref[1:2, cols] = jnp.sum(direction * direction, 0, keepdims=True)


def precondition(codes, scales, root_left, right_half, own_count):
    count, half, width = codes.shape
    rows = root_left.shape[1]

    def spec(*shape):
        return pl.BlockSpec((None,) + shape, lambda b: (b,) + (0,) * len(shape))

    mine = jax.ShapeDtypeStruct((count, rows, width), jnp.float32)
    return pl.pallas_call(
        functools.partial(precondition_kernel, own_count),
        grid=(count,),
        out_shape=(mine, mine, mine, mine, jax.ShapeDtypeStruct((count, 2, width), jnp.float32)),
        in_specs=[
            spec(half, width),
            spec(half // PIECE, 1, width),
            spec(rows, width),
            spec(half, width),
        ],
        out_specs=(spec(rows, width),) * 4 + (spec(2, width),),
        scratch_shapes=[
            pltpu.VMEM((half, width), jnp.bfloat16),
            pltpu.VMEM((half, width), jnp.bfloat16),
        ],
        compiler_params=pltpu.CompilerParams(vmem_limit_bytes=32 << 20),
        name="precondition",
    )(codes, scales, root_left, right_half)


def sum_kernel(dp_count, cls_count, in_ref, out_ref, slots, send_sem, recv_sem):
    dp, cls = lax.axis_index("dp"), lax.axis_index("cls")
    total = dp_count * cls_count
    me = dp * cls_count + cls
    barrier = pltpu.get_barrier_semaphore()

    def mate(n):
        other = lax.rem(me + n, total)
        return (other // cls_count, lax.rem(other, cls_count))

    for n in range(1, total):
        pl.semaphore_signal(barrier, inc=1, device_id=mate(n), device_id_type=MESH)
    pl.semaphore_wait(barrier, total - 1)

    def copy(n):
        return pltpu.make_async_remote_copy(
            src_ref=in_ref, dst_ref=slots.at[me],
            send_sem=send_sem.at[n], recv_sem=recv_sem.at[me],
            device_id=mate(n), device_id_type=MESH,
        )

    def arrival(n):
        source = lax.rem(me + n, total)
        return pltpu.make_async_remote_copy(
            src_ref=in_ref, dst_ref=slots.at[source],
            send_sem=send_sem.at[n], recv_sem=recv_sem.at[source],
            device_id=mate(n), device_id_type=MESH,
        )

    for n in range(1, total):
        copy(n).start()
    slots[me] = in_ref[...]
    for n in range(1, total):
        copy(n).wait_send()
        arrival(n).wait_recv()
    value = slots[0]
    for n in range(1, total):
        value = value + slots[n]
    out_ref[...] = value


def sum_everywhere(values, dp_count, cls_count):
    total = dp_count * cls_count
    vmem = pl.BlockSpec(memory_space=pltpu.VMEM)
    return pl.pallas_call(
        functools.partial(sum_kernel, dp_count, cls_count),
        out_shape=jax.ShapeDtypeStruct(values.shape, jnp.float32),
        in_specs=[vmem],
        out_specs=vmem,
        scratch_shapes=[
            pltpu.VMEM((total,) + values.shape, jnp.float32),
            pltpu.SemaphoreType.DMA((total,)),
            pltpu.SemaphoreType.DMA((total,)),
        ],
        compiler_params=pltpu.CompilerParams(collective_id=2, has_side_effects=True),
        name="sum_everywhere",
    )(values)


def gather_kernel(own_ref, vec_ref, out_ref, vec_out_ref, send_sem, recv_sem, copy_sem, vec_send, vec_recv):
    count, rows, width = own_ref.shape
    cols = width // 2
    z, y, x, core = torus_place()
    me = z * 2 + y
    mate_core = torus_device(z, y, x, 1 - core)
    mate_x = torus_device(z, y, 1 - x, core)
    mate_y = torus_device(z, 1 - y, x, core)
    mate_up = torus_device(jnp.minimum(z + 1, 3), y, x, core)
    mate_down = torus_device(jnp.maximum(z - 1, 0), y, x, core)
    has_up = z < 3
    has_down = z > 0

    def column_mate(n):
        other = lax.rem(me + n, SHARES)
        return torus_device(other // 2, lax.rem(other, 2), x, core)

    barrier = pltpu.get_barrier_semaphore()
    for mate in [mate_core, mate_x] + [column_mate(n) for n in range(1, SHARES)]:
        pl.semaphore_signal(barrier, inc=1, device_id=mate, device_id_type=MESH)
    pl.semaphore_wait(barrier, SHARES + 1)

    own_cols = pl.ds(pl.multiple_of(core * cols, 128), cols)
    other_cols = pl.ds(pl.multiple_of((1 - core) * cols, 128), cols)

    def vec_copy(n, slot):
        return pltpu.make_async_remote_copy(
            src_ref=vec_ref, dst_ref=vec_out_ref.at[slot],
            send_sem=vec_send.at[n], recv_sem=vec_recv.at[slot],
            device_id=column_mate(n), device_id_type=MESH,
        )

    for n in range(1, SHARES):
        vec_copy(n, me).start()
    vec_out_ref[me] = vec_ref[...]

    def share(m, zz, yy, start, size, columns=own_cols):
        begin = (zz * 2 + yy) * rows + start
        return out_ref.at[m, pl.ds(pl.multiple_of(begin, 16), size), columns]

    def copy(stage, m, source, target, mate):
        return pltpu.make_async_remote_copy(
            src_ref=source, dst_ref=target,
            send_sem=send_sem.at[stage, m % 2], recv_sem=recv_sem.at[stage, m],
            device_id=mate, device_id_type=MESH,
        )

    span_start = x * (rows - SPAN)
    lack = rows - SPAN
    lack_mine = x * SPAN
    lack_theirs = (1 - x) * SPAN

    def local(m):
        return pltpu.make_async_copy(
            own_ref.at[m, :, own_cols], share(m, z, y, 0, rows), copy_sem.at[m % 2]
        )

    def chain(m, turn, upward):
        origin = z - (turn - 1) if upward else z + (turn - 1)
        stage = (turn - 1) * 2 + (0 if upward else 1)
        target = share(m, origin, y, span_start, SPAN)
        if turn == 1:
            source = own_ref.at[m, pl.ds(pl.multiple_of(span_start, 16), SPAN), own_cols]
        else:
            source = target
        return copy(stage, m, source, target, mate_up if upward else mate_down)

    def chain_sends(turn, upward):
        if upward:
            return has_up & (z - (turn - 1) >= 0)
        return has_down & (z + (turn - 1) <= 3)

    def chain_comes(turn, upward):
        return (z - turn >= 0) if upward else (z + turn <= 3)

    def arriving(m, turn, upward):
        origin = z - turn if upward else z + turn
        stage = (turn - 1) * 2 + (0 if upward else 1)
        target = share(m, origin, y, span_start, SPAN)
        return copy(stage, m, target, target, mate_up)

    def patch_out(m, n):
        zz = lax.rem(z + n, 4)
        block = share(m, zz, y, lack_mine, lack)
        return copy(5 + n, m, block, block, mate_x)

    def patch_in(m, n):
        zz = lax.rem(z + n, 4)
        block = share(m, zz, y, lack_theirs, lack)
        return copy(5 + n, m, block, block, mate_x)

    def cross(m, n, yy, stage, plane, mate):
        block = share(m, plane * 2 + n, yy, 0, rows)
        return copy(stage + n, m, block, block, mate)

    def swap(m, columns):
        block = out_ref.at[m, :, columns]
        return copy(13, m, block, block, mate_core)

    def step(t, carry):
        @pl.when(t < count)
        def _():
            local(t).start()
            for upward in (True, False):
                @pl.when(chain_sends(1, upward))
                def _(upward=upward):
                    chain(t, 1, upward).start()

        for turn in (2, 3):
            @pl.when((t >= turn - 1) & (t < count + turn - 1))
            def _(turn=turn):
                m = t - (turn - 1)
                if turn == 2:
                    local(m).wait()
                for upward in (True, False):
                    @pl.when(chain_sends(turn - 1, upward))
                    def _(upward=upward):
                        chain(m, turn - 1, upward).wait_send()

                    @pl.when(chain_comes(turn - 1, upward))
                    def _(upward=upward):
                        arriving(m, turn - 1, upward).wait_recv()

                    @pl.when(chain_sends(turn, upward))
                    def _(upward=upward):
                        chain(m, turn, upward).start()

        @pl.when((t >= 3) & (t < count + 3))
        def _():
            m = t - 3
            for upward in (True, False):
                @pl.when(chain_sends(3, upward))
                def _(upward=upward):
                    chain(m, 3, upward).wait_send()

                @pl.when(chain_comes(3, upward))
                def _(upward=upward):
                    arriving(m, 3, upward).wait_recv()
            if lack:
                for n in range(1, 4):
                    patch_out(m, n).start()

        @pl.when((t >= 4) & (t < count + 4))
        def _():
            m = t - 4
            if lack:
                for n in range(1, 4):
                    patch_out(m, n).wait_send()
                    patch_in(m, n).wait_recv()
            for n in range(2):
                cross(m, n, y, 9, x, mate_y).start()

        @pl.when((t >= 5) & (t < count + 5))
        def _():
            m = t - 5
            for n in range(2):
                cross(m, n, y, 9, x, mate_y).wait_send()
                cross(m, n, 1 - y, 9, x, mate_y).wait_recv()
                cross(m, n, 1 - y, 11, x, mate_x).start()

        @pl.when((t >= 6) & (t < count + 6))
        def _():
            m = t - 6
            for n in range(2):
                cross(m, n, 1 - y, 11, x, mate_x).wait_send()
                cross(m, n, 1 - y, 11, 1 - x, mate_x).wait_recv()
            swap(m, own_cols).start()

        @pl.when((t >= 7) & (t < count + 7))
        def _():
            m = t - 7
            swap(m, own_cols).wait_send()
            swap(m, other_cols).wait_recv()

        return carry

    lax.fori_loop(0, count + 7, step, 0)
    for n in range(1, SHARES):
        vec_copy(n, me).wait_send()
        vec_copy(n, lax.rem(me + n, SHARES)).wait_recv()


def gather_weights(own, vec):
    count, rows, width = own.shape
    hbm = pl.BlockSpec(memory_space=pl.ANY)
    vmem = pl.BlockSpec(memory_space=pltpu.VMEM)
    return pl.pallas_call(
        gather_kernel,
        out_shape=(
            jax.ShapeDtypeStruct((count, SHARES * rows, width), own.dtype),
            jax.ShapeDtypeStruct((SHARES,) + vec.shape, vec.dtype),
        ),
        in_specs=[vmem, vmem],
        out_specs=(hbm, vmem),
        scratch_shapes=[
            pltpu.SemaphoreType.DMA((14, 2)),
            pltpu.SemaphoreType.DMA((14, count)),
            pltpu.SemaphoreType.DMA((2,)),
            pltpu.SemaphoreType.DMA((SHARES,)),
            pltpu.SemaphoreType.DMA((SHARES,)),
        ],
        compiler_params=pltpu.CompilerParams(
            collective_id=3, has_side_effects=True, vmem_limit_bytes=32 << 20
        ),
        name="gather_weights",
    )(own, vec)


def adam_step(weight, grad, first, second, count):
    first = BETA_FIRST * first + (1.0 - BETA_FIRST) * grad
    second = BETA_SECOND * second + (1.0 - BETA_SECOND) * grad * grad
    fix_first = 1.0 - jnp.power(BETA_FIRST, count)
    fix_second = 1.0 - jnp.power(BETA_SECOND, count)
    update = first / fix_first / (jnp.sqrt(second / fix_second) + ADAM_EPS) + WEIGHT_DECAY * weight
    return (weight - ADAM_RATE * update, first, second)


def split_halves(values, half_size):
    block_count, row_count, feature_dim = values.shape
    return values.reshape(block_count, row_count, 2, half_size)


def reduced_half(values, half_groups):
    part = lax.psum_scatter(values, ("dp", "cls"), scatter_dimension=1, tiled=True)
    return lax.all_gather(part, ("dp", "cls"), axis=1, tiled=True, axis_index_groups=half_groups)


def preconditioned_rows(grad_half, root_left, right_half, own_start):
    count, row_count, width = root_left.shape
    half_size = width // 2
    block_rows = lax.dynamic_slice_in_dim(grad_half, own_start, row_count, 1)
    grad_quads = split_halves(grad_half, half_size)
    rows_quads = split_halves(block_rows, half_size)
    cols_quads = lax.dynamic_slice_in_dim(grad_quads, own_start, row_count, 3)
    precise = FULL_PRECISION
    left_add = jnp.einsum("brjk,bljk->brjl", rows_quads, grad_quads, precision=precise)
    right_add = jnp.einsum("bkja,bkjm->bajm", cols_quads, grad_quads, precision=precise)
    direction = jnp.einsum(
        "brjk,bkjm->brjm", split_halves(root_left, half_size), grad_quads, precision=precise
    )
    direction = jnp.einsum(
        "brjk,bkjm->brjm", direction, split_halves(right_half, half_size), precision=precise
    )
    flat = (count, row_count, width)
    return left_add.reshape(flat), right_add.reshape(flat), direction.reshape(flat), block_rows


def on_device(
    patches,
    image_ids,
    keep,
    labels,
    owner,
    step,
    enc_weights,
    stats_left,
    stats_right,
    root_left,
    root_right,
    head_weights,
    head_m,
    head_v,
    vectors,
    vec_m,
    vec_v,
):
    dp_count = lax.axis_size("dp")
    cls_count = lax.axis_size("cls")
    dp_index = lax.axis_index("dp")
    cls_index = lax.axis_index("cls")
    block_count, row_count, feature_dim = enc_weights.shape
    up_count = (block_count - 5) // 2
    half_size = feature_dim // 2
    part_rows = row_count // cls_count
    half_dp = dp_count // 2
    half_group = half_dp * cls_count
    half_groups = [
        list(range(half_group)),
        list(range(half_group, 2 * half_group)),
    ]

    def my_part(values):
        return lax.dynamic_slice_in_dim(values, cls_index * part_rows, part_rows, 1)

    on_torus = dp_count == 8 and cls_count == 4
    if on_torus:
        vec_block = jnp.pad(vectors, ((0, -vectors.shape[0] % 8), (0, -row_count % 128)))
        blocks, vec_blocks = gather_weights(enc_weights.astype(jnp.bfloat16), vec_block)
        vec_low = jnp.transpose(vec_blocks[:, : vectors.shape[0], :row_count], (1, 0, 2))
        vec_all = lax.reduce_precision(vec_low.reshape(vectors.shape[0], feature_dim), 8, 7)
    else:
        blocks = lax.all_gather(
            my_part(enc_weights.astype(jnp.bfloat16)), ("dp", "cls"), axis=1, tiled=True
        )
        vec_low = lax.all_gather(vectors.astype(jnp.bfloat16), "dp", axis=1, tiled=True)
        vec_all = vec_low.astype(jnp.float32)
    head_low = lax.all_gather(head_weights.astype(jnp.bfloat16), "dp", axis=0, tiled=True)
    right_half = lax.all_gather(
        my_part(root_right), ("dp", "cls"), axis=1, tiled=True, axis_index_groups=half_groups
    )
    final_gain = vec_all[9 + up_count]
    final_shift = vec_all[10 + up_count]
    pack_ids, pack_keep = image_ids[0], keep[0]
    key_codes = jnp.where(pack_keep == 1, pack_ids, -1)

    output, saved = layer_forward(blocks, vec_all, patches, pack_ids, key_codes)
    pooled = pool_rows(output, final_gain, final_shift, pack_ids, pack_keep)
    group = lax.all_gather(pooled.astype(jnp.bfloat16), "cls", axis=0, tiled=True)
    logits = jnp.dot(group, head_low, preferred_element_type=jnp.float32)
    class_dev = head_low.shape[1]
    class_ids = cls_index * class_dev + jnp.arange(class_dev)
    valid = class_ids[None, :] < LABELS_REAL
    target = jnp.any(labels[:, :, None] == class_ids[None, None, :], 1).astype(jnp.float32)
    image_total = labels.shape[0] * dp_count
    loss_part = (
        jnp.sum(jnp.where(valid, jax.nn.softplus(logits) - target * logits, 0.0)) / image_total
    )
    grad_logits = (jnp.where(valid, jax.nn.sigmoid(logits) - target, 0.0) / image_total).astype(
        jnp.bfloat16
    )
    group_grad = jnp.einsum("gc,dc->gd", grad_logits, head_low, preferred_element_type=jnp.float32)
    grad_pooled = lax.psum_scatter(group_grad, "cls", scatter_dimension=0, tiled=True)
    head_rows = lax.all_gather(
        jnp.concatenate([group, grad_logits], 1), "dp", axis=0, tiled=True
    )
    pooled_all, grad_logits_all = head_rows[:, :feature_dim], head_rows[:, feature_dim:]
    pooled_mine = lax.dynamic_slice_in_dim(pooled_all, dp_index * row_count, row_count, 1)
    head_grad = jnp.einsum(
        "gr,gc->rc", pooled_mine, grad_logits_all, preferred_element_type=jnp.float32
    )

    def pool_local(rows_in, gain, shift):
        return pool_rows(rows_in, gain, shift, pack_ids, pack_keep)

    pool_back = jax.vjp(pool_local, output, final_gain, final_shift)[1]
    grad_output, grad_gain, grad_shift = pool_back(grad_pooled)
    grad_arrays, grad_vectors = layer_backward(
        blocks,
        vec_all,
        patches,
        saved,
        pack_ids,
        key_codes,
        grad_output,
        grad_gain,
        grad_shift,
    )

    if on_torus:
        padded = jnp.pad(grad_vectors, ((0, -grad_vectors.shape[0] % 8), (0, 0)))
        codes, scales, vector_sum = reduce_gradients(grad_arrays, padded)
        vector_sum = vector_sum[: grad_vectors.shape[0]]
        left_add, right_add, direction, block_rows, squares = precondition(
            codes, scales, root_left, right_half, half_dp
        )
        layer_squares = jnp.sum(squares[:, 0])
        block_squares = jnp.sum(squares[:, 1].reshape(block_count, 2, half_size), -1)
    else:
        grad_half = reduced_half(jnp.concatenate(grad_arrays, 0), half_groups)
        vector_sum = lax.psum(grad_vectors, ("dp", "cls"))
        left_add, right_add, direction, block_rows = preconditioned_rows(
            grad_half, root_left, right_half, (dp_index % half_dp) * row_count
        )
        layer_squares = jnp.sum(block_rows * block_rows)
        block_squares = jnp.sum(split_halves(direction * direction, half_size), (1, 3))
    vector_rows = lax.dynamic_slice_in_dim(vector_sum, dp_index * row_count, row_count, 1)
    in_top = (dp_index < half_dp).astype(jnp.float32)
    once = (cls_index == 0).astype(jnp.float32)
    own_squares = once * (layer_squares + jnp.sum(vector_rows * vector_rows))
    packed = jnp.concatenate(
        [
            (once * in_top * block_squares).reshape(-1),
            (once * (1.0 - in_top) * block_squares).reshape(-1),
            jnp.stack([own_squares + jnp.sum(head_grad * head_grad), loss_part]),
        ]
    )
    if on_torus:
        spare = -packed.shape[0] % 1024
        packed = sum_everywhere(
            jnp.pad(packed, (0, spare)).reshape(8, 128), dp_count, cls_count
        ).reshape(-1)
    else:
        packed = lax.psum(packed, ("dp", "cls"))
    loss = packed[4 * block_count + 1]
    grad_norm = jnp.sqrt(packed[4 * block_count])
    factor = CLIP_NORM / jnp.maximum(grad_norm, CLIP_NORM)
    sums = packed[: 4 * block_count].reshape(2, block_count, 2)
    mean_squares = jnp.where(dp_index < half_dp, sums[0], sums[1]) / (half_size * half_size)
    mean_squares = mean_squares * factor * factor
    scale = factor * lax.rsqrt(mean_squares + ROOT_EPS)
    wide_scale = jnp.repeat(SHAMPOO_RATE * scale, half_size, axis=1)
    new_blocks = enc_weights - direction * wide_scale[:, None, :]
    square_factor = 0.5 * factor * factor
    new_left = 0.5 * stats_left + square_factor * left_add
    new_right = 0.5 * stats_right + square_factor * right_add
    count = step.astype(jnp.float32)
    new_vec, new_vec_m, new_vec_v = adam_step(vectors, vector_rows * factor, vec_m, vec_v, count)
    new_head, new_head_m, new_head_v = adam_step(
        head_weights, head_grad * factor, head_m, head_v, count
    )
    return (
        loss,
        grad_norm,
        new_blocks,
        block_rows * factor,
        new_left,
        new_right,
        new_vec,
        new_vec_m,
        new_vec_v,
        new_head,
        new_head_m,
        new_head_v,
    )


def solution(mesh):
    return jax.shard_map(
        on_device,
        mesh=mesh,
        in_specs=(
            P(("dp", "cls"), None),
            P(("dp", "cls"), None),
            P(("dp", "cls"), None),
            P("dp", None),
            P(),
            P(),
            P(None, "dp", None),
            P(None, "dp", None),
            P(None, "dp", None),
            P(None, "dp", None),
            P(None, "dp", None),
            P("dp", "cls"),
            P("dp", "cls"),
            P("dp", "cls"),
            P(None, "dp"),
            P(None, "dp"),
            P(None, "dp"),
        ),
        out_specs=(
            P(),
            P(),
            P(None, "dp", None),
            P(None, "dp", None),
            P(None, "dp", None),
            P(None, "dp", None),
            P(None, "dp"),
            P(None, "dp"),
            P(None, "dp"),
            P("dp", "cls"),
            P("dp", "cls"),
            P("dp", "cls"),
        ),
        check_vma=False,
    )
```

```python
import functools

import jax
import jax.numpy as jnp
from jax import lax
from jax.experimental import pallas as pl
from jax.experimental.pallas import tpu as pltpu
from jax.sharding import PartitionSpec as P

HEADS = 12
HEAD = 64
LABELS_REAL = 21843
IMAGE_MAX = 196
QTILE = 256
PAIR = 2 * HEAD
ROWS = 256
HIDDEN_TILE = 384
MESH = pl.DeviceIdType.MESH
CODE_TOP = 32766.0
CODE_FLOOR = 1e-33
PIECE = 48
SPAN = 48
SHARES = 8
IMG_PACK = 8


FULL_PRECISION = lax.Precision.HIGHEST
NORM_EPS = 1e-06
CLIP_NORM = 1.0
ADAM_RATE = 0.02
SHAMPOO_RATE = 0.01
BETA_FIRST = 0.9
BETA_SECOND = 0.999
ADAM_EPS = 1e-08
WEIGHT_DECAY = 0.1
ROOT_EPS = 1e-06


def norm_rows(values, gain, shift):
    centred = values - jnp.mean(values, -1, keepdims=True)
    spread = jnp.mean(centred * centred, -1, keepdims=True)
    return centred * lax.rsqrt(spread + NORM_EPS) * gain + shift


def pool_rows(output, gain, shift, pack_ids, pack_keep):
    final = norm_rows(output, gain, shift)
    member = (
        (pack_ids[None, :] == jnp.arange(IMG_PACK)[:, None]) & (pack_keep[None, :] == 1)
    ).astype(jnp.float32)
    counted = jnp.maximum(jnp.sum(member, 1), 1.0)
    return jnp.dot(member, final, precision=FULL_PRECISION) / counted[:, None]


def key_window(tile, length):
    reach = -(-(IMAGE_MAX - 1) // 128) * 128
    low = max(0, tile * QTILE - reach)
    high = min(length, (tile + 1) * QTILE + reach)
    return low, high


def attention_forward_kernel(qids_ref, kcodes_ref, q_ref, k_ref, v_ref, out_ref, bias_ref):
    length = q_ref.shape[0]
    lane = lax.broadcasted_iota(jnp.int32, (QTILE, PAIR), 1)

    @pl.when(pl.program_id(0) == 0)
    def _():
        for tile in range(length // QTILE):
            low, high = key_window(tile, length)
            shape = (QTILE, high - low)
            rows = lax.broadcasted_iota(jnp.int32, shape, 0) + tile * QTILE
            cols = lax.broadcasted_iota(jnp.int32, shape, 1) + low
            same = qids_ref[tile * QTILE : (tile + 1) * QTILE, :] == kcodes_ref[:, low:high]
            bias_ref[tile, :, : high - low] = jnp.where(same | (rows == cols), 0.0, -1e30)

    for tile in range(length // QTILE):
        low, high = key_window(tile, length)
        rows = pl.ds(tile * QTILE, QTILE)
        queries = q_ref[rows, :] * jnp.bfloat16(HEAD ** (-0.5))
        keys = k_ref[low:high, :]
        values = v_ref[low:high, :]
        halves = []
        for head in range(2):
            mine = (lane >= head * HEAD) & (lane < (head + 1) * HEAD)
            picked = jnp.where(mine, queries, jnp.zeros_like(queries))
            scores = lax.dot_general(
                picked, keys, (((1,), (1,)), ((), ())), preferred_element_type=jnp.float32
            )
            scores = scores + bias_ref[tile, :, : high - low]
            top = jnp.max(scores, -1, keepdims=True)
            weights = jnp.exp(scores - top)
            probs = weights * (1.0 / jnp.sum(weights, -1, keepdims=True))
            halves.append(
                jnp.dot(probs.astype(jnp.bfloat16), values, preferred_element_type=jnp.float32)
            )
        out_ref[rows, :] = jnp.where(lane < HEAD, halves[0], halves[1]).astype(jnp.bfloat16)


def attention_backward_kernel(
    qids_ref, kcodes_ref, q_ref, k_ref, v_ref, do_ref, out_ref, bias_ref, dk_ref, dv_ref
):
    length = q_ref.shape[0]
    lane = lax.broadcasted_iota(jnp.int32, (QTILE, PAIR), 1)
    scale = jnp.bfloat16(HEAD ** (-0.5))

    @pl.when(pl.program_id(0) == 0)
    def _():
        for tile in range(length // QTILE):
            low, high = key_window(tile, length)
            shape = (high - low, QTILE)
            rows = lax.broadcasted_iota(jnp.int32, shape, 0) + low
            cols = lax.broadcasted_iota(jnp.int32, shape, 1) + tile * QTILE
            same = kcodes_ref[low:high, :] == qids_ref[:, tile * QTILE : (tile + 1) * QTILE]
            bias_ref[tile, : high - low, :] = jnp.where(same | (rows == cols), 0.0, -1e30)

    dk_ref[...] = jnp.zeros_like(dk_ref)
    dv_ref[...] = jnp.zeros_like(dv_ref)
    for tile in range(length // QTILE):
        low, high = key_window(tile, length)
        rows = pl.ds(tile * QTILE, QTILE)
        window = pl.ds(low, high - low)
        queries = q_ref[rows, :] * scale
        keys = k_ref[window, :]
        values = v_ref[window, :]
        grads = do_ref[rows, :]
        halves = []
        for head in range(2):
            mine = (lane >= head * HEAD) & (lane < (head + 1) * HEAD)
            picked = jnp.where(mine, queries, jnp.zeros_like(queries))
            picked_grads = jnp.where(mine, grads, jnp.zeros_like(grads))
            scores = lax.dot_general(
                keys, picked, (((1,), (1,)), ((), ())), preferred_element_type=jnp.float32
            )
            scores = scores + bias_ref[tile, : high - low, :]
            top = jnp.max(scores, 0, keepdims=True)
            weights = jnp.exp(scores - top)
            probs = weights * (1.0 / jnp.sum(weights, 0, keepdims=True))
            grad_probs = lax.dot_general(
                values, picked_grads, (((1,), (1,)), ((), ())), preferred_element_type=jnp.float32
            )
            inner = jnp.sum(probs * grad_probs, 0, keepdims=True)
            grad_scores = (probs * (grad_probs - inner)).astype(jnp.bfloat16)
            dv_ref[window, :] += jnp.dot(
                probs.astype(jnp.bfloat16), picked_grads, preferred_element_type=jnp.float32
            )
            dk_ref[window, :] += jnp.dot(
                grad_scores, picked, preferred_element_type=jnp.float32
            )
            halves.append(
                lax.dot_general(
                    grad_scores,
                    keys,
                    (((0,), (0,)), ((), ())),
                    preferred_element_type=jnp.float32,
                )
            )
        grad_queries = jnp.where(lane < HEAD, halves[0], halves[1]) * HEAD ** (-0.5)
        out_ref[0, rows, :] = grad_queries.astype(jnp.bfloat16)
    out_ref[1] = dk_ref[...].astype(jnp.bfloat16)
    out_ref[2] = dv_ref[...].astype(jnp.bfloat16)


def pair_spec(length, part=None):
    if part is None:
        return pl.BlockSpec((length, PAIR), lambda pair: (0, pair))
    return pl.BlockSpec((None, length, PAIR), lambda pair: (part, 0, pair))


def whole_spec(shape):
    return pl.BlockSpec(shape, lambda pair: (0,) * len(shape))


def attention_forward(qkv_rows, pack_ids, key_codes):
    _, length, width = qkv_rows.shape
    tiles = length // QTILE
    window = max(high - low for low, high in (key_window(t, length) for t in range(tiles)))
    return pl.pallas_call(
        attention_forward_kernel,
        grid=(width // PAIR,),
        out_shape=jax.ShapeDtypeStruct((length, width), jnp.bfloat16),
        in_specs=[whole_spec((length, 1)), whole_spec((1, length))]
        + [pair_spec(length, part) for part in range(3)],
        out_specs=pair_spec(length),
        scratch_shapes=[pltpu.VMEM((tiles, QTILE, window), jnp.float32)],
        compiler_params=pltpu.CompilerParams(vmem_limit_bytes=40 << 20),
        name="attention_forward",
    )(pack_ids[:, None], key_codes[None, :], qkv_rows, qkv_rows, qkv_rows)


def attention_backward(qkv_rows, pack_ids, key_codes, grad_attended):
    _, length, width = qkv_rows.shape
    tiles = length // QTILE
    window = max(high - low for low, high in (key_window(t, length) for t in range(tiles)))
    return pl.pallas_call(
        attention_backward_kernel,
        grid=(width // PAIR,),
        out_shape=jax.ShapeDtypeStruct((3, length, width), jnp.bfloat16),
        in_specs=[whole_spec((1, length)), whole_spec((length, 1))]
        + [pair_spec(length, part) for part in range(3)]
        + [pair_spec(length)],
        out_specs=pl.BlockSpec((3, length, PAIR), lambda pair: (0, 0, pair)),
        scratch_shapes=[
            pltpu.VMEM((tiles, window, QTILE), jnp.float32),
            pltpu.VMEM((length, PAIR), jnp.float32),
            pltpu.VMEM((length, PAIR), jnp.float32),
        ],
        compiler_params=pltpu.CompilerParams(vmem_limit_bytes=40 << 20),
        name="attention_backward",
    )(pack_ids[None, :], key_codes[:, None], qkv_rows, qkv_rows, qkv_rows, grad_attended)


def mlp_forward_kernel(x_ref, up_ref, bias_ref, down_ref, units_ref, slope_ref, out_ref):
    first = pl.program_id(0) == 0

    @pl.when(first)
    def _():
        out_ref[...] = jnp.zeros_like(out_ref)

    for start in range(0, x_ref.shape[0], ROWS):
        rows = pl.ds(start, ROWS)
        pre = jnp.dot(x_ref[rows, :], up_ref[...], preferred_element_type=jnp.float32)
        pre = pre + bias_ref[...]
        half = 0.5 + 0.5 * lax.erf(pre * 0.7071067811865476)
        bell = jnp.exp(-0.5 * pre * pre) * 0.3989422804014327
        units = (pre * half).astype(jnp.bfloat16)
        units_ref[rows, :] = units
        slope_ref[rows, :] = half + pre * bell
        out_ref[rows, :] += jnp.dot(units, down_ref[...], preferred_element_type=jnp.float32)


def mlp_backward_kernel(
    x_ref, dm_ref, up_ref, down_ref, units_ref, slope_ref,
    grad_up_ref, grad_down_ref, bias_ref, dx_ref, dpre_ref
):
    @pl.when(pl.program_id(0) == 0)
    def _():
        dx_ref[...] = jnp.zeros_like(dx_ref)

    total = jnp.zeros((1, HIDDEN_TILE), jnp.float32)
    for start in range(0, x_ref.shape[0], ROWS):
        rows = pl.ds(start, ROWS)
        units_back = lax.dot_general(
            dm_ref[rows, :], down_ref[...], (((1,), (1,)), ((), ())),
            preferred_element_type=jnp.float32,
        )
        grad_pre = (units_back * slope_ref[rows, :]).astype(jnp.bfloat16)
        dpre_ref[rows, :] = grad_pre
        total = total + jnp.sum(grad_pre.astype(jnp.float32), 0, keepdims=True)
        dx_ref[rows, :] += lax.dot_general(
            grad_pre, up_ref[...], (((1,), (1,)), ((), ())), preferred_element_type=jnp.float32
        )
    bias_ref[...] = total
    over_rows = (((0,), (0,)), ((), ()))
    grad_down_ref[...] = lax.dot_general(
        units_ref[...], dm_ref[...], over_rows, preferred_element_type=jnp.float32
    )
    grad_up_ref[...] = lax.dot_general(
        x_ref[...], dpre_ref[...], over_rows, preferred_element_type=jnp.float32
    )


def mlp_specs(length, width, up_count):
    split = width // HIDDEN_TILE
    resident = pl.BlockSpec((length, width), lambda t: (0, 0))
    up = pl.BlockSpec((None, width, HIDDEN_TILE), lambda t: (5 + t // split, 0, t % split))
    down = pl.BlockSpec(
        (None, HIDDEN_TILE, width), lambda t: (5 + up_count + t // split, t % split, 0)
    )
    hidden = pl.BlockSpec((length, HIDDEN_TILE), lambda t: (0, t))
    bias = pl.BlockSpec((1, HIDDEN_TILE), lambda t: (0, t))
    return split, resident, up, down, hidden, bias


def mlp_forward(rows, blocks, up_bias):
    length, width = rows.shape
    up_count = (blocks.shape[0] - 5) // 2
    split, resident, up, down, hidden, bias = mlp_specs(length, width, up_count)
    hidden_size = up_count * width
    return pl.pallas_call(
        mlp_forward_kernel,
        grid=(up_count * split,),
        out_shape=(
            jax.ShapeDtypeStruct((length, hidden_size), jnp.bfloat16),
            jax.ShapeDtypeStruct((length, hidden_size), jnp.float32),
            jax.ShapeDtypeStruct((length, width), jnp.float32),
        ),
        in_specs=[resident, up, bias, down],
        out_specs=(hidden, hidden, resident),
        compiler_params=pltpu.CompilerParams(vmem_limit_bytes=48 << 20),
        name="mlp_forward",
    )(rows, blocks, up_bias.reshape(1, hidden_size), blocks)


def mlp_backward(rows, grad_branch, blocks, units, slopes):
    length, width = rows.shape
    up_count = (blocks.shape[0] - 5) // 2
    split, resident, up, down, hidden, bias = mlp_specs(length, width, up_count)
    hidden_size = up_count * width
    return pl.pallas_call(
        mlp_backward_kernel,
        grid=(up_count * split,),
        out_shape=(
            jax.ShapeDtypeStruct((up_count, width, width), jnp.float32),
            jax.ShapeDtypeStruct((up_count, width, width), jnp.float32),
            jax.ShapeDtypeStruct((1, hidden_size), jnp.float32),
            jax.ShapeDtypeStruct((length, width), jnp.float32),
        ),
        in_specs=[resident, resident, up, down, hidden, hidden],
        out_specs=(
            pl.BlockSpec((None, width, HIDDEN_TILE), lambda t: (t // split, 0, t % split)),
            pl.BlockSpec((None, HIDDEN_TILE, width), lambda t: (t // split, t % split, 0)),
            bias,
            resident,
        ),
        scratch_shapes=[pltpu.VMEM((length, HIDDEN_TILE), jnp.bfloat16)],
        compiler_params=pltpu.CompilerParams(vmem_limit_bytes=48 << 20),
        name="mlp_backward",
    )(rows, grad_branch, blocks, blocks, units, slopes)


def layer_forward(blocks, vec_all, patch, pack_ids, key_codes):
    up_count = (blocks.shape[0] - 5) // 2
    embedded = jnp.dot(patch, blocks[0], preferred_element_type=jnp.float32) + vec_all[0]
    normed_one = norm_rows(embedded, vec_all[1], vec_all[2]).astype(jnp.bfloat16)
    qkv_rows = jnp.einsum(
        "td,kde->kte", normed_one, blocks[1:4], preferred_element_type=jnp.float32
    )
    qkv_bias = jnp.stack([vec_all[3], jnp.zeros_like(vec_all[3]), vec_all[4]])
    qkv_rows = (qkv_rows + qkv_bias[:, None, :]).astype(jnp.bfloat16)
    attended = attention_forward(qkv_rows, pack_ids, key_codes)
    hidden = (
        embedded + jnp.dot(attended, blocks[4], preferred_element_type=jnp.float32) + vec_all[5]
    )
    normed_two = norm_rows(hidden, vec_all[6], vec_all[7]).astype(jnp.bfloat16)
    units, slopes, branch = mlp_forward(normed_two, blocks, vec_all[8 : 8 + up_count])
    output = hidden + branch + vec_all[8 + up_count]
    return (
        output,
        (embedded, normed_one, qkv_rows, attended, hidden, normed_two, slopes, units),
    )


def layer_backward(
    blocks, vec_all, patch, saved, pack_ids, key_codes, grad_output, grad_gain, grad_shift
):
    embedded, normed_one, qkv_rows, attended, hidden, normed_two, slopes, units = saved
    feature_dim = patch.shape[1]
    up_count = (blocks.shape[0] - 5) // 2
    grad_branch = grad_output.astype(jnp.bfloat16)
    grad_up, grad_down, up_sums, grad_normed_two = mlp_backward(
        normed_two, grad_branch, blocks, units, slopes
    )
    norm_two_back = jax.vjp(norm_rows, hidden, vec_all[6], vec_all[7])[1]
    grad_hidden_norm, grad_gain_two, grad_shift_two = norm_two_back(grad_normed_two)
    grad_hidden = grad_output + grad_hidden_norm
    grad_attn_out = grad_hidden.astype(jnp.bfloat16)
    grad_out_proj = jnp.einsum(
        "te,td->ed", attended, grad_attn_out, preferred_element_type=jnp.float32
    )
    grad_attended = jnp.einsum(
        "td,ed->te", grad_attn_out, blocks[4], preferred_element_type=jnp.float32
    ).astype(jnp.bfloat16)
    grad_qkv = attention_backward(qkv_rows, pack_ids, key_codes, grad_attended)
    grad_qkv_proj = jnp.einsum(
        "td,kte->kde", normed_one, grad_qkv, preferred_element_type=jnp.float32
    )
    grad_normed_one = jnp.einsum(
        "kte,kde->td", grad_qkv, blocks[1:4], preferred_element_type=jnp.float32
    )
    norm_one_back = jax.vjp(norm_rows, embedded, vec_all[1], vec_all[2])[1]
    grad_embed_norm, grad_gain_one, grad_shift_one = norm_one_back(grad_normed_one)
    grad_embedded = (grad_hidden + grad_embed_norm).astype(jnp.bfloat16)
    grad_patch = jnp.einsum("tp,td->pd", patch, grad_embedded, preferred_element_type=jnp.float32)
    grad_arrays = (grad_patch[None], grad_qkv_proj, grad_out_proj[None], grad_up, grad_down)
    bias_sums = jnp.stack(
        [
            jnp.sum(grad_embedded.astype(jnp.float32), 0),
            grad_gain_one,
            grad_shift_one,
            jnp.sum(grad_qkv[0].astype(jnp.float32), 0),
            jnp.sum(grad_qkv[2].astype(jnp.float32), 0),
            jnp.sum(grad_attn_out.astype(jnp.float32), 0),
            grad_gain_two,
            grad_shift_two,
        ]
    )
    up_sums = up_sums.reshape(up_count, feature_dim)
    tail_sums = jnp.stack([jnp.sum(grad_branch.astype(jnp.float32), 0), grad_gain, grad_shift])
    return (grad_arrays, jnp.concatenate([bias_sums, up_sums, tail_sums], 0))


def torus_place():
    dp, cls = lax.axis_index("dp"), lax.axis_index("cls")
    return dp // 2, dp % 2, cls // 2, cls % 2


def torus_device(z, y, x, core):
    return (z * 2 + y, x * 2 + core)


def encode(pieces, code_refs, scale_ref):
    top = None
    for piece in pieces:
        peak = jnp.max(jnp.abs(piece()), 0, keepdims=True)
        top = peak if top is None else jnp.maximum(top, peak)
    top = jnp.maximum(top, CODE_FLOOR)
    inverse = CODE_TOP / top
    for piece, code_ref in zip(pieces, code_refs):
        code_ref[...] = jnp.round(piece() * inverse).astype(jnp.int32).astype(jnp.int16)
    scale_ref[...] = top * (1.0 / CODE_TOP)


def decode(code, scale):
    return code.astype(jnp.int32).astype(jnp.float32) * scale


def reduce_kernel(counts, *refs):
    sources, refs = refs[: len(counts)], refs[len(counts) :]
    (vec_ref, tail_ref, left_hbm, right_hbm,
     own_hbm, left_out_hbm, right_out_hbm, step_hbm, sums_ref, tail_out_ref, vec_out_ref,
     left_buf, right_buf, outs_buf, squares, high_buf, low_buf, sum_slots, tail_slots,
     in_sem, sum_send, sum_recv, tail_send, tail_recv,
     acc, spare, kept, sent0, got0, sent1, got1, sent2, got2, sent3, got3, sent4, got4,
     ss0, gs0, ss1, gs1, ss2, gs2, ss3, gs3, ss4, gs4, codes, scales, vec_got,
     load_sem, out_sem, send_sem, recv_sem, send_scale_sem, recv_scale_sem,
     vec_send_sem, vec_recv_sem) = refs
    total = sum(counts)
    half, width = codes.shape[1], codes.shape[2]
    cols = width // 2
    z, y, x, core = torus_place()
    upper = z // 2
    inner = (z % 2) != upper
    mate_core = torus_device(z, y, x, 1 - core)
    mate_x = torus_device(z, y, 1 - x, core)
    mate_y = torus_device(z, 1 - y, x, core)
    mate_z = torus_device(z + 1 - 2 * (z % 2), y, x, core)
    mate_mid = torus_device(3 - z, y, x, core)
    mate_far = torus_device((z + 2) % 4, y, x, core)

    barrier = pltpu.get_barrier_semaphore()
    dp, cls = lax.axis_index("dp"), lax.axis_index("cls")
    everyone = tail_slots.shape[0]
    quarter = sum_slots.shape[0]
    me = dp * 4 + cls

    def any_mate(n):
        other = lax.rem(me + n, everyone)
        return (other // 4, lax.rem(other, 4))

    def half_mate(n):
        return (upper * quarter + lax.rem(dp + n, quarter), cls)

    for n in range(1, everyone):
        pl.semaphore_signal(barrier, inc=1, device_id=any_mate(n), device_id_type=MESH)
    pl.semaphore_wait(barrier, everyone - 1)
    own = lax.rem(dp, quarter) * left_buf.shape[1]

    own_cols = pl.ds(pl.multiple_of(core * cols, 128), cols)
    other_cols = pl.ds(pl.multiple_of((1 - core) * cols, 128), cols)

    def rows_at(start, size):
        return pl.ds(pl.multiple_of(start, PIECE), size)

    def loads(m, body):
        start = 0
        for source, count in zip(sources, counts):
            def one(source=source, start=start):
                pair = (
                    pltpu.make_async_copy(
                        source.at[m - start, :, own_cols], acc.at[m % 5], load_sem.at[m % 2, 0]
                    ),
                    pltpu.make_async_copy(
                        source.at[m - start, :, other_cols], spare.at[m % 2], load_sem.at[m % 2, 1]
                    ),
                )
                for copy in pair:
                    body(copy)

            pl.when((m >= start) & (m < start + count))(one)
            start += count

    def message(stage, m, source, scale_source, target, scale_target, mate):
        return (
            pltpu.make_async_remote_copy(
                src_ref=source, dst_ref=target,
                send_sem=send_sem.at[stage, m % 2], recv_sem=recv_sem.at[stage, m],
                device_id=mate, device_id_type=MESH,
            ),
            pltpu.make_async_remote_copy(
                src_ref=scale_source, dst_ref=scale_target,
                send_sem=send_scale_sem.at[stage, m % 2], recv_sem=recv_scale_sem.at[stage, m],
                device_id=mate, device_id_type=MESH,
            ),
        )

    def first(m):
        return message(0, m, sent0.at[m % 2], ss0.at[m % 2], got0.at[m], gs0.at[m], mate_core)

    def second(m, b):
        return message(
            1 + b, m, sent1.at[m % 2, b], ss1.at[m % 2, b], got1.at[m, b], gs1.at[m, b],
            mate_y if b else mate_x,
        )

    def third(m, b):
        return message(
            3 + b, m, sent2.at[m % 2, b], ss2.at[m % 2, b], got2.at[m, b], gs2.at[m, b],
            mate_x if b else mate_y,
        )

    def fourth(m):
        return message(5, m, sent3.at[m % 2], ss3.at[m % 2], got3.at[m], gs3.at[m], mate_z)

    def fifth(m):
        return message(6, m, sent4.at[m % 2], ss4.at[m % 2], got4.at[m], gs4.at[m], mate_mid)

    piece_a = 2 * x + y
    piece_b = 4 + 2 * y + x

    def spread(stage, m, piece, count, mate, columns=own_cols):
        rows = pl.ds(pl.multiple_of(piece * PIECE, PIECE), count * PIECE)
        block = codes.at[m, rows, columns]
        scale = scales.at[m, pl.ds(piece, count), :, columns]
        return message(stage, m, block, scale, block, scale, mate)

    def start(copies):
        for copy in copies:
            copy.start()

    def wait_send(copies):
        for copy in copies:
            copy.wait_send()

    def wait_recv(copies):
        for copy in copies:
            copy.wait_recv()

    def vec_copy(step, mate):
        return pltpu.make_async_remote_copy(
            src_ref=vec_got.at[step, 0], dst_ref=vec_got.at[step, 1],
            send_sem=vec_send_sem.at[step], recv_sem=vec_recv_sem.at[step],
            device_id=mate, device_id_type=MESH,
        )

    vec_mates = (mate_core, mate_x, mate_y, mate_z, mate_far)

    loads(jnp.int32(0), lambda copy: copy.start())
    vec_got[0, 0] = vec_ref[...]
    vec_copy(0, vec_mates[0]).start()

    def step(t, carry):
        for n in range(1, 6):
            @pl.when(t == n)
            def _(n=n):
                vec_copy(n - 1, vec_mates[n - 1]).wait()
                value = vec_got[n - 1, 0] + vec_got[n - 1, 1]
                if n < 5:
                    vec_got[n, 0] = value
                    vec_copy(n, vec_mates[n]).start()
                else:
                    vec_out_ref[...] = value

        @pl.when(t < total)
        def _():
            m = t
            loads(m, lambda copy: copy.wait())

            @pl.when(m + 1 < total)
            def _():
                loads(m + 1, lambda copy: copy.start())

            span = 2 * PIECE
            encode(
                [lambda r=r: spare[m % 2, r : r + span, :] for r in range(0, 2 * half, span)],
                [sent0.at[m % 2, r : r + span, :] for r in range(0, 2 * half, span)],
                ss0.at[m % 2],
            )
            start(first(m))

        @pl.when((t >= 1) & (t < total + 1))
        def _():
            m = t - 1
            copies = first(m)
            wait_send(copies)
            wait_recv(copies)
            slot = m % 5
            span = 2 * PIECE
            for r in range(0, 2 * half, span):
                acc[slot, r : r + span, :] += decode(got0[m, r : r + span, :], gs0[m])
            for b in range(2):
                other = (1 - y) if b else (1 - x)
                begins = [h * half + b * 4 * PIECE + other * span for h in range(2)]
                encode(
                    [lambda s=s: acc[slot, rows_at(s, span), :] for s in begins],
                    [sent1.at[m % 2, b, h] for h in range(2)],
                    ss1.at[m % 2, b],
                )
                start(second(m, b))

        @pl.when((t >= 2) & (t < total + 2))
        def _():
            m = t - 2
            slot = m % 5
            span = 2 * PIECE
            for b in range(2):
                copies = second(m, b)
                wait_send(copies)
                wait_recv(copies)
                mine = y if b else x
                other = (1 - x) if b else (1 - y)
                begins = [h * half + b * 4 * PIECE + mine * span for h in range(2)]
                for h, s in enumerate(begins):
                    acc[slot, rows_at(s, span), :] += decode(got1[m, b, h], gs1[m, b])
                encode(
                    [lambda s=s: acc[slot, rows_at(s + other * PIECE, PIECE), :] for s in begins],
                    [sent2.at[m % 2, b, h] for h in range(2)],
                    ss2.at[m % 2, b],
                )
                start(third(m, b))

        @pl.when((t >= 3) & (t < total + 3))
        def _():
            m = t - 3
            slot = m % 5
            for b in range(2):
                copies = third(m, b)
                wait_send(copies)
                wait_recv(copies)
                place = piece_b if b else piece_a
                for h in range(2):
                    kept[m % 3, h, b] = acc[
                        slot, rows_at(h * half + place * PIECE, PIECE), :
                    ] + decode(got2[m, b, h], gs2[m, b])

            @pl.when(jnp.logical_not(inner))
            def _():
                pairs = [(h, b) for h in range(2) for b in range(2)]
                encode(
                    [lambda h=h, b=b: kept[m % 3, h, b] for h, b in pairs],
                    [sent3.at[m % 2, h, b] for h, b in pairs],
                    ss3.at[m % 2],
                )
                start(fourth(m))

        @pl.when((t >= 4) & (t < total + 4))
        def _():
            m = t - 4
            copies = fourth(m)

            @pl.when(jnp.logical_not(inner))
            def _():
                wait_send(copies)

            @pl.when(inner)
            def _():
                wait_recv(copies)
                for h in range(2):
                    for b in range(2):
                        kept[m % 3, h, b] += decode(got3[m, h, b], gs3[m])
                encode(
                    [lambda b=b: kept[m % 3, 1 - upper, b] for b in range(2)],
                    [sent4.at[m % 2, b] for b in range(2)],
                    ss4.at[m % 2],
                )
                start(fifth(m))

        @pl.when((t >= 5) & (t < total + 5))
        def _():
            m = t - 5

            @pl.when(inner)
            def _():
                copies = fifth(m)
                wait_send(copies)
                wait_recv(copies)
                for b in range(2):
                    place = piece_b if b else piece_a
                    value = kept[m % 3, upper, b] + decode(got4[m, b], gs4[m])
                    encode(
                        [lambda value=value: value],
                        [codes.at[m, rows_at(place * PIECE, PIECE), own_cols]],
                        scales.at[m, place, :, own_cols],
                    )
                    start(spread(7 + b, m, place, 1, mate_z))

        @pl.when((t >= 6) & (t < total + 6))
        def _():
            m = t - 6
            for b in range(2):
                place = piece_b if b else piece_a
                copies = spread(7 + b, m, place, 1, mate_z)

                @pl.when(inner)
                def _(copies=copies):
                    wait_send(copies)

                @pl.when(jnp.logical_not(inner))
                def _(copies=copies):
                    wait_recv(copies)

                start(spread(9 + b, m, place, 1, mate_x if b else mate_y))

        @pl.when((t >= 7) & (t < total + 7))
        def _():
            m = t - 7
            for b in range(2):
                place = piece_b if b else piece_a
                theirs = (4 + 2 * y + 1 - x) if b else (2 * x + 1 - y)
                wait_send(spread(9 + b, m, place, 1, mate_x if b else mate_y))
                wait_recv(spread(9 + b, m, theirs, 1, mate_x if b else mate_y))
                begin = (4 + 2 * y) if b else 2 * x
                start(spread(11 + b, m, begin, 2, mate_y if b else mate_x))

        @pl.when((t >= 8) & (t < total + 8))
        def _():
            m = t - 8
            for b in range(2):
                begin = (4 + 2 * y) if b else 2 * x
                theirs = (4 + 2 * (1 - y)) if b else 2 * (1 - x)
                wait_send(spread(11 + b, m, begin, 2, mate_y if b else mate_x))
                wait_recv(spread(11 + b, m, theirs, 2, mate_y if b else mate_x))
            start(spread(13, m, 0, 8, mate_core))

        def ins(m):
            return (
                pltpu.make_async_copy(left_hbm.at[m], left_buf.at[m % 2], in_sem.at[m % 2, 0]),
                pltpu.make_async_copy(right_hbm.at[m], right_buf.at[m % 2], in_sem.at[m % 2, 1]),
            )

        def outs(m):
            targets = (own_hbm, left_out_hbm, right_out_hbm, step_hbm)
            return [
                pltpu.make_async_copy(
                    outs_buf.at[m % 2, n], target.at[m], out_sem.at[m % 2, n]
                )
                for n, target in enumerate(targets)
            ]

        @pl.when((t >= 8) & (t < total + 8))
        def _():
            start(ins(t - 8))

        @pl.when((t >= 11) & (t < total + 11))
        def _():
            for copy in outs(t - 11):
                copy.wait()

        @pl.when((t >= 9) & (t < total + 9))
        def _():
            m = t - 9
            wait_send(spread(13, m, 0, 8, mate_core))
            wait_recv(spread(13, m, 0, 8, mate_core, other_cols))
            for copy in ins(m):
                copy.wait()
            precondition_block(
                own, codes.at[m], scales.at[m], left_buf.at[m % 2], right_buf.at[m % 2],
                outs_buf.at[m % 2], squares.at[m], high_buf, low_buf,
            )
            start(outs(m))

        return carry

    lax.fori_loop(0, total + 11, step, 0)

    def folded(row):
        return sum(row[:, n * 128 : (n + 1) * 128] for n in range(row.shape[1] // 128))

    sums_ref[...] = jnp.zeros_like(sums_ref)
    layer = jnp.zeros((1, 128), jnp.float32)
    for m in range(total):
        layer = layer + folded(squares[m, 0:1, :])
        for quad in range(2):
            part = squares[m, 1:2, quad * cols : (quad + 1) * cols]
            sums_ref[2 * m + quad : 2 * m + quad + 1, :] = folded(part)
    sum_slots[lax.rem(dp, quarter)] = sums_ref[...]
    once = (cls == 0).astype(jnp.float32)
    first_row = lax.broadcasted_iota(jnp.int32, tail_ref.shape, 0) == 0
    tail_slots[me] = tail_ref[...] + jnp.where(first_row, once * layer, 0.0)

    def sum_copy(n, slot):
        return pltpu.make_async_remote_copy(
            src_ref=sum_slots.at[slot], dst_ref=sum_slots.at[slot],
            send_sem=sum_send.at[n], recv_sem=sum_recv.at[slot],
            device_id=half_mate(n), device_id_type=MESH,
        )

    def tail_copy(n, slot):
        return pltpu.make_async_remote_copy(
            src_ref=tail_slots.at[slot], dst_ref=tail_slots.at[slot],
            send_sem=tail_send.at[n], recv_sem=tail_recv.at[slot],
            device_id=any_mate(n), device_id_type=MESH,
        )

    for n in range(1, quarter):
        sum_copy(n, lax.rem(dp, quarter)).start()
    for n in range(1, everyone):
        tail_copy(n, me).start()
    for n in range(1, quarter):
        sum_copy(n, lax.rem(dp, quarter)).wait_send()
        sum_copy(n, lax.rem(dp + n, quarter)).wait_recv()
    for n in range(1, everyone):
        tail_copy(n, me).wait_send()
        tail_copy(n, lax.rem(me + n, everyone)).wait_recv()
    value = sum_slots[0]
    for n in range(1, quarter):
        value = value + sum_slots[n]
    sums_ref[...] = value
    value = tail_slots[0]
    for n in range(1, everyone):
        value = value + tail_slots[n]
    tail_out_ref[...] = value


def reduce_gradients(arrays, vec_sums, tail, root_left, right_half, dp_count, cls_count):
    counts = tuple(array.shape[0] for array in arrays)
    total = sum(counts)
    width = arrays[0].shape[1]
    rows = root_left.shape[1]
    half, cols = width // 2, width // 2
    sum_rows = 2 * total + -2 * total % 8
    f32, i16 = jnp.float32, jnp.int16

    def pair(*shape):
        return [pltpu.VMEM((2,) + shape, i16), pltpu.VMEM((total,) + shape, i16)]

    def scale_pair(*shape):
        return [
            pltpu.VMEM((2,) + shape + (1, cols), f32),
            pltpu.VMEM((total,) + shape + (1, cols), f32),
        ]

    hbm = pl.BlockSpec(memory_space=pl.ANY)
    vmem = pl.BlockSpec(memory_space=pltpu.VMEM)
    return pl.pallas_call(
        functools.partial(reduce_kernel, counts),
        out_shape=(jax.ShapeDtypeStruct((total, rows, width), f32),) * 4
        + (
            jax.ShapeDtypeStruct((sum_rows, 128), f32),
            jax.ShapeDtypeStruct(tail.shape, f32),
            jax.ShapeDtypeStruct(vec_sums.shape, f32),
        ),
        in_specs=[hbm] * len(arrays) + [vmem, vmem, hbm, hbm],
        out_specs=(hbm,) * 4 + (vmem,) * 3,
        scratch_shapes=[
            pltpu.VMEM((2, rows, width), f32),
            pltpu.VMEM((2, half, width), f32),
            pltpu.VMEM((2, 4, rows, width), f32),
            pltpu.VMEM((total, 2, width), f32),
            pltpu.VMEM((half, width), jnp.bfloat16),
            pltpu.VMEM((half, width), jnp.bfloat16),
            pltpu.VMEM((dp_count // 2, sum_rows, 128), f32),
            pltpu.VMEM((dp_count * cls_count,) + tail.shape, f32),
            pltpu.SemaphoreType.DMA((2, 2)),
            pltpu.SemaphoreType.DMA((dp_count // 2,)),
            pltpu.SemaphoreType.DMA((dp_count // 2,)),
            pltpu.SemaphoreType.DMA((dp_count * cls_count,)),
            pltpu.SemaphoreType.DMA((dp_count * cls_count,)),
            pltpu.VMEM((5, width, cols), f32),
            pltpu.VMEM((2, width, cols), f32),
            pltpu.VMEM((3, 2, 2, PIECE, cols), f32),
        ]
        + pair(width, cols)
        + pair(2, 2, 2 * PIECE, cols)
        + pair(2, 2, PIECE, cols)
        + pair(2, 2, PIECE, cols)
        + pair(2, PIECE, cols)
        + scale_pair()
        + scale_pair(2)
        + scale_pair(2)
        + scale_pair()
        + scale_pair()
        + [
            pltpu.VMEM((total, half, width), i16),
            pltpu.VMEM((total, half // PIECE, 1, width), f32),
            pltpu.VMEM((5, 2) + vec_sums.shape, f32),
            pltpu.SemaphoreType.DMA((2, 2)),
            pltpu.SemaphoreType.DMA((2, 4)),
            pltpu.SemaphoreType.DMA((14, 2)),
            pltpu.SemaphoreType.DMA((14, total)),
            pltpu.SemaphoreType.DMA((14, 2)),
            pltpu.SemaphoreType.DMA((14, total)),
            pltpu.SemaphoreType.DMA((5,)),
            pltpu.SemaphoreType.DMA((5,)),
        ],
        compiler_params=pltpu.CompilerParams(
            collective_id=1, has_side_effects=True, vmem_limit_bytes=60 << 20
        ),
        name="reduce_gradients",
    )(*arrays, vec_sums, tail, root_left, right_half)


def split_float(values):
    high = values.astype(jnp.bfloat16)
    return high, (values - high.astype(jnp.float32)).astype(jnp.bfloat16)


def stacked_dot(lefts, right, contract_last):
    rows = lefts[0].shape[0]
    left = jnp.concatenate(lefts, 0) if len(lefts) > 1 else lefts[0]
    dims = (((1,), (1 if contract_last else 0,)), ((), ()))
    out = lax.dot_general(left, right, dims, preferred_element_type=jnp.float32)
    return [out[n * rows : (n + 1) * rows] for n in range(len(lefts))]


def precondition_block(
    own, codes_ref, scales_ref, left_ref, right_ref, outs_ref, squares_ref, high_ref, low_ref
):
    half, width = codes_ref.shape
    rows = left_ref.shape[0]
    own_rows = pl.ds(pl.multiple_of(own, PIECE), rows)
    for piece in range(half // PIECE):
        part = slice(piece * PIECE, (piece + 1) * PIECE)
        high_ref[part, :], low_ref[part, :] = split_float(
            decode(codes_ref[part, :], scales_ref[piece])
        )
    own_value = high_ref[own_rows, :].astype(jnp.float32) + low_ref[own_rows, :].astype(jnp.float32)
    outs_ref[0] = own_value
    squares_ref[0:1, :] = jnp.sum(own_value * own_value, 0, keepdims=True)
    picks = (
        lax.broadcasted_iota(jnp.int32, (rows, half), 1)
        == lax.broadcasted_iota(jnp.int32, (rows, half), 0) + own
    ).astype(jnp.float32).astype(jnp.bfloat16)
    for quad in range(2):
        cols = slice(quad * half, (quad + 1) * half)
        high, low = high_ref[:, cols], low_ref[:, cols]
        mine_high, mine_low = high_ref[own_rows, cols], low_ref[own_rows, cols]
        hh, lh, turned_high = stacked_dot([mine_high, mine_low, picks], high, True)
        hl, turned_low = stacked_dot([mine_high, picks], low, True)
        outs_ref[1, :, cols] = hh + (lh + hl)
        turned_high = turned_high.astype(jnp.bfloat16)
        turned_low = turned_low.astype(jnp.bfloat16)
        root_high, root_low = split_float(left_ref[:, cols])
        thh, tlh, rhh, rlh = stacked_dot([turned_high, turned_low, root_high, root_low], high, False)
        thl, rhl = stacked_dot([turned_high, root_high], low, False)
        outs_ref[2, :, cols] = thh + (tlh + thl)
        half_step = rhh + (rlh + rhl)
        step_high, step_low = split_float(half_step)
        right_high, right_low = split_float(right_ref[:, cols])
        shh, slh = stacked_dot([step_high, step_low], right_high, False)
        (shl,) = stacked_dot([step_high], right_low, False)
        direction = shh + (slh + shl)
        outs_ref[3, :, cols] = direction
        squares_ref[1:2, cols] = jnp.sum(direction * direction, 0, keepdims=True)


def class_sum_kernel(in_ref, out_ref, slots, send_sem, recv_sem):
    dp, cls = lax.axis_index("dp"), lax.axis_index("cls")
    total, rows = slots.shape[0], slots.shape[1]
    barrier = pltpu.get_barrier_semaphore()
    for n in range(1, total):
        pl.semaphore_signal(
            barrier, inc=1, device_id=(dp, lax.rem(cls + n, total)), device_id_type=MESH
        )
    pl.semaphore_wait(barrier, total - 1)

    def part(index):
        return in_ref.at[pl.ds(pl.multiple_of(index * rows, 8), rows)]

    def copy(n, slot):
        mate = lax.rem(cls + n, total)
        return pltpu.make_async_remote_copy(
            src_ref=part(mate), dst_ref=slots.at[slot],
            send_sem=send_sem.at[n], recv_sem=recv_sem.at[slot],
            device_id=(dp, mate), device_id_type=MESH,
        )

    for n in range(1, total):
        copy(n, cls).start()
    slots[cls] = part(cls)[...]
    for n in range(1, total):
        copy(n, cls).wait_send()
        copy(n, lax.rem(cls + n, total)).wait_recv()
    value = slots[0]
    for n in range(1, total):
        value = value + slots[n]
    out_ref[...] = value


def class_sum(values, cls_count):
    rows = values.shape[0] // cls_count
    vmem = pl.BlockSpec(memory_space=pltpu.VMEM)
    return pl.pallas_call(
        class_sum_kernel,
        out_shape=jax.ShapeDtypeStruct((rows, values.shape[1]), jnp.float32),
        in_specs=[vmem],
        out_specs=vmem,
        scratch_shapes=[
            pltpu.VMEM((cls_count, rows, values.shape[1]), jnp.float32),
            pltpu.SemaphoreType.DMA((cls_count,)),
            pltpu.SemaphoreType.DMA((cls_count,)),
        ],
        compiler_params=pltpu.CompilerParams(collective_id=2, has_side_effects=True),
        name="class_sum",
    )(values)


def gather_kernel(own_ref, vec_ref, out_ref, vec_out_ref, send_sem, recv_sem, copy_sem, vec_send, vec_recv):
    count, rows, width = own_ref.shape
    cols = width // 2
    z, y, x, core = torus_place()
    me = z * 2 + y
    mate_core = torus_device(z, y, x, 1 - core)
    mate_x = torus_device(z, y, 1 - x, core)
    mate_y = torus_device(z, 1 - y, x, core)
    mate_up = torus_device(jnp.minimum(z + 1, 3), y, x, core)
    mate_down = torus_device(jnp.maximum(z - 1, 0), y, x, core)
    has_up = z < 3
    has_down = z > 0

    def column_mate(n):
        other = lax.rem(me + n, SHARES)
        return torus_device(other // 2, lax.rem(other, 2), x, core)

    barrier = pltpu.get_barrier_semaphore()
    for mate in [mate_core, mate_x] + [column_mate(n) for n in range(1, SHARES)]:
        pl.semaphore_signal(barrier, inc=1, device_id=mate, device_id_type=MESH)
    pl.semaphore_wait(barrier, SHARES + 1)

    own_cols = pl.ds(pl.multiple_of(core * cols, 128), cols)
    other_cols = pl.ds(pl.multiple_of((1 - core) * cols, 128), cols)

    def vec_copy(n, slot):
        return pltpu.make_async_remote_copy(
            src_ref=vec_ref, dst_ref=vec_out_ref.at[slot],
            send_sem=vec_send.at[n], recv_sem=vec_recv.at[slot],
            device_id=column_mate(n), device_id_type=MESH,
        )

    for n in range(1, SHARES):
        vec_copy(n, me).start()
    vec_out_ref[me] = vec_ref[...]

    def share(m, zz, yy, start, size, columns=own_cols):
        begin = (zz * 2 + yy) * rows + start
        return out_ref.at[m, pl.ds(pl.multiple_of(begin, 16), size), columns]

    def copy(stage, m, source, target, mate):
        return pltpu.make_async_remote_copy(
            src_ref=source, dst_ref=target,
            send_sem=send_sem.at[stage, m % 2], recv_sem=recv_sem.at[stage, m],
            device_id=mate, device_id_type=MESH,
        )

    span_start = x * (rows - SPAN)
    lack = rows - SPAN
    lack_mine = x * SPAN
    lack_theirs = (1 - x) * SPAN

    def local(m):
        return pltpu.make_async_copy(
            own_ref.at[m, :, own_cols], share(m, z, y, 0, rows), copy_sem.at[m % 2]
        )

    def chain(m, turn, upward):
        origin = z - (turn - 1) if upward else z + (turn - 1)
        stage = (turn - 1) * 2 + (0 if upward else 1)
        target = share(m, origin, y, span_start, SPAN)
        if turn == 1:
            source = own_ref.at[m, pl.ds(pl.multiple_of(span_start, 16), SPAN), own_cols]
        else:
            source = target
        return copy(stage, m, source, target, mate_up if upward else mate_down)

    def chain_sends(turn, upward):
        if upward:
            return has_up & (z - (turn - 1) >= 0)
        return has_down & (z + (turn - 1) <= 3)

    def chain_comes(turn, upward):
        return (z - turn >= 0) if upward else (z + turn <= 3)

    def arriving(m, turn, upward):
        origin = z - turn if upward else z + turn
        stage = (turn - 1) * 2 + (0 if upward else 1)
        target = share(m, origin, y, span_start, SPAN)
        return copy(stage, m, target, target, mate_up)

    def patch_out(m, n):
        zz = lax.rem(z + n, 4)
        block = share(m, zz, y, lack_mine, lack)
        return copy(5 + n, m, block, block, mate_x)

    def patch_in(m, n):
        zz = lax.rem(z + n, 4)
        block = share(m, zz, y, lack_theirs, lack)
        return copy(5 + n, m, block, block, mate_x)

    def cross(m, n, yy, stage, plane, mate):
        block = share(m, plane * 2 + n, yy, 0, rows)
        return copy(stage + n, m, block, block, mate)

    def swap(m, columns):
        block = out_ref.at[m, :, columns]
        return copy(13, m, block, block, mate_core)

    def step(t, carry):
        @pl.when(t < count)
        def _():
            local(t).start()
            for upward in (True, False):
                @pl.when(chain_sends(1, upward))
                def _(upward=upward):
                    chain(t, 1, upward).start()

        for turn in (2, 3):
            @pl.when((t >= turn - 1) & (t < count + turn - 1))
            def _(turn=turn):
                m = t - (turn - 1)
                if turn == 2:
                    local(m).wait()
                for upward in (True, False):
                    @pl.when(chain_sends(turn - 1, upward))
                    def _(upward=upward):
                        chain(m, turn - 1, upward).wait_send()

                    @pl.when(chain_comes(turn - 1, upward))
                    def _(upward=upward):
                        arriving(m, turn - 1, upward).wait_recv()

                    @pl.when(chain_sends(turn, upward))
                    def _(upward=upward):
                        chain(m, turn, upward).start()

        @pl.when((t >= 3) & (t < count + 3))
        def _():
            m = t - 3
            for upward in (True, False):
                @pl.when(chain_sends(3, upward))
                def _(upward=upward):
                    chain(m, 3, upward).wait_send()

                @pl.when(chain_comes(3, upward))
                def _(upward=upward):
                    arriving(m, 3, upward).wait_recv()
            if lack:
                for n in range(1, 4):
                    patch_out(m, n).start()

        @pl.when((t >= 4) & (t < count + 4))
        def _():
            m = t - 4
            if lack:
                for n in range(1, 4):
                    patch_out(m, n).wait_send()
                    patch_in(m, n).wait_recv()
            for n in range(2):
                cross(m, n, y, 9, x, mate_y).start()

        @pl.when((t >= 5) & (t < count + 5))
        def _():
            m = t - 5
            for n in range(2):
                cross(m, n, y, 9, x, mate_y).wait_send()
                cross(m, n, 1 - y, 9, x, mate_y).wait_recv()
                cross(m, n, 1 - y, 11, x, mate_x).start()

        @pl.when((t >= 6) & (t < count + 6))
        def _():
            m = t - 6
            for n in range(2):
                cross(m, n, 1 - y, 11, x, mate_x).wait_send()
                cross(m, n, 1 - y, 11, 1 - x, mate_x).wait_recv()
            swap(m, own_cols).start()

        @pl.when((t >= 7) & (t < count + 7))
        def _():
            m = t - 7
            swap(m, own_cols).wait_send()
            swap(m, other_cols).wait_recv()

        return carry

    lax.fori_loop(0, count + 7, step, 0)
    for n in range(1, SHARES):
        vec_copy(n, me).wait_send()
        vec_copy(n, lax.rem(me + n, SHARES)).wait_recv()


def gather_weights(own, vec):
    count, rows, width = own.shape
    hbm = pl.BlockSpec(memory_space=pl.ANY)
    vmem = pl.BlockSpec(memory_space=pltpu.VMEM)
    return pl.pallas_call(
        gather_kernel,
        out_shape=(
            jax.ShapeDtypeStruct((count, SHARES * rows, width), own.dtype),
            jax.ShapeDtypeStruct((SHARES,) + vec.shape, vec.dtype),
        ),
        in_specs=[vmem, vmem],
        out_specs=(hbm, vmem),
        scratch_shapes=[
            pltpu.SemaphoreType.DMA((14, 2)),
            pltpu.SemaphoreType.DMA((14, count)),
            pltpu.SemaphoreType.DMA((2,)),
            pltpu.SemaphoreType.DMA((SHARES,)),
            pltpu.SemaphoreType.DMA((SHARES,)),
        ],
        compiler_params=pltpu.CompilerParams(
            collective_id=3, has_side_effects=True, vmem_limit_bytes=32 << 20
        ),
        name="gather_weights",
    )(own, vec)


def adam_step(weight, grad, first, second, count):
    first = BETA_FIRST * first + (1.0 - BETA_FIRST) * grad
    second = BETA_SECOND * second + (1.0 - BETA_SECOND) * grad * grad
    fix_first = 1.0 - jnp.power(BETA_FIRST, count)
    fix_second = 1.0 - jnp.power(BETA_SECOND, count)
    update = first / fix_first / (jnp.sqrt(second / fix_second) + ADAM_EPS) + WEIGHT_DECAY * weight
    return (weight - ADAM_RATE * update, first, second)


def split_halves(values, half_size):
    block_count, row_count, feature_dim = values.shape
    return values.reshape(block_count, row_count, 2, half_size)


def reduced_half(values, half_groups):
    part = lax.psum_scatter(values, ("dp", "cls"), scatter_dimension=1, tiled=True)
    return lax.all_gather(part, ("dp", "cls"), axis=1, tiled=True, axis_index_groups=half_groups)


def preconditioned_rows(grad_half, root_left, right_half, own_start):
    count, row_count, width = root_left.shape
    half_size = width // 2
    block_rows = lax.dynamic_slice_in_dim(grad_half, own_start, row_count, 1)
    grad_quads = split_halves(grad_half, half_size)
    rows_quads = split_halves(block_rows, half_size)
    cols_quads = lax.dynamic_slice_in_dim(grad_quads, own_start, row_count, 3)
    precise = FULL_PRECISION
    left_add = jnp.einsum("brjk,bljk->brjl", rows_quads, grad_quads, precision=precise)
    right_add = jnp.einsum("bkja,bkjm->bajm", cols_quads, grad_quads, precision=precise)
    direction = jnp.einsum(
        "brjk,bkjm->brjm", split_halves(root_left, half_size), grad_quads, precision=precise
    )
    direction = jnp.einsum(
        "brjk,bkjm->brjm", direction, split_halves(right_half, half_size), precision=precise
    )
    flat = (count, row_count, width)
    return left_add.reshape(flat), right_add.reshape(flat), direction.reshape(flat), block_rows


def on_device(
    patches,
    image_ids,
    keep,
    labels,
    owner,
    step,
    enc_weights,
    stats_left,
    stats_right,
    root_left,
    root_right,
    head_weights,
    head_m,
    head_v,
    vectors,
    vec_m,
    vec_v,
):
    dp_count = lax.axis_size("dp")
    cls_count = lax.axis_size("cls")
    dp_index = lax.axis_index("dp")
    cls_index = lax.axis_index("cls")
    block_count, row_count, feature_dim = enc_weights.shape
    up_count = (block_count - 5) // 2
    half_size = feature_dim // 2
    part_rows = row_count // cls_count
    half_dp = dp_count // 2
    half_group = half_dp * cls_count
    half_groups = [
        list(range(half_group)),
        list(range(half_group, 2 * half_group)),
    ]

    def my_part(values):
        return lax.dynamic_slice_in_dim(values, cls_index * part_rows, part_rows, 1)

    on_torus = dp_count == 8 and cls_count == 4
    if on_torus:
        vec_block = jnp.pad(vectors, ((0, -vectors.shape[0] % 8), (0, -row_count % 128)))
        blocks, vec_blocks = gather_weights(enc_weights.astype(jnp.bfloat16), vec_block)
        vec_low = jnp.transpose(vec_blocks[:, : vectors.shape[0], :row_count], (1, 0, 2))
        vec_all = lax.reduce_precision(vec_low.reshape(vectors.shape[0], feature_dim), 8, 7)
    else:
        blocks = lax.all_gather(
            my_part(enc_weights.astype(jnp.bfloat16)), ("dp", "cls"), axis=1, tiled=True
        )
        vec_low = lax.all_gather(vectors.astype(jnp.bfloat16), "dp", axis=1, tiled=True)
        vec_all = vec_low.astype(jnp.float32)
    head_low = lax.all_gather(head_weights.astype(jnp.bfloat16), "dp", axis=0, tiled=True)
    final_gain = vec_all[9 + up_count]
    final_shift = vec_all[10 + up_count]
    pack_ids, pack_keep = image_ids[0], keep[0]
    key_codes = jnp.where(pack_keep == 1, pack_ids, -1)

    output, saved = layer_forward(blocks, vec_all, patches, pack_ids, key_codes)
    right_part, output = lax.optimization_barrier((my_part(root_right), output))
    right_half = lax.all_gather(
        right_part, ("dp", "cls"), axis=1, tiled=True, axis_index_groups=half_groups
    )
    pooled = pool_rows(output, final_gain, final_shift, pack_ids, pack_keep)
    group = lax.all_gather(pooled.astype(jnp.bfloat16), "cls", axis=0, tiled=True)
    logits = jnp.dot(group, head_low, preferred_element_type=jnp.float32)
    class_dev = head_low.shape[1]
    class_ids = cls_index * class_dev + jnp.arange(class_dev)
    valid = class_ids[None, :] < LABELS_REAL
    target = jnp.any(labels[:, :, None] == class_ids[None, None, :], 1).astype(jnp.float32)
    image_total = labels.shape[0] * dp_count
    loss_part = (
        jnp.sum(jnp.where(valid, jax.nn.softplus(logits) - target * logits, 0.0)) / image_total
    )
    grad_logits = (jnp.where(valid, jax.nn.sigmoid(logits) - target, 0.0) / image_total).astype(
        jnp.bfloat16
    )
    group_grad = jnp.einsum("gc,dc->gd", grad_logits, head_low, preferred_element_type=jnp.float32)
    if on_torus:
        grad_pooled = class_sum(group_grad, cls_count)
    else:
        grad_pooled = lax.psum_scatter(group_grad, "cls", scatter_dimension=0, tiled=True)
    head_rows = lax.all_gather(
        jnp.concatenate([group, grad_logits], 1), "dp", axis=0, tiled=True
    )
    pooled_all, grad_logits_all = head_rows[:, :feature_dim], head_rows[:, feature_dim:]
    pooled_mine = lax.dynamic_slice_in_dim(pooled_all, dp_index * row_count, row_count, 1)
    head_grad = jnp.einsum(
        "gr,gc->rc", pooled_mine, grad_logits_all, preferred_element_type=jnp.float32
    )

    def pool_local(rows_in, gain, shift):
        return pool_rows(rows_in, gain, shift, pack_ids, pack_keep)

    pool_back = jax.vjp(pool_local, output, final_gain, final_shift)[1]
    grad_output, grad_gain, grad_shift = pool_back(grad_pooled)
    grad_arrays, grad_vectors = layer_backward(
        blocks,
        vec_all,
        patches,
        saved,
        pack_ids,
        key_codes,
        grad_output,
        grad_gain,
        grad_shift,
    )

    head_squares = jnp.sum(head_grad * head_grad)
    if on_torus:
        padded = jnp.pad(grad_vectors, ((0, -grad_vectors.shape[0] % 8), (0, 0)))
        tail = jnp.pad(jnp.stack([head_squares, loss_part])[:, None], ((0, 6), (0, 127)))
        block_rows, left_add, right_add, direction, sums, tail, vector_sum = reduce_gradients(
            grad_arrays, padded, tail, root_left, right_half, dp_count, cls_count
        )
        vector_sum = vector_sum[: grad_vectors.shape[0]]
        loss = tail[1, 0]
        all_squares = jnp.sum(tail[0])
        block_squares = jnp.sum(sums[: 2 * block_count], -1).reshape(block_count, 2)
    else:
        grad_half = reduced_half(jnp.concatenate(grad_arrays, 0), half_groups)
        vector_sum = lax.psum(grad_vectors, ("dp", "cls"))
        left_add, right_add, direction, block_rows = preconditioned_rows(
            grad_half, root_left, right_half, (dp_index % half_dp) * row_count
        )
        squares = jnp.sum(split_halves(direction * direction, half_size), (1, 3))
        in_top = (dp_index < half_dp).astype(jnp.float32)
        once = (cls_index == 0).astype(jnp.float32)
        all_squares = head_squares + once * jnp.sum(block_rows * block_rows)
        packed = jnp.concatenate(
            [
                (once * in_top * squares).reshape(-1),
                (once * (1.0 - in_top) * squares).reshape(-1),
                jnp.stack([all_squares, loss_part]),
            ]
        )
        packed = lax.psum(packed, ("dp", "cls"))
        loss = packed[4 * block_count + 1]
        all_squares = packed[4 * block_count]
        sums = packed[: 4 * block_count].reshape(2, block_count, 2)
        block_squares = jnp.where(dp_index < half_dp, sums[0], sums[1])
    vector_rows = lax.dynamic_slice_in_dim(vector_sum, dp_index * row_count, row_count, 1)
    grad_norm = jnp.sqrt(all_squares + jnp.sum(vector_sum * vector_sum))
    factor = CLIP_NORM / jnp.maximum(grad_norm, CLIP_NORM)
    mean_squares = block_squares / (half_size * half_size)
    mean_squares = mean_squares * factor * factor
    scale = factor * lax.rsqrt(mean_squares + ROOT_EPS)
    wide_scale = jnp.repeat(SHAMPOO_RATE * scale, half_size, axis=1)
    new_blocks = enc_weights - direction * wide_scale[:, None, :]
    square_factor = 0.5 * factor * factor
    new_left = 0.5 * stats_left + square_factor * left_add
    new_right = 0.5 * stats_right + square_factor * right_add
    count = step.astype(jnp.float32)
    new_vec, new_vec_m, new_vec_v = adam_step(vectors, vector_rows * factor, vec_m, vec_v, count)
    new_head, new_head_m, new_head_v = adam_step(
        head_weights, head_grad * factor, head_m, head_v, count
    )
    return (
        loss,
        grad_norm,
        new_blocks,
        block_rows * factor,
        new_left,
        new_right,
        new_vec,
        new_vec_m,
        new_vec_v,
        new_head,
        new_head_m,
        new_head_v,
    )


def solution(mesh):
    return jax.shard_map(
        on_device,
        mesh=mesh,
        in_specs=(
            P(("dp", "cls"), None),
            P(("dp", "cls"), None),
            P(("dp", "cls"), None),
            P("dp", None),
            P(),
            P(),
            P(None, "dp", None),
            P(None, "dp", None),
            P(None, "dp", None),
            P(None, "dp", None),
            P(None, "dp", None),
            P("dp", "cls"),
            P("dp", "cls"),
            P("dp", "cls"),
            P(None, "dp"),
            P(None, "dp"),
            P(None, "dp"),
        ),
        out_specs=(
            P(),
            P(),
            P(None, "dp", None),
            P(None, "dp", None),
            P(None, "dp", None),
            P(None, "dp", None),
            P(None, "dp"),
            P(None, "dp"),
            P(None, "dp"),
            P("dp", "cls"),
            P("dp", "cls"),
            P("dp", "cls"),
        ),
        check_vma=False,
    )
```

```python
import functools

import jax
import jax.numpy as jnp
from jax import lax
from jax.experimental import pallas as pl
from jax.experimental.pallas import tpu as pltpu
from jax.sharding import PartitionSpec as P

HEADS = 12
HEAD = 64
LABELS_REAL = 21843
IMAGE_MAX = 196
QTILE = 256
PAIR = 2 * HEAD
ROWS = 256
HIDDEN_TILE = 384
MESH = pl.DeviceIdType.MESH
CODE_TOP = 32766.0
CODE_FLOOR = 1e-33
PIECE = 48
SPAN = 48
SHARES = 8
GATHER_DEPTH = 7
IMG_PACK = 8


FULL_PRECISION = lax.Precision.HIGHEST
NORM_EPS = 1e-06
CLIP_NORM = 1.0
ADAM_RATE = 0.02
SHAMPOO_RATE = 0.01
BETA_FIRST = 0.9
BETA_SECOND = 0.999
ADAM_EPS = 1e-08
WEIGHT_DECAY = 0.1
ROOT_EPS = 1e-06


def norm_rows(values, gain, shift):
    centred = values - jnp.mean(values, -1, keepdims=True)
    spread = jnp.mean(centred * centred, -1, keepdims=True)
    return centred * lax.rsqrt(spread + NORM_EPS) * gain + shift


def pool_rows(output, gain, shift, pack_ids, pack_keep):
    final = norm_rows(output, gain, shift)
    member = (
        (pack_ids[None, :] == jnp.arange(IMG_PACK)[:, None]) & (pack_keep[None, :] == 1)
    ).astype(jnp.float32)
    counted = jnp.maximum(jnp.sum(member, 1), 1.0)
    return jnp.dot(member, final, precision=FULL_PRECISION) / counted[:, None]


def key_window(tile, length):
    reach = -(-(IMAGE_MAX - 1) // 128) * 128
    low = max(0, tile * QTILE - reach)
    high = min(length, (tile + 1) * QTILE + reach)
    return low, high


def attention_bias(qids_ref, kcodes_ref, bias_ref):
    length = qids_ref.shape[0]

    @pl.when(pl.program_id(0) == 0)
    def _():
        for tile in range(length // QTILE):
            low, high = key_window(tile, length)
            shape = (QTILE, high - low)
            rows = lax.broadcasted_iota(jnp.int32, shape, 0) + tile * QTILE
            cols = lax.broadcasted_iota(jnp.int32, shape, 1) + low
            same = qids_ref[tile * QTILE : (tile + 1) * QTILE, :] == kcodes_ref[:, low:high]
            bias_ref[tile, :, : high - low] = jnp.where(same | (rows == cols), 0.0, -1e30)


def attention_tile(tile, q_ref, k_ref, v_ref, out_ref, bias_ref):
    lane = lax.broadcasted_iota(jnp.int32, (QTILE, PAIR), 1)
    low, high = key_window(tile, q_ref.shape[0])
    rows = pl.ds(tile * QTILE, QTILE)
    queries = q_ref[rows, :] * jnp.bfloat16(HEAD ** (-0.5))
    keys = k_ref[low:high, :]
    values = v_ref[low:high, :]
    halves = []
    for head in range(2):
        mine = (lane >= head * HEAD) & (lane < (head + 1) * HEAD)
        picked = jnp.where(mine, queries, jnp.zeros_like(queries))
        scores = lax.dot_general(
            picked, keys, (((1,), (1,)), ((), ())), preferred_element_type=jnp.float32
        )
        scores = scores + bias_ref[tile, :, : high - low]
        top = jnp.max(scores, -1, keepdims=True)
        weights = jnp.exp(scores - top)
        probs = weights * (1.0 / jnp.sum(weights, -1, keepdims=True))
        halves.append(
            jnp.dot(probs.astype(jnp.bfloat16), values, preferred_element_type=jnp.float32)
        )
    out_ref[rows, :] = jnp.where(lane < HEAD, halves[0], halves[1]).astype(jnp.bfloat16)


def attention_forward_kernel(qids_ref, kcodes_ref, q_ref, k_ref, v_ref, out_ref, bias_ref):
    attention_bias(qids_ref, kcodes_ref, bias_ref)
    for tile in range(q_ref.shape[0] // QTILE):
        attention_tile(tile, q_ref, k_ref, v_ref, out_ref, bias_ref)


def attention_backward_kernel(
    qids_ref, kcodes_ref, q_ref, k_ref, v_ref, do_ref, out_ref, bias_ref, dk_ref, dv_ref
):
    length = q_ref.shape[0]
    lane = lax.broadcasted_iota(jnp.int32, (QTILE, PAIR), 1)
    scale = jnp.bfloat16(HEAD ** (-0.5))

    @pl.when(pl.program_id(0) == 0)
    def _():
        for tile in range(length // QTILE):
            low, high = key_window(tile, length)
            shape = (high - low, QTILE)
            rows = lax.broadcasted_iota(jnp.int32, shape, 0) + low
            cols = lax.broadcasted_iota(jnp.int32, shape, 1) + tile * QTILE
            same = kcodes_ref[low:high, :] == qids_ref[:, tile * QTILE : (tile + 1) * QTILE]
            bias_ref[tile, : high - low, :] = jnp.where(same | (rows == cols), 0.0, -1e30)

    dk_ref[...] = jnp.zeros_like(dk_ref)
    dv_ref[...] = jnp.zeros_like(dv_ref)
    for tile in range(length // QTILE):
        low, high = key_window(tile, length)
        rows = pl.ds(tile * QTILE, QTILE)
        window = pl.ds(low, high - low)
        queries = q_ref[rows, :] * scale
        keys = k_ref[window, :]
        values = v_ref[window, :]
        grads = do_ref[rows, :]
        halves = []
        for head in range(2):
            mine = (lane >= head * HEAD) & (lane < (head + 1) * HEAD)
            picked = jnp.where(mine, queries, jnp.zeros_like(queries))
            picked_grads = jnp.where(mine, grads, jnp.zeros_like(grads))
            scores = lax.dot_general(
                keys, picked, (((1,), (1,)), ((), ())), preferred_element_type=jnp.float32
            )
            scores = scores + bias_ref[tile, : high - low, :]
            top = jnp.max(scores, 0, keepdims=True)
            weights = jnp.exp(scores - top)
            probs = weights * (1.0 / jnp.sum(weights, 0, keepdims=True))
            grad_probs = lax.dot_general(
                values, picked_grads, (((1,), (1,)), ((), ())), preferred_element_type=jnp.float32
            )
            inner = jnp.sum(probs * grad_probs, 0, keepdims=True)
            grad_scores = (probs * (grad_probs - inner)).astype(jnp.bfloat16)
            dv_ref[window, :] += jnp.dot(
                probs.astype(jnp.bfloat16), picked_grads, preferred_element_type=jnp.float32
            )
            dk_ref[window, :] += jnp.dot(
                grad_scores, picked, preferred_element_type=jnp.float32
            )
            halves.append(
                lax.dot_general(
                    grad_scores,
                    keys,
                    (((0,), (0,)), ((), ())),
                    preferred_element_type=jnp.float32,
                )
            )
        grad_queries = jnp.where(lane < HEAD, halves[0], halves[1]) * HEAD ** (-0.5)
        out_ref[0, rows, :] = grad_queries.astype(jnp.bfloat16)
    out_ref[1] = dk_ref[...].astype(jnp.bfloat16)
    out_ref[2] = dv_ref[...].astype(jnp.bfloat16)


def pair_spec(length, part=None):
    if part is None:
        return pl.BlockSpec((length, PAIR), lambda pair: (0, pair))
    return pl.BlockSpec((None, length, PAIR), lambda pair: (part, 0, pair))


def whole_spec(shape):
    return pl.BlockSpec(shape, lambda pair: (0,) * len(shape))


def bias_shape(length):
    tiles = length // QTILE
    window = max(high - low for low, high in (key_window(t, length) for t in range(tiles)))
    return tiles, QTILE, window


def attention_forward(qkv_rows, pack_ids, key_codes):
    _, length, width = qkv_rows.shape
    return pl.pallas_call(
        attention_forward_kernel,
        grid=(width // PAIR,),
        out_shape=jax.ShapeDtypeStruct((length, width), jnp.bfloat16),
        in_specs=[whole_spec((length, 1)), whole_spec((1, length))]
        + [pair_spec(length, part) for part in range(3)],
        out_specs=pair_spec(length),
        scratch_shapes=[pltpu.VMEM(bias_shape(length), jnp.float32)],
        compiler_params=pltpu.CompilerParams(vmem_limit_bytes=40 << 20),
        name="attention_forward",
    )(pack_ids[:, None], key_codes[None, :], qkv_rows, qkv_rows, qkv_rows)


def attention_backward(qkv_rows, pack_ids, key_codes, grad_attended):
    _, length, width = qkv_rows.shape
    tiles = length // QTILE
    window = max(high - low for low, high in (key_window(t, length) for t in range(tiles)))
    return pl.pallas_call(
        attention_backward_kernel,
        grid=(width // PAIR,),
        out_shape=jax.ShapeDtypeStruct((3, length, width), jnp.bfloat16),
        in_specs=[whole_spec((1, length)), whole_spec((length, 1))]
        + [pair_spec(length, part) for part in range(3)]
        + [pair_spec(length)],
        out_specs=pl.BlockSpec((3, length, PAIR), lambda pair: (0, 0, pair)),
        scratch_shapes=[
            pltpu.VMEM((tiles, window, QTILE), jnp.float32),
            pltpu.VMEM((length, PAIR), jnp.float32),
            pltpu.VMEM((length, PAIR), jnp.float32),
        ],
        compiler_params=pltpu.CompilerParams(vmem_limit_bytes=40 << 20),
        name="attention_backward",
    )(pack_ids[None, :], key_codes[:, None], qkv_rows, qkv_rows, qkv_rows, grad_attended)


def mlp_forward_kernel(x_ref, up_ref, bias_ref, down_ref, units_ref, slope_ref, out_ref):
    first = pl.program_id(0) == 0

    @pl.when(first)
    def _():
        out_ref[...] = jnp.zeros_like(out_ref)

    for start in range(0, x_ref.shape[0], ROWS):
        rows = pl.ds(start, ROWS)
        pre = jnp.dot(x_ref[rows, :], up_ref[...], preferred_element_type=jnp.float32)
        pre = pre + bias_ref[...]
        half = 0.5 + 0.5 * lax.erf(pre * 0.7071067811865476)
        bell = jnp.exp(-0.5 * pre * pre) * 0.3989422804014327
        units = (pre * half).astype(jnp.bfloat16)
        units_ref[rows, :] = units
        slope_ref[rows, :] = half + pre * bell
        out_ref[rows, :] += jnp.dot(units, down_ref[...], preferred_element_type=jnp.float32)


def mlp_backward_kernel(
    x_ref, dm_ref, up_ref, down_ref, units_ref, slope_ref,
    grad_up_ref, grad_down_ref, bias_ref, dx_ref, dpre_ref
):
    @pl.when(pl.program_id(0) == 0)
    def _():
        dx_ref[...] = jnp.zeros_like(dx_ref)

    total = jnp.zeros((1, HIDDEN_TILE), jnp.float32)
    for start in range(0, x_ref.shape[0], ROWS):
        rows = pl.ds(start, ROWS)
        units_back = lax.dot_general(
            dm_ref[rows, :], down_ref[...], (((1,), (1,)), ((), ())),
            preferred_element_type=jnp.float32,
        )
        grad_pre = (units_back * slope_ref[rows, :]).astype(jnp.bfloat16)
        dpre_ref[rows, :] = grad_pre
        total = total + jnp.sum(grad_pre.astype(jnp.float32), 0, keepdims=True)
        dx_ref[rows, :] += lax.dot_general(
            grad_pre, up_ref[...], (((1,), (1,)), ((), ())), preferred_element_type=jnp.float32
        )
    bias_ref[...] = total
    over_rows = (((0,), (0,)), ((), ()))
    grad_down_ref[...] = lax.dot_general(
        units_ref[...], dm_ref[...], over_rows, preferred_element_type=jnp.float32
    )
    grad_up_ref[...] = lax.dot_general(
        x_ref[...], dpre_ref[...], over_rows, preferred_element_type=jnp.float32
    )


def mlp_specs(length, width, up_count):
    split = width // HIDDEN_TILE
    resident = pl.BlockSpec((length, width), lambda t: (0, 0))
    up = pl.BlockSpec((None, width, HIDDEN_TILE), lambda t: (t // split, 0, t % split))
    down = pl.BlockSpec(
        (None, HIDDEN_TILE, width), lambda t: (up_count + t // split, t % split, 0)
    )
    hidden = pl.BlockSpec((length, HIDDEN_TILE), lambda t: (0, t))
    bias = pl.BlockSpec((1, HIDDEN_TILE), lambda t: (0, t))
    return split, resident, up, down, hidden, bias


def mlp_forward(rows, blocks, up_bias):
    length, width = rows.shape
    up_count = blocks.shape[0] // 2
    split, resident, up, down, hidden, bias = mlp_specs(length, width, up_count)
    hidden_size = up_count * width
    return pl.pallas_call(
        mlp_forward_kernel,
        grid=(up_count * split,),
        out_shape=(
            jax.ShapeDtypeStruct((length, hidden_size), jnp.bfloat16),
            jax.ShapeDtypeStruct((length, hidden_size), jnp.float32),
            jax.ShapeDtypeStruct((length, width), jnp.float32),
        ),
        in_specs=[resident, up, bias, down],
        out_specs=(hidden, hidden, resident),
        compiler_params=pltpu.CompilerParams(vmem_limit_bytes=48 << 20),
        name="mlp_forward",
    )(rows, blocks, up_bias.reshape(1, hidden_size), blocks)


def mlp_backward(rows, grad_branch, blocks, units, slopes):
    length, width = rows.shape
    up_count = blocks.shape[0] // 2
    split, resident, up, down, hidden, bias = mlp_specs(length, width, up_count)
    hidden_size = up_count * width
    return pl.pallas_call(
        mlp_backward_kernel,
        grid=(up_count * split,),
        out_shape=(
            jax.ShapeDtypeStruct((up_count, width, width), jnp.float32),
            jax.ShapeDtypeStruct((up_count, width, width), jnp.float32),
            jax.ShapeDtypeStruct((1, hidden_size), jnp.float32),
            jax.ShapeDtypeStruct((length, width), jnp.float32),
        ),
        in_specs=[resident, resident, up, down, hidden, hidden],
        out_specs=(
            pl.BlockSpec((None, width, HIDDEN_TILE), lambda t: (t // split, 0, t % split)),
            pl.BlockSpec((None, HIDDEN_TILE, width), lambda t: (t // split, t % split, 0)),
            bias,
            resident,
        ),
        scratch_shapes=[pltpu.VMEM((length, HIDDEN_TILE), jnp.bfloat16)],
        compiler_params=pltpu.CompilerParams(vmem_limit_bytes=48 << 20),
        name="mlp_backward",
    )(rows, grad_branch, blocks, blocks, units, slopes)


def layer_forward(blocks, vec_all, patch, attend):
    embedded = jnp.dot(patch, blocks[0], preferred_element_type=jnp.float32) + vec_all[0]
    normed_one = norm_rows(embedded, vec_all[1], vec_all[2]).astype(jnp.bfloat16)
    qkv_rows = jnp.einsum(
        "td,kde->kte", normed_one, blocks[1:4], preferred_element_type=jnp.float32
    )
    qkv_bias = jnp.stack([vec_all[3], jnp.zeros_like(vec_all[3]), vec_all[4]])
    qkv_rows = (qkv_rows + qkv_bias[:, None, :]).astype(jnp.bfloat16)
    attended, mlp_blocks = attend(qkv_rows)
    up_count = mlp_blocks.shape[0] // 2
    hidden = (
        embedded + jnp.dot(attended, blocks[4], preferred_element_type=jnp.float32) + vec_all[5]
    )
    normed_two = norm_rows(hidden, vec_all[6], vec_all[7]).astype(jnp.bfloat16)
    units, slopes, branch = mlp_forward(normed_two, mlp_blocks, vec_all[8 : 8 + up_count])
    output = hidden + branch + vec_all[8 + up_count]
    return (
        output,
        mlp_blocks,
        (embedded, normed_one, qkv_rows, attended, hidden, normed_two, slopes, units),
    )


def layer_backward(
    blocks,
    mlp_blocks,
    vec_all,
    patch,
    saved,
    pack_ids,
    key_codes,
    grad_output,
    grad_gain,
    grad_shift,
):
    embedded, normed_one, qkv_rows, attended, hidden, normed_two, slopes, units = saved
    feature_dim = patch.shape[1]
    up_count = mlp_blocks.shape[0] // 2
    grad_branch = grad_output.astype(jnp.bfloat16)
    grad_up, grad_down, up_sums, grad_normed_two = mlp_backward(
        normed_two, grad_branch, mlp_blocks, units, slopes
    )
    norm_two_back = jax.vjp(norm_rows, hidden, vec_all[6], vec_all[7])[1]
    grad_hidden_norm, grad_gain_two, grad_shift_two = norm_two_back(grad_normed_two)
    grad_hidden = grad_output + grad_hidden_norm
    grad_attn_out = grad_hidden.astype(jnp.bfloat16)
    grad_out_proj = jnp.einsum(
        "te,td->ed", attended, grad_attn_out, preferred_element_type=jnp.float32
    )
    grad_attended = jnp.einsum(
        "td,ed->te", grad_attn_out, blocks[4], preferred_element_type=jnp.float32
    ).astype(jnp.bfloat16)
    grad_qkv = attention_backward(qkv_rows, pack_ids, key_codes, grad_attended)
    grad_qkv_proj = jnp.einsum(
        "td,kte->kde", normed_one, grad_qkv, preferred_element_type=jnp.float32
    )
    grad_normed_one = jnp.einsum(
        "kte,kde->td", grad_qkv, blocks[1:4], preferred_element_type=jnp.float32
    )
    norm_one_back = jax.vjp(norm_rows, embedded, vec_all[1], vec_all[2])[1]
    grad_embed_norm, grad_gain_one, grad_shift_one = norm_one_back(grad_normed_one)
    grad_embedded = (grad_hidden + grad_embed_norm).astype(jnp.bfloat16)
    grad_patch = jnp.einsum("tp,td->pd", patch, grad_embedded, preferred_element_type=jnp.float32)
    grad_arrays = (grad_patch[None], grad_qkv_proj, grad_out_proj[None], grad_up, grad_down)
    bias_sums = jnp.stack(
        [
            jnp.sum(grad_embedded.astype(jnp.float32), 0),
            grad_gain_one,
            grad_shift_one,
            jnp.sum(grad_qkv[0].astype(jnp.float32), 0),
            jnp.sum(grad_qkv[2].astype(jnp.float32), 0),
            jnp.sum(grad_attn_out.astype(jnp.float32), 0),
            grad_gain_two,
            grad_shift_two,
        ]
    )
    up_sums = up_sums.reshape(up_count, feature_dim)
    tail_sums = jnp.stack([jnp.sum(grad_branch.astype(jnp.float32), 0), grad_gain, grad_shift])
    return (grad_arrays, jnp.concatenate([bias_sums, up_sums, tail_sums], 0))


def torus_place():
    dp, cls = lax.axis_index("dp"), lax.axis_index("cls")
    return dp // 2, dp % 2, cls // 2, cls % 2


def torus_device(z, y, x, core):
    return (z * 2 + y, x * 2 + core)


def encode(pieces, code_refs, scale_ref):
    top = None
    for piece in pieces:
        peak = jnp.max(jnp.abs(piece()), 0, keepdims=True)
        top = peak if top is None else jnp.maximum(top, peak)
    top = jnp.maximum(top, CODE_FLOOR)
    inverse = CODE_TOP / top
    for piece, code_ref in zip(pieces, code_refs):
        code_ref[...] = jnp.round(piece() * inverse).astype(jnp.int32).astype(jnp.int16)
    scale_ref[...] = top * (1.0 / CODE_TOP)


def decode(code, scale):
    return code.astype(jnp.int32).astype(jnp.float32) * scale


def reduce_kernel(counts, *refs):
    sources, refs = refs[: len(counts)], refs[len(counts) :]
    (vec_ref, tail_ref, left_hbm, right_hbm,
     own_hbm, left_out_hbm, right_out_hbm, step_hbm, sums_ref, tail_out_ref, vec_out_ref,
     left_buf, right_buf, outs_buf, squares, high_buf, low_buf, sum_slots, tail_slots,
     in_sem, sum_send, sum_recv, tail_send, tail_recv,
     acc, spare, kept, sent0, got0, sent1, got1, sent2, got2, sent3, got3, sent4, got4,
     ss0, gs0, ss1, gs1, ss2, gs2, ss3, gs3, ss4, gs4, codes, scales, vec_got,
     load_sem, out_sem, send_sem, recv_sem, send_scale_sem, recv_scale_sem,
     vec_send_sem, vec_recv_sem) = refs
    total = sum(counts)
    half, width = codes.shape[1], codes.shape[2]
    cols = width // 2
    z, y, x, core = torus_place()
    upper = z // 2
    inner = (z % 2) != upper
    mate_core = torus_device(z, y, x, 1 - core)
    mate_x = torus_device(z, y, 1 - x, core)
    mate_y = torus_device(z, 1 - y, x, core)
    mate_z = torus_device(z + 1 - 2 * (z % 2), y, x, core)
    mate_mid = torus_device(3 - z, y, x, core)
    mate_far = torus_device((z + 2) % 4, y, x, core)

    barrier = pltpu.get_barrier_semaphore()
    dp, cls = lax.axis_index("dp"), lax.axis_index("cls")
    everyone = tail_slots.shape[0]
    quarter = sum_slots.shape[0]
    me = dp * 4 + cls

    def any_mate(n):
        other = lax.rem(me + n, everyone)
        return (other // 4, lax.rem(other, 4))

    def half_mate(n):
        return (upper * quarter + lax.rem(dp + n, quarter), cls)

    for n in range(1, everyone):
        pl.semaphore_signal(barrier, inc=1, device_id=any_mate(n), device_id_type=MESH)
    pl.semaphore_wait(barrier, everyone - 1)
    own = lax.rem(dp, quarter) * left_buf.shape[1]

    own_cols = pl.ds(pl.multiple_of(core * cols, 128), cols)
    other_cols = pl.ds(pl.multiple_of((1 - core) * cols, 128), cols)

    def rows_at(start, size):
        return pl.ds(pl.multiple_of(start, PIECE), size)

    def loads(m, body):
        start = 0
        for source, count in zip(sources, counts):
            def one(source=source, start=start):
                pair = (
                    pltpu.make_async_copy(
                        source.at[m - start, :, own_cols], acc.at[m % 5], load_sem.at[m % 2, 0]
                    ),
                    pltpu.make_async_copy(
                        source.at[m - start, :, other_cols], spare.at[m % 2], load_sem.at[m % 2, 1]
                    ),
                )
                for copy in pair:
                    body(copy)

            pl.when((m >= start) & (m < start + count))(one)
            start += count

    def message(stage, m, source, scale_source, target, scale_target, mate):
        return (
            pltpu.make_async_remote_copy(
                src_ref=source, dst_ref=target,
                send_sem=send_sem.at[stage, m % 2], recv_sem=recv_sem.at[stage, m],
                device_id=mate, device_id_type=MESH,
            ),
            pltpu.make_async_remote_copy(
                src_ref=scale_source, dst_ref=scale_target,
                send_sem=send_scale_sem.at[stage, m % 2], recv_sem=recv_scale_sem.at[stage, m],
                device_id=mate, device_id_type=MESH,
            ),
        )

    def first(m):
        return message(0, m, sent0.at[m % 2], ss0.at[m % 2], got0.at[m], gs0.at[m], mate_core)

    def second(m, b):
        return message(
            1 + b, m, sent1.at[m % 2, b], ss1.at[m % 2, b], got1.at[m, b], gs1.at[m, b],
            mate_y if b else mate_x,
        )

    def third(m, b):
        return message(
            3 + b, m, sent2.at[m % 2, b], ss2.at[m % 2, b], got2.at[m, b], gs2.at[m, b],
            mate_x if b else mate_y,
        )

    def fourth(m):
        return message(5, m, sent3.at[m % 2], ss3.at[m % 2], got3.at[m], gs3.at[m], mate_z)

    def fifth(m):
        return message(6, m, sent4.at[m % 2], ss4.at[m % 2], got4.at[m], gs4.at[m], mate_mid)

    piece_a = 2 * x + y
    piece_b = 4 + 2 * y + x

    def spread(stage, m, piece, count, mate, columns=own_cols):
        rows = pl.ds(pl.multiple_of(piece * PIECE, PIECE), count * PIECE)
        block = codes.at[m, rows, columns]
        scale = scales.at[m, pl.ds(piece, count), :, columns]
        return message(stage, m, block, scale, block, scale, mate)

    def start(copies):
        for copy in copies:
            copy.start()

    def wait_send(copies):
        for copy in copies:
            copy.wait_send()

    def wait_recv(copies):
        for copy in copies:
            copy.wait_recv()

    def vec_copy(step, mate):
        return pltpu.make_async_remote_copy(
            src_ref=vec_got.at[step, 0], dst_ref=vec_got.at[step, 1],
            send_sem=vec_send_sem.at[step], recv_sem=vec_recv_sem.at[step],
            device_id=mate, device_id_type=MESH,
        )

    vec_mates = (mate_core, mate_x, mate_y, mate_z, mate_far)

    loads(jnp.int32(0), lambda copy: copy.start())
    vec_got[0, 0] = vec_ref[...]
    vec_copy(0, vec_mates[0]).start()

    def step(t, carry):
        for n in range(1, 6):
            @pl.when(t == n)
            def _(n=n):
                vec_copy(n - 1, vec_mates[n - 1]).wait()
                value = vec_got[n - 1, 0] + vec_got[n - 1, 1]
                if n < 5:
                    vec_got[n, 0] = value
                    vec_copy(n, vec_mates[n]).start()
                else:
                    vec_out_ref[...] = value

        @pl.when(t < total)
        def _():
            m = t
            loads(m, lambda copy: copy.wait())

            @pl.when(m + 1 < total)
            def _():
                loads(m + 1, lambda copy: copy.start())

            span = 2 * PIECE
            encode(
                [lambda r=r: spare[m % 2, r : r + span, :] for r in range(0, 2 * half, span)],
                [sent0.at[m % 2, r : r + span, :] for r in range(0, 2 * half, span)],
                ss0.at[m % 2],
            )
            start(first(m))

        @pl.when((t >= 1) & (t < total + 1))
        def _():
            m = t - 1
            copies = first(m)
            wait_send(copies)
            wait_recv(copies)
            slot = m % 5
            span = 2 * PIECE
            for r in range(0, 2 * half, span):
                acc[slot, r : r + span, :] += decode(got0[m, r : r + span, :], gs0[m])
            for b in range(2):
                other = (1 - y) if b else (1 - x)
                begins = [h * half + b * 4 * PIECE + other * span for h in range(2)]
                encode(
                    [lambda s=s: acc[slot, rows_at(s, span), :] for s in begins],
                    [sent1.at[m % 2, b, h] for h in range(2)],
                    ss1.at[m % 2, b],
                )
                start(second(m, b))

        @pl.when((t >= 2) & (t < total + 2))
        def _():
            m = t - 2
            slot = m % 5
            span = 2 * PIECE
            for b in range(2):
                copies = second(m, b)
                wait_send(copies)
                wait_recv(copies)
                mine = y if b else x
                other = (1 - x) if b else (1 - y)
                begins = [h * half + b * 4 * PIECE + mine * span for h in range(2)]
                for h, s in enumerate(begins):
                    acc[slot, rows_at(s, span), :] += decode(got1[m, b, h], gs1[m, b])
                encode(
                    [lambda s=s: acc[slot, rows_at(s + other * PIECE, PIECE), :] for s in begins],
                    [sent2.at[m % 2, b, h] for h in range(2)],
                    ss2.at[m % 2, b],
                )
                start(third(m, b))

        @pl.when((t >= 3) & (t < total + 3))
        def _():
            m = t - 3
            slot = m % 5
            for b in range(2):
                copies = third(m, b)
                wait_send(copies)
                wait_recv(copies)
                place = piece_b if b else piece_a
                for h in range(2):
                    kept[m % 3, h, b] = acc[
                        slot, rows_at(h * half + place * PIECE, PIECE), :
                    ] + decode(got2[m, b, h], gs2[m, b])

            @pl.when(jnp.logical_not(inner))
            def _():
                pairs = [(h, b) for h in range(2) for b in range(2)]
                encode(
                    [lambda h=h, b=b: kept[m % 3, h, b] for h, b in pairs],
                    [sent3.at[m % 2, h, b] for h, b in pairs],
                    ss3.at[m % 2],
                )
                start(fourth(m))

        @pl.when((t >= 4) & (t < total + 4))
        def _():
            m = t - 4
            copies = fourth(m)

            @pl.when(jnp.logical_not(inner))
            def _():
                wait_send(copies)

            @pl.when(inner)
            def _():
                wait_recv(copies)
                for h in range(2):
                    for b in range(2):
                        kept[m % 3, h, b] += decode(got3[m, h, b], gs3[m])
                encode(
                    [lambda b=b: kept[m % 3, 1 - upper, b] for b in range(2)],
                    [sent4.at[m % 2, b] for b in range(2)],
                    ss4.at[m % 2],
                )
                start(fifth(m))

        @pl.when((t >= 5) & (t < total + 5))
        def _():
            m = t - 5

            @pl.when(inner)
            def _():
                copies = fifth(m)
                wait_send(copies)
                wait_recv(copies)
                for b in range(2):
                    place = piece_b if b else piece_a
                    value = kept[m % 3, upper, b] + decode(got4[m, b], gs4[m])
                    encode(
                        [lambda value=value: value],
                        [codes.at[m, rows_at(place * PIECE, PIECE), own_cols]],
                        scales.at[m, place, :, own_cols],
                    )
                    start(spread(7 + b, m, place, 1, mate_z))

        @pl.when((t >= 6) & (t < total + 6))
        def _():
            m = t - 6
            for b in range(2):
                place = piece_b if b else piece_a
                copies = spread(7 + b, m, place, 1, mate_z)

                @pl.when(inner)
                def _(copies=copies):
                    wait_send(copies)

                @pl.when(jnp.logical_not(inner))
                def _(copies=copies):
                    wait_recv(copies)

                start(spread(9 + b, m, place, 1, mate_x if b else mate_y))

        @pl.when((t >= 7) & (t < total + 7))
        def _():
            m = t - 7
            for b in range(2):
                place = piece_b if b else piece_a
                theirs = (4 + 2 * y + 1 - x) if b else (2 * x + 1 - y)
                wait_send(spread(9 + b, m, place, 1, mate_x if b else mate_y))
                wait_recv(spread(9 + b, m, theirs, 1, mate_x if b else mate_y))
                begin = (4 + 2 * y) if b else 2 * x
                start(spread(11 + b, m, begin, 2, mate_y if b else mate_x))

        @pl.when((t >= 8) & (t < total + 8))
        def _():
            m = t - 8
            for b in range(2):
                begin = (4 + 2 * y) if b else 2 * x
                theirs = (4 + 2 * (1 - y)) if b else 2 * (1 - x)
                wait_send(spread(11 + b, m, begin, 2, mate_y if b else mate_x))
                wait_recv(spread(11 + b, m, theirs, 2, mate_y if b else mate_x))
            start(spread(13, m, 0, 8, mate_core))

        def ins(m):
            return (
                pltpu.make_async_copy(left_hbm.at[m], left_buf.at[m % 2], in_sem.at[m % 2, 0]),
                pltpu.make_async_copy(right_hbm.at[m], right_buf.at[m % 2], in_sem.at[m % 2, 1]),
            )

        def outs(m):
            targets = (own_hbm, left_out_hbm, right_out_hbm, step_hbm)
            return [
                pltpu.make_async_copy(
                    outs_buf.at[m % 2, n], target.at[m], out_sem.at[m % 2, n]
                )
                for n, target in enumerate(targets)
            ]

        @pl.when((t >= 8) & (t < total + 8))
        def _():
            start(ins(t - 8))

        @pl.when((t >= 11) & (t < total + 11))
        def _():
            for copy in outs(t - 11):
                copy.wait()

        @pl.when((t >= 9) & (t < total + 9))
        def _():
            m = t - 9
            wait_send(spread(13, m, 0, 8, mate_core))
            wait_recv(spread(13, m, 0, 8, mate_core, other_cols))
            for copy in ins(m):
                copy.wait()
            precondition_block(
                own, codes.at[m], scales.at[m], left_buf.at[m % 2], right_buf.at[m % 2],
                outs_buf.at[m % 2], squares.at[m], high_buf, low_buf,
            )
            start(outs(m))

        return carry

    lax.fori_loop(0, total + 11, step, 0)

    def folded(row):
        return sum(row[:, n * 128 : (n + 1) * 128] for n in range(row.shape[1] // 128))

    sums_ref[...] = jnp.zeros_like(sums_ref)
    layer = jnp.zeros((1, 128), jnp.float32)
    for m in range(total):
        layer = layer + folded(squares[m, 0:1, :])
        for quad in range(2):
            part = squares[m, 1:2, quad * cols : (quad + 1) * cols]
            sums_ref[2 * m + quad : 2 * m + quad + 1, :] = folded(part)
    sum_slots[lax.rem(dp, quarter)] = sums_ref[...]
    once = (cls == 0).astype(jnp.float32)
    first_row = lax.broadcasted_iota(jnp.int32, tail_ref.shape, 0) == 0
    tail_slots[me] = tail_ref[...] + jnp.where(first_row, once * layer, 0.0)

    def sum_copy(n, slot):
        return pltpu.make_async_remote_copy(
            src_ref=sum_slots.at[slot], dst_ref=sum_slots.at[slot],
            send_sem=sum_send.at[n], recv_sem=sum_recv.at[slot],
            device_id=half_mate(n), device_id_type=MESH,
        )

    def tail_copy(n, slot):
        return pltpu.make_async_remote_copy(
            src_ref=tail_slots.at[slot], dst_ref=tail_slots.at[slot],
            send_sem=tail_send.at[n], recv_sem=tail_recv.at[slot],
            device_id=any_mate(n), device_id_type=MESH,
        )

    for n in range(1, quarter):
        sum_copy(n, lax.rem(dp, quarter)).start()
    for n in range(1, everyone):
        tail_copy(n, me).start()
    for n in range(1, quarter):
        sum_copy(n, lax.rem(dp, quarter)).wait_send()
        sum_copy(n, lax.rem(dp + n, quarter)).wait_recv()
    for n in range(1, everyone):
        tail_copy(n, me).wait_send()
        tail_copy(n, lax.rem(me + n, everyone)).wait_recv()
    value = sum_slots[0]
    for n in range(1, quarter):
        value = value + sum_slots[n]
    sums_ref[...] = value
    value = tail_slots[0]
    for n in range(1, everyone):
        value = value + tail_slots[n]
    tail_out_ref[...] = value


def reduce_gradients(arrays, vec_sums, tail, root_left, right_half, dp_count, cls_count):
    counts = tuple(array.shape[0] for array in arrays)
    total = sum(counts)
    width = arrays[0].shape[1]
    rows = root_left.shape[1]
    half, cols = width // 2, width // 2
    sum_rows = 2 * total + -2 * total % 8
    f32, i16 = jnp.float32, jnp.int16

    def pair(*shape):
        return [pltpu.VMEM((2,) + shape, i16), pltpu.VMEM((total,) + shape, i16)]

    def scale_pair(*shape):
        return [
            pltpu.VMEM((2,) + shape + (1, cols), f32),
            pltpu.VMEM((total,) + shape + (1, cols), f32),
        ]

    hbm = pl.BlockSpec(memory_space=pl.ANY)
    vmem = pl.BlockSpec(memory_space=pltpu.VMEM)
    return pl.pallas_call(
        functools.partial(reduce_kernel, counts),
        out_shape=(jax.ShapeDtypeStruct((total, rows, width), f32),) * 4
        + (
            jax.ShapeDtypeStruct((sum_rows, 128), f32),
            jax.ShapeDtypeStruct(tail.shape, f32),
            jax.ShapeDtypeStruct(vec_sums.shape, f32),
        ),
        in_specs=[hbm] * len(arrays) + [vmem, vmem, hbm, hbm],
        out_specs=(hbm,) * 4 + (vmem,) * 3,
        scratch_shapes=[
            pltpu.VMEM((2, rows, width), f32),
            pltpu.VMEM((2, half, width), f32),
            pltpu.VMEM((2, 4, rows, width), f32),
            pltpu.VMEM((total, 2, width), f32),
            pltpu.VMEM((half, width), jnp.bfloat16),
            pltpu.VMEM((half, width), jnp.bfloat16),
            pltpu.VMEM((dp_count // 2, sum_rows, 128), f32),
            pltpu.VMEM((dp_count * cls_count,) + tail.shape, f32),
            pltpu.SemaphoreType.DMA((2, 2)),
            pltpu.SemaphoreType.DMA((dp_count // 2,)),
            pltpu.SemaphoreType.DMA((dp_count // 2,)),
            pltpu.SemaphoreType.DMA((dp_count * cls_count,)),
            pltpu.SemaphoreType.DMA((dp_count * cls_count,)),
            pltpu.VMEM((5, width, cols), f32),
            pltpu.VMEM((2, width, cols), f32),
            pltpu.VMEM((3, 2, 2, PIECE, cols), f32),
        ]
        + pair(width, cols)
        + pair(2, 2, 2 * PIECE, cols)
        + pair(2, 2, PIECE, cols)
        + pair(2, 2, PIECE, cols)
        + pair(2, PIECE, cols)
        + scale_pair()
        + scale_pair(2)
        + scale_pair(2)
        + scale_pair()
        + scale_pair()
        + [
            pltpu.VMEM((total, half, width), i16),
            pltpu.VMEM((total, half // PIECE, 1, width), f32),
            pltpu.VMEM((5, 2) + vec_sums.shape, f32),
            pltpu.SemaphoreType.DMA((2, 2)),
            pltpu.SemaphoreType.DMA((2, 4)),
            pltpu.SemaphoreType.DMA((14, 2)),
            pltpu.SemaphoreType.DMA((14, total)),
            pltpu.SemaphoreType.DMA((14, 2)),
            pltpu.SemaphoreType.DMA((14, total)),
            pltpu.SemaphoreType.DMA((5,)),
            pltpu.SemaphoreType.DMA((5,)),
        ],
        compiler_params=pltpu.CompilerParams(
            collective_id=1, has_side_effects=True, vmem_limit_bytes=60 << 20
        ),
        name="reduce_gradients",
    )(*arrays, vec_sums, tail, root_left, right_half)


def split_float(values):
    high = values.astype(jnp.bfloat16)
    return high, (values - high.astype(jnp.float32)).astype(jnp.bfloat16)


def stacked_dot(lefts, right, contract_last):
    rows = lefts[0].shape[0]
    left = jnp.concatenate(lefts, 0) if len(lefts) > 1 else lefts[0]
    dims = (((1,), (1 if contract_last else 0,)), ((), ()))
    out = lax.dot_general(left, right, dims, preferred_element_type=jnp.float32)
    return [out[n * rows : (n + 1) * rows] for n in range(len(lefts))]


def precondition_block(
    own, codes_ref, scales_ref, left_ref, right_ref, outs_ref, squares_ref, high_ref, low_ref
):
    half, width = codes_ref.shape
    rows = left_ref.shape[0]
    own_rows = pl.ds(pl.multiple_of(own, PIECE), rows)
    for piece in range(half // PIECE):
        part = slice(piece * PIECE, (piece + 1) * PIECE)
        high_ref[part, :], low_ref[part, :] = split_float(
            decode(codes_ref[part, :], scales_ref[piece])
        )
    own_value = high_ref[own_rows, :].astype(jnp.float32) + low_ref[own_rows, :].astype(jnp.float32)
    outs_ref[0] = own_value
    squares_ref[0:1, :] = jnp.sum(own_value * own_value, 0, keepdims=True)
    picks = (
        lax.broadcasted_iota(jnp.int32, (rows, half), 1)
        == lax.broadcasted_iota(jnp.int32, (rows, half), 0) + own
    ).astype(jnp.float32).astype(jnp.bfloat16)
    for quad in range(2):
        cols = slice(quad * half, (quad + 1) * half)
        high, low = high_ref[:, cols], low_ref[:, cols]
        mine_high, mine_low = high_ref[own_rows, cols], low_ref[own_rows, cols]
        hh, lh, turned_high = stacked_dot([mine_high, mine_low, picks], high, True)
        hl, turned_low = stacked_dot([mine_high, picks], low, True)
        outs_ref[1, :, cols] = hh + (lh + hl)
        turned_high = turned_high.astype(jnp.bfloat16)
        turned_low = turned_low.astype(jnp.bfloat16)
        root_high, root_low = split_float(left_ref[:, cols])
        thh, tlh, rhh, rlh = stacked_dot([turned_high, turned_low, root_high, root_low], high, False)
        thl, rhl = stacked_dot([turned_high, root_high], low, False)
        outs_ref[2, :, cols] = thh + (tlh + thl)
        half_step = rhh + (rlh + rhl)
        step_high, step_low = split_float(half_step)
        right_high, right_low = split_float(right_ref[:, cols])
        shh, slh = stacked_dot([step_high, step_low], right_high, False)
        (shl,) = stacked_dot([step_high], right_low, False)
        direction = shh + (slh + shl)
        outs_ref[3, :, cols] = direction
        squares_ref[1:2, cols] = jnp.sum(direction * direction, 0, keepdims=True)


def class_sum_kernel(in_ref, out_ref, slots, send_sem, recv_sem):
    dp, cls = lax.axis_index("dp"), lax.axis_index("cls")
    total, rows = slots.shape[0], slots.shape[1]
    barrier = pltpu.get_barrier_semaphore()
    for n in range(1, total):
        pl.semaphore_signal(
            barrier, inc=1, device_id=(dp, lax.rem(cls + n, total)), device_id_type=MESH
        )
    pl.semaphore_wait(barrier, total - 1)

    def part(index):
        return in_ref.at[pl.ds(pl.multiple_of(index * rows, 8), rows)]

    def copy(n, slot):
        mate = lax.rem(cls + n, total)
        return pltpu.make_async_remote_copy(
            src_ref=part(mate), dst_ref=slots.at[slot],
            send_sem=send_sem.at[n], recv_sem=recv_sem.at[slot],
            device_id=(dp, mate), device_id_type=MESH,
        )

    for n in range(1, total):
        copy(n, cls).start()
    slots[cls] = part(cls)[...]
    for n in range(1, total):
        copy(n, cls).wait_send()
        copy(n, lax.rem(cls + n, total)).wait_recv()
    value = slots[0]
    for n in range(1, total):
        value = value + slots[n]
    out_ref[...] = value


def class_sum(values, cls_count):
    rows = values.shape[0] // cls_count
    vmem = pl.BlockSpec(memory_space=pltpu.VMEM)
    return pl.pallas_call(
        class_sum_kernel,
        out_shape=jax.ShapeDtypeStruct((rows, values.shape[1]), jnp.float32),
        in_specs=[vmem],
        out_specs=vmem,
        scratch_shapes=[
            pltpu.VMEM((cls_count, rows, values.shape[1]), jnp.float32),
            pltpu.SemaphoreType.DMA((cls_count,)),
            pltpu.SemaphoreType.DMA((cls_count,)),
        ],
        compiler_params=pltpu.CompilerParams(collective_id=2, has_side_effects=True),
        name="class_sum",
    )(values)


def gather_steps(own_ref, out_ref, send_sem, recv_sem, copy_sem):
    count, rows, width = own_ref.shape
    cols = width // 2
    z, y, x, core = torus_place()
    mate_core = torus_device(z, y, x, 1 - core)
    mate_x = torus_device(z, y, 1 - x, core)
    mate_y = torus_device(z, 1 - y, x, core)
    mate_up = torus_device(jnp.minimum(z + 1, 3), y, x, core)
    mate_down = torus_device(jnp.maximum(z - 1, 0), y, x, core)
    has_up = z < 3
    has_down = z > 0
    own_cols = pl.ds(pl.multiple_of(core * cols, 128), cols)
    other_cols = pl.ds(pl.multiple_of((1 - core) * cols, 128), cols)

    def share(m, zz, yy, start, size, columns=own_cols):
        begin = (zz * 2 + yy) * rows + start
        return out_ref.at[m, pl.ds(pl.multiple_of(begin, 16), size), columns]

    def copy(stage, m, source, target, mate):
        return pltpu.make_async_remote_copy(
            src_ref=source, dst_ref=target,
            send_sem=send_sem.at[stage, m % 2], recv_sem=recv_sem.at[stage, m],
            device_id=mate, device_id_type=MESH,
        )

    span_start = x * (rows - SPAN)
    lack = rows - SPAN
    lack_mine = x * SPAN
    lack_theirs = (1 - x) * SPAN

    def local(m):
        return pltpu.make_async_copy(
            own_ref.at[m, :, own_cols], share(m, z, y, 0, rows), copy_sem.at[m % 2]
        )

    def chain(m, turn, upward):
        origin = z - (turn - 1) if upward else z + (turn - 1)
        stage = (turn - 1) * 2 + (0 if upward else 1)
        target = share(m, origin, y, span_start, SPAN)
        if turn == 1:
            source = own_ref.at[m, pl.ds(pl.multiple_of(span_start, 16), SPAN), own_cols]
        else:
            source = target
        return copy(stage, m, source, target, mate_up if upward else mate_down)

    def chain_sends(turn, upward):
        if upward:
            return has_up & (z - (turn - 1) >= 0)
        return has_down & (z + (turn - 1) <= 3)

    def chain_comes(turn, upward):
        return (z - turn >= 0) if upward else (z + turn <= 3)

    def arriving(m, turn, upward):
        origin = z - turn if upward else z + turn
        stage = (turn - 1) * 2 + (0 if upward else 1)
        target = share(m, origin, y, span_start, SPAN)
        return copy(stage, m, target, target, mate_up)

    def patch_out(m, n):
        zz = lax.rem(z + n, 4)
        block = share(m, zz, y, lack_mine, lack)
        return copy(5 + n, m, block, block, mate_x)

    def patch_in(m, n):
        zz = lax.rem(z + n, 4)
        block = share(m, zz, y, lack_theirs, lack)
        return copy(5 + n, m, block, block, mate_x)

    def cross(m, n, yy, stage, plane, mate):
        block = share(m, plane * 2 + n, yy, 0, rows)
        return copy(stage + n, m, block, block, mate)

    def swap(m, columns):
        block = out_ref.at[m, :, columns]
        return copy(13, m, block, block, mate_core)

    def step(t):
        @pl.when(t < count)
        def _():
            local(t).start()
            for upward in (True, False):
                @pl.when(chain_sends(1, upward))
                def _(upward=upward):
                    chain(t, 1, upward).start()

        for turn in (2, 3):
            @pl.when((t >= turn - 1) & (t < count + turn - 1))
            def _(turn=turn):
                m = t - (turn - 1)
                if turn == 2:
                    local(m).wait()
                for upward in (True, False):
                    @pl.when(chain_sends(turn - 1, upward))
                    def _(upward=upward):
                        chain(m, turn - 1, upward).wait_send()

                    @pl.when(chain_comes(turn - 1, upward))
                    def _(upward=upward):
                        arriving(m, turn - 1, upward).wait_recv()

                    @pl.when(chain_sends(turn, upward))
                    def _(upward=upward):
                        chain(m, turn, upward).start()

        @pl.when((t >= 3) & (t < count + 3))
        def _():
            m = t - 3
            for upward in (True, False):
                @pl.when(chain_sends(3, upward))
                def _(upward=upward):
                    chain(m, 3, upward).wait_send()

                @pl.when(chain_comes(3, upward))
                def _(upward=upward):
                    arriving(m, 3, upward).wait_recv()
            if lack:
                for n in range(1, 4):
                    patch_out(m, n).start()

        @pl.when((t >= 4) & (t < count + 4))
        def _():
            m = t - 4
            if lack:
                for n in range(1, 4):
                    patch_out(m, n).wait_send()
                    patch_in(m, n).wait_recv()
            for n in range(2):
                cross(m, n, y, 9, x, mate_y).start()

        @pl.when((t >= 5) & (t < count + 5))
        def _():
            m = t - 5
            for n in range(2):
                cross(m, n, y, 9, x, mate_y).wait_send()
                cross(m, n, 1 - y, 9, x, mate_y).wait_recv()
                cross(m, n, 1 - y, 11, x, mate_x).start()

        @pl.when((t >= 6) & (t < count + 6))
        def _():
            m = t - 6
            for n in range(2):
                cross(m, n, 1 - y, 11, x, mate_x).wait_send()
                cross(m, n, 1 - y, 11, 1 - x, mate_x).wait_recv()
            swap(m, own_cols).start()

        @pl.when((t >= 7) & (t < count + 7))
        def _():
            m = t - 7
            swap(m, own_cols).wait_send()
            swap(m, other_cols).wait_recv()

    return step, count + GATHER_DEPTH


def column_mate(n):
    z, y, x, core = torus_place()
    other = lax.rem(z * 2 + y + n, SHARES)
    return torus_device(other // 2, lax.rem(other, 2), x, core)


def gather_barrier():
    z, y, x, core = torus_place()
    barrier = pltpu.get_barrier_semaphore()
    mates = [torus_device(z, y, x, 1 - core), torus_device(z, y, 1 - x, core)]
    for mate in mates + [column_mate(n) for n in range(1, SHARES)]:
        pl.semaphore_signal(barrier, inc=1, device_id=mate, device_id_type=MESH)
    pl.semaphore_wait(barrier, SHARES + 1)


def gather_kernel(
    own_ref, vec_ref, out_ref, vec_out_ref, send_sem, recv_sem, copy_sem, vec_send, vec_recv
):
    z, y, _, _ = torus_place()
    me = z * 2 + y
    gather_barrier()

    def vec_copy(n, slot):
        return pltpu.make_async_remote_copy(
            src_ref=vec_ref, dst_ref=vec_out_ref.at[slot],
            send_sem=vec_send.at[n], recv_sem=vec_recv.at[slot],
            device_id=column_mate(n), device_id_type=MESH,
        )

    for n in range(1, SHARES):
        vec_copy(n, me).start()
    vec_out_ref[me] = vec_ref[...]
    gather_step, turns = gather_steps(own_ref, out_ref, send_sem, recv_sem, copy_sem)

    def step(t, carry):
        gather_step(t)
        return carry

    lax.fori_loop(0, turns, step, 0)
    for n in range(1, SHARES):
        vec_copy(n, me).wait_send()
        vec_copy(n, lax.rem(me + n, SHARES)).wait_recv()


def gather_semaphores(count):
    return [
        pltpu.SemaphoreType.DMA((14, 2)),
        pltpu.SemaphoreType.DMA((14, count)),
        pltpu.SemaphoreType.DMA((2,)),
    ]


def attention_gather_kernel(
    qids_ref, kcodes_ref, q_ref, k_ref, v_ref, own_ref, out_ref, blocks_ref,
    bias_ref, send_sem, recv_sem, copy_sem
):
    pair, tiles = pl.program_id(0), q_ref.shape[0] // QTILE
    slots = pl.num_programs(0) * tiles

    @pl.when(pair == 0)
    def _():
        gather_barrier()

    gather_step, turns = gather_steps(own_ref, blocks_ref, send_sem, recv_sem, copy_sem)
    attention_bias(qids_ref, kcodes_ref, bias_ref)
    for tile in range(tiles):
        slot = pair * tiles + tile
        begin, end = slot * turns // slots, (slot + 1) * turns // slots

        @pl.when(begin < end)
        def _(begin=begin):
            gather_step(begin)

        attention_tile(tile, q_ref, k_ref, v_ref, out_ref, bias_ref)


def attention_forward_gathering(qkv_rows, pack_ids, key_codes, own):
    _, length, width = qkv_rows.shape
    count, rows, _ = own.shape
    tiles = length // QTILE
    assert count + GATHER_DEPTH <= tiles * (width // PAIR)
    return pl.pallas_call(
        attention_gather_kernel,
        grid=(width // PAIR,),
        out_shape=(
            jax.ShapeDtypeStruct((length, width), jnp.bfloat16),
            jax.ShapeDtypeStruct((count, SHARES * rows, width), own.dtype),
        ),
        in_specs=[whole_spec((length, 1)), whole_spec((1, length))]
        + [pair_spec(length, part) for part in range(3)]
        + [whole_spec(own.shape)],
        out_specs=(pair_spec(length), pl.BlockSpec(memory_space=pl.ANY)),
        scratch_shapes=[pltpu.VMEM(bias_shape(length), jnp.float32)] + gather_semaphores(count),
        compiler_params=pltpu.CompilerParams(
            collective_id=4, has_side_effects=True, vmem_limit_bytes=40 << 20
        ),
        name="attention_forward",
    )(pack_ids[:, None], key_codes[None, :], qkv_rows, qkv_rows, qkv_rows, own)


def gather_weights(own, vec):
    count, rows, width = own.shape
    hbm = pl.BlockSpec(memory_space=pl.ANY)
    vmem = pl.BlockSpec(memory_space=pltpu.VMEM)
    return pl.pallas_call(
        gather_kernel,
        out_shape=(
            jax.ShapeDtypeStruct((count, SHARES * rows, width), own.dtype),
            jax.ShapeDtypeStruct((SHARES,) + vec.shape, vec.dtype),
        ),
        in_specs=[vmem, vmem],
        out_specs=(hbm, vmem),
        scratch_shapes=gather_semaphores(count)
        + [pltpu.SemaphoreType.DMA((SHARES,)), pltpu.SemaphoreType.DMA((SHARES,))],
        compiler_params=pltpu.CompilerParams(
            collective_id=3, has_side_effects=True, vmem_limit_bytes=32 << 20
        ),
        name="gather_weights",
    )(own, vec)


def adam_step(weight, grad, first, second, count):
    first = BETA_FIRST * first + (1.0 - BETA_FIRST) * grad
    second = BETA_SECOND * second + (1.0 - BETA_SECOND) * grad * grad
    fix_first = 1.0 - jnp.power(BETA_FIRST, count)
    fix_second = 1.0 - jnp.power(BETA_SECOND, count)
    update = first / fix_first / (jnp.sqrt(second / fix_second) + ADAM_EPS) + WEIGHT_DECAY * weight
    return (weight - ADAM_RATE * update, first, second)


def split_halves(values, half_size):
    block_count, row_count, feature_dim = values.shape
    return values.reshape(block_count, row_count, 2, half_size)


def reduced_half(values, half_groups):
    part = lax.psum_scatter(values, ("dp", "cls"), scatter_dimension=1, tiled=True)
    return lax.all_gather(part, ("dp", "cls"), axis=1, tiled=True, axis_index_groups=half_groups)


def preconditioned_rows(grad_half, root_left, right_half, own_start):
    count, row_count, width = root_left.shape
    half_size = width // 2
    block_rows = lax.dynamic_slice_in_dim(grad_half, own_start, row_count, 1)
    grad_quads = split_halves(grad_half, half_size)
    rows_quads = split_halves(block_rows, half_size)
    cols_quads = lax.dynamic_slice_in_dim(grad_quads, own_start, row_count, 3)
    precise = FULL_PRECISION
    left_add = jnp.einsum("brjk,bljk->brjl", rows_quads, grad_quads, precision=precise)
    right_add = jnp.einsum("bkja,bkjm->bajm", cols_quads, grad_quads, precision=precise)
    direction = jnp.einsum(
        "brjk,bkjm->brjm", split_halves(root_left, half_size), grad_quads, precision=precise
    )
    direction = jnp.einsum(
        "brjk,bkjm->brjm", direction, split_halves(right_half, half_size), precision=precise
    )
    flat = (count, row_count, width)
    return left_add.reshape(flat), right_add.reshape(flat), direction.reshape(flat), block_rows


def on_device(
    patches,
    image_ids,
    keep,
    labels,
    owner,
    step,
    enc_weights,
    stats_left,
    stats_right,
    root_left,
    root_right,
    head_weights,
    head_m,
    head_v,
    vectors,
    vec_m,
    vec_v,
):
    dp_count = lax.axis_size("dp")
    cls_count = lax.axis_size("cls")
    dp_index = lax.axis_index("dp")
    cls_index = lax.axis_index("cls")
    block_count, row_count, feature_dim = enc_weights.shape
    up_count = (block_count - 5) // 2
    half_size = feature_dim // 2
    part_rows = row_count // cls_count
    half_dp = dp_count // 2
    half_group = half_dp * cls_count
    half_groups = [
        list(range(half_group)),
        list(range(half_group, 2 * half_group)),
    ]

    def my_part(values):
        return lax.dynamic_slice_in_dim(values, cls_index * part_rows, part_rows, 1)

    on_torus = dp_count == 8 and cls_count == 4
    if on_torus:
        vec_block = jnp.pad(vectors, ((0, -vectors.shape[0] % 8), (0, -row_count % 128)))
        own_low = enc_weights.astype(jnp.bfloat16)
        blocks, vec_blocks = gather_weights(own_low[:5], vec_block)
        right_part, vec_blocks = lax.optimization_barrier((my_part(root_right), vec_blocks))
        vec_low = jnp.transpose(vec_blocks[:, : vectors.shape[0], :row_count], (1, 0, 2))
        vec_all = lax.reduce_precision(vec_low.reshape(vectors.shape[0], feature_dim), 8, 7)
    else:
        right_part = my_part(root_right)
        all_blocks = lax.all_gather(
            my_part(enc_weights.astype(jnp.bfloat16)), ("dp", "cls"), axis=1, tiled=True
        )
        blocks = all_blocks[:5]
        vec_low = lax.all_gather(vectors.astype(jnp.bfloat16), "dp", axis=1, tiled=True)
        vec_all = vec_low.astype(jnp.float32)
    head_low = lax.all_gather(head_weights.astype(jnp.bfloat16), "dp", axis=0, tiled=True)
    final_gain = vec_all[9 + up_count]
    final_shift = vec_all[10 + up_count]
    pack_ids, pack_keep = image_ids[0], keep[0]
    key_codes = jnp.where(pack_keep == 1, pack_ids, -1)

    def attend(qkv_rows):
        if on_torus:
            return attention_forward_gathering(qkv_rows, pack_ids, key_codes, own_low[5:])
        return attention_forward(qkv_rows, pack_ids, key_codes), all_blocks[5:]

    output, mlp_blocks, saved = layer_forward(blocks, vec_all, patches, attend)
    right_half = lax.all_gather(
        right_part, ("dp", "cls"), axis=1, tiled=True, axis_index_groups=half_groups
    )
    pooled = pool_rows(output, final_gain, final_shift, pack_ids, pack_keep)
    group = lax.all_gather(pooled.astype(jnp.bfloat16), "cls", axis=0, tiled=True)
    logits = jnp.dot(group, head_low, preferred_element_type=jnp.float32)
    class_dev = head_low.shape[1]
    class_ids = cls_index * class_dev + jnp.arange(class_dev)
    valid = class_ids[None, :] < LABELS_REAL
    target = jnp.any(labels[:, :, None] == class_ids[None, None, :], 1).astype(jnp.float32)
    image_total = labels.shape[0] * dp_count
    loss_part = (
        jnp.sum(jnp.where(valid, jax.nn.softplus(logits) - target * logits, 0.0)) / image_total
    )
    grad_logits = (jnp.where(valid, jax.nn.sigmoid(logits) - target, 0.0) / image_total).astype(
        jnp.bfloat16
    )
    group_grad = jnp.einsum("gc,dc->gd", grad_logits, head_low, preferred_element_type=jnp.float32)
    if on_torus:
        grad_pooled = class_sum(group_grad, cls_count)
    else:
        grad_pooled = lax.psum_scatter(group_grad, "cls", scatter_dimension=0, tiled=True)
    head_rows = lax.all_gather(
        jnp.concatenate([group, grad_logits], 1), "dp", axis=0, tiled=True
    )
    pooled_all, grad_logits_all = head_rows[:, :feature_dim], head_rows[:, feature_dim:]
    pooled_mine = lax.dynamic_slice_in_dim(pooled_all, dp_index * row_count, row_count, 1)
    head_grad = jnp.einsum(
        "gr,gc->rc", pooled_mine, grad_logits_all, preferred_element_type=jnp.float32
    )

    def pool_local(rows_in, gain, shift):
        return pool_rows(rows_in, gain, shift, pack_ids, pack_keep)

    pool_back = jax.vjp(pool_local, output, final_gain, final_shift)[1]
    grad_output, grad_gain, grad_shift = pool_back(grad_pooled)
    grad_arrays, grad_vectors = layer_backward(
        blocks,
        mlp_blocks,
        vec_all,
        patches,
        saved,
        pack_ids,
        key_codes,
        grad_output,
        grad_gain,
        grad_shift,
    )

    head_squares = jnp.sum(head_grad * head_grad)
    if on_torus:
        padded = jnp.pad(grad_vectors, ((0, -grad_vectors.shape[0] % 8), (0, 0)))
        tail = jnp.pad(jnp.stack([head_squares, loss_part])[:, None], ((0, 6), (0, 127)))
        block_rows, left_add, right_add, direction, sums, tail, vector_sum = reduce_gradients(
            grad_arrays, padded, tail, root_left, right_half, dp_count, cls_count
        )
        vector_sum = vector_sum[: grad_vectors.shape[0]]
        loss = tail[1, 0]
        all_squares = jnp.sum(tail[0])
        block_squares = jnp.sum(sums[: 2 * block_count], -1).reshape(block_count, 2)
    else:
        grad_half = reduced_half(jnp.concatenate(grad_arrays, 0), half_groups)
        vector_sum = lax.psum(grad_vectors, ("dp", "cls"))
        left_add, right_add, direction, block_rows = preconditioned_rows(
            grad_half, root_left, right_half, (dp_index % half_dp) * row_count
        )
        squares = jnp.sum(split_halves(direction * direction, half_size), (1, 3))
        in_top = (dp_index < half_dp).astype(jnp.float32)
        once = (cls_index == 0).astype(jnp.float32)
        all_squares = head_squares + once * jnp.sum(block_rows * block_rows)
        packed = jnp.concatenate(
            [
                (once * in_top * squares).reshape(-1),
                (once * (1.0 - in_top) * squares).reshape(-1),
                jnp.stack([all_squares, loss_part]),
            ]
        )
        packed = lax.psum(packed, ("dp", "cls"))
        loss = packed[4 * block_count + 1]
        all_squares = packed[4 * block_count]
        sums = packed[: 4 * block_count].reshape(2, block_count, 2)
        block_squares = jnp.where(dp_index < half_dp, sums[0], sums[1])
    vector_rows = lax.dynamic_slice_in_dim(vector_sum, dp_index * row_count, row_count, 1)
    grad_norm = jnp.sqrt(all_squares + jnp.sum(vector_sum * vector_sum))
    factor = CLIP_NORM / jnp.maximum(grad_norm, CLIP_NORM)
    mean_squares = block_squares / (half_size * half_size)
    mean_squares = mean_squares * factor * factor
    scale = factor * lax.rsqrt(mean_squares + ROOT_EPS)
    wide_scale = jnp.repeat(SHAMPOO_RATE * scale, half_size, axis=1)
    new_blocks = enc_weights - direction * wide_scale[:, None, :]
    square_factor = 0.5 * factor * factor
    new_left = 0.5 * stats_left + square_factor * left_add
    new_right = 0.5 * stats_right + square_factor * right_add
    count = step.astype(jnp.float32)
    new_vec, new_vec_m, new_vec_v = adam_step(vectors, vector_rows * factor, vec_m, vec_v, count)
    new_head, new_head_m, new_head_v = adam_step(
        head_weights, head_grad * factor, head_m, head_v, count
    )
    return (
        loss,
        grad_norm,
        new_blocks,
        block_rows * factor,
        new_left,
        new_right,
        new_vec,
        new_vec_m,
        new_vec_v,
        new_head,
        new_head_m,
        new_head_v,
    )


def solution(mesh):
    return jax.shard_map(
        on_device,
        mesh=mesh,
        in_specs=(
            P(("dp", "cls"), None),
            P(("dp", "cls"), None),
            P(("dp", "cls"), None),
            P("dp", None),
            P(),
            P(),
            P(None, "dp", None),
            P(None, "dp", None),
            P(None, "dp", None),
            P(None, "dp", None),
            P(None, "dp", None),
            P("dp", "cls"),
            P("dp", "cls"),
            P("dp", "cls"),
            P(None, "dp"),
            P(None, "dp"),
            P(None, "dp"),
        ),
        out_specs=(
            P(),
            P(),
            P(None, "dp", None),
            P(None, "dp", None),
            P(None, "dp", None),
            P(None, "dp", None),
            P(None, "dp"),
            P(None, "dp"),
            P(None, "dp"),
            P("dp", "cls"),
            P("dp", "cls"),
            P("dp", "cls"),
        ),
        check_vma=False,
    )
```

```python
import functools

import jax
import jax.numpy as jnp
from jax import lax
from jax.experimental import pallas as pl
from jax.experimental.pallas import tpu as pltpu
from jax.sharding import PartitionSpec as P

HEADS = 12
HEAD = 64
LABELS_REAL = 21843
IMAGE_MAX = 196
QTILE = 256
PAIR = 2 * HEAD
ROWS = 256
HIDDEN_TILE = 384
MESH = pl.DeviceIdType.MESH
CODE_TOP = 32766.0
CODE_FLOOR = 1e-33
PIECE = 48
FEATURE_TILE = 128
SPAN = 48
SHARES = 8
GATHER_DEPTH = 4
IMG_PACK = 8


FULL_PRECISION = lax.Precision.HIGHEST
NORM_EPS = 1e-06
CLIP_NORM = 1.0
ADAM_RATE = 0.02
SHAMPOO_RATE = 0.01
BETA_FIRST = 0.9
BETA_SECOND = 0.999
ADAM_EPS = 1e-08
WEIGHT_DECAY = 0.1
ROOT_EPS = 1e-06


def norm_rows(values, gain, shift):
    centred = values - jnp.mean(values, -1, keepdims=True)
    spread = jnp.mean(centred * centred, -1, keepdims=True)
    return centred * lax.rsqrt(spread + NORM_EPS) * gain + shift


def pool_rows(output, gain, shift, pack_ids, pack_keep):
    final = norm_rows(output, gain, shift)
    member = (
        (pack_ids[None, :] == jnp.arange(IMG_PACK)[:, None]) & (pack_keep[None, :] == 1)
    ).astype(jnp.float32)
    counted = jnp.maximum(jnp.sum(member, 1), 1.0)
    return jnp.dot(member, final, precision=FULL_PRECISION) / counted[:, None]


def key_window(tile, length):
    reach = -(-(IMAGE_MAX - 1) // 128) * 128
    low = max(0, tile * QTILE - reach)
    high = min(length, (tile + 1) * QTILE + reach)
    return low, high


def attention_bias(qids_ref, kcodes_ref, bias_ref):
    length = qids_ref.shape[0]

    @pl.when(pl.program_id(0) == 0)
    def _():
        for tile in range(length // QTILE):
            low, high = key_window(tile, length)
            shape = (QTILE, high - low)
            rows = lax.broadcasted_iota(jnp.int32, shape, 0) + tile * QTILE
            cols = lax.broadcasted_iota(jnp.int32, shape, 1) + low
            same = qids_ref[tile * QTILE : (tile + 1) * QTILE, :] == kcodes_ref[:, low:high]
            bias_ref[tile, :, : high - low] = jnp.where(same | (rows == cols), 0.0, -1e30)


def attention_tile(tile, q_ref, k_ref, v_ref, out_ref, bias_ref):
    lane = lax.broadcasted_iota(jnp.int32, (QTILE, PAIR), 1)
    low, high = key_window(tile, q_ref.shape[0])
    rows = pl.ds(tile * QTILE, QTILE)
    queries = q_ref[rows, :] * jnp.bfloat16(HEAD ** (-0.5))
    keys = k_ref[low:high, :]
    values = v_ref[low:high, :]
    halves = []
    for head in range(2):
        mine = (lane >= head * HEAD) & (lane < (head + 1) * HEAD)
        picked = jnp.where(mine, queries, jnp.zeros_like(queries))
        scores = lax.dot_general(
            picked, keys, (((1,), (1,)), ((), ())), preferred_element_type=jnp.float32
        )
        scores = scores + bias_ref[tile, :, : high - low]
        top = jnp.max(scores, -1, keepdims=True)
        weights = jnp.exp(scores - top)
        probs = weights * (1.0 / jnp.sum(weights, -1, keepdims=True))
        halves.append(
            jnp.dot(probs.astype(jnp.bfloat16), values, preferred_element_type=jnp.float32)
        )
    out_ref[rows, :] = jnp.where(lane < HEAD, halves[0], halves[1]).astype(jnp.bfloat16)


def attention_forward_kernel(qids_ref, kcodes_ref, q_ref, k_ref, v_ref, out_ref, bias_ref):
    attention_bias(qids_ref, kcodes_ref, bias_ref)
    for tile in range(q_ref.shape[0] // QTILE):
        attention_tile(tile, q_ref, k_ref, v_ref, out_ref, bias_ref)


def attention_backward_kernel(
    qids_ref, kcodes_ref, q_ref, k_ref, v_ref, do_ref, out_ref, bias_ref, dk_ref, dv_ref
):
    length = q_ref.shape[0]
    lane = lax.broadcasted_iota(jnp.int32, (QTILE, PAIR), 1)
    scale = jnp.bfloat16(HEAD ** (-0.5))

    @pl.when(pl.program_id(0) == 0)
    def _():
        for tile in range(length // QTILE):
            low, high = key_window(tile, length)
            shape = (high - low, QTILE)
            rows = lax.broadcasted_iota(jnp.int32, shape, 0) + low
            cols = lax.broadcasted_iota(jnp.int32, shape, 1) + tile * QTILE
            same = kcodes_ref[low:high, :] == qids_ref[:, tile * QTILE : (tile + 1) * QTILE]
            bias_ref[tile, : high - low, :] = jnp.where(same | (rows == cols), 0.0, -1e30)

    dk_ref[...] = jnp.zeros_like(dk_ref)
    dv_ref[...] = jnp.zeros_like(dv_ref)
    for tile in range(length // QTILE):
        low, high = key_window(tile, length)
        rows = pl.ds(tile * QTILE, QTILE)
        window = pl.ds(low, high - low)
        queries = q_ref[rows, :] * scale
        keys = k_ref[window, :]
        values = v_ref[window, :]
        grads = do_ref[rows, :]
        halves = []
        for head in range(2):
            mine = (lane >= head * HEAD) & (lane < (head + 1) * HEAD)
            picked = jnp.where(mine, queries, jnp.zeros_like(queries))
            picked_grads = jnp.where(mine, grads, jnp.zeros_like(grads))
            scores = lax.dot_general(
                keys, picked, (((1,), (1,)), ((), ())), preferred_element_type=jnp.float32
            )
            scores = scores + bias_ref[tile, : high - low, :]
            top = jnp.max(scores, 0, keepdims=True)
            weights = jnp.exp(scores - top)
            probs = weights * (1.0 / jnp.sum(weights, 0, keepdims=True))
            grad_probs = lax.dot_general(
                values, picked_grads, (((1,), (1,)), ((), ())), preferred_element_type=jnp.float32
            )
            inner = jnp.sum(probs * grad_probs, 0, keepdims=True)
            grad_scores = (probs * (grad_probs - inner)).astype(jnp.bfloat16)
            dv_ref[window, :] += jnp.dot(
                probs.astype(jnp.bfloat16), picked_grads, preferred_element_type=jnp.float32
            )
            dk_ref[window, :] += jnp.dot(
                grad_scores, picked, preferred_element_type=jnp.float32
            )
            halves.append(
                lax.dot_general(
                    grad_scores,
                    keys,
                    (((0,), (0,)), ((), ())),
                    preferred_element_type=jnp.float32,
                )
            )
        grad_queries = jnp.where(lane < HEAD, halves[0], halves[1]) * HEAD ** (-0.5)
        out_ref[0, rows, :] = grad_queries.astype(jnp.bfloat16)
    out_ref[1] = dk_ref[...].astype(jnp.bfloat16)
    out_ref[2] = dv_ref[...].astype(jnp.bfloat16)


def pair_spec(length, part=None):
    if part is None:
        return pl.BlockSpec((length, PAIR), lambda pair: (0, pair))
    return pl.BlockSpec((None, length, PAIR), lambda pair: (part, 0, pair))


def whole_spec(shape):
    return pl.BlockSpec(shape, lambda pair: (0,) * len(shape))


def bias_shape(length):
    tiles = length // QTILE
    window = max(high - low for low, high in (key_window(t, length) for t in range(tiles)))
    return tiles, QTILE, window


def attention_forward(qkv_rows, pack_ids, key_codes):
    _, length, width = qkv_rows.shape
    return pl.pallas_call(
        attention_forward_kernel,
        grid=(width // PAIR,),
        out_shape=jax.ShapeDtypeStruct((length, width), jnp.bfloat16),
        in_specs=[whole_spec((length, 1)), whole_spec((1, length))]
        + [pair_spec(length, part) for part in range(3)],
        out_specs=pair_spec(length),
        scratch_shapes=[pltpu.VMEM(bias_shape(length), jnp.float32)],
        compiler_params=pltpu.CompilerParams(vmem_limit_bytes=40 << 20),
        name="attention_forward",
    )(pack_ids[:, None], key_codes[None, :], qkv_rows, qkv_rows, qkv_rows)


def attention_backward(qkv_rows, pack_ids, key_codes, grad_attended):
    _, length, width = qkv_rows.shape
    tiles = length // QTILE
    window = max(high - low for low, high in (key_window(t, length) for t in range(tiles)))
    return pl.pallas_call(
        attention_backward_kernel,
        grid=(width // PAIR,),
        out_shape=jax.ShapeDtypeStruct((3, length, width), jnp.bfloat16),
        in_specs=[whole_spec((1, length)), whole_spec((length, 1))]
        + [pair_spec(length, part) for part in range(3)]
        + [pair_spec(length)],
        out_specs=pl.BlockSpec((3, length, PAIR), lambda pair: (0, 0, pair)),
        scratch_shapes=[
            pltpu.VMEM((tiles, window, QTILE), jnp.float32),
            pltpu.VMEM((length, PAIR), jnp.float32),
            pltpu.VMEM((length, PAIR), jnp.float32),
        ],
        compiler_params=pltpu.CompilerParams(vmem_limit_bytes=40 << 20),
        name="attention_backward",
    )(pack_ids[None, :], key_codes[:, None], qkv_rows, qkv_rows, qkv_rows, grad_attended)


def mlp_forward_kernel(x_ref, up_ref, bias_ref, down_ref, units_ref, slope_ref, out_ref):
    first = pl.program_id(0) == 0

    @pl.when(first)
    def _():
        out_ref[...] = jnp.zeros_like(out_ref)

    for start in range(0, x_ref.shape[0], ROWS):
        rows = pl.ds(start, ROWS)
        pre = jnp.dot(x_ref[rows, :], up_ref[...], preferred_element_type=jnp.float32)
        pre = pre + bias_ref[...]
        half = 0.5 + 0.5 * lax.erf(pre * 0.7071067811865476)
        bell = jnp.exp(-0.5 * pre * pre) * 0.3989422804014327
        units = (pre * half).astype(jnp.bfloat16)
        units_ref[rows, :] = units
        slope_ref[rows, :] = half + pre * bell
        out_ref[rows, :] += jnp.dot(units, down_ref[...], preferred_element_type=jnp.float32)


def mlp_backward_kernel(
    x_ref, dm_ref, up_ref, down_ref, units_ref, slope_ref,
    grad_up_ref, grad_down_ref, bias_ref, dx_ref, dpre_ref
):
    @pl.when(pl.program_id(0) == 0)
    def _():
        dx_ref[...] = jnp.zeros_like(dx_ref)

    total = jnp.zeros((1, HIDDEN_TILE), jnp.float32)
    for start in range(0, x_ref.shape[0], ROWS):
        rows = pl.ds(start, ROWS)
        units_back = lax.dot_general(
            dm_ref[rows, :], down_ref[...], (((1,), (1,)), ((), ())),
            preferred_element_type=jnp.float32,
        )
        grad_pre = (units_back * slope_ref[rows, :]).astype(jnp.bfloat16)
        dpre_ref[rows, :] = grad_pre
        total = total + jnp.sum(grad_pre.astype(jnp.float32), 0, keepdims=True)
        dx_ref[rows, :] += lax.dot_general(
            grad_pre, up_ref[...], (((1,), (1,)), ((), ())), preferred_element_type=jnp.float32
        )
    bias_ref[...] = total
    over_rows = (((0,), (0,)), ((), ()))
    grad_down_ref[...] = lax.dot_general(
        units_ref[...], dm_ref[...], over_rows, preferred_element_type=jnp.float32
    )
    grad_up_ref[...] = lax.dot_general(
        x_ref[...], dpre_ref[...], over_rows, preferred_element_type=jnp.float32
    )


def mlp_specs(length, width, up_count):
    split = width // HIDDEN_TILE
    resident = pl.BlockSpec((length, width), lambda t: (0, 0))
    up = pl.BlockSpec((None, width, HIDDEN_TILE), lambda t: (t // split, 0, t % split))
    down = pl.BlockSpec(
        (None, HIDDEN_TILE, width), lambda t: (up_count + t // split, t % split, 0)
    )
    hidden = pl.BlockSpec((length, HIDDEN_TILE), lambda t: (0, t))
    bias = pl.BlockSpec((1, HIDDEN_TILE), lambda t: (0, t))
    return split, resident, up, down, hidden, bias


def mlp_forward(rows, blocks, up_bias):
    length, width = rows.shape
    up_count = blocks.shape[0] // 2
    split, resident, up, down, hidden, bias = mlp_specs(length, width, up_count)
    hidden_size = up_count * width
    return pl.pallas_call(
        mlp_forward_kernel,
        grid=(up_count * split,),
        out_shape=(
            jax.ShapeDtypeStruct((length, hidden_size), jnp.bfloat16),
            jax.ShapeDtypeStruct((length, hidden_size), jnp.float32),
            jax.ShapeDtypeStruct((length, width), jnp.float32),
        ),
        in_specs=[resident, up, bias, down],
        out_specs=(hidden, hidden, resident),
        compiler_params=pltpu.CompilerParams(vmem_limit_bytes=48 << 20),
        name="mlp_forward",
    )(rows, blocks, up_bias.reshape(1, hidden_size), blocks)


def mlp_backward(rows, grad_branch, blocks, units, slopes):
    length, width = rows.shape
    up_count = blocks.shape[0] // 2
    split, resident, up, down, hidden, bias = mlp_specs(length, width, up_count)
    hidden_size = up_count * width
    return pl.pallas_call(
        mlp_backward_kernel,
        grid=(up_count * split,),
        out_shape=(
            jax.ShapeDtypeStruct((up_count, width, width), jnp.float32),
            jax.ShapeDtypeStruct((up_count, width, width), jnp.float32),
            jax.ShapeDtypeStruct((1, hidden_size), jnp.float32),
            jax.ShapeDtypeStruct((length, width), jnp.float32),
        ),
        in_specs=[resident, resident, up, down, hidden, hidden],
        out_specs=(
            pl.BlockSpec((None, width, HIDDEN_TILE), lambda t: (t // split, 0, t % split)),
            pl.BlockSpec((None, HIDDEN_TILE, width), lambda t: (t // split, t % split, 0)),
            bias,
            resident,
        ),
        scratch_shapes=[pltpu.VMEM((length, HIDDEN_TILE), jnp.bfloat16)],
        compiler_params=pltpu.CompilerParams(vmem_limit_bytes=48 << 20),
        name="mlp_backward",
    )(rows, grad_branch, blocks, blocks, units, slopes)


def layer_forward(blocks, vec_all, patch, attend):
    embedded = jnp.dot(patch, blocks[0], preferred_element_type=jnp.float32) + vec_all[0]
    normed_one = norm_rows(embedded, vec_all[1], vec_all[2]).astype(jnp.bfloat16)
    qkv_rows = jnp.einsum(
        "td,kde->kte", normed_one, blocks[1:4], preferred_element_type=jnp.float32
    )
    qkv_bias = jnp.stack([vec_all[3], jnp.zeros_like(vec_all[3]), vec_all[4]])
    qkv_rows = (qkv_rows + qkv_bias[:, None, :]).astype(jnp.bfloat16)
    attended, mlp_blocks = attend(qkv_rows)
    up_count = mlp_blocks.shape[0] // 2
    hidden = (
        embedded + jnp.dot(attended, blocks[4], preferred_element_type=jnp.float32) + vec_all[5]
    )
    normed_two = norm_rows(hidden, vec_all[6], vec_all[7]).astype(jnp.bfloat16)
    units, slopes, branch = mlp_forward(normed_two, mlp_blocks, vec_all[8 : 8 + up_count])
    output = hidden + branch + vec_all[8 + up_count]
    return (
        output,
        mlp_blocks,
        (embedded, normed_one, qkv_rows, attended, hidden, normed_two, slopes, units),
    )


def layer_backward(
    blocks,
    mlp_blocks,
    vec_all,
    patch,
    saved,
    pack_ids,
    key_codes,
    grad_output,
    grad_gain,
    grad_shift,
):
    embedded, normed_one, qkv_rows, attended, hidden, normed_two, slopes, units = saved
    feature_dim = patch.shape[1]
    up_count = mlp_blocks.shape[0] // 2
    grad_branch = grad_output.astype(jnp.bfloat16)
    grad_up, grad_down, up_sums, grad_normed_two = mlp_backward(
        normed_two, grad_branch, mlp_blocks, units, slopes
    )
    norm_two_back = jax.vjp(norm_rows, hidden, vec_all[6], vec_all[7])[1]
    grad_hidden_norm, grad_gain_two, grad_shift_two = norm_two_back(grad_normed_two)
    grad_hidden = grad_output + grad_hidden_norm
    grad_attn_out = grad_hidden.astype(jnp.bfloat16)
    grad_attended = jnp.einsum(
        "td,ed->te", grad_attn_out, blocks[4], preferred_element_type=jnp.float32
    ).astype(jnp.bfloat16)
    grad_qkv = attention_backward(qkv_rows, pack_ids, key_codes, grad_attended)
    grad_normed_one = jnp.einsum(
        "kte,kde->td", grad_qkv, blocks[1:4], preferred_element_type=jnp.float32
    )
    norm_one_back = jax.vjp(norm_rows, embedded, vec_all[1], vec_all[2])[1]
    grad_embed_norm, grad_gain_one, grad_shift_one = norm_one_back(grad_normed_one)
    grad_embedded = (grad_hidden + grad_embed_norm).astype(jnp.bfloat16)
    lefts = (patch, normed_one, attended)
    rights = (grad_embedded, grad_qkv, grad_attn_out)
    bias_sums = jnp.stack(
        [
            jnp.sum(grad_embedded.astype(jnp.float32), 0),
            grad_gain_one,
            grad_shift_one,
            jnp.sum(grad_qkv[0].astype(jnp.float32), 0),
            jnp.sum(grad_qkv[2].astype(jnp.float32), 0),
            jnp.sum(grad_attn_out.astype(jnp.float32), 0),
            grad_gain_two,
            grad_shift_two,
        ]
    )
    up_sums = up_sums.reshape(up_count, feature_dim)
    tail_sums = jnp.stack([jnp.sum(grad_branch.astype(jnp.float32), 0), grad_gain, grad_shift])
    return (lefts, rights, (grad_up, grad_down), jnp.concatenate([bias_sums, up_sums, tail_sums], 0))


def torus_place():
    dp, cls = lax.axis_index("dp"), lax.axis_index("cls")
    return dp // 2, dp % 2, cls // 2, cls % 2


def torus_device(z, y, x, core):
    return (z * 2 + y, x * 2 + core)


def encode(pieces, code_refs, scale_ref):
    top = None
    for piece in pieces:
        peak = jnp.max(jnp.abs(piece()), 0, keepdims=True)
        top = peak if top is None else jnp.maximum(top, peak)
    top = jnp.maximum(top, CODE_FLOOR)
    inverse = CODE_TOP / top
    for piece, code_ref in zip(pieces, code_refs):
        code_ref[...] = jnp.round(piece() * inverse).astype(jnp.int32).astype(jnp.int16)
    scale_ref[...] = top * (1.0 / CODE_TOP)


def decode(code, scale):
    return code.astype(jnp.int32).astype(jnp.float32) * scale


def reduce_kernel(counts, *refs):
    sources, refs = refs[: len(counts)], refs[len(counts) :]
    (patch_hbm, first_hbm, mid_hbm, dpatch_hbm, dfirst_hbm, dmid_hbm,
     vec_ref, tail_ref, left_hbm, right_hbm,
     own_hbm, left_out_hbm, right_out_hbm, step_hbm, wide_ref, facts_ref, vec_out_ref,
     left_buf, right_buf, right_full, outs_buf, squares, high_buf, low_buf, sum_slots, tail_slots,
     lhs_buf, rhs_buf, pair_sem,
     in_sem, sum_send, sum_recv, tail_send, tail_recv,
     acc, spare, kept, sent0, got0, sent1, got1, sent2, got2, sent3, got3, sent4, got4,
     ss0, gs0, ss1, gs1, ss2, gs2, ss3, gs3, ss4, gs4, codes, scales, vec_got,
     load_sem, out_sem, send_sem, recv_sem, send_scale_sem, recv_scale_sem,
     vec_send_sem, vec_recv_sem) = refs
    stored = sum(counts)
    paired = dfirst_hbm.shape[0] + 2
    total = stored + paired
    half, width = codes.shape[1], codes.shape[2]
    cols = width // 2
    z, y, x, core = torus_place()
    upper = z // 2
    inner = (z % 2) != upper
    mate_core = torus_device(z, y, x, 1 - core)
    mate_x = torus_device(z, y, 1 - x, core)
    mate_y = torus_device(z, 1 - y, x, core)
    mate_z = torus_device(z + 1 - 2 * (z % 2), y, x, core)
    mate_mid = torus_device(3 - z, y, x, core)
    mate_far = torus_device((z + 2) % 4, y, x, core)

    barrier = pltpu.get_barrier_semaphore()
    dp, cls = lax.axis_index("dp"), lax.axis_index("cls")
    everyone = tail_slots.shape[0]
    quarter = sum_slots.shape[0]
    me = dp * 4 + cls

    def any_mate(n):
        other = lax.rem(me + n, everyone)
        return (other // 4, lax.rem(other, 4))

    def half_mate(n):
        return (upper * quarter + lax.rem(dp + n, quarter), cls)

    for n in range(1, everyone):
        pl.semaphore_signal(barrier, inc=1, device_id=any_mate(n), device_id_type=MESH)
    pl.semaphore_wait(barrier, everyone - 1)
    own = lax.rem(dp, quarter) * left_buf.shape[1]

    own_cols = pl.ds(pl.multiple_of(core * cols, 128), cols)
    other_cols = pl.ds(pl.multiple_of((1 - core) * cols, 128), cols)

    def rows_at(start, size):
        return pl.ds(pl.multiple_of(start, PIECE), size)

    def loads(m, body):
        start = 0
        for source, count in zip(sources, counts):
            def one(source=source, start=start):
                pair = (
                    pltpu.make_async_copy(
                        source.at[m - start, :, own_cols], acc.at[m % 5], load_sem.at[m % 2, 0]
                    ),
                    pltpu.make_async_copy(
                        source.at[m - start, :, other_cols], spare.at[m % 2], load_sem.at[m % 2, 1]
                    ),
                )
                for copy in pair:
                    body(copy)

            pl.when((m >= start) & (m < start + count))(one)
            start += count

    def block_of(m):
        return lax.rem(m + paired, total)

    def pair_loads(m, body):
        index = m - stored
        last = paired - 1

        def run(left, right):
            body(pltpu.make_async_copy(left, lhs_buf.at[m % 2], pair_sem.at[m % 2, 0]))
            body(pltpu.make_async_copy(right, rhs_buf.at[m % 2], pair_sem.at[m % 2, 1]))

        pl.when(index == 0)(lambda: run(patch_hbm, dpatch_hbm))
        pl.when((index > 0) & (index < last))(
            lambda: run(first_hbm, dfirst_hbm.at[jnp.clip(index - 1, 0, last - 2)])
        )
        pl.when(index == last)(lambda: run(mid_hbm, dmid_hbm))

    def pair_product(m):
        chunk = 2 * FEATURE_TILE
        for r in range(0, width, chunk):
            left = lhs_buf[m % 2, :, r : r + chunk].T
            for target, columns in ((acc.at[m % 5], own_cols), (spare.at[m % 2], other_cols)):
                target[r : r + chunk, :] = jnp.dot(
                    left, rhs_buf[m % 2, :, columns], preferred_element_type=jnp.float32
                )

    def message(stage, m, source, scale_source, target, scale_target, mate):
        return (
            pltpu.make_async_remote_copy(
                src_ref=source, dst_ref=target,
                send_sem=send_sem.at[stage, m % 2], recv_sem=recv_sem.at[stage, m],
                device_id=mate, device_id_type=MESH,
            ),
            pltpu.make_async_remote_copy(
                src_ref=scale_source, dst_ref=scale_target,
                send_sem=send_scale_sem.at[stage, m % 2], recv_sem=recv_scale_sem.at[stage, m],
                device_id=mate, device_id_type=MESH,
            ),
        )

    def first(m):
        return message(0, m, sent0.at[m % 2], ss0.at[m % 2], got0.at[m], gs0.at[m], mate_core)

    def second(m, b):
        return message(
            1 + b, m, sent1.at[m % 2, b], ss1.at[m % 2, b], got1.at[m, b], gs1.at[m, b],
            mate_y if b else mate_x,
        )

    def third(m, b):
        return message(
            3 + b, m, sent2.at[m % 2, b], ss2.at[m % 2, b], got2.at[m, b], gs2.at[m, b],
            mate_x if b else mate_y,
        )

    def fourth(m):
        return message(5, m, sent3.at[m % 2], ss3.at[m % 2], got3.at[m], gs3.at[m], mate_z)

    def fifth(m):
        return message(6, m, sent4.at[m % 2], ss4.at[m % 2], got4.at[m], gs4.at[m], mate_mid)

    piece_a = 2 * x + y
    piece_b = 4 + 2 * y + x

    def spread(stage, m, piece, count, mate, columns=own_cols):
        rows = pl.ds(pl.multiple_of(piece * PIECE, PIECE), count * PIECE)
        block = codes.at[m, rows, columns]
        scale = scales.at[m, pl.ds(piece, count), :, columns]
        return message(stage, m, block, scale, block, scale, mate)

    def start(copies):
        for copy in copies:
            copy.start()

    def wait_send(copies):
        for copy in copies:
            copy.wait_send()

    def wait_recv(copies):
        for copy in copies:
            copy.wait_recv()

    def vec_copy(step, mate):
        return pltpu.make_async_remote_copy(
            src_ref=vec_got.at[step, 0], dst_ref=vec_got.at[step, 1],
            send_sem=vec_send_sem.at[step], recv_sem=vec_recv_sem.at[step],
            device_id=mate, device_id_type=MESH,
        )

    vec_mates = (mate_core, mate_x, mate_y, mate_z, mate_far)

    loads(jnp.int32(0), lambda copy: copy.start())
    vec_got[0, 0] = vec_ref[...]
    vec_copy(0, vec_mates[0]).start()

    def step(t, carry):
        for n in range(1, 6):
            @pl.when(t == n)
            def _(n=n):
                vec_copy(n - 1, vec_mates[n - 1]).wait()
                value = vec_got[n - 1, 0] + vec_got[n - 1, 1]
                if n < 5:
                    vec_got[n, 0] = value
                    vec_copy(n, vec_mates[n]).start()
                else:
                    vec_out_ref[...] = value

        @pl.when(t < total)
        def _():
            m = t

            @pl.when(m < stored)
            def _():
                loads(m, lambda copy: copy.wait())

            @pl.when(m + 1 < stored)
            def _():
                loads(m + 1, lambda copy: copy.start())

            @pl.when((m + 1 >= stored) & (m + 1 < total))
            def _():
                pair_loads(m + 1, lambda copy: copy.start())

            @pl.when(m >= stored)
            def _():
                pair_loads(m, lambda copy: copy.wait())
                pair_product(m)

            span = 2 * PIECE
            encode(
                [lambda r=r: spare[m % 2, r : r + span, :] for r in range(0, 2 * half, span)],
                [sent0.at[m % 2, r : r + span, :] for r in range(0, 2 * half, span)],
                ss0.at[m % 2],
            )
            start(first(m))

        @pl.when((t >= 1) & (t < total + 1))
        def _():
            m = t - 1
            copies = first(m)
            wait_send(copies)
            wait_recv(copies)
            slot = m % 5
            span = 2 * PIECE
            for r in range(0, 2 * half, span):
                acc[slot, r : r + span, :] += decode(got0[m, r : r + span, :], gs0[m])
            for b in range(2):
                other = (1 - y) if b else (1 - x)
                begins = [h * half + b * 4 * PIECE + other * span for h in range(2)]
                encode(
                    [lambda s=s: acc[slot, rows_at(s, span), :] for s in begins],
                    [sent1.at[m % 2, b, h] for h in range(2)],
                    ss1.at[m % 2, b],
                )
                start(second(m, b))

        @pl.when((t >= 2) & (t < total + 2))
        def _():
            m = t - 2
            slot = m % 5
            span = 2 * PIECE
            for b in range(2):
                copies = second(m, b)
                wait_send(copies)
                wait_recv(copies)
                mine = y if b else x
                other = (1 - x) if b else (1 - y)
                begins = [h * half + b * 4 * PIECE + mine * span for h in range(2)]
                for h, s in enumerate(begins):
                    acc[slot, rows_at(s, span), :] += decode(got1[m, b, h], gs1[m, b])
                encode(
                    [lambda s=s: acc[slot, rows_at(s + other * PIECE, PIECE), :] for s in begins],
                    [sent2.at[m % 2, b, h] for h in range(2)],
                    ss2.at[m % 2, b],
                )
                start(third(m, b))

        @pl.when((t >= 3) & (t < total + 3))
        def _():
            m = t - 3
            slot = m % 5
            for b in range(2):
                copies = third(m, b)
                wait_send(copies)
                wait_recv(copies)
                place = piece_b if b else piece_a
                for h in range(2):
                    kept[m % 3, h, b] = acc[
                        slot, rows_at(h * half + place * PIECE, PIECE), :
                    ] + decode(got2[m, b, h], gs2[m, b])

            @pl.when(jnp.logical_not(inner))
            def _():
                pairs = [(h, b) for h in range(2) for b in range(2)]
                encode(
                    [lambda h=h, b=b: kept[m % 3, h, b] for h, b in pairs],
                    [sent3.at[m % 2, h, b] for h, b in pairs],
                    ss3.at[m % 2],
                )
                start(fourth(m))

        @pl.when((t >= 4) & (t < total + 4))
        def _():
            m = t - 4
            copies = fourth(m)

            @pl.when(jnp.logical_not(inner))
            def _():
                wait_send(copies)

            @pl.when(inner)
            def _():
                wait_recv(copies)
                for h in range(2):
                    for b in range(2):
                        kept[m % 3, h, b] += decode(got3[m, h, b], gs3[m])
                encode(
                    [lambda b=b: kept[m % 3, 1 - upper, b] for b in range(2)],
                    [sent4.at[m % 2, b] for b in range(2)],
                    ss4.at[m % 2],
                )
                start(fifth(m))

        @pl.when((t >= 5) & (t < total + 5))
        def _():
            m = t - 5

            @pl.when(inner)
            def _():
                copies = fifth(m)
                wait_send(copies)
                wait_recv(copies)
                for b in range(2):
                    place = piece_b if b else piece_a
                    value = kept[m % 3, upper, b] + decode(got4[m, b], gs4[m])
                    encode(
                        [lambda value=value: value],
                        [codes.at[m, rows_at(place * PIECE, PIECE), own_cols]],
                        scales.at[m, place, :, own_cols],
                    )
                    start(spread(7 + b, m, place, 1, mate_z))

        @pl.when((t >= 6) & (t < total + 6))
        def _():
            m = t - 6
            for b in range(2):
                place = piece_b if b else piece_a
                copies = spread(7 + b, m, place, 1, mate_z)

                @pl.when(inner)
                def _(copies=copies):
                    wait_send(copies)

                @pl.when(jnp.logical_not(inner))
                def _(copies=copies):
                    wait_recv(copies)

                start(spread(9 + b, m, place, 1, mate_x if b else mate_y))

        @pl.when((t >= 7) & (t < total + 7))
        def _():
            m = t - 7
            for b in range(2):
                place = piece_b if b else piece_a
                theirs = (4 + 2 * y + 1 - x) if b else (2 * x + 1 - y)
                wait_send(spread(9 + b, m, place, 1, mate_x if b else mate_y))
                wait_recv(spread(9 + b, m, theirs, 1, mate_x if b else mate_y))
                begin = (4 + 2 * y) if b else 2 * x
                start(spread(11 + b, m, begin, 2, mate_y if b else mate_x))

        @pl.when((t >= 8) & (t < total + 8))
        def _():
            m = t - 8
            for b in range(2):
                begin = (4 + 2 * y) if b else 2 * x
                theirs = (4 + 2 * (1 - y)) if b else 2 * (1 - x)
                wait_send(spread(11 + b, m, begin, 2, mate_y if b else mate_x))
                wait_recv(spread(11 + b, m, theirs, 2, mate_y if b else mate_x))
            start(spread(13, m, 0, 8, mate_core))

        def ins(m):
            return (
                pltpu.make_async_copy(
                    left_hbm.at[block_of(m)], left_buf.at[m % 2], in_sem.at[m % 2, 0]
                ),
                pltpu.make_async_copy(
                    right_hbm.at[:, block_of(m)], right_buf.at[m % 2], in_sem.at[m % 2, 1]
                ),
            )

        def outs(m):
            targets = (own_hbm, left_out_hbm, right_out_hbm, step_hbm)
            return [
                pltpu.make_async_copy(
                    outs_buf.at[m % 2, n], target.at[block_of(m)], out_sem.at[m % 2, n]
                )
                for n, target in enumerate(targets)
            ]

        @pl.when((t >= 8) & (t < total + 8))
        def _():
            start(ins(t - 8))

        @pl.when((t >= 11) & (t < total + 11))
        def _():
            for copy in outs(t - 11):
                copy.wait()

        @pl.when((t >= 9) & (t < total + 9))
        def _():
            m = t - 9
            wait_send(spread(13, m, 0, 8, mate_core))
            wait_recv(spread(13, m, 0, 8, mate_core, other_cols))
            for copy in ins(m):
                copy.wait()
            precondition_block(
                own, codes.at[m], scales.at[m], left_buf.at[m % 2], right_buf.at[m % 2],
                outs_buf.at[m % 2], squares.at[m], high_buf, low_buf, right_full,
            )
            start(outs(m))

        return carry

    lax.fori_loop(0, total + 11, step, 0)

    def folded(row):
        return sum(row[:, n * 128 : (n + 1) * 128] for n in range(row.shape[1] // 128))

    layer = jnp.zeros((1, 128), jnp.float32)
    mine = lax.rem(dp, quarter)
    sum_slots[mine] = jnp.zeros(sum_slots.shape[1:], jnp.float32)
    for m in range(total):
        layer = layer + folded(squares[m, 0:1, :])
        for quad in range(2):
            part = squares[m, 1:2, quad * cols : (quad + 1) * cols]
            row = 2 * ((m + paired) % total) + quad
            sum_slots[mine, row : row + 1, :] = folded(part)
    once = (cls == 0).astype(jnp.float32)
    first_row = lax.broadcasted_iota(jnp.int32, tail_ref.shape, 0) == 0
    tail_slots[me] = tail_ref[...] + jnp.where(first_row, once * layer, 0.0)

    def sum_copy(n, slot):
        return pltpu.make_async_remote_copy(
            src_ref=sum_slots.at[slot], dst_ref=sum_slots.at[slot],
            send_sem=sum_send.at[n], recv_sem=sum_recv.at[slot],
            device_id=half_mate(n), device_id_type=MESH,
        )

    def tail_copy(n, slot):
        return pltpu.make_async_remote_copy(
            src_ref=tail_slots.at[slot], dst_ref=tail_slots.at[slot],
            send_sem=tail_send.at[n], recv_sem=tail_recv.at[slot],
            device_id=any_mate(n), device_id_type=MESH,
        )

    for n in range(1, quarter):
        sum_copy(n, lax.rem(dp, quarter)).start()
    for n in range(1, everyone):
        tail_copy(n, me).start()
    for n in range(1, quarter):
        sum_copy(n, lax.rem(dp, quarter)).wait_send()
        sum_copy(n, lax.rem(dp + n, quarter)).wait_recv()
    for n in range(1, everyone):
        tail_copy(n, me).wait_send()
        tail_copy(n, lax.rem(me + n, everyone)).wait_recv()
    value = sum_slots[0]
    for n in range(1, quarter):
        value = value + sum_slots[n]
    tail = tail_slots[0]
    for n in range(1, everyone):
        tail = tail + tail_slots[n]
    vec = vec_out_ref[...]
    vec_squares = jnp.sum(jnp.sum(vec * vec, 0, keepdims=True), 1, keepdims=True)
    norm = jnp.sqrt(jnp.sum(tail[0:1], 1, keepdims=True) + vec_squares)
    factor = CLIP_NORM / jnp.maximum(norm, CLIP_NORM)
    mean_squares = jnp.sum(value, 1, keepdims=True) / (half * cols) * factor * factor
    scale = SHAMPOO_RATE * factor * lax.rsqrt(mean_squares + ROOT_EPS)
    for b in range(total):
        for quad in range(2):
            row = 2 * b + quad
            wide_ref[b, :, quad * cols : (quad + 1) * cols] = jnp.broadcast_to(
                scale[row : row + 1], (1, cols)
            )
    rows = lax.broadcasted_iota(jnp.int32, facts_ref.shape, 0)
    loss = jnp.sum(tail[1:2], 1, keepdims=True)
    facts_ref[...] = jnp.where(rows == 0, loss, jnp.where(rows == 1, norm, factor))


def reduce_gradients(
    arrays, lefts, rights, vec_sums, tail, root_left, right_codes, dp_count, cls_count
):
    counts = tuple(array.shape[0] for array in arrays)
    total, rows, width = root_left.shape
    length = lefts[0].shape[0]
    parts, coded_rows = right_codes.shape[0], right_codes.shape[2]
    half, cols = width // 2, width // 2
    sum_rows = 2 * total + -2 * total % 8
    f32, i16 = jnp.float32, jnp.int16

    def pair(*shape):
        return [pltpu.VMEM((2,) + shape, i16), pltpu.VMEM((total,) + shape, i16)]

    def scale_pair(*shape):
        return [
            pltpu.VMEM((2,) + shape + (1, cols), f32),
            pltpu.VMEM((total,) + shape + (1, cols), f32),
        ]

    hbm = pl.BlockSpec(memory_space=pl.ANY)
    vmem = pl.BlockSpec(memory_space=pltpu.VMEM)
    return pl.pallas_call(
        functools.partial(reduce_kernel, counts),
        out_shape=(jax.ShapeDtypeStruct((total, rows, width), f32),) * 4
        + (
            jax.ShapeDtypeStruct((total, 1, width), f32),
            jax.ShapeDtypeStruct(tail.shape, f32),
            jax.ShapeDtypeStruct(vec_sums.shape, f32),
        ),
        in_specs=[hbm] * (len(arrays) + 6) + [vmem, vmem, hbm, hbm],
        out_specs=(hbm,) * 4 + (vmem,) * 3,
        scratch_shapes=[
            pltpu.VMEM((2, rows, width), f32),
            pltpu.VMEM((2, parts, coded_rows, width), jnp.int32),
            pltpu.VMEM((half, width), f32),
            pltpu.VMEM((2, 4, rows, width), f32),
            pltpu.VMEM((total, 2, width), f32),
            pltpu.VMEM((half, width), jnp.bfloat16),
            pltpu.VMEM((half, width), jnp.bfloat16),
            pltpu.VMEM((dp_count // 2, sum_rows, 128), f32),
            pltpu.VMEM((dp_count * cls_count,) + tail.shape, f32),
            pltpu.VMEM((2, length, width), jnp.bfloat16),
            pltpu.VMEM((2, length, width), jnp.bfloat16),
            pltpu.SemaphoreType.DMA((2, 2)),
            pltpu.SemaphoreType.DMA((2, 2)),
            pltpu.SemaphoreType.DMA((dp_count // 2,)),
            pltpu.SemaphoreType.DMA((dp_count // 2,)),
            pltpu.SemaphoreType.DMA((dp_count * cls_count,)),
            pltpu.SemaphoreType.DMA((dp_count * cls_count,)),
            pltpu.VMEM((5, width, cols), f32),
            pltpu.VMEM((2, width, cols), f32),
            pltpu.VMEM((3, 2, 2, PIECE, cols), f32),
        ]
        + pair(width, cols)
        + pair(2, 2, 2 * PIECE, cols)
        + pair(2, 2, PIECE, cols)
        + pair(2, 2, PIECE, cols)
        + pair(2, PIECE, cols)
        + scale_pair()
        + scale_pair(2)
        + scale_pair(2)
        + scale_pair()
        + scale_pair()
        + [
            pltpu.VMEM((total, half, width), i16),
            pltpu.VMEM((total, half // PIECE, 1, width), f32),
            pltpu.VMEM((5, 2) + vec_sums.shape, f32),
            pltpu.SemaphoreType.DMA((2, 2)),
            pltpu.SemaphoreType.DMA((2, 4)),
            pltpu.SemaphoreType.DMA((14, 2)),
            pltpu.SemaphoreType.DMA((14, total)),
            pltpu.SemaphoreType.DMA((14, 2)),
            pltpu.SemaphoreType.DMA((14, total)),
            pltpu.SemaphoreType.DMA((5,)),
            pltpu.SemaphoreType.DMA((5,)),
        ],
        compiler_params=pltpu.CompilerParams(
            collective_id=1, has_side_effects=True, vmem_limit_bytes=60 << 20
        ),
        name="reduce_gradients",
    )(*arrays, *lefts, *rights, vec_sums, tail, root_left, right_codes)


def split_float(values):
    high = values.astype(jnp.bfloat16)
    return high, (values - high.astype(jnp.float32)).astype(jnp.bfloat16)


def stacked_dot(lefts, right, contract_last):
    rows = lefts[0].shape[0]
    left = jnp.concatenate(lefts, 0) if len(lefts) > 1 else lefts[0]
    dims = (((1,), (1 if contract_last else 0,)), ((), ()))
    out = lax.dot_general(left, right, dims, preferred_element_type=jnp.float32)
    return [out[n * rows : (n + 1) * rows] for n in range(len(lefts))]


def encode_roots(part):
    top = jnp.max(jnp.abs(part), 1, keepdims=True)
    level = jnp.ceil(jnp.log2(jnp.maximum(top, 1e-30)))
    codes = jnp.round(part * jnp.exp2(15.0 - level))
    codes = jnp.clip(codes, -32767.0, 32767.0).astype(jnp.int32)
    levels = jnp.broadcast_to(level.astype(jnp.int32), (part.shape[0], 8, part.shape[2]))
    upper = jnp.concatenate([codes[:, 0:8], codes[:, 16:24]], 1)
    lower = jnp.concatenate([codes[:, 8:16], levels], 1)
    return upper * 65536 + (lower + 32768)


def precondition_block(
    own, codes_ref, scales_ref, left_ref, right_codes, outs_ref, squares_ref, high_ref, low_ref,
    right_ref
):
    half, width = codes_ref.shape
    rows = left_ref.shape[0]
    own_rows = pl.ds(pl.multiple_of(own, PIECE), rows)
    parts = right_codes.shape[0]
    size = half // parts
    for n in range(parts):
        packed = right_codes[n]
        upper = lax.shift_right_arithmetic(packed, jnp.full_like(packed, 16)).astype(jnp.float32)
        lower = ((packed & 65535) - 32768).astype(jnp.float32)
        scale = jnp.exp2(lower[8:9] - 15.0)
        right_ref[n * size : n * size + 8, :] = upper[0:8] * scale
        right_ref[n * size + 8 : n * size + 16, :] = lower[0:8] * scale
        right_ref[n * size + 16 : n * size + 24, :] = upper[8:16] * scale
    for piece in range(half // PIECE):
        part = slice(piece * PIECE, (piece + 1) * PIECE)
        high_ref[part, :], low_ref[part, :] = split_float(
            decode(codes_ref[part, :], scales_ref[piece])
        )
    own_value = high_ref[own_rows, :].astype(jnp.float32) + low_ref[own_rows, :].astype(jnp.float32)
    outs_ref[0] = own_value
    squares_ref[0:1, :] = jnp.sum(own_value * own_value, 0, keepdims=True)
    picks = (
        lax.broadcasted_iota(jnp.int32, (rows, half), 1)
        == lax.broadcasted_iota(jnp.int32, (rows, half), 0) + own
    ).astype(jnp.float32).astype(jnp.bfloat16)
    for quad in range(2):
        cols = slice(quad * half, (quad + 1) * half)
        high, low = high_ref[:, cols], low_ref[:, cols]
        mine_high, mine_low = high_ref[own_rows, cols], low_ref[own_rows, cols]
        hh, lh, turned_high = stacked_dot([mine_high, mine_low, picks], high, True)
        hl, turned_low = stacked_dot([mine_high, picks], low, True)
        outs_ref[1, :, cols] = hh + (lh + hl)
        turned_high = turned_high.astype(jnp.bfloat16)
        turned_low = turned_low.astype(jnp.bfloat16)
        root_high, root_low = split_float(left_ref[:, cols])
        thh, tlh, rhh, rlh = stacked_dot([turned_high, turned_low, root_high, root_low], high, False)
        thl, rhl = stacked_dot([turned_high, root_high], low, False)
        outs_ref[2, :, cols] = thh + (tlh + thl)
        half_step = rhh + (rlh + rhl)
        step_high, step_low = split_float(half_step)
        right_high, right_low = split_float(right_ref[:, cols])
        shh, slh = stacked_dot([step_high, step_low], right_high, False)
        (shl,) = stacked_dot([step_high], right_low, False)
        direction = shh + (slh + shl)
        outs_ref[3, :, cols] = direction
        squares_ref[1:2, cols] = jnp.sum(direction * direction, 0, keepdims=True)


def class_sum_kernel(in_ref, out_ref, slots, send_sem, recv_sem):
    dp, cls = lax.axis_index("dp"), lax.axis_index("cls")
    total, rows = slots.shape[0], slots.shape[1]
    barrier = pltpu.get_barrier_semaphore()
    for n in range(1, total):
        pl.semaphore_signal(
            barrier, inc=1, device_id=(dp, lax.rem(cls + n, total)), device_id_type=MESH
        )
    pl.semaphore_wait(barrier, total - 1)

    def part(index):
        return in_ref.at[pl.ds(pl.multiple_of(index * rows, 8), rows)]

    def copy(n, slot):
        mate = lax.rem(cls + n, total)
        return pltpu.make_async_remote_copy(
            src_ref=part(mate), dst_ref=slots.at[slot],
            send_sem=send_sem.at[n], recv_sem=recv_sem.at[slot],
            device_id=(dp, mate), device_id_type=MESH,
        )

    for n in range(1, total):
        copy(n, cls).start()
    slots[cls] = part(cls)[...]
    for n in range(1, total):
        copy(n, cls).wait_send()
        copy(n, lax.rem(cls + n, total)).wait_recv()
    value = slots[0]
    for n in range(1, total):
        value = value + slots[n]
    out_ref[...] = value


def class_sum(values, cls_count):
    rows = values.shape[0] // cls_count
    vmem = pl.BlockSpec(memory_space=pltpu.VMEM)
    return pl.pallas_call(
        class_sum_kernel,
        out_shape=jax.ShapeDtypeStruct((rows, values.shape[1]), jnp.float32),
        in_specs=[vmem],
        out_specs=vmem,
        scratch_shapes=[
            pltpu.VMEM((cls_count, rows, values.shape[1]), jnp.float32),
            pltpu.SemaphoreType.DMA((cls_count,)),
            pltpu.SemaphoreType.DMA((cls_count,)),
        ],
        compiler_params=pltpu.CompilerParams(collective_id=2, has_side_effects=True),
        name="class_sum",
    )(values)


def gather_steps(own_ref, out_ref, send_sem, recv_sem, copy_sem):
    count, rows, width = own_ref.shape
    cols = width // 2
    z, y, x, core = torus_place()
    mate_core = torus_device(z, y, x, 1 - core)
    mate_x = torus_device(z, y, 1 - x, core)
    mate_y = torus_device(z, 1 - y, x, core)
    own_cols = pl.ds(pl.multiple_of(core * cols, 128), cols)
    other_cols = pl.ds(pl.multiple_of((1 - core) * cols, 128), cols)
    spare = rows - SPAN
    held = x * spare
    lone = (x * SPAN, (1 - x) * SPAN)

    def share(m, zz, yy, start, size):
        begin = (zz * 2 + yy) * rows + start
        return out_ref.at[m, pl.ds(pl.multiple_of(begin, 16), size), own_cols]

    def copy(slot, arrival, m, source, target, mate):
        return pltpu.make_async_remote_copy(
            src_ref=source, dst_ref=target,
            send_sem=send_sem.at[slot, m % 2], recv_sem=recv_sem.at[arrival, m],
            device_id=mate, device_id_type=MESH,
        )

    def local(m):
        return pltpu.make_async_copy(
            own_ref.at[m, :, own_cols], share(m, z, y, 0, rows), copy_sem.at[m % 2]
        )

    def along(m, n, outgoing):
        other = lax.rem(z + n, 4)
        origin = z if outgoing else other
        source = own_ref.at[m, pl.ds(pl.multiple_of(held, 16), SPAN), own_cols]
        mate = torus_device(other, y, x, core)
        return copy(n - 1, origin, m, source, share(m, origin, y, held, SPAN), mate)

    def cross(m, n, outgoing):
        block = share(m, n, y if outgoing else 1 - y, held, SPAN)
        return copy(3 + n, 4 + n, m, block, block, mate_y)

    def patch(m, n, outgoing):
        index = lax.rem(z * 2 + y + n, SHARES)
        block = share(m, index // 2, lax.rem(index, 2), lone[0 if outgoing else 1], spare)
        return copy(6 + n, 7 + n, m, block, block, mate_x)

    def swap(m, columns):
        block = out_ref.at[m, :, columns]
        return copy(14, 15, m, block, block, mate_core)

    def finish(copies):
        for outgoing, incoming in copies:
            outgoing.wait_send()
            incoming.wait_recv()

    def step(t):
        @pl.when(t < count)
        def _():
            local(t).start()
            for n in range(1, 4):
                along(t, n, True).start()

        @pl.when((t >= 1) & (t < count + 1))
        def _():
            m = t - 1
            local(m).wait()
            finish([(along(m, n, True), along(m, n, False)) for n in range(1, 4)])
            for n in range(4):
                cross(m, n, True).start()

        @pl.when((t >= 2) & (t < count + 2))
        def _():
            m = t - 2
            finish([(cross(m, n, True), cross(m, n, False)) for n in range(4)])
            for n in range(1, SHARES):
                patch(m, n, True).start()

        @pl.when((t >= 3) & (t < count + 3))
        def _():
            m = t - 3
            finish([(patch(m, n, True), patch(m, n, False)) for n in range(1, SHARES)])
            swap(m, own_cols).start()

        @pl.when((t >= 4) & (t < count + 4))
        def _():
            m = t - 4
            swap(m, own_cols).wait_send()
            swap(m, other_cols).wait_recv()

    return step, count + GATHER_DEPTH


def column_mate(n):
    z, y, x, core = torus_place()
    other = lax.rem(z * 2 + y + n, SHARES)
    return torus_device(other // 2, lax.rem(other, 2), x, core)


def gather_barrier():
    z, y, x, core = torus_place()
    barrier = pltpu.get_barrier_semaphore()
    mates = [torus_device(z, y, x, 1 - core), torus_device(z, y, 1 - x, core)]
    for mate in mates + [column_mate(n) for n in range(1, SHARES)]:
        pl.semaphore_signal(barrier, inc=1, device_id=mate, device_id_type=MESH)
    pl.semaphore_wait(barrier, SHARES + 1)


def gather_kernel(
    own_ref, vec_ref, out_ref, vec_out_ref, send_sem, recv_sem, copy_sem, vec_send, vec_recv
):
    z, y, _, _ = torus_place()
    me = z * 2 + y
    gather_barrier()

    def vec_copy(n, slot):
        return pltpu.make_async_remote_copy(
            src_ref=vec_ref, dst_ref=vec_out_ref.at[slot],
            send_sem=vec_send.at[n], recv_sem=vec_recv.at[slot],
            device_id=column_mate(n), device_id_type=MESH,
        )

    for n in range(1, SHARES):
        vec_copy(n, me).start()
    vec_out_ref[me] = vec_ref[...]
    gather_step, turns = gather_steps(own_ref, out_ref, send_sem, recv_sem, copy_sem)

    def step(t, carry):
        gather_step(t)
        return carry

    lax.fori_loop(0, turns, step, 0)
    for n in range(1, SHARES):
        vec_copy(n, me).wait_send()
        vec_copy(n, lax.rem(me + n, SHARES)).wait_recv()


def gather_semaphores(count):
    return [
        pltpu.SemaphoreType.DMA((15, 2)),
        pltpu.SemaphoreType.DMA((16, count)),
        pltpu.SemaphoreType.DMA((2,)),
    ]


def attention_gather_kernel(
    qids_ref, kcodes_ref, q_ref, k_ref, v_ref, own_ref, out_ref, blocks_ref,
    bias_ref, send_sem, recv_sem, copy_sem
):
    pair, tiles = pl.program_id(0), q_ref.shape[0] // QTILE
    slots = pl.num_programs(0) * tiles

    @pl.when(pair == 0)
    def _():
        gather_barrier()

    gather_step, turns = gather_steps(own_ref, blocks_ref, send_sem, recv_sem, copy_sem)
    attention_bias(qids_ref, kcodes_ref, bias_ref)
    for tile in range(tiles):
        slot = pair * tiles + tile
        begin, end = slot * turns // slots, (slot + 1) * turns // slots

        @pl.when(begin < end)
        def _(begin=begin):
            gather_step(begin)

        attention_tile(tile, q_ref, k_ref, v_ref, out_ref, bias_ref)


def attention_forward_gathering(qkv_rows, pack_ids, key_codes, own):
    _, length, width = qkv_rows.shape
    count, rows, _ = own.shape
    tiles = length // QTILE
    assert count + GATHER_DEPTH <= tiles * (width // PAIR)
    return pl.pallas_call(
        attention_gather_kernel,
        grid=(width // PAIR,),
        out_shape=(
            jax.ShapeDtypeStruct((length, width), jnp.bfloat16),
            jax.ShapeDtypeStruct((count, SHARES * rows, width), own.dtype),
        ),
        in_specs=[whole_spec((length, 1)), whole_spec((1, length))]
        + [pair_spec(length, part) for part in range(3)]
        + [whole_spec(own.shape)],
        out_specs=(pair_spec(length), pl.BlockSpec(memory_space=pl.ANY)),
        scratch_shapes=[pltpu.VMEM(bias_shape(length), jnp.float32)] + gather_semaphores(count),
        compiler_params=pltpu.CompilerParams(
            collective_id=4, has_side_effects=True, vmem_limit_bytes=40 << 20
        ),
        name="attention_forward",
    )(pack_ids[:, None], key_codes[None, :], qkv_rows, qkv_rows, qkv_rows, own)


def gather_weights(own, vec):
    count, rows, width = own.shape
    hbm = pl.BlockSpec(memory_space=pl.ANY)
    vmem = pl.BlockSpec(memory_space=pltpu.VMEM)
    return pl.pallas_call(
        gather_kernel,
        out_shape=(
            jax.ShapeDtypeStruct((count, SHARES * rows, width), own.dtype),
            jax.ShapeDtypeStruct((SHARES,) + vec.shape, vec.dtype),
        ),
        in_specs=[vmem, vmem],
        out_specs=(hbm, vmem),
        scratch_shapes=gather_semaphores(count)
        + [pltpu.SemaphoreType.DMA((SHARES,)), pltpu.SemaphoreType.DMA((SHARES,))],
        compiler_params=pltpu.CompilerParams(
            collective_id=3, has_side_effects=True, vmem_limit_bytes=32 << 20
        ),
        name="gather_weights",
    )(own, vec)


def adam_step(weight, grad, first, second, count):
    first = BETA_FIRST * first + (1.0 - BETA_FIRST) * grad
    second = BETA_SECOND * second + (1.0 - BETA_SECOND) * grad * grad
    fix_first = 1.0 - jnp.power(BETA_FIRST, count)
    fix_second = 1.0 - jnp.power(BETA_SECOND, count)
    update = first / fix_first / (jnp.sqrt(second / fix_second) + ADAM_EPS) + WEIGHT_DECAY * weight
    return (weight - ADAM_RATE * update, first, second)


def split_halves(values, half_size):
    block_count, row_count, feature_dim = values.shape
    return values.reshape(block_count, row_count, 2, half_size)


def reduced_half(values, half_groups):
    part = lax.psum_scatter(values, ("dp", "cls"), scatter_dimension=1, tiled=True)
    return lax.all_gather(part, ("dp", "cls"), axis=1, tiled=True, axis_index_groups=half_groups)


def preconditioned_rows(grad_half, root_left, right_half, own_start):
    count, row_count, width = root_left.shape
    half_size = width // 2
    block_rows = lax.dynamic_slice_in_dim(grad_half, own_start, row_count, 1)
    grad_quads = split_halves(grad_half, half_size)
    rows_quads = split_halves(block_rows, half_size)
    cols_quads = lax.dynamic_slice_in_dim(grad_quads, own_start, row_count, 3)
    precise = FULL_PRECISION
    left_add = jnp.einsum("brjk,bljk->brjl", rows_quads, grad_quads, precision=precise)
    right_add = jnp.einsum("bkja,bkjm->bajm", cols_quads, grad_quads, precision=precise)
    direction = jnp.einsum(
        "brjk,bkjm->brjm", split_halves(root_left, half_size), grad_quads, precision=precise
    )
    direction = jnp.einsum(
        "brjk,bkjm->brjm", direction, split_halves(right_half, half_size), precision=precise
    )
    flat = (count, row_count, width)
    return left_add.reshape(flat), right_add.reshape(flat), direction.reshape(flat), block_rows


def on_device(
    patches,
    image_ids,
    keep,
    labels,
    owner,
    step,
    enc_weights,
    stats_left,
    stats_right,
    root_left,
    root_right,
    head_weights,
    head_m,
    head_v,
    vectors,
    vec_m,
    vec_v,
):
    dp_count = lax.axis_size("dp")
    cls_count = lax.axis_size("cls")
    dp_index = lax.axis_index("dp")
    cls_index = lax.axis_index("cls")
    block_count, row_count, feature_dim = enc_weights.shape
    up_count = (block_count - 5) // 2
    half_size = feature_dim // 2
    part_rows = row_count // cls_count
    half_dp = dp_count // 2
    half_group = half_dp * cls_count
    half_groups = [
        list(range(half_group)),
        list(range(half_group, 2 * half_group)),
    ]

    def my_part(values):
        return lax.dynamic_slice_in_dim(values, cls_index * part_rows, part_rows, 1)

    on_torus = dp_count == 8 and cls_count == 4
    if on_torus:
        vec_block = jnp.pad(vectors, ((0, -vectors.shape[0] % 8), (0, -row_count % 128)))
        own_low = enc_weights.astype(jnp.bfloat16)
        blocks, vec_blocks = gather_weights(own_low[:5], vec_block)
        right_part, vec_blocks = lax.optimization_barrier((my_part(root_right), vec_blocks))
        vec_low = jnp.transpose(vec_blocks[:, : vectors.shape[0], :row_count], (1, 0, 2))
        vec_all = lax.reduce_precision(vec_low.reshape(vectors.shape[0], feature_dim), 8, 7)
    else:
        right_part = my_part(root_right)
        all_blocks = lax.all_gather(
            my_part(enc_weights.astype(jnp.bfloat16)), ("dp", "cls"), axis=1, tiled=True
        )
        blocks = all_blocks[:5]
        vec_low = lax.all_gather(vectors.astype(jnp.bfloat16), "dp", axis=1, tiled=True)
        vec_all = vec_low.astype(jnp.float32)
    head_low = lax.all_gather(head_weights.astype(jnp.bfloat16), "dp", axis=0, tiled=True)
    final_gain = vec_all[9 + up_count]
    final_shift = vec_all[10 + up_count]
    pack_ids, pack_keep = image_ids[0], keep[0]
    key_codes = jnp.where(pack_keep == 1, pack_ids, -1)

    def attend(qkv_rows):
        if on_torus:
            return attention_forward_gathering(qkv_rows, pack_ids, key_codes, own_low[5:])
        return attention_forward(qkv_rows, pack_ids, key_codes), all_blocks[5:]

    output, mlp_blocks, saved = layer_forward(blocks, vec_all, patches, attend)
    if on_torus:
        right_codes = lax.all_gather(
            encode_roots(right_part), ("dp", "cls"), axis=0, axis_index_groups=half_groups
        )
    else:
        right_half = lax.all_gather(
            right_part, ("dp", "cls"), axis=1, tiled=True, axis_index_groups=half_groups
        )
    pooled = pool_rows(output, final_gain, final_shift, pack_ids, pack_keep)
    group = lax.all_gather(pooled.astype(jnp.bfloat16), "cls", axis=0, tiled=True)
    logits = jnp.dot(group, head_low, preferred_element_type=jnp.float32)
    class_dev = head_low.shape[1]
    class_ids = cls_index * class_dev + jnp.arange(class_dev)
    valid = class_ids[None, :] < LABELS_REAL
    target = jnp.any(labels[:, :, None] == class_ids[None, None, :], 1).astype(jnp.float32)
    image_total = labels.shape[0] * dp_count
    loss_part = (
        jnp.sum(jnp.where(valid, jax.nn.softplus(logits) - target * logits, 0.0)) / image_total
    )
    grad_logits = (jnp.where(valid, jax.nn.sigmoid(logits) - target, 0.0) / image_total).astype(
        jnp.bfloat16
    )
    group_grad = jnp.einsum("gc,dc->gd", grad_logits, head_low, preferred_element_type=jnp.float32)
    if on_torus:
        grad_pooled = class_sum(group_grad, cls_count)
    else:
        grad_pooled = lax.psum_scatter(group_grad, "cls", scatter_dimension=0, tiled=True)
    head_rows = lax.all_gather(
        jnp.concatenate([group, grad_logits], 1), "dp", axis=0, tiled=True
    )
    pooled_all, grad_logits_all = head_rows[:, :feature_dim], head_rows[:, feature_dim:]
    pooled_mine = lax.dynamic_slice_in_dim(pooled_all, dp_index * row_count, row_count, 1)
    head_grad = jnp.einsum(
        "gr,gc->rc", pooled_mine, grad_logits_all, preferred_element_type=jnp.float32
    )

    def pool_local(rows_in, gain, shift):
        return pool_rows(rows_in, gain, shift, pack_ids, pack_keep)

    pool_back = jax.vjp(pool_local, output, final_gain, final_shift)[1]
    grad_output, grad_gain, grad_shift = pool_back(grad_pooled)
    lefts, rights, mlp_grads, grad_vectors = layer_backward(
        blocks,
        mlp_blocks,
        vec_all,
        patches,
        saved,
        pack_ids,
        key_codes,
        grad_output,
        grad_gain,
        grad_shift,
    )

    head_squares = jnp.sum(head_grad * head_grad)
    if on_torus:
        padded = jnp.pad(grad_vectors, ((0, -grad_vectors.shape[0] % 8), (0, 0)))
        tail = jnp.pad(jnp.stack([head_squares, loss_part])[:, None], ((0, 6), (0, 127)))
        block_rows, left_add, right_add, direction, wide_scale, facts, vector_sum = (
            reduce_gradients(
                mlp_grads, lefts, rights, padded, tail, root_left, right_codes,
                dp_count, cls_count,
            )
        )
        vector_sum = vector_sum[: grad_vectors.shape[0]]
        loss, grad_norm, factor = facts[0, 0], facts[1, 0], facts[2, 0]
    else:
        over_rows = "td,te->de"
        first_grads = [
            jnp.einsum(over_rows, left, right, preferred_element_type=jnp.float32)[None]
            for left, right in (
                (lefts[0], rights[0]),
                (lefts[1], rights[1][0]),
                (lefts[1], rights[1][1]),
                (lefts[1], rights[1][2]),
                (lefts[2], rights[2]),
            )
        ]
        grad_half = reduced_half(jnp.concatenate(first_grads + list(mlp_grads), 0), half_groups)
        vector_sum = lax.psum(grad_vectors, ("dp", "cls"))
        left_add, right_add, direction, block_rows = preconditioned_rows(
            grad_half, root_left, right_half, (dp_index % half_dp) * row_count
        )
        squares = jnp.sum(split_halves(direction * direction, half_size), (1, 3))
        in_top = (dp_index < half_dp).astype(jnp.float32)
        once = (cls_index == 0).astype(jnp.float32)
        all_squares = head_squares + once * jnp.sum(block_rows * block_rows)
        packed = jnp.concatenate(
            [
                (once * in_top * squares).reshape(-1),
                (once * (1.0 - in_top) * squares).reshape(-1),
                jnp.stack([all_squares, loss_part]),
            ]
        )
        packed = lax.psum(packed, ("dp", "cls"))
        loss = packed[4 * block_count + 1]
        all_squares = packed[4 * block_count]
        sums = packed[: 4 * block_count].reshape(2, block_count, 2)
        block_squares = jnp.where(dp_index < half_dp, sums[0], sums[1])
        grad_norm = jnp.sqrt(all_squares + jnp.sum(vector_sum * vector_sum))
        factor = CLIP_NORM / jnp.maximum(grad_norm, CLIP_NORM)
        mean_squares = block_squares / (half_size * half_size) * factor * factor
        scale = SHAMPOO_RATE * factor * lax.rsqrt(mean_squares + ROOT_EPS)
        wide_scale = jnp.repeat(scale, half_size, axis=1)[:, None, :]
    vector_rows = lax.dynamic_slice_in_dim(vector_sum, dp_index * row_count, row_count, 1)
    new_blocks = enc_weights - direction * wide_scale
    square_factor = 0.5 * factor * factor
    new_left = 0.5 * stats_left + square_factor * left_add
    new_right = 0.5 * stats_right + square_factor * right_add
    count = step.astype(jnp.float32)
    new_vec, new_vec_m, new_vec_v = adam_step(vectors, vector_rows * factor, vec_m, vec_v, count)
    new_head, new_head_m, new_head_v = adam_step(
        head_weights, head_grad * factor, head_m, head_v, count
    )
    return (
        loss,
        grad_norm,
        new_blocks,
        block_rows * factor,
        new_left,
        new_right,
        new_vec,
        new_vec_m,
        new_vec_v,
        new_head,
        new_head_m,
        new_head_v,
    )


def solution(mesh):
    return jax.shard_map(
        on_device,
        mesh=mesh,
        in_specs=(
            P(("dp", "cls"), None),
            P(("dp", "cls"), None),
            P(("dp", "cls"), None),
            P("dp", None),
            P(),
            P(),
            P(None, "dp", None),
            P(None, "dp", None),
            P(None, "dp", None),
            P(None, "dp", None),
            P(None, "dp", None),
            P("dp", "cls"),
            P("dp", "cls"),
            P("dp", "cls"),
            P(None, "dp"),
            P(None, "dp"),
            P(None, "dp"),
        ),
        out_specs=(
            P(),
            P(),
            P(None, "dp", None),
            P(None, "dp", None),
            P(None, "dp", None),
            P(None, "dp", None),
            P(None, "dp"),
            P(None, "dp"),
            P(None, "dp"),
            P("dp", "cls"),
            P("dp", "cls"),
            P("dp", "cls"),
        ),
        check_vma=False,
    )
```

```python
import functools

import jax
import jax.numpy as jnp
from jax import lax
from jax.experimental import pallas as pl
from jax.experimental.pallas import tpu as pltpu
from jax.sharding import PartitionSpec as P

HEADS = 12
HEAD = 64
LABELS_REAL = 21843
IMAGE_MAX = 196
QTILE = 256
PAIR = 2 * HEAD
ROWS = 256
HIDDEN_TILE = 384
MESH = pl.DeviceIdType.MESH
CODE_TOP = 32766.0
CODE_FLOOR = 1e-33
PIECE = 48
FEATURE_TILE = 128
SPAN = 48
SHARES = 8
GATHER_DEPTH = 4
CLASS_TILE = 512
ROW_CHUNK = 7 * 128
EARLY_CHUNKS = 3
LATE_CHUNKS = 4
IMG_PACK = 8


FULL_PRECISION = lax.Precision.HIGHEST
NORM_EPS = 1e-06
CLIP_NORM = 1.0
ADAM_RATE = 0.02
SHAMPOO_RATE = 0.01
BETA_FIRST = 0.9
BETA_SECOND = 0.999
ADAM_EPS = 1e-08
WEIGHT_DECAY = 0.1
ROOT_EPS = 1e-06


def norm_rows(values, gain, shift):
    centred = values - jnp.mean(values, -1, keepdims=True)
    spread = jnp.mean(centred * centred, -1, keepdims=True)
    return centred * lax.rsqrt(spread + NORM_EPS) * gain + shift


def pool_rows(output, gain, shift, pack_ids, pack_keep):
    final = norm_rows(output, gain, shift)
    member = (
        (pack_ids[None, :] == jnp.arange(IMG_PACK)[:, None]) & (pack_keep[None, :] == 1)
    ).astype(jnp.float32)
    counted = jnp.maximum(jnp.sum(member, 1), 1.0)
    return jnp.dot(member, final, precision=FULL_PRECISION) / counted[:, None]


def key_window(tile, length):
    reach = -(-(IMAGE_MAX - 1) // 128) * 128
    low = max(0, tile * QTILE - reach)
    high = min(length, (tile + 1) * QTILE + reach)
    return low, high


def attention_bias(qids_ref, kcodes_ref, bias_ref):
    length = qids_ref.shape[0]

    @pl.when(pl.program_id(0) == 0)
    def _():
        for tile in range(length // QTILE):
            low, high = key_window(tile, length)
            shape = (QTILE, high - low)
            rows = lax.broadcasted_iota(jnp.int32, shape, 0) + tile * QTILE
            cols = lax.broadcasted_iota(jnp.int32, shape, 1) + low
            same = qids_ref[tile * QTILE : (tile + 1) * QTILE, :] == kcodes_ref[:, low:high]
            bias_ref[tile, :, : high - low] = jnp.where(same | (rows == cols), 0.0, -1e30)


def attention_tile(tile, q_ref, k_ref, v_ref, out_ref, bias_ref):
    lane = lax.broadcasted_iota(jnp.int32, (QTILE, PAIR), 1)
    low, high = key_window(tile, q_ref.shape[0])
    rows = pl.ds(tile * QTILE, QTILE)
    queries = q_ref[rows, :] * jnp.bfloat16(HEAD ** (-0.5))
    keys = k_ref[low:high, :]
    values = v_ref[low:high, :]
    halves = []
    for head in range(2):
        mine = (lane >= head * HEAD) & (lane < (head + 1) * HEAD)
        picked = jnp.where(mine, queries, jnp.zeros_like(queries))
        scores = lax.dot_general(
            picked, keys, (((1,), (1,)), ((), ())), preferred_element_type=jnp.float32
        )
        scores = scores + bias_ref[tile, :, : high - low]
        top = jnp.max(scores, -1, keepdims=True)
        weights = jnp.exp(scores - top)
        probs = weights * (1.0 / jnp.sum(weights, -1, keepdims=True))
        halves.append(
            jnp.dot(probs.astype(jnp.bfloat16), values, preferred_element_type=jnp.float32)
        )
    out_ref[rows, :] = jnp.where(lane < HEAD, halves[0], halves[1]).astype(jnp.bfloat16)


def attention_forward_kernel(qids_ref, kcodes_ref, q_ref, k_ref, v_ref, out_ref, bias_ref):
    attention_bias(qids_ref, kcodes_ref, bias_ref)
    for tile in range(q_ref.shape[0] // QTILE):
        attention_tile(tile, q_ref, k_ref, v_ref, out_ref, bias_ref)


def attention_back_bias(qids_ref, kcodes_ref, bias_ref):
    length = kcodes_ref.shape[0]

    @pl.when(pl.program_id(0) == 0)
    def _():
        for tile in range(length // QTILE):
            low, high = key_window(tile, length)
            shape = (high - low, QTILE)
            rows = lax.broadcasted_iota(jnp.int32, shape, 0) + low
            cols = lax.broadcasted_iota(jnp.int32, shape, 1) + tile * QTILE
            same = kcodes_ref[low:high, :] == qids_ref[:, tile * QTILE : (tile + 1) * QTILE]
            bias_ref[tile, : high - low, :] = jnp.where(same | (rows == cols), 0.0, -1e30)


def attention_back_tile(tile, q_ref, k_ref, v_ref, do_ref, out_ref, bias_ref, dk_ref, dv_ref):
    length = q_ref.shape[0]
    lane = lax.broadcasted_iota(jnp.int32, (QTILE, PAIR), 1)
    scale = jnp.bfloat16(HEAD ** (-0.5))
    low, high = key_window(tile, length)
    rows = pl.ds(tile * QTILE, QTILE)
    window = pl.ds(low, high - low)
    queries = q_ref[rows, :] * scale
    keys = k_ref[window, :]
    values = v_ref[window, :]
    grads = do_ref[rows, :]
    halves = []
    for head in range(2):
        mine = (lane >= head * HEAD) & (lane < (head + 1) * HEAD)
        picked = jnp.where(mine, queries, jnp.zeros_like(queries))
        picked_grads = jnp.where(mine, grads, jnp.zeros_like(grads))
        scores = lax.dot_general(
            keys, picked, (((1,), (1,)), ((), ())), preferred_element_type=jnp.float32
        )
        scores = scores + bias_ref[tile, : high - low, :]
        top = jnp.max(scores, 0, keepdims=True)
        weights = jnp.exp(scores - top)
        probs = weights * (1.0 / jnp.sum(weights, 0, keepdims=True))
        grad_probs = lax.dot_general(
            values, picked_grads, (((1,), (1,)), ((), ())), preferred_element_type=jnp.float32
        )
        inner = jnp.sum(probs * grad_probs, 0, keepdims=True)
        grad_scores = (probs * (grad_probs - inner)).astype(jnp.bfloat16)
        dv_ref[window, :] += jnp.dot(
            probs.astype(jnp.bfloat16), picked_grads, preferred_element_type=jnp.float32
        )
        dk_ref[window, :] += jnp.dot(
            grad_scores, picked, preferred_element_type=jnp.float32
        )
        halves.append(
            lax.dot_general(
                grad_scores,
                keys,
                (((0,), (0,)), ((), ())),
                preferred_element_type=jnp.float32,
            )
        )
    grad_queries = jnp.where(lane < HEAD, halves[0], halves[1]) * HEAD ** (-0.5)
    out_ref[0, rows, :] = grad_queries.astype(jnp.bfloat16)


def attention_backward_kernel(
    qids_ref, kcodes_ref, q_ref, k_ref, v_ref, do_ref, *refs
):
    gathering = len(refs) > 4
    if gathering:
        own_ref, out_ref, rows_ref, bias_ref, dk_ref, dv_ref, send_sem, recv_sem, copy_sem = refs
        pair, tiles = pl.program_id(0), q_ref.shape[0] // QTILE
        slots = pl.num_programs(0) * tiles

        pl.when(pair == 0)(column_barrier)
        row_step, turns = row_steps(
            EARLY_CHUNKS, own_ref, rows_ref, send_sem, recv_sem, copy_sem
        )
    else:
        out_ref, bias_ref, dk_ref, dv_ref = refs
    attention_back_bias(qids_ref, kcodes_ref, bias_ref)
    dk_ref[...] = jnp.zeros_like(dk_ref)
    dv_ref[...] = jnp.zeros_like(dv_ref)
    for tile in range(q_ref.shape[0] // QTILE):
        if gathering:
            slot = pair * tiles + tile
            begin, end = slot * turns // slots, (slot + 1) * turns // slots

            @pl.when(begin < end)
            def _(begin=begin):
                row_step(begin)

        attention_back_tile(tile, q_ref, k_ref, v_ref, do_ref, out_ref, bias_ref, dk_ref, dv_ref)
    out_ref[1] = dk_ref[...].astype(jnp.bfloat16)
    out_ref[2] = dv_ref[...].astype(jnp.bfloat16)


def pair_spec(length, part=None):
    if part is None:
        return pl.BlockSpec((length, PAIR), lambda pair: (0, pair))
    return pl.BlockSpec((None, length, PAIR), lambda pair: (part, 0, pair))


def whole_spec(shape):
    return pl.BlockSpec(shape, lambda pair: (0,) * len(shape))


def bias_shape(length):
    tiles = length // QTILE
    window = max(high - low for low, high in (key_window(t, length) for t in range(tiles)))
    return tiles, QTILE, window


def attention_forward(qkv_rows, pack_ids, key_codes):
    _, length, width = qkv_rows.shape
    return pl.pallas_call(
        attention_forward_kernel,
        grid=(width // PAIR,),
        out_shape=jax.ShapeDtypeStruct((length, width), jnp.bfloat16),
        in_specs=[whole_spec((length, 1)), whole_spec((1, length))]
        + [pair_spec(length, part) for part in range(3)],
        out_specs=pair_spec(length),
        scratch_shapes=[pltpu.VMEM(bias_shape(length), jnp.float32)],
        compiler_params=pltpu.CompilerParams(vmem_limit_bytes=40 << 20),
        name="attention_forward",
    )(pack_ids[:, None], key_codes[None, :], qkv_rows, qkv_rows, qkv_rows)


def attention_backward(qkv_rows, pack_ids, key_codes, grad_attended, own_rows=None):
    _, length, width = qkv_rows.shape
    tiles, _, window = bias_shape(length)
    out_shape = [jax.ShapeDtypeStruct((3, length, width), jnp.bfloat16)]
    out_specs = [pl.BlockSpec((3, length, PAIR), lambda pair: (0, 0, pair))]
    extra_in, extra_spec, extra_scratch, collective = [], [], [], {}
    if own_rows is not None:
        rows_shape, extra_scratch = row_operands(own_rows, LATE_CHUNKS)
        out_shape.append(rows_shape)
        out_specs.append(pl.BlockSpec(memory_space=pl.ANY))
        extra_in, extra_spec = [own_rows], [whole_spec(own_rows.shape)]
        collective = dict(collective_id=5, has_side_effects=True)
    return pl.pallas_call(
        attention_backward_kernel,
        grid=(width // PAIR,),
        out_shape=out_shape,
        in_specs=[whole_spec((1, length)), whole_spec((length, 1))]
        + [pair_spec(length, part) for part in range(3)]
        + [pair_spec(length)]
        + extra_spec,
        out_specs=out_specs,
        scratch_shapes=[
            pltpu.VMEM((tiles, window, QTILE), jnp.float32),
            pltpu.VMEM((length, PAIR), jnp.float32),
            pltpu.VMEM((length, PAIR), jnp.float32),
        ]
        + extra_scratch,
        compiler_params=pltpu.CompilerParams(vmem_limit_bytes=40 << 20, **collective),
        name="attention_backward",
    )(pack_ids[None, :], key_codes[:, None], qkv_rows, qkv_rows, qkv_rows, grad_attended, *extra_in)


def mlp_forward_kernel(x_ref, up_ref, bias_ref, down_ref, units_ref, slope_ref, out_ref):
    first = pl.program_id(0) == 0

    @pl.when(first)
    def _():
        out_ref[...] = jnp.zeros_like(out_ref)

    for start in range(0, x_ref.shape[0], ROWS):
        rows = pl.ds(start, ROWS)
        pre = jnp.dot(x_ref[rows, :], up_ref[...], preferred_element_type=jnp.float32)
        pre = pre + bias_ref[...]
        half = 0.5 + 0.5 * lax.erf(pre * 0.7071067811865476)
        bell = jnp.exp(-0.5 * pre * pre) * 0.3989422804014327
        units = (pre * half).astype(jnp.bfloat16)
        units_ref[rows, :] = units
        slope_ref[rows, :] = half + pre * bell
        out_ref[rows, :] += jnp.dot(units, down_ref[...], preferred_element_type=jnp.float32)


def mlp_backward_kernel(x_ref, dm_ref, up_ref, down_ref, units_ref, slope_ref, *refs):
    if len(refs) > 5:
        own_ref, grad_up_ref, grad_down_ref, bias_ref, dx_ref, rows_ref, dpre_ref, *sems = refs
        turn = pl.program_id(0)
        pl.when(turn == 0)(column_barrier)
        row_step, turns = row_steps(0, own_ref, rows_ref, *sems)
        pl.when(turn < turns)(lambda: row_step(turn))
    else:
        grad_up_ref, grad_down_ref, bias_ref, dx_ref, dpre_ref = refs

    @pl.when(pl.program_id(0) == 0)
    def _():
        dx_ref[...] = jnp.zeros_like(dx_ref)

    total = jnp.zeros((1, HIDDEN_TILE), jnp.float32)
    for start in range(0, x_ref.shape[0], ROWS):
        rows = pl.ds(start, ROWS)
        units_back = lax.dot_general(
            dm_ref[rows, :], down_ref[...], (((1,), (1,)), ((), ())),
            preferred_element_type=jnp.float32,
        )
        grad_pre = (units_back * slope_ref[rows, :]).astype(jnp.bfloat16)
        dpre_ref[rows, :] = grad_pre
        total = total + jnp.sum(grad_pre.astype(jnp.float32), 0, keepdims=True)
        dx_ref[rows, :] += lax.dot_general(
            grad_pre, up_ref[...], (((1,), (1,)), ((), ())), preferred_element_type=jnp.float32
        )
    bias_ref[...] = total
    over_rows = (((0,), (0,)), ((), ()))
    grad_down_ref[...] = lax.dot_general(
        units_ref[...], dm_ref[...], over_rows, preferred_element_type=jnp.float32
    )
    grad_up_ref[...] = lax.dot_general(
        x_ref[...], dpre_ref[...], over_rows, preferred_element_type=jnp.float32
    )


def mlp_specs(length, width, up_count):
    split = width // HIDDEN_TILE
    resident = pl.BlockSpec((length, width), lambda t: (0, 0))
    up = pl.BlockSpec((None, width, HIDDEN_TILE), lambda t: (t // split, 0, t % split))
    down = pl.BlockSpec(
        (None, HIDDEN_TILE, width), lambda t: (up_count + t // split, t % split, 0)
    )
    hidden = pl.BlockSpec((length, HIDDEN_TILE), lambda t: (0, t))
    bias = pl.BlockSpec((1, HIDDEN_TILE), lambda t: (0, t))
    return split, resident, up, down, hidden, bias


def mlp_forward(rows, blocks, up_bias):
    length, width = rows.shape
    up_count = blocks.shape[0] // 2
    split, resident, up, down, hidden, bias = mlp_specs(length, width, up_count)
    hidden_size = up_count * width
    return pl.pallas_call(
        mlp_forward_kernel,
        grid=(up_count * split,),
        out_shape=(
            jax.ShapeDtypeStruct((length, hidden_size), jnp.bfloat16),
            jax.ShapeDtypeStruct((length, hidden_size), jnp.float32),
            jax.ShapeDtypeStruct((length, width), jnp.float32),
        ),
        in_specs=[resident, up, bias, down],
        out_specs=(hidden, hidden, resident),
        compiler_params=pltpu.CompilerParams(vmem_limit_bytes=48 << 20),
        name="mlp_forward",
    )(rows, blocks, up_bias.reshape(1, hidden_size), blocks)


def mlp_backward(rows, grad_branch, blocks, units, slopes, own_rows=None):
    length, width = rows.shape
    up_count = blocks.shape[0] // 2
    split, resident, up, down, hidden, bias = mlp_specs(length, width, up_count)
    hidden_size = up_count * width
    out_shape = [
        jax.ShapeDtypeStruct((up_count, width, width), jnp.float32),
        jax.ShapeDtypeStruct((up_count, width, width), jnp.float32),
        jax.ShapeDtypeStruct((1, hidden_size), jnp.float32),
        jax.ShapeDtypeStruct((length, width), jnp.float32),
    ]
    out_specs = [
        pl.BlockSpec((None, width, HIDDEN_TILE), lambda t: (t // split, 0, t % split)),
        pl.BlockSpec((None, HIDDEN_TILE, width), lambda t: (t // split, t % split, 0)),
        bias,
        resident,
    ]
    extra_in, extra_spec, extra_scratch, collective = [], [], [], {}
    if own_rows is not None:
        assert EARLY_CHUNKS + 2 <= up_count * split
        rows_shape, extra_scratch = row_operands(own_rows, EARLY_CHUNKS)
        out_shape.append(rows_shape)
        out_specs.append(pl.BlockSpec(memory_space=pl.ANY))
        extra_in, extra_spec = [own_rows], [whole_spec(own_rows.shape)]
        collective = dict(collective_id=6, has_side_effects=True)
    return pl.pallas_call(
        mlp_backward_kernel,
        grid=(up_count * split,),
        out_shape=out_shape,
        in_specs=[resident, resident, up, down, hidden, hidden] + extra_spec,
        out_specs=out_specs,
        scratch_shapes=[pltpu.VMEM((length, HIDDEN_TILE), jnp.bfloat16)] + extra_scratch,
        compiler_params=pltpu.CompilerParams(vmem_limit_bytes=48 << 20, **collective),
        name="mlp_backward",
    )(rows, grad_branch, blocks, blocks, units, slopes, *extra_in)


def layer_forward(blocks, vec_all, patch, attend):
    embedded = jnp.dot(patch, blocks[0], preferred_element_type=jnp.float32) + vec_all[0]
    normed_one = norm_rows(embedded, vec_all[1], vec_all[2]).astype(jnp.bfloat16)
    qkv_rows = jnp.einsum(
        "td,kde->kte", normed_one, blocks[1:4], preferred_element_type=jnp.float32
    )
    qkv_bias = jnp.stack([vec_all[3], jnp.zeros_like(vec_all[3]), vec_all[4]])
    qkv_rows = (qkv_rows + qkv_bias[:, None, :]).astype(jnp.bfloat16)
    attended, mlp_blocks = attend(qkv_rows)
    up_count = mlp_blocks.shape[0] // 2
    hidden = (
        embedded + jnp.dot(attended, blocks[4], preferred_element_type=jnp.float32) + vec_all[5]
    )
    normed_two = norm_rows(hidden, vec_all[6], vec_all[7]).astype(jnp.bfloat16)
    units, slopes, branch = mlp_forward(normed_two, mlp_blocks, vec_all[8 : 8 + up_count])
    output = hidden + branch + vec_all[8 + up_count]
    return (
        output,
        mlp_blocks,
        (embedded, normed_one, qkv_rows, attended, hidden, normed_two, slopes, units),
    )


def layer_backward(
    blocks,
    mlp_blocks,
    vec_all,
    patch,
    saved,
    pack_ids,
    key_codes,
    grad_output,
    grad_gain,
    grad_shift,
    own_rows=None,
):
    embedded, normed_one, qkv_rows, attended, hidden, normed_two, slopes, units = saved
    feature_dim = patch.shape[1]
    up_count = mlp_blocks.shape[0] // 2
    grad_branch = grad_output.astype(jnp.bfloat16)
    grad_up, grad_down, up_sums, grad_normed_two, *early = mlp_backward(
        normed_two, grad_branch, mlp_blocks, units, slopes, own_rows
    )
    norm_two_back = jax.vjp(norm_rows, hidden, vec_all[6], vec_all[7])[1]
    grad_hidden_norm, grad_gain_two, grad_shift_two = norm_two_back(grad_normed_two)
    grad_hidden = grad_output + grad_hidden_norm
    grad_attn_out = grad_hidden.astype(jnp.bfloat16)
    grad_attended = jnp.einsum(
        "td,ed->te", grad_attn_out, blocks[4], preferred_element_type=jnp.float32
    ).astype(jnp.bfloat16)
    grad_qkv, *late = attention_backward(
        qkv_rows, pack_ids, key_codes, grad_attended, own_rows
    )
    grad_normed_one = jnp.einsum(
        "kte,kde->td", grad_qkv, blocks[1:4], preferred_element_type=jnp.float32
    )
    norm_one_back = jax.vjp(norm_rows, embedded, vec_all[1], vec_all[2])[1]
    grad_embed_norm, grad_gain_one, grad_shift_one = norm_one_back(grad_normed_one)
    grad_embedded = (grad_hidden + grad_embed_norm).astype(jnp.bfloat16)
    lefts = (patch, normed_one, attended)
    rights = (grad_embedded, grad_qkv, grad_attn_out)
    bias_sums = jnp.stack(
        [
            jnp.sum(grad_embedded.astype(jnp.float32), 0),
            grad_gain_one,
            grad_shift_one,
            jnp.sum(grad_qkv[0].astype(jnp.float32), 0),
            jnp.sum(grad_qkv[2].astype(jnp.float32), 0),
            jnp.sum(grad_attn_out.astype(jnp.float32), 0),
            grad_gain_two,
            grad_shift_two,
        ]
    )
    up_sums = up_sums.reshape(up_count, feature_dim)
    tail_sums = jnp.stack([jnp.sum(grad_branch.astype(jnp.float32), 0), grad_gain, grad_shift])
    grad_vectors = jnp.concatenate([bias_sums, up_sums, tail_sums], 0)
    return (lefts, rights, (grad_up, grad_down), grad_vectors, early + late)


def torus_place():
    dp, cls = lax.axis_index("dp"), lax.axis_index("cls")
    return dp // 2, dp % 2, cls // 2, cls % 2


def torus_device(z, y, x, core):
    return (z * 2 + y, x * 2 + core)


def encode(pieces, code_refs, scale_ref):
    top = None
    for piece in pieces:
        peak = jnp.max(jnp.abs(piece()), 0, keepdims=True)
        top = peak if top is None else jnp.maximum(top, peak)
    top = jnp.maximum(top, CODE_FLOOR)
    inverse = CODE_TOP / top
    for piece, code_ref in zip(pieces, code_refs):
        code_ref[...] = jnp.round(piece() * inverse).astype(jnp.int32).astype(jnp.int16)
    scale_ref[...] = top * (1.0 / CODE_TOP)


def decode(code, scale):
    return code.astype(jnp.int32).astype(jnp.float32) * scale


def reduce_kernel(counts, *refs):
    sources, refs = refs[: len(counts)], refs[len(counts) :]
    (patch_hbm, first_hbm, mid_hbm, dpatch_hbm, dfirst_hbm, dmid_hbm,
     vec_ref, tail_ref, left_hbm, right_hbm,
     own_hbm, left_out_hbm, right_out_hbm, step_hbm, wide_ref, facts_ref, vec_out_ref,
     left_buf, right_buf, right_full, outs_buf, squares, high_buf, low_buf, sum_slots, tail_slots,
     lhs_buf, rhs_buf, pair_sem,
     in_sem, sum_send, sum_recv, tail_send, tail_recv,
     acc, spare, kept, sent0, got0, sent1, got1, sent2, got2, sent3, got3, sent4, got4,
     ss0, gs0, ss1, gs1, ss2, gs2, ss3, gs3, ss4, gs4, codes, scales, vec_got,
     load_sem, out_sem, send_sem, recv_sem, send_scale_sem, recv_scale_sem,
     vec_send_sem, vec_recv_sem) = refs
    stored = sum(counts)
    paired = dfirst_hbm.shape[0] + 2
    total = stored + paired
    half, width = codes.shape[1], codes.shape[2]
    cols = width // 2
    z, y, x, core = torus_place()
    upper = z // 2
    inner = (z % 2) != upper
    mate_core = torus_device(z, y, x, 1 - core)
    mate_x = torus_device(z, y, 1 - x, core)
    mate_y = torus_device(z, 1 - y, x, core)
    mate_z = torus_device(z + 1 - 2 * (z % 2), y, x, core)
    mate_mid = torus_device(3 - z, y, x, core)
    mate_far = torus_device((z + 2) % 4, y, x, core)

    barrier = pltpu.get_barrier_semaphore()
    dp, cls = lax.axis_index("dp"), lax.axis_index("cls")
    everyone = tail_slots.shape[0]
    quarter = sum_slots.shape[0]
    me = dp * 4 + cls

    def any_mate(n):
        other = lax.rem(me + n, everyone)
        return (other // 4, lax.rem(other, 4))

    def half_mate(n):
        return (upper * quarter + lax.rem(dp + n, quarter), cls)

    for n in range(1, everyone):
        pl.semaphore_signal(barrier, inc=1, device_id=any_mate(n), device_id_type=MESH)
    pl.semaphore_wait(barrier, everyone - 1)
    own = lax.rem(dp, quarter) * left_buf.shape[1]

    own_cols = pl.ds(pl.multiple_of(core * cols, 128), cols)
    other_cols = pl.ds(pl.multiple_of((1 - core) * cols, 128), cols)

    def rows_at(start, size):
        return pl.ds(pl.multiple_of(start, PIECE), size)

    def loads(m, body):
        start = 0
        for source, count in zip(sources, counts):
            def one(source=source, start=start):
                pair = (
                    pltpu.make_async_copy(
                        source.at[m - start, :, own_cols], acc.at[m % 5], load_sem.at[m % 2, 0]
                    ),
                    pltpu.make_async_copy(
                        source.at[m - start, :, other_cols], spare.at[m % 2], load_sem.at[m % 2, 1]
                    ),
                )
                for copy in pair:
                    body(copy)

            pl.when((m >= start) & (m < start + count))(one)
            start += count

    def block_of(m):
        return lax.rem(m + paired, total)

    def pair_loads(m, body):
        index = m - stored
        last = paired - 1

        def run(left, right):
            body(pltpu.make_async_copy(left, lhs_buf.at[m % 2], pair_sem.at[m % 2, 0]))
            body(pltpu.make_async_copy(right, rhs_buf.at[m % 2], pair_sem.at[m % 2, 1]))

        pl.when(index == 0)(lambda: run(patch_hbm, dpatch_hbm))
        pl.when((index > 0) & (index < last))(
            lambda: run(first_hbm, dfirst_hbm.at[jnp.clip(index - 1, 0, last - 2)])
        )
        pl.when(index == last)(lambda: run(mid_hbm, dmid_hbm))

    def pair_product(m):
        chunk = 2 * FEATURE_TILE
        for r in range(0, width, chunk):
            left = lhs_buf[m % 2, :, r : r + chunk].T
            for target, columns in ((acc.at[m % 5], own_cols), (spare.at[m % 2], other_cols)):
                target[r : r + chunk, :] = jnp.dot(
                    left, rhs_buf[m % 2, :, columns], preferred_element_type=jnp.float32
                )

    def message(stage, m, source, scale_source, target, scale_target, mate):
        return (
            pltpu.make_async_remote_copy(
                src_ref=source, dst_ref=target,
                send_sem=send_sem.at[stage, m % 2], recv_sem=recv_sem.at[stage, m],
                device_id=mate, device_id_type=MESH,
            ),
            pltpu.make_async_remote_copy(
                src_ref=scale_source, dst_ref=scale_target,
                send_sem=send_scale_sem.at[stage, m % 2], recv_sem=recv_scale_sem.at[stage, m],
                device_id=mate, device_id_type=MESH,
            ),
        )

    def first(m):
        return message(0, m, sent0.at[m % 2], ss0.at[m % 2], got0.at[m], gs0.at[m], mate_core)

    def second(m, b):
        return message(
            1 + b, m, sent1.at[m % 2, b], ss1.at[m % 2, b], got1.at[m, b], gs1.at[m, b],
            mate_y if b else mate_x,
        )

    def third(m, b):
        return message(
            3 + b, m, sent2.at[m % 2, b], ss2.at[m % 2, b], got2.at[m, b], gs2.at[m, b],
            mate_x if b else mate_y,
        )

    def fourth(m):
        return message(5, m, sent3.at[m % 2], ss3.at[m % 2], got3.at[m], gs3.at[m], mate_z)

    def fifth(m):
        return message(6, m, sent4.at[m % 2], ss4.at[m % 2], got4.at[m], gs4.at[m], mate_mid)

    piece_a = 2 * x + y
    piece_b = 4 + 2 * y + x

    def spread(stage, m, piece, count, mate, columns=own_cols):
        rows = pl.ds(pl.multiple_of(piece * PIECE, PIECE), count * PIECE)
        block = codes.at[m, rows, columns]
        scale = scales.at[m, pl.ds(piece, count), :, columns]
        return message(stage, m, block, scale, block, scale, mate)

    def start(copies):
        for copy in copies:
            copy.start()

    def wait_send(copies):
        for copy in copies:
            copy.wait_send()

    def wait_recv(copies):
        for copy in copies:
            copy.wait_recv()

    def vec_copy(step, mate):
        return pltpu.make_async_remote_copy(
            src_ref=vec_got.at[step, 0], dst_ref=vec_got.at[step, 1],
            send_sem=vec_send_sem.at[step], recv_sem=vec_recv_sem.at[step],
            device_id=mate, device_id_type=MESH,
        )

    vec_mates = (mate_core, mate_x, mate_y, mate_z, mate_far)

    loads(jnp.int32(0), lambda copy: copy.start())
    vec_got[0, 0] = vec_ref[...]
    vec_copy(0, vec_mates[0]).start()

    def step(t, carry):
        for n in range(1, 6):
            @pl.when(t == n)
            def _(n=n):
                vec_copy(n - 1, vec_mates[n - 1]).wait()
                value = vec_got[n - 1, 0] + vec_got[n - 1, 1]
                if n < 5:
                    vec_got[n, 0] = value
                    vec_copy(n, vec_mates[n]).start()
                else:
                    vec_out_ref[...] = value

        @pl.when(t < total)
        def _():
            m = t

            @pl.when(m < stored)
            def _():
                loads(m, lambda copy: copy.wait())

            @pl.when(m + 1 < stored)
            def _():
                loads(m + 1, lambda copy: copy.start())

            @pl.when((m + 1 >= stored) & (m + 1 < total))
            def _():
                pair_loads(m + 1, lambda copy: copy.start())

            @pl.when(m >= stored)
            def _():
                pair_loads(m, lambda copy: copy.wait())
                pair_product(m)

            span = 2 * PIECE
            encode(
                [lambda r=r: spare[m % 2, r : r + span, :] for r in range(0, 2 * half, span)],
                [sent0.at[m % 2, r : r + span, :] for r in range(0, 2 * half, span)],
                ss0.at[m % 2],
            )
            start(first(m))

        @pl.when((t >= 1) & (t < total + 1))
        def _():
            m = t - 1
            copies = first(m)
            wait_send(copies)
            wait_recv(copies)
            slot = m % 5
            span = 2 * PIECE
            for r in range(0, 2 * half, span):
                acc[slot, r : r + span, :] += decode(got0[m, r : r + span, :], gs0[m])
            for b in range(2):
                other = (1 - y) if b else (1 - x)
                begins = [h * half + b * 4 * PIECE + other * span for h in range(2)]
                encode(
                    [lambda s=s: acc[slot, rows_at(s, span), :] for s in begins],
                    [sent1.at[m % 2, b, h] for h in range(2)],
                    ss1.at[m % 2, b],
                )
                start(second(m, b))

        @pl.when((t >= 2) & (t < total + 2))
        def _():
            m = t - 2
            slot = m % 5
            span = 2 * PIECE
            for b in range(2):
                copies = second(m, b)
                wait_send(copies)
                wait_recv(copies)
                mine = y if b else x
                other = (1 - x) if b else (1 - y)
                begins = [h * half + b * 4 * PIECE + mine * span for h in range(2)]
                for h, s in enumerate(begins):
                    acc[slot, rows_at(s, span), :] += decode(got1[m, b, h], gs1[m, b])
                encode(
                    [lambda s=s: acc[slot, rows_at(s + other * PIECE, PIECE), :] for s in begins],
                    [sent2.at[m % 2, b, h] for h in range(2)],
                    ss2.at[m % 2, b],
                )
                start(third(m, b))

        @pl.when((t >= 3) & (t < total + 3))
        def _():
            m = t - 3
            slot = m % 5
            for b in range(2):
                copies = third(m, b)
                wait_send(copies)
                wait_recv(copies)
                place = piece_b if b else piece_a
                for h in range(2):
                    kept[m % 3, h, b] = acc[
                        slot, rows_at(h * half + place * PIECE, PIECE), :
                    ] + decode(got2[m, b, h], gs2[m, b])

            @pl.when(jnp.logical_not(inner))
            def _():
                pairs = [(h, b) for h in range(2) for b in range(2)]
                encode(
                    [lambda h=h, b=b: kept[m % 3, h, b] for h, b in pairs],
                    [sent3.at[m % 2, h, b] for h, b in pairs],
                    ss3.at[m % 2],
                )
                start(fourth(m))

        @pl.when((t >= 4) & (t < total + 4))
        def _():
            m = t - 4
            copies = fourth(m)

            @pl.when(jnp.logical_not(inner))
            def _():
                wait_send(copies)

            @pl.when(inner)
            def _():
                wait_recv(copies)
                for h in range(2):
                    for b in range(2):
                        kept[m % 3, h, b] += decode(got3[m, h, b], gs3[m])
                encode(
                    [lambda b=b: kept[m % 3, 1 - upper, b] for b in range(2)],
                    [sent4.at[m % 2, b] for b in range(2)],
                    ss4.at[m % 2],
                )
                start(fifth(m))

        @pl.when((t >= 5) & (t < total + 5))
        def _():
            m = t - 5

            @pl.when(inner)
            def _():
                copies = fifth(m)
                wait_send(copies)
                wait_recv(copies)
                for b in range(2):
                    place = piece_b if b else piece_a
                    value = kept[m % 3, upper, b] + decode(got4[m, b], gs4[m])
                    encode(
                        [lambda value=value: value],
                        [codes.at[m, rows_at(place * PIECE, PIECE), own_cols]],
                        scales.at[m, place, :, own_cols],
                    )
                    start(spread(7 + b, m, place, 1, mate_z))

        @pl.when((t >= 6) & (t < total + 6))
        def _():
            m = t - 6
            for b in range(2):
                place = piece_b if b else piece_a
                copies = spread(7 + b, m, place, 1, mate_z)

                @pl.when(inner)
                def _(copies=copies):
                    wait_send(copies)

                @pl.when(jnp.logical_not(inner))
                def _(copies=copies):
                    wait_recv(copies)

                start(spread(9 + b, m, place, 1, mate_x if b else mate_y))

        @pl.when((t >= 7) & (t < total + 7))
        def _():
            m = t - 7
            for b in range(2):
                place = piece_b if b else piece_a
                theirs = (4 + 2 * y + 1 - x) if b else (2 * x + 1 - y)
                wait_send(spread(9 + b, m, place, 1, mate_x if b else mate_y))
                wait_recv(spread(9 + b, m, theirs, 1, mate_x if b else mate_y))
                begin = (4 + 2 * y) if b else 2 * x
                start(spread(11 + b, m, begin, 2, mate_y if b else mate_x))

        @pl.when((t >= 8) & (t < total + 8))
        def _():
            m = t - 8
            for b in range(2):
                begin = (4 + 2 * y) if b else 2 * x
                theirs = (4 + 2 * (1 - y)) if b else 2 * (1 - x)
                wait_send(spread(11 + b, m, begin, 2, mate_y if b else mate_x))
                wait_recv(spread(11 + b, m, theirs, 2, mate_y if b else mate_x))
            start(spread(13, m, 0, 8, mate_core))

        def ins(m):
            return (
                pltpu.make_async_copy(
                    left_hbm.at[block_of(m)], left_buf.at[m % 2], in_sem.at[m % 2, 0]
                ),
                pltpu.make_async_copy(
                    right_hbm.at[:, block_of(m)], right_buf.at[m % 2], in_sem.at[m % 2, 1]
                ),
            )

        def outs(m):
            targets = (own_hbm, left_out_hbm, right_out_hbm, step_hbm)
            return [
                pltpu.make_async_copy(
                    outs_buf.at[m % 2, n], target.at[block_of(m)], out_sem.at[m % 2, n]
                )
                for n, target in enumerate(targets)
            ]

        @pl.when((t >= 8) & (t < total + 8))
        def _():
            start(ins(t - 8))

        @pl.when((t >= 11) & (t < total + 11))
        def _():
            for copy in outs(t - 11):
                copy.wait()

        @pl.when((t >= 9) & (t < total + 9))
        def _():
            m = t - 9
            wait_send(spread(13, m, 0, 8, mate_core))
            wait_recv(spread(13, m, 0, 8, mate_core, other_cols))
            for copy in ins(m):
                copy.wait()
            precondition_block(
                own, codes.at[m], scales.at[m], left_buf.at[m % 2], right_buf.at[m % 2],
                outs_buf.at[m % 2], squares.at[m], high_buf, low_buf, right_full,
            )
            start(outs(m))

        return carry

    lax.fori_loop(0, total + 11, step, 0)

    def folded(row):
        return sum(row[:, n * 128 : (n + 1) * 128] for n in range(row.shape[1] // 128))

    layer = jnp.zeros((1, 128), jnp.float32)
    mine = lax.rem(dp, quarter)
    sum_slots[mine] = jnp.zeros(sum_slots.shape[1:], jnp.float32)
    for m in range(total):
        layer = layer + folded(squares[m, 0:1, :])
        for quad in range(2):
            part = squares[m, 1:2, quad * cols : (quad + 1) * cols]
            row = 2 * ((m + paired) % total) + quad
            sum_slots[mine, row : row + 1, :] = folded(part)
    once = (cls == 0).astype(jnp.float32)
    first_row = lax.broadcasted_iota(jnp.int32, tail_ref.shape, 0) == 0
    tail_slots[me] = tail_ref[...] + jnp.where(first_row, once * layer, 0.0)

    def sum_copy(n, slot):
        return pltpu.make_async_remote_copy(
            src_ref=sum_slots.at[slot], dst_ref=sum_slots.at[slot],
            send_sem=sum_send.at[n], recv_sem=sum_recv.at[slot],
            device_id=half_mate(n), device_id_type=MESH,
        )

    def tail_copy(n, slot):
        return pltpu.make_async_remote_copy(
            src_ref=tail_slots.at[slot], dst_ref=tail_slots.at[slot],
            send_sem=tail_send.at[n], recv_sem=tail_recv.at[slot],
            device_id=any_mate(n), device_id_type=MESH,
        )

    for n in range(1, quarter):
        sum_copy(n, lax.rem(dp, quarter)).start()
    for n in range(1, everyone):
        tail_copy(n, me).start()
    for n in range(1, quarter):
        sum_copy(n, lax.rem(dp, quarter)).wait_send()
        sum_copy(n, lax.rem(dp + n, quarter)).wait_recv()
    for n in range(1, everyone):
        tail_copy(n, me).wait_send()
        tail_copy(n, lax.rem(me + n, everyone)).wait_recv()
    value = sum_slots[0]
    for n in range(1, quarter):
        value = value + sum_slots[n]
    tail = tail_slots[0]
    for n in range(1, everyone):
        tail = tail + tail_slots[n]
    vec = vec_out_ref[...]
    vec_squares = jnp.sum(jnp.sum(vec * vec, 0, keepdims=True), 1, keepdims=True)
    norm = jnp.sqrt(jnp.sum(tail[0:1], 1, keepdims=True) + vec_squares)
    factor = CLIP_NORM / jnp.maximum(norm, CLIP_NORM)
    mean_squares = jnp.sum(value, 1, keepdims=True) / (half * cols) * factor * factor
    scale = SHAMPOO_RATE * factor * lax.rsqrt(mean_squares + ROOT_EPS)
    for b in range(total):
        for quad in range(2):
            row = 2 * b + quad
            wide_ref[b, :, quad * cols : (quad + 1) * cols] = jnp.broadcast_to(
                scale[row : row + 1], (1, cols)
            )
    rows = lax.broadcasted_iota(jnp.int32, facts_ref.shape, 0)
    loss = jnp.sum(tail[1:2], 1, keepdims=True)
    facts_ref[...] = jnp.where(rows == 0, loss, jnp.where(rows == 1, norm, factor))


def reduce_gradients(
    arrays, lefts, rights, vec_sums, tail, root_left, right_codes, dp_count, cls_count
):
    counts = tuple(array.shape[0] for array in arrays)
    total, rows, width = root_left.shape
    length = lefts[0].shape[0]
    parts, coded_rows = right_codes.shape[0], right_codes.shape[2]
    half, cols = width // 2, width // 2
    sum_rows = 2 * total + -2 * total % 8
    f32, i16 = jnp.float32, jnp.int16

    def pair(*shape):
        return [pltpu.VMEM((2,) + shape, i16), pltpu.VMEM((total,) + shape, i16)]

    def scale_pair(*shape):
        return [
            pltpu.VMEM((2,) + shape + (1, cols), f32),
            pltpu.VMEM((total,) + shape + (1, cols), f32),
        ]

    hbm = pl.BlockSpec(memory_space=pl.ANY)
    vmem = pl.BlockSpec(memory_space=pltpu.VMEM)
    return pl.pallas_call(
        functools.partial(reduce_kernel, counts),
        out_shape=(jax.ShapeDtypeStruct((total, rows, width), f32),) * 4
        + (
            jax.ShapeDtypeStruct((total, 1, width), f32),
            jax.ShapeDtypeStruct(tail.shape, f32),
            jax.ShapeDtypeStruct(vec_sums.shape, f32),
        ),
        in_specs=[hbm] * (len(arrays) + 6) + [vmem, vmem, hbm, hbm],
        out_specs=(hbm,) * 4 + (vmem,) * 3,
        scratch_shapes=[
            pltpu.VMEM((2, rows, width), f32),
            pltpu.VMEM((2, parts, coded_rows, width), jnp.int32),
            pltpu.VMEM((half, width), f32),
            pltpu.VMEM((2, 4, rows, width), f32),
            pltpu.VMEM((total, 2, width), f32),
            pltpu.VMEM((half, width), jnp.bfloat16),
            pltpu.VMEM((half, width), jnp.bfloat16),
            pltpu.VMEM((dp_count // 2, sum_rows, 128), f32),
            pltpu.VMEM((dp_count * cls_count,) + tail.shape, f32),
            pltpu.VMEM((2, length, width), jnp.bfloat16),
            pltpu.VMEM((2, length, width), jnp.bfloat16),
            pltpu.SemaphoreType.DMA((2, 2)),
            pltpu.SemaphoreType.DMA((2, 2)),
            pltpu.SemaphoreType.DMA((dp_count // 2,)),
            pltpu.SemaphoreType.DMA((dp_count // 2,)),
            pltpu.SemaphoreType.DMA((dp_count * cls_count,)),
            pltpu.SemaphoreType.DMA((dp_count * cls_count,)),
            pltpu.VMEM((5, width, cols), f32),
            pltpu.VMEM((2, width, cols), f32),
            pltpu.VMEM((3, 2, 2, PIECE, cols), f32),
        ]
        + pair(width, cols)
        + pair(2, 2, 2 * PIECE, cols)
        + pair(2, 2, PIECE, cols)
        + pair(2, 2, PIECE, cols)
        + pair(2, PIECE, cols)
        + scale_pair()
        + scale_pair(2)
        + scale_pair(2)
        + scale_pair()
        + scale_pair()
        + [
            pltpu.VMEM((total, half, width), i16),
            pltpu.VMEM((total, half // PIECE, 1, width), f32),
            pltpu.VMEM((5, 2) + vec_sums.shape, f32),
            pltpu.SemaphoreType.DMA((2, 2)),
            pltpu.SemaphoreType.DMA((2, 4)),
            pltpu.SemaphoreType.DMA((14, 2)),
            pltpu.SemaphoreType.DMA((14, total)),
            pltpu.SemaphoreType.DMA((14, 2)),
            pltpu.SemaphoreType.DMA((14, total)),
            pltpu.SemaphoreType.DMA((5,)),
            pltpu.SemaphoreType.DMA((5,)),
        ],
        compiler_params=pltpu.CompilerParams(
            collective_id=1, has_side_effects=True, vmem_limit_bytes=60 << 20
        ),
        name="reduce_gradients",
    )(*arrays, *lefts, *rights, vec_sums, tail, root_left, right_codes)


def split_float(values):
    high = values.astype(jnp.bfloat16)
    return high, (values - high.astype(jnp.float32)).astype(jnp.bfloat16)


def stacked_dot(lefts, right, contract_last):
    rows = lefts[0].shape[0]
    left = jnp.concatenate(lefts, 0) if len(lefts) > 1 else lefts[0]
    dims = (((1,), (1 if contract_last else 0,)), ((), ()))
    out = lax.dot_general(left, right, dims, preferred_element_type=jnp.float32)
    return [out[n * rows : (n + 1) * rows] for n in range(len(lefts))]


def encode_roots(part):
    top = jnp.max(jnp.abs(part), 1, keepdims=True)
    level = jnp.ceil(jnp.log2(jnp.maximum(top, 1e-30)))
    codes = jnp.round(part * jnp.exp2(15.0 - level))
    codes = jnp.clip(codes, -32767.0, 32767.0).astype(jnp.int32)
    levels = jnp.broadcast_to(level.astype(jnp.int32), (part.shape[0], 8, part.shape[2]))
    upper = jnp.concatenate([codes[:, 0:8], codes[:, 16:24]], 1)
    lower = jnp.concatenate([codes[:, 8:16], levels], 1)
    return upper * 65536 + (lower + 32768)


def precondition_block(
    own, codes_ref, scales_ref, left_ref, right_codes, outs_ref, squares_ref, high_ref, low_ref,
    right_ref
):
    half, width = codes_ref.shape
    rows = left_ref.shape[0]
    own_rows = pl.ds(pl.multiple_of(own, PIECE), rows)
    parts = right_codes.shape[0]
    size = half // parts
    for n in range(parts):
        packed = right_codes[n]
        upper = lax.shift_right_arithmetic(packed, jnp.full_like(packed, 16)).astype(jnp.float32)
        lower = ((packed & 65535) - 32768).astype(jnp.float32)
        scale = jnp.exp2(lower[8:9] - 15.0)
        right_ref[n * size : n * size + 8, :] = upper[0:8] * scale
        right_ref[n * size + 8 : n * size + 16, :] = lower[0:8] * scale
        right_ref[n * size + 16 : n * size + 24, :] = upper[8:16] * scale
    for piece in range(half // PIECE):
        part = slice(piece * PIECE, (piece + 1) * PIECE)
        high_ref[part, :], low_ref[part, :] = split_float(
            decode(codes_ref[part, :], scales_ref[piece])
        )
    own_value = high_ref[own_rows, :].astype(jnp.float32) + low_ref[own_rows, :].astype(jnp.float32)
    outs_ref[0] = own_value
    squares_ref[0:1, :] = jnp.sum(own_value * own_value, 0, keepdims=True)
    picks = (
        lax.broadcasted_iota(jnp.int32, (rows, half), 1)
        == lax.broadcasted_iota(jnp.int32, (rows, half), 0) + own
    ).astype(jnp.float32).astype(jnp.bfloat16)
    for quad in range(2):
        cols = slice(quad * half, (quad + 1) * half)
        high, low = high_ref[:, cols], low_ref[:, cols]
        mine_high, mine_low = high_ref[own_rows, cols], low_ref[own_rows, cols]
        hh, lh, turned_high = stacked_dot([mine_high, mine_low, picks], high, True)
        hl, turned_low = stacked_dot([mine_high, picks], low, True)
        outs_ref[1, :, cols] = hh + (lh + hl)
        turned_high = turned_high.astype(jnp.bfloat16)
        turned_low = turned_low.astype(jnp.bfloat16)
        root_high, root_low = split_float(left_ref[:, cols])
        thh, tlh, rhh, rlh = stacked_dot([turned_high, turned_low, root_high, root_low], high, False)
        thl, rhl = stacked_dot([turned_high, root_high], low, False)
        outs_ref[2, :, cols] = thh + (tlh + thl)
        half_step = rhh + (rlh + rhl)
        step_high, step_low = split_float(half_step)
        right_high, right_low = split_float(right_ref[:, cols])
        shh, slh = stacked_dot([step_high, step_low], right_high, False)
        (shl,) = stacked_dot([step_high], right_low, False)
        direction = shh + (slh + shl)
        outs_ref[3, :, cols] = direction
        squares_ref[1:2, cols] = jnp.sum(direction * direction, 0, keepdims=True)


def head_kernel(
    image_total, pooled_ref, labels_ref, head_hbm,
    grad_ref, rows_ref, loss_ref,
    head_buf, group_buf, total_buf, slots, load_sem, send_sem, recv_sem, sum_send, sum_recv
):
    dp, cls = lax.axis_index("dp"), lax.axis_index("cls")
    count, rows, width = slots.shape
    images = count * rows
    classes = head_buf.shape[1]
    load = pltpu.make_async_copy(head_hbm, head_buf, load_sem)
    load.start()
    barrier = pltpu.get_barrier_semaphore()
    for n in range(1, count):
        pl.semaphore_signal(
            barrier, inc=1, device_id=(dp, lax.rem(cls + n, count)), device_id_type=MESH
        )
    pl.semaphore_wait(barrier, count - 1)

    def part(ref, index):
        return ref.at[pl.ds(pl.multiple_of(index * rows, 8), rows)]

    def share(n, slot):
        return pltpu.make_async_remote_copy(
            src_ref=pooled_ref, dst_ref=part(group_buf, slot),
            send_sem=send_sem.at[n], recv_sem=recv_sem.at[slot],
            device_id=(dp, lax.rem(cls + n, count)), device_id_type=MESH,
        )

    for n in range(1, count):
        share(n, cls).start()
    part(group_buf, cls)[...] = pooled_ref[...]
    rows_ref[:, width + classes :] = jnp.zeros(
        (images, rows_ref.shape[1] - width - classes), rows_ref.dtype
    )
    for n in range(1, count):
        share(n, cls).wait_send()
        share(n, lax.rem(cls + n, count)).wait_recv()
    load.wait()
    group = group_buf[...].astype(jnp.bfloat16)
    rows_ref[:, :width] = group
    loss = jnp.zeros((1, 1), jnp.float32)
    total = jnp.zeros((images, width), jnp.float32)
    for start in range(0, classes, CLASS_TILE):
        stop = min(classes, start + CLASS_TILE)
        weights = head_buf[:, start:stop]
        logits = jnp.dot(group, weights, preferred_element_type=jnp.float32)
        ids = lax.broadcasted_iota(jnp.int32, logits.shape, 1) + (cls * classes + start)
        target = ids == labels_ref[:, 0:1]
        for n in range(1, labels_ref.shape[1]):
            target = target | (ids == labels_ref[:, n : n + 1])
        target = target.astype(jnp.float32)
        valid = ids < LABELS_REAL
        shrunk = jnp.exp(-jnp.abs(logits))
        terms = jnp.maximum(logits, 0.0) + jnp.log1p(shrunk) - target * logits
        terms = jnp.where(valid, terms, 0.0)
        loss = loss + jnp.sum(jnp.sum(terms, 0, keepdims=True), 1, keepdims=True)
        chance = jnp.where(logits >= 0.0, 1.0, shrunk) / (1.0 + shrunk)
        grads = jnp.where(valid, chance - target, 0.0) / image_total
        grads = grads.astype(jnp.bfloat16)
        rows_ref[:, width + start : width + stop] = grads
        total = total + lax.dot_general(
            grads, weights, (((1,), (1,)), ((), ())), preferred_element_type=jnp.float32
        )
    loss_ref[...] = jnp.broadcast_to(loss / image_total, loss_ref.shape)
    total_buf[...] = total

    def back(n, slot):
        mate = lax.rem(cls + n, count)
        return pltpu.make_async_remote_copy(
            src_ref=part(total_buf, mate), dst_ref=slots.at[slot],
            send_sem=sum_send.at[n], recv_sem=sum_recv.at[slot],
            device_id=(dp, mate), device_id_type=MESH,
        )

    for n in range(1, count):
        back(n, cls).start()
    slots[cls] = part(total_buf, cls)[...]
    for n in range(1, count):
        back(n, cls).wait_send()
        back(n, lax.rem(cls + n, count)).wait_recv()
    value = slots[0]
    for n in range(1, count):
        value = value + slots[n]
    grad_ref[...] = value


def classify(pooled, labels, head_low, cls_count, image_total):
    rows, width = pooled.shape
    images, classes = rows * cls_count, head_low.shape[1]
    wide = ROW_CHUNK * (EARLY_CHUNKS + LATE_CHUNKS)
    assert wide >= width + classes
    f32 = jnp.float32
    vmem = pl.BlockSpec(memory_space=pltpu.VMEM)
    return pl.pallas_call(
        functools.partial(head_kernel, image_total),
        out_shape=(
            jax.ShapeDtypeStruct((rows, width), f32),
            jax.ShapeDtypeStruct((images, wide), jnp.bfloat16),
            jax.ShapeDtypeStruct((8, 128), f32),
        ),
        in_specs=[vmem, vmem, pl.BlockSpec(memory_space=pltpu.HBM)],
        out_specs=(vmem, vmem, vmem),
        scratch_shapes=[
            pltpu.VMEM((width, classes), jnp.bfloat16),
            pltpu.VMEM((images, width), f32),
            pltpu.VMEM((images, width), f32),
            pltpu.VMEM((cls_count, rows, width), f32),
            pltpu.SemaphoreType.DMA,
        ]
        + [pltpu.SemaphoreType.DMA((cls_count,)) for _ in range(4)],
        compiler_params=pltpu.CompilerParams(
            collective_id=2, has_side_effects=True, vmem_limit_bytes=32 << 20
        ),
        name="classify",
    )(pooled, labels, head_low)


def column_barrier():
    barrier = pltpu.get_barrier_semaphore()
    for n in range(1, SHARES):
        pl.semaphore_signal(barrier, inc=1, device_id=column_mate(n), device_id_type=MESH)
    pl.semaphore_wait(barrier, SHARES - 1)


def row_operands(own_rows, chunks):
    shape = (SHARES, own_rows.shape[0], chunks * ROW_CHUNK)
    scratch = [
        pltpu.SemaphoreType.DMA((7, 2)),
        pltpu.SemaphoreType.DMA((8, chunks)),
        pltpu.SemaphoreType.DMA((2,)),
    ]
    return jax.ShapeDtypeStruct(shape, own_rows.dtype), scratch


def row_steps(first, own_ref, out_ref, send_sem, recv_sem, copy_sem):
    z, y, x, core = torus_place()
    mate_y = torus_device(z, 1 - y, x, core)
    count = recv_sem.shape[1]

    def columns(m):
        return pl.ds(pl.multiple_of(m * ROW_CHUNK, 128), ROW_CHUNK)

    def own_columns(m):
        return own_ref.at[:, pl.ds(pl.multiple_of((m + first) * ROW_CHUNK, 128), ROW_CHUNK)]

    def copy(slot, arrival, m, source, target, mate):
        return pltpu.make_async_remote_copy(
            src_ref=source, dst_ref=target,
            send_sem=send_sem.at[slot, m % 2], recv_sem=recv_sem.at[arrival, m],
            device_id=mate, device_id_type=MESH,
        )

    def local(m):
        return pltpu.make_async_copy(
            own_columns(m), out_ref.at[z * 2 + y, :, columns(m)], copy_sem.at[m % 2]
        )

    def along(m, n, outgoing):
        other = lax.rem(z + n, 4)
        origin = z if outgoing else other
        target = out_ref.at[origin * 2 + y, :, columns(m)]
        mate = torus_device(other, y, x, core)
        return copy(n - 1, origin, m, own_columns(m), target, mate)

    def cross(m, n, outgoing):
        block = out_ref.at[n * 2 + (y if outgoing else 1 - y), :, columns(m)]
        return copy(3 + n, 4 + n, m, block, block, mate_y)

    def step(t):
        @pl.when(t < count)
        def _():
            local(t).start()
            for n in range(1, 4):
                along(t, n, True).start()

        @pl.when((t >= 1) & (t < count + 1))
        def _():
            m = t - 1
            local(m).wait()
            for n in range(1, 4):
                along(m, n, True).wait_send()
                along(m, n, False).wait_recv()
            for n in range(4):
                cross(m, n, True).start()

        @pl.when((t >= 2) & (t < count + 2))
        def _():
            m = t - 2
            for n in range(4):
                cross(m, n, True).wait_send()
                cross(m, n, False).wait_recv()

    return step, count + 2


def gather_steps(own_ref, out_ref, send_sem, recv_sem, copy_sem):
    count, rows, width = own_ref.shape
    cols = width // 2
    z, y, x, core = torus_place()
    mate_core = torus_device(z, y, x, 1 - core)
    mate_x = torus_device(z, y, 1 - x, core)
    mate_y = torus_device(z, 1 - y, x, core)
    own_cols = pl.ds(pl.multiple_of(core * cols, 128), cols)
    other_cols = pl.ds(pl.multiple_of((1 - core) * cols, 128), cols)
    spare = rows - SPAN
    held = x * spare
    lone = (x * SPAN, (1 - x) * SPAN)

    def share(m, zz, yy, start, size):
        begin = (zz * 2 + yy) * rows + start
        return out_ref.at[m, pl.ds(pl.multiple_of(begin, 16), size), own_cols]

    def copy(slot, arrival, m, source, target, mate):
        return pltpu.make_async_remote_copy(
            src_ref=source, dst_ref=target,
            send_sem=send_sem.at[slot, m % 2], recv_sem=recv_sem.at[arrival, m],
            device_id=mate, device_id_type=MESH,
        )

    def local(m):
        return pltpu.make_async_copy(
            own_ref.at[m, :, own_cols], share(m, z, y, 0, rows), copy_sem.at[m % 2]
        )

    def along(m, n, outgoing):
        other = lax.rem(z + n, 4)
        origin = z if outgoing else other
        source = own_ref.at[m, pl.ds(pl.multiple_of(held, 16), SPAN), own_cols]
        mate = torus_device(other, y, x, core)
        return copy(n - 1, origin, m, source, share(m, origin, y, held, SPAN), mate)

    def cross(m, n, outgoing):
        block = share(m, n, y if outgoing else 1 - y, held, SPAN)
        return copy(3 + n, 4 + n, m, block, block, mate_y)

    def patch(m, n, outgoing):
        index = lax.rem(z * 2 + y + n, SHARES)
        block = share(m, index // 2, lax.rem(index, 2), lone[0 if outgoing else 1], spare)
        return copy(6 + n, 7 + n, m, block, block, mate_x)

    def swap(m, columns):
        block = out_ref.at[m, :, columns]
        return copy(14, 15, m, block, block, mate_core)

    def finish(copies):
        for outgoing, incoming in copies:
            outgoing.wait_send()
            incoming.wait_recv()

    def step(t):
        @pl.when(t < count)
        def _():
            local(t).start()
            for n in range(1, 4):
                along(t, n, True).start()

        @pl.when((t >= 1) & (t < count + 1))
        def _():
            m = t - 1
            local(m).wait()
            finish([(along(m, n, True), along(m, n, False)) for n in range(1, 4)])
            for n in range(4):
                cross(m, n, True).start()

        @pl.when((t >= 2) & (t < count + 2))
        def _():
            m = t - 2
            finish([(cross(m, n, True), cross(m, n, False)) for n in range(4)])
            for n in range(1, SHARES):
                patch(m, n, True).start()

        @pl.when((t >= 3) & (t < count + 3))
        def _():
            m = t - 3
            finish([(patch(m, n, True), patch(m, n, False)) for n in range(1, SHARES)])
            swap(m, own_cols).start()

        @pl.when((t >= 4) & (t < count + 4))
        def _():
            m = t - 4
            swap(m, own_cols).wait_send()
            swap(m, other_cols).wait_recv()

    return step, count + GATHER_DEPTH


def column_mate(n):
    z, y, x, core = torus_place()
    other = lax.rem(z * 2 + y + n, SHARES)
    return torus_device(other // 2, lax.rem(other, 2), x, core)


def gather_barrier():
    z, y, x, core = torus_place()
    barrier = pltpu.get_barrier_semaphore()
    mates = [torus_device(z, y, x, 1 - core), torus_device(z, y, 1 - x, core)]
    for mate in mates + [column_mate(n) for n in range(1, SHARES)]:
        pl.semaphore_signal(barrier, inc=1, device_id=mate, device_id_type=MESH)
    pl.semaphore_wait(barrier, SHARES + 1)


def gather_kernel(
    own_ref, vec_ref, out_ref, vec_out_ref, send_sem, recv_sem, copy_sem, vec_send, vec_recv
):
    z, y, _, _ = torus_place()
    me = z * 2 + y
    gather_barrier()

    def vec_copy(n, slot):
        return pltpu.make_async_remote_copy(
            src_ref=vec_ref, dst_ref=vec_out_ref.at[slot],
            send_sem=vec_send.at[n], recv_sem=vec_recv.at[slot],
            device_id=column_mate(n), device_id_type=MESH,
        )

    for n in range(1, SHARES):
        vec_copy(n, me).start()
    vec_out_ref[me] = vec_ref[...]
    gather_step, turns = gather_steps(own_ref, out_ref, send_sem, recv_sem, copy_sem)

    def step(t, carry):
        gather_step(t)
        return carry

    lax.fori_loop(0, turns, step, 0)
    for n in range(1, SHARES):
        vec_copy(n, me).wait_send()
        vec_copy(n, lax.rem(me + n, SHARES)).wait_recv()


def gather_semaphores(count):
    return [
        pltpu.SemaphoreType.DMA((15, 2)),
        pltpu.SemaphoreType.DMA((16, count)),
        pltpu.SemaphoreType.DMA((2,)),
    ]


def attention_gather_kernel(
    qids_ref, kcodes_ref, q_ref, k_ref, v_ref, own_ref, out_ref, blocks_ref,
    bias_ref, send_sem, recv_sem, copy_sem
):
    pair, tiles = pl.program_id(0), q_ref.shape[0] // QTILE
    slots = pl.num_programs(0) * tiles

    @pl.when(pair == 0)
    def _():
        gather_barrier()

    gather_step, turns = gather_steps(own_ref, blocks_ref, send_sem, recv_sem, copy_sem)
    attention_bias(qids_ref, kcodes_ref, bias_ref)
    for tile in range(tiles):
        slot = pair * tiles + tile
        begin, end = slot * turns // slots, (slot + 1) * turns // slots

        @pl.when(begin < end)
        def _(begin=begin):
            gather_step(begin)

        attention_tile(tile, q_ref, k_ref, v_ref, out_ref, bias_ref)


def attention_forward_gathering(qkv_rows, pack_ids, key_codes, own):
    _, length, width = qkv_rows.shape
    count, rows, _ = own.shape
    tiles = length // QTILE
    assert count + GATHER_DEPTH <= tiles * (width // PAIR)
    return pl.pallas_call(
        attention_gather_kernel,
        grid=(width // PAIR,),
        out_shape=(
            jax.ShapeDtypeStruct((length, width), jnp.bfloat16),
            jax.ShapeDtypeStruct((count, SHARES * rows, width), own.dtype),
        ),
        in_specs=[whole_spec((length, 1)), whole_spec((1, length))]
        + [pair_spec(length, part) for part in range(3)]
        + [whole_spec(own.shape)],
        out_specs=(pair_spec(length), pl.BlockSpec(memory_space=pl.ANY)),
        scratch_shapes=[pltpu.VMEM(bias_shape(length), jnp.float32)] + gather_semaphores(count),
        compiler_params=pltpu.CompilerParams(
            collective_id=4, has_side_effects=True, vmem_limit_bytes=40 << 20
        ),
        name="attention_forward",
    )(pack_ids[:, None], key_codes[None, :], qkv_rows, qkv_rows, qkv_rows, own)


def gather_weights(own, vec):
    count, rows, width = own.shape
    hbm = pl.BlockSpec(memory_space=pl.ANY)
    vmem = pl.BlockSpec(memory_space=pltpu.VMEM)
    return pl.pallas_call(
        gather_kernel,
        out_shape=(
            jax.ShapeDtypeStruct((count, SHARES * rows, width), own.dtype),
            jax.ShapeDtypeStruct((SHARES,) + vec.shape, vec.dtype),
        ),
        in_specs=[vmem, vmem],
        out_specs=(hbm, vmem),
        scratch_shapes=gather_semaphores(count)
        + [pltpu.SemaphoreType.DMA((SHARES,)), pltpu.SemaphoreType.DMA((SHARES,))],
        compiler_params=pltpu.CompilerParams(
            collective_id=3, has_side_effects=True, vmem_limit_bytes=32 << 20
        ),
        name="gather_weights",
    )(own, vec)


def adam_step(weight, grad, first, second, count):
    first = BETA_FIRST * first + (1.0 - BETA_FIRST) * grad
    second = BETA_SECOND * second + (1.0 - BETA_SECOND) * grad * grad
    fix_first = 1.0 - jnp.power(BETA_FIRST, count)
    fix_second = 1.0 - jnp.power(BETA_SECOND, count)
    update = first / fix_first / (jnp.sqrt(second / fix_second) + ADAM_EPS) + WEIGHT_DECAY * weight
    return (weight - ADAM_RATE * update, first, second)


def split_halves(values, half_size):
    block_count, row_count, feature_dim = values.shape
    return values.reshape(block_count, row_count, 2, half_size)


def reduced_half(values, half_groups):
    part = lax.psum_scatter(values, ("dp", "cls"), scatter_dimension=1, tiled=True)
    return lax.all_gather(part, ("dp", "cls"), axis=1, tiled=True, axis_index_groups=half_groups)


def preconditioned_rows(grad_half, root_left, right_half, own_start):
    count, row_count, width = root_left.shape
    half_size = width // 2
    block_rows = lax.dynamic_slice_in_dim(grad_half, own_start, row_count, 1)
    grad_quads = split_halves(grad_half, half_size)
    rows_quads = split_halves(block_rows, half_size)
    cols_quads = lax.dynamic_slice_in_dim(grad_quads, own_start, row_count, 3)
    precise = FULL_PRECISION
    left_add = jnp.einsum("brjk,bljk->brjl", rows_quads, grad_quads, precision=precise)
    right_add = jnp.einsum("bkja,bkjm->bajm", cols_quads, grad_quads, precision=precise)
    direction = jnp.einsum(
        "brjk,bkjm->brjm", split_halves(root_left, half_size), grad_quads, precision=precise
    )
    direction = jnp.einsum(
        "brjk,bkjm->brjm", direction, split_halves(right_half, half_size), precision=precise
    )
    flat = (count, row_count, width)
    return left_add.reshape(flat), right_add.reshape(flat), direction.reshape(flat), block_rows


def on_device(
    patches,
    image_ids,
    keep,
    labels,
    owner,
    step,
    enc_weights,
    stats_left,
    stats_right,
    root_left,
    root_right,
    head_weights,
    head_m,
    head_v,
    vectors,
    vec_m,
    vec_v,
):
    dp_count = lax.axis_size("dp")
    cls_count = lax.axis_size("cls")
    dp_index = lax.axis_index("dp")
    cls_index = lax.axis_index("cls")
    block_count, row_count, feature_dim = enc_weights.shape
    up_count = (block_count - 5) // 2
    half_size = feature_dim // 2
    part_rows = row_count // cls_count
    half_dp = dp_count // 2
    half_group = half_dp * cls_count
    half_groups = [
        list(range(half_group)),
        list(range(half_group, 2 * half_group)),
    ]

    def my_part(values):
        return lax.dynamic_slice_in_dim(values, cls_index * part_rows, part_rows, 1)

    on_torus = dp_count == 8 and cls_count == 4
    if on_torus:
        vec_block = jnp.pad(vectors, ((0, -vectors.shape[0] % 8), (0, -row_count % 128)))
        own_low = enc_weights.astype(jnp.bfloat16)
        blocks, vec_blocks = gather_weights(own_low[:5], vec_block)
        right_part, vec_blocks = lax.optimization_barrier((my_part(root_right), vec_blocks))
        vec_low = jnp.transpose(vec_blocks[:, : vectors.shape[0], :row_count], (1, 0, 2))
        vec_all = lax.reduce_precision(vec_low.reshape(vectors.shape[0], feature_dim), 8, 7)
    else:
        right_part = my_part(root_right)
        all_blocks = lax.all_gather(
            my_part(enc_weights.astype(jnp.bfloat16)), ("dp", "cls"), axis=1, tiled=True
        )
        blocks = all_blocks[:5]
        vec_low = lax.all_gather(vectors.astype(jnp.bfloat16), "dp", axis=1, tiled=True)
        vec_all = vec_low.astype(jnp.float32)
    head_low = lax.all_gather(head_weights.astype(jnp.bfloat16), "dp", axis=0, tiled=True)
    final_gain = vec_all[9 + up_count]
    final_shift = vec_all[10 + up_count]
    pack_ids, pack_keep = image_ids[0], keep[0]
    key_codes = jnp.where(pack_keep == 1, pack_ids, -1)

    def attend(qkv_rows):
        if on_torus:
            return attention_forward_gathering(qkv_rows, pack_ids, key_codes, own_low[5:])
        return attention_forward(qkv_rows, pack_ids, key_codes), all_blocks[5:]

    output, mlp_blocks, saved = layer_forward(blocks, vec_all, patches, attend)
    if on_torus:
        right_codes = lax.all_gather(
            encode_roots(right_part), ("dp", "cls"), axis=0, axis_index_groups=half_groups
        )
    else:
        right_half = lax.all_gather(
            right_part, ("dp", "cls"), axis=1, tiled=True, axis_index_groups=half_groups
        )
    pooled = pool_rows(output, final_gain, final_shift, pack_ids, pack_keep)
    class_dev = head_low.shape[1]
    image_total = labels.shape[0] * dp_count
    if on_torus:
        grad_pooled, own_rows, loss_rows = classify(
            lax.reduce_precision(pooled, 8, 7), labels, head_low, cls_count, image_total
        )
        loss_part = loss_rows[0, 0]
    else:
        group = lax.all_gather(pooled.astype(jnp.bfloat16), "cls", axis=0, tiled=True)
        logits = jnp.dot(group, head_low, preferred_element_type=jnp.float32)
        class_ids = cls_index * class_dev + jnp.arange(class_dev)
        valid = class_ids[None, :] < LABELS_REAL
        target = jnp.any(labels[:, :, None] == class_ids[None, None, :], 1).astype(jnp.float32)
        terms = jax.nn.softplus(logits) - target * logits
        loss_part = jnp.sum(jnp.where(valid, terms, 0.0)) / image_total
        grad_logits = jnp.where(valid, jax.nn.sigmoid(logits) - target, 0.0) / image_total
        grad_logits = grad_logits.astype(jnp.bfloat16)
        group_grad = jnp.einsum(
            "gc,dc->gd", grad_logits, head_low, preferred_element_type=jnp.float32
        )
        grad_pooled = lax.psum_scatter(group_grad, "cls", scatter_dimension=0, tiled=True)
        own_rows = jnp.concatenate([group, grad_logits], 1)

    def pool_local(rows_in, gain, shift):
        return pool_rows(rows_in, gain, shift, pack_ids, pack_keep)

    pool_back = jax.vjp(pool_local, output, final_gain, final_shift)[1]
    grad_output, grad_gain, grad_shift = pool_back(grad_pooled)
    lefts, rights, mlp_grads, grad_vectors, gathered = layer_backward(
        blocks,
        mlp_blocks,
        vec_all,
        patches,
        saved,
        pack_ids,
        key_codes,
        grad_output,
        grad_gain,
        grad_shift,
        own_rows if on_torus else None,
    )
    if on_torus:
        head_rows = jnp.concatenate(gathered, 2).reshape(image_total, -1)
    else:
        head_rows = lax.all_gather(own_rows, "dp", axis=0, tiled=True)
    pooled_all = head_rows[:, :feature_dim]
    grad_logits_all = head_rows[:, feature_dim : feature_dim + class_dev]
    pooled_mine = lax.dynamic_slice_in_dim(pooled_all, dp_index * row_count, row_count, 1)
    head_grad = jnp.einsum(
        "gr,gc->rc", pooled_mine, grad_logits_all, preferred_element_type=jnp.float32
    )

    head_squares = jnp.sum(head_grad * head_grad)
    if on_torus:
        padded = jnp.pad(grad_vectors, ((0, -grad_vectors.shape[0] % 8), (0, 0)))
        tail = jnp.pad(jnp.stack([head_squares, loss_part])[:, None], ((0, 6), (0, 127)))
        block_rows, left_add, right_add, direction, wide_scale, facts, vector_sum = (
            reduce_gradients(
                mlp_grads, lefts, rights, padded, tail, root_left, right_codes,
                dp_count, cls_count,
            )
        )
        vector_sum = vector_sum[: grad_vectors.shape[0]]
        loss, grad_norm, factor = facts[0, 0], facts[1, 0], facts[2, 0]
    else:
        over_rows = "td,te->de"
        first_grads = [
            jnp.einsum(over_rows, left, right, preferred_element_type=jnp.float32)[None]
            for left, right in (
                (lefts[0], rights[0]),
                (lefts[1], rights[1][0]),
                (lefts[1], rights[1][1]),
                (lefts[1], rights[1][2]),
                (lefts[2], rights[2]),
            )
        ]
        grad_half = reduced_half(jnp.concatenate(first_grads + list(mlp_grads), 0), half_groups)
        vector_sum = lax.psum(grad_vectors, ("dp", "cls"))
        left_add, right_add, direction, block_rows = preconditioned_rows(
            grad_half, root_left, right_half, (dp_index % half_dp) * row_count
        )
        squares = jnp.sum(split_halves(direction * direction, half_size), (1, 3))
        in_top = (dp_index < half_dp).astype(jnp.float32)
        once = (cls_index == 0).astype(jnp.float32)
        all_squares = head_squares + once * jnp.sum(block_rows * block_rows)
        packed = jnp.concatenate(
            [
                (once * in_top * squares).reshape(-1),
                (once * (1.0 - in_top) * squares).reshape(-1),
                jnp.stack([all_squares, loss_part]),
            ]
        )
        packed = lax.psum(packed, ("dp", "cls"))
        loss = packed[4 * block_count + 1]
        all_squares = packed[4 * block_count]
        sums = packed[: 4 * block_count].reshape(2, block_count, 2)
        block_squares = jnp.where(dp_index < half_dp, sums[0], sums[1])
        grad_norm = jnp.sqrt(all_squares + jnp.sum(vector_sum * vector_sum))
        factor = CLIP_NORM / jnp.maximum(grad_norm, CLIP_NORM)
        mean_squares = block_squares / (half_size * half_size) * factor * factor
        scale = SHAMPOO_RATE * factor * lax.rsqrt(mean_squares + ROOT_EPS)
        wide_scale = jnp.repeat(scale, half_size, axis=1)[:, None, :]
    vector_rows = lax.dynamic_slice_in_dim(vector_sum, dp_index * row_count, row_count, 1)
    new_blocks = enc_weights - direction * wide_scale
    square_factor = 0.5 * factor * factor
    new_left = 0.5 * stats_left + square_factor * left_add
    new_right = 0.5 * stats_right + square_factor * right_add
    count = step.astype(jnp.float32)
    new_vec, new_vec_m, new_vec_v = adam_step(vectors, vector_rows * factor, vec_m, vec_v, count)
    new_head, new_head_m, new_head_v = adam_step(
        head_weights, head_grad * factor, head_m, head_v, count
    )
    return (
        loss,
        grad_norm,
        new_blocks,
        block_rows * factor,
        new_left,
        new_right,
        new_vec,
        new_vec_m,
        new_vec_v,
        new_head,
        new_head_m,
        new_head_v,
    )


def solution(mesh):
    return jax.shard_map(
        on_device,
        mesh=mesh,
        in_specs=(
            P(("dp", "cls"), None),
            P(("dp", "cls"), None),
            P(("dp", "cls"), None),
            P("dp", None),
            P(),
            P(),
            P(None, "dp", None),
            P(None, "dp", None),
            P(None, "dp", None),
            P(None, "dp", None),
            P(None, "dp", None),
            P("dp", "cls"),
            P("dp", "cls"),
            P("dp", "cls"),
            P(None, "dp"),
            P(None, "dp"),
            P(None, "dp"),
        ),
        out_specs=(
            P(),
            P(),
            P(None, "dp", None),
            P(None, "dp", None),
            P(None, "dp", None),
            P(None, "dp", None),
            P(None, "dp"),
            P(None, "dp"),
            P(None, "dp"),
            P("dp", "cls"),
            P("dp", "cls"),
            P("dp", "cls"),
        ),
        check_vma=False,
    )
```

```python
import functools

import jax
import jax.numpy as jnp
from jax import lax
from jax.experimental import pallas as pl
from jax.experimental.pallas import tpu as pltpu
from jax.sharding import PartitionSpec as P

HEADS = 12
HEAD = 64
LABELS_REAL = 21843
IMAGE_MAX = 196
QTILE = 256
PAIR = 2 * HEAD
ROWS = 256
HIDDEN_TILE = 384
MESH = pl.DeviceIdType.MESH
CODE_TOP = 32766.0
CODE_FLOOR = 1e-33
PIECE = 48
FEATURE_TILE = 128
SPAN = 48
SHARES = 8
GATHER_DEPTH = 4
CLASS_TILE = 512
IMG_PACK = 8


FULL_PRECISION = lax.Precision.HIGHEST
NORM_EPS = 1e-06
CLIP_NORM = 1.0
ADAM_RATE = 0.02
SHAMPOO_RATE = 0.01
BETA_FIRST = 0.9
BETA_SECOND = 0.999
ADAM_EPS = 1e-08
WEIGHT_DECAY = 0.1
ROOT_EPS = 1e-06


def norm_rows(values, gain, shift):
    centred = values - jnp.mean(values, -1, keepdims=True)
    spread = jnp.mean(centred * centred, -1, keepdims=True)
    return centred * lax.rsqrt(spread + NORM_EPS) * gain + shift


def pool_rows(output, gain, shift, pack_ids, pack_keep):
    final = norm_rows(output, gain, shift)
    member = (
        (pack_ids[None, :] == jnp.arange(IMG_PACK)[:, None]) & (pack_keep[None, :] == 1)
    ).astype(jnp.float32)
    counted = jnp.maximum(jnp.sum(member, 1), 1.0)
    return jnp.dot(member, final, precision=FULL_PRECISION) / counted[:, None]


def key_window(tile, length):
    reach = -(-(IMAGE_MAX - 1) // 128) * 128
    low = max(0, tile * QTILE - reach)
    high = min(length, (tile + 1) * QTILE + reach)
    return low, high


def attention_bias(qids_ref, kcodes_ref, bias_ref):
    length = qids_ref.shape[0]

    @pl.when(pl.program_id(0) == 0)
    def _():
        for tile in range(length // QTILE):
            low, high = key_window(tile, length)
            shape = (QTILE, high - low)
            rows = lax.broadcasted_iota(jnp.int32, shape, 0) + tile * QTILE
            cols = lax.broadcasted_iota(jnp.int32, shape, 1) + low
            same = qids_ref[tile * QTILE : (tile + 1) * QTILE, :] == kcodes_ref[:, low:high]
            bias_ref[tile, :, : high - low] = jnp.where(same | (rows == cols), 0.0, -1e30)


def attention_tile(tile, q_ref, k_ref, v_ref, out_ref, bias_ref):
    lane = lax.broadcasted_iota(jnp.int32, (QTILE, PAIR), 1)
    low, high = key_window(tile, q_ref.shape[0])
    rows = pl.ds(tile * QTILE, QTILE)
    queries = q_ref[rows, :] * jnp.bfloat16(HEAD ** (-0.5))
    keys = k_ref[low:high, :]
    values = v_ref[low:high, :]
    halves = []
    for head in range(2):
        mine = (lane >= head * HEAD) & (lane < (head + 1) * HEAD)
        picked = jnp.where(mine, queries, jnp.zeros_like(queries))
        scores = lax.dot_general(
            picked, keys, (((1,), (1,)), ((), ())), preferred_element_type=jnp.float32
        )
        scores = scores + bias_ref[tile, :, : high - low]
        top = jnp.max(scores, -1, keepdims=True)
        weights = jnp.exp(scores - top)
        probs = weights * (1.0 / jnp.sum(weights, -1, keepdims=True))
        halves.append(
            jnp.dot(probs.astype(jnp.bfloat16), values, preferred_element_type=jnp.float32)
        )
    out_ref[rows, :] = jnp.where(lane < HEAD, halves[0], halves[1]).astype(jnp.bfloat16)


def attention_forward_kernel(qids_ref, kcodes_ref, q_ref, k_ref, v_ref, out_ref, bias_ref):
    attention_bias(qids_ref, kcodes_ref, bias_ref)
    for tile in range(q_ref.shape[0] // QTILE):
        attention_tile(tile, q_ref, k_ref, v_ref, out_ref, bias_ref)


def attention_back_bias(qids_ref, kcodes_ref, bias_ref):
    length = kcodes_ref.shape[0]

    @pl.when(pl.program_id(0) == 0)
    def _():
        for tile in range(length // QTILE):
            low, high = key_window(tile, length)
            shape = (high - low, QTILE)
            rows = lax.broadcasted_iota(jnp.int32, shape, 0) + low
            cols = lax.broadcasted_iota(jnp.int32, shape, 1) + tile * QTILE
            same = kcodes_ref[low:high, :] == qids_ref[:, tile * QTILE : (tile + 1) * QTILE]
            bias_ref[tile, : high - low, :] = jnp.where(same | (rows == cols), 0.0, -1e30)


def attention_back_tile(tile, q_ref, k_ref, v_ref, do_ref, out_ref, bias_ref, dk_ref, dv_ref):
    length = q_ref.shape[0]
    lane = lax.broadcasted_iota(jnp.int32, (QTILE, PAIR), 1)
    scale = jnp.bfloat16(HEAD ** (-0.5))
    low, high = key_window(tile, length)
    rows = pl.ds(tile * QTILE, QTILE)
    window = pl.ds(low, high - low)
    queries = q_ref[rows, :] * scale
    keys = k_ref[window, :]
    values = v_ref[window, :]
    grads = do_ref[rows, :]
    halves = []
    for head in range(2):
        mine = (lane >= head * HEAD) & (lane < (head + 1) * HEAD)
        picked = jnp.where(mine, queries, jnp.zeros_like(queries))
        picked_grads = jnp.where(mine, grads, jnp.zeros_like(grads))
        scores = lax.dot_general(
            keys, picked, (((1,), (1,)), ((), ())), preferred_element_type=jnp.float32
        )
        scores = scores + bias_ref[tile, : high - low, :]
        top = jnp.max(scores, 0, keepdims=True)
        weights = jnp.exp(scores - top)
        probs = weights * (1.0 / jnp.sum(weights, 0, keepdims=True))
        grad_probs = lax.dot_general(
            values, picked_grads, (((1,), (1,)), ((), ())), preferred_element_type=jnp.float32
        )
        inner = jnp.sum(probs * grad_probs, 0, keepdims=True)
        grad_scores = (probs * (grad_probs - inner)).astype(jnp.bfloat16)
        dv_ref[window, :] += jnp.dot(
            probs.astype(jnp.bfloat16), picked_grads, preferred_element_type=jnp.float32
        )
        dk_ref[window, :] += jnp.dot(
            grad_scores, picked, preferred_element_type=jnp.float32
        )
        halves.append(
            lax.dot_general(
                grad_scores,
                keys,
                (((0,), (0,)), ((), ())),
                preferred_element_type=jnp.float32,
            )
        )
    grad_queries = jnp.where(lane < HEAD, halves[0], halves[1]) * HEAD ** (-0.5)
    out_ref[0, rows, :] = grad_queries.astype(jnp.bfloat16)


def attention_backward_kernel(
    qids_ref, kcodes_ref, q_ref, k_ref, v_ref, do_ref, out_ref, bias_ref, dk_ref, dv_ref
):
    attention_back_bias(qids_ref, kcodes_ref, bias_ref)
    dk_ref[...] = jnp.zeros_like(dk_ref)
    dv_ref[...] = jnp.zeros_like(dv_ref)
    for tile in range(q_ref.shape[0] // QTILE):
        attention_back_tile(tile, q_ref, k_ref, v_ref, do_ref, out_ref, bias_ref, dk_ref, dv_ref)
    out_ref[1] = dk_ref[...].astype(jnp.bfloat16)
    out_ref[2] = dv_ref[...].astype(jnp.bfloat16)


def pair_spec(length, part=None):
    if part is None:
        return pl.BlockSpec((length, PAIR), lambda pair: (0, pair))
    return pl.BlockSpec((None, length, PAIR), lambda pair: (part, 0, pair))


def whole_spec(shape):
    return pl.BlockSpec(shape, lambda pair: (0,) * len(shape))


def bias_shape(length):
    tiles = length // QTILE
    window = max(high - low for low, high in (key_window(t, length) for t in range(tiles)))
    return tiles, QTILE, window


def attention_forward(qkv_rows, pack_ids, key_codes):
    _, length, width = qkv_rows.shape
    return pl.pallas_call(
        attention_forward_kernel,
        grid=(width // PAIR,),
        out_shape=jax.ShapeDtypeStruct((length, width), jnp.bfloat16),
        in_specs=[whole_spec((length, 1)), whole_spec((1, length))]
        + [pair_spec(length, part) for part in range(3)],
        out_specs=pair_spec(length),
        scratch_shapes=[pltpu.VMEM(bias_shape(length), jnp.float32)],
        compiler_params=pltpu.CompilerParams(vmem_limit_bytes=40 << 20),
        name="attention_forward",
    )(pack_ids[:, None], key_codes[None, :], qkv_rows, qkv_rows, qkv_rows)


def attention_backward(qkv_rows, pack_ids, key_codes, grad_attended):
    _, length, width = qkv_rows.shape
    tiles = length // QTILE
    window = max(high - low for low, high in (key_window(t, length) for t in range(tiles)))
    return pl.pallas_call(
        attention_backward_kernel,
        grid=(width // PAIR,),
        out_shape=jax.ShapeDtypeStruct((3, length, width), jnp.bfloat16),
        in_specs=[whole_spec((1, length)), whole_spec((length, 1))]
        + [pair_spec(length, part) for part in range(3)]
        + [pair_spec(length)],
        out_specs=pl.BlockSpec((3, length, PAIR), lambda pair: (0, 0, pair)),
        scratch_shapes=[
            pltpu.VMEM((tiles, window, QTILE), jnp.float32),
            pltpu.VMEM((length, PAIR), jnp.float32),
            pltpu.VMEM((length, PAIR), jnp.float32),
        ],
        compiler_params=pltpu.CompilerParams(vmem_limit_bytes=40 << 20),
        name="attention_backward",
    )(pack_ids[None, :], key_codes[:, None], qkv_rows, qkv_rows, qkv_rows, grad_attended)


def mlp_forward_kernel(x_ref, up_ref, bias_ref, down_ref, units_ref, slope_ref, out_ref):
    first = pl.program_id(0) == 0

    @pl.when(first)
    def _():
        out_ref[...] = jnp.zeros_like(out_ref)

    for start in range(0, x_ref.shape[0], ROWS):
        rows = pl.ds(start, ROWS)
        pre = jnp.dot(x_ref[rows, :], up_ref[...], preferred_element_type=jnp.float32)
        pre = pre + bias_ref[...]
        half = 0.5 + 0.5 * lax.erf(pre * 0.7071067811865476)
        bell = jnp.exp(-0.5 * pre * pre) * 0.3989422804014327
        units = (pre * half).astype(jnp.bfloat16)
        units_ref[rows, :] = units
        slope_ref[rows, :] = half + pre * bell
        out_ref[rows, :] += jnp.dot(units, down_ref[...], preferred_element_type=jnp.float32)


def mlp_backward_kernel(
    x_ref, dm_ref, up_ref, down_ref, units_ref, slope_ref,
    grad_up_ref, grad_down_ref, bias_ref, dx_ref, dpre_ref
):
    @pl.when(pl.program_id(0) == 0)
    def _():
        dx_ref[...] = jnp.zeros_like(dx_ref)

    total = jnp.zeros((1, HIDDEN_TILE), jnp.float32)
    for start in range(0, x_ref.shape[0], ROWS):
        rows = pl.ds(start, ROWS)
        units_back = lax.dot_general(
            dm_ref[rows, :], down_ref[...], (((1,), (1,)), ((), ())),
            preferred_element_type=jnp.float32,
        )
        grad_pre = (units_back * slope_ref[rows, :]).astype(jnp.bfloat16)
        dpre_ref[rows, :] = grad_pre
        total = total + jnp.sum(grad_pre.astype(jnp.float32), 0, keepdims=True)
        dx_ref[rows, :] += lax.dot_general(
            grad_pre, up_ref[...], (((1,), (1,)), ((), ())), preferred_element_type=jnp.float32
        )
    bias_ref[...] = total
    over_rows = (((0,), (0,)), ((), ()))
    grad_down_ref[...] = lax.dot_general(
        units_ref[...], dm_ref[...], over_rows, preferred_element_type=jnp.float32
    )
    grad_up_ref[...] = lax.dot_general(
        x_ref[...], dpre_ref[...], over_rows, preferred_element_type=jnp.float32
    )


def mlp_specs(length, width, up_count):
    split = width // HIDDEN_TILE
    resident = pl.BlockSpec((length, width), lambda t: (0, 0))
    up = pl.BlockSpec((None, width, HIDDEN_TILE), lambda t: (t // split, 0, t % split))
    down = pl.BlockSpec(
        (None, HIDDEN_TILE, width), lambda t: (up_count + t // split, t % split, 0)
    )
    hidden = pl.BlockSpec((length, HIDDEN_TILE), lambda t: (0, t))
    bias = pl.BlockSpec((1, HIDDEN_TILE), lambda t: (0, t))
    return split, resident, up, down, hidden, bias


def mlp_forward(rows, blocks, up_bias):
    length, width = rows.shape
    up_count = blocks.shape[0] // 2
    split, resident, up, down, hidden, bias = mlp_specs(length, width, up_count)
    hidden_size = up_count * width
    return pl.pallas_call(
        mlp_forward_kernel,
        grid=(up_count * split,),
        out_shape=(
            jax.ShapeDtypeStruct((length, hidden_size), jnp.bfloat16),
            jax.ShapeDtypeStruct((length, hidden_size), jnp.float32),
            jax.ShapeDtypeStruct((length, width), jnp.float32),
        ),
        in_specs=[resident, up, bias, down],
        out_specs=(hidden, hidden, resident),
        compiler_params=pltpu.CompilerParams(vmem_limit_bytes=48 << 20),
        name="mlp_forward",
    )(rows, blocks, up_bias.reshape(1, hidden_size), blocks)


def mlp_backward(rows, grad_branch, blocks, units, slopes):
    length, width = rows.shape
    up_count = blocks.shape[0] // 2
    split, resident, up, down, hidden, bias = mlp_specs(length, width, up_count)
    hidden_size = up_count * width
    return pl.pallas_call(
        mlp_backward_kernel,
        grid=(up_count * split,),
        out_shape=(
            jax.ShapeDtypeStruct((up_count, width, width), jnp.float32),
            jax.ShapeDtypeStruct((up_count, width, width), jnp.float32),
            jax.ShapeDtypeStruct((1, hidden_size), jnp.float32),
            jax.ShapeDtypeStruct((length, width), jnp.float32),
        ),
        in_specs=[resident, resident, up, down, hidden, hidden],
        out_specs=(
            pl.BlockSpec((None, width, HIDDEN_TILE), lambda t: (t // split, 0, t % split)),
            pl.BlockSpec((None, HIDDEN_TILE, width), lambda t: (t // split, t % split, 0)),
            bias,
            resident,
        ),
        scratch_shapes=[pltpu.VMEM((length, HIDDEN_TILE), jnp.bfloat16)],
        compiler_params=pltpu.CompilerParams(vmem_limit_bytes=48 << 20),
        name="mlp_backward",
    )(rows, grad_branch, blocks, blocks, units, slopes)


def layer_forward(blocks, vec_all, patch, attend):
    embedded = jnp.dot(patch, blocks[0], preferred_element_type=jnp.float32) + vec_all[0]
    normed_one = norm_rows(embedded, vec_all[1], vec_all[2]).astype(jnp.bfloat16)
    qkv_rows = jnp.einsum(
        "td,kde->kte", normed_one, blocks[1:4], preferred_element_type=jnp.float32
    )
    qkv_bias = jnp.stack([vec_all[3], jnp.zeros_like(vec_all[3]), vec_all[4]])
    qkv_rows = (qkv_rows + qkv_bias[:, None, :]).astype(jnp.bfloat16)
    attended, mlp_blocks = attend(qkv_rows)
    up_count = mlp_blocks.shape[0] // 2
    hidden = (
        embedded + jnp.dot(attended, blocks[4], preferred_element_type=jnp.float32) + vec_all[5]
    )
    normed_two = norm_rows(hidden, vec_all[6], vec_all[7]).astype(jnp.bfloat16)
    units, slopes, branch = mlp_forward(normed_two, mlp_blocks, vec_all[8 : 8 + up_count])
    output = hidden + branch + vec_all[8 + up_count]
    return (
        output,
        mlp_blocks,
        (embedded, normed_one, qkv_rows, attended, hidden, normed_two, slopes, units),
    )


def layer_backward(
    blocks,
    mlp_blocks,
    vec_all,
    patch,
    saved,
    pack_ids,
    key_codes,
    grad_output,
    grad_gain,
    grad_shift,
    released,
):
    embedded, normed_one, qkv_rows, attended, hidden, normed_two, slopes, units = saved
    feature_dim = patch.shape[1]
    up_count = mlp_blocks.shape[0] // 2
    grad_branch = grad_output.astype(jnp.bfloat16)
    grad_up, grad_down, up_sums, grad_normed_two = mlp_backward(
        normed_two, grad_branch, mlp_blocks, units, slopes
    )
    up_sums, released = lax.optimization_barrier((up_sums, released))
    norm_two_back = jax.vjp(norm_rows, hidden, vec_all[6], vec_all[7])[1]
    grad_hidden_norm, grad_gain_two, grad_shift_two = norm_two_back(grad_normed_two)
    grad_hidden = grad_output + grad_hidden_norm
    grad_attn_out = grad_hidden.astype(jnp.bfloat16)
    grad_attended = jnp.einsum(
        "td,ed->te", grad_attn_out, blocks[4], preferred_element_type=jnp.float32
    ).astype(jnp.bfloat16)
    grad_qkv = attention_backward(qkv_rows, pack_ids, key_codes, grad_attended)
    grad_normed_one = jnp.einsum(
        "kte,kde->td", grad_qkv, blocks[1:4], preferred_element_type=jnp.float32
    )
    norm_one_back = jax.vjp(norm_rows, embedded, vec_all[1], vec_all[2])[1]
    grad_embed_norm, grad_gain_one, grad_shift_one = norm_one_back(grad_normed_one)
    grad_embedded = (grad_hidden + grad_embed_norm).astype(jnp.bfloat16)
    lefts = (patch, normed_one, attended)
    rights = (grad_embedded, grad_qkv, grad_attn_out)
    bias_sums = jnp.stack(
        [
            jnp.sum(grad_embedded.astype(jnp.float32), 0),
            grad_gain_one,
            grad_shift_one,
            jnp.sum(grad_qkv[0].astype(jnp.float32), 0),
            jnp.sum(grad_qkv[2].astype(jnp.float32), 0),
            jnp.sum(grad_attn_out.astype(jnp.float32), 0),
            grad_gain_two,
            grad_shift_two,
        ]
    )
    up_sums = up_sums.reshape(up_count, feature_dim)
    tail_sums = jnp.stack([jnp.sum(grad_branch.astype(jnp.float32), 0), grad_gain, grad_shift])
    grad_vectors = jnp.concatenate([bias_sums, up_sums, tail_sums], 0)
    return (lefts, rights, (grad_up, grad_down), grad_vectors, released)


def torus_place():
    dp, cls = lax.axis_index("dp"), lax.axis_index("cls")
    return dp // 2, dp % 2, cls // 2, cls % 2


def torus_device(z, y, x, core):
    return (z * 2 + y, x * 2 + core)


def encode(pieces, code_refs, scale_ref):
    top = None
    for piece in pieces:
        peak = jnp.max(jnp.abs(piece()), 0, keepdims=True)
        top = peak if top is None else jnp.maximum(top, peak)
    top = jnp.maximum(top, CODE_FLOOR)
    inverse = CODE_TOP / top
    for piece, code_ref in zip(pieces, code_refs):
        code_ref[...] = jnp.round(piece() * inverse).astype(jnp.int32).astype(jnp.int16)
    scale_ref[...] = top * (1.0 / CODE_TOP)


def decode(code, scale):
    return code.astype(jnp.int32).astype(jnp.float32) * scale


def reduce_kernel(counts, *refs):
    sources, refs = refs[: len(counts)], refs[len(counts) :]
    (patch_hbm, first_hbm, mid_hbm, dpatch_hbm, dfirst_hbm, dmid_hbm,
     vec_ref, tail_ref, left_hbm, right_hbm,
     own_hbm, left_out_hbm, right_out_hbm, step_hbm, wide_ref, facts_ref, vec_out_ref,
     left_buf, right_buf, right_full, outs_buf, squares, high_buf, low_buf, sum_slots, tail_slots,
     lhs_buf, rhs_buf, pair_sem,
     in_sem, sum_send, sum_recv, tail_send, tail_recv,
     acc, spare, kept, sent0, got0, sent1, got1, sent2, got2, sent3, got3, sent4, got4,
     ss0, gs0, ss1, gs1, ss2, gs2, ss3, gs3, ss4, gs4, codes, scales, vec_got,
     load_sem, out_sem, send_sem, recv_sem, send_scale_sem, recv_scale_sem,
     vec_send_sem, vec_recv_sem) = refs
    stored = sum(counts)
    paired = dfirst_hbm.shape[0] + 2
    total = stored + paired
    half, width = codes.shape[1], codes.shape[2]
    cols = width // 2
    z, y, x, core = torus_place()
    upper = z // 2
    inner = (z % 2) != upper
    mate_core = torus_device(z, y, x, 1 - core)
    mate_x = torus_device(z, y, 1 - x, core)
    mate_y = torus_device(z, 1 - y, x, core)
    mate_z = torus_device(z + 1 - 2 * (z % 2), y, x, core)
    mate_mid = torus_device(3 - z, y, x, core)
    mate_far = torus_device((z + 2) % 4, y, x, core)

    barrier = pltpu.get_barrier_semaphore()
    dp, cls = lax.axis_index("dp"), lax.axis_index("cls")
    everyone = tail_slots.shape[0]
    quarter = sum_slots.shape[0]
    me = dp * 4 + cls

    def any_mate(n):
        other = lax.rem(me + n, everyone)
        return (other // 4, lax.rem(other, 4))

    def half_mate(n):
        return (upper * quarter + lax.rem(dp + n, quarter), cls)

    for n in range(1, everyone):
        pl.semaphore_signal(barrier, inc=1, device_id=any_mate(n), device_id_type=MESH)
    pl.semaphore_wait(barrier, everyone - 1)
    own = lax.rem(dp, quarter) * left_buf.shape[1]

    own_cols = pl.ds(pl.multiple_of(core * cols, 128), cols)
    other_cols = pl.ds(pl.multiple_of((1 - core) * cols, 128), cols)

    def rows_at(start, size):
        return pl.ds(pl.multiple_of(start, PIECE), size)

    def loads(m, body):
        start = 0
        for source, count in zip(sources, counts):
            def one(source=source, start=start):
                pair = (
                    pltpu.make_async_copy(
                        source.at[m - start, :, own_cols], acc.at[m % 5], load_sem.at[m % 2, 0]
                    ),
                    pltpu.make_async_copy(
                        source.at[m - start, :, other_cols], spare.at[m % 2], load_sem.at[m % 2, 1]
                    ),
                )
                for copy in pair:
                    body(copy)

            pl.when((m >= start) & (m < start + count))(one)
            start += count

    def block_of(m):
        return lax.rem(m + paired, total)

    def pair_loads(m, body):
        index = m - stored
        last = paired - 1

        def run(left, right):
            body(pltpu.make_async_copy(left, lhs_buf.at[m % 2], pair_sem.at[m % 2, 0]))
            body(pltpu.make_async_copy(right, rhs_buf.at[m % 2], pair_sem.at[m % 2, 1]))

        pl.when(index == 0)(lambda: run(patch_hbm, dpatch_hbm))
        pl.when((index > 0) & (index < last))(
            lambda: run(first_hbm, dfirst_hbm.at[jnp.clip(index - 1, 0, last - 2)])
        )
        pl.when(index == last)(lambda: run(mid_hbm, dmid_hbm))

    def pair_product(m):
        chunk = 2 * FEATURE_TILE
        for r in range(0, width, chunk):
            left = lhs_buf[m % 2, :, r : r + chunk].T
            for target, columns in ((acc.at[m % 5], own_cols), (spare.at[m % 2], other_cols)):
                target[r : r + chunk, :] = jnp.dot(
                    left, rhs_buf[m % 2, :, columns], preferred_element_type=jnp.float32
                )

    def message(stage, m, source, scale_source, target, scale_target, mate):
        return (
            pltpu.make_async_remote_copy(
                src_ref=source, dst_ref=target,
                send_sem=send_sem.at[stage, m % 2], recv_sem=recv_sem.at[stage, m],
                device_id=mate, device_id_type=MESH,
            ),
            pltpu.make_async_remote_copy(
                src_ref=scale_source, dst_ref=scale_target,
                send_sem=send_scale_sem.at[stage, m % 2], recv_sem=recv_scale_sem.at[stage, m],
                device_id=mate, device_id_type=MESH,
            ),
        )

    def first(m):
        return message(0, m, sent0.at[m % 2], ss0.at[m % 2], got0.at[m], gs0.at[m], mate_core)

    def second(m, b):
        return message(
            1 + b, m, sent1.at[m % 2, b], ss1.at[m % 2, b], got1.at[m, b], gs1.at[m, b],
            mate_y if b else mate_x,
        )

    def third(m, b):
        return message(
            3 + b, m, sent2.at[m % 2, b], ss2.at[m % 2, b], got2.at[m, b], gs2.at[m, b],
            mate_x if b else mate_y,
        )

    def fourth(m):
        return message(5, m, sent3.at[m % 2], ss3.at[m % 2], got3.at[m], gs3.at[m], mate_z)

    def fifth(m):
        return message(6, m, sent4.at[m % 2], ss4.at[m % 2], got4.at[m], gs4.at[m], mate_mid)

    piece_a = 2 * x + y
    piece_b = 4 + 2 * y + x

    def spread(stage, m, piece, count, mate, columns=own_cols):
        rows = pl.ds(pl.multiple_of(piece * PIECE, PIECE), count * PIECE)
        block = codes.at[m, rows, columns]
        scale = scales.at[m, pl.ds(piece, count), :, columns]
        return message(stage, m, block, scale, block, scale, mate)

    def start(copies):
        for copy in copies:
            copy.start()

    def wait_send(copies):
        for copy in copies:
            copy.wait_send()

    def wait_recv(copies):
        for copy in copies:
            copy.wait_recv()

    def vec_copy(step, mate):
        return pltpu.make_async_remote_copy(
            src_ref=vec_got.at[step, 0], dst_ref=vec_got.at[step, 1],
            send_sem=vec_send_sem.at[step], recv_sem=vec_recv_sem.at[step],
            device_id=mate, device_id_type=MESH,
        )

    vec_mates = (mate_core, mate_x, mate_y, mate_z, mate_far)

    loads(jnp.int32(0), lambda copy: copy.start())
    vec_got[0, 0] = vec_ref[...]
    vec_copy(0, vec_mates[0]).start()

    def step(t, carry):
        for n in range(1, 6):
            @pl.when(t == n)
            def _(n=n):
                vec_copy(n - 1, vec_mates[n - 1]).wait()
                value = vec_got[n - 1, 0] + vec_got[n - 1, 1]
                if n < 5:
                    vec_got[n, 0] = value
                    vec_copy(n, vec_mates[n]).start()
                else:
                    vec_out_ref[...] = value

        @pl.when(t < total)
        def _():
            m = t

            @pl.when(m < stored)
            def _():
                loads(m, lambda copy: copy.wait())

            @pl.when(m + 1 < stored)
            def _():
                loads(m + 1, lambda copy: copy.start())

            @pl.when((m + 1 >= stored) & (m + 1 < total))
            def _():
                pair_loads(m + 1, lambda copy: copy.start())

            @pl.when(m >= stored)
            def _():
                pair_loads(m, lambda copy: copy.wait())
                pair_product(m)

            span = 2 * PIECE
            encode(
                [lambda r=r: spare[m % 2, r : r + span, :] for r in range(0, 2 * half, span)],
                [sent0.at[m % 2, r : r + span, :] for r in range(0, 2 * half, span)],
                ss0.at[m % 2],
            )
            start(first(m))

        @pl.when((t >= 1) & (t < total + 1))
        def _():
            m = t - 1
            copies = first(m)
            wait_send(copies)
            wait_recv(copies)
            slot = m % 5
            span = 2 * PIECE
            for r in range(0, 2 * half, span):
                acc[slot, r : r + span, :] += decode(got0[m, r : r + span, :], gs0[m])
            for b in range(2):
                other = (1 - y) if b else (1 - x)
                begins = [h * half + b * 4 * PIECE + other * span for h in range(2)]
                encode(
                    [lambda s=s: acc[slot, rows_at(s, span), :] for s in begins],
                    [sent1.at[m % 2, b, h] for h in range(2)],
                    ss1.at[m % 2, b],
                )
                start(second(m, b))

        @pl.when((t >= 2) & (t < total + 2))
        def _():
            m = t - 2
            slot = m % 5
            span = 2 * PIECE
            for b in range(2):
                copies = second(m, b)
                wait_send(copies)
                wait_recv(copies)
                mine = y if b else x
                other = (1 - x) if b else (1 - y)
                begins = [h * half + b * 4 * PIECE + mine * span for h in range(2)]
                for h, s in enumerate(begins):
                    acc[slot, rows_at(s, span), :] += decode(got1[m, b, h], gs1[m, b])
                encode(
                    [lambda s=s: acc[slot, rows_at(s + other * PIECE, PIECE), :] for s in begins],
                    [sent2.at[m % 2, b, h] for h in range(2)],
                    ss2.at[m % 2, b],
                )
                start(third(m, b))

        @pl.when((t >= 3) & (t < total + 3))
        def _():
            m = t - 3
            slot = m % 5
            for b in range(2):
                copies = third(m, b)
                wait_send(copies)
                wait_recv(copies)
                place = piece_b if b else piece_a
                for h in range(2):
                    kept[m % 3, h, b] = acc[
                        slot, rows_at(h * half + place * PIECE, PIECE), :
                    ] + decode(got2[m, b, h], gs2[m, b])

            @pl.when(jnp.logical_not(inner))
            def _():
                pairs = [(h, b) for h in range(2) for b in range(2)]
                encode(
                    [lambda h=h, b=b: kept[m % 3, h, b] for h, b in pairs],
                    [sent3.at[m % 2, h, b] for h, b in pairs],
                    ss3.at[m % 2],
                )
                start(fourth(m))

        @pl.when((t >= 4) & (t < total + 4))
        def _():
            m = t - 4
            copies = fourth(m)

            @pl.when(jnp.logical_not(inner))
            def _():
                wait_send(copies)

            @pl.when(inner)
            def _():
                wait_recv(copies)
                for h in range(2):
                    for b in range(2):
                        kept[m % 3, h, b] += decode(got3[m, h, b], gs3[m])
                encode(
                    [lambda b=b: kept[m % 3, 1 - upper, b] for b in range(2)],
                    [sent4.at[m % 2, b] for b in range(2)],
                    ss4.at[m % 2],
                )
                start(fifth(m))

        @pl.when((t >= 5) & (t < total + 5))
        def _():
            m = t - 5

            @pl.when(inner)
            def _():
                copies = fifth(m)
                wait_send(copies)
                wait_recv(copies)
                for b in range(2):
                    place = piece_b if b else piece_a
                    value = kept[m % 3, upper, b] + decode(got4[m, b], gs4[m])
                    encode(
                        [lambda value=value: value],
                        [codes.at[m, rows_at(place * PIECE, PIECE), own_cols]],
                        scales.at[m, place, :, own_cols],
                    )
                    start(spread(7 + b, m, place, 1, mate_z))

        @pl.when((t >= 6) & (t < total + 6))
        def _():
            m = t - 6
            for b in range(2):
                place = piece_b if b else piece_a
                copies = spread(7 + b, m, place, 1, mate_z)

                @pl.when(inner)
                def _(copies=copies):
                    wait_send(copies)

                @pl.when(jnp.logical_not(inner))
                def _(copies=copies):
                    wait_recv(copies)

                start(spread(9 + b, m, place, 1, mate_x if b else mate_y))

        @pl.when((t >= 7) & (t < total + 7))
        def _():
            m = t - 7
            for b in range(2):
                place = piece_b if b else piece_a
                theirs = (4 + 2 * y + 1 - x) if b else (2 * x + 1 - y)
                wait_send(spread(9 + b, m, place, 1, mate_x if b else mate_y))
                wait_recv(spread(9 + b, m, theirs, 1, mate_x if b else mate_y))
                begin = (4 + 2 * y) if b else 2 * x
                start(spread(11 + b, m, begin, 2, mate_y if b else mate_x))

        @pl.when((t >= 8) & (t < total + 8))
        def _():
            m = t - 8
            for b in range(2):
                begin = (4 + 2 * y) if b else 2 * x
                theirs = (4 + 2 * (1 - y)) if b else 2 * (1 - x)
                wait_send(spread(11 + b, m, begin, 2, mate_y if b else mate_x))
                wait_recv(spread(11 + b, m, theirs, 2, mate_y if b else mate_x))
            start(spread(13, m, 0, 8, mate_core))

        def ins(m):
            return (
                pltpu.make_async_copy(
                    left_hbm.at[block_of(m)], left_buf.at[m % 2], in_sem.at[m % 2, 0]
                ),
                pltpu.make_async_copy(
                    right_hbm.at[:, block_of(m)], right_buf.at[m % 2], in_sem.at[m % 2, 1]
                ),
            )

        def outs(m):
            targets = (own_hbm, left_out_hbm, right_out_hbm, step_hbm)
            return [
                pltpu.make_async_copy(
                    outs_buf.at[m % 2, n], target.at[block_of(m)], out_sem.at[m % 2, n]
                )
                for n, target in enumerate(targets)
            ]

        @pl.when((t >= 8) & (t < total + 8))
        def _():
            start(ins(t - 8))

        @pl.when((t >= 11) & (t < total + 11))
        def _():
            for copy in outs(t - 11):
                copy.wait()

        @pl.when((t >= 9) & (t < total + 9))
        def _():
            m = t - 9
            wait_send(spread(13, m, 0, 8, mate_core))
            wait_recv(spread(13, m, 0, 8, mate_core, other_cols))
            for copy in ins(m):
                copy.wait()
            precondition_block(
                own, codes.at[m], scales.at[m], left_buf.at[m % 2], right_buf.at[m % 2],
                outs_buf.at[m % 2], squares.at[m], high_buf, low_buf, right_full,
            )
            start(outs(m))

        return carry

    lax.fori_loop(0, total + 11, step, 0)

    def folded(row):
        return sum(row[:, n * 128 : (n + 1) * 128] for n in range(row.shape[1] // 128))

    layer = jnp.zeros((1, 128), jnp.float32)
    mine = lax.rem(dp, quarter)
    sum_slots[mine] = jnp.zeros(sum_slots.shape[1:], jnp.float32)
    for m in range(total):
        layer = layer + folded(squares[m, 0:1, :])
        for quad in range(2):
            part = squares[m, 1:2, quad * cols : (quad + 1) * cols]
            row = 2 * ((m + paired) % total) + quad
            sum_slots[mine, row : row + 1, :] = folded(part)
    once = (cls == 0).astype(jnp.float32)
    first_row = lax.broadcasted_iota(jnp.int32, tail_ref.shape, 0) == 0
    tail_slots[me] = tail_ref[...] + jnp.where(first_row, once * layer, 0.0)

    def sum_copy(n, slot):
        return pltpu.make_async_remote_copy(
            src_ref=sum_slots.at[slot], dst_ref=sum_slots.at[slot],
            send_sem=sum_send.at[n], recv_sem=sum_recv.at[slot],
            device_id=half_mate(n), device_id_type=MESH,
        )

    def tail_copy(n, slot):
        return pltpu.make_async_remote_copy(
            src_ref=tail_slots.at[slot], dst_ref=tail_slots.at[slot],
            send_sem=tail_send.at[n], recv_sem=tail_recv.at[slot],
            device_id=any_mate(n), device_id_type=MESH,
        )

    for n in range(1, quarter):
        sum_copy(n, lax.rem(dp, quarter)).start()
    for n in range(1, everyone):
        tail_copy(n, me).start()
    for n in range(1, quarter):
        sum_copy(n, lax.rem(dp, quarter)).wait_send()
        sum_copy(n, lax.rem(dp + n, quarter)).wait_recv()
    for n in range(1, everyone):
        tail_copy(n, me).wait_send()
        tail_copy(n, lax.rem(me + n, everyone)).wait_recv()
    value = sum_slots[0]
    for n in range(1, quarter):
        value = value + sum_slots[n]
    tail = tail_slots[0]
    for n in range(1, everyone):
        tail = tail + tail_slots[n]
    vec = vec_out_ref[...]
    vec_squares = jnp.sum(jnp.sum(vec * vec, 0, keepdims=True), 1, keepdims=True)
    norm = jnp.sqrt(jnp.sum(tail[0:1], 1, keepdims=True) + vec_squares)
    factor = CLIP_NORM / jnp.maximum(norm, CLIP_NORM)
    mean_squares = jnp.sum(value, 1, keepdims=True) / (half * cols) * factor * factor
    scale = SHAMPOO_RATE * factor * lax.rsqrt(mean_squares + ROOT_EPS)
    for b in range(total):
        for quad in range(2):
            row = 2 * b + quad
            wide_ref[b, :, quad * cols : (quad + 1) * cols] = jnp.broadcast_to(
                scale[row : row + 1], (1, cols)
            )
    rows = lax.broadcasted_iota(jnp.int32, facts_ref.shape, 0)
    loss = jnp.sum(tail[1:2], 1, keepdims=True)
    facts_ref[...] = jnp.where(rows == 0, loss, jnp.where(rows == 1, norm, factor))


def reduce_gradients(
    arrays, lefts, rights, vec_sums, tail, root_left, right_codes, dp_count, cls_count
):
    counts = tuple(array.shape[0] for array in arrays)
    total, rows, width = root_left.shape
    length = lefts[0].shape[0]
    parts, coded_rows = right_codes.shape[0], right_codes.shape[2]
    half, cols = width // 2, width // 2
    sum_rows = 2 * total + -2 * total % 8
    f32, i16 = jnp.float32, jnp.int16

    def pair(*shape):
        return [pltpu.VMEM((2,) + shape, i16), pltpu.VMEM((total,) + shape, i16)]

    def scale_pair(*shape):
        return [
            pltpu.VMEM((2,) + shape + (1, cols), f32),
            pltpu.VMEM((total,) + shape + (1, cols), f32),
        ]

    hbm = pl.BlockSpec(memory_space=pl.ANY)
    vmem = pl.BlockSpec(memory_space=pltpu.VMEM)
    return pl.pallas_call(
        functools.partial(reduce_kernel, counts),
        out_shape=(jax.ShapeDtypeStruct((total, rows, width), f32),) * 4
        + (
            jax.ShapeDtypeStruct((total, 1, width), f32),
            jax.ShapeDtypeStruct(tail.shape, f32),
            jax.ShapeDtypeStruct(vec_sums.shape, f32),
        ),
        in_specs=[hbm] * (len(arrays) + 6) + [vmem, vmem, hbm, hbm],
        out_specs=(hbm,) * 4 + (vmem,) * 3,
        scratch_shapes=[
            pltpu.VMEM((2, rows, width), f32),
            pltpu.VMEM((2, parts, coded_rows, width), jnp.int32),
            pltpu.VMEM((half, width), f32),
            pltpu.VMEM((2, 4, rows, width), f32),
            pltpu.VMEM((total, 2, width), f32),
            pltpu.VMEM((half, width), jnp.bfloat16),
            pltpu.VMEM((half, width), jnp.bfloat16),
            pltpu.VMEM((dp_count // 2, sum_rows, 128), f32),
            pltpu.VMEM((dp_count * cls_count,) + tail.shape, f32),
            pltpu.VMEM((2, length, width), jnp.bfloat16),
            pltpu.VMEM((2, length, width), jnp.bfloat16),
            pltpu.SemaphoreType.DMA((2, 2)),
            pltpu.SemaphoreType.DMA((2, 2)),
            pltpu.SemaphoreType.DMA((dp_count // 2,)),
            pltpu.SemaphoreType.DMA((dp_count // 2,)),
            pltpu.SemaphoreType.DMA((dp_count * cls_count,)),
            pltpu.SemaphoreType.DMA((dp_count * cls_count,)),
            pltpu.VMEM((5, width, cols), f32),
            pltpu.VMEM((2, width, cols), f32),
            pltpu.VMEM((3, 2, 2, PIECE, cols), f32),
        ]
        + pair(width, cols)
        + pair(2, 2, 2 * PIECE, cols)
        + pair(2, 2, PIECE, cols)
        + pair(2, 2, PIECE, cols)
        + pair(2, PIECE, cols)
        + scale_pair()
        + scale_pair(2)
        + scale_pair(2)
        + scale_pair()
        + scale_pair()
        + [
            pltpu.VMEM((total, half, width), i16),
            pltpu.VMEM((total, half // PIECE, 1, width), f32),
            pltpu.VMEM((5, 2) + vec_sums.shape, f32),
            pltpu.SemaphoreType.DMA((2, 2)),
            pltpu.SemaphoreType.DMA((2, 4)),
            pltpu.SemaphoreType.DMA((14, 2)),
            pltpu.SemaphoreType.DMA((14, total)),
            pltpu.SemaphoreType.DMA((14, 2)),
            pltpu.SemaphoreType.DMA((14, total)),
            pltpu.SemaphoreType.DMA((5,)),
            pltpu.SemaphoreType.DMA((5,)),
        ],
        compiler_params=pltpu.CompilerParams(
            collective_id=1, has_side_effects=True, vmem_limit_bytes=60 << 20
        ),
        name="reduce_gradients",
    )(*arrays, *lefts, *rights, vec_sums, tail, root_left, right_codes)


def split_float(values):
    high = values.astype(jnp.bfloat16)
    return high, (values - high.astype(jnp.float32)).astype(jnp.bfloat16)


def stacked_dot(lefts, right, contract_last):
    rows = lefts[0].shape[0]
    left = jnp.concatenate(lefts, 0) if len(lefts) > 1 else lefts[0]
    dims = (((1,), (1 if contract_last else 0,)), ((), ()))
    out = lax.dot_general(left, right, dims, preferred_element_type=jnp.float32)
    return [out[n * rows : (n + 1) * rows] for n in range(len(lefts))]


def encode_roots(part):
    top = jnp.max(jnp.abs(part), 1, keepdims=True)
    level = jnp.ceil(jnp.log2(jnp.maximum(top, 1e-30)))
    codes = jnp.round(part * jnp.exp2(15.0 - level))
    codes = jnp.clip(codes, -32767.0, 32767.0).astype(jnp.int32)
    levels = jnp.broadcast_to(level.astype(jnp.int32), (part.shape[0], 8, part.shape[2]))
    upper = jnp.concatenate([codes[:, 0:8], codes[:, 16:24]], 1)
    lower = jnp.concatenate([codes[:, 8:16], levels], 1)
    return upper * 65536 + (lower + 32768)


def precondition_block(
    own, codes_ref, scales_ref, left_ref, right_codes, outs_ref, squares_ref, high_ref, low_ref,
    right_ref
):
    half, width = codes_ref.shape
    rows = left_ref.shape[0]
    own_rows = pl.ds(pl.multiple_of(own, PIECE), rows)
    parts = right_codes.shape[0]
    size = half // parts
    for n in range(parts):
        packed = right_codes[n]
        upper = lax.shift_right_arithmetic(packed, jnp.full_like(packed, 16)).astype(jnp.float32)
        lower = ((packed & 65535) - 32768).astype(jnp.float32)
        scale = jnp.exp2(lower[8:9] - 15.0)
        right_ref[n * size : n * size + 8, :] = upper[0:8] * scale
        right_ref[n * size + 8 : n * size + 16, :] = lower[0:8] * scale
        right_ref[n * size + 16 : n * size + 24, :] = upper[8:16] * scale
    for piece in range(half // PIECE):
        part = slice(piece * PIECE, (piece + 1) * PIECE)
        high_ref[part, :], low_ref[part, :] = split_float(
            decode(codes_ref[part, :], scales_ref[piece])
        )
    own_value = high_ref[own_rows, :].astype(jnp.float32) + low_ref[own_rows, :].astype(jnp.float32)
    outs_ref[0] = own_value
    squares_ref[0:1, :] = jnp.sum(own_value * own_value, 0, keepdims=True)
    picks = (
        lax.broadcasted_iota(jnp.int32, (rows, half), 1)
        == lax.broadcasted_iota(jnp.int32, (rows, half), 0) + own
    ).astype(jnp.float32).astype(jnp.bfloat16)
    for quad in range(2):
        cols = slice(quad * half, (quad + 1) * half)
        high, low = high_ref[:, cols], low_ref[:, cols]
        mine_high, mine_low = high_ref[own_rows, cols], low_ref[own_rows, cols]
        hh, lh, turned_high = stacked_dot([mine_high, mine_low, picks], high, True)
        hl, turned_low = stacked_dot([mine_high, picks], low, True)
        outs_ref[1, :, cols] = hh + (lh + hl)
        turned_high = turned_high.astype(jnp.bfloat16)
        turned_low = turned_low.astype(jnp.bfloat16)
        root_high, root_low = split_float(left_ref[:, cols])
        thh, tlh, rhh, rlh = stacked_dot([turned_high, turned_low, root_high, root_low], high, False)
        thl, rhl = stacked_dot([turned_high, root_high], low, False)
        outs_ref[2, :, cols] = thh + (tlh + thl)
        half_step = rhh + (rlh + rhl)
        step_high, step_low = split_float(half_step)
        right_high, right_low = split_float(right_ref[:, cols])
        shh, slh = stacked_dot([step_high, step_low], right_high, False)
        (shl,) = stacked_dot([step_high], right_low, False)
        direction = shh + (slh + shl)
        outs_ref[3, :, cols] = direction
        squares_ref[1:2, cols] = jnp.sum(direction * direction, 0, keepdims=True)


def head_kernel(
    image_total, pooled_ref, labels_ref, head_hbm,
    grad_ref, rows_ref, loss_ref,
    head_buf, group_buf, total_buf, slots, load_sem, send_sem, recv_sem, sum_send, sum_recv
):
    dp, cls = lax.axis_index("dp"), lax.axis_index("cls")
    count, rows, width = slots.shape
    images = count * rows
    classes = head_buf.shape[1]
    load = pltpu.make_async_copy(head_hbm, head_buf, load_sem)
    load.start()
    barrier = pltpu.get_barrier_semaphore()
    for n in range(1, count):
        pl.semaphore_signal(
            barrier, inc=1, device_id=(dp, lax.rem(cls + n, count)), device_id_type=MESH
        )
    pl.semaphore_wait(barrier, count - 1)

    def part(ref, index):
        return ref.at[pl.ds(pl.multiple_of(index * rows, 8), rows)]

    def share(n, slot):
        return pltpu.make_async_remote_copy(
            src_ref=pooled_ref, dst_ref=part(group_buf, slot),
            send_sem=send_sem.at[n], recv_sem=recv_sem.at[slot],
            device_id=(dp, lax.rem(cls + n, count)), device_id_type=MESH,
        )

    for n in range(1, count):
        share(n, cls).start()
    part(group_buf, cls)[...] = pooled_ref[...]
    rows_ref[:, width + classes :] = jnp.zeros(
        (images, rows_ref.shape[1] - width - classes), rows_ref.dtype
    )
    for n in range(1, count):
        share(n, cls).wait_send()
        share(n, lax.rem(cls + n, count)).wait_recv()
    load.wait()
    group = group_buf[...].astype(jnp.bfloat16)
    rows_ref[:, :width] = group
    loss = jnp.zeros((1, 1), jnp.float32)
    total = jnp.zeros((images, width), jnp.float32)
    for start in range(0, classes, CLASS_TILE):
        stop = min(classes, start + CLASS_TILE)
        weights = head_buf[:, start:stop]
        logits = jnp.dot(group, weights, preferred_element_type=jnp.float32)
        ids = lax.broadcasted_iota(jnp.int32, logits.shape, 1) + (cls * classes + start)
        target = ids == labels_ref[:, 0:1]
        for n in range(1, labels_ref.shape[1]):
            target = target | (ids == labels_ref[:, n : n + 1])
        target = target.astype(jnp.float32)
        valid = ids < LABELS_REAL
        shrunk = jnp.exp(-jnp.abs(logits))
        terms = jnp.maximum(logits, 0.0) + jnp.log1p(shrunk) - target * logits
        terms = jnp.where(valid, terms, 0.0)
        loss = loss + jnp.sum(jnp.sum(terms, 0, keepdims=True), 1, keepdims=True)
        chance = jnp.where(logits >= 0.0, 1.0, shrunk) / (1.0 + shrunk)
        grads = jnp.where(valid, chance - target, 0.0) / image_total
        grads = grads.astype(jnp.bfloat16)
        rows_ref[:, width + start : width + stop] = grads
        total = total + lax.dot_general(
            grads, weights, (((1,), (1,)), ((), ())), preferred_element_type=jnp.float32
        )
    loss_ref[...] = jnp.broadcast_to(loss / image_total, loss_ref.shape)
    total_buf[...] = total

    def back(n, slot):
        mate = lax.rem(cls + n, count)
        return pltpu.make_async_remote_copy(
            src_ref=part(total_buf, mate), dst_ref=slots.at[slot],
            send_sem=sum_send.at[n], recv_sem=sum_recv.at[slot],
            device_id=(dp, mate), device_id_type=MESH,
        )

    for n in range(1, count):
        back(n, cls).start()
    slots[cls] = part(total_buf, cls)[...]
    for n in range(1, count):
        back(n, cls).wait_send()
        back(n, lax.rem(cls + n, count)).wait_recv()
    value = slots[0]
    for n in range(1, count):
        value = value + slots[n]
    grad_ref[...] = value


def classify(pooled, labels, head_low, cls_count, image_total):
    rows, width = pooled.shape
    images, classes = rows * cls_count, head_low.shape[1]
    wide = width + classes
    wide = wide + -wide % 128
    f32 = jnp.float32
    vmem = pl.BlockSpec(memory_space=pltpu.VMEM)
    return pl.pallas_call(
        functools.partial(head_kernel, image_total),
        out_shape=(
            jax.ShapeDtypeStruct((rows, width), f32),
            jax.ShapeDtypeStruct((images, wide), jnp.bfloat16),
            jax.ShapeDtypeStruct((8, 128), f32),
        ),
        in_specs=[vmem, vmem, pl.BlockSpec(memory_space=pltpu.HBM)],
        out_specs=(vmem, vmem, vmem),
        scratch_shapes=[
            pltpu.VMEM((width, classes), jnp.bfloat16),
            pltpu.VMEM((images, width), f32),
            pltpu.VMEM((images, width), f32),
            pltpu.VMEM((cls_count, rows, width), f32),
            pltpu.SemaphoreType.DMA,
        ]
        + [pltpu.SemaphoreType.DMA((cls_count,)) for _ in range(4)],
        compiler_params=pltpu.CompilerParams(
            collective_id=2, has_side_effects=True, vmem_limit_bytes=60 << 20
        ),
        name="classify",
    )(pooled, labels, head_low)


def gather_steps(own_ref, out_ref, send_sem, recv_sem, copy_sem):
    count, rows, width = own_ref.shape
    cols = width // 2
    z, y, x, core = torus_place()
    mate_core = torus_device(z, y, x, 1 - core)
    mate_x = torus_device(z, y, 1 - x, core)
    mate_y = torus_device(z, 1 - y, x, core)
    own_cols = pl.ds(pl.multiple_of(core * cols, 128), cols)
    other_cols = pl.ds(pl.multiple_of((1 - core) * cols, 128), cols)
    spare = rows - SPAN
    held = x * spare
    lone = (x * SPAN, (1 - x) * SPAN)

    def share(m, zz, yy, start, size):
        begin = (zz * 2 + yy) * rows + start
        return out_ref.at[m, pl.ds(pl.multiple_of(begin, 16), size), own_cols]

    def copy(slot, arrival, m, source, target, mate):
        return pltpu.make_async_remote_copy(
            src_ref=source, dst_ref=target,
            send_sem=send_sem.at[slot, m % 2], recv_sem=recv_sem.at[arrival, m],
            device_id=mate, device_id_type=MESH,
        )

    def local(m):
        return pltpu.make_async_copy(
            own_ref.at[m, :, own_cols], share(m, z, y, 0, rows), copy_sem.at[m % 2]
        )

    def along(m, n, outgoing):
        other = lax.rem(z + n, 4)
        origin = z if outgoing else other
        source = own_ref.at[m, pl.ds(pl.multiple_of(held, 16), SPAN), own_cols]
        mate = torus_device(other, y, x, core)
        return copy(n - 1, origin, m, source, share(m, origin, y, held, SPAN), mate)

    def cross(m, n, outgoing):
        block = share(m, n, y if outgoing else 1 - y, held, SPAN)
        return copy(3 + n, 4 + n, m, block, block, mate_y)

    def patch(m, n, outgoing):
        index = lax.rem(z * 2 + y + n, SHARES)
        block = share(m, index // 2, lax.rem(index, 2), lone[0 if outgoing else 1], spare)
        return copy(6 + n, 7 + n, m, block, block, mate_x)

    def swap(m, columns):
        block = out_ref.at[m, :, columns]
        return copy(14, 15, m, block, block, mate_core)

    def finish(copies):
        for outgoing, incoming in copies:
            outgoing.wait_send()
            incoming.wait_recv()

    def step(t):
        @pl.when(t < count)
        def _():
            local(t).start()
            for n in range(1, 4):
                along(t, n, True).start()

        @pl.when((t >= 1) & (t < count + 1))
        def _():
            m = t - 1
            local(m).wait()
            finish([(along(m, n, True), along(m, n, False)) for n in range(1, 4)])
            for n in range(4):
                cross(m, n, True).start()

        @pl.when((t >= 2) & (t < count + 2))
        def _():
            m = t - 2
            finish([(cross(m, n, True), cross(m, n, False)) for n in range(4)])
            for n in range(1, SHARES):
                patch(m, n, True).start()

        @pl.when((t >= 3) & (t < count + 3))
        def _():
            m = t - 3
            finish([(patch(m, n, True), patch(m, n, False)) for n in range(1, SHARES)])
            swap(m, own_cols).start()

        @pl.when((t >= 4) & (t < count + 4))
        def _():
            m = t - 4
            swap(m, own_cols).wait_send()
            swap(m, other_cols).wait_recv()

    return step, count + GATHER_DEPTH


def column_mate(n):
    z, y, x, core = torus_place()
    other = lax.rem(z * 2 + y + n, SHARES)
    return torus_device(other // 2, lax.rem(other, 2), x, core)


def gather_barrier():
    z, y, x, core = torus_place()
    barrier = pltpu.get_barrier_semaphore()
    mates = [torus_device(z, y, x, 1 - core), torus_device(z, y, 1 - x, core)]
    for mate in mates + [column_mate(n) for n in range(1, SHARES)]:
        pl.semaphore_signal(barrier, inc=1, device_id=mate, device_id_type=MESH)
    pl.semaphore_wait(barrier, SHARES + 1)


def gather_kernel(
    own_ref, vec_ref, out_ref, vec_out_ref, send_sem, recv_sem, copy_sem, vec_send, vec_recv
):
    z, y, _, _ = torus_place()
    me = z * 2 + y
    gather_barrier()

    def vec_copy(n, slot):
        return pltpu.make_async_remote_copy(
            src_ref=vec_ref, dst_ref=vec_out_ref.at[slot],
            send_sem=vec_send.at[n], recv_sem=vec_recv.at[slot],
            device_id=column_mate(n), device_id_type=MESH,
        )

    for n in range(1, SHARES):
        vec_copy(n, me).start()
    vec_out_ref[me] = vec_ref[...]
    gather_step, turns = gather_steps(own_ref, out_ref, send_sem, recv_sem, copy_sem)

    def step(t, carry):
        gather_step(t)
        return carry

    lax.fori_loop(0, turns, step, 0)
    for n in range(1, SHARES):
        vec_copy(n, me).wait_send()
        vec_copy(n, lax.rem(me + n, SHARES)).wait_recv()


def gather_semaphores(count):
    return [
        pltpu.SemaphoreType.DMA((15, 2)),
        pltpu.SemaphoreType.DMA((16, count)),
        pltpu.SemaphoreType.DMA((2,)),
    ]


def attention_gather_kernel(
    qids_ref, kcodes_ref, q_ref, k_ref, v_ref, own_ref, out_ref, blocks_ref,
    bias_ref, send_sem, recv_sem, copy_sem
):
    pair, tiles = pl.program_id(0), q_ref.shape[0] // QTILE
    slots = pl.num_programs(0) * tiles

    @pl.when(pair == 0)
    def _():
        gather_barrier()

    gather_step, turns = gather_steps(own_ref, blocks_ref, send_sem, recv_sem, copy_sem)
    attention_bias(qids_ref, kcodes_ref, bias_ref)
    for tile in range(tiles):
        slot = pair * tiles + tile
        begin, end = slot * turns // slots, (slot + 1) * turns // slots

        @pl.when(begin < end)
        def _(begin=begin):
            gather_step(begin)

        attention_tile(tile, q_ref, k_ref, v_ref, out_ref, bias_ref)


def attention_forward_gathering(qkv_rows, pack_ids, key_codes, own):
    _, length, width = qkv_rows.shape
    count, rows, _ = own.shape
    tiles = length // QTILE
    assert count + GATHER_DEPTH <= tiles * (width // PAIR)
    return pl.pallas_call(
        attention_gather_kernel,
        grid=(width // PAIR,),
        out_shape=(
            jax.ShapeDtypeStruct((length, width), jnp.bfloat16),
            jax.ShapeDtypeStruct((count, SHARES * rows, width), own.dtype),
        ),
        in_specs=[whole_spec((length, 1)), whole_spec((1, length))]
        + [pair_spec(length, part) for part in range(3)]
        + [whole_spec(own.shape)],
        out_specs=(pair_spec(length), pl.BlockSpec(memory_space=pl.ANY)),
        scratch_shapes=[pltpu.VMEM(bias_shape(length), jnp.float32)] + gather_semaphores(count),
        compiler_params=pltpu.CompilerParams(
            collective_id=4, has_side_effects=True, vmem_limit_bytes=40 << 20
        ),
        name="attention_forward",
    )(pack_ids[:, None], key_codes[None, :], qkv_rows, qkv_rows, qkv_rows, own)


def gather_weights(own, vec):
    count, rows, width = own.shape
    hbm = pl.BlockSpec(memory_space=pl.ANY)
    vmem = pl.BlockSpec(memory_space=pltpu.VMEM)
    return pl.pallas_call(
        gather_kernel,
        out_shape=(
            jax.ShapeDtypeStruct((count, SHARES * rows, width), own.dtype),
            jax.ShapeDtypeStruct((SHARES,) + vec.shape, vec.dtype),
        ),
        in_specs=[vmem, vmem],
        out_specs=(hbm, vmem),
        scratch_shapes=gather_semaphores(count)
        + [pltpu.SemaphoreType.DMA((SHARES,)), pltpu.SemaphoreType.DMA((SHARES,))],
        compiler_params=pltpu.CompilerParams(
            collective_id=3, has_side_effects=True, vmem_limit_bytes=32 << 20
        ),
        name="gather_weights",
    )(own, vec)


def adam_step(weight, grad, first, second, count):
    first = BETA_FIRST * first + (1.0 - BETA_FIRST) * grad
    second = BETA_SECOND * second + (1.0 - BETA_SECOND) * grad * grad
    fix_first = 1.0 - jnp.power(BETA_FIRST, count)
    fix_second = 1.0 - jnp.power(BETA_SECOND, count)
    update = first / fix_first / (jnp.sqrt(second / fix_second) + ADAM_EPS) + WEIGHT_DECAY * weight
    return (weight - ADAM_RATE * update, first, second)


def split_halves(values, half_size):
    block_count, row_count, feature_dim = values.shape
    return values.reshape(block_count, row_count, 2, half_size)


def reduced_half(values, half_groups):
    part = lax.psum_scatter(values, ("dp", "cls"), scatter_dimension=1, tiled=True)
    return lax.all_gather(part, ("dp", "cls"), axis=1, tiled=True, axis_index_groups=half_groups)


def preconditioned_rows(grad_half, root_left, right_half, own_start):
    count, row_count, width = root_left.shape
    half_size = width // 2
    block_rows = lax.dynamic_slice_in_dim(grad_half, own_start, row_count, 1)
    grad_quads = split_halves(grad_half, half_size)
    rows_quads = split_halves(block_rows, half_size)
    cols_quads = lax.dynamic_slice_in_dim(grad_quads, own_start, row_count, 3)
    precise = FULL_PRECISION
    left_add = jnp.einsum("brjk,bljk->brjl", rows_quads, grad_quads, precision=precise)
    right_add = jnp.einsum("bkja,bkjm->bajm", cols_quads, grad_quads, precision=precise)
    direction = jnp.einsum(
        "brjk,bkjm->brjm", split_halves(root_left, half_size), grad_quads, precision=precise
    )
    direction = jnp.einsum(
        "brjk,bkjm->brjm", direction, split_halves(right_half, half_size), precision=precise
    )
    flat = (count, row_count, width)
    return left_add.reshape(flat), right_add.reshape(flat), direction.reshape(flat), block_rows


def on_device(
    patches,
    image_ids,
    keep,
    labels,
    owner,
    step,
    enc_weights,
    stats_left,
    stats_right,
    root_left,
    root_right,
    head_weights,
    head_m,
    head_v,
    vectors,
    vec_m,
    vec_v,
):
    dp_count = lax.axis_size("dp")
    cls_count = lax.axis_size("cls")
    dp_index = lax.axis_index("dp")
    cls_index = lax.axis_index("cls")
    block_count, row_count, feature_dim = enc_weights.shape
    up_count = (block_count - 5) // 2
    half_size = feature_dim // 2
    part_rows = row_count // cls_count
    half_dp = dp_count // 2
    half_group = half_dp * cls_count
    half_groups = [
        list(range(half_group)),
        list(range(half_group, 2 * half_group)),
    ]

    def my_part(values):
        return lax.dynamic_slice_in_dim(values, cls_index * part_rows, part_rows, 1)

    on_torus = dp_count == 8 and cls_count == 4
    if on_torus:
        vec_block = jnp.pad(vectors, ((0, -vectors.shape[0] % 8), (0, -row_count % 128)))
        own_low = enc_weights.astype(jnp.bfloat16)
        blocks, vec_blocks = gather_weights(own_low[:5], vec_block)
        right_part, vec_blocks = lax.optimization_barrier((my_part(root_right), vec_blocks))
        vec_low = jnp.transpose(vec_blocks[:, : vectors.shape[0], :row_count], (1, 0, 2))
        vec_all = lax.reduce_precision(vec_low.reshape(vectors.shape[0], feature_dim), 8, 7)
    else:
        right_part = my_part(root_right)
        all_blocks = lax.all_gather(
            my_part(enc_weights.astype(jnp.bfloat16)), ("dp", "cls"), axis=1, tiled=True
        )
        blocks = all_blocks[:5]
        vec_low = lax.all_gather(vectors.astype(jnp.bfloat16), "dp", axis=1, tiled=True)
        vec_all = vec_low.astype(jnp.float32)
    head_low = lax.all_gather(head_weights.astype(jnp.bfloat16), "dp", axis=0, tiled=True)
    final_gain = vec_all[9 + up_count]
    final_shift = vec_all[10 + up_count]
    pack_ids, pack_keep = image_ids[0], keep[0]
    key_codes = jnp.where(pack_keep == 1, pack_ids, -1)

    def attend(qkv_rows):
        if on_torus:
            return attention_forward_gathering(qkv_rows, pack_ids, key_codes, own_low[5:])
        return attention_forward(qkv_rows, pack_ids, key_codes), all_blocks[5:]

    output, mlp_blocks, saved = layer_forward(blocks, vec_all, patches, attend)
    if on_torus:
        right_codes = lax.all_gather(
            encode_roots(right_part), ("dp", "cls"), axis=0, axis_index_groups=half_groups
        )
    else:
        right_half = lax.all_gather(
            right_part, ("dp", "cls"), axis=1, tiled=True, axis_index_groups=half_groups
        )
    pooled = pool_rows(output, final_gain, final_shift, pack_ids, pack_keep)
    class_dev = head_low.shape[1]
    image_total = labels.shape[0] * dp_count
    if on_torus:
        grad_pooled, own_rows, loss_rows = classify(
            lax.reduce_precision(pooled, 8, 7), labels, head_low, cls_count, image_total
        )
        loss_part = loss_rows[0, 0]
    else:
        group = lax.all_gather(pooled.astype(jnp.bfloat16), "cls", axis=0, tiled=True)
        logits = jnp.dot(group, head_low, preferred_element_type=jnp.float32)
        class_ids = cls_index * class_dev + jnp.arange(class_dev)
        valid = class_ids[None, :] < LABELS_REAL
        target = jnp.any(labels[:, :, None] == class_ids[None, None, :], 1).astype(jnp.float32)
        terms = jax.nn.softplus(logits) - target * logits
        loss_part = jnp.sum(jnp.where(valid, terms, 0.0)) / image_total
        grad_logits = jnp.where(valid, jax.nn.sigmoid(logits) - target, 0.0) / image_total
        grad_logits = grad_logits.astype(jnp.bfloat16)
        group_grad = jnp.einsum(
            "gc,dc->gd", grad_logits, head_low, preferred_element_type=jnp.float32
        )
        grad_pooled = lax.psum_scatter(group_grad, "cls", scatter_dimension=0, tiled=True)
        own_rows = jnp.concatenate([group, grad_logits], 1)

    def pool_local(rows_in, gain, shift):
        return pool_rows(rows_in, gain, shift, pack_ids, pack_keep)

    pool_back = jax.vjp(pool_local, output, final_gain, final_shift)[1]
    grad_output, grad_gain, grad_shift = pool_back(grad_pooled)
    lefts, rights, mlp_grads, grad_vectors, (own_rows, roots) = layer_backward(
        blocks,
        mlp_blocks,
        vec_all,
        patches,
        saved,
        pack_ids,
        key_codes,
        grad_output,
        grad_gain,
        grad_shift,
        (own_rows, right_codes if on_torus else right_half),
    )
    head_rows = lax.all_gather(own_rows, "dp", axis=0, tiled=True)
    pooled_all = head_rows[:, :feature_dim]
    grad_logits_all = head_rows[:, feature_dim : feature_dim + class_dev]
    pooled_mine = lax.dynamic_slice_in_dim(pooled_all, dp_index * row_count, row_count, 1)
    head_grad = jnp.einsum(
        "gr,gc->rc", pooled_mine, grad_logits_all, preferred_element_type=jnp.float32
    )

    head_squares = jnp.sum(head_grad * head_grad)
    if on_torus:
        padded = jnp.pad(grad_vectors, ((0, -grad_vectors.shape[0] % 8), (0, 0)))
        tail = jnp.pad(jnp.stack([head_squares, loss_part])[:, None], ((0, 6), (0, 127)))
        block_rows, left_add, right_add, direction, wide_scale, facts, vector_sum = (
            reduce_gradients(
                mlp_grads, lefts, rights, padded, tail, root_left, roots,
                dp_count, cls_count,
            )
        )
        vector_sum = vector_sum[: grad_vectors.shape[0]]
        loss, grad_norm, factor = facts[0, 0], facts[1, 0], facts[2, 0]
    else:
        over_rows = "td,te->de"
        first_grads = [
            jnp.einsum(over_rows, left, right, preferred_element_type=jnp.float32)[None]
            for left, right in (
                (lefts[0], rights[0]),
                (lefts[1], rights[1][0]),
                (lefts[1], rights[1][1]),
                (lefts[1], rights[1][2]),
                (lefts[2], rights[2]),
            )
        ]
        grad_half = reduced_half(jnp.concatenate(first_grads + list(mlp_grads), 0), half_groups)
        vector_sum = lax.psum(grad_vectors, ("dp", "cls"))
        left_add, right_add, direction, block_rows = preconditioned_rows(
            grad_half, root_left, roots, (dp_index % half_dp) * row_count
        )
        squares = jnp.sum(split_halves(direction * direction, half_size), (1, 3))
        in_top = (dp_index < half_dp).astype(jnp.float32)
        once = (cls_index == 0).astype(jnp.float32)
        all_squares = head_squares + once * jnp.sum(block_rows * block_rows)
        packed = jnp.concatenate(
            [
                (once * in_top * squares).reshape(-1),
                (once * (1.0 - in_top) * squares).reshape(-1),
                jnp.stack([all_squares, loss_part]),
            ]
        )
        packed = lax.psum(packed, ("dp", "cls"))
        loss = packed[4 * block_count + 1]
        all_squares = packed[4 * block_count]
        sums = packed[: 4 * block_count].reshape(2, block_count, 2)
        block_squares = jnp.where(dp_index < half_dp, sums[0], sums[1])
        grad_norm = jnp.sqrt(all_squares + jnp.sum(vector_sum * vector_sum))
        factor = CLIP_NORM / jnp.maximum(grad_norm, CLIP_NORM)
        mean_squares = block_squares / (half_size * half_size) * factor * factor
        scale = SHAMPOO_RATE * factor * lax.rsqrt(mean_squares + ROOT_EPS)
        wide_scale = jnp.repeat(scale, half_size, axis=1)[:, None, :]
    vector_rows = lax.dynamic_slice_in_dim(vector_sum, dp_index * row_count, row_count, 1)
    new_blocks = enc_weights - direction * wide_scale
    square_factor = 0.5 * factor * factor
    new_left = 0.5 * stats_left + square_factor * left_add
    new_right = 0.5 * stats_right + square_factor * right_add
    count = step.astype(jnp.float32)
    new_vec, new_vec_m, new_vec_v = adam_step(vectors, vector_rows * factor, vec_m, vec_v, count)
    new_head, new_head_m, new_head_v = adam_step(
        head_weights, head_grad * factor, head_m, head_v, count
    )
    return (
        loss,
        grad_norm,
        new_blocks,
        block_rows * factor,
        new_left,
        new_right,
        new_vec,
        new_vec_m,
        new_vec_v,
        new_head,
        new_head_m,
        new_head_v,
    )


def solution(mesh):
    return jax.shard_map(
        on_device,
        mesh=mesh,
        in_specs=(
            P(("dp", "cls"), None),
            P(("dp", "cls"), None),
            P(("dp", "cls"), None),
            P("dp", None),
            P(),
            P(),
            P(None, "dp", None),
            P(None, "dp", None),
            P(None, "dp", None),
            P(None, "dp", None),
            P(None, "dp", None),
            P("dp", "cls"),
            P("dp", "cls"),
            P("dp", "cls"),
            P(None, "dp"),
            P(None, "dp"),
            P(None, "dp"),
        ),
        out_specs=(
            P(),
            P(),
            P(None, "dp", None),
            P(None, "dp", None),
            P(None, "dp", None),
            P(None, "dp", None),
            P(None, "dp"),
            P(None, "dp"),
            P(None, "dp"),
            P("dp", "cls"),
            P("dp", "cls"),
            P("dp", "cls"),
        ),
        check_vma=False,
    )
```

```python
import functools

import jax
import jax.numpy as jnp
from jax import lax
from jax.experimental import pallas as pl
from jax.experimental.pallas import tpu as pltpu
from jax.sharding import PartitionSpec as P

HEADS = 12
HEAD = 64
LABELS_REAL = 21843
IMAGE_MAX = 196
QTILE = 256
PAIR = 2 * HEAD
ROWS = 256
HIDDEN_TILE = 384
MESH = pl.DeviceIdType.MESH
CODE_TOP = 32766.0
CODE_FLOOR = 1e-33
PIECE = 48
FEATURE_TILE = 128
SPAN = 48
SHARES = 8
GATHER_DEPTH = 4
CLASS_TILE = 512
IMG_PACK = 8


FULL_PRECISION = lax.Precision.HIGHEST
NORM_EPS = 1e-06
CLIP_NORM = 1.0
ADAM_RATE = 0.02
SHAMPOO_RATE = 0.01
BETA_FIRST = 0.9
BETA_SECOND = 0.999
ADAM_EPS = 1e-08
WEIGHT_DECAY = 0.1
ROOT_EPS = 1e-06


def norm_rows(values, gain, shift):
    centred = values - jnp.mean(values, -1, keepdims=True)
    spread = jnp.mean(centred * centred, -1, keepdims=True)
    return centred * lax.rsqrt(spread + NORM_EPS) * gain + shift


def pool_rows(output, gain, shift, pack_ids, pack_keep):
    final = norm_rows(output, gain, shift)
    member = (
        (pack_ids[None, :] == jnp.arange(IMG_PACK)[:, None]) & (pack_keep[None, :] == 1)
    ).astype(jnp.float32)
    counted = jnp.maximum(jnp.sum(member, 1), 1.0)
    return jnp.dot(member, final, precision=FULL_PRECISION) / counted[:, None]


def key_window(tile, length):
    reach = -(-(IMAGE_MAX - 1) // 128) * 128
    low = max(0, tile * QTILE - reach)
    high = min(length, (tile + 1) * QTILE + reach)
    return low, high


def attention_bias(qids_ref, kcodes_ref, bias_ref):
    length = qids_ref.shape[0]

    @pl.when(pl.program_id(0) == 0)
    def _():
        for tile in range(length // QTILE):
            low, high = key_window(tile, length)
            shape = (QTILE, high - low)
            rows = lax.broadcasted_iota(jnp.int32, shape, 0) + tile * QTILE
            cols = lax.broadcasted_iota(jnp.int32, shape, 1) + low
            same = qids_ref[tile * QTILE : (tile + 1) * QTILE, :] == kcodes_ref[:, low:high]
            bias_ref[tile, :, : high - low] = jnp.where(same | (rows == cols), 0.0, -1e30)


def attention_tile(tile, q_ref, k_ref, v_ref, out_ref, bias_ref):
    lane = lax.broadcasted_iota(jnp.int32, (QTILE, PAIR), 1)
    low, high = key_window(tile, q_ref.shape[0])
    rows = pl.ds(tile * QTILE, QTILE)
    queries = q_ref[rows, :] * jnp.bfloat16(HEAD ** (-0.5))
    keys = k_ref[low:high, :]
    values = v_ref[low:high, :]
    halves = []
    for head in range(2):
        mine = (lane >= head * HEAD) & (lane < (head + 1) * HEAD)
        picked = jnp.where(mine, queries, jnp.zeros_like(queries))
        scores = lax.dot_general(
            picked, keys, (((1,), (1,)), ((), ())), preferred_element_type=jnp.float32
        )
        scores = scores + bias_ref[tile, :, : high - low]
        top = jnp.max(scores, -1, keepdims=True)
        weights = jnp.exp(scores - top)
        probs = weights * (1.0 / jnp.sum(weights, -1, keepdims=True))
        halves.append(
            jnp.dot(probs.astype(jnp.bfloat16), values, preferred_element_type=jnp.float32)
        )
    out_ref[rows, :] = jnp.where(lane < HEAD, halves[0], halves[1]).astype(jnp.bfloat16)


def attention_forward_kernel(qids_ref, kcodes_ref, q_ref, k_ref, v_ref, out_ref, bias_ref):
    attention_bias(qids_ref, kcodes_ref, bias_ref)
    for tile in range(q_ref.shape[0] // QTILE):
        attention_tile(tile, q_ref, k_ref, v_ref, out_ref, bias_ref)


def attention_back_bias(qids_ref, kcodes_ref, bias_ref):
    length = kcodes_ref.shape[0]

    @pl.when(pl.program_id(0) == 0)
    def _():
        for tile in range(length // QTILE):
            low, high = key_window(tile, length)
            shape = (high - low, QTILE)
            rows = lax.broadcasted_iota(jnp.int32, shape, 0) + low
            cols = lax.broadcasted_iota(jnp.int32, shape, 1) + tile * QTILE
            same = kcodes_ref[low:high, :] == qids_ref[:, tile * QTILE : (tile + 1) * QTILE]
            bias_ref[tile, : high - low, :] = jnp.where(same | (rows == cols), 0.0, -1e30)


def attention_back_tile(tile, q_ref, k_ref, v_ref, do_ref, out_ref, bias_ref, dk_ref, dv_ref):
    length = q_ref.shape[0]
    lane = lax.broadcasted_iota(jnp.int32, (QTILE, PAIR), 1)
    scale = jnp.bfloat16(HEAD ** (-0.5))
    low, high = key_window(tile, length)
    rows = pl.ds(tile * QTILE, QTILE)
    window = pl.ds(low, high - low)
    queries = q_ref[rows, :] * scale
    keys = k_ref[window, :]
    values = v_ref[window, :]
    grads = do_ref[rows, :]
    halves = []
    for head in range(2):
        mine = (lane >= head * HEAD) & (lane < (head + 1) * HEAD)
        picked = jnp.where(mine, queries, jnp.zeros_like(queries))
        picked_grads = jnp.where(mine, grads, jnp.zeros_like(grads))
        scores = lax.dot_general(
            keys, picked, (((1,), (1,)), ((), ())), preferred_element_type=jnp.float32
        )
        scores = scores + bias_ref[tile, : high - low, :]
        top = jnp.max(scores, 0, keepdims=True)
        weights = jnp.exp(scores - top)
        probs = weights * (1.0 / jnp.sum(weights, 0, keepdims=True))
        grad_probs = lax.dot_general(
            values, picked_grads, (((1,), (1,)), ((), ())), preferred_element_type=jnp.float32
        )
        inner = jnp.sum(probs * grad_probs, 0, keepdims=True)
        grad_scores = (probs * (grad_probs - inner)).astype(jnp.bfloat16)
        dv_ref[window, :] += jnp.dot(
            probs.astype(jnp.bfloat16), picked_grads, preferred_element_type=jnp.float32
        )
        dk_ref[window, :] += jnp.dot(
            grad_scores, picked, preferred_element_type=jnp.float32
        )
        halves.append(
            lax.dot_general(
                grad_scores,
                keys,
                (((0,), (0,)), ((), ())),
                preferred_element_type=jnp.float32,
            )
        )
    grad_queries = jnp.where(lane < HEAD, halves[0], halves[1]) * HEAD ** (-0.5)
    out_ref[0, rows, :] = grad_queries.astype(jnp.bfloat16)


def attention_backward_kernel(
    qids_ref, kcodes_ref, q_ref, k_ref, v_ref, do_ref, out_ref, bias_ref, dk_ref, dv_ref
):
    attention_back_bias(qids_ref, kcodes_ref, bias_ref)
    dk_ref[...] = jnp.zeros_like(dk_ref)
    dv_ref[...] = jnp.zeros_like(dv_ref)
    for tile in range(q_ref.shape[0] // QTILE):
        attention_back_tile(tile, q_ref, k_ref, v_ref, do_ref, out_ref, bias_ref, dk_ref, dv_ref)
    out_ref[1] = dk_ref[...].astype(jnp.bfloat16)
    out_ref[2] = dv_ref[...].astype(jnp.bfloat16)


def pair_spec(length, part=None):
    if part is None:
        return pl.BlockSpec((length, PAIR), lambda pair: (0, pair))
    return pl.BlockSpec((None, length, PAIR), lambda pair: (part, 0, pair))


def whole_spec(shape):
    return pl.BlockSpec(shape, lambda pair: (0,) * len(shape))


def bias_shape(length):
    tiles = length // QTILE
    window = max(high - low for low, high in (key_window(t, length) for t in range(tiles)))
    return tiles, QTILE, window


def attention_forward(qkv_rows, pack_ids, key_codes):
    _, length, width = qkv_rows.shape
    return pl.pallas_call(
        attention_forward_kernel,
        grid=(width // PAIR,),
        out_shape=jax.ShapeDtypeStruct((length, width), jnp.bfloat16),
        in_specs=[whole_spec((length, 1)), whole_spec((1, length))]
        + [pair_spec(length, part) for part in range(3)],
        out_specs=pair_spec(length),
        scratch_shapes=[pltpu.VMEM(bias_shape(length), jnp.float32)],
        compiler_params=pltpu.CompilerParams(vmem_limit_bytes=40 << 20),
        name="attention_forward",
    )(pack_ids[:, None], key_codes[None, :], qkv_rows, qkv_rows, qkv_rows)


def attention_backward(qkv_rows, pack_ids, key_codes, grad_attended):
    _, length, width = qkv_rows.shape
    tiles = length // QTILE
    window = max(high - low for low, high in (key_window(t, length) for t in range(tiles)))
    return pl.pallas_call(
        attention_backward_kernel,
        grid=(width // PAIR,),
        out_shape=jax.ShapeDtypeStruct((3, length, width), jnp.bfloat16),
        in_specs=[whole_spec((1, length)), whole_spec((length, 1))]
        + [pair_spec(length, part) for part in range(3)]
        + [pair_spec(length)],
        out_specs=pl.BlockSpec((3, length, PAIR), lambda pair: (0, 0, pair)),
        scratch_shapes=[
            pltpu.VMEM((tiles, window, QTILE), jnp.float32),
            pltpu.VMEM((length, PAIR), jnp.float32),
            pltpu.VMEM((length, PAIR), jnp.float32),
        ],
        compiler_params=pltpu.CompilerParams(vmem_limit_bytes=40 << 20),
        name="attention_backward",
    )(pack_ids[None, :], key_codes[:, None], qkv_rows, qkv_rows, qkv_rows, grad_attended)


def mlp_forward_kernel(x_ref, up_ref, bias_ref, down_ref, units_ref, slope_ref, out_ref):
    first = pl.program_id(0) == 0

    @pl.when(first)
    def _():
        out_ref[...] = jnp.zeros_like(out_ref)

    for start in range(0, x_ref.shape[0], ROWS):
        rows = pl.ds(start, ROWS)
        pre = jnp.dot(x_ref[rows, :], up_ref[...], preferred_element_type=jnp.float32)
        pre = pre + bias_ref[...]
        half = 0.5 + 0.5 * lax.erf(pre * 0.7071067811865476)
        bell = jnp.exp(-0.5 * pre * pre) * 0.3989422804014327
        units = (pre * half).astype(jnp.bfloat16)
        units_ref[rows, :] = units
        slope_ref[rows, :] = half + pre * bell
        out_ref[rows, :] += jnp.dot(units, down_ref[...], preferred_element_type=jnp.float32)


def mlp_backward_kernel(
    x_ref, dm_ref, up_ref, down_ref, units_ref, slope_ref,
    grad_up_ref, grad_down_ref, bias_ref, dx_ref, dpre_ref
):
    @pl.when(pl.program_id(0) == 0)
    def _():
        dx_ref[...] = jnp.zeros_like(dx_ref)

    total = jnp.zeros((1, HIDDEN_TILE), jnp.float32)
    for start in range(0, x_ref.shape[0], ROWS):
        rows = pl.ds(start, ROWS)
        units_back = lax.dot_general(
            dm_ref[rows, :], down_ref[...], (((1,), (1,)), ((), ())),
            preferred_element_type=jnp.float32,
        )
        grad_pre = (units_back * slope_ref[rows, :]).astype(jnp.bfloat16)
        dpre_ref[rows, :] = grad_pre
        total = total + jnp.sum(grad_pre.astype(jnp.float32), 0, keepdims=True)
        dx_ref[rows, :] += lax.dot_general(
            grad_pre, up_ref[...], (((1,), (1,)), ((), ())), preferred_element_type=jnp.float32
        )
    bias_ref[...] = total
    over_rows = (((0,), (0,)), ((), ()))
    grad_down_ref[...] = lax.dot_general(
        units_ref[...], dm_ref[...], over_rows, preferred_element_type=jnp.float32
    )
    grad_up_ref[...] = lax.dot_general(
        x_ref[...], dpre_ref[...], over_rows, preferred_element_type=jnp.float32
    )


def mlp_specs(length, width, up_count):
    split = width // HIDDEN_TILE
    resident = pl.BlockSpec((length, width), lambda t: (0, 0))
    up = pl.BlockSpec((None, width, HIDDEN_TILE), lambda t: (5 + t // split, 0, t % split))
    down = pl.BlockSpec(
        (None, HIDDEN_TILE, width), lambda t: (5 + up_count + t // split, t % split, 0)
    )
    hidden = pl.BlockSpec((length, HIDDEN_TILE), lambda t: (0, t))
    bias = pl.BlockSpec((1, HIDDEN_TILE), lambda t: (0, t))
    return split, resident, up, down, hidden, bias


def mlp_forward(rows, blocks, up_bias):
    length, width = rows.shape
    up_count = (blocks.shape[0] - 5) // 2
    split, resident, up, down, hidden, bias = mlp_specs(length, width, up_count)
    hidden_size = up_count * width
    return pl.pallas_call(
        mlp_forward_kernel,
        grid=(up_count * split,),
        out_shape=(
            jax.ShapeDtypeStruct((length, hidden_size), jnp.bfloat16),
            jax.ShapeDtypeStruct((length, hidden_size), jnp.float32),
            jax.ShapeDtypeStruct((length, width), jnp.float32),
        ),
        in_specs=[resident, up, bias, down],
        out_specs=(hidden, hidden, resident),
        compiler_params=pltpu.CompilerParams(vmem_limit_bytes=48 << 20),
        name="mlp_forward",
    )(rows, blocks, up_bias.reshape(1, hidden_size), blocks)


def mlp_backward(rows, grad_branch, blocks, units, slopes):
    length, width = rows.shape
    up_count = (blocks.shape[0] - 5) // 2
    split, resident, up, down, hidden, bias = mlp_specs(length, width, up_count)
    hidden_size = up_count * width
    return pl.pallas_call(
        mlp_backward_kernel,
        grid=(up_count * split,),
        out_shape=(
            jax.ShapeDtypeStruct((up_count, width, width), jnp.float32),
            jax.ShapeDtypeStruct((up_count, width, width), jnp.float32),
            jax.ShapeDtypeStruct((1, hidden_size), jnp.float32),
            jax.ShapeDtypeStruct((length, width), jnp.float32),
        ),
        in_specs=[resident, resident, up, down, hidden, hidden],
        out_specs=(
            pl.BlockSpec((None, width, HIDDEN_TILE), lambda t: (t // split, 0, t % split)),
            pl.BlockSpec((None, HIDDEN_TILE, width), lambda t: (t // split, t % split, 0)),
            bias,
            resident,
        ),
        scratch_shapes=[pltpu.VMEM((length, HIDDEN_TILE), jnp.bfloat16)],
        compiler_params=pltpu.CompilerParams(vmem_limit_bytes=48 << 20),
        name="mlp_backward",
    )(rows, grad_branch, blocks, blocks, units, slopes)


def layer_forward(blocks, vec_all, patch, pack_ids, key_codes):
    up_count = (blocks.shape[0] - 5) // 2
    embedded = jnp.dot(patch, blocks[0], preferred_element_type=jnp.float32) + vec_all[0]
    normed_one = norm_rows(embedded, vec_all[1], vec_all[2]).astype(jnp.bfloat16)
    qkv_rows = jnp.einsum(
        "td,kde->kte", normed_one, blocks[1:4], preferred_element_type=jnp.float32
    )
    qkv_bias = jnp.stack([vec_all[3], jnp.zeros_like(vec_all[3]), vec_all[4]])
    qkv_rows = (qkv_rows + qkv_bias[:, None, :]).astype(jnp.bfloat16)
    attended = attention_forward(qkv_rows, pack_ids, key_codes)
    hidden = (
        embedded + jnp.dot(attended, blocks[4], preferred_element_type=jnp.float32) + vec_all[5]
    )
    normed_two = norm_rows(hidden, vec_all[6], vec_all[7]).astype(jnp.bfloat16)
    units, slopes, branch = mlp_forward(normed_two, blocks, vec_all[8 : 8 + up_count])
    output = hidden + branch + vec_all[8 + up_count]
    return (
        output,
        (embedded, normed_one, qkv_rows, attended, hidden, normed_two, slopes, units),
    )


def layer_backward(
    blocks,
    vec_all,
    patch,
    saved,
    pack_ids,
    key_codes,
    grad_output,
    grad_gain,
    grad_shift,
    released,
):
    embedded, normed_one, qkv_rows, attended, hidden, normed_two, slopes, units = saved
    feature_dim = patch.shape[1]
    up_count = (blocks.shape[0] - 5) // 2
    grad_branch = grad_output.astype(jnp.bfloat16)
    grad_up, grad_down, up_sums, grad_normed_two = mlp_backward(
        normed_two, grad_branch, blocks, units, slopes
    )
    up_sums, released = lax.optimization_barrier((up_sums, released))
    norm_two_back = jax.vjp(norm_rows, hidden, vec_all[6], vec_all[7])[1]
    grad_hidden_norm, grad_gain_two, grad_shift_two = norm_two_back(grad_normed_two)
    grad_hidden = grad_output + grad_hidden_norm
    grad_attn_out = grad_hidden.astype(jnp.bfloat16)
    grad_attended = jnp.einsum(
        "td,ed->te", grad_attn_out, blocks[4], preferred_element_type=jnp.float32
    ).astype(jnp.bfloat16)
    grad_qkv = attention_backward(qkv_rows, pack_ids, key_codes, grad_attended)
    grad_normed_one = jnp.einsum(
        "kte,kde->td", grad_qkv, blocks[1:4], preferred_element_type=jnp.float32
    )
    norm_one_back = jax.vjp(norm_rows, embedded, vec_all[1], vec_all[2])[1]
    grad_embed_norm, grad_gain_one, grad_shift_one = norm_one_back(grad_normed_one)
    grad_embedded = (grad_hidden + grad_embed_norm).astype(jnp.bfloat16)
    lefts = (patch, normed_one, attended)
    rights = (grad_embedded, grad_qkv, grad_attn_out)
    bias_sums = jnp.stack(
        [
            jnp.sum(grad_embedded.astype(jnp.float32), 0),
            grad_gain_one,
            grad_shift_one,
            jnp.sum(grad_qkv[0].astype(jnp.float32), 0),
            jnp.sum(grad_qkv[2].astype(jnp.float32), 0),
            jnp.sum(grad_attn_out.astype(jnp.float32), 0),
            grad_gain_two,
            grad_shift_two,
        ]
    )
    up_sums = up_sums.reshape(up_count, feature_dim)
    tail_sums = jnp.stack([jnp.sum(grad_branch.astype(jnp.float32), 0), grad_gain, grad_shift])
    grad_vectors = jnp.concatenate([bias_sums, up_sums, tail_sums], 0)
    return (lefts, rights, (grad_up, grad_down), grad_vectors, released)


def torus_place():
    dp, cls = lax.axis_index("dp"), lax.axis_index("cls")
    return dp // 2, dp % 2, cls // 2, cls % 2


def torus_device(z, y, x, core):
    return (z * 2 + y, x * 2 + core)


def encode(pieces, code_refs, scale_ref):
    top = None
    for piece in pieces:
        peak = jnp.max(jnp.abs(piece()), 0, keepdims=True)
        top = peak if top is None else jnp.maximum(top, peak)
    top = jnp.maximum(top, CODE_FLOOR)
    inverse = CODE_TOP / top
    for piece, code_ref in zip(pieces, code_refs):
        code_ref[...] = jnp.round(piece() * inverse).astype(jnp.int32).astype(jnp.int16)
    scale_ref[...] = top * (1.0 / CODE_TOP)


def decode(code, scale):
    return code.astype(jnp.int32).astype(jnp.float32) * scale


def reduce_kernel(counts, *refs):
    sources, refs = refs[: len(counts)], refs[len(counts) :]
    (patch_hbm, first_hbm, mid_hbm, dpatch_hbm, dfirst_hbm, dmid_hbm,
     vec_ref, tail_ref, left_hbm, right_hbm,
     own_hbm, left_out_hbm, right_out_hbm, step_hbm, wide_ref, facts_ref, vec_out_ref,
     left_buf, right_buf, right_full, outs_buf, squares, high_buf, low_buf, sum_slots, tail_slots,
     lhs_buf, rhs_buf, pair_sem,
     in_sem, sum_send, sum_recv, tail_send, tail_recv,
     acc, spare, kept, sent0, got0, sent1, got1, sent2, got2, sent3, got3, sent4, got4,
     ss0, gs0, ss1, gs1, ss2, gs2, ss3, gs3, ss4, gs4, codes, scales, vec_got,
     load_sem, out_sem, send_sem, recv_sem, send_scale_sem, recv_scale_sem,
     vec_send_sem, vec_recv_sem) = refs
    stored = sum(counts)
    paired = dfirst_hbm.shape[0] + 2
    total = stored + paired
    half, width = codes.shape[1], codes.shape[2]
    cols = width // 2
    z, y, x, core = torus_place()
    upper = z // 2
    inner = (z % 2) != upper
    mate_core = torus_device(z, y, x, 1 - core)
    mate_x = torus_device(z, y, 1 - x, core)
    mate_y = torus_device(z, 1 - y, x, core)
    mate_z = torus_device(z + 1 - 2 * (z % 2), y, x, core)
    mate_mid = torus_device(3 - z, y, x, core)
    mate_far = torus_device((z + 2) % 4, y, x, core)

    barrier = pltpu.get_barrier_semaphore()
    dp, cls = lax.axis_index("dp"), lax.axis_index("cls")
    everyone = tail_slots.shape[0]
    quarter = sum_slots.shape[0]
    me = dp * 4 + cls

    def any_mate(n):
        other = lax.rem(me + n, everyone)
        return (other // 4, lax.rem(other, 4))

    def half_mate(n):
        return (upper * quarter + lax.rem(dp + n, quarter), cls)

    for n in range(1, everyone):
        pl.semaphore_signal(barrier, inc=1, device_id=any_mate(n), device_id_type=MESH)
    pl.semaphore_wait(barrier, everyone - 1)
    own = lax.rem(dp, quarter) * left_buf.shape[1]

    own_cols = pl.ds(pl.multiple_of(core * cols, 128), cols)
    other_cols = pl.ds(pl.multiple_of((1 - core) * cols, 128), cols)

    def rows_at(start, size):
        return pl.ds(pl.multiple_of(start, PIECE), size)

    def loads(m, body):
        start = 0
        for source, count in zip(sources, counts):
            def one(source=source, start=start):
                pair = (
                    pltpu.make_async_copy(
                        source.at[m - start, :, own_cols], acc.at[m % 5], load_sem.at[m % 2, 0]
                    ),
                    pltpu.make_async_copy(
                        source.at[m - start, :, other_cols], spare.at[m % 2], load_sem.at[m % 2, 1]
                    ),
                )
                for copy in pair:
                    body(copy)

            pl.when((m >= start) & (m < start + count))(one)
            start += count

    def block_of(m):
        return lax.rem(m + paired, total)

    def pair_loads(m, body):
        index = m - stored
        last = paired - 1

        def run(left, right):
            body(pltpu.make_async_copy(left, lhs_buf.at[m % 2], pair_sem.at[m % 2, 0]))
            body(pltpu.make_async_copy(right, rhs_buf.at[m % 2], pair_sem.at[m % 2, 1]))

        pl.when(index == 0)(lambda: run(patch_hbm, dpatch_hbm))
        pl.when((index > 0) & (index < last))(
            lambda: run(first_hbm, dfirst_hbm.at[jnp.clip(index - 1, 0, last - 2)])
        )
        pl.when(index == last)(lambda: run(mid_hbm, dmid_hbm))

    def pair_product(m):
        chunk = 2 * FEATURE_TILE
        for r in range(0, width, chunk):
            left = lhs_buf[m % 2, :, r : r + chunk].T
            for target, columns in ((acc.at[m % 5], own_cols), (spare.at[m % 2], other_cols)):
                target[r : r + chunk, :] = jnp.dot(
                    left, rhs_buf[m % 2, :, columns], preferred_element_type=jnp.float32
                )

    def message(stage, m, source, scale_source, target, scale_target, mate):
        return (
            pltpu.make_async_remote_copy(
                src_ref=source, dst_ref=target,
                send_sem=send_sem.at[stage, m % 2], recv_sem=recv_sem.at[stage, m],
                device_id=mate, device_id_type=MESH,
            ),
            pltpu.make_async_remote_copy(
                src_ref=scale_source, dst_ref=scale_target,
                send_sem=send_scale_sem.at[stage, m % 2], recv_sem=recv_scale_sem.at[stage, m],
                device_id=mate, device_id_type=MESH,
            ),
        )

    def first(m):
        return message(0, m, sent0.at[m % 2], ss0.at[m % 2], got0.at[m], gs0.at[m], mate_core)

    def second(m, b):
        return message(
            1 + b, m, sent1.at[m % 2, b], ss1.at[m % 2, b], got1.at[m, b], gs1.at[m, b],
            mate_y if b else mate_x,
        )

    def third(m, b):
        return message(
            3 + b, m, sent2.at[m % 2, b], ss2.at[m % 2, b], got2.at[m, b], gs2.at[m, b],
            mate_x if b else mate_y,
        )

    def fourth(m):
        return message(5, m, sent3.at[m % 2], ss3.at[m % 2], got3.at[m], gs3.at[m], mate_z)

    def fifth(m):
        return message(6, m, sent4.at[m % 2], ss4.at[m % 2], got4.at[m], gs4.at[m], mate_mid)

    piece_a = 2 * x + y
    piece_b = 4 + 2 * y + x

    def spread(stage, m, piece, count, mate, columns=own_cols):
        rows = pl.ds(pl.multiple_of(piece * PIECE, PIECE), count * PIECE)
        block = codes.at[m, rows, columns]
        scale = scales.at[m, pl.ds(piece, count), :, columns]
        return message(stage, m, block, scale, block, scale, mate)

    def start(copies):
        for copy in copies:
            copy.start()

    def wait_send(copies):
        for copy in copies:
            copy.wait_send()

    def wait_recv(copies):
        for copy in copies:
            copy.wait_recv()

    def vec_copy(step, mate):
        return pltpu.make_async_remote_copy(
            src_ref=vec_got.at[step, 0], dst_ref=vec_got.at[step, 1],
            send_sem=vec_send_sem.at[step], recv_sem=vec_recv_sem.at[step],
            device_id=mate, device_id_type=MESH,
        )

    vec_mates = (mate_core, mate_x, mate_y, mate_z, mate_far)

    loads(jnp.int32(0), lambda copy: copy.start())
    vec_got[0, 0] = vec_ref[...]
    vec_copy(0, vec_mates[0]).start()

    def step(t, carry):
        for n in range(1, 6):
            @pl.when(t == n)
            def _(n=n):
                vec_copy(n - 1, vec_mates[n - 1]).wait()
                value = vec_got[n - 1, 0] + vec_got[n - 1, 1]
                if n < 5:
                    vec_got[n, 0] = value
                    vec_copy(n, vec_mates[n]).start()
                else:
                    vec_out_ref[...] = value

        @pl.when(t < total)
        def _():
            m = t

            @pl.when(m < stored)
            def _():
                loads(m, lambda copy: copy.wait())

            @pl.when(m + 1 < stored)
            def _():
                loads(m + 1, lambda copy: copy.start())

            @pl.when((m + 1 >= stored) & (m + 1 < total))
            def _():
                pair_loads(m + 1, lambda copy: copy.start())

            @pl.when(m >= stored)
            def _():
                pair_loads(m, lambda copy: copy.wait())
                pair_product(m)

            span = 2 * PIECE
            encode(
                [lambda r=r: spare[m % 2, r : r + span, :] for r in range(0, 2 * half, span)],
                [sent0.at[m % 2, r : r + span, :] for r in range(0, 2 * half, span)],
                ss0.at[m % 2],
            )
            start(first(m))

        @pl.when((t >= 1) & (t < total + 1))
        def _():
            m = t - 1
            copies = first(m)
            wait_send(copies)
            wait_recv(copies)
            slot = m % 5
            span = 2 * PIECE
            for r in range(0, 2 * half, span):
                acc[slot, r : r + span, :] += decode(got0[m, r : r + span, :], gs0[m])
            for b in range(2):
                other = (1 - y) if b else (1 - x)
                begins = [h * half + b * 4 * PIECE + other * span for h in range(2)]
                encode(
                    [lambda s=s: acc[slot, rows_at(s, span), :] for s in begins],
                    [sent1.at[m % 2, b, h] for h in range(2)],
                    ss1.at[m % 2, b],
                )
                start(second(m, b))

        @pl.when((t >= 2) & (t < total + 2))
        def _():
            m = t - 2
            slot = m % 5
            span = 2 * PIECE
            for b in range(2):
                copies = second(m, b)
                wait_send(copies)
                wait_recv(copies)
                mine = y if b else x
                other = (1 - x) if b else (1 - y)
                begins = [h * half + b * 4 * PIECE + mine * span for h in range(2)]
                for h, s in enumerate(begins):
                    acc[slot, rows_at(s, span), :] += decode(got1[m, b, h], gs1[m, b])
                encode(
                    [lambda s=s: acc[slot, rows_at(s + other * PIECE, PIECE), :] for s in begins],
                    [sent2.at[m % 2, b, h] for h in range(2)],
                    ss2.at[m % 2, b],
                )
                start(third(m, b))

        @pl.when((t >= 3) & (t < total + 3))
        def _():
            m = t - 3
            slot = m % 5
            for b in range(2):
                copies = third(m, b)
                wait_send(copies)
                wait_recv(copies)
                place = piece_b if b else piece_a
                for h in range(2):
                    kept[m % 3, h, b] = acc[
                        slot, rows_at(h * half + place * PIECE, PIECE), :
                    ] + decode(got2[m, b, h], gs2[m, b])

            @pl.when(jnp.logical_not(inner))
            def _():
                pairs = [(h, b) for h in range(2) for b in range(2)]
                encode(
                    [lambda h=h, b=b: kept[m % 3, h, b] for h, b in pairs],
                    [sent3.at[m % 2, h, b] for h, b in pairs],
                    ss3.at[m % 2],
                )
                start(fourth(m))

        @pl.when((t >= 4) & (t < total + 4))
        def _():
            m = t - 4
            copies = fourth(m)

            @pl.when(jnp.logical_not(inner))
            def _():
                wait_send(copies)

            @pl.when(inner)
            def _():
                wait_recv(copies)
                for h in range(2):
                    for b in range(2):
                        kept[m % 3, h, b] += decode(got3[m, h, b], gs3[m])
                encode(
                    [lambda b=b: kept[m % 3, 1 - upper, b] for b in range(2)],
                    [sent4.at[m % 2, b] for b in range(2)],
                    ss4.at[m % 2],
                )
                start(fifth(m))

        @pl.when((t >= 5) & (t < total + 5))
        def _():
            m = t - 5

            @pl.when(inner)
            def _():
                copies = fifth(m)
                wait_send(copies)
                wait_recv(copies)
                for b in range(2):
                    place = piece_b if b else piece_a
                    value = kept[m % 3, upper, b] + decode(got4[m, b], gs4[m])
                    encode(
                        [lambda value=value: value],
                        [codes.at[m, rows_at(place * PIECE, PIECE), own_cols]],
                        scales.at[m, place, :, own_cols],
                    )
                    start(spread(7 + b, m, place, 1, mate_z))

        @pl.when((t >= 6) & (t < total + 6))
        def _():
            m = t - 6
            for b in range(2):
                place = piece_b if b else piece_a
                copies = spread(7 + b, m, place, 1, mate_z)

                @pl.when(inner)
                def _(copies=copies):
                    wait_send(copies)

                @pl.when(jnp.logical_not(inner))
                def _(copies=copies):
                    wait_recv(copies)

                start(spread(9 + b, m, place, 1, mate_x if b else mate_y))

        @pl.when((t >= 7) & (t < total + 7))
        def _():
            m = t - 7
            for b in range(2):
                place = piece_b if b else piece_a
                theirs = (4 + 2 * y + 1 - x) if b else (2 * x + 1 - y)
                wait_send(spread(9 + b, m, place, 1, mate_x if b else mate_y))
                wait_recv(spread(9 + b, m, theirs, 1, mate_x if b else mate_y))
                begin = (4 + 2 * y) if b else 2 * x
                start(spread(11 + b, m, begin, 2, mate_y if b else mate_x))

        @pl.when((t >= 8) & (t < total + 8))
        def _():
            m = t - 8
            for b in range(2):
                begin = (4 + 2 * y) if b else 2 * x
                theirs = (4 + 2 * (1 - y)) if b else 2 * (1 - x)
                wait_send(spread(11 + b, m, begin, 2, mate_y if b else mate_x))
                wait_recv(spread(11 + b, m, theirs, 2, mate_y if b else mate_x))
            start(spread(13, m, 0, 8, mate_core))

        def ins(m):
            return (
                pltpu.make_async_copy(
                    left_hbm.at[block_of(m)], left_buf.at[m % 2], in_sem.at[m % 2, 0]
                ),
                pltpu.make_async_copy(
                    right_hbm.at[:, block_of(m)], right_buf.at[m % 2], in_sem.at[m % 2, 1]
                ),
            )

        def outs(m):
            targets = (own_hbm, left_out_hbm, right_out_hbm, step_hbm)
            return [
                pltpu.make_async_copy(
                    outs_buf.at[m % 2, n], target.at[block_of(m)], out_sem.at[m % 2, n]
                )
                for n, target in enumerate(targets)
            ]

        @pl.when((t >= 8) & (t < total + 8))
        def _():
            start(ins(t - 8))

        @pl.when((t >= 11) & (t < total + 11))
        def _():
            for copy in outs(t - 11):
                copy.wait()

        @pl.when((t >= 9) & (t < total + 9))
        def _():
            m = t - 9
            wait_send(spread(13, m, 0, 8, mate_core))
            wait_recv(spread(13, m, 0, 8, mate_core, other_cols))
            for copy in ins(m):
                copy.wait()
            precondition_block(
                own, codes.at[m], scales.at[m], left_buf.at[m % 2], right_buf.at[m % 2],
                outs_buf.at[m % 2], squares.at[m], high_buf, low_buf, right_full,
            )
            start(outs(m))

        return carry

    lax.fori_loop(0, total + 11, step, 0)

    def folded(row):
        return sum(row[:, n * 128 : (n + 1) * 128] for n in range(row.shape[1] // 128))

    layer = jnp.zeros((1, 128), jnp.float32)
    mine = lax.rem(dp, quarter)
    sum_slots[mine] = jnp.zeros(sum_slots.shape[1:], jnp.float32)
    for m in range(total):
        layer = layer + folded(squares[m, 0:1, :])
        for quad in range(2):
            part = squares[m, 1:2, quad * cols : (quad + 1) * cols]
            row = 2 * ((m + paired) % total) + quad
            sum_slots[mine, row : row + 1, :] = folded(part)
    once = (cls == 0).astype(jnp.float32)
    first_row = lax.broadcasted_iota(jnp.int32, tail_ref.shape, 0) == 0
    tail_slots[me] = tail_ref[...] + jnp.where(first_row, once * layer, 0.0)

    def sum_copy(n, slot):
        return pltpu.make_async_remote_copy(
            src_ref=sum_slots.at[slot], dst_ref=sum_slots.at[slot],
            send_sem=sum_send.at[n], recv_sem=sum_recv.at[slot],
            device_id=half_mate(n), device_id_type=MESH,
        )

    def tail_copy(n, slot):
        return pltpu.make_async_remote_copy(
            src_ref=tail_slots.at[slot], dst_ref=tail_slots.at[slot],
            send_sem=tail_send.at[n], recv_sem=tail_recv.at[slot],
            device_id=any_mate(n), device_id_type=MESH,
        )

    for n in range(1, quarter):
        sum_copy(n, lax.rem(dp, quarter)).start()
    for n in range(1, everyone):
        tail_copy(n, me).start()
    for n in range(1, quarter):
        sum_copy(n, lax.rem(dp, quarter)).wait_send()
        sum_copy(n, lax.rem(dp + n, quarter)).wait_recv()
    for n in range(1, everyone):
        tail_copy(n, me).wait_send()
        tail_copy(n, lax.rem(me + n, everyone)).wait_recv()
    value = sum_slots[0]
    for n in range(1, quarter):
        value = value + sum_slots[n]
    tail = tail_slots[0]
    for n in range(1, everyone):
        tail = tail + tail_slots[n]
    vec = vec_out_ref[...]
    vec_squares = jnp.sum(jnp.sum(vec * vec, 0, keepdims=True), 1, keepdims=True)
    norm = jnp.sqrt(jnp.sum(tail[0:1], 1, keepdims=True) + vec_squares)
    factor = CLIP_NORM / jnp.maximum(norm, CLIP_NORM)
    mean_squares = jnp.sum(value, 1, keepdims=True) / (half * cols) * factor * factor
    scale = SHAMPOO_RATE * factor * lax.rsqrt(mean_squares + ROOT_EPS)
    for b in range(total):
        for quad in range(2):
            row = 2 * b + quad
            wide_ref[b, :, quad * cols : (quad + 1) * cols] = jnp.broadcast_to(
                scale[row : row + 1], (1, cols)
            )
    rows = lax.broadcasted_iota(jnp.int32, facts_ref.shape, 0)
    loss = jnp.sum(tail[1:2], 1, keepdims=True)
    facts_ref[...] = jnp.where(rows == 0, loss, jnp.where(rows == 1, norm, factor))


def reduce_gradients(
    arrays, lefts, rights, vec_sums, tail, root_left, right_codes, dp_count, cls_count
):
    counts = tuple(array.shape[0] for array in arrays)
    total, rows, width = root_left.shape
    length = lefts[0].shape[0]
    parts, coded_rows = right_codes.shape[0], right_codes.shape[2]
    half, cols = width // 2, width // 2
    sum_rows = 2 * total + -2 * total % 8
    f32, i16 = jnp.float32, jnp.int16

    def pair(*shape):
        return [pltpu.VMEM((2,) + shape, i16), pltpu.VMEM((total,) + shape, i16)]

    def scale_pair(*shape):
        return [
            pltpu.VMEM((2,) + shape + (1, cols), f32),
            pltpu.VMEM((total,) + shape + (1, cols), f32),
        ]

    hbm = pl.BlockSpec(memory_space=pl.ANY)
    vmem = pl.BlockSpec(memory_space=pltpu.VMEM)
    return pl.pallas_call(
        functools.partial(reduce_kernel, counts),
        out_shape=(jax.ShapeDtypeStruct((total, rows, width), f32),) * 4
        + (
            jax.ShapeDtypeStruct((total, 1, width), f32),
            jax.ShapeDtypeStruct(tail.shape, f32),
            jax.ShapeDtypeStruct(vec_sums.shape, f32),
        ),
        in_specs=[hbm] * (len(arrays) + 6) + [vmem, vmem, hbm, hbm],
        out_specs=(hbm,) * 4 + (vmem,) * 3,
        scratch_shapes=[
            pltpu.VMEM((2, rows, width), f32),
            pltpu.VMEM((2, parts, coded_rows, width), jnp.int32),
            pltpu.VMEM((half, width), f32),
            pltpu.VMEM((2, 4, rows, width), f32),
            pltpu.VMEM((total, 2, width), f32),
            pltpu.VMEM((half, width), jnp.bfloat16),
            pltpu.VMEM((half, width), jnp.bfloat16),
            pltpu.VMEM((dp_count // 2, sum_rows, 128), f32),
            pltpu.VMEM((dp_count * cls_count,) + tail.shape, f32),
            pltpu.VMEM((2, length, width), jnp.bfloat16),
            pltpu.VMEM((2, length, width), jnp.bfloat16),
            pltpu.SemaphoreType.DMA((2, 2)),
            pltpu.SemaphoreType.DMA((2, 2)),
            pltpu.SemaphoreType.DMA((dp_count // 2,)),
            pltpu.SemaphoreType.DMA((dp_count // 2,)),
            pltpu.SemaphoreType.DMA((dp_count * cls_count,)),
            pltpu.SemaphoreType.DMA((dp_count * cls_count,)),
            pltpu.VMEM((5, width, cols), f32),
            pltpu.VMEM((2, width, cols), f32),
            pltpu.VMEM((3, 2, 2, PIECE, cols), f32),
        ]
        + pair(width, cols)
        + pair(2, 2, 2 * PIECE, cols)
        + pair(2, 2, PIECE, cols)
        + pair(2, 2, PIECE, cols)
        + pair(2, PIECE, cols)
        + scale_pair()
        + scale_pair(2)
        + scale_pair(2)
        + scale_pair()
        + scale_pair()
        + [
            pltpu.VMEM((total, half, width), i16),
            pltpu.VMEM((total, half // PIECE, 1, width), f32),
            pltpu.VMEM((5, 2) + vec_sums.shape, f32),
            pltpu.SemaphoreType.DMA((2, 2)),
            pltpu.SemaphoreType.DMA((2, 4)),
            pltpu.SemaphoreType.DMA((14, 2)),
            pltpu.SemaphoreType.DMA((14, total)),
            pltpu.SemaphoreType.DMA((14, 2)),
            pltpu.SemaphoreType.DMA((14, total)),
            pltpu.SemaphoreType.DMA((5,)),
            pltpu.SemaphoreType.DMA((5,)),
        ],
        compiler_params=pltpu.CompilerParams(
            collective_id=1, has_side_effects=True, vmem_limit_bytes=60 << 20
        ),
        name="reduce_gradients",
    )(*arrays, *lefts, *rights, vec_sums, tail, root_left, right_codes)


def split_float(values):
    high = values.astype(jnp.bfloat16)
    return high, (values - high.astype(jnp.float32)).astype(jnp.bfloat16)


def stacked_dot(lefts, right, contract_last):
    rows = lefts[0].shape[0]
    left = jnp.concatenate(lefts, 0) if len(lefts) > 1 else lefts[0]
    dims = (((1,), (1 if contract_last else 0,)), ((), ()))
    out = lax.dot_general(left, right, dims, preferred_element_type=jnp.float32)
    return [out[n * rows : (n + 1) * rows] for n in range(len(lefts))]


def encode_roots(part):
    top = jnp.max(jnp.abs(part), 1, keepdims=True)
    level = jnp.ceil(jnp.log2(jnp.maximum(top, 1e-30)))
    codes = jnp.round(part * jnp.exp2(15.0 - level))
    codes = jnp.clip(codes, -32767.0, 32767.0).astype(jnp.int32)
    levels = jnp.broadcast_to(level.astype(jnp.int32), (part.shape[0], 8, part.shape[2]))
    upper = jnp.concatenate([codes[:, 0:8], codes[:, 16:24]], 1)
    lower = jnp.concatenate([codes[:, 8:16], levels], 1)
    return upper * 65536 + (lower + 32768)


def precondition_block(
    own, codes_ref, scales_ref, left_ref, right_codes, outs_ref, squares_ref, high_ref, low_ref,
    right_ref
):
    half, width = codes_ref.shape
    rows = left_ref.shape[0]
    own_rows = pl.ds(pl.multiple_of(own, PIECE), rows)
    parts = right_codes.shape[0]
    size = half // parts
    for n in range(parts):
        packed = right_codes[n]
        upper = lax.shift_right_arithmetic(packed, jnp.full_like(packed, 16)).astype(jnp.float32)
        lower = ((packed & 65535) - 32768).astype(jnp.float32)
        scale = jnp.exp2(lower[8:9] - 15.0)
        right_ref[n * size : n * size + 8, :] = upper[0:8] * scale
        right_ref[n * size + 8 : n * size + 16, :] = lower[0:8] * scale
        right_ref[n * size + 16 : n * size + 24, :] = upper[8:16] * scale
    for piece in range(half // PIECE):
        part = slice(piece * PIECE, (piece + 1) * PIECE)
        high_ref[part, :], low_ref[part, :] = split_float(
            decode(codes_ref[part, :], scales_ref[piece])
        )
    own_value = high_ref[own_rows, :].astype(jnp.float32) + low_ref[own_rows, :].astype(jnp.float32)
    outs_ref[0] = own_value
    squares_ref[0:1, :] = jnp.sum(own_value * own_value, 0, keepdims=True)
    picks = (
        lax.broadcasted_iota(jnp.int32, (rows, half), 1)
        == lax.broadcasted_iota(jnp.int32, (rows, half), 0) + own
    ).astype(jnp.float32).astype(jnp.bfloat16)
    for quad in range(2):
        cols = slice(quad * half, (quad + 1) * half)
        high, low = high_ref[:, cols], low_ref[:, cols]
        mine_high, mine_low = high_ref[own_rows, cols], low_ref[own_rows, cols]
        hh, lh, turned_high = stacked_dot([mine_high, mine_low, picks], high, True)
        hl, turned_low = stacked_dot([mine_high, picks], low, True)
        outs_ref[1, :, cols] = hh + (lh + hl)
        turned_high = turned_high.astype(jnp.bfloat16)
        turned_low = turned_low.astype(jnp.bfloat16)
        root_high, root_low = split_float(left_ref[:, cols])
        thh, tlh, rhh, rlh = stacked_dot([turned_high, turned_low, root_high, root_low], high, False)
        thl, rhl = stacked_dot([turned_high, root_high], low, False)
        outs_ref[2, :, cols] = thh + (tlh + thl)
        half_step = rhh + (rlh + rhl)
        step_high, step_low = split_float(half_step)
        right_high, right_low = split_float(right_ref[:, cols])
        shh, slh = stacked_dot([step_high, step_low], right_high, False)
        (shl,) = stacked_dot([step_high], right_low, False)
        direction = shh + (slh + shl)
        outs_ref[3, :, cols] = direction
        squares_ref[1:2, cols] = jnp.sum(direction * direction, 0, keepdims=True)


def head_kernel(
    image_total, pooled_ref, labels_ref, head_hbm,
    grad_ref, rows_ref, loss_ref,
    head_buf, group_buf, total_buf, slots, load_sem, send_sem, recv_sem, sum_send, sum_recv
):
    dp, cls = lax.axis_index("dp"), lax.axis_index("cls")
    count, rows, width = slots.shape
    images = count * rows
    classes = head_buf.shape[1]
    load = pltpu.make_async_copy(head_hbm, head_buf, load_sem)
    load.start()
    barrier = pltpu.get_barrier_semaphore()
    for n in range(1, count):
        pl.semaphore_signal(
            barrier, inc=1, device_id=(dp, lax.rem(cls + n, count)), device_id_type=MESH
        )
    pl.semaphore_wait(barrier, count - 1)

    def part(ref, index):
        return ref.at[pl.ds(pl.multiple_of(index * rows, 8), rows)]

    def share(n, slot):
        return pltpu.make_async_remote_copy(
            src_ref=pooled_ref, dst_ref=part(group_buf, slot),
            send_sem=send_sem.at[n], recv_sem=recv_sem.at[slot],
            device_id=(dp, lax.rem(cls + n, count)), device_id_type=MESH,
        )

    for n in range(1, count):
        share(n, cls).start()
    part(group_buf, cls)[...] = pooled_ref[...]
    rows_ref[:, width + classes :] = jnp.zeros(
        (images, rows_ref.shape[1] - width - classes), rows_ref.dtype
    )
    for n in range(1, count):
        share(n, cls).wait_send()
        share(n, lax.rem(cls + n, count)).wait_recv()
    load.wait()
    group = group_buf[...].astype(jnp.bfloat16)
    rows_ref[:, :width] = group
    loss = jnp.zeros((1, 1), jnp.float32)
    total = jnp.zeros((images, width), jnp.float32)
    for start in range(0, classes, CLASS_TILE):
        stop = min(classes, start + CLASS_TILE)
        weights = head_buf[:, start:stop]
        logits = jnp.dot(group, weights, preferred_element_type=jnp.float32)
        ids = lax.broadcasted_iota(jnp.int32, logits.shape, 1) + (cls * classes + start)
        target = ids == labels_ref[:, 0:1]
        for n in range(1, labels_ref.shape[1]):
            target = target | (ids == labels_ref[:, n : n + 1])
        target = target.astype(jnp.float32)
        valid = ids < LABELS_REAL
        shrunk = jnp.exp(-jnp.abs(logits))
        terms = jnp.maximum(logits, 0.0) + jnp.log1p(shrunk) - target * logits
        terms = jnp.where(valid, terms, 0.0)
        loss = loss + jnp.sum(jnp.sum(terms, 0, keepdims=True), 1, keepdims=True)
        chance = jnp.where(logits >= 0.0, 1.0, shrunk) / (1.0 + shrunk)
        grads = jnp.where(valid, chance - target, 0.0) / image_total
        grads = grads.astype(jnp.bfloat16)
        rows_ref[:, width + start : width + stop] = grads
        total = total + lax.dot_general(
            grads, weights, (((1,), (1,)), ((), ())), preferred_element_type=jnp.float32
        )
    loss_ref[...] = jnp.broadcast_to(loss / image_total, loss_ref.shape)
    total_buf[...] = total

    def back(n, slot):
        mate = lax.rem(cls + n, count)
        return pltpu.make_async_remote_copy(
            src_ref=part(total_buf, mate), dst_ref=slots.at[slot],
            send_sem=sum_send.at[n], recv_sem=sum_recv.at[slot],
            device_id=(dp, mate), device_id_type=MESH,
        )

    for n in range(1, count):
        back(n, cls).start()
    slots[cls] = part(total_buf, cls)[...]
    for n in range(1, count):
        back(n, cls).wait_send()
        back(n, lax.rem(cls + n, count)).wait_recv()
    value = slots[0]
    for n in range(1, count):
        value = value + slots[n]
    grad_ref[...] = value


def classify(pooled, labels, head_low, cls_count, image_total):
    rows, width = pooled.shape
    images, classes = rows * cls_count, head_low.shape[1]
    wide = width + classes
    wide = wide + -wide % 128
    f32 = jnp.float32
    vmem = pl.BlockSpec(memory_space=pltpu.VMEM)
    return pl.pallas_call(
        functools.partial(head_kernel, image_total),
        out_shape=(
            jax.ShapeDtypeStruct((rows, width), f32),
            jax.ShapeDtypeStruct((images, wide), jnp.bfloat16),
            jax.ShapeDtypeStruct((8, 128), f32),
        ),
        in_specs=[vmem, vmem, pl.BlockSpec(memory_space=pltpu.HBM)],
        out_specs=(vmem, vmem, vmem),
        scratch_shapes=[
            pltpu.VMEM((width, classes), jnp.bfloat16),
            pltpu.VMEM((images, width), f32),
            pltpu.VMEM((images, width), f32),
            pltpu.VMEM((cls_count, rows, width), f32),
            pltpu.SemaphoreType.DMA,
        ]
        + [pltpu.SemaphoreType.DMA((cls_count,)) for _ in range(4)],
        compiler_params=pltpu.CompilerParams(
            collective_id=2, has_side_effects=True, vmem_limit_bytes=60 << 20
        ),
        name="classify",
    )(pooled, labels, head_low)


def gather_steps(own_ref, out_ref, send_sem, recv_sem, copy_sem):
    count, rows, width = own_ref.shape
    cols = width // 2
    z, y, x, core = torus_place()
    mate_core = torus_device(z, y, x, 1 - core)
    mate_x = torus_device(z, y, 1 - x, core)
    mate_y = torus_device(z, 1 - y, x, core)
    own_cols = pl.ds(pl.multiple_of(core * cols, 128), cols)
    other_cols = pl.ds(pl.multiple_of((1 - core) * cols, 128), cols)
    spare = rows - SPAN
    held = x * spare
    lone = (x * SPAN, (1 - x) * SPAN)

    def share(m, zz, yy, start, size):
        begin = (zz * 2 + yy) * rows + start
        return out_ref.at[m, pl.ds(pl.multiple_of(begin, 16), size), own_cols]

    def copy(slot, arrival, m, source, target, mate):
        return pltpu.make_async_remote_copy(
            src_ref=source, dst_ref=target,
            send_sem=send_sem.at[slot, m % 2], recv_sem=recv_sem.at[arrival, m],
            device_id=mate, device_id_type=MESH,
        )

    def local(m):
        return pltpu.make_async_copy(
            own_ref.at[m, :, own_cols], share(m, z, y, 0, rows), copy_sem.at[m % 2]
        )

    def along(m, n, outgoing):
        other = lax.rem(z + n, 4)
        origin = z if outgoing else other
        source = own_ref.at[m, pl.ds(pl.multiple_of(held, 16), SPAN), own_cols]
        mate = torus_device(other, y, x, core)
        return copy(n - 1, origin, m, source, share(m, origin, y, held, SPAN), mate)

    def cross(m, n, outgoing):
        block = share(m, n, y if outgoing else 1 - y, held, SPAN)
        return copy(3 + n, 4 + n, m, block, block, mate_y)

    def patch(m, n, outgoing):
        index = lax.rem(z * 2 + y + n, SHARES)
        block = share(m, index // 2, lax.rem(index, 2), lone[0 if outgoing else 1], spare)
        return copy(6 + n, 7 + n, m, block, block, mate_x)

    def swap(m, columns):
        block = out_ref.at[m, :, columns]
        return copy(14, 15, m, block, block, mate_core)

    def finish(copies):
        for outgoing, incoming in copies:
            outgoing.wait_send()
            incoming.wait_recv()

    def step(t):
        @pl.when(t < count)
        def _():
            local(t).start()
            for n in range(1, 4):
                along(t, n, True).start()

        @pl.when((t >= 1) & (t < count + 1))
        def _():
            m = t - 1
            local(m).wait()
            finish([(along(m, n, True), along(m, n, False)) for n in range(1, 4)])
            for n in range(4):
                cross(m, n, True).start()

        @pl.when((t >= 2) & (t < count + 2))
        def _():
            m = t - 2
            finish([(cross(m, n, True), cross(m, n, False)) for n in range(4)])
            for n in range(1, SHARES):
                patch(m, n, True).start()

        @pl.when((t >= 3) & (t < count + 3))
        def _():
            m = t - 3
            finish([(patch(m, n, True), patch(m, n, False)) for n in range(1, SHARES)])
            swap(m, own_cols).start()

        @pl.when((t >= 4) & (t < count + 4))
        def _():
            m = t - 4
            swap(m, own_cols).wait_send()
            swap(m, other_cols).wait_recv()

    return step, count + GATHER_DEPTH


def column_mate(n):
    z, y, x, core = torus_place()
    other = lax.rem(z * 2 + y + n, SHARES)
    return torus_device(other // 2, lax.rem(other, 2), x, core)


def gather_barrier():
    z, y, x, core = torus_place()
    barrier = pltpu.get_barrier_semaphore()
    mates = [torus_device(z, y, x, 1 - core), torus_device(z, y, 1 - x, core)]
    for mate in mates + [column_mate(n) for n in range(1, SHARES)]:
        pl.semaphore_signal(barrier, inc=1, device_id=mate, device_id_type=MESH)
    pl.semaphore_wait(barrier, SHARES + 1)


def gather_kernel(
    own_ref, vec_ref, out_ref, vec_out_ref, send_sem, recv_sem, copy_sem, vec_send, vec_recv
):
    z, y, _, _ = torus_place()
    me = z * 2 + y
    gather_barrier()

    def vec_copy(n, slot):
        return pltpu.make_async_remote_copy(
            src_ref=vec_ref, dst_ref=vec_out_ref.at[slot],
            send_sem=vec_send.at[n], recv_sem=vec_recv.at[slot],
            device_id=column_mate(n), device_id_type=MESH,
        )

    for n in range(1, SHARES):
        vec_copy(n, me).start()
    vec_out_ref[me] = vec_ref[...]
    gather_step, turns = gather_steps(own_ref, out_ref, send_sem, recv_sem, copy_sem)

    def step(t, carry):
        gather_step(t)
        return carry

    lax.fori_loop(0, turns, step, 0)
    for n in range(1, SHARES):
        vec_copy(n, me).wait_send()
        vec_copy(n, lax.rem(me + n, SHARES)).wait_recv()


def gather_semaphores(count):
    return [
        pltpu.SemaphoreType.DMA((15, 2)),
        pltpu.SemaphoreType.DMA((16, count)),
        pltpu.SemaphoreType.DMA((2,)),
    ]


def gather_weights(own, vec):
    count, rows, width = own.shape
    hbm = pl.BlockSpec(memory_space=pl.ANY)
    vmem = pl.BlockSpec(memory_space=pltpu.VMEM)
    return pl.pallas_call(
        gather_kernel,
        out_shape=(
            jax.ShapeDtypeStruct((count, SHARES * rows, width), own.dtype),
            jax.ShapeDtypeStruct((SHARES,) + vec.shape, vec.dtype),
        ),
        in_specs=[vmem, vmem],
        out_specs=(hbm, vmem),
        scratch_shapes=gather_semaphores(count)
        + [pltpu.SemaphoreType.DMA((SHARES,)), pltpu.SemaphoreType.DMA((SHARES,))],
        compiler_params=pltpu.CompilerParams(
            collective_id=3, has_side_effects=True, vmem_limit_bytes=60 << 20
        ),
        name="gather_weights",
    )(own, vec)


def adam_step(weight, grad, first, second, count):
    first = BETA_FIRST * first + (1.0 - BETA_FIRST) * grad
    second = BETA_SECOND * second + (1.0 - BETA_SECOND) * grad * grad
    fix_first = 1.0 - jnp.power(BETA_FIRST, count)
    fix_second = 1.0 - jnp.power(BETA_SECOND, count)
    update = first / fix_first / (jnp.sqrt(second / fix_second) + ADAM_EPS) + WEIGHT_DECAY * weight
    return (weight - ADAM_RATE * update, first, second)


def split_halves(values, half_size):
    block_count, row_count, feature_dim = values.shape
    return values.reshape(block_count, row_count, 2, half_size)


def finish_kernel(
    facts_ref, wide_ref, own_ref, left_add_ref, right_add_ref, step_ref, enc_ref, left_ref, right_ref,
    new_ref, grad_ref, new_left_ref, new_right_ref
):
    factor = facts_ref[2:3, 0:1]
    share = 0.5 * factor * factor
    new_ref[...] = enc_ref[...] - step_ref[...] * wide_ref[...]
    grad_ref[...] = own_ref[...] * factor
    new_left_ref[...] = 0.5 * left_ref[...] + share * left_add_ref[...]
    new_right_ref[...] = 0.5 * right_ref[...] + share * right_add_ref[...]


def finish_blocks(facts, wide_scale, *arrays):
    count, rows, width = arrays[0].shape
    block = pl.BlockSpec((None, rows, width), lambda b: (b, 0, 0))
    return pl.pallas_call(
        finish_kernel,
        grid=(count,),
        out_shape=(jax.ShapeDtypeStruct((count, rows, width), jnp.float32),) * 4,
        in_specs=[
            pl.BlockSpec(facts.shape, lambda b: (0, 0)),
            pl.BlockSpec((None, 1, width), lambda b: (b, 0, 0)),
        ]
        + [block] * len(arrays),
        out_specs=(block,) * 4,
        compiler_params=pltpu.CompilerParams(vmem_limit_bytes=32 << 20),
        name="finish_blocks",
    )(facts, wide_scale, *arrays)


def adam_kernel(
    facts_ref, fixes_ref, weight_ref, grad_ref, first_ref, second_ref,
    new_ref, new_first_ref, new_second_ref
):
    grad = grad_ref[...] * facts_ref[2:3, 0:1]
    weight = weight_ref[...]
    first = BETA_FIRST * first_ref[...] + (1.0 - BETA_FIRST) * grad
    second = BETA_SECOND * second_ref[...] + (1.0 - BETA_SECOND) * grad * grad
    root = jnp.sqrt(second / fixes_ref[1:2, 0:1]) + ADAM_EPS
    update = first / fixes_ref[0:1, 0:1] / root + WEIGHT_DECAY * weight
    new_ref[...] = weight - ADAM_RATE * update
    new_first_ref[...] = first
    new_second_ref[...] = second


def adam_rows(facts, fixes, *arrays):
    rows, width = arrays[0].shape
    block = pl.BlockSpec((8, width), lambda r: (r, 0))
    small = pl.BlockSpec(facts.shape, lambda r: (0, 0))
    return pl.pallas_call(
        adam_kernel,
        grid=(rows // 8,),
        out_shape=(jax.ShapeDtypeStruct((rows, width), jnp.float32),) * 3,
        in_specs=[small, small] + [block] * 4,
        out_specs=(block,) * 3,
        compiler_params=pltpu.CompilerParams(vmem_limit_bytes=32 << 20),
        name="adam_rows",
    )(facts, fixes, *arrays)


def reduced_half(values, half_groups):
    part = lax.psum_scatter(values, ("dp", "cls"), scatter_dimension=1, tiled=True)
    return lax.all_gather(part, ("dp", "cls"), axis=1, tiled=True, axis_index_groups=half_groups)


def preconditioned_rows(grad_half, root_left, right_half, own_start):
    count, row_count, width = root_left.shape
    half_size = width // 2
    block_rows = lax.dynamic_slice_in_dim(grad_half, own_start, row_count, 1)
    grad_quads = split_halves(grad_half, half_size)
    rows_quads = split_halves(block_rows, half_size)
    cols_quads = lax.dynamic_slice_in_dim(grad_quads, own_start, row_count, 3)
    precise = FULL_PRECISION
    left_add = jnp.einsum("brjk,bljk->brjl", rows_quads, grad_quads, precision=precise)
    right_add = jnp.einsum("bkja,bkjm->bajm", cols_quads, grad_quads, precision=precise)
    direction = jnp.einsum(
        "brjk,bkjm->brjm", split_halves(root_left, half_size), grad_quads, precision=precise
    )
    direction = jnp.einsum(
        "brjk,bkjm->brjm", direction, split_halves(right_half, half_size), precision=precise
    )
    flat = (count, row_count, width)
    return left_add.reshape(flat), right_add.reshape(flat), direction.reshape(flat), block_rows


def on_device(
    patches,
    image_ids,
    keep,
    labels,
    owner,
    step,
    enc_weights,
    stats_left,
    stats_right,
    root_left,
    root_right,
    head_weights,
    head_m,
    head_v,
    vectors,
    vec_m,
    vec_v,
):
    dp_count = lax.axis_size("dp")
    cls_count = lax.axis_size("cls")
    dp_index = lax.axis_index("dp")
    cls_index = lax.axis_index("cls")
    block_count, row_count, feature_dim = enc_weights.shape
    up_count = (block_count - 5) // 2
    half_size = feature_dim // 2
    part_rows = row_count // cls_count
    half_dp = dp_count // 2
    half_group = half_dp * cls_count
    half_groups = [
        list(range(half_group)),
        list(range(half_group, 2 * half_group)),
    ]

    def my_part(values):
        return lax.dynamic_slice_in_dim(values, cls_index * part_rows, part_rows, 1)

    on_torus = dp_count == 8 and cls_count == 4
    if on_torus:
        vec_block = jnp.pad(vectors, ((0, -vectors.shape[0] % 8), (0, -row_count % 128)))
        own_low = enc_weights.astype(jnp.bfloat16)
        blocks, vec_blocks = gather_weights(own_low, vec_block)
        right_part, vec_blocks = lax.optimization_barrier((my_part(root_right), vec_blocks))
        vec_low = jnp.transpose(vec_blocks[:, : vectors.shape[0], :row_count], (1, 0, 2))
        vec_all = lax.reduce_precision(vec_low.reshape(vectors.shape[0], feature_dim), 8, 7)
    else:
        right_part = my_part(root_right)
        blocks = lax.all_gather(
            my_part(enc_weights.astype(jnp.bfloat16)), ("dp", "cls"), axis=1, tiled=True
        )
        vec_low = lax.all_gather(vectors.astype(jnp.bfloat16), "dp", axis=1, tiled=True)
        vec_all = vec_low.astype(jnp.float32)
    head_low = lax.all_gather(head_weights.astype(jnp.bfloat16), "dp", axis=0, tiled=True)
    final_gain = vec_all[9 + up_count]
    final_shift = vec_all[10 + up_count]
    pack_ids, pack_keep = image_ids[0], keep[0]
    key_codes = jnp.where(pack_keep == 1, pack_ids, -1)

    output, saved = layer_forward(blocks, vec_all, patches, pack_ids, key_codes)
    if on_torus:
        right_codes = lax.all_gather(
            encode_roots(right_part), ("dp", "cls"), axis=0, axis_index_groups=half_groups
        )
    else:
        right_half = lax.all_gather(
            right_part, ("dp", "cls"), axis=1, tiled=True, axis_index_groups=half_groups
        )
    pooled = pool_rows(output, final_gain, final_shift, pack_ids, pack_keep)
    class_dev = head_low.shape[1]
    image_total = labels.shape[0] * dp_count
    if on_torus:
        grad_pooled, own_rows, loss_rows = classify(
            lax.reduce_precision(pooled, 8, 7), labels, head_low, cls_count, image_total
        )
        loss_part = loss_rows[0, 0]
    else:
        group = lax.all_gather(pooled.astype(jnp.bfloat16), "cls", axis=0, tiled=True)
        logits = jnp.dot(group, head_low, preferred_element_type=jnp.float32)
        class_ids = cls_index * class_dev + jnp.arange(class_dev)
        valid = class_ids[None, :] < LABELS_REAL
        target = jnp.any(labels[:, :, None] == class_ids[None, None, :], 1).astype(jnp.float32)
        terms = jax.nn.softplus(logits) - target * logits
        loss_part = jnp.sum(jnp.where(valid, terms, 0.0)) / image_total
        grad_logits = jnp.where(valid, jax.nn.sigmoid(logits) - target, 0.0) / image_total
        grad_logits = grad_logits.astype(jnp.bfloat16)
        group_grad = jnp.einsum(
            "gc,dc->gd", grad_logits, head_low, preferred_element_type=jnp.float32
        )
        grad_pooled = lax.psum_scatter(group_grad, "cls", scatter_dimension=0, tiled=True)
        own_rows = jnp.concatenate([group, grad_logits], 1)

    def pool_local(rows_in, gain, shift):
        return pool_rows(rows_in, gain, shift, pack_ids, pack_keep)

    pool_back = jax.vjp(pool_local, output, final_gain, final_shift)[1]
    grad_output, grad_gain, grad_shift = pool_back(grad_pooled)
    lefts, rights, mlp_grads, grad_vectors, (own_rows, roots) = layer_backward(
        blocks,
        vec_all,
        patches,
        saved,
        pack_ids,
        key_codes,
        grad_output,
        grad_gain,
        grad_shift,
        (own_rows, right_codes if on_torus else right_half),
    )
    head_rows = lax.all_gather(own_rows, "dp", axis=0, tiled=True)
    pooled_all = head_rows[:, :feature_dim]
    grad_logits_all = head_rows[:, feature_dim : feature_dim + class_dev]
    pooled_mine = lax.dynamic_slice_in_dim(pooled_all, dp_index * row_count, row_count, 1)
    head_grad = jnp.einsum(
        "gr,gc->rc", pooled_mine, grad_logits_all, preferred_element_type=jnp.float32
    )

    head_squares = jnp.sum(head_grad * head_grad)
    if on_torus:
        padded = jnp.pad(grad_vectors, ((0, -grad_vectors.shape[0] % 8), (0, 0)))
        tail = jnp.pad(jnp.stack([head_squares, loss_part])[:, None], ((0, 6), (0, 127)))
        block_rows, left_add, right_add, direction, wide_scale, facts, vector_sum = (
            reduce_gradients(
                mlp_grads, lefts, rights, padded, tail, root_left, roots,
                dp_count, cls_count,
            )
        )
        vector_sum = vector_sum[: grad_vectors.shape[0]]
        loss, grad_norm, factor = facts[0, 0], facts[1, 0], facts[2, 0]
    else:
        over_rows = "td,te->de"
        first_grads = [
            jnp.einsum(over_rows, left, right, preferred_element_type=jnp.float32)[None]
            for left, right in (
                (lefts[0], rights[0]),
                (lefts[1], rights[1][0]),
                (lefts[1], rights[1][1]),
                (lefts[1], rights[1][2]),
                (lefts[2], rights[2]),
            )
        ]
        grad_half = reduced_half(jnp.concatenate(first_grads + list(mlp_grads), 0), half_groups)
        vector_sum = lax.psum(grad_vectors, ("dp", "cls"))
        left_add, right_add, direction, block_rows = preconditioned_rows(
            grad_half, root_left, roots, (dp_index % half_dp) * row_count
        )
        squares = jnp.sum(split_halves(direction * direction, half_size), (1, 3))
        in_top = (dp_index < half_dp).astype(jnp.float32)
        once = (cls_index == 0).astype(jnp.float32)
        all_squares = head_squares + once * jnp.sum(block_rows * block_rows)
        packed = jnp.concatenate(
            [
                (once * in_top * squares).reshape(-1),
                (once * (1.0 - in_top) * squares).reshape(-1),
                jnp.stack([all_squares, loss_part]),
            ]
        )
        packed = lax.psum(packed, ("dp", "cls"))
        loss = packed[4 * block_count + 1]
        all_squares = packed[4 * block_count]
        sums = packed[: 4 * block_count].reshape(2, block_count, 2)
        block_squares = jnp.where(dp_index < half_dp, sums[0], sums[1])
        grad_norm = jnp.sqrt(all_squares + jnp.sum(vector_sum * vector_sum))
        factor = CLIP_NORM / jnp.maximum(grad_norm, CLIP_NORM)
        mean_squares = block_squares / (half_size * half_size) * factor * factor
        scale = SHAMPOO_RATE * factor * lax.rsqrt(mean_squares + ROOT_EPS)
        wide_scale = jnp.repeat(scale, half_size, axis=1)[:, None, :]
    vector_rows = lax.dynamic_slice_in_dim(vector_sum, dp_index * row_count, row_count, 1)
    count = step.astype(jnp.float32)
    new_vec, new_vec_m, new_vec_v = adam_step(vectors, vector_rows * factor, vec_m, vec_v, count)
    if on_torus:
        new_blocks, block_clip, new_left, new_right = finish_blocks(
            facts, wide_scale, block_rows, left_add, right_add, direction,
            enc_weights, stats_left, stats_right,
        )
        fixes = jnp.stack([1.0 - jnp.power(BETA_FIRST, count), 1.0 - jnp.power(BETA_SECOND, count)])
        fixes = jnp.broadcast_to(jnp.pad(fixes, (0, 6))[:, None], facts.shape)
        new_head, new_head_m, new_head_v = adam_rows(
            facts, fixes, head_weights, head_grad, head_m, head_v
        )
    else:
        block_clip = block_rows * factor
        new_blocks = enc_weights - direction * wide_scale
        square_factor = 0.5 * factor * factor
        new_left = 0.5 * stats_left + square_factor * left_add
        new_right = 0.5 * stats_right + square_factor * right_add
        new_head, new_head_m, new_head_v = adam_step(
            head_weights, head_grad * factor, head_m, head_v, count
        )
    return (
        loss,
        grad_norm,
        new_blocks,
        block_clip,
        new_left,
        new_right,
        new_vec,
        new_vec_m,
        new_vec_v,
        new_head,
        new_head_m,
        new_head_v,
    )


def solution(mesh):
    return jax.shard_map(
        on_device,
        mesh=mesh,
        in_specs=(
            P(("dp", "cls"), None),
            P(("dp", "cls"), None),
            P(("dp", "cls"), None),
            P("dp", None),
            P(),
            P(),
            P(None, "dp", None),
            P(None, "dp", None),
            P(None, "dp", None),
            P(None, "dp", None),
            P(None, "dp", None),
            P("dp", "cls"),
            P("dp", "cls"),
            P("dp", "cls"),
            P(None, "dp"),
            P(None, "dp"),
            P(None, "dp"),
        ),
        out_specs=(
            P(),
            P(),
            P(None, "dp", None),
            P(None, "dp", None),
            P(None, "dp", None),
            P(None, "dp", None),
            P(None, "dp"),
            P(None, "dp"),
            P(None, "dp"),
            P("dp", "cls"),
            P("dp", "cls"),
            P("dp", "cls"),
        ),
        check_vma=False,
    )
```

```python
import functools

import jax
import jax.numpy as jnp
from jax import lax
from jax.experimental import pallas as pl
from jax.experimental.pallas import tpu as pltpu
from jax.sharding import PartitionSpec as P

HEADS = 12
HEAD = 64
LABELS_REAL = 21843
IMAGE_MAX = 196
QTILE = 256
PAIR = 2 * HEAD
ROWS = 256
HIDDEN_TILE = 384
MESH = pl.DeviceIdType.MESH
CODE_TOP = 32766.0
CODE_FLOOR = 1e-33
PIECE = 48
FEATURE_TILE = 128
SPAN = 48
SHARES = 8
GATHER_DEPTH = 4
CLASS_TILE = 512
IMG_PACK = 8


FULL_PRECISION = lax.Precision.HIGHEST
NORM_EPS = 1e-06
CLIP_NORM = 1.0
ADAM_RATE = 0.02
SHAMPOO_RATE = 0.01
BETA_FIRST = 0.9
BETA_SECOND = 0.999
ADAM_EPS = 1e-08
WEIGHT_DECAY = 0.1
ROOT_EPS = 1e-06


def norm_rows(values, gain, shift):
    centred = values - jnp.mean(values, -1, keepdims=True)
    spread = jnp.mean(centred * centred, -1, keepdims=True)
    return centred * lax.rsqrt(spread + NORM_EPS) * gain + shift


def pool_rows(output, gain, shift, pack_ids, pack_keep):
    final = norm_rows(output, gain, shift)
    member = (
        (pack_ids[None, :] == jnp.arange(IMG_PACK)[:, None]) & (pack_keep[None, :] == 1)
    ).astype(jnp.float32)
    counted = jnp.maximum(jnp.sum(member, 1), 1.0)
    return jnp.dot(member, final, precision=FULL_PRECISION) / counted[:, None]


def key_window(tile, length):
    reach = -(-(IMAGE_MAX - 1) // 128) * 128
    low = max(0, tile * QTILE - reach)
    high = min(length, (tile + 1) * QTILE + reach)
    return low, high


def attention_bias(qids_ref, kcodes_ref, bias_ref):
    length = qids_ref.shape[0]

    @pl.when(pl.program_id(0) == 0)
    def _():
        for tile in range(length // QTILE):
            low, high = key_window(tile, length)
            shape = (QTILE, high - low)
            rows = lax.broadcasted_iota(jnp.int32, shape, 0) + tile * QTILE
            cols = lax.broadcasted_iota(jnp.int32, shape, 1) + low
            same = qids_ref[tile * QTILE : (tile + 1) * QTILE, :] == kcodes_ref[:, low:high]
            bias_ref[tile, :, : high - low] = jnp.where(same | (rows == cols), 0.0, -1e30)


def attention_tile(tile, q_ref, k_ref, v_ref, out_ref, bias_ref):
    lane = lax.broadcasted_iota(jnp.int32, (QTILE, PAIR), 1)
    low, high = key_window(tile, q_ref.shape[0])
    rows = pl.ds(tile * QTILE, QTILE)
    queries = q_ref[rows, :] * jnp.bfloat16(HEAD ** (-0.5))
    keys = k_ref[low:high, :]
    values = v_ref[low:high, :]
    halves = []
    for head in range(2):
        mine = (lane >= head * HEAD) & (lane < (head + 1) * HEAD)
        picked = jnp.where(mine, queries, jnp.zeros_like(queries))
        scores = lax.dot_general(
            picked, keys, (((1,), (1,)), ((), ())), preferred_element_type=jnp.float32
        )
        scores = scores + bias_ref[tile, :, : high - low]
        top = jnp.max(scores, -1, keepdims=True)
        weights = jnp.exp(scores - top)
        probs = weights * (1.0 / jnp.sum(weights, -1, keepdims=True))
        halves.append(
            jnp.dot(probs.astype(jnp.bfloat16), values, preferred_element_type=jnp.float32)
        )
    out_ref[rows, :] = jnp.where(lane < HEAD, halves[0], halves[1]).astype(jnp.bfloat16)


def attention_forward_kernel(qids_ref, kcodes_ref, q_ref, k_ref, v_ref, out_ref, bias_ref):
    attention_bias(qids_ref, kcodes_ref, bias_ref)
    for tile in range(q_ref.shape[0] // QTILE):
        attention_tile(tile, q_ref, k_ref, v_ref, out_ref, bias_ref)


def attention_back_bias(qids_ref, kcodes_ref, bias_ref):
    length = kcodes_ref.shape[0]

    @pl.when(pl.program_id(0) == 0)
    def _():
        for tile in range(length // QTILE):
            low, high = key_window(tile, length)
            shape = (high - low, QTILE)
            rows = lax.broadcasted_iota(jnp.int32, shape, 0) + low
            cols = lax.broadcasted_iota(jnp.int32, shape, 1) + tile * QTILE
            same = kcodes_ref[low:high, :] == qids_ref[:, tile * QTILE : (tile + 1) * QTILE]
            bias_ref[tile, : high - low, :] = jnp.where(same | (rows == cols), 0.0, -1e30)


def attention_back_tile(tile, q_ref, k_ref, v_ref, do_ref, out_ref, bias_ref, dk_ref, dv_ref):
    length = q_ref.shape[0]
    lane = lax.broadcasted_iota(jnp.int32, (QTILE, PAIR), 1)
    scale = jnp.bfloat16(HEAD ** (-0.5))
    low, high = key_window(tile, length)
    rows = pl.ds(tile * QTILE, QTILE)
    window = pl.ds(low, high - low)
    queries = q_ref[rows, :] * scale
    keys = k_ref[window, :]
    values = v_ref[window, :]
    grads = do_ref[rows, :]
    halves = []
    for head in range(2):
        mine = (lane >= head * HEAD) & (lane < (head + 1) * HEAD)
        picked = jnp.where(mine, queries, jnp.zeros_like(queries))
        picked_grads = jnp.where(mine, grads, jnp.zeros_like(grads))
        scores = lax.dot_general(
            keys, picked, (((1,), (1,)), ((), ())), preferred_element_type=jnp.float32
        )
        scores = scores + bias_ref[tile, : high - low, :]
        top = jnp.max(scores, 0, keepdims=True)
        weights = jnp.exp(scores - top)
        probs = weights * (1.0 / jnp.sum(weights, 0, keepdims=True))
        grad_probs = lax.dot_general(
            values, picked_grads, (((1,), (1,)), ((), ())), preferred_element_type=jnp.float32
        )
        inner = jnp.sum(probs * grad_probs, 0, keepdims=True)
        grad_scores = (probs * (grad_probs - inner)).astype(jnp.bfloat16)
        dv_ref[window, :] += jnp.dot(
            probs.astype(jnp.bfloat16), picked_grads, preferred_element_type=jnp.float32
        )
        dk_ref[window, :] += jnp.dot(
            grad_scores, picked, preferred_element_type=jnp.float32
        )
        halves.append(
            lax.dot_general(
                grad_scores,
                keys,
                (((0,), (0,)), ((), ())),
                preferred_element_type=jnp.float32,
            )
        )
    grad_queries = jnp.where(lane < HEAD, halves[0], halves[1]) * HEAD ** (-0.5)
    out_ref[0, rows, :] = grad_queries.astype(jnp.bfloat16)


def attention_backward_kernel(
    qids_ref, kcodes_ref, q_ref, k_ref, v_ref, do_ref, out_ref, bias_ref, dk_ref, dv_ref
):
    attention_back_bias(qids_ref, kcodes_ref, bias_ref)
    dk_ref[...] = jnp.zeros_like(dk_ref)
    dv_ref[...] = jnp.zeros_like(dv_ref)
    for tile in range(q_ref.shape[0] // QTILE):
        attention_back_tile(tile, q_ref, k_ref, v_ref, do_ref, out_ref, bias_ref, dk_ref, dv_ref)
    out_ref[1] = dk_ref[...].astype(jnp.bfloat16)
    out_ref[2] = dv_ref[...].astype(jnp.bfloat16)


def pair_spec(length, part=None):
    if part is None:
        return pl.BlockSpec((length, PAIR), lambda pair: (0, pair))
    return pl.BlockSpec((None, length, PAIR), lambda pair: (part, 0, pair))


def whole_spec(shape):
    return pl.BlockSpec(shape, lambda pair: (0,) * len(shape))


def bias_shape(length):
    tiles = length // QTILE
    window = max(high - low for low, high in (key_window(t, length) for t in range(tiles)))
    return tiles, QTILE, window


def attention_forward(qkv_rows, pack_ids, key_codes):
    _, length, width = qkv_rows.shape
    return pl.pallas_call(
        attention_forward_kernel,
        grid=(width // PAIR,),
        out_shape=jax.ShapeDtypeStruct((length, width), jnp.bfloat16),
        in_specs=[whole_spec((length, 1)), whole_spec((1, length))]
        + [pair_spec(length, part) for part in range(3)],
        out_specs=pair_spec(length),
        scratch_shapes=[pltpu.VMEM(bias_shape(length), jnp.float32)],
        compiler_params=pltpu.CompilerParams(vmem_limit_bytes=40 << 20),
        name="attention_forward",
    )(pack_ids[:, None], key_codes[None, :], qkv_rows, qkv_rows, qkv_rows)


def attention_backward(qkv_rows, pack_ids, key_codes, grad_attended):
    _, length, width = qkv_rows.shape
    tiles = length // QTILE
    window = max(high - low for low, high in (key_window(t, length) for t in range(tiles)))
    return pl.pallas_call(
        attention_backward_kernel,
        grid=(width // PAIR,),
        out_shape=jax.ShapeDtypeStruct((3, length, width), jnp.bfloat16),
        in_specs=[whole_spec((1, length)), whole_spec((length, 1))]
        + [pair_spec(length, part) for part in range(3)]
        + [pair_spec(length)],
        out_specs=pl.BlockSpec((3, length, PAIR), lambda pair: (0, 0, pair)),
        scratch_shapes=[
            pltpu.VMEM((tiles, window, QTILE), jnp.float32),
            pltpu.VMEM((length, PAIR), jnp.float32),
            pltpu.VMEM((length, PAIR), jnp.float32),
        ],
        compiler_params=pltpu.CompilerParams(vmem_limit_bytes=40 << 20),
        name="attention_backward",
    )(pack_ids[None, :], key_codes[:, None], qkv_rows, qkv_rows, qkv_rows, grad_attended)


def mlp_forward_kernel(x_ref, up_ref, bias_ref, down_ref, units_ref, slope_ref, out_ref):
    first = pl.program_id(0) == 0

    @pl.when(first)
    def _():
        out_ref[...] = jnp.zeros_like(out_ref)

    for start in range(0, x_ref.shape[0], ROWS):
        rows = pl.ds(start, ROWS)
        pre = jnp.dot(x_ref[rows, :], up_ref[...], preferred_element_type=jnp.float32)
        pre = pre + bias_ref[...]
        half = 0.5 + 0.5 * lax.erf(pre * 0.7071067811865476)
        bell = jnp.exp(-0.5 * pre * pre) * 0.3989422804014327
        units = (pre * half).astype(jnp.bfloat16)
        units_ref[rows, :] = units
        slope_ref[rows, :] = half + pre * bell
        out_ref[rows, :] += jnp.dot(units, down_ref[...], preferred_element_type=jnp.float32)


def mlp_backward_kernel(
    x_ref, dm_ref, up_ref, down_ref, units_ref, slope_ref,
    grad_up_ref, grad_down_ref, bias_ref, dx_ref, dpre_ref
):
    @pl.when(pl.program_id(0) == 0)
    def _():
        dx_ref[...] = jnp.zeros_like(dx_ref)

    total = jnp.zeros((1, HIDDEN_TILE), jnp.float32)
    for start in range(0, x_ref.shape[0], ROWS):
        rows = pl.ds(start, ROWS)
        units_back = lax.dot_general(
            dm_ref[rows, :], down_ref[...], (((1,), (1,)), ((), ())),
            preferred_element_type=jnp.float32,
        )
        grad_pre = (units_back * slope_ref[rows, :]).astype(jnp.bfloat16)
        dpre_ref[rows, :] = grad_pre
        total = total + jnp.sum(grad_pre.astype(jnp.float32), 0, keepdims=True)
        dx_ref[rows, :] += lax.dot_general(
            grad_pre, up_ref[...], (((1,), (1,)), ((), ())), preferred_element_type=jnp.float32
        )
    bias_ref[...] = total
    over_rows = (((0,), (0,)), ((), ()))
    grad_down_ref[...] = lax.dot_general(
        units_ref[...], dm_ref[...], over_rows, preferred_element_type=jnp.float32
    )
    grad_up_ref[...] = lax.dot_general(
        x_ref[...], dpre_ref[...], over_rows, preferred_element_type=jnp.float32
    )


def mlp_specs(length, width, up_count):
    split = width // HIDDEN_TILE
    resident = pl.BlockSpec((length, width), lambda t: (0, 0))
    up = pl.BlockSpec((None, width, HIDDEN_TILE), lambda t: (t // split, 0, t % split))
    down = pl.BlockSpec(
        (None, HIDDEN_TILE, width), lambda t: (up_count + t // split, t % split, 0)
    )
    hidden = pl.BlockSpec((length, HIDDEN_TILE), lambda t: (0, t))
    bias = pl.BlockSpec((1, HIDDEN_TILE), lambda t: (0, t))
    return split, resident, up, down, hidden, bias


def mlp_forward(rows, blocks, up_bias):
    length, width = rows.shape
    up_count = blocks.shape[0] // 2
    split, resident, up, down, hidden, bias = mlp_specs(length, width, up_count)
    hidden_size = up_count * width
    return pl.pallas_call(
        mlp_forward_kernel,
        grid=(up_count * split,),
        out_shape=(
            jax.ShapeDtypeStruct((length, hidden_size), jnp.bfloat16),
            jax.ShapeDtypeStruct((length, hidden_size), jnp.float32),
            jax.ShapeDtypeStruct((length, width), jnp.float32),
        ),
        in_specs=[resident, up, bias, down],
        out_specs=(hidden, hidden, resident),
        compiler_params=pltpu.CompilerParams(vmem_limit_bytes=48 << 20),
        name="mlp_forward",
    )(rows, blocks, up_bias.reshape(1, hidden_size), blocks)


def mlp_backward(rows, grad_branch, blocks, units, slopes):
    length, width = rows.shape
    up_count = blocks.shape[0] // 2
    split, resident, up, down, hidden, bias = mlp_specs(length, width, up_count)
    hidden_size = up_count * width
    return pl.pallas_call(
        mlp_backward_kernel,
        grid=(up_count * split,),
        out_shape=(
            jax.ShapeDtypeStruct((up_count, width, width), jnp.float32),
            jax.ShapeDtypeStruct((up_count, width, width), jnp.float32),
            jax.ShapeDtypeStruct((1, hidden_size), jnp.float32),
            jax.ShapeDtypeStruct((length, width), jnp.float32),
        ),
        in_specs=[resident, resident, up, down, hidden, hidden],
        out_specs=(
            pl.BlockSpec((None, width, HIDDEN_TILE), lambda t: (t // split, 0, t % split)),
            pl.BlockSpec((None, HIDDEN_TILE, width), lambda t: (t // split, t % split, 0)),
            bias,
            resident,
        ),
        scratch_shapes=[pltpu.VMEM((length, HIDDEN_TILE), jnp.bfloat16)],
        compiler_params=pltpu.CompilerParams(vmem_limit_bytes=48 << 20),
        name="mlp_backward",
    )(rows, grad_branch, blocks, blocks, units, slopes)


def layer_forward(blocks, vec_all, patch, attend):
    embedded = jnp.dot(patch, blocks[0], preferred_element_type=jnp.float32) + vec_all[0]
    normed_one = norm_rows(embedded, vec_all[1], vec_all[2]).astype(jnp.bfloat16)
    qkv_rows = jnp.einsum(
        "td,kde->kte", normed_one, blocks[1:4], preferred_element_type=jnp.float32
    )
    qkv_bias = jnp.stack([vec_all[3], jnp.zeros_like(vec_all[3]), vec_all[4]])
    qkv_rows = (qkv_rows + qkv_bias[:, None, :]).astype(jnp.bfloat16)
    attended, mlp_blocks = attend(qkv_rows)
    up_count = mlp_blocks.shape[0] // 2
    hidden = (
        embedded + jnp.dot(attended, blocks[4], preferred_element_type=jnp.float32) + vec_all[5]
    )
    normed_two = norm_rows(hidden, vec_all[6], vec_all[7]).astype(jnp.bfloat16)
    units, slopes, branch = mlp_forward(normed_two, mlp_blocks, vec_all[8 : 8 + up_count])
    output = hidden + branch + vec_all[8 + up_count]
    return (
        output,
        mlp_blocks,
        (embedded, normed_one, qkv_rows, attended, hidden, normed_two, slopes, units),
    )


def layer_backward(
    blocks,
    mlp_blocks,
    vec_all,
    patch,
    saved,
    pack_ids,
    key_codes,
    grad_output,
    grad_gain,
    grad_shift,
    released,
):
    embedded, normed_one, qkv_rows, attended, hidden, normed_two, slopes, units = saved
    feature_dim = patch.shape[1]
    up_count = mlp_blocks.shape[0] // 2
    grad_branch = grad_output.astype(jnp.bfloat16)
    grad_up, grad_down, up_sums, grad_normed_two = mlp_backward(
        normed_two, grad_branch, mlp_blocks, units, slopes
    )
    up_sums, released = lax.optimization_barrier((up_sums, released))
    norm_two_back = jax.vjp(norm_rows, hidden, vec_all[6], vec_all[7])[1]
    grad_hidden_norm, grad_gain_two, grad_shift_two = norm_two_back(grad_normed_two)
    grad_hidden = grad_output + grad_hidden_norm
    grad_attn_out = grad_hidden.astype(jnp.bfloat16)
    grad_attended = jnp.einsum(
        "td,ed->te", grad_attn_out, blocks[4], preferred_element_type=jnp.float32
    ).astype(jnp.bfloat16)
    grad_qkv = attention_backward(qkv_rows, pack_ids, key_codes, grad_attended)
    grad_normed_one = jnp.einsum(
        "kte,kde->td", grad_qkv, blocks[1:4], preferred_element_type=jnp.float32
    )
    norm_one_back = jax.vjp(norm_rows, embedded, vec_all[1], vec_all[2])[1]
    grad_embed_norm, grad_gain_one, grad_shift_one = norm_one_back(grad_normed_one)
    grad_embedded = (grad_hidden + grad_embed_norm).astype(jnp.bfloat16)
    lefts = (patch, normed_one, attended)
    rights = (grad_embedded, grad_qkv, grad_attn_out)
    bias_sums = jnp.stack(
        [
            jnp.sum(grad_embedded.astype(jnp.float32), 0),
            grad_gain_one,
            grad_shift_one,
            jnp.sum(grad_qkv[0].astype(jnp.float32), 0),
            jnp.sum(grad_qkv[2].astype(jnp.float32), 0),
            jnp.sum(grad_attn_out.astype(jnp.float32), 0),
            grad_gain_two,
            grad_shift_two,
        ]
    )
    up_sums = up_sums.reshape(up_count, feature_dim)
    tail_sums = jnp.stack([jnp.sum(grad_branch.astype(jnp.float32), 0), grad_gain, grad_shift])
    grad_vectors = jnp.concatenate([bias_sums, up_sums, tail_sums], 0)
    return (lefts, rights, (grad_up, grad_down), grad_vectors, released)


def torus_place():
    dp, cls = lax.axis_index("dp"), lax.axis_index("cls")
    return dp // 2, dp % 2, cls // 2, cls % 2


def torus_device(z, y, x, core):
    return (z * 2 + y, x * 2 + core)


def encode(pieces, code_refs, scale_ref):
    top = None
    for piece in pieces:
        peak = jnp.max(jnp.abs(piece()), 0, keepdims=True)
        top = peak if top is None else jnp.maximum(top, peak)
    top = jnp.maximum(top, CODE_FLOOR)
    inverse = CODE_TOP / top
    for piece, code_ref in zip(pieces, code_refs):
        code_ref[...] = jnp.round(piece() * inverse).astype(jnp.int32).astype(jnp.int16)
    scale_ref[...] = top * (1.0 / CODE_TOP)


def decode(code, scale):
    return code.astype(jnp.int32).astype(jnp.float32) * scale


def reduce_kernel(counts, *refs):
    sources, refs = refs[: len(counts)], refs[len(counts) :]
    (patch_hbm, first_hbm, mid_hbm, dpatch_hbm, dfirst_hbm, dmid_hbm,
     vec_ref, tail_ref, left_hbm, right_hbm,
     own_hbm, left_out_hbm, right_out_hbm, step_hbm, wide_ref, facts_ref, vec_out_ref,
     left_buf, right_buf, right_full, outs_buf, squares, high_buf, low_buf, sum_slots, tail_slots,
     lhs_buf, rhs_buf, pair_sem,
     in_sem, sum_send, sum_recv, tail_send, tail_recv,
     acc, spare, kept, sent0, got0, sent1, got1, sent2, got2, sent3, got3, sent4, got4,
     ss0, gs0, ss1, gs1, ss2, gs2, ss3, gs3, ss4, gs4, codes, scales, vec_got,
     load_sem, out_sem, send_sem, recv_sem, send_scale_sem, recv_scale_sem,
     vec_send_sem, vec_recv_sem) = refs
    stored = sum(counts)
    paired = dfirst_hbm.shape[0] + 2
    total = stored + paired
    half, width = codes.shape[1], codes.shape[2]
    cols = width // 2
    z, y, x, core = torus_place()
    upper = z // 2
    inner = (z % 2) != upper
    mate_core = torus_device(z, y, x, 1 - core)
    mate_x = torus_device(z, y, 1 - x, core)
    mate_y = torus_device(z, 1 - y, x, core)
    mate_z = torus_device(z + 1 - 2 * (z % 2), y, x, core)
    mate_mid = torus_device(3 - z, y, x, core)
    mate_far = torus_device((z + 2) % 4, y, x, core)

    barrier = pltpu.get_barrier_semaphore()
    dp, cls = lax.axis_index("dp"), lax.axis_index("cls")
    everyone = tail_slots.shape[0]
    quarter = sum_slots.shape[0]
    me = dp * 4 + cls

    def any_mate(n):
        other = lax.rem(me + n, everyone)
        return (other // 4, lax.rem(other, 4))

    def half_mate(n):
        return (upper * quarter + lax.rem(dp + n, quarter), cls)

    for n in range(1, everyone):
        pl.semaphore_signal(barrier, inc=1, device_id=any_mate(n), device_id_type=MESH)
    pl.semaphore_wait(barrier, everyone - 1)
    own = lax.rem(dp, quarter) * left_buf.shape[1]

    own_cols = pl.ds(pl.multiple_of(core * cols, 128), cols)
    other_cols = pl.ds(pl.multiple_of((1 - core) * cols, 128), cols)

    def rows_at(start, size):
        return pl.ds(pl.multiple_of(start, PIECE), size)

    def loads(m, body):
        start = 0
        for source, count in zip(sources, counts):
            def one(source=source, start=start):
                pair = (
                    pltpu.make_async_copy(
                        source.at[m - start, :, own_cols], acc.at[m % 5], load_sem.at[m % 2, 0]
                    ),
                    pltpu.make_async_copy(
                        source.at[m - start, :, other_cols], spare.at[m % 2], load_sem.at[m % 2, 1]
                    ),
                )
                for copy in pair:
                    body(copy)

            pl.when((m >= start) & (m < start + count))(one)
            start += count

    def block_of(m):
        return lax.rem(m + paired, total)

    def pair_loads(m, body):
        index = m - stored
        last = paired - 1

        def run(left, right):
            body(pltpu.make_async_copy(left, lhs_buf.at[m % 2], pair_sem.at[m % 2, 0]))
            body(pltpu.make_async_copy(right, rhs_buf.at[m % 2], pair_sem.at[m % 2, 1]))

        pl.when(index == 0)(lambda: run(patch_hbm, dpatch_hbm))
        pl.when((index > 0) & (index < last))(
            lambda: run(first_hbm, dfirst_hbm.at[jnp.clip(index - 1, 0, last - 2)])
        )
        pl.when(index == last)(lambda: run(mid_hbm, dmid_hbm))

    def pair_product(m):
        chunk = 2 * FEATURE_TILE
        for r in range(0, width, chunk):
            left = lhs_buf[m % 2, :, r : r + chunk].T
            for target, columns in ((acc.at[m % 5], own_cols), (spare.at[m % 2], other_cols)):
                target[r : r + chunk, :] = jnp.dot(
                    left, rhs_buf[m % 2, :, columns], preferred_element_type=jnp.float32
                )

    def message(stage, m, source, scale_source, target, scale_target, mate):
        return (
            pltpu.make_async_remote_copy(
                src_ref=source, dst_ref=target,
                send_sem=send_sem.at[stage, m % 2], recv_sem=recv_sem.at[stage, m],
                device_id=mate, device_id_type=MESH,
            ),
            pltpu.make_async_remote_copy(
                src_ref=scale_source, dst_ref=scale_target,
                send_sem=send_scale_sem.at[stage, m % 2], recv_sem=recv_scale_sem.at[stage, m],
                device_id=mate, device_id_type=MESH,
            ),
        )

    def first(m):
        return message(0, m, sent0.at[m % 2], ss0.at[m % 2], got0.at[m], gs0.at[m], mate_core)

    def second(m, b):
        return message(
            1 + b, m, sent1.at[m % 2, b], ss1.at[m % 2, b], got1.at[m, b], gs1.at[m, b],
            mate_y if b else mate_x,
        )

    def third(m, b):
        return message(
            3 + b, m, sent2.at[m % 2, b], ss2.at[m % 2, b], got2.at[m, b], gs2.at[m, b],
            mate_x if b else mate_y,
        )

    def fourth(m):
        return message(5, m, sent3.at[m % 2], ss3.at[m % 2], got3.at[m], gs3.at[m], mate_z)

    def fifth(m):
        return message(6, m, sent4.at[m % 2], ss4.at[m % 2], got4.at[m], gs4.at[m], mate_mid)

    piece_a = 2 * x + y
    piece_b = 4 + 2 * y + x

    def spread(stage, m, piece, count, mate, columns=own_cols):
        rows = pl.ds(pl.multiple_of(piece * PIECE, PIECE), count * PIECE)
        block = codes.at[m, rows, columns]
        scale = scales.at[m, pl.ds(piece, count), :, columns]
        return message(stage, m, block, scale, block, scale, mate)

    def start(copies):
        for copy in copies:
            copy.start()

    def wait_send(copies):
        for copy in copies:
            copy.wait_send()

    def wait_recv(copies):
        for copy in copies:
            copy.wait_recv()

    def vec_copy(step, mate):
        return pltpu.make_async_remote_copy(
            src_ref=vec_got.at[step, 0], dst_ref=vec_got.at[step, 1],
            send_sem=vec_send_sem.at[step], recv_sem=vec_recv_sem.at[step],
            device_id=mate, device_id_type=MESH,
        )

    vec_mates = (mate_core, mate_x, mate_y, mate_z, mate_far)

    loads(jnp.int32(0), lambda copy: copy.start())
    vec_got[0, 0] = vec_ref[...]
    vec_copy(0, vec_mates[0]).start()

    def step(t, carry):
        for n in range(1, 6):
            @pl.when(t == n)
            def _(n=n):
                vec_copy(n - 1, vec_mates[n - 1]).wait()
                value = vec_got[n - 1, 0] + vec_got[n - 1, 1]
                if n < 5:
                    vec_got[n, 0] = value
                    vec_copy(n, vec_mates[n]).start()
                else:
                    vec_out_ref[...] = value

        @pl.when(t < total)
        def _():
            m = t

            @pl.when(m < stored)
            def _():
                loads(m, lambda copy: copy.wait())

            @pl.when(m + 1 < stored)
            def _():
                loads(m + 1, lambda copy: copy.start())

            @pl.when((m + 1 >= stored) & (m + 1 < total))
            def _():
                pair_loads(m + 1, lambda copy: copy.start())

            @pl.when(m >= stored)
            def _():
                pair_loads(m, lambda copy: copy.wait())
                pair_product(m)

            span = 2 * PIECE
            encode(
                [lambda r=r: spare[m % 2, r : r + span, :] for r in range(0, 2 * half, span)],
                [sent0.at[m % 2, r : r + span, :] for r in range(0, 2 * half, span)],
                ss0.at[m % 2],
            )
            start(first(m))

        @pl.when((t >= 1) & (t < total + 1))
        def _():
            m = t - 1
            copies = first(m)
            wait_send(copies)
            wait_recv(copies)
            slot = m % 5
            span = 2 * PIECE
            for r in range(0, 2 * half, span):
                acc[slot, r : r + span, :] += decode(got0[m, r : r + span, :], gs0[m])
            for b in range(2):
                other = (1 - y) if b else (1 - x)
                begins = [h * half + b * 4 * PIECE + other * span for h in range(2)]
                encode(
                    [lambda s=s: acc[slot, rows_at(s, span), :] for s in begins],
                    [sent1.at[m % 2, b, h] for h in range(2)],
                    ss1.at[m % 2, b],
                )
                start(second(m, b))

        @pl.when((t >= 2) & (t < total + 2))
        def _():
            m = t - 2
            slot = m % 5
            span = 2 * PIECE
            for b in range(2):
                copies = second(m, b)
                wait_send(copies)
                wait_recv(copies)
                mine = y if b else x
                other = (1 - x) if b else (1 - y)
                begins = [h * half + b * 4 * PIECE + mine * span for h in range(2)]
                for h, s in enumerate(begins):
                    acc[slot, rows_at(s, span), :] += decode(got1[m, b, h], gs1[m, b])
                encode(
                    [lambda s=s: acc[slot, rows_at(s + other * PIECE, PIECE), :] for s in begins],
                    [sent2.at[m % 2, b, h] for h in range(2)],
                    ss2.at[m % 2, b],
                )
                start(third(m, b))

        @pl.when((t >= 3) & (t < total + 3))
        def _():
            m = t - 3
            slot = m % 5
            for b in range(2):
                copies = third(m, b)
                wait_send(copies)
                wait_recv(copies)
                place = piece_b if b else piece_a
                for h in range(2):
                    kept[m % 3, h, b] = acc[
                        slot, rows_at(h * half + place * PIECE, PIECE), :
                    ] + decode(got2[m, b, h], gs2[m, b])

            @pl.when(jnp.logical_not(inner))
            def _():
                pairs = [(h, b) for h in range(2) for b in range(2)]
                encode(
                    [lambda h=h, b=b: kept[m % 3, h, b] for h, b in pairs],
                    [sent3.at[m % 2, h, b] for h, b in pairs],
                    ss3.at[m % 2],
                )
                start(fourth(m))

        @pl.when((t >= 4) & (t < total + 4))
        def _():
            m = t - 4
            copies = fourth(m)

            @pl.when(jnp.logical_not(inner))
            def _():
                wait_send(copies)

            @pl.when(inner)
            def _():
                wait_recv(copies)
                for h in range(2):
                    for b in range(2):
                        kept[m % 3, h, b] += decode(got3[m, h, b], gs3[m])
                encode(
                    [lambda b=b: kept[m % 3, 1 - upper, b] for b in range(2)],
                    [sent4.at[m % 2, b] for b in range(2)],
                    ss4.at[m % 2],
                )
                start(fifth(m))

        @pl.when((t >= 5) & (t < total + 5))
        def _():
            m = t - 5

            @pl.when(inner)
            def _():
                copies = fifth(m)
                wait_send(copies)
                wait_recv(copies)
                for b in range(2):
                    place = piece_b if b else piece_a
                    value = kept[m % 3, upper, b] + decode(got4[m, b], gs4[m])
                    encode(
                        [lambda value=value: value],
                        [codes.at[m, rows_at(place * PIECE, PIECE), own_cols]],
                        scales.at[m, place, :, own_cols],
                    )
                    start(spread(7 + b, m, place, 1, mate_z))

        @pl.when((t >= 6) & (t < total + 6))
        def _():
            m = t - 6
            for b in range(2):
                place = piece_b if b else piece_a
                copies = spread(7 + b, m, place, 1, mate_z)

                @pl.when(inner)
                def _(copies=copies):
                    wait_send(copies)

                @pl.when(jnp.logical_not(inner))
                def _(copies=copies):
                    wait_recv(copies)

                start(spread(9 + b, m, place, 1, mate_x if b else mate_y))

        @pl.when((t >= 7) & (t < total + 7))
        def _():
            m = t - 7
            for b in range(2):
                place = piece_b if b else piece_a
                theirs = (4 + 2 * y + 1 - x) if b else (2 * x + 1 - y)
                wait_send(spread(9 + b, m, place, 1, mate_x if b else mate_y))
                wait_recv(spread(9 + b, m, theirs, 1, mate_x if b else mate_y))
                begin = (4 + 2 * y) if b else 2 * x
                start(spread(11 + b, m, begin, 2, mate_y if b else mate_x))

        @pl.when((t >= 8) & (t < total + 8))
        def _():
            m = t - 8
            for b in range(2):
                begin = (4 + 2 * y) if b else 2 * x
                theirs = (4 + 2 * (1 - y)) if b else 2 * (1 - x)
                wait_send(spread(11 + b, m, begin, 2, mate_y if b else mate_x))
                wait_recv(spread(11 + b, m, theirs, 2, mate_y if b else mate_x))
            start(spread(13, m, 0, 8, mate_core))

        def ins(m):
            return (
                pltpu.make_async_copy(
                    left_hbm.at[block_of(m)], left_buf.at[m % 2], in_sem.at[m % 2, 0]
                ),
                pltpu.make_async_copy(
                    right_hbm.at[:, block_of(m)], right_buf.at[m % 2], in_sem.at[m % 2, 1]
                ),
            )

        def outs(m):
            targets = (own_hbm, left_out_hbm, right_out_hbm, step_hbm)
            return [
                pltpu.make_async_copy(
                    outs_buf.at[m % 2, n], target.at[block_of(m)], out_sem.at[m % 2, n]
                )
                for n, target in enumerate(targets)
            ]

        @pl.when((t >= 8) & (t < total + 8))
        def _():
            start(ins(t - 8))

        @pl.when((t >= 11) & (t < total + 11))
        def _():
            for copy in outs(t - 11):
                copy.wait()

        @pl.when((t >= 9) & (t < total + 9))
        def _():
            m = t - 9
            wait_send(spread(13, m, 0, 8, mate_core))
            wait_recv(spread(13, m, 0, 8, mate_core, other_cols))
            for copy in ins(m):
                copy.wait()
            precondition_block(
                own, codes.at[m], scales.at[m], left_buf.at[m % 2], right_buf.at[m % 2],
                outs_buf.at[m % 2], squares.at[m], high_buf, low_buf, right_full,
            )
            start(outs(m))

        return carry

    lax.fori_loop(0, total + 11, step, 0)

    def folded(row):
        return sum(row[:, n * 128 : (n + 1) * 128] for n in range(row.shape[1] // 128))

    layer = jnp.zeros((1, 128), jnp.float32)
    mine = lax.rem(dp, quarter)
    sum_slots[mine] = jnp.zeros(sum_slots.shape[1:], jnp.float32)
    for m in range(total):
        layer = layer + folded(squares[m, 0:1, :])
        for quad in range(2):
            part = squares[m, 1:2, quad * cols : (quad + 1) * cols]
            row = 2 * ((m + paired) % total) + quad
            sum_slots[mine, row : row + 1, :] = folded(part)
    once = (cls == 0).astype(jnp.float32)
    first_row = lax.broadcasted_iota(jnp.int32, tail_ref.shape, 0) == 0
    tail_slots[me] = tail_ref[...] + jnp.where(first_row, once * layer, 0.0)

    def sum_copy(n, slot):
        return pltpu.make_async_remote_copy(
            src_ref=sum_slots.at[slot], dst_ref=sum_slots.at[slot],
            send_sem=sum_send.at[n], recv_sem=sum_recv.at[slot],
            device_id=half_mate(n), device_id_type=MESH,
        )

    def tail_copy(n, slot):
        return pltpu.make_async_remote_copy(
            src_ref=tail_slots.at[slot], dst_ref=tail_slots.at[slot],
            send_sem=tail_send.at[n], recv_sem=tail_recv.at[slot],
            device_id=any_mate(n), device_id_type=MESH,
        )

    for n in range(1, quarter):
        sum_copy(n, lax.rem(dp, quarter)).start()
    for n in range(1, everyone):
        tail_copy(n, me).start()
    for n in range(1, quarter):
        sum_copy(n, lax.rem(dp, quarter)).wait_send()
        sum_copy(n, lax.rem(dp + n, quarter)).wait_recv()
    for n in range(1, everyone):
        tail_copy(n, me).wait_send()
        tail_copy(n, lax.rem(me + n, everyone)).wait_recv()
    value = sum_slots[0]
    for n in range(1, quarter):
        value = value + sum_slots[n]
    tail = tail_slots[0]
    for n in range(1, everyone):
        tail = tail + tail_slots[n]
    vec = vec_out_ref[...]
    vec_squares = jnp.sum(jnp.sum(vec * vec, 0, keepdims=True), 1, keepdims=True)
    norm = jnp.sqrt(jnp.sum(tail[0:1], 1, keepdims=True) + vec_squares)
    factor = CLIP_NORM / jnp.maximum(norm, CLIP_NORM)
    mean_squares = jnp.sum(value, 1, keepdims=True) / (half * cols) * factor * factor
    scale = SHAMPOO_RATE * factor * lax.rsqrt(mean_squares + ROOT_EPS)
    for b in range(total):
        for quad in range(2):
            row = 2 * b + quad
            wide_ref[b, :, quad * cols : (quad + 1) * cols] = jnp.broadcast_to(
                scale[row : row + 1], (1, cols)
            )
    rows = lax.broadcasted_iota(jnp.int32, facts_ref.shape, 0)
    loss = jnp.sum(tail[1:2], 1, keepdims=True)
    facts_ref[...] = jnp.where(rows == 0, loss, jnp.where(rows == 1, norm, factor))


def reduce_gradients(
    arrays, lefts, rights, vec_sums, tail, root_left, right_codes, dp_count, cls_count
):
    counts = tuple(array.shape[0] for array in arrays)
    total, rows, width = root_left.shape
    length = lefts[0].shape[0]
    parts, coded_rows = right_codes.shape[0], right_codes.shape[2]
    half, cols = width // 2, width // 2
    sum_rows = 2 * total + -2 * total % 8
    f32, i16 = jnp.float32, jnp.int16

    def pair(*shape):
        return [pltpu.VMEM((2,) + shape, i16), pltpu.VMEM((total,) + shape, i16)]

    def scale_pair(*shape):
        return [
            pltpu.VMEM((2,) + shape + (1, cols), f32),
            pltpu.VMEM((total,) + shape + (1, cols), f32),
        ]

    hbm = pl.BlockSpec(memory_space=pl.ANY)
    vmem = pl.BlockSpec(memory_space=pltpu.VMEM)
    return pl.pallas_call(
        functools.partial(reduce_kernel, counts),
        out_shape=(jax.ShapeDtypeStruct((total, rows, width), f32),) * 4
        + (
            jax.ShapeDtypeStruct((total, 1, width), f32),
            jax.ShapeDtypeStruct(tail.shape, f32),
            jax.ShapeDtypeStruct(vec_sums.shape, f32),
        ),
        in_specs=[hbm] * (len(arrays) + 6) + [vmem, vmem, hbm, hbm],
        out_specs=(hbm,) * 4 + (vmem,) * 3,
        scratch_shapes=[
            pltpu.VMEM((2, rows, width), f32),
            pltpu.VMEM((2, parts, coded_rows, width), jnp.int32),
            pltpu.VMEM((half, width), f32),
            pltpu.VMEM((2, 4, rows, width), f32),
            pltpu.VMEM((total, 2, width), f32),
            pltpu.VMEM((half, width), jnp.bfloat16),
            pltpu.VMEM((half, width), jnp.bfloat16),
            pltpu.VMEM((dp_count // 2, sum_rows, 128), f32),
            pltpu.VMEM((dp_count * cls_count,) + tail.shape, f32),
            pltpu.VMEM((2, length, width), jnp.bfloat16),
            pltpu.VMEM((2, length, width), jnp.bfloat16),
            pltpu.SemaphoreType.DMA((2, 2)),
            pltpu.SemaphoreType.DMA((2, 2)),
            pltpu.SemaphoreType.DMA((dp_count // 2,)),
            pltpu.SemaphoreType.DMA((dp_count // 2,)),
            pltpu.SemaphoreType.DMA((dp_count * cls_count,)),
            pltpu.SemaphoreType.DMA((dp_count * cls_count,)),
            pltpu.VMEM((5, width, cols), f32),
            pltpu.VMEM((2, width, cols), f32),
            pltpu.VMEM((3, 2, 2, PIECE, cols), f32),
        ]
        + pair(width, cols)
        + pair(2, 2, 2 * PIECE, cols)
        + pair(2, 2, PIECE, cols)
        + pair(2, 2, PIECE, cols)
        + pair(2, PIECE, cols)
        + scale_pair()
        + scale_pair(2)
        + scale_pair(2)
        + scale_pair()
        + scale_pair()
        + [
            pltpu.VMEM((total, half, width), i16),
            pltpu.VMEM((total, half // PIECE, 1, width), f32),
            pltpu.VMEM((5, 2) + vec_sums.shape, f32),
            pltpu.SemaphoreType.DMA((2, 2)),
            pltpu.SemaphoreType.DMA((2, 4)),
            pltpu.SemaphoreType.DMA((14, 2)),
            pltpu.SemaphoreType.DMA((14, total)),
            pltpu.SemaphoreType.DMA((14, 2)),
            pltpu.SemaphoreType.DMA((14, total)),
            pltpu.SemaphoreType.DMA((5,)),
            pltpu.SemaphoreType.DMA((5,)),
        ],
        compiler_params=pltpu.CompilerParams(
            collective_id=1, has_side_effects=True, vmem_limit_bytes=60 << 20
        ),
        name="reduce_gradients",
    )(*arrays, *lefts, *rights, vec_sums, tail, root_left, right_codes)


def split_float(values):
    high = values.astype(jnp.bfloat16)
    return high, (values - high.astype(jnp.float32)).astype(jnp.bfloat16)


def stacked_dot(lefts, right, contract_last):
    rows = lefts[0].shape[0]
    left = jnp.concatenate(lefts, 0) if len(lefts) > 1 else lefts[0]
    dims = (((1,), (1 if contract_last else 0,)), ((), ()))
    out = lax.dot_general(left, right, dims, preferred_element_type=jnp.float32)
    return [out[n * rows : (n + 1) * rows] for n in range(len(lefts))]


def encode_roots(part):
    top = jnp.max(jnp.abs(part), 1, keepdims=True)
    level = jnp.ceil(jnp.log2(jnp.maximum(top, 1e-30)))
    codes = jnp.round(part * jnp.exp2(15.0 - level))
    codes = jnp.clip(codes, -32767.0, 32767.0).astype(jnp.int32)
    levels = jnp.broadcast_to(level.astype(jnp.int32), (part.shape[0], 8, part.shape[2]))
    upper = jnp.concatenate([codes[:, 0:8], codes[:, 16:24]], 1)
    lower = jnp.concatenate([codes[:, 8:16], levels], 1)
    return upper * 65536 + (lower + 32768)


def precondition_block(
    own, codes_ref, scales_ref, left_ref, right_codes, outs_ref, squares_ref, high_ref, low_ref,
    right_ref
):
    half, width = codes_ref.shape
    rows = left_ref.shape[0]
    own_rows = pl.ds(pl.multiple_of(own, PIECE), rows)
    parts = right_codes.shape[0]
    size = half // parts
    for n in range(parts):
        packed = right_codes[n]
        upper = lax.shift_right_arithmetic(packed, jnp.full_like(packed, 16)).astype(jnp.float32)
        lower = ((packed & 65535) - 32768).astype(jnp.float32)
        scale = jnp.exp2(lower[8:9] - 15.0)
        right_ref[n * size : n * size + 8, :] = upper[0:8] * scale
        right_ref[n * size + 8 : n * size + 16, :] = lower[0:8] * scale
        right_ref[n * size + 16 : n * size + 24, :] = upper[8:16] * scale
    for piece in range(half // PIECE):
        part = slice(piece * PIECE, (piece + 1) * PIECE)
        high_ref[part, :], low_ref[part, :] = split_float(
            decode(codes_ref[part, :], scales_ref[piece])
        )
    own_value = high_ref[own_rows, :].astype(jnp.float32) + low_ref[own_rows, :].astype(jnp.float32)
    outs_ref[0] = own_value
    squares_ref[0:1, :] = jnp.sum(own_value * own_value, 0, keepdims=True)
    picks = (
        lax.broadcasted_iota(jnp.int32, (rows, half), 1)
        == lax.broadcasted_iota(jnp.int32, (rows, half), 0) + own
    ).astype(jnp.float32).astype(jnp.bfloat16)
    for quad in range(2):
        cols = slice(quad * half, (quad + 1) * half)
        high, low = high_ref[:, cols], low_ref[:, cols]
        mine_high, mine_low = high_ref[own_rows, cols], low_ref[own_rows, cols]
        hh, lh, turned_high = stacked_dot([mine_high, mine_low, picks], high, True)
        hl, turned_low = stacked_dot([mine_high, picks], low, True)
        outs_ref[1, :, cols] = hh + (lh + hl)
        turned_high = turned_high.astype(jnp.bfloat16)
        turned_low = turned_low.astype(jnp.bfloat16)
        root_high, root_low = split_float(left_ref[:, cols])
        thh, tlh, rhh, rlh = stacked_dot([turned_high, turned_low, root_high, root_low], high, False)
        thl, rhl = stacked_dot([turned_high, root_high], low, False)
        outs_ref[2, :, cols] = thh + (tlh + thl)
        half_step = rhh + (rlh + rhl)
        step_high, step_low = split_float(half_step)
        right_high, right_low = split_float(right_ref[:, cols])
        shh, slh = stacked_dot([step_high, step_low], right_high, False)
        (shl,) = stacked_dot([step_high], right_low, False)
        direction = shh + (slh + shl)
        outs_ref[3, :, cols] = direction
        squares_ref[1:2, cols] = jnp.sum(direction * direction, 0, keepdims=True)


def head_kernel(
    image_total, pooled_ref, labels_ref, head_hbm,
    grad_ref, rows_ref, loss_ref,
    head_buf, group_buf, total_buf, slots, load_sem, send_sem, recv_sem, sum_send, sum_recv
):
    dp, cls = lax.axis_index("dp"), lax.axis_index("cls")
    count, rows, width = slots.shape
    images = count * rows
    classes = head_buf.shape[1]
    load = pltpu.make_async_copy(head_hbm, head_buf, load_sem)
    load.start()
    barrier = pltpu.get_barrier_semaphore()
    for n in range(1, count):
        pl.semaphore_signal(
            barrier, inc=1, device_id=(dp, lax.rem(cls + n, count)), device_id_type=MESH
        )
    pl.semaphore_wait(barrier, count - 1)

    def part(ref, index):
        return ref.at[pl.ds(pl.multiple_of(index * rows, 8), rows)]

    def share(n, slot):
        return pltpu.make_async_remote_copy(
            src_ref=pooled_ref, dst_ref=part(group_buf, slot),
            send_sem=send_sem.at[n], recv_sem=recv_sem.at[slot],
            device_id=(dp, lax.rem(cls + n, count)), device_id_type=MESH,
        )

    for n in range(1, count):
        share(n, cls).start()
    part(group_buf, cls)[...] = pooled_ref[...]
    rows_ref[:, width + classes :] = jnp.zeros(
        (images, rows_ref.shape[1] - width - classes), rows_ref.dtype
    )
    for n in range(1, count):
        share(n, cls).wait_send()
        share(n, lax.rem(cls + n, count)).wait_recv()
    load.wait()
    group = group_buf[...].astype(jnp.bfloat16)
    rows_ref[:, :width] = group
    loss = jnp.zeros((1, 1), jnp.float32)
    total = jnp.zeros((images, width), jnp.float32)
    for start in range(0, classes, CLASS_TILE):
        stop = min(classes, start + CLASS_TILE)
        weights = head_buf[:, start:stop]
        logits = jnp.dot(group, weights, preferred_element_type=jnp.float32)
        ids = lax.broadcasted_iota(jnp.int32, logits.shape, 1) + (cls * classes + start)
        target = ids == labels_ref[:, 0:1]
        for n in range(1, labels_ref.shape[1]):
            target = target | (ids == labels_ref[:, n : n + 1])
        target = target.astype(jnp.float32)
        valid = ids < LABELS_REAL
        shrunk = jnp.exp(-jnp.abs(logits))
        terms = jnp.maximum(logits, 0.0) + jnp.log1p(shrunk) - target * logits
        terms = jnp.where(valid, terms, 0.0)
        loss = loss + jnp.sum(jnp.sum(terms, 0, keepdims=True), 1, keepdims=True)
        chance = jnp.where(logits >= 0.0, 1.0, shrunk) / (1.0 + shrunk)
        grads = jnp.where(valid, chance - target, 0.0) / image_total
        grads = grads.astype(jnp.bfloat16)
        rows_ref[:, width + start : width + stop] = grads
        total = total + lax.dot_general(
            grads, weights, (((1,), (1,)), ((), ())), preferred_element_type=jnp.float32
        )
    loss_ref[...] = jnp.broadcast_to(loss / image_total, loss_ref.shape)
    total_buf[...] = total

    def back(n, slot):
        mate = lax.rem(cls + n, count)
        return pltpu.make_async_remote_copy(
            src_ref=part(total_buf, mate), dst_ref=slots.at[slot],
            send_sem=sum_send.at[n], recv_sem=sum_recv.at[slot],
            device_id=(dp, mate), device_id_type=MESH,
        )

    for n in range(1, count):
        back(n, cls).start()
    slots[cls] = part(total_buf, cls)[...]
    for n in range(1, count):
        back(n, cls).wait_send()
        back(n, lax.rem(cls + n, count)).wait_recv()
    value = slots[0]
    for n in range(1, count):
        value = value + slots[n]
    grad_ref[...] = value


def classify(pooled, labels, head_low, cls_count, image_total):
    rows, width = pooled.shape
    images, classes = rows * cls_count, head_low.shape[1]
    wide = width + classes
    wide = wide + -wide % 128
    f32 = jnp.float32
    vmem = pl.BlockSpec(memory_space=pltpu.VMEM)
    return pl.pallas_call(
        functools.partial(head_kernel, image_total),
        out_shape=(
            jax.ShapeDtypeStruct((rows, width), f32),
            jax.ShapeDtypeStruct((images, wide), jnp.bfloat16),
            jax.ShapeDtypeStruct((8, 128), f32),
        ),
        in_specs=[vmem, vmem, pl.BlockSpec(memory_space=pltpu.HBM)],
        out_specs=(vmem, vmem, vmem),
        scratch_shapes=[
            pltpu.VMEM((width, classes), jnp.bfloat16),
            pltpu.VMEM((images, width), f32),
            pltpu.VMEM((images, width), f32),
            pltpu.VMEM((cls_count, rows, width), f32),
            pltpu.SemaphoreType.DMA,
        ]
        + [pltpu.SemaphoreType.DMA((cls_count,)) for _ in range(4)],
        compiler_params=pltpu.CompilerParams(
            collective_id=2, has_side_effects=True, vmem_limit_bytes=60 << 20
        ),
        name="classify",
    )(pooled, labels, head_low)


def gather_steps(own_ref, out_ref, send_sem, recv_sem, copy_sem):
    count, rows, width = own_ref.shape
    cols = width // 2
    z, y, x, core = torus_place()
    mate_core = torus_device(z, y, x, 1 - core)
    mate_x = torus_device(z, y, 1 - x, core)
    mate_y = torus_device(z, 1 - y, x, core)
    own_cols = pl.ds(pl.multiple_of(core * cols, 128), cols)
    other_cols = pl.ds(pl.multiple_of((1 - core) * cols, 128), cols)
    spare = rows - SPAN
    held = x * spare
    lone = (x * SPAN, (1 - x) * SPAN)

    def share(m, zz, yy, start, size):
        begin = (zz * 2 + yy) * rows + start
        return out_ref.at[m, pl.ds(pl.multiple_of(begin, 16), size), own_cols]

    def copy(slot, arrival, m, source, target, mate):
        return pltpu.make_async_remote_copy(
            src_ref=source, dst_ref=target,
            send_sem=send_sem.at[slot, m % 2], recv_sem=recv_sem.at[arrival, m],
            device_id=mate, device_id_type=MESH,
        )

    def local(m):
        return pltpu.make_async_copy(
            own_ref.at[m, :, own_cols], share(m, z, y, 0, rows), copy_sem.at[m % 2]
        )

    def along(m, n, outgoing):
        other = lax.rem(z + n, 4)
        origin = z if outgoing else other
        source = own_ref.at[m, pl.ds(pl.multiple_of(held, 16), SPAN), own_cols]
        mate = torus_device(other, y, x, core)
        return copy(n - 1, origin, m, source, share(m, origin, y, held, SPAN), mate)

    def cross(m, n, outgoing):
        block = share(m, n, y if outgoing else 1 - y, held, SPAN)
        return copy(3 + n, 4 + n, m, block, block, mate_y)

    def patch(m, n, outgoing):
        index = lax.rem(z * 2 + y + n, SHARES)
        block = share(m, index // 2, lax.rem(index, 2), lone[0 if outgoing else 1], spare)
        return copy(6 + n, 7 + n, m, block, block, mate_x)

    def swap(m, columns):
        block = out_ref.at[m, :, columns]
        return copy(14, 15, m, block, block, mate_core)

    def finish(copies):
        for outgoing, incoming in copies:
            outgoing.wait_send()
            incoming.wait_recv()

    def step(t):
        @pl.when(t < count)
        def _():
            local(t).start()
            for n in range(1, 4):
                along(t, n, True).start()

        @pl.when((t >= 1) & (t < count + 1))
        def _():
            m = t - 1
            local(m).wait()
            finish([(along(m, n, True), along(m, n, False)) for n in range(1, 4)])
            for n in range(4):
                cross(m, n, True).start()

        @pl.when((t >= 2) & (t < count + 2))
        def _():
            m = t - 2
            finish([(cross(m, n, True), cross(m, n, False)) for n in range(4)])
            for n in range(1, SHARES):
                patch(m, n, True).start()

        @pl.when((t >= 3) & (t < count + 3))
        def _():
            m = t - 3
            finish([(patch(m, n, True), patch(m, n, False)) for n in range(1, SHARES)])
            swap(m, own_cols).start()

        @pl.when((t >= 4) & (t < count + 4))
        def _():
            m = t - 4
            swap(m, own_cols).wait_send()
            swap(m, other_cols).wait_recv()

    return step, count + GATHER_DEPTH


def column_mate(n):
    z, y, x, core = torus_place()
    other = lax.rem(z * 2 + y + n, SHARES)
    return torus_device(other // 2, lax.rem(other, 2), x, core)


def gather_barrier():
    z, y, x, core = torus_place()
    barrier = pltpu.get_barrier_semaphore()
    mates = [torus_device(z, y, x, 1 - core), torus_device(z, y, 1 - x, core)]
    for mate in mates + [column_mate(n) for n in range(1, SHARES)]:
        pl.semaphore_signal(barrier, inc=1, device_id=mate, device_id_type=MESH)
    pl.semaphore_wait(barrier, SHARES + 1)


def gather_kernel(
    own_ref, vec_ref, out_ref, vec_out_ref, send_sem, recv_sem, copy_sem, vec_send, vec_recv
):
    z, y, _, _ = torus_place()
    me = z * 2 + y
    gather_barrier()

    def vec_copy(n, slot):
        return pltpu.make_async_remote_copy(
            src_ref=vec_ref, dst_ref=vec_out_ref.at[slot],
            send_sem=vec_send.at[n], recv_sem=vec_recv.at[slot],
            device_id=column_mate(n), device_id_type=MESH,
        )

    for n in range(1, SHARES):
        vec_copy(n, me).start()
    vec_out_ref[me] = vec_ref[...]
    gather_step, turns = gather_steps(own_ref, out_ref, send_sem, recv_sem, copy_sem)

    def step(t, carry):
        gather_step(t)
        return carry

    lax.fori_loop(0, turns, step, 0)
    for n in range(1, SHARES):
        vec_copy(n, me).wait_send()
        vec_copy(n, lax.rem(me + n, SHARES)).wait_recv()


def gather_semaphores(count):
    return [
        pltpu.SemaphoreType.DMA((15, 2)),
        pltpu.SemaphoreType.DMA((16, count)),
        pltpu.SemaphoreType.DMA((2,)),
    ]


def attention_gather_kernel(
    qids_ref, kcodes_ref, q_ref, k_ref, v_ref, own_ref, out_ref, blocks_ref,
    bias_ref, send_sem, recv_sem, copy_sem
):
    pair, tiles = pl.program_id(0), q_ref.shape[0] // QTILE
    slots = pl.num_programs(0) * tiles

    @pl.when(pair == 0)
    def _():
        gather_barrier()

    gather_step, turns = gather_steps(own_ref, blocks_ref, send_sem, recv_sem, copy_sem)
    attention_bias(qids_ref, kcodes_ref, bias_ref)
    for tile in range(tiles):
        slot = pair * tiles + tile
        begin, end = slot * turns // slots, (slot + 1) * turns // slots

        @pl.when(begin < end)
        def _(begin=begin):
            gather_step(begin)

        attention_tile(tile, q_ref, k_ref, v_ref, out_ref, bias_ref)


def attention_forward_gathering(qkv_rows, pack_ids, key_codes, own):
    _, length, width = qkv_rows.shape
    count, rows, _ = own.shape
    tiles = length // QTILE
    assert count + GATHER_DEPTH <= tiles * (width // PAIR)
    return pl.pallas_call(
        attention_gather_kernel,
        grid=(width // PAIR,),
        out_shape=(
            jax.ShapeDtypeStruct((length, width), jnp.bfloat16),
            jax.ShapeDtypeStruct((count, SHARES * rows, width), own.dtype),
        ),
        in_specs=[whole_spec((length, 1)), whole_spec((1, length))]
        + [pair_spec(length, part) for part in range(3)]
        + [whole_spec(own.shape)],
        out_specs=(pair_spec(length), pl.BlockSpec(memory_space=pl.ANY)),
        scratch_shapes=[pltpu.VMEM(bias_shape(length), jnp.float32)] + gather_semaphores(count),
        compiler_params=pltpu.CompilerParams(
            collective_id=4, has_side_effects=True, vmem_limit_bytes=40 << 20
        ),
        name="attention_forward",
    )(pack_ids[:, None], key_codes[None, :], qkv_rows, qkv_rows, qkv_rows, own)


def gather_weights(own, vec):
    count, rows, width = own.shape
    hbm = pl.BlockSpec(memory_space=pl.ANY)
    vmem = pl.BlockSpec(memory_space=pltpu.VMEM)
    return pl.pallas_call(
        gather_kernel,
        out_shape=(
            jax.ShapeDtypeStruct((count, SHARES * rows, width), own.dtype),
            jax.ShapeDtypeStruct((SHARES,) + vec.shape, vec.dtype),
        ),
        in_specs=[vmem, vmem],
        out_specs=(hbm, vmem),
        scratch_shapes=gather_semaphores(count)
        + [pltpu.SemaphoreType.DMA((SHARES,)), pltpu.SemaphoreType.DMA((SHARES,))],
        compiler_params=pltpu.CompilerParams(
            collective_id=3, has_side_effects=True, vmem_limit_bytes=32 << 20
        ),
        name="gather_weights",
    )(own, vec)


def adam_step(weight, grad, first, second, count):
    first = BETA_FIRST * first + (1.0 - BETA_FIRST) * grad
    second = BETA_SECOND * second + (1.0 - BETA_SECOND) * grad * grad
    fix_first = 1.0 - jnp.power(BETA_FIRST, count)
    fix_second = 1.0 - jnp.power(BETA_SECOND, count)
    update = first / fix_first / (jnp.sqrt(second / fix_second) + ADAM_EPS) + WEIGHT_DECAY * weight
    return (weight - ADAM_RATE * update, first, second)


def split_halves(values, half_size):
    block_count, row_count, feature_dim = values.shape
    return values.reshape(block_count, row_count, 2, half_size)


def finish_kernel(
    facts_ref, wide_ref, own_ref, left_add_ref, right_add_ref, step_ref, enc_ref, left_ref, right_ref,
    new_ref, grad_ref, new_left_ref, new_right_ref
):
    factor = facts_ref[2:3, 0:1]
    share = 0.5 * factor * factor
    new_ref[...] = enc_ref[...] - step_ref[...] * wide_ref[...]
    grad_ref[...] = own_ref[...] * factor
    new_left_ref[...] = 0.5 * left_ref[...] + share * left_add_ref[...]
    new_right_ref[...] = 0.5 * right_ref[...] + share * right_add_ref[...]


def finish_blocks(facts, wide_scale, *arrays):
    count, rows, width = arrays[0].shape
    block = pl.BlockSpec((None, rows, width), lambda b: (b, 0, 0))
    return pl.pallas_call(
        finish_kernel,
        grid=(count,),
        out_shape=(jax.ShapeDtypeStruct((count, rows, width), jnp.float32),) * 4,
        in_specs=[
            pl.BlockSpec(facts.shape, lambda b: (0, 0)),
            pl.BlockSpec((None, 1, width), lambda b: (b, 0, 0)),
        ]
        + [block] * len(arrays),
        out_specs=(block,) * 4,
        compiler_params=pltpu.CompilerParams(vmem_limit_bytes=60 << 20),
        name="finish_blocks",
    )(facts, wide_scale, *arrays)


def adam_kernel(
    facts_ref, fixes_ref, weight_ref, grad_ref, first_ref, second_ref,
    new_ref, new_first_ref, new_second_ref
):
    grad = grad_ref[...] * facts_ref[2:3, 0:1]
    weight = weight_ref[...]
    first = BETA_FIRST * first_ref[...] + (1.0 - BETA_FIRST) * grad
    second = BETA_SECOND * second_ref[...] + (1.0 - BETA_SECOND) * grad * grad
    root = jnp.sqrt(second / fixes_ref[1:2, 0:1]) + ADAM_EPS
    update = first / fixes_ref[0:1, 0:1] / root + WEIGHT_DECAY * weight
    new_ref[...] = weight - ADAM_RATE * update
    new_first_ref[...] = first
    new_second_ref[...] = second


def adam_rows(facts, fixes, *arrays):
    rows, width = arrays[0].shape
    block = pl.BlockSpec((8, width), lambda r: (r, 0))
    small = pl.BlockSpec(facts.shape, lambda r: (0, 0))
    return pl.pallas_call(
        adam_kernel,
        grid=(rows // 8,),
        out_shape=(jax.ShapeDtypeStruct((rows, width), jnp.float32),) * 3,
        in_specs=[small, small] + [block] * 4,
        out_specs=(block,) * 3,
        compiler_params=pltpu.CompilerParams(vmem_limit_bytes=60 << 20),
        name="adam_rows",
    )(facts, fixes, *arrays)


def reduced_half(values, half_groups):
    part = lax.psum_scatter(values, ("dp", "cls"), scatter_dimension=1, tiled=True)
    return lax.all_gather(part, ("dp", "cls"), axis=1, tiled=True, axis_index_groups=half_groups)


def preconditioned_rows(grad_half, root_left, right_half, own_start):
    count, row_count, width = root_left.shape
    half_size = width // 2
    block_rows = lax.dynamic_slice_in_dim(grad_half, own_start, row_count, 1)
    grad_quads = split_halves(grad_half, half_size)
    rows_quads = split_halves(block_rows, half_size)
    cols_quads = lax.dynamic_slice_in_dim(grad_quads, own_start, row_count, 3)
    precise = FULL_PRECISION
    left_add = jnp.einsum("brjk,bljk->brjl", rows_quads, grad_quads, precision=precise)
    right_add = jnp.einsum("bkja,bkjm->bajm", cols_quads, grad_quads, precision=precise)
    direction = jnp.einsum(
        "brjk,bkjm->brjm", split_halves(root_left, half_size), grad_quads, precision=precise
    )
    direction = jnp.einsum(
        "brjk,bkjm->brjm", direction, split_halves(right_half, half_size), precision=precise
    )
    flat = (count, row_count, width)
    return left_add.reshape(flat), right_add.reshape(flat), direction.reshape(flat), block_rows


def on_device(
    patches,
    image_ids,
    keep,
    labels,
    owner,
    step,
    enc_weights,
    stats_left,
    stats_right,
    root_left,
    root_right,
    head_weights,
    head_m,
    head_v,
    vectors,
    vec_m,
    vec_v,
):
    dp_count = lax.axis_size("dp")
    cls_count = lax.axis_size("cls")
    dp_index = lax.axis_index("dp")
    cls_index = lax.axis_index("cls")
    block_count, row_count, feature_dim = enc_weights.shape
    up_count = (block_count - 5) // 2
    half_size = feature_dim // 2
    part_rows = row_count // cls_count
    half_dp = dp_count // 2
    half_group = half_dp * cls_count
    half_groups = [
        list(range(half_group)),
        list(range(half_group, 2 * half_group)),
    ]

    def my_part(values):
        return lax.dynamic_slice_in_dim(values, cls_index * part_rows, part_rows, 1)

    on_torus = dp_count == 8 and cls_count == 4
    if on_torus:
        vec_block = jnp.pad(vectors, ((0, -vectors.shape[0] % 8), (0, -row_count % 128)))
        own_low = enc_weights.astype(jnp.bfloat16)
        blocks, vec_blocks = gather_weights(own_low[:5], vec_block)
        right_part, vec_blocks = lax.optimization_barrier((my_part(root_right), vec_blocks))
        vec_low = jnp.transpose(vec_blocks[:, : vectors.shape[0], :row_count], (1, 0, 2))
        vec_all = lax.reduce_precision(vec_low.reshape(vectors.shape[0], feature_dim), 8, 7)
    else:
        right_part = my_part(root_right)
        all_blocks = lax.all_gather(
            my_part(enc_weights.astype(jnp.bfloat16)), ("dp", "cls"), axis=1, tiled=True
        )
        blocks = all_blocks[:5]
        vec_low = lax.all_gather(vectors.astype(jnp.bfloat16), "dp", axis=1, tiled=True)
        vec_all = vec_low.astype(jnp.float32)
    head_low = lax.all_gather(head_weights.astype(jnp.bfloat16), "dp", axis=0, tiled=True)
    final_gain = vec_all[9 + up_count]
    final_shift = vec_all[10 + up_count]
    pack_ids, pack_keep = image_ids[0], keep[0]
    key_codes = jnp.where(pack_keep == 1, pack_ids, -1)

    def attend(qkv_rows):
        if on_torus:
            return attention_forward_gathering(qkv_rows, pack_ids, key_codes, own_low[5:])
        return attention_forward(qkv_rows, pack_ids, key_codes), all_blocks[5:]

    output, mlp_blocks, saved = layer_forward(blocks, vec_all, patches, attend)
    if on_torus:
        right_codes = lax.all_gather(
            encode_roots(right_part), ("dp", "cls"), axis=0, axis_index_groups=half_groups
        )
    else:
        right_half = lax.all_gather(
            right_part, ("dp", "cls"), axis=1, tiled=True, axis_index_groups=half_groups
        )
    pooled = pool_rows(output, final_gain, final_shift, pack_ids, pack_keep)
    class_dev = head_low.shape[1]
    image_total = labels.shape[0] * dp_count
    if on_torus:
        grad_pooled, own_rows, loss_rows = classify(
            lax.reduce_precision(pooled, 8, 7), labels, head_low, cls_count, image_total
        )
        loss_part = loss_rows[0, 0]
    else:
        group = lax.all_gather(pooled.astype(jnp.bfloat16), "cls", axis=0, tiled=True)
        logits = jnp.dot(group, head_low, preferred_element_type=jnp.float32)
        class_ids = cls_index * class_dev + jnp.arange(class_dev)
        valid = class_ids[None, :] < LABELS_REAL
        target = jnp.any(labels[:, :, None] == class_ids[None, None, :], 1).astype(jnp.float32)
        terms = jax.nn.softplus(logits) - target * logits
        loss_part = jnp.sum(jnp.where(valid, terms, 0.0)) / image_total
        grad_logits = jnp.where(valid, jax.nn.sigmoid(logits) - target, 0.0) / image_total
        grad_logits = grad_logits.astype(jnp.bfloat16)
        group_grad = jnp.einsum(
            "gc,dc->gd", grad_logits, head_low, preferred_element_type=jnp.float32
        )
        grad_pooled = lax.psum_scatter(group_grad, "cls", scatter_dimension=0, tiled=True)
        own_rows = jnp.concatenate([group, grad_logits], 1)

    def pool_local(rows_in, gain, shift):
        return pool_rows(rows_in, gain, shift, pack_ids, pack_keep)

    pool_back = jax.vjp(pool_local, output, final_gain, final_shift)[1]
    grad_output, grad_gain, grad_shift = pool_back(grad_pooled)
    lefts, rights, mlp_grads, grad_vectors, (own_rows, roots) = layer_backward(
        blocks,
        mlp_blocks,
        vec_all,
        patches,
        saved,
        pack_ids,
        key_codes,
        grad_output,
        grad_gain,
        grad_shift,
        (own_rows, right_codes if on_torus else right_half),
    )
    head_rows = lax.all_gather(own_rows, "dp", axis=0, tiled=True)
    pooled_all = head_rows[:, :feature_dim]
    grad_logits_all = head_rows[:, feature_dim : feature_dim + class_dev]
    pooled_mine = lax.dynamic_slice_in_dim(pooled_all, dp_index * row_count, row_count, 1)
    head_grad = jnp.einsum(
        "gr,gc->rc", pooled_mine, grad_logits_all, preferred_element_type=jnp.float32
    )

    head_squares = jnp.sum(head_grad * head_grad)
    if on_torus:
        padded = jnp.pad(grad_vectors, ((0, -grad_vectors.shape[0] % 8), (0, 0)))
        tail = jnp.pad(jnp.stack([head_squares, loss_part])[:, None], ((0, 6), (0, 127)))
        block_rows, left_add, right_add, direction, wide_scale, facts, vector_sum = (
            reduce_gradients(
                mlp_grads, lefts, rights, padded, tail, root_left, roots,
                dp_count, cls_count,
            )
        )
        vector_sum = vector_sum[: grad_vectors.shape[0]]
        loss, grad_norm, factor = facts[0, 0], facts[1, 0], facts[2, 0]
    else:
        over_rows = "td,te->de"
        first_grads = [
            jnp.einsum(over_rows, left, right, preferred_element_type=jnp.float32)[None]
            for left, right in (
                (lefts[0], rights[0]),
                (lefts[1], rights[1][0]),
                (lefts[1], rights[1][1]),
                (lefts[1], rights[1][2]),
                (lefts[2], rights[2]),
            )
        ]
        grad_half = reduced_half(jnp.concatenate(first_grads + list(mlp_grads), 0), half_groups)
        vector_sum = lax.psum(grad_vectors, ("dp", "cls"))
        left_add, right_add, direction, block_rows = preconditioned_rows(
            grad_half, root_left, roots, (dp_index % half_dp) * row_count
        )
        squares = jnp.sum(split_halves(direction * direction, half_size), (1, 3))
        in_top = (dp_index < half_dp).astype(jnp.float32)
        once = (cls_index == 0).astype(jnp.float32)
        all_squares = head_squares + once * jnp.sum(block_rows * block_rows)
        packed = jnp.concatenate(
            [
                (once * in_top * squares).reshape(-1),
                (once * (1.0 - in_top) * squares).reshape(-1),
                jnp.stack([all_squares, loss_part]),
            ]
        )
        packed = lax.psum(packed, ("dp", "cls"))
        loss = packed[4 * block_count + 1]
        all_squares = packed[4 * block_count]
        sums = packed[: 4 * block_count].reshape(2, block_count, 2)
        block_squares = jnp.where(dp_index < half_dp, sums[0], sums[1])
        grad_norm = jnp.sqrt(all_squares + jnp.sum(vector_sum * vector_sum))
        factor = CLIP_NORM / jnp.maximum(grad_norm, CLIP_NORM)
        mean_squares = block_squares / (half_size * half_size) * factor * factor
        scale = SHAMPOO_RATE * factor * lax.rsqrt(mean_squares + ROOT_EPS)
        wide_scale = jnp.repeat(scale, half_size, axis=1)[:, None, :]
    vector_rows = lax.dynamic_slice_in_dim(vector_sum, dp_index * row_count, row_count, 1)
    count = step.astype(jnp.float32)
    new_vec, new_vec_m, new_vec_v = adam_step(vectors, vector_rows * factor, vec_m, vec_v, count)
    if on_torus:
        new_blocks, block_clip, new_left, new_right = finish_blocks(
            facts, wide_scale, block_rows, left_add, right_add, direction,
            enc_weights, stats_left, stats_right,
        )
        fixes = jnp.stack([1.0 - jnp.power(BETA_FIRST, count), 1.0 - jnp.power(BETA_SECOND, count)])
        fixes = jnp.broadcast_to(jnp.pad(fixes, (0, 6))[:, None], facts.shape)
        new_head, new_head_m, new_head_v = adam_rows(
            facts, fixes, head_weights, head_grad, head_m, head_v
        )
    else:
        block_clip = block_rows * factor
        new_blocks = enc_weights - direction * wide_scale
        square_factor = 0.5 * factor * factor
        new_left = 0.5 * stats_left + square_factor * left_add
        new_right = 0.5 * stats_right + square_factor * right_add
        new_head, new_head_m, new_head_v = adam_step(
            head_weights, head_grad * factor, head_m, head_v, count
        )
    return (
        loss,
        grad_norm,
        new_blocks,
        block_clip,
        new_left,
        new_right,
        new_vec,
        new_vec_m,
        new_vec_v,
        new_head,
        new_head_m,
        new_head_v,
    )


def solution(mesh):
    return jax.shard_map(
        on_device,
        mesh=mesh,
        in_specs=(
            P(("dp", "cls"), None),
            P(("dp", "cls"), None),
            P(("dp", "cls"), None),
            P("dp", None),
            P(),
            P(),
            P(None, "dp", None),
            P(None, "dp", None),
            P(None, "dp", None),
            P(None, "dp", None),
            P(None, "dp", None),
            P("dp", "cls"),
            P("dp", "cls"),
            P("dp", "cls"),
            P(None, "dp"),
            P(None, "dp"),
            P(None, "dp"),
        ),
        out_specs=(
            P(),
            P(),
            P(None, "dp", None),
            P(None, "dp", None),
            P(None, "dp", None),
            P(None, "dp", None),
            P(None, "dp"),
            P(None, "dp"),
            P(None, "dp"),
            P("dp", "cls"),
            P("dp", "cls"),
            P("dp", "cls"),
        ),
        check_vma=False,
    )
```

```python
import functools

import jax
import jax.numpy as jnp
from jax import lax
from jax.experimental import pallas as pl
from jax.experimental.pallas import tpu as pltpu
from jax.sharding import PartitionSpec as P

HEADS = 12
HEAD = 64
LABELS_REAL = 21843
IMAGE_MAX = 196
QTILE = 256
PAIR = 2 * HEAD
ROWS = 256
HIDDEN_TILE = 384
MESH = pl.DeviceIdType.MESH
CODE_TOP = 32766.0
CODE_FLOOR = 1e-33
PIECE = 48
FEATURE_TILE = 128
SPAN = 48
SHARES = 8
GATHER_DEPTH = 4
CLASS_TILE = 512
IMG_PACK = 8


FULL_PRECISION = lax.Precision.HIGHEST
NORM_EPS = 1e-06
CLIP_NORM = 1.0
ADAM_RATE = 0.02
SHAMPOO_RATE = 0.01
BETA_FIRST = 0.9
BETA_SECOND = 0.999
ADAM_EPS = 1e-08
WEIGHT_DECAY = 0.1
ROOT_EPS = 1e-06


def norm_rows(values, gain, shift):
    centred = values - jnp.mean(values, -1, keepdims=True)
    spread = jnp.mean(centred * centred, -1, keepdims=True)
    return centred * lax.rsqrt(spread + NORM_EPS) * gain + shift


def pool_rows(output, gain, shift, pack_ids, pack_keep):
    final = norm_rows(output, gain, shift)
    member = (
        (pack_ids[None, :] == jnp.arange(IMG_PACK)[:, None]) & (pack_keep[None, :] == 1)
    ).astype(jnp.float32)
    counted = jnp.maximum(jnp.sum(member, 1), 1.0)
    return jnp.dot(member, final, precision=FULL_PRECISION) / counted[:, None]


def key_window(tile, length):
    reach = -(-(IMAGE_MAX - 1) // 128) * 128
    low = max(0, tile * QTILE - reach)
    high = min(length, (tile + 1) * QTILE + reach)
    return low, high


def attention_bias(qids_ref, kcodes_ref, bias_ref):
    length = qids_ref.shape[0]

    @pl.when(pl.program_id(0) == 0)
    def _():
        for tile in range(length // QTILE):
            low, high = key_window(tile, length)
            shape = (QTILE, high - low)
            rows = lax.broadcasted_iota(jnp.int32, shape, 0) + tile * QTILE
            cols = lax.broadcasted_iota(jnp.int32, shape, 1) + low
            same = qids_ref[tile * QTILE : (tile + 1) * QTILE, :] == kcodes_ref[:, low:high]
            bias_ref[tile, :, : high - low] = jnp.where(same | (rows == cols), 0.0, -1e30)


def attention_tile(tile, q_ref, k_ref, v_ref, out_ref, bias_ref):
    lane = lax.broadcasted_iota(jnp.int32, (QTILE, PAIR), 1)
    low, high = key_window(tile, q_ref.shape[0])
    rows = pl.ds(tile * QTILE, QTILE)
    queries = q_ref[rows, :] * jnp.bfloat16(HEAD ** (-0.5))
    keys = k_ref[low:high, :]
    values = v_ref[low:high, :]
    halves = []
    for head in range(2):
        mine = (lane >= head * HEAD) & (lane < (head + 1) * HEAD)
        picked = jnp.where(mine, queries, jnp.zeros_like(queries))
        scores = lax.dot_general(
            picked, keys, (((1,), (1,)), ((), ())), preferred_element_type=jnp.float32
        )
        scores = scores + bias_ref[tile, :, : high - low]
        top = jnp.max(scores, -1, keepdims=True)
        weights = jnp.exp(scores - top)
        probs = weights * (1.0 / jnp.sum(weights, -1, keepdims=True))
        halves.append(
            jnp.dot(probs.astype(jnp.bfloat16), values, preferred_element_type=jnp.float32)
        )
    out_ref[rows, :] = jnp.where(lane < HEAD, halves[0], halves[1]).astype(jnp.bfloat16)


def attention_forward_kernel(qids_ref, kcodes_ref, q_ref, k_ref, v_ref, out_ref, bias_ref):
    attention_bias(qids_ref, kcodes_ref, bias_ref)
    for tile in range(q_ref.shape[0] // QTILE):
        attention_tile(tile, q_ref, k_ref, v_ref, out_ref, bias_ref)


def attention_back_bias(qids_ref, kcodes_ref, bias_ref):
    length = kcodes_ref.shape[0]

    @pl.when(pl.program_id(0) == 0)
    def _():
        for tile in range(length // QTILE):
            low, high = key_window(tile, length)
            shape = (high - low, QTILE)
            rows = lax.broadcasted_iota(jnp.int32, shape, 0) + low
            cols = lax.broadcasted_iota(jnp.int32, shape, 1) + tile * QTILE
            same = kcodes_ref[low:high, :] == qids_ref[:, tile * QTILE : (tile + 1) * QTILE]
            bias_ref[tile, : high - low, :] = jnp.where(same | (rows == cols), 0.0, -1e30)


def attention_back_tile(tile, q_ref, k_ref, v_ref, do_ref, out_ref, bias_ref, dk_ref, dv_ref):
    length = q_ref.shape[0]
    lane = lax.broadcasted_iota(jnp.int32, (QTILE, PAIR), 1)
    scale = jnp.bfloat16(HEAD ** (-0.5))
    low, high = key_window(tile, length)
    rows = pl.ds(tile * QTILE, QTILE)
    window = pl.ds(low, high - low)
    queries = q_ref[rows, :] * scale
    keys = k_ref[window, :]
    values = v_ref[window, :]
    grads = do_ref[rows, :]
    halves = []
    for head in range(2):
        mine = (lane >= head * HEAD) & (lane < (head + 1) * HEAD)
        picked = jnp.where(mine, queries, jnp.zeros_like(queries))
        picked_grads = jnp.where(mine, grads, jnp.zeros_like(grads))
        scores = lax.dot_general(
            keys, picked, (((1,), (1,)), ((), ())), preferred_element_type=jnp.float32
        )
        scores = scores + bias_ref[tile, : high - low, :]
        top = jnp.max(scores, 0, keepdims=True)
        weights = jnp.exp(scores - top)
        probs = weights * (1.0 / jnp.sum(weights, 0, keepdims=True))
        grad_probs = lax.dot_general(
            values, picked_grads, (((1,), (1,)), ((), ())), preferred_element_type=jnp.float32
        )
        inner = jnp.sum(probs * grad_probs, 0, keepdims=True)
        grad_scores = (probs * (grad_probs - inner)).astype(jnp.bfloat16)
        dv_ref[window, :] += jnp.dot(
            probs.astype(jnp.bfloat16), picked_grads, preferred_element_type=jnp.float32
        )
        dk_ref[window, :] += jnp.dot(
            grad_scores, picked, preferred_element_type=jnp.float32
        )
        halves.append(
            lax.dot_general(
                grad_scores,
                keys,
                (((0,), (0,)), ((), ())),
                preferred_element_type=jnp.float32,
            )
        )
    grad_queries = jnp.where(lane < HEAD, halves[0], halves[1]) * HEAD ** (-0.5)
    out_ref[0, rows, :] = grad_queries.astype(jnp.bfloat16)


def attention_backward_kernel(
    qids_ref, kcodes_ref, q_ref, k_ref, v_ref, do_ref, out_ref, bias_ref, dk_ref, dv_ref
):
    attention_back_bias(qids_ref, kcodes_ref, bias_ref)
    dk_ref[...] = jnp.zeros_like(dk_ref)
    dv_ref[...] = jnp.zeros_like(dv_ref)
    for tile in range(q_ref.shape[0] // QTILE):
        attention_back_tile(tile, q_ref, k_ref, v_ref, do_ref, out_ref, bias_ref, dk_ref, dv_ref)
    out_ref[1] = dk_ref[...].astype(jnp.bfloat16)
    out_ref[2] = dv_ref[...].astype(jnp.bfloat16)


def pair_spec(length, part=None):
    if part is None:
        return pl.BlockSpec((length, PAIR), lambda pair: (0, pair))
    return pl.BlockSpec((None, length, PAIR), lambda pair: (part, 0, pair))


def whole_spec(shape):
    return pl.BlockSpec(shape, lambda pair: (0,) * len(shape))


def bias_shape(length):
    tiles = length // QTILE
    window = max(high - low for low, high in (key_window(t, length) for t in range(tiles)))
    return tiles, QTILE, window


def attention_forward(qkv_rows, pack_ids, key_codes):
    _, length, width = qkv_rows.shape
    return pl.pallas_call(
        attention_forward_kernel,
        grid=(width // PAIR,),
        out_shape=jax.ShapeDtypeStruct((length, width), jnp.bfloat16),
        in_specs=[whole_spec((length, 1)), whole_spec((1, length))]
        + [pair_spec(length, part) for part in range(3)],
        out_specs=pair_spec(length),
        scratch_shapes=[pltpu.VMEM(bias_shape(length), jnp.float32)],
        compiler_params=pltpu.CompilerParams(vmem_limit_bytes=40 << 20),
        name="attention_forward",
    )(pack_ids[:, None], key_codes[None, :], qkv_rows, qkv_rows, qkv_rows)


def attention_backward(qkv_rows, pack_ids, key_codes, grad_attended):
    _, length, width = qkv_rows.shape
    tiles = length // QTILE
    window = max(high - low for low, high in (key_window(t, length) for t in range(tiles)))
    return pl.pallas_call(
        attention_backward_kernel,
        grid=(width // PAIR,),
        out_shape=jax.ShapeDtypeStruct((3, length, width), jnp.bfloat16),
        in_specs=[whole_spec((1, length)), whole_spec((length, 1))]
        + [pair_spec(length, part) for part in range(3)]
        + [pair_spec(length)],
        out_specs=pl.BlockSpec((3, length, PAIR), lambda pair: (0, 0, pair)),
        scratch_shapes=[
            pltpu.VMEM((tiles, window, QTILE), jnp.float32),
            pltpu.VMEM((length, PAIR), jnp.float32),
            pltpu.VMEM((length, PAIR), jnp.float32),
        ],
        compiler_params=pltpu.CompilerParams(vmem_limit_bytes=40 << 20),
        name="attention_backward",
    )(pack_ids[None, :], key_codes[:, None], qkv_rows, qkv_rows, qkv_rows, grad_attended)


def mlp_forward_kernel(x_ref, up_ref, bias_ref, down_ref, units_ref, slope_ref, out_ref):
    first = pl.program_id(0) == 0

    @pl.when(first)
    def _():
        out_ref[...] = jnp.zeros_like(out_ref)

    for start in range(0, x_ref.shape[0], ROWS):
        rows = pl.ds(start, ROWS)
        pre = jnp.dot(x_ref[rows, :], up_ref[...], preferred_element_type=jnp.float32)
        pre = pre + bias_ref[...]
        half = 0.5 + 0.5 * lax.erf(pre * 0.7071067811865476)
        bell = jnp.exp(-0.5 * pre * pre) * 0.3989422804014327
        units = (pre * half).astype(jnp.bfloat16)
        units_ref[rows, :] = units
        slope_ref[rows, :] = half + pre * bell
        out_ref[rows, :] += jnp.dot(units, down_ref[...], preferred_element_type=jnp.float32)


def mlp_backward_kernel(
    x_ref, dm_ref, up_ref, down_ref, units_ref, slope_ref,
    grad_up_ref, grad_down_ref, bias_ref, dx_ref, dpre_ref
):
    @pl.when(pl.program_id(0) == 0)
    def _():
        dx_ref[...] = jnp.zeros_like(dx_ref)

    total = jnp.zeros((1, HIDDEN_TILE), jnp.float32)
    for start in range(0, x_ref.shape[0], ROWS):
        rows = pl.ds(start, ROWS)
        units_back = lax.dot_general(
            dm_ref[rows, :], down_ref[...], (((1,), (1,)), ((), ())),
            preferred_element_type=jnp.float32,
        )
        grad_pre = (units_back * slope_ref[rows, :]).astype(jnp.bfloat16)
        dpre_ref[rows, :] = grad_pre
        total = total + jnp.sum(grad_pre.astype(jnp.float32), 0, keepdims=True)
        dx_ref[rows, :] += lax.dot_general(
            grad_pre, up_ref[...], (((1,), (1,)), ((), ())), preferred_element_type=jnp.float32
        )
    bias_ref[...] = total
    over_rows = (((0,), (0,)), ((), ()))
    grad_down_ref[...] = lax.dot_general(
        units_ref[...], dm_ref[...], over_rows, preferred_element_type=jnp.float32
    )
    grad_up_ref[...] = lax.dot_general(
        x_ref[...], dpre_ref[...], over_rows, preferred_element_type=jnp.float32
    )


def mlp_specs(length, width, up_count):
    split = width // HIDDEN_TILE
    resident = pl.BlockSpec((length, width), lambda t: (0, 0))
    up = pl.BlockSpec((None, width, HIDDEN_TILE), lambda t: (t // split, 0, t % split))
    down = pl.BlockSpec(
        (None, HIDDEN_TILE, width), lambda t: (up_count + t // split, t % split, 0)
    )
    hidden = pl.BlockSpec((length, HIDDEN_TILE), lambda t: (0, t))
    bias = pl.BlockSpec((1, HIDDEN_TILE), lambda t: (0, t))
    return split, resident, up, down, hidden, bias


def mlp_forward(rows, blocks, up_bias):
    length, width = rows.shape
    up_count = blocks.shape[0] // 2
    split, resident, up, down, hidden, bias = mlp_specs(length, width, up_count)
    hidden_size = up_count * width
    return pl.pallas_call(
        mlp_forward_kernel,
        grid=(up_count * split,),
        out_shape=(
            jax.ShapeDtypeStruct((length, hidden_size), jnp.bfloat16),
            jax.ShapeDtypeStruct((length, hidden_size), jnp.float32),
            jax.ShapeDtypeStruct((length, width), jnp.float32),
        ),
        in_specs=[resident, up, bias, down],
        out_specs=(hidden, hidden, resident),
        compiler_params=pltpu.CompilerParams(vmem_limit_bytes=48 << 20),
        name="mlp_forward",
    )(rows, blocks, up_bias.reshape(1, hidden_size), blocks)


def mlp_backward(rows, grad_branch, blocks, units, slopes):
    length, width = rows.shape
    up_count = blocks.shape[0] // 2
    split, resident, up, down, hidden, bias = mlp_specs(length, width, up_count)
    hidden_size = up_count * width
    return pl.pallas_call(
        mlp_backward_kernel,
        grid=(up_count * split,),
        out_shape=(
            jax.ShapeDtypeStruct((up_count, width, width), jnp.float32),
            jax.ShapeDtypeStruct((up_count, width, width), jnp.float32),
            jax.ShapeDtypeStruct((1, hidden_size), jnp.float32),
            jax.ShapeDtypeStruct((length, width), jnp.float32),
        ),
        in_specs=[resident, resident, up, down, hidden, hidden],
        out_specs=(
            pl.BlockSpec((None, width, HIDDEN_TILE), lambda t: (t // split, 0, t % split)),
            pl.BlockSpec((None, HIDDEN_TILE, width), lambda t: (t // split, t % split, 0)),
            bias,
            resident,
        ),
        scratch_shapes=[pltpu.VMEM((length, HIDDEN_TILE), jnp.bfloat16)],
        compiler_params=pltpu.CompilerParams(vmem_limit_bytes=48 << 20),
        name="mlp_backward",
    )(rows, grad_branch, blocks, blocks, units, slopes)


def attend_rows(blocks, vec_all, patch, pack_ids, key_codes):
    embedded = jnp.dot(patch, blocks[0], preferred_element_type=jnp.float32) + vec_all[0]
    normed_one = norm_rows(embedded, vec_all[1], vec_all[2]).astype(jnp.bfloat16)
    qkv_rows = jnp.einsum(
        "td,kde->kte", normed_one, blocks[1:4], preferred_element_type=jnp.float32
    )
    qkv_bias = jnp.stack([vec_all[3], jnp.zeros_like(vec_all[3]), vec_all[4]])
    qkv_rows = (qkv_rows + qkv_bias[:, None, :]).astype(jnp.bfloat16)
    attended = attention_forward(qkv_rows, pack_ids, key_codes)
    return attended, embedded, normed_one, qkv_rows


def layer_forward(blocks, vec_all, attend):
    attended, mlp_blocks, embedded, normed_one, qkv_rows = attend()
    up_count = mlp_blocks.shape[0] // 2
    hidden = (
        embedded + jnp.dot(attended, blocks[4], preferred_element_type=jnp.float32) + vec_all[5]
    )
    normed_two = norm_rows(hidden, vec_all[6], vec_all[7]).astype(jnp.bfloat16)
    units, slopes, branch = mlp_forward(normed_two, mlp_blocks, vec_all[8 : 8 + up_count])
    output = hidden + branch + vec_all[8 + up_count]
    return (
        output,
        mlp_blocks,
        (embedded, normed_one, qkv_rows, attended, hidden, normed_two, slopes, units),
    )


def layer_backward(
    blocks,
    mlp_blocks,
    vec_all,
    patch,
    saved,
    pack_ids,
    key_codes,
    grad_output,
    grad_gain,
    grad_shift,
    released,
):
    embedded, normed_one, qkv_rows, attended, hidden, normed_two, slopes, units = saved
    feature_dim = patch.shape[1]
    up_count = mlp_blocks.shape[0] // 2
    grad_branch = grad_output.astype(jnp.bfloat16)
    grad_up, grad_down, up_sums, grad_normed_two = mlp_backward(
        normed_two, grad_branch, mlp_blocks, units, slopes
    )
    up_sums, released = lax.optimization_barrier((up_sums, released))
    norm_two_back = jax.vjp(norm_rows, hidden, vec_all[6], vec_all[7])[1]
    grad_hidden_norm, grad_gain_two, grad_shift_two = norm_two_back(grad_normed_two)
    grad_hidden = grad_output + grad_hidden_norm
    grad_attn_out = grad_hidden.astype(jnp.bfloat16)
    grad_attended = jnp.einsum(
        "td,ed->te", grad_attn_out, blocks[4], preferred_element_type=jnp.float32
    ).astype(jnp.bfloat16)
    grad_qkv = attention_backward(qkv_rows, pack_ids, key_codes, grad_attended)
    grad_normed_one = jnp.einsum(
        "kte,kde->td", grad_qkv, blocks[1:4], preferred_element_type=jnp.float32
    )
    norm_one_back = jax.vjp(norm_rows, embedded, vec_all[1], vec_all[2])[1]
    grad_embed_norm, grad_gain_one, grad_shift_one = norm_one_back(grad_normed_one)
    grad_embedded = (grad_hidden + grad_embed_norm).astype(jnp.bfloat16)
    lefts = (patch, normed_one, attended)
    rights = (grad_embedded, grad_qkv, grad_attn_out)
    bias_sums = jnp.stack(
        [
            jnp.sum(grad_embedded.astype(jnp.float32), 0),
            grad_gain_one,
            grad_shift_one,
            jnp.sum(grad_qkv[0].astype(jnp.float32), 0),
            jnp.sum(grad_qkv[2].astype(jnp.float32), 0),
            jnp.sum(grad_attn_out.astype(jnp.float32), 0),
            grad_gain_two,
            grad_shift_two,
        ]
    )
    up_sums = up_sums.reshape(up_count, feature_dim)
    tail_sums = jnp.stack([jnp.sum(grad_branch.astype(jnp.float32), 0), grad_gain, grad_shift])
    grad_vectors = jnp.concatenate([bias_sums, up_sums, tail_sums], 0)
    return (lefts, rights, (grad_up, grad_down), grad_vectors, released)


def torus_place():
    dp, cls = lax.axis_index("dp"), lax.axis_index("cls")
    return dp // 2, dp % 2, cls // 2, cls % 2


def torus_device(z, y, x, core):
    return (z * 2 + y, x * 2 + core)


def encode(pieces, code_refs, scale_ref):
    top = None
    for piece in pieces:
        peak = jnp.max(jnp.abs(piece()), 0, keepdims=True)
        top = peak if top is None else jnp.maximum(top, peak)
    top = jnp.maximum(top, CODE_FLOOR)
    inverse = CODE_TOP / top
    for piece, code_ref in zip(pieces, code_refs):
        code_ref[...] = jnp.round(piece() * inverse).astype(jnp.int32).astype(jnp.int16)
    scale_ref[...] = top * (1.0 / CODE_TOP)


def decode(code, scale):
    return code.astype(jnp.int32).astype(jnp.float32) * scale


def reduce_kernel(counts, *refs):
    sources, refs = refs[: len(counts)], refs[len(counts) :]
    (patch_hbm, first_hbm, mid_hbm, dpatch_hbm, dfirst_hbm, dmid_hbm,
     vec_ref, tail_ref, left_hbm, right_hbm,
     own_hbm, left_out_hbm, right_out_hbm, step_hbm, wide_ref, facts_ref, vec_out_ref,
     left_buf, right_buf, right_full, outs_buf, squares, high_buf, low_buf, sum_slots, tail_slots,
     lhs_buf, rhs_buf, pair_sem,
     in_sem, sum_send, sum_recv, tail_send, tail_recv,
     acc, spare, kept, sent0, got0, sent1, got1, sent2, got2, sent3, got3, sent4, got4,
     ss0, gs0, ss1, gs1, ss2, gs2, ss3, gs3, ss4, gs4, codes, scales, vec_got,
     load_sem, out_sem, send_sem, recv_sem, send_scale_sem, recv_scale_sem,
     vec_send_sem, vec_recv_sem) = refs
    stored = sum(counts)
    paired = dfirst_hbm.shape[0] + 2
    total = stored + paired
    half, width = codes.shape[1], codes.shape[2]
    cols = width // 2
    z, y, x, core = torus_place()
    upper = z // 2
    inner = (z % 2) != upper
    mate_core = torus_device(z, y, x, 1 - core)
    mate_x = torus_device(z, y, 1 - x, core)
    mate_y = torus_device(z, 1 - y, x, core)
    mate_z = torus_device(z + 1 - 2 * (z % 2), y, x, core)
    mate_mid = torus_device(3 - z, y, x, core)
    mate_far = torus_device((z + 2) % 4, y, x, core)

    barrier = pltpu.get_barrier_semaphore()
    dp, cls = lax.axis_index("dp"), lax.axis_index("cls")
    everyone = tail_slots.shape[0]
    quarter = sum_slots.shape[0]
    me = dp * 4 + cls

    def any_mate(n):
        other = lax.rem(me + n, everyone)
        return (other // 4, lax.rem(other, 4))

    def half_mate(n):
        return (upper * quarter + lax.rem(dp + n, quarter), cls)

    for n in range(1, everyone):
        pl.semaphore_signal(barrier, inc=1, device_id=any_mate(n), device_id_type=MESH)
    pl.semaphore_wait(barrier, everyone - 1)
    own = lax.rem(dp, quarter) * left_buf.shape[1]

    own_cols = pl.ds(pl.multiple_of(core * cols, 128), cols)
    other_cols = pl.ds(pl.multiple_of((1 - core) * cols, 128), cols)

    def rows_at(start, size):
        return pl.ds(pl.multiple_of(start, PIECE), size)

    def loads(m, body):
        start = 0
        for source, count in zip(sources, counts):
            def one(source=source, start=start):
                pair = (
                    pltpu.make_async_copy(
                        source.at[m - start, :, own_cols], acc.at[m % 5], load_sem.at[m % 2, 0]
                    ),
                    pltpu.make_async_copy(
                        source.at[m - start, :, other_cols], spare.at[m % 2], load_sem.at[m % 2, 1]
                    ),
                )
                for copy in pair:
                    body(copy)

            pl.when((m >= start) & (m < start + count))(one)
            start += count

    def block_of(m):
        return lax.rem(m + paired, total)

    def pair_loads(m, body):
        index = m - stored
        last = paired - 1

        def run(left, right):
            body(pltpu.make_async_copy(left, lhs_buf.at[m % 2], pair_sem.at[m % 2, 0]))
            body(pltpu.make_async_copy(right, rhs_buf.at[m % 2], pair_sem.at[m % 2, 1]))

        pl.when(index == 0)(lambda: run(patch_hbm, dpatch_hbm))
        pl.when((index > 0) & (index < last))(
            lambda: run(first_hbm, dfirst_hbm.at[jnp.clip(index - 1, 0, last - 2)])
        )
        pl.when(index == last)(lambda: run(mid_hbm, dmid_hbm))

    def pair_product(m):
        chunk = 2 * FEATURE_TILE
        for r in range(0, width, chunk):
            left = lhs_buf[m % 2, :, r : r + chunk].T
            for target, columns in ((acc.at[m % 5], own_cols), (spare.at[m % 2], other_cols)):
                target[r : r + chunk, :] = jnp.dot(
                    left, rhs_buf[m % 2, :, columns], preferred_element_type=jnp.float32
                )

    def message(stage, m, source, scale_source, target, scale_target, mate):
        return (
            pltpu.make_async_remote_copy(
                src_ref=source, dst_ref=target,
                send_sem=send_sem.at[stage, m % 2], recv_sem=recv_sem.at[stage, m],
                device_id=mate, device_id_type=MESH,
            ),
            pltpu.make_async_remote_copy(
                src_ref=scale_source, dst_ref=scale_target,
                send_sem=send_scale_sem.at[stage, m % 2], recv_sem=recv_scale_sem.at[stage, m],
                device_id=mate, device_id_type=MESH,
            ),
        )

    def first(m):
        return message(0, m, sent0.at[m % 2], ss0.at[m % 2], got0.at[m], gs0.at[m], mate_core)

    def second(m, b):
        return message(
            1 + b, m, sent1.at[m % 2, b], ss1.at[m % 2, b], got1.at[m, b], gs1.at[m, b],
            mate_y if b else mate_x,
        )

    def third(m, b):
        return message(
            3 + b, m, sent2.at[m % 2, b], ss2.at[m % 2, b], got2.at[m, b], gs2.at[m, b],
            mate_x if b else mate_y,
        )

    def fourth(m):
        return message(5, m, sent3.at[m % 2], ss3.at[m % 2], got3.at[m], gs3.at[m], mate_z)

    def fifth(m):
        return message(6, m, sent4.at[m % 2], ss4.at[m % 2], got4.at[m], gs4.at[m], mate_mid)

    piece_a = 2 * x + y
    piece_b = 4 + 2 * y + x

    def spread(stage, m, piece, count, mate, columns=own_cols):
        rows = pl.ds(pl.multiple_of(piece * PIECE, PIECE), count * PIECE)
        block = codes.at[m, rows, columns]
        scale = scales.at[m, pl.ds(piece, count), :, columns]
        return message(stage, m, block, scale, block, scale, mate)

    def start(copies):
        for copy in copies:
            copy.start()

    def wait_send(copies):
        for copy in copies:
            copy.wait_send()

    def wait_recv(copies):
        for copy in copies:
            copy.wait_recv()

    def vec_copy(step, mate):
        return pltpu.make_async_remote_copy(
            src_ref=vec_got.at[step, 0], dst_ref=vec_got.at[step, 1],
            send_sem=vec_send_sem.at[step], recv_sem=vec_recv_sem.at[step],
            device_id=mate, device_id_type=MESH,
        )

    vec_mates = (mate_core, mate_x, mate_y, mate_z, mate_far)

    loads(jnp.int32(0), lambda copy: copy.start())
    vec_got[0, 0] = vec_ref[...]
    vec_copy(0, vec_mates[0]).start()

    def step(t, carry):
        for n in range(1, 6):
            @pl.when(t == n)
            def _(n=n):
                vec_copy(n - 1, vec_mates[n - 1]).wait()
                value = vec_got[n - 1, 0] + vec_got[n - 1, 1]
                if n < 5:
                    vec_got[n, 0] = value
                    vec_copy(n, vec_mates[n]).start()
                else:
                    vec_out_ref[...] = value

        @pl.when(t < total)
        def _():
            m = t

            @pl.when(m < stored)
            def _():
                loads(m, lambda copy: copy.wait())

            @pl.when(m + 1 < stored)
            def _():
                loads(m + 1, lambda copy: copy.start())

            @pl.when((m + 1 >= stored) & (m + 1 < total))
            def _():
                pair_loads(m + 1, lambda copy: copy.start())

            @pl.when(m >= stored)
            def _():
                pair_loads(m, lambda copy: copy.wait())
                pair_product(m)

            span = 2 * PIECE
            encode(
                [lambda r=r: spare[m % 2, r : r + span, :] for r in range(0, 2 * half, span)],
                [sent0.at[m % 2, r : r + span, :] for r in range(0, 2 * half, span)],
                ss0.at[m % 2],
            )
            start(first(m))

        @pl.when((t >= 1) & (t < total + 1))
        def _():
            m = t - 1
            copies = first(m)
            wait_send(copies)
            wait_recv(copies)
            slot = m % 5
            span = 2 * PIECE
            for r in range(0, 2 * half, span):
                acc[slot, r : r + span, :] += decode(got0[m, r : r + span, :], gs0[m])
            for b in range(2):
                other = (1 - y) if b else (1 - x)
                begins = [h * half + b * 4 * PIECE + other * span for h in range(2)]
                encode(
                    [lambda s=s: acc[slot, rows_at(s, span), :] for s in begins],
                    [sent1.at[m % 2, b, h] for h in range(2)],
                    ss1.at[m % 2, b],
                )
                start(second(m, b))

        @pl.when((t >= 2) & (t < total + 2))
        def _():
            m = t - 2
            slot = m % 5
            span = 2 * PIECE
            for b in range(2):
                copies = second(m, b)
                wait_send(copies)
                wait_recv(copies)
                mine = y if b else x
                other = (1 - x) if b else (1 - y)
                begins = [h * half + b * 4 * PIECE + mine * span for h in range(2)]
                for h, s in enumerate(begins):
                    acc[slot, rows_at(s, span), :] += decode(got1[m, b, h], gs1[m, b])
                encode(
                    [lambda s=s: acc[slot, rows_at(s + other * PIECE, PIECE), :] for s in begins],
                    [sent2.at[m % 2, b, h] for h in range(2)],
                    ss2.at[m % 2, b],
                )
                start(third(m, b))

        @pl.when((t >= 3) & (t < total + 3))
        def _():
            m = t - 3
            slot = m % 5
            for b in range(2):
                copies = third(m, b)
                wait_send(copies)
                wait_recv(copies)
                place = piece_b if b else piece_a
                for h in range(2):
                    kept[m % 3, h, b] = acc[
                        slot, rows_at(h * half + place * PIECE, PIECE), :
                    ] + decode(got2[m, b, h], gs2[m, b])

            @pl.when(jnp.logical_not(inner))
            def _():
                pairs = [(h, b) for h in range(2) for b in range(2)]
                encode(
                    [lambda h=h, b=b: kept[m % 3, h, b] for h, b in pairs],
                    [sent3.at[m % 2, h, b] for h, b in pairs],
                    ss3.at[m % 2],
                )
                start(fourth(m))

        @pl.when((t >= 4) & (t < total + 4))
        def _():
            m = t - 4
            copies = fourth(m)

            @pl.when(jnp.logical_not(inner))
            def _():
                wait_send(copies)

            @pl.when(inner)
            def _():
                wait_recv(copies)
                for h in range(2):
                    for b in range(2):
                        kept[m % 3, h, b] += decode(got3[m, h, b], gs3[m])
                encode(
                    [lambda b=b: kept[m % 3, 1 - upper, b] for b in range(2)],
                    [sent4.at[m % 2, b] for b in range(2)],
                    ss4.at[m % 2],
                )
                start(fifth(m))

        @pl.when((t >= 5) & (t < total + 5))
        def _():
            m = t - 5

            @pl.when(inner)
            def _():
                copies = fifth(m)
                wait_send(copies)
                wait_recv(copies)
                for b in range(2):
                    place = piece_b if b else piece_a
                    value = kept[m % 3, upper, b] + decode(got4[m, b], gs4[m])
                    encode(
                        [lambda value=value: value],
                        [codes.at[m, rows_at(place * PIECE, PIECE), own_cols]],
                        scales.at[m, place, :, own_cols],
                    )
                    start(spread(7 + b, m, place, 1, mate_z))

        @pl.when((t >= 6) & (t < total + 6))
        def _():
            m = t - 6
            for b in range(2):
                place = piece_b if b else piece_a
                copies = spread(7 + b, m, place, 1, mate_z)

                @pl.when(inner)
                def _(copies=copies):
                    wait_send(copies)

                @pl.when(jnp.logical_not(inner))
                def _(copies=copies):
                    wait_recv(copies)

                start(spread(9 + b, m, place, 1, mate_x if b else mate_y))

        @pl.when((t >= 7) & (t < total + 7))
        def _():
            m = t - 7
            for b in range(2):
                place = piece_b if b else piece_a
                theirs = (4 + 2 * y + 1 - x) if b else (2 * x + 1 - y)
                wait_send(spread(9 + b, m, place, 1, mate_x if b else mate_y))
                wait_recv(spread(9 + b, m, theirs, 1, mate_x if b else mate_y))
                begin = (4 + 2 * y) if b else 2 * x
                start(spread(11 + b, m, begin, 2, mate_y if b else mate_x))

        @pl.when((t >= 8) & (t < total + 8))
        def _():
            m = t - 8
            for b in range(2):
                begin = (4 + 2 * y) if b else 2 * x
                theirs = (4 + 2 * (1 - y)) if b else 2 * (1 - x)
                wait_send(spread(11 + b, m, begin, 2, mate_y if b else mate_x))
                wait_recv(spread(11 + b, m, theirs, 2, mate_y if b else mate_x))
            start(spread(13, m, 0, 8, mate_core))

        def ins(m):
            return (
                pltpu.make_async_copy(
                    left_hbm.at[block_of(m)], left_buf.at[m % 2], in_sem.at[m % 2, 0]
                ),
                pltpu.make_async_copy(
                    right_hbm.at[:, block_of(m)], right_buf.at[m % 2], in_sem.at[m % 2, 1]
                ),
            )

        def outs(m):
            targets = (own_hbm, left_out_hbm, right_out_hbm, step_hbm)
            return [
                pltpu.make_async_copy(
                    outs_buf.at[m % 2, n], target.at[block_of(m)], out_sem.at[m % 2, n]
                )
                for n, target in enumerate(targets)
            ]

        @pl.when((t >= 8) & (t < total + 8))
        def _():
            start(ins(t - 8))

        @pl.when((t >= 11) & (t < total + 11))
        def _():
            for copy in outs(t - 11):
                copy.wait()

        @pl.when((t >= 9) & (t < total + 9))
        def _():
            m = t - 9
            wait_send(spread(13, m, 0, 8, mate_core))
            wait_recv(spread(13, m, 0, 8, mate_core, other_cols))
            for copy in ins(m):
                copy.wait()
            precondition_block(
                own, codes.at[m], scales.at[m], left_buf.at[m % 2], right_buf.at[m % 2],
                outs_buf.at[m % 2], squares.at[m], high_buf, low_buf, right_full,
            )
            start(outs(m))

        return carry

    lax.fori_loop(0, total + 11, step, 0)

    def folded(row):
        return sum(row[:, n * 128 : (n + 1) * 128] for n in range(row.shape[1] // 128))

    layer = jnp.zeros((1, 128), jnp.float32)
    mine = lax.rem(dp, quarter)
    sum_slots[mine] = jnp.zeros(sum_slots.shape[1:], jnp.float32)
    for m in range(total):
        layer = layer + folded(squares[m, 0:1, :])
        for quad in range(2):
            part = squares[m, 1:2, quad * cols : (quad + 1) * cols]
            row = 2 * ((m + paired) % total) + quad
            sum_slots[mine, row : row + 1, :] = folded(part)
    once = (cls == 0).astype(jnp.float32)
    first_row = lax.broadcasted_iota(jnp.int32, tail_ref.shape, 0) == 0
    tail_slots[me] = tail_ref[...] + jnp.where(first_row, once * layer, 0.0)

    def sum_copy(n, slot):
        return pltpu.make_async_remote_copy(
            src_ref=sum_slots.at[slot], dst_ref=sum_slots.at[slot],
            send_sem=sum_send.at[n], recv_sem=sum_recv.at[slot],
            device_id=half_mate(n), device_id_type=MESH,
        )

    def tail_copy(n, slot):
        return pltpu.make_async_remote_copy(
            src_ref=tail_slots.at[slot], dst_ref=tail_slots.at[slot],
            send_sem=tail_send.at[n], recv_sem=tail_recv.at[slot],
            device_id=any_mate(n), device_id_type=MESH,
        )

    for n in range(1, quarter):
        sum_copy(n, lax.rem(dp, quarter)).start()
    for n in range(1, everyone):
        tail_copy(n, me).start()
    for n in range(1, quarter):
        sum_copy(n, lax.rem(dp, quarter)).wait_send()
        sum_copy(n, lax.rem(dp + n, quarter)).wait_recv()
    for n in range(1, everyone):
        tail_copy(n, me).wait_send()
        tail_copy(n, lax.rem(me + n, everyone)).wait_recv()
    value = sum_slots[0]
    for n in range(1, quarter):
        value = value + sum_slots[n]
    tail = tail_slots[0]
    for n in range(1, everyone):
        tail = tail + tail_slots[n]
    vec = vec_out_ref[...]
    vec_squares = jnp.sum(jnp.sum(vec * vec, 0, keepdims=True), 1, keepdims=True)
    norm = jnp.sqrt(jnp.sum(tail[0:1], 1, keepdims=True) + vec_squares)
    factor = CLIP_NORM / jnp.maximum(norm, CLIP_NORM)
    mean_squares = jnp.sum(value, 1, keepdims=True) / (half * cols) * factor * factor
    scale = SHAMPOO_RATE * factor * lax.rsqrt(mean_squares + ROOT_EPS)
    for b in range(total):
        for quad in range(2):
            row = 2 * b + quad
            wide_ref[b, :, quad * cols : (quad + 1) * cols] = jnp.broadcast_to(
                scale[row : row + 1], (1, cols)
            )
    rows = lax.broadcasted_iota(jnp.int32, facts_ref.shape, 0)
    loss = jnp.sum(tail[1:2], 1, keepdims=True)
    facts_ref[...] = jnp.where(rows == 0, loss, jnp.where(rows == 1, norm, factor))


def reduce_gradients(
    arrays, lefts, rights, vec_sums, tail, root_left, right_codes, dp_count, cls_count
):
    counts = tuple(array.shape[0] for array in arrays)
    total, rows, width = root_left.shape
    length = lefts[0].shape[0]
    parts, coded_rows = right_codes.shape[0], right_codes.shape[2]
    half, cols = width // 2, width // 2
    sum_rows = 2 * total + -2 * total % 8
    f32, i16 = jnp.float32, jnp.int16

    def pair(*shape):
        return [pltpu.VMEM((2,) + shape, i16), pltpu.VMEM((total,) + shape, i16)]

    def scale_pair(*shape):
        return [
            pltpu.VMEM((2,) + shape + (1, cols), f32),
            pltpu.VMEM((total,) + shape + (1, cols), f32),
        ]

    hbm = pl.BlockSpec(memory_space=pl.ANY)
    vmem = pl.BlockSpec(memory_space=pltpu.VMEM)
    return pl.pallas_call(
        functools.partial(reduce_kernel, counts),
        out_shape=(jax.ShapeDtypeStruct((total, rows, width), f32),) * 4
        + (
            jax.ShapeDtypeStruct((total, 1, width), f32),
            jax.ShapeDtypeStruct(tail.shape, f32),
            jax.ShapeDtypeStruct(vec_sums.shape, f32),
        ),
        in_specs=[hbm] * (len(arrays) + 6) + [vmem, vmem, hbm, hbm],
        out_specs=(hbm,) * 4 + (vmem,) * 3,
        scratch_shapes=[
            pltpu.VMEM((2, rows, width), f32),
            pltpu.VMEM((2, parts, coded_rows, width), jnp.int32),
            pltpu.VMEM((half, width), f32),
            pltpu.VMEM((2, 4, rows, width), f32),
            pltpu.VMEM((total, 2, width), f32),
            pltpu.VMEM((half, width), jnp.bfloat16),
            pltpu.VMEM((half, width), jnp.bfloat16),
            pltpu.VMEM((dp_count // 2, sum_rows, 128), f32),
            pltpu.VMEM((dp_count * cls_count,) + tail.shape, f32),
            pltpu.VMEM((2, length, width), jnp.bfloat16),
            pltpu.VMEM((2, length, width), jnp.bfloat16),
            pltpu.SemaphoreType.DMA((2, 2)),
            pltpu.SemaphoreType.DMA((2, 2)),
            pltpu.SemaphoreType.DMA((dp_count // 2,)),
            pltpu.SemaphoreType.DMA((dp_count // 2,)),
            pltpu.SemaphoreType.DMA((dp_count * cls_count,)),
            pltpu.SemaphoreType.DMA((dp_count * cls_count,)),
            pltpu.VMEM((5, width, cols), f32),
            pltpu.VMEM((2, width, cols), f32),
            pltpu.VMEM((3, 2, 2, PIECE, cols), f32),
        ]
        + pair(width, cols)
        + pair(2, 2, 2 * PIECE, cols)
        + pair(2, 2, PIECE, cols)
        + pair(2, 2, PIECE, cols)
        + pair(2, PIECE, cols)
        + scale_pair()
        + scale_pair(2)
        + scale_pair(2)
        + scale_pair()
        + scale_pair()
        + [
            pltpu.VMEM((total, half, width), i16),
            pltpu.VMEM((total, half // PIECE, 1, width), f32),
            pltpu.VMEM((5, 2) + vec_sums.shape, f32),
            pltpu.SemaphoreType.DMA((2, 2)),
            pltpu.SemaphoreType.DMA((2, 4)),
            pltpu.SemaphoreType.DMA((14, 2)),
            pltpu.SemaphoreType.DMA((14, total)),
            pltpu.SemaphoreType.DMA((14, 2)),
            pltpu.SemaphoreType.DMA((14, total)),
            pltpu.SemaphoreType.DMA((5,)),
            pltpu.SemaphoreType.DMA((5,)),
        ],
        compiler_params=pltpu.CompilerParams(
            collective_id=1, has_side_effects=True, vmem_limit_bytes=60 << 20
        ),
        name="reduce_gradients",
    )(*arrays, *lefts, *rights, vec_sums, tail, root_left, right_codes)


def split_float(values):
    high = values.astype(jnp.bfloat16)
    return high, (values - high.astype(jnp.float32)).astype(jnp.bfloat16)


def stacked_dot(lefts, right, contract_last):
    rows = lefts[0].shape[0]
    left = jnp.concatenate(lefts, 0) if len(lefts) > 1 else lefts[0]
    dims = (((1,), (1 if contract_last else 0,)), ((), ()))
    out = lax.dot_general(left, right, dims, preferred_element_type=jnp.float32)
    return [out[n * rows : (n + 1) * rows] for n in range(len(lefts))]


def encode_roots(part):
    top = jnp.max(jnp.abs(part), 1, keepdims=True)
    level = jnp.ceil(jnp.log2(jnp.maximum(top, 1e-30)))
    codes = jnp.round(part * jnp.exp2(15.0 - level))
    codes = jnp.clip(codes, -32767.0, 32767.0).astype(jnp.int32)
    levels = jnp.broadcast_to(level.astype(jnp.int32), (part.shape[0], 8, part.shape[2]))
    upper = jnp.concatenate([codes[:, 0:8], codes[:, 16:24]], 1)
    lower = jnp.concatenate([codes[:, 8:16], levels], 1)
    return upper * 65536 + (lower + 32768)


def precondition_block(
    own, codes_ref, scales_ref, left_ref, right_codes, outs_ref, squares_ref, high_ref, low_ref,
    right_ref
):
    half, width = codes_ref.shape
    rows = left_ref.shape[0]
    own_rows = pl.ds(pl.multiple_of(own, PIECE), rows)
    parts = right_codes.shape[0]
    size = half // parts
    for n in range(parts):
        packed = right_codes[n]
        upper = lax.shift_right_arithmetic(packed, jnp.full_like(packed, 16)).astype(jnp.float32)
        lower = ((packed & 65535) - 32768).astype(jnp.float32)
        scale = jnp.exp2(lower[8:9] - 15.0)
        right_ref[n * size : n * size + 8, :] = upper[0:8] * scale
        right_ref[n * size + 8 : n * size + 16, :] = lower[0:8] * scale
        right_ref[n * size + 16 : n * size + 24, :] = upper[8:16] * scale
    for piece in range(half // PIECE):
        part = slice(piece * PIECE, (piece + 1) * PIECE)
        high_ref[part, :], low_ref[part, :] = split_float(
            decode(codes_ref[part, :], scales_ref[piece])
        )
    own_value = high_ref[own_rows, :].astype(jnp.float32) + low_ref[own_rows, :].astype(jnp.float32)
    outs_ref[0] = own_value
    squares_ref[0:1, :] = jnp.sum(own_value * own_value, 0, keepdims=True)
    picks = (
        lax.broadcasted_iota(jnp.int32, (rows, half), 1)
        == lax.broadcasted_iota(jnp.int32, (rows, half), 0) + own
    ).astype(jnp.float32).astype(jnp.bfloat16)
    for quad in range(2):
        cols = slice(quad * half, (quad + 1) * half)
        high, low = high_ref[:, cols], low_ref[:, cols]
        mine_high, mine_low = high_ref[own_rows, cols], low_ref[own_rows, cols]
        hh, lh, turned_high = stacked_dot([mine_high, mine_low, picks], high, True)
        hl, turned_low = stacked_dot([mine_high, picks], low, True)
        outs_ref[1, :, cols] = hh + (lh + hl)
        turned_high = turned_high.astype(jnp.bfloat16)
        turned_low = turned_low.astype(jnp.bfloat16)
        root_high, root_low = split_float(left_ref[:, cols])
        thh, tlh, rhh, rlh = stacked_dot([turned_high, turned_low, root_high, root_low], high, False)
        thl, rhl = stacked_dot([turned_high, root_high], low, False)
        outs_ref[2, :, cols] = thh + (tlh + thl)
        half_step = rhh + (rlh + rhl)
        step_high, step_low = split_float(half_step)
        right_high, right_low = split_float(right_ref[:, cols])
        shh, slh = stacked_dot([step_high, step_low], right_high, False)
        (shl,) = stacked_dot([step_high], right_low, False)
        direction = shh + (slh + shl)
        outs_ref[3, :, cols] = direction
        squares_ref[1:2, cols] = jnp.sum(direction * direction, 0, keepdims=True)


def head_kernel(
    image_total, pooled_ref, labels_ref, head_hbm,
    grad_ref, rows_ref, loss_ref,
    head_buf, group_buf, total_buf, slots, load_sem, send_sem, recv_sem, sum_send, sum_recv
):
    dp, cls = lax.axis_index("dp"), lax.axis_index("cls")
    count, rows, width = slots.shape
    images = count * rows
    classes = head_buf.shape[1]
    load = pltpu.make_async_copy(head_hbm, head_buf, load_sem)
    load.start()
    barrier = pltpu.get_barrier_semaphore()
    for n in range(1, count):
        pl.semaphore_signal(
            barrier, inc=1, device_id=(dp, lax.rem(cls + n, count)), device_id_type=MESH
        )
    pl.semaphore_wait(barrier, count - 1)

    def part(ref, index):
        return ref.at[pl.ds(pl.multiple_of(index * rows, 8), rows)]

    def share(n, slot):
        return pltpu.make_async_remote_copy(
            src_ref=pooled_ref, dst_ref=part(group_buf, slot),
            send_sem=send_sem.at[n], recv_sem=recv_sem.at[slot],
            device_id=(dp, lax.rem(cls + n, count)), device_id_type=MESH,
        )

    for n in range(1, count):
        share(n, cls).start()
    part(group_buf, cls)[...] = pooled_ref[...]
    rows_ref[:, width + classes :] = jnp.zeros(
        (images, rows_ref.shape[1] - width - classes), rows_ref.dtype
    )
    for n in range(1, count):
        share(n, cls).wait_send()
        share(n, lax.rem(cls + n, count)).wait_recv()
    load.wait()
    group = group_buf[...].astype(jnp.bfloat16)
    rows_ref[:, :width] = group
    loss = jnp.zeros((1, 1), jnp.float32)
    total = jnp.zeros((images, width), jnp.float32)
    for start in range(0, classes, CLASS_TILE):
        stop = min(classes, start + CLASS_TILE)
        weights = head_buf[:, start:stop]
        logits = jnp.dot(group, weights, preferred_element_type=jnp.float32)
        ids = lax.broadcasted_iota(jnp.int32, logits.shape, 1) + (cls * classes + start)
        target = ids == labels_ref[:, 0:1]
        for n in range(1, labels_ref.shape[1]):
            target = target | (ids == labels_ref[:, n : n + 1])
        target = target.astype(jnp.float32)
        valid = ids < LABELS_REAL
        shrunk = jnp.exp(-jnp.abs(logits))
        terms = jnp.maximum(logits, 0.0) + jnp.log1p(shrunk) - target * logits
        terms = jnp.where(valid, terms, 0.0)
        loss = loss + jnp.sum(jnp.sum(terms, 0, keepdims=True), 1, keepdims=True)
        chance = jnp.where(logits >= 0.0, 1.0, shrunk) / (1.0 + shrunk)
        grads = jnp.where(valid, chance - target, 0.0) / image_total
        grads = grads.astype(jnp.bfloat16)
        rows_ref[:, width + start : width + stop] = grads
        total = total + lax.dot_general(
            grads, weights, (((1,), (1,)), ((), ())), preferred_element_type=jnp.float32
        )
    loss_ref[...] = jnp.broadcast_to(loss / image_total, loss_ref.shape)
    total_buf[...] = total

    def back(n, slot):
        mate = lax.rem(cls + n, count)
        return pltpu.make_async_remote_copy(
            src_ref=part(total_buf, mate), dst_ref=slots.at[slot],
            send_sem=sum_send.at[n], recv_sem=sum_recv.at[slot],
            device_id=(dp, mate), device_id_type=MESH,
        )

    for n in range(1, count):
        back(n, cls).start()
    slots[cls] = part(total_buf, cls)[...]
    for n in range(1, count):
        back(n, cls).wait_send()
        back(n, lax.rem(cls + n, count)).wait_recv()
    value = slots[0]
    for n in range(1, count):
        value = value + slots[n]
    grad_ref[...] = value


def classify(pooled, labels, head_low, cls_count, image_total):
    rows, width = pooled.shape
    images, classes = rows * cls_count, head_low.shape[1]
    wide = width + classes
    wide = wide + -wide % 128
    f32 = jnp.float32
    vmem = pl.BlockSpec(memory_space=pltpu.VMEM)
    return pl.pallas_call(
        functools.partial(head_kernel, image_total),
        out_shape=(
            jax.ShapeDtypeStruct((rows, width), f32),
            jax.ShapeDtypeStruct((images, wide), jnp.bfloat16),
            jax.ShapeDtypeStruct((8, 128), f32),
        ),
        in_specs=[vmem, vmem, pl.BlockSpec(memory_space=pltpu.HBM)],
        out_specs=(vmem, vmem, vmem),
        scratch_shapes=[
            pltpu.VMEM((width, classes), jnp.bfloat16),
            pltpu.VMEM((images, width), f32),
            pltpu.VMEM((images, width), f32),
            pltpu.VMEM((cls_count, rows, width), f32),
            pltpu.SemaphoreType.DMA,
        ]
        + [pltpu.SemaphoreType.DMA((cls_count,)) for _ in range(4)],
        compiler_params=pltpu.CompilerParams(
            collective_id=2, has_side_effects=True, vmem_limit_bytes=60 << 20
        ),
        name="classify",
    )(pooled, labels, head_low)


def gather_steps(own_ref, out_ref, send_sem, recv_sem, copy_sem):
    count, rows, width = own_ref.shape
    cols = width // 2
    z, y, x, core = torus_place()
    mate_core = torus_device(z, y, x, 1 - core)
    mate_x = torus_device(z, y, 1 - x, core)
    mate_y = torus_device(z, 1 - y, x, core)
    own_cols = pl.ds(pl.multiple_of(core * cols, 128), cols)
    other_cols = pl.ds(pl.multiple_of((1 - core) * cols, 128), cols)
    spare = rows - SPAN
    held = x * spare
    lone = (x * SPAN, (1 - x) * SPAN)

    def share(m, zz, yy, start, size):
        begin = (zz * 2 + yy) * rows + start
        return out_ref.at[m, pl.ds(pl.multiple_of(begin, 16), size), own_cols]

    def copy(slot, arrival, m, source, target, mate):
        return pltpu.make_async_remote_copy(
            src_ref=source, dst_ref=target,
            send_sem=send_sem.at[slot, m % 2], recv_sem=recv_sem.at[arrival, m],
            device_id=mate, device_id_type=MESH,
        )

    def local(m):
        return pltpu.make_async_copy(
            own_ref.at[m, :, own_cols], share(m, z, y, 0, rows), copy_sem.at[m % 2]
        )

    def along(m, n, outgoing):
        other = lax.rem(z + n, 4)
        origin = z if outgoing else other
        source = own_ref.at[m, pl.ds(pl.multiple_of(held, 16), SPAN), own_cols]
        mate = torus_device(other, y, x, core)
        return copy(n - 1, origin, m, source, share(m, origin, y, held, SPAN), mate)

    def cross(m, n, outgoing):
        block = share(m, n, y if outgoing else 1 - y, held, SPAN)
        return copy(3 + n, 4 + n, m, block, block, mate_y)

    def patch(m, n, outgoing):
        index = lax.rem(z * 2 + y + n, SHARES)
        block = share(m, index // 2, lax.rem(index, 2), lone[0 if outgoing else 1], spare)
        return copy(6 + n, 7 + n, m, block, block, mate_x)

    def swap(m, columns):
        block = out_ref.at[m, :, columns]
        return copy(14, 15, m, block, block, mate_core)

    def finish(copies):
        for outgoing, incoming in copies:
            outgoing.wait_send()
            incoming.wait_recv()

    def step(t):
        @pl.when(t < count)
        def _():
            local(t).start()
            for n in range(1, 4):
                along(t, n, True).start()

        @pl.when((t >= 1) & (t < count + 1))
        def _():
            m = t - 1
            local(m).wait()
            finish([(along(m, n, True), along(m, n, False)) for n in range(1, 4)])
            for n in range(4):
                cross(m, n, True).start()

        @pl.when((t >= 2) & (t < count + 2))
        def _():
            m = t - 2
            finish([(cross(m, n, True), cross(m, n, False)) for n in range(4)])
            for n in range(1, SHARES):
                patch(m, n, True).start()

        @pl.when((t >= 3) & (t < count + 3))
        def _():
            m = t - 3
            finish([(patch(m, n, True), patch(m, n, False)) for n in range(1, SHARES)])
            swap(m, own_cols).start()

        @pl.when((t >= 4) & (t < count + 4))
        def _():
            m = t - 4
            swap(m, own_cols).wait_send()
            swap(m, other_cols).wait_recv()

    return step, count + GATHER_DEPTH


def column_mate(n):
    z, y, x, core = torus_place()
    other = lax.rem(z * 2 + y + n, SHARES)
    return torus_device(other // 2, lax.rem(other, 2), x, core)


def gather_barrier():
    z, y, x, core = torus_place()
    barrier = pltpu.get_barrier_semaphore()
    mates = [torus_device(z, y, x, 1 - core), torus_device(z, y, 1 - x, core)]
    for mate in mates + [column_mate(n) for n in range(1, SHARES)]:
        pl.semaphore_signal(barrier, inc=1, device_id=mate, device_id_type=MESH)
    pl.semaphore_wait(barrier, SHARES + 1)


def gather_kernel(
    own_ref, vec_ref, out_ref, vec_out_ref, send_sem, recv_sem, copy_sem, vec_send, vec_recv
):
    z, y, _, _ = torus_place()
    me = z * 2 + y
    gather_barrier()

    def vec_copy(n, slot):
        return pltpu.make_async_remote_copy(
            src_ref=vec_ref, dst_ref=vec_out_ref.at[slot],
            send_sem=vec_send.at[n], recv_sem=vec_recv.at[slot],
            device_id=column_mate(n), device_id_type=MESH,
        )

    for n in range(1, SHARES):
        vec_copy(n, me).start()
    vec_out_ref[me] = vec_ref[...]
    gather_step, turns = gather_steps(own_ref, out_ref, send_sem, recv_sem, copy_sem)

    def step(t, carry):
        gather_step(t)
        return carry

    lax.fori_loop(0, turns, step, 0)
    for n in range(1, SHARES):
        vec_copy(n, me).wait_send()
        vec_copy(n, lax.rem(me + n, SHARES)).wait_recv()


def gather_semaphores(count):
    return [
        pltpu.SemaphoreType.DMA((15, 2)),
        pltpu.SemaphoreType.DMA((16, count)),
        pltpu.SemaphoreType.DMA((2,)),
    ]


def attention_gather_kernel(
    qids_ref, kcodes_ref, patch_ref, first_ref, vec_ref, own_ref,
    out_ref, blocks_ref, embedded_ref, normed_ref, qkv_ref,
    bias_ref, send_sem, recv_sem, copy_sem
):
    turn, tiles = pl.program_id(0), patch_ref.shape[0] // QTILE
    slots = pl.num_programs(0) * tiles
    pair = jnp.maximum(turn - 1, 0)
    columns = pl.ds(pl.multiple_of(pair * PAIR, PAIR), PAIR)
    pl.when(turn == 0)(gather_barrier)
    gather_step, turns = gather_steps(own_ref, blocks_ref, send_sem, recv_sem, copy_sem)
    attention_bias(qids_ref, kcodes_ref, bias_ref)

    def project(index):
        rows = pl.ds(index * QTILE, QTILE)
        embedded = jnp.dot(patch_ref[rows, :], first_ref[0], preferred_element_type=jnp.float32)
        embedded = embedded + vec_ref[0:1, :]
        embedded_ref[rows, :] = embedded
        normed = norm_rows(embedded, vec_ref[1:2, :], vec_ref[2:3, :]).astype(jnp.bfloat16)
        normed_ref[rows, :] = normed
        for part, shift in enumerate((vec_ref[3:4, :], None, vec_ref[4:5, :])):
            value = jnp.dot(normed, first_ref[1 + part], preferred_element_type=jnp.float32)
            value = value if shift is None else value + shift
            qkv_ref[part, rows, :] = value.astype(jnp.bfloat16)

    for tile in range(tiles):
        slot = turn * tiles + tile
        begin, end = slot * turns // slots, (slot + 1) * turns // slots

        @pl.when(begin < end)
        def _(begin=begin):
            gather_step(begin)

        @pl.when(turn == 0)
        def _(tile=tile):
            project(tile)

        @pl.when(turn > 0)
        def _(tile=tile):
            views = [qkv_ref.at[part, :, columns] for part in range(3)]
            attention_tile(tile, *views, out_ref, bias_ref)


def attention_forward_gathering(patch, first_blocks, vec_all, pack_ids, key_codes, own):
    length, width = patch.shape
    count, rows, _ = own.shape
    tiles = length // QTILE
    steps = 1 + width // PAIR
    assert count + GATHER_DEPTH <= tiles * steps
    bf16 = jnp.bfloat16
    return pl.pallas_call(
        attention_gather_kernel,
        grid=(steps,),
        out_shape=(
            jax.ShapeDtypeStruct((length, width), bf16),
            jax.ShapeDtypeStruct((count, SHARES * rows, width), own.dtype),
            jax.ShapeDtypeStruct((length, width), jnp.float32),
            jax.ShapeDtypeStruct((length, width), bf16),
            jax.ShapeDtypeStruct((3, length, width), bf16),
        ),
        in_specs=[
            whole_spec((length, 1)),
            whole_spec((1, length)),
            whole_spec((length, width)),
            pl.BlockSpec(
                first_blocks.shape, lambda turn: (0, 0, 0), pipeline_mode=pl.Buffered(1)
            ),
            whole_spec(vec_all.shape),
            whole_spec(own.shape),
        ],
        out_specs=(
            pl.BlockSpec((length, PAIR), lambda turn: (0, jnp.maximum(turn - 1, 0))),
            pl.BlockSpec(memory_space=pl.ANY),
            whole_spec((length, width)),
            whole_spec((length, width)),
            whole_spec((3, length, width)),
        ),
        scratch_shapes=[pltpu.VMEM(bias_shape(length), jnp.float32)] + gather_semaphores(count),
        compiler_params=pltpu.CompilerParams(
            collective_id=4, has_side_effects=True, vmem_limit_bytes=56 << 20
        ),
        name="attention_forward",
    )(pack_ids[:, None], key_codes[None, :], patch, first_blocks, vec_all, own)


def gather_weights(own, vec):
    count, rows, width = own.shape
    hbm = pl.BlockSpec(memory_space=pl.ANY)
    vmem = pl.BlockSpec(memory_space=pltpu.VMEM)
    return pl.pallas_call(
        gather_kernel,
        out_shape=(
            jax.ShapeDtypeStruct((count, SHARES * rows, width), own.dtype),
            jax.ShapeDtypeStruct((SHARES,) + vec.shape, vec.dtype),
        ),
        in_specs=[vmem, vmem],
        out_specs=(hbm, vmem),
        scratch_shapes=gather_semaphores(count)
        + [pltpu.SemaphoreType.DMA((SHARES,)), pltpu.SemaphoreType.DMA((SHARES,))],
        compiler_params=pltpu.CompilerParams(
            collective_id=3, has_side_effects=True, vmem_limit_bytes=32 << 20
        ),
        name="gather_weights",
    )(own, vec)


def adam_step(weight, grad, first, second, count):
    first = BETA_FIRST * first + (1.0 - BETA_FIRST) * grad
    second = BETA_SECOND * second + (1.0 - BETA_SECOND) * grad * grad
    fix_first = 1.0 - jnp.power(BETA_FIRST, count)
    fix_second = 1.0 - jnp.power(BETA_SECOND, count)
    update = first / fix_first / (jnp.sqrt(second / fix_second) + ADAM_EPS) + WEIGHT_DECAY * weight
    return (weight - ADAM_RATE * update, first, second)


def split_halves(values, half_size):
    block_count, row_count, feature_dim = values.shape
    return values.reshape(block_count, row_count, 2, half_size)


def reduced_half(values, half_groups):
    part = lax.psum_scatter(values, ("dp", "cls"), scatter_dimension=1, tiled=True)
    return lax.all_gather(part, ("dp", "cls"), axis=1, tiled=True, axis_index_groups=half_groups)


def preconditioned_rows(grad_half, root_left, right_half, own_start):
    count, row_count, width = root_left.shape
    half_size = width // 2
    block_rows = lax.dynamic_slice_in_dim(grad_half, own_start, row_count, 1)
    grad_quads = split_halves(grad_half, half_size)
    rows_quads = split_halves(block_rows, half_size)
    cols_quads = lax.dynamic_slice_in_dim(grad_quads, own_start, row_count, 3)
    precise = FULL_PRECISION
    left_add = jnp.einsum("brjk,bljk->brjl", rows_quads, grad_quads, precision=precise)
    right_add = jnp.einsum("bkja,bkjm->bajm", cols_quads, grad_quads, precision=precise)
    direction = jnp.einsum(
        "brjk,bkjm->brjm", split_halves(root_left, half_size), grad_quads, precision=precise
    )
    direction = jnp.einsum(
        "brjk,bkjm->brjm", direction, split_halves(right_half, half_size), precision=precise
    )
    flat = (count, row_count, width)
    return left_add.reshape(flat), right_add.reshape(flat), direction.reshape(flat), block_rows


def on_device(
    patches,
    image_ids,
    keep,
    labels,
    owner,
    step,
    enc_weights,
    stats_left,
    stats_right,
    root_left,
    root_right,
    head_weights,
    head_m,
    head_v,
    vectors,
    vec_m,
    vec_v,
):
    dp_count = lax.axis_size("dp")
    cls_count = lax.axis_size("cls")
    dp_index = lax.axis_index("dp")
    cls_index = lax.axis_index("cls")
    block_count, row_count, feature_dim = enc_weights.shape
    up_count = (block_count - 5) // 2
    half_size = feature_dim // 2
    part_rows = row_count // cls_count
    half_dp = dp_count // 2
    half_group = half_dp * cls_count
    half_groups = [
        list(range(half_group)),
        list(range(half_group, 2 * half_group)),
    ]

    def my_part(values):
        return lax.dynamic_slice_in_dim(values, cls_index * part_rows, part_rows, 1)

    on_torus = dp_count == 8 and cls_count == 4
    if on_torus:
        vec_block = jnp.pad(vectors, ((0, -vectors.shape[0] % 8), (0, -row_count % 128)))
        own_low = enc_weights.astype(jnp.bfloat16)
        blocks, vec_blocks = gather_weights(own_low[:5], vec_block)
        right_part, vec_blocks = lax.optimization_barrier((my_part(root_right), vec_blocks))
        vec_low = jnp.transpose(vec_blocks[:, : vectors.shape[0], :row_count], (1, 0, 2))
        vec_all = lax.reduce_precision(vec_low.reshape(vectors.shape[0], feature_dim), 8, 7)
    else:
        right_part = my_part(root_right)
        all_blocks = lax.all_gather(
            my_part(enc_weights.astype(jnp.bfloat16)), ("dp", "cls"), axis=1, tiled=True
        )
        blocks = all_blocks[:5]
        vec_low = lax.all_gather(vectors.astype(jnp.bfloat16), "dp", axis=1, tiled=True)
        vec_all = vec_low.astype(jnp.float32)
    head_low = lax.all_gather(head_weights.astype(jnp.bfloat16), "dp", axis=0, tiled=True)
    final_gain = vec_all[9 + up_count]
    final_shift = vec_all[10 + up_count]
    pack_ids, pack_keep = image_ids[0], keep[0]
    key_codes = jnp.where(pack_keep == 1, pack_ids, -1)

    def attend():
        if on_torus:
            return attention_forward_gathering(
                patches, blocks, vec_all, pack_ids, key_codes, own_low[5:]
            )
        attended, *rest = attend_rows(blocks, vec_all, patches, pack_ids, key_codes)
        return (attended, all_blocks[5:], *rest)

    output, mlp_blocks, saved = layer_forward(blocks, vec_all, attend)
    if on_torus:
        right_codes = lax.all_gather(
            encode_roots(right_part), ("dp", "cls"), axis=0, axis_index_groups=half_groups
        )
    else:
        right_half = lax.all_gather(
            right_part, ("dp", "cls"), axis=1, tiled=True, axis_index_groups=half_groups
        )
    pooled = pool_rows(output, final_gain, final_shift, pack_ids, pack_keep)
    class_dev = head_low.shape[1]
    image_total = labels.shape[0] * dp_count
    if on_torus:
        grad_pooled, own_rows, loss_rows = classify(
            lax.reduce_precision(pooled, 8, 7), labels, head_low, cls_count, image_total
        )
        loss_part = loss_rows[0, 0]
    else:
        group = lax.all_gather(pooled.astype(jnp.bfloat16), "cls", axis=0, tiled=True)
        logits = jnp.dot(group, head_low, preferred_element_type=jnp.float32)
        class_ids = cls_index * class_dev + jnp.arange(class_dev)
        valid = class_ids[None, :] < LABELS_REAL
        target = jnp.any(labels[:, :, None] == class_ids[None, None, :], 1).astype(jnp.float32)
        terms = jax.nn.softplus(logits) - target * logits
        loss_part = jnp.sum(jnp.where(valid, terms, 0.0)) / image_total
        grad_logits = jnp.where(valid, jax.nn.sigmoid(logits) - target, 0.0) / image_total
        grad_logits = grad_logits.astype(jnp.bfloat16)
        group_grad = jnp.einsum(
            "gc,dc->gd", grad_logits, head_low, preferred_element_type=jnp.float32
        )
        grad_pooled = lax.psum_scatter(group_grad, "cls", scatter_dimension=0, tiled=True)
        own_rows = jnp.concatenate([group, grad_logits], 1)

    def pool_local(rows_in, gain, shift):
        return pool_rows(rows_in, gain, shift, pack_ids, pack_keep)

    pool_back = jax.vjp(pool_local, output, final_gain, final_shift)[1]
    grad_output, grad_gain, grad_shift = pool_back(grad_pooled)
    lefts, rights, mlp_grads, grad_vectors, (own_rows, roots) = layer_backward(
        blocks,
        mlp_blocks,
        vec_all,
        patches,
        saved,
        pack_ids,
        key_codes,
        grad_output,
        grad_gain,
        grad_shift,
        (own_rows, right_codes if on_torus else right_half),
    )
    head_rows = lax.all_gather(own_rows, "dp", axis=0, tiled=True)
    pooled_all = head_rows[:, :feature_dim]
    grad_logits_all = head_rows[:, feature_dim : feature_dim + class_dev]
    pooled_mine = lax.dynamic_slice_in_dim(pooled_all, dp_index * row_count, row_count, 1)
    head_grad = jnp.einsum(
        "gr,gc->rc", pooled_mine, grad_logits_all, preferred_element_type=jnp.float32
    )

    head_squares = jnp.sum(head_grad * head_grad)
    if on_torus:
        padded = jnp.pad(grad_vectors, ((0, -grad_vectors.shape[0] % 8), (0, 0)))
        tail = jnp.pad(jnp.stack([head_squares, loss_part])[:, None], ((0, 6), (0, 127)))
        block_rows, left_add, right_add, direction, wide_scale, facts, vector_sum = (
            reduce_gradients(
                mlp_grads, lefts, rights, padded, tail, root_left, roots,
                dp_count, cls_count,
            )
        )
        vector_sum = vector_sum[: grad_vectors.shape[0]]
        loss, grad_norm, factor = facts[0, 0], facts[1, 0], facts[2, 0]
    else:
        over_rows = "td,te->de"
        first_grads = [
            jnp.einsum(over_rows, left, right, preferred_element_type=jnp.float32)[None]
            for left, right in (
                (lefts[0], rights[0]),
                (lefts[1], rights[1][0]),
                (lefts[1], rights[1][1]),
                (lefts[1], rights[1][2]),
                (lefts[2], rights[2]),
            )
        ]
        grad_half = reduced_half(jnp.concatenate(first_grads + list(mlp_grads), 0), half_groups)
        vector_sum = lax.psum(grad_vectors, ("dp", "cls"))
        left_add, right_add, direction, block_rows = preconditioned_rows(
            grad_half, root_left, roots, (dp_index % half_dp) * row_count
        )
        squares = jnp.sum(split_halves(direction * direction, half_size), (1, 3))
        in_top = (dp_index < half_dp).astype(jnp.float32)
        once = (cls_index == 0).astype(jnp.float32)
        all_squares = head_squares + once * jnp.sum(block_rows * block_rows)
        packed = jnp.concatenate(
            [
                (once * in_top * squares).reshape(-1),
                (once * (1.0 - in_top) * squares).reshape(-1),
                jnp.stack([all_squares, loss_part]),
            ]
        )
        packed = lax.psum(packed, ("dp", "cls"))
        loss = packed[4 * block_count + 1]
        all_squares = packed[4 * block_count]
        sums = packed[: 4 * block_count].reshape(2, block_count, 2)
        block_squares = jnp.where(dp_index < half_dp, sums[0], sums[1])
        grad_norm = jnp.sqrt(all_squares + jnp.sum(vector_sum * vector_sum))
        factor = CLIP_NORM / jnp.maximum(grad_norm, CLIP_NORM)
        mean_squares = block_squares / (half_size * half_size) * factor * factor
        scale = SHAMPOO_RATE * factor * lax.rsqrt(mean_squares + ROOT_EPS)
        wide_scale = jnp.repeat(scale, half_size, axis=1)[:, None, :]
    vector_rows = lax.dynamic_slice_in_dim(vector_sum, dp_index * row_count, row_count, 1)
    new_blocks = enc_weights - direction * wide_scale
    square_factor = 0.5 * factor * factor
    new_left = 0.5 * stats_left + square_factor * left_add
    new_right = 0.5 * stats_right + square_factor * right_add
    count = step.astype(jnp.float32)
    new_vec, new_vec_m, new_vec_v = adam_step(vectors, vector_rows * factor, vec_m, vec_v, count)
    new_head, new_head_m, new_head_v = adam_step(
        head_weights, head_grad * factor, head_m, head_v, count
    )
    return (
        loss,
        grad_norm,
        new_blocks,
        block_rows * factor,
        new_left,
        new_right,
        new_vec,
        new_vec_m,
        new_vec_v,
        new_head,
        new_head_m,
        new_head_v,
    )


def solution(mesh):
    return jax.shard_map(
        on_device,
        mesh=mesh,
        in_specs=(
            P(("dp", "cls"), None),
            P(("dp", "cls"), None),
            P(("dp", "cls"), None),
            P("dp", None),
            P(),
            P(),
            P(None, "dp", None),
            P(None, "dp", None),
            P(None, "dp", None),
            P(None, "dp", None),
            P(None, "dp", None),
            P("dp", "cls"),
            P("dp", "cls"),
            P("dp", "cls"),
            P(None, "dp"),
            P(None, "dp"),
            P(None, "dp"),
        ),
        out_specs=(
            P(),
            P(),
            P(None, "dp", None),
            P(None, "dp", None),
            P(None, "dp", None),
            P(None, "dp", None),
            P(None, "dp"),
            P(None, "dp"),
            P(None, "dp"),
            P("dp", "cls"),
            P("dp", "cls"),
            P("dp", "cls"),
        ),
        check_vma=False,
    )
```

```python
import functools

import jax
import jax.numpy as jnp
from jax import lax
from jax.experimental import pallas as pl
from jax.experimental.pallas import tpu as pltpu
from jax.sharding import PartitionSpec as P

HEADS = 12
HEAD = 64
LABELS_REAL = 21843
IMAGE_MAX = 196
QTILE = 256
PAIR = 2 * HEAD
ROWS = 256
HIDDEN_TILE = 768
MESH = pl.DeviceIdType.MESH
CODE_TOP = 32766.0
CODE_FLOOR = 1e-33
PIECE = 48
FEATURE_TILE = 128
SPAN = 48
SHARES = 8
GATHER_DEPTH = 4
CLASS_TILE = 512
IMG_PACK = 8


FULL_PRECISION = lax.Precision.HIGHEST
NORM_EPS = 1e-06
CLIP_NORM = 1.0
ADAM_RATE = 0.02
SHAMPOO_RATE = 0.01
BETA_FIRST = 0.9
BETA_SECOND = 0.999
ADAM_EPS = 1e-08
WEIGHT_DECAY = 0.1
ROOT_EPS = 1e-06


def norm_rows(values, gain, shift):
    centred = values - jnp.mean(values, -1, keepdims=True)
    spread = jnp.mean(centred * centred, -1, keepdims=True)
    return centred * lax.rsqrt(spread + NORM_EPS) * gain + shift


def pool_rows(output, gain, shift, pack_ids, pack_keep):
    final = norm_rows(output, gain, shift)
    member = (
        (pack_ids[None, :] == jnp.arange(IMG_PACK)[:, None]) & (pack_keep[None, :] == 1)
    ).astype(jnp.float32)
    counted = jnp.maximum(jnp.sum(member, 1), 1.0)
    return jnp.dot(member, final, precision=FULL_PRECISION) / counted[:, None]


def key_window(tile, length):
    reach = -(-(IMAGE_MAX - 1) // 128) * 128
    low = max(0, tile * QTILE - reach)
    high = min(length, (tile + 1) * QTILE + reach)
    return low, high


def attention_bias(qids_ref, kcodes_ref, bias_ref):
    length = qids_ref.shape[0]

    @pl.when(pl.program_id(0) == 0)
    def _():
        for tile in range(length // QTILE):
            low, high = key_window(tile, length)
            shape = (QTILE, high - low)
            rows = lax.broadcasted_iota(jnp.int32, shape, 0) + tile * QTILE
            cols = lax.broadcasted_iota(jnp.int32, shape, 1) + low
            same = qids_ref[tile * QTILE : (tile + 1) * QTILE, :] == kcodes_ref[:, low:high]
            bias_ref[tile, :, : high - low] = jnp.where(same | (rows == cols), 0.0, -1e30)


def attention_tile(tile, q_ref, k_ref, v_ref, out_ref, bias_ref):
    lane = lax.broadcasted_iota(jnp.int32, (QTILE, PAIR), 1)
    low, high = key_window(tile, q_ref.shape[0])
    rows = pl.ds(tile * QTILE, QTILE)
    queries = q_ref[rows, :] * jnp.bfloat16(HEAD ** (-0.5))
    keys = k_ref[low:high, :]
    values = v_ref[low:high, :]
    halves = []
    for head in range(2):
        mine = (lane >= head * HEAD) & (lane < (head + 1) * HEAD)
        picked = jnp.where(mine, queries, jnp.zeros_like(queries))
        scores = lax.dot_general(
            picked, keys, (((1,), (1,)), ((), ())), preferred_element_type=jnp.float32
        )
        scores = scores + bias_ref[tile, :, : high - low]
        top = jnp.max(scores, -1, keepdims=True)
        weights = jnp.exp(scores - top)
        probs = weights * (1.0 / jnp.sum(weights, -1, keepdims=True))
        halves.append(
            jnp.dot(probs.astype(jnp.bfloat16), values, preferred_element_type=jnp.float32)
        )
    out_ref[rows, :] = jnp.where(lane < HEAD, halves[0], halves[1]).astype(jnp.bfloat16)


def attention_forward_kernel(qids_ref, kcodes_ref, q_ref, k_ref, v_ref, out_ref, bias_ref):
    attention_bias(qids_ref, kcodes_ref, bias_ref)
    for tile in range(q_ref.shape[0] // QTILE):
        attention_tile(tile, q_ref, k_ref, v_ref, out_ref, bias_ref)


def attention_back_bias(qids_ref, kcodes_ref, bias_ref):
    length = kcodes_ref.shape[0]

    @pl.when(pl.program_id(0) == 0)
    def _():
        for tile in range(length // QTILE):
            low, high = key_window(tile, length)
            shape = (high - low, QTILE)
            rows = lax.broadcasted_iota(jnp.int32, shape, 0) + low
            cols = lax.broadcasted_iota(jnp.int32, shape, 1) + tile * QTILE
            same = kcodes_ref[low:high, :] == qids_ref[:, tile * QTILE : (tile + 1) * QTILE]
            bias_ref[tile, : high - low, :] = jnp.where(same | (rows == cols), 0.0, -1e30)


def attention_back_tile(tile, q_ref, k_ref, v_ref, do_ref, out_ref, bias_ref, dk_ref, dv_ref):
    length = q_ref.shape[0]
    lane = lax.broadcasted_iota(jnp.int32, (QTILE, PAIR), 1)
    scale = jnp.bfloat16(HEAD ** (-0.5))
    low, high = key_window(tile, length)
    rows = pl.ds(tile * QTILE, QTILE)
    window = pl.ds(low, high - low)
    queries = q_ref[rows, :] * scale
    keys = k_ref[window, :]
    values = v_ref[window, :]
    grads = do_ref[rows, :]
    halves = []
    for head in range(2):
        mine = (lane >= head * HEAD) & (lane < (head + 1) * HEAD)
        picked = jnp.where(mine, queries, jnp.zeros_like(queries))
        picked_grads = jnp.where(mine, grads, jnp.zeros_like(grads))
        scores = lax.dot_general(
            keys, picked, (((1,), (1,)), ((), ())), preferred_element_type=jnp.float32
        )
        scores = scores + bias_ref[tile, : high - low, :]
        top = jnp.max(scores, 0, keepdims=True)
        weights = jnp.exp(scores - top)
        probs = weights * (1.0 / jnp.sum(weights, 0, keepdims=True))
        grad_probs = lax.dot_general(
            values, picked_grads, (((1,), (1,)), ((), ())), preferred_element_type=jnp.float32
        )
        inner = jnp.sum(probs * grad_probs, 0, keepdims=True)
        grad_scores = (probs * (grad_probs - inner)).astype(jnp.bfloat16)
        dv_ref[window, :] += jnp.dot(
            probs.astype(jnp.bfloat16), picked_grads, preferred_element_type=jnp.float32
        )
        dk_ref[window, :] += jnp.dot(
            grad_scores, picked, preferred_element_type=jnp.float32
        )
        halves.append(
            lax.dot_general(
                grad_scores,
                keys,
                (((0,), (0,)), ((), ())),
                preferred_element_type=jnp.float32,
            )
        )
    grad_queries = jnp.where(lane < HEAD, halves[0], halves[1]) * HEAD ** (-0.5)
    out_ref[0, rows, :] = grad_queries.astype(jnp.bfloat16)


def attention_backward_kernel(
    qids_ref, kcodes_ref, q_ref, k_ref, v_ref, do_ref, out_ref, bias_ref, dk_ref, dv_ref
):
    attention_back_bias(qids_ref, kcodes_ref, bias_ref)
    dk_ref[...] = jnp.zeros_like(dk_ref)
    dv_ref[...] = jnp.zeros_like(dv_ref)
    for tile in range(q_ref.shape[0] // QTILE):
        attention_back_tile(tile, q_ref, k_ref, v_ref, do_ref, out_ref, bias_ref, dk_ref, dv_ref)
    out_ref[1] = dk_ref[...].astype(jnp.bfloat16)
    out_ref[2] = dv_ref[...].astype(jnp.bfloat16)


def pair_spec(length, part=None):
    if part is None:
        return pl.BlockSpec((length, PAIR), lambda pair: (0, pair))
    return pl.BlockSpec((None, length, PAIR), lambda pair: (part, 0, pair))


def whole_spec(shape):
    return pl.BlockSpec(shape, lambda pair: (0,) * len(shape))


def bias_shape(length):
    tiles = length // QTILE
    window = max(high - low for low, high in (key_window(t, length) for t in range(tiles)))
    return tiles, QTILE, window


def attention_forward(qkv_rows, pack_ids, key_codes):
    _, length, width = qkv_rows.shape
    return pl.pallas_call(
        attention_forward_kernel,
        grid=(width // PAIR,),
        out_shape=jax.ShapeDtypeStruct((length, width), jnp.bfloat16),
        in_specs=[whole_spec((length, 1)), whole_spec((1, length))]
        + [pair_spec(length, part) for part in range(3)],
        out_specs=pair_spec(length),
        scratch_shapes=[pltpu.VMEM(bias_shape(length), jnp.float32)],
        compiler_params=pltpu.CompilerParams(vmem_limit_bytes=40 << 20),
        name="attention_forward",
    )(pack_ids[:, None], key_codes[None, :], qkv_rows, qkv_rows, qkv_rows)


def attention_backward(qkv_rows, pack_ids, key_codes, grad_attended):
    _, length, width = qkv_rows.shape
    tiles = length // QTILE
    window = max(high - low for low, high in (key_window(t, length) for t in range(tiles)))
    return pl.pallas_call(
        attention_backward_kernel,
        grid=(width // PAIR,),
        out_shape=jax.ShapeDtypeStruct((3, length, width), jnp.bfloat16),
        in_specs=[whole_spec((1, length)), whole_spec((length, 1))]
        + [pair_spec(length, part) for part in range(3)]
        + [pair_spec(length)],
        out_specs=pl.BlockSpec((3, length, PAIR), lambda pair: (0, 0, pair)),
        scratch_shapes=[
            pltpu.VMEM((tiles, window, QTILE), jnp.float32),
            pltpu.VMEM((length, PAIR), jnp.float32),
            pltpu.VMEM((length, PAIR), jnp.float32),
        ],
        compiler_params=pltpu.CompilerParams(vmem_limit_bytes=40 << 20),
        name="attention_backward",
    )(pack_ids[None, :], key_codes[:, None], qkv_rows, qkv_rows, qkv_rows, grad_attended)


def mlp_forward_kernel(x_ref, up_ref, bias_ref, down_ref, units_ref, slope_ref, out_ref):
    first = pl.program_id(0) == 0

    @pl.when(first)
    def _():
        out_ref[...] = jnp.zeros_like(out_ref)

    for start in range(0, x_ref.shape[0], ROWS):
        rows = pl.ds(start, ROWS)
        pre = jnp.dot(x_ref[rows, :], up_ref[...], preferred_element_type=jnp.float32)
        pre = pre + bias_ref[...]
        half = 0.5 + 0.5 * lax.erf(pre * 0.7071067811865476)
        bell = jnp.exp(-0.5 * pre * pre) * 0.3989422804014327
        units = (pre * half).astype(jnp.bfloat16)
        units_ref[rows, :] = units
        slope_ref[rows, :] = half + pre * bell
        out_ref[rows, :] += jnp.dot(units, down_ref[...], preferred_element_type=jnp.float32)


def mlp_backward_kernel(
    x_ref, dm_ref, up_ref, down_ref, units_ref, slope_ref,
    grad_up_ref, grad_down_ref, bias_ref, dx_ref, dpre_ref
):
    @pl.when(pl.program_id(0) == 0)
    def _():
        dx_ref[...] = jnp.zeros_like(dx_ref)

    total = jnp.zeros((1, HIDDEN_TILE), jnp.float32)
    for start in range(0, x_ref.shape[0], ROWS):
        rows = pl.ds(start, ROWS)
        units_back = lax.dot_general(
            dm_ref[rows, :], down_ref[...], (((1,), (1,)), ((), ())),
            preferred_element_type=jnp.float32,
        )
        grad_pre = (units_back * slope_ref[rows, :]).astype(jnp.bfloat16)
        dpre_ref[rows, :] = grad_pre
        total = total + jnp.sum(grad_pre.astype(jnp.float32), 0, keepdims=True)
        dx_ref[rows, :] += lax.dot_general(
            grad_pre, up_ref[...], (((1,), (1,)), ((), ())), preferred_element_type=jnp.float32
        )
    bias_ref[...] = total
    over_rows = (((0,), (0,)), ((), ()))
    grad_down_ref[...] = lax.dot_general(
        units_ref[...], dm_ref[...], over_rows, preferred_element_type=jnp.float32
    )
    grad_up_ref[...] = lax.dot_general(
        x_ref[...], dpre_ref[...], over_rows, preferred_element_type=jnp.float32
    )


def mlp_specs(length, width, up_count):
    split = width // HIDDEN_TILE
    resident = pl.BlockSpec((length, width), lambda t: (0, 0))
    up = pl.BlockSpec((None, width, HIDDEN_TILE), lambda t: (t // split, 0, t % split))
    down = pl.BlockSpec(
        (None, HIDDEN_TILE, width), lambda t: (up_count + t // split, t % split, 0)
    )
    hidden = pl.BlockSpec((length, HIDDEN_TILE), lambda t: (0, t))
    bias = pl.BlockSpec((1, HIDDEN_TILE), lambda t: (0, t))
    return split, resident, up, down, hidden, bias


def mlp_forward(rows, blocks, up_bias):
    length, width = rows.shape
    up_count = blocks.shape[0] // 2
    split, resident, up, down, hidden, bias = mlp_specs(length, width, up_count)
    hidden_size = up_count * width
    return pl.pallas_call(
        mlp_forward_kernel,
        grid=(up_count * split,),
        out_shape=(
            jax.ShapeDtypeStruct((length, hidden_size), jnp.bfloat16),
            jax.ShapeDtypeStruct((length, hidden_size), jnp.float32),
            jax.ShapeDtypeStruct((length, width), jnp.float32),
        ),
        in_specs=[resident, up, bias, down],
        out_specs=(hidden, hidden, resident),
        compiler_params=pltpu.CompilerParams(vmem_limit_bytes=48 << 20),
        name="mlp_forward",
    )(rows, blocks, up_bias.reshape(1, hidden_size), blocks)


def mlp_backward(rows, grad_branch, blocks, units, slopes):
    length, width = rows.shape
    up_count = blocks.shape[0] // 2
    split, resident, up, down, hidden, bias = mlp_specs(length, width, up_count)
    hidden_size = up_count * width
    return pl.pallas_call(
        mlp_backward_kernel,
        grid=(up_count * split,),
        out_shape=(
            jax.ShapeDtypeStruct((up_count, width, width), jnp.float32),
            jax.ShapeDtypeStruct((up_count, width, width), jnp.float32),
            jax.ShapeDtypeStruct((1, hidden_size), jnp.float32),
            jax.ShapeDtypeStruct((length, width), jnp.float32),
        ),
        in_specs=[resident, resident, up, down, hidden, hidden],
        out_specs=(
            pl.BlockSpec((None, width, HIDDEN_TILE), lambda t: (t // split, 0, t % split)),
            pl.BlockSpec((None, HIDDEN_TILE, width), lambda t: (t // split, t % split, 0)),
            bias,
            resident,
        ),
        scratch_shapes=[pltpu.VMEM((length, HIDDEN_TILE), jnp.bfloat16)],
        compiler_params=pltpu.CompilerParams(vmem_limit_bytes=48 << 20),
        name="mlp_backward",
    )(rows, grad_branch, blocks, blocks, units, slopes)


def layer_forward(blocks, vec_all, patch, attend):
    embedded = jnp.dot(patch, blocks[0], preferred_element_type=jnp.float32) + vec_all[0]
    normed_one = norm_rows(embedded, vec_all[1], vec_all[2]).astype(jnp.bfloat16)
    qkv_rows = jnp.einsum(
        "td,kde->kte", normed_one, blocks[1:4], preferred_element_type=jnp.float32
    )
    qkv_bias = jnp.stack([vec_all[3], jnp.zeros_like(vec_all[3]), vec_all[4]])
    qkv_rows = (qkv_rows + qkv_bias[:, None, :]).astype(jnp.bfloat16)
    attended, mlp_blocks = attend(qkv_rows)
    up_count = mlp_blocks.shape[0] // 2
    hidden = (
        embedded + jnp.dot(attended, blocks[4], preferred_element_type=jnp.float32) + vec_all[5]
    )
    normed_two = norm_rows(hidden, vec_all[6], vec_all[7]).astype(jnp.bfloat16)
    units, slopes, branch = mlp_forward(normed_two, mlp_blocks, vec_all[8 : 8 + up_count])
    output = hidden + branch + vec_all[8 + up_count]
    return (
        output,
        mlp_blocks,
        (embedded, normed_one, qkv_rows, attended, hidden, normed_two, slopes, units),
    )


def layer_backward(
    blocks,
    mlp_blocks,
    vec_all,
    patch,
    saved,
    pack_ids,
    key_codes,
    grad_output,
    grad_gain,
    grad_shift,
    released,
):
    embedded, normed_one, qkv_rows, attended, hidden, normed_two, slopes, units = saved
    feature_dim = patch.shape[1]
    up_count = mlp_blocks.shape[0] // 2
    grad_branch = grad_output.astype(jnp.bfloat16)
    grad_up, grad_down, up_sums, grad_normed_two = mlp_backward(
        normed_two, grad_branch, mlp_blocks, units, slopes
    )
    up_sums, released = lax.optimization_barrier((up_sums, released))
    norm_two_back = jax.vjp(norm_rows, hidden, vec_all[6], vec_all[7])[1]
    grad_hidden_norm, grad_gain_two, grad_shift_two = norm_two_back(grad_normed_two)
    grad_hidden = grad_output + grad_hidden_norm
    grad_attn_out = grad_hidden.astype(jnp.bfloat16)
    grad_attended = jnp.einsum(
        "td,ed->te", grad_attn_out, blocks[4], preferred_element_type=jnp.float32
    ).astype(jnp.bfloat16)
    grad_qkv = attention_backward(qkv_rows, pack_ids, key_codes, grad_attended)
    grad_normed_one = jnp.einsum(
        "kte,kde->td", grad_qkv, blocks[1:4], preferred_element_type=jnp.float32
    )
    norm_one_back = jax.vjp(norm_rows, embedded, vec_all[1], vec_all[2])[1]
    grad_embed_norm, grad_gain_one, grad_shift_one = norm_one_back(grad_normed_one)
    grad_embedded = (grad_hidden + grad_embed_norm).astype(jnp.bfloat16)
    lefts = (patch, normed_one, attended)
    rights = (grad_embedded, grad_qkv, grad_attn_out)
    bias_sums = jnp.stack(
        [
            jnp.sum(grad_embedded.astype(jnp.float32), 0),
            grad_gain_one,
            grad_shift_one,
            jnp.sum(grad_qkv[0].astype(jnp.float32), 0),
            jnp.sum(grad_qkv[2].astype(jnp.float32), 0),
            jnp.sum(grad_attn_out.astype(jnp.float32), 0),
            grad_gain_two,
            grad_shift_two,
        ]
    )
    up_sums = up_sums.reshape(up_count, feature_dim)
    tail_sums = jnp.stack([jnp.sum(grad_branch.astype(jnp.float32), 0), grad_gain, grad_shift])
    grad_vectors = jnp.concatenate([bias_sums, up_sums, tail_sums], 0)
    return (lefts, rights, (grad_up, grad_down), grad_vectors, released)


def torus_place():
    dp, cls = lax.axis_index("dp"), lax.axis_index("cls")
    return dp // 2, dp % 2, cls // 2, cls % 2


def torus_device(z, y, x, core):
    return (z * 2 + y, x * 2 + core)


def encode(pieces, code_refs, scale_ref):
    top = None
    for piece in pieces:
        peak = jnp.max(jnp.abs(piece()), 0, keepdims=True)
        top = peak if top is None else jnp.maximum(top, peak)
    top = jnp.maximum(top, CODE_FLOOR)
    inverse = CODE_TOP / top
    for piece, code_ref in zip(pieces, code_refs):
        code_ref[...] = jnp.round(piece() * inverse).astype(jnp.int32).astype(jnp.int16)
    scale_ref[...] = top * (1.0 / CODE_TOP)


def decode(code, scale):
    return code.astype(jnp.int32).astype(jnp.float32) * scale


def reduce_kernel(counts, *refs):
    sources, refs = refs[: len(counts)], refs[len(counts) :]
    (patch_hbm, first_hbm, mid_hbm, dpatch_hbm, dfirst_hbm, dmid_hbm,
     vec_ref, tail_ref, left_hbm, right_hbm,
     own_hbm, left_out_hbm, right_out_hbm, step_hbm, wide_ref, facts_ref, vec_out_ref,
     left_buf, right_buf, right_full, outs_buf, squares, high_buf, low_buf, sum_slots, tail_slots,
     lhs_buf, rhs_buf, pair_sem,
     in_sem, sum_send, sum_recv, tail_send, tail_recv,
     acc, spare, kept, sent0, got0, sent1, got1, sent2, got2, sent3, got3, sent4, got4,
     ss0, gs0, ss1, gs1, ss2, gs2, ss3, gs3, ss4, gs4, codes, scales, vec_got,
     load_sem, out_sem, send_sem, recv_sem, send_scale_sem, recv_scale_sem,
     vec_send_sem, vec_recv_sem) = refs
    stored = sum(counts)
    paired = dfirst_hbm.shape[0] + 2
    total = stored + paired
    half, width = codes.shape[1], codes.shape[2]
    cols = width // 2
    z, y, x, core = torus_place()
    upper = z // 2
    inner = (z % 2) != upper
    mate_core = torus_device(z, y, x, 1 - core)
    mate_x = torus_device(z, y, 1 - x, core)
    mate_y = torus_device(z, 1 - y, x, core)
    mate_z = torus_device(z + 1 - 2 * (z % 2), y, x, core)
    mate_mid = torus_device(3 - z, y, x, core)
    mate_far = torus_device((z + 2) % 4, y, x, core)

    barrier = pltpu.get_barrier_semaphore()
    dp, cls = lax.axis_index("dp"), lax.axis_index("cls")
    everyone = tail_slots.shape[0]
    quarter = sum_slots.shape[0]
    me = dp * 4 + cls

    def any_mate(n):
        other = lax.rem(me + n, everyone)
        return (other // 4, lax.rem(other, 4))

    def half_mate(n):
        return (upper * quarter + lax.rem(dp + n, quarter), cls)

    for n in range(1, everyone):
        pl.semaphore_signal(barrier, inc=1, device_id=any_mate(n), device_id_type=MESH)
    pl.semaphore_wait(barrier, everyone - 1)
    own = lax.rem(dp, quarter) * left_buf.shape[1]

    own_cols = pl.ds(pl.multiple_of(core * cols, 128), cols)
    other_cols = pl.ds(pl.multiple_of((1 - core) * cols, 128), cols)

    def rows_at(start, size):
        return pl.ds(pl.multiple_of(start, PIECE), size)

    def loads(m, body):
        start = 0
        for source, count in zip(sources, counts):
            def one(source=source, start=start):
                pair = (
                    pltpu.make_async_copy(
                        source.at[m - start, :, own_cols], acc.at[m % 5], load_sem.at[m % 2, 0]
                    ),
                    pltpu.make_async_copy(
                        source.at[m - start, :, other_cols], spare.at[m % 2], load_sem.at[m % 2, 1]
                    ),
                )
                for copy in pair:
                    body(copy)

            pl.when((m >= start) & (m < start + count))(one)
            start += count

    def block_of(m):
        return lax.rem(m + paired, total)

    def pair_loads(m, body):
        index = m - stored
        last = paired - 1

        def run(left, right):
            body(pltpu.make_async_copy(left, lhs_buf.at[m % 2], pair_sem.at[m % 2, 0]))
            body(pltpu.make_async_copy(right, rhs_buf.at[m % 2], pair_sem.at[m % 2, 1]))

        pl.when(index == 0)(lambda: run(patch_hbm, dpatch_hbm))
        pl.when((index > 0) & (index < last))(
            lambda: run(first_hbm, dfirst_hbm.at[jnp.clip(index - 1, 0, last - 2)])
        )
        pl.when(index == last)(lambda: run(mid_hbm, dmid_hbm))

    def pair_product(m):
        chunk = 2 * FEATURE_TILE
        for r in range(0, width, chunk):
            left = lhs_buf[m % 2, :, r : r + chunk].T
            for target, columns in ((acc.at[m % 5], own_cols), (spare.at[m % 2], other_cols)):
                target[r : r + chunk, :] = jnp.dot(
                    left, rhs_buf[m % 2, :, columns], preferred_element_type=jnp.float32
                )

    def message(stage, m, source, scale_source, target, scale_target, mate):
        return (
            pltpu.make_async_remote_copy(
                src_ref=source, dst_ref=target,
                send_sem=send_sem.at[stage, m % 2], recv_sem=recv_sem.at[stage, m],
                device_id=mate, device_id_type=MESH,
            ),
            pltpu.make_async_remote_copy(
                src_ref=scale_source, dst_ref=scale_target,
                send_sem=send_scale_sem.at[stage, m % 2], recv_sem=recv_scale_sem.at[stage, m],
                device_id=mate, device_id_type=MESH,
            ),
        )

    def first(m):
        return message(0, m, sent0.at[m % 2], ss0.at[m % 2], got0.at[m], gs0.at[m], mate_core)

    def second(m, b):
        return message(
            1 + b, m, sent1.at[m % 2, b], ss1.at[m % 2, b], got1.at[m, b], gs1.at[m, b],
            mate_y if b else mate_x,
        )

    def third(m, b):
        return message(
            3 + b, m, sent2.at[m % 2, b], ss2.at[m % 2, b], got2.at[m, b], gs2.at[m, b],
            mate_x if b else mate_y,
        )

    def fourth(m):
        return message(5, m, sent3.at[m % 2], ss3.at[m % 2], got3.at[m], gs3.at[m], mate_z)

    def fifth(m):
        return message(6, m, sent4.at[m % 2], ss4.at[m % 2], got4.at[m], gs4.at[m], mate_mid)

    piece_a = 2 * x + y
    piece_b = 4 + 2 * y + x

    def spread(stage, m, piece, count, mate, columns=own_cols):
        rows = pl.ds(pl.multiple_of(piece * PIECE, PIECE), count * PIECE)
        block = codes.at[m, rows, columns]
        scale = scales.at[m, pl.ds(piece, count), :, columns]
        return message(stage, m, block, scale, block, scale, mate)

    def start(copies):
        for copy in copies:
            copy.start()

    def wait_send(copies):
        for copy in copies:
            copy.wait_send()

    def wait_recv(copies):
        for copy in copies:
            copy.wait_recv()

    def vec_copy(step, mate):
        return pltpu.make_async_remote_copy(
            src_ref=vec_got.at[step, 0], dst_ref=vec_got.at[step, 1],
            send_sem=vec_send_sem.at[step], recv_sem=vec_recv_sem.at[step],
            device_id=mate, device_id_type=MESH,
        )

    vec_mates = (mate_core, mate_x, mate_y, mate_z, mate_far)

    loads(jnp.int32(0), lambda copy: copy.start())
    vec_got[0, 0] = vec_ref[...]
    vec_copy(0, vec_mates[0]).start()

    def step(t, carry):
        for n in range(1, 6):
            @pl.when(t == n)
            def _(n=n):
                vec_copy(n - 1, vec_mates[n - 1]).wait()
                value = vec_got[n - 1, 0] + vec_got[n - 1, 1]
                if n < 5:
                    vec_got[n, 0] = value
                    vec_copy(n, vec_mates[n]).start()
                else:
                    vec_out_ref[...] = value

        @pl.when(t < total)
        def _():
            m = t

            @pl.when(m < stored)
            def _():
                loads(m, lambda copy: copy.wait())

            @pl.when(m + 1 < stored)
            def _():
                loads(m + 1, lambda copy: copy.start())

            @pl.when((m + 1 >= stored) & (m + 1 < total))
            def _():
                pair_loads(m + 1, lambda copy: copy.start())

            @pl.when(m >= stored)
            def _():
                pair_loads(m, lambda copy: copy.wait())
                pair_product(m)

            span = 2 * PIECE
            encode(
                [lambda r=r: spare[m % 2, r : r + span, :] for r in range(0, 2 * half, span)],
                [sent0.at[m % 2, r : r + span, :] for r in range(0, 2 * half, span)],
                ss0.at[m % 2],
            )
            start(first(m))

        @pl.when((t >= 1) & (t < total + 1))
        def _():
            m = t - 1
            copies = first(m)
            wait_send(copies)
            wait_recv(copies)
            slot = m % 5
            span = 2 * PIECE
            for r in range(0, 2 * half, span):
                acc[slot, r : r + span, :] += decode(got0[m, r : r + span, :], gs0[m])
            for b in range(2):
                other = (1 - y) if b else (1 - x)
                begins = [h * half + b * 4 * PIECE + other * span for h in range(2)]
                encode(
                    [lambda s=s: acc[slot, rows_at(s, span), :] for s in begins],
                    [sent1.at[m % 2, b, h] for h in range(2)],
                    ss1.at[m % 2, b],
                )
                start(second(m, b))

        @pl.when((t >= 2) & (t < total + 2))
        def _():
            m = t - 2
            slot = m % 5
            span = 2 * PIECE
            for b in range(2):
                copies = second(m, b)
                wait_send(copies)
                wait_recv(copies)
                mine = y if b else x
                other = (1 - x) if b else (1 - y)
                begins = [h * half + b * 4 * PIECE + mine * span for h in range(2)]
                for h, s in enumerate(begins):
                    acc[slot, rows_at(s, span), :] += decode(got1[m, b, h], gs1[m, b])
                encode(
                    [lambda s=s: acc[slot, rows_at(s + other * PIECE, PIECE), :] for s in begins],
                    [sent2.at[m % 2, b, h] for h in range(2)],
                    ss2.at[m % 2, b],
                )
                start(third(m, b))

        @pl.when((t >= 3) & (t < total + 3))
        def _():
            m = t - 3
            slot = m % 5
            for b in range(2):
                copies = third(m, b)
                wait_send(copies)
                wait_recv(copies)
                place = piece_b if b else piece_a
                for h in range(2):
                    kept[m % 3, h, b] = acc[
                        slot, rows_at(h * half + place * PIECE, PIECE), :
                    ] + decode(got2[m, b, h], gs2[m, b])

            @pl.when(jnp.logical_not(inner))
            def _():
                pairs = [(h, b) for h in range(2) for b in range(2)]
                encode(
                    [lambda h=h, b=b: kept[m % 3, h, b] for h, b in pairs],
                    [sent3.at[m % 2, h, b] for h, b in pairs],
                    ss3.at[m % 2],
                )
                start(fourth(m))

        @pl.when((t >= 4) & (t < total + 4))
        def _():
            m = t - 4
            copies = fourth(m)

            @pl.when(jnp.logical_not(inner))
            def _():
                wait_send(copies)

            @pl.when(inner)
            def _():
                wait_recv(copies)
                for h in range(2):
                    for b in range(2):
                        kept[m % 3, h, b] += decode(got3[m, h, b], gs3[m])
                encode(
                    [lambda b=b: kept[m % 3, 1 - upper, b] for b in range(2)],
                    [sent4.at[m % 2, b] for b in range(2)],
                    ss4.at[m % 2],
                )
                start(fifth(m))

        @pl.when((t >= 5) & (t < total + 5))
        def _():
            m = t - 5

            @pl.when(inner)
            def _():
                copies = fifth(m)
                wait_send(copies)
                wait_recv(copies)
                for b in range(2):
                    place = piece_b if b else piece_a
                    value = kept[m % 3, upper, b] + decode(got4[m, b], gs4[m])
                    encode(
                        [lambda value=value: value],
                        [codes.at[m, rows_at(place * PIECE, PIECE), own_cols]],
                        scales.at[m, place, :, own_cols],
                    )
                    start(spread(7 + b, m, place, 1, mate_z))

        @pl.when((t >= 6) & (t < total + 6))
        def _():
            m = t - 6
            for b in range(2):
                place = piece_b if b else piece_a
                copies = spread(7 + b, m, place, 1, mate_z)

                @pl.when(inner)
                def _(copies=copies):
                    wait_send(copies)

                @pl.when(jnp.logical_not(inner))
                def _(copies=copies):
                    wait_recv(copies)

                start(spread(9 + b, m, place, 1, mate_x if b else mate_y))

        @pl.when((t >= 7) & (t < total + 7))
        def _():
            m = t - 7
            for b in range(2):
                place = piece_b if b else piece_a
                theirs = (4 + 2 * y + 1 - x) if b else (2 * x + 1 - y)
                wait_send(spread(9 + b, m, place, 1, mate_x if b else mate_y))
                wait_recv(spread(9 + b, m, theirs, 1, mate_x if b else mate_y))
                begin = (4 + 2 * y) if b else 2 * x
                start(spread(11 + b, m, begin, 2, mate_y if b else mate_x))

        @pl.when((t >= 8) & (t < total + 8))
        def _():
            m = t - 8
            for b in range(2):
                begin = (4 + 2 * y) if b else 2 * x
                theirs = (4 + 2 * (1 - y)) if b else 2 * (1 - x)
                wait_send(spread(11 + b, m, begin, 2, mate_y if b else mate_x))
                wait_recv(spread(11 + b, m, theirs, 2, mate_y if b else mate_x))
            start(spread(13, m, 0, 8, mate_core))

        def ins(m):
            return (
                pltpu.make_async_copy(
                    left_hbm.at[block_of(m)], left_buf.at[m % 2], in_sem.at[m % 2, 0]
                ),
                pltpu.make_async_copy(
                    right_hbm.at[:, block_of(m)], right_buf.at[m % 2], in_sem.at[m % 2, 1]
                ),
            )

        def outs(m):
            targets = (own_hbm, left_out_hbm, right_out_hbm, step_hbm)
            return [
                pltpu.make_async_copy(
                    outs_buf.at[m % 2, n], target.at[block_of(m)], out_sem.at[m % 2, n]
                )
                for n, target in enumerate(targets)
            ]

        @pl.when((t >= 8) & (t < total + 8))
        def _():
            start(ins(t - 8))

        @pl.when((t >= 11) & (t < total + 11))
        def _():
            for copy in outs(t - 11):
                copy.wait()

        @pl.when((t >= 9) & (t < total + 9))
        def _():
            m = t - 9
            wait_send(spread(13, m, 0, 8, mate_core))
            wait_recv(spread(13, m, 0, 8, mate_core, other_cols))
            for copy in ins(m):
                copy.wait()
            precondition_block(
                own, codes.at[m], scales.at[m], left_buf.at[m % 2], right_buf.at[m % 2],
                outs_buf.at[m % 2], squares.at[m], high_buf, low_buf, right_full,
            )
            start(outs(m))

        return carry

    lax.fori_loop(0, total + 11, step, 0)

    def folded(row):
        return sum(row[:, n * 128 : (n + 1) * 128] for n in range(row.shape[1] // 128))

    layer = jnp.zeros((1, 128), jnp.float32)
    mine = lax.rem(dp, quarter)
    sum_slots[mine] = jnp.zeros(sum_slots.shape[1:], jnp.float32)
    for m in range(total):
        layer = layer + folded(squares[m, 0:1, :])
        for quad in range(2):
            part = squares[m, 1:2, quad * cols : (quad + 1) * cols]
            row = 2 * ((m + paired) % total) + quad
            sum_slots[mine, row : row + 1, :] = folded(part)
    once = (cls == 0).astype(jnp.float32)
    first_row = lax.broadcasted_iota(jnp.int32, tail_ref.shape, 0) == 0
    tail_slots[me] = tail_ref[...] + jnp.where(first_row, once * layer, 0.0)

    def sum_copy(n, slot):
        return pltpu.make_async_remote_copy(
            src_ref=sum_slots.at[slot], dst_ref=sum_slots.at[slot],
            send_sem=sum_send.at[n], recv_sem=sum_recv.at[slot],
            device_id=half_mate(n), device_id_type=MESH,
        )

    def tail_copy(n, slot):
        return pltpu.make_async_remote_copy(
            src_ref=tail_slots.at[slot], dst_ref=tail_slots.at[slot],
            send_sem=tail_send.at[n], recv_sem=tail_recv.at[slot],
            device_id=any_mate(n), device_id_type=MESH,
        )

    for n in range(1, quarter):
        sum_copy(n, lax.rem(dp, quarter)).start()
    for n in range(1, everyone):
        tail_copy(n, me).start()
    for n in range(1, quarter):
        sum_copy(n, lax.rem(dp, quarter)).wait_send()
        sum_copy(n, lax.rem(dp + n, quarter)).wait_recv()
    for n in range(1, everyone):
        tail_copy(n, me).wait_send()
        tail_copy(n, lax.rem(me + n, everyone)).wait_recv()
    value = sum_slots[0]
    for n in range(1, quarter):
        value = value + sum_slots[n]
    tail = tail_slots[0]
    for n in range(1, everyone):
        tail = tail + tail_slots[n]
    vec = vec_out_ref[...]
    vec_squares = jnp.sum(jnp.sum(vec * vec, 0, keepdims=True), 1, keepdims=True)
    norm = jnp.sqrt(jnp.sum(tail[0:1], 1, keepdims=True) + vec_squares)
    factor = CLIP_NORM / jnp.maximum(norm, CLIP_NORM)
    mean_squares = jnp.sum(value, 1, keepdims=True) / (half * cols) * factor * factor
    scale = SHAMPOO_RATE * factor * lax.rsqrt(mean_squares + ROOT_EPS)
    for b in range(total):
        for quad in range(2):
            row = 2 * b + quad
            wide_ref[b, :, quad * cols : (quad + 1) * cols] = jnp.broadcast_to(
                scale[row : row + 1], (1, cols)
            )
    rows = lax.broadcasted_iota(jnp.int32, facts_ref.shape, 0)
    loss = jnp.sum(tail[1:2], 1, keepdims=True)
    facts_ref[...] = jnp.where(rows == 0, loss, jnp.where(rows == 1, norm, factor))


def reduce_gradients(
    arrays, lefts, rights, vec_sums, tail, root_left, right_codes, dp_count, cls_count
):
    counts = tuple(array.shape[0] for array in arrays)
    total, rows, width = root_left.shape
    length = lefts[0].shape[0]
    parts, coded_rows = right_codes.shape[0], right_codes.shape[2]
    half, cols = width // 2, width // 2
    sum_rows = 2 * total + -2 * total % 8
    f32, i16 = jnp.float32, jnp.int16

    def pair(*shape):
        return [pltpu.VMEM((2,) + shape, i16), pltpu.VMEM((total,) + shape, i16)]

    def scale_pair(*shape):
        return [
            pltpu.VMEM((2,) + shape + (1, cols), f32),
            pltpu.VMEM((total,) + shape + (1, cols), f32),
        ]

    hbm = pl.BlockSpec(memory_space=pl.ANY)
    vmem = pl.BlockSpec(memory_space=pltpu.VMEM)
    return pl.pallas_call(
        functools.partial(reduce_kernel, counts),
        out_shape=(jax.ShapeDtypeStruct((total, rows, width), f32),) * 4
        + (
            jax.ShapeDtypeStruct((total, 1, width), f32),
            jax.ShapeDtypeStruct(tail.shape, f32),
            jax.ShapeDtypeStruct(vec_sums.shape, f32),
        ),
        in_specs=[hbm] * (len(arrays) + 6) + [vmem, vmem, hbm, hbm],
        out_specs=(hbm,) * 4 + (vmem,) * 3,
        scratch_shapes=[
            pltpu.VMEM((2, rows, width), f32),
            pltpu.VMEM((2, parts, coded_rows, width), jnp.int32),
            pltpu.VMEM((half, width), f32),
            pltpu.VMEM((2, 4, rows, width), f32),
            pltpu.VMEM((total, 2, width), f32),
            pltpu.VMEM((half, width), jnp.bfloat16),
            pltpu.VMEM((half, width), jnp.bfloat16),
            pltpu.VMEM((dp_count // 2, sum_rows, 128), f32),
            pltpu.VMEM((dp_count * cls_count,) + tail.shape, f32),
            pltpu.VMEM((2, length, width), jnp.bfloat16),
            pltpu.VMEM((2, length, width), jnp.bfloat16),
            pltpu.SemaphoreType.DMA((2, 2)),
            pltpu.SemaphoreType.DMA((2, 2)),
            pltpu.SemaphoreType.DMA((dp_count // 2,)),
            pltpu.SemaphoreType.DMA((dp_count // 2,)),
            pltpu.SemaphoreType.DMA((dp_count * cls_count,)),
            pltpu.SemaphoreType.DMA((dp_count * cls_count,)),
            pltpu.VMEM((5, width, cols), f32),
            pltpu.VMEM((2, width, cols), f32),
            pltpu.VMEM((3, 2, 2, PIECE, cols), f32),
        ]
        + pair(width, cols)
        + pair(2, 2, 2 * PIECE, cols)
        + pair(2, 2, PIECE, cols)
        + pair(2, 2, PIECE, cols)
        + pair(2, PIECE, cols)
        + scale_pair()
        + scale_pair(2)
        + scale_pair(2)
        + scale_pair()
        + scale_pair()
        + [
            pltpu.VMEM((total, half, width), i16),
            pltpu.VMEM((total, half // PIECE, 1, width), f32),
            pltpu.VMEM((5, 2) + vec_sums.shape, f32),
            pltpu.SemaphoreType.DMA((2, 2)),
            pltpu.SemaphoreType.DMA((2, 4)),
            pltpu.SemaphoreType.DMA((14, 2)),
            pltpu.SemaphoreType.DMA((14, total)),
            pltpu.SemaphoreType.DMA((14, 2)),
            pltpu.SemaphoreType.DMA((14, total)),
            pltpu.SemaphoreType.DMA((5,)),
            pltpu.SemaphoreType.DMA((5,)),
        ],
        compiler_params=pltpu.CompilerParams(
            collective_id=1, has_side_effects=True, vmem_limit_bytes=60 << 20
        ),
        name="reduce_gradients",
    )(*arrays, *lefts, *rights, vec_sums, tail, root_left, right_codes)


def split_float(values):
    high = values.astype(jnp.bfloat16)
    return high, (values - high.astype(jnp.float32)).astype(jnp.bfloat16)


def stacked_dot(lefts, right, contract_last):
    rows = lefts[0].shape[0]
    left = jnp.concatenate(lefts, 0) if len(lefts) > 1 else lefts[0]
    dims = (((1,), (1 if contract_last else 0,)), ((), ()))
    out = lax.dot_general(left, right, dims, preferred_element_type=jnp.float32)
    return [out[n * rows : (n + 1) * rows] for n in range(len(lefts))]


def encode_roots(part):
    top = jnp.max(jnp.abs(part), 1, keepdims=True)
    level = jnp.ceil(jnp.log2(jnp.maximum(top, 1e-30)))
    codes = jnp.round(part * jnp.exp2(15.0 - level))
    codes = jnp.clip(codes, -32767.0, 32767.0).astype(jnp.int32)
    levels = jnp.broadcast_to(level.astype(jnp.int32), (part.shape[0], 8, part.shape[2]))
    upper = jnp.concatenate([codes[:, 0:8], codes[:, 16:24]], 1)
    lower = jnp.concatenate([codes[:, 8:16], levels], 1)
    return upper * 65536 + (lower + 32768)


def precondition_block(
    own, codes_ref, scales_ref, left_ref, right_codes, outs_ref, squares_ref, high_ref, low_ref,
    right_ref
):
    half, width = codes_ref.shape
    rows = left_ref.shape[0]
    own_rows = pl.ds(pl.multiple_of(own, PIECE), rows)
    parts = right_codes.shape[0]
    size = half // parts
    for n in range(parts):
        packed = right_codes[n]
        upper = lax.shift_right_arithmetic(packed, jnp.full_like(packed, 16)).astype(jnp.float32)
        lower = ((packed & 65535) - 32768).astype(jnp.float32)
        scale = jnp.exp2(lower[8:9] - 15.0)
        right_ref[n * size : n * size + 8, :] = upper[0:8] * scale
        right_ref[n * size + 8 : n * size + 16, :] = lower[0:8] * scale
        right_ref[n * size + 16 : n * size + 24, :] = upper[8:16] * scale
    for piece in range(half // PIECE):
        part = slice(piece * PIECE, (piece + 1) * PIECE)
        high_ref[part, :], low_ref[part, :] = split_float(
            decode(codes_ref[part, :], scales_ref[piece])
        )
    own_value = high_ref[own_rows, :].astype(jnp.float32) + low_ref[own_rows, :].astype(jnp.float32)
    outs_ref[0] = own_value
    squares_ref[0:1, :] = jnp.sum(own_value * own_value, 0, keepdims=True)
    picks = (
        lax.broadcasted_iota(jnp.int32, (rows, half), 1)
        == lax.broadcasted_iota(jnp.int32, (rows, half), 0) + own
    ).astype(jnp.float32).astype(jnp.bfloat16)
    for quad in range(2):
        cols = slice(quad * half, (quad + 1) * half)
        high, low = high_ref[:, cols], low_ref[:, cols]
        mine_high, mine_low = high_ref[own_rows, cols], low_ref[own_rows, cols]
        hh, lh, turned_high = stacked_dot([mine_high, mine_low, picks], high, True)
        hl, turned_low = stacked_dot([mine_high, picks], low, True)
        outs_ref[1, :, cols] = hh + (lh + hl)
        turned_high = turned_high.astype(jnp.bfloat16)
        turned_low = turned_low.astype(jnp.bfloat16)
        root_high, root_low = split_float(left_ref[:, cols])
        thh, tlh, rhh, rlh = stacked_dot([turned_high, turned_low, root_high, root_low], high, False)
        thl, rhl = stacked_dot([turned_high, root_high], low, False)
        outs_ref[2, :, cols] = thh + (tlh + thl)
        half_step = rhh + (rlh + rhl)
        step_high, step_low = split_float(half_step)
        right_high, right_low = split_float(right_ref[:, cols])
        shh, slh = stacked_dot([step_high, step_low], right_high, False)
        (shl,) = stacked_dot([step_high], right_low, False)
        direction = shh + (slh + shl)
        outs_ref[3, :, cols] = direction
        squares_ref[1:2, cols] = jnp.sum(direction * direction, 0, keepdims=True)


def head_kernel(
    image_total, pooled_ref, labels_ref, head_hbm,
    grad_ref, rows_ref, loss_ref,
    head_buf, group_buf, total_buf, slots, load_sem, send_sem, recv_sem, sum_send, sum_recv
):
    dp, cls = lax.axis_index("dp"), lax.axis_index("cls")
    count, rows, width = slots.shape
    images = count * rows
    classes = head_buf.shape[1]
    load = pltpu.make_async_copy(head_hbm, head_buf, load_sem)
    load.start()
    barrier = pltpu.get_barrier_semaphore()
    for n in range(1, count):
        pl.semaphore_signal(
            barrier, inc=1, device_id=(dp, lax.rem(cls + n, count)), device_id_type=MESH
        )
    pl.semaphore_wait(barrier, count - 1)

    def part(ref, index):
        return ref.at[pl.ds(pl.multiple_of(index * rows, 8), rows)]

    def share(n, slot):
        return pltpu.make_async_remote_copy(
            src_ref=pooled_ref, dst_ref=part(group_buf, slot),
            send_sem=send_sem.at[n], recv_sem=recv_sem.at[slot],
            device_id=(dp, lax.rem(cls + n, count)), device_id_type=MESH,
        )

    for n in range(1, count):
        share(n, cls).start()
    part(group_buf, cls)[...] = pooled_ref[...]
    rows_ref[:, width + classes :] = jnp.zeros(
        (images, rows_ref.shape[1] - width - classes), rows_ref.dtype
    )
    for n in range(1, count):
        share(n, cls).wait_send()
        share(n, lax.rem(cls + n, count)).wait_recv()
    load.wait()
    group = group_buf[...].astype(jnp.bfloat16)
    rows_ref[:, :width] = group
    loss = jnp.zeros((1, 1), jnp.float32)
    total = jnp.zeros((images, width), jnp.float32)
    for start in range(0, classes, CLASS_TILE):
        stop = min(classes, start + CLASS_TILE)
        weights = head_buf[:, start:stop]
        logits = jnp.dot(group, weights, preferred_element_type=jnp.float32)
        ids = lax.broadcasted_iota(jnp.int32, logits.shape, 1) + (cls * classes + start)
        target = ids == labels_ref[:, 0:1]
        for n in range(1, labels_ref.shape[1]):
            target = target | (ids == labels_ref[:, n : n + 1])
        target = target.astype(jnp.float32)
        valid = ids < LABELS_REAL
        shrunk = jnp.exp(-jnp.abs(logits))
        terms = jnp.maximum(logits, 0.0) + jnp.log1p(shrunk) - target * logits
        terms = jnp.where(valid, terms, 0.0)
        loss = loss + jnp.sum(jnp.sum(terms, 0, keepdims=True), 1, keepdims=True)
        chance = jnp.where(logits >= 0.0, 1.0, shrunk) / (1.0 + shrunk)
        grads = jnp.where(valid, chance - target, 0.0) / image_total
        grads = grads.astype(jnp.bfloat16)
        rows_ref[:, width + start : width + stop] = grads
        total = total + lax.dot_general(
            grads, weights, (((1,), (1,)), ((), ())), preferred_element_type=jnp.float32
        )
    loss_ref[...] = jnp.broadcast_to(loss / image_total, loss_ref.shape)
    total_buf[...] = total

    def back(n, slot):
        mate = lax.rem(cls + n, count)
        return pltpu.make_async_remote_copy(
            src_ref=part(total_buf, mate), dst_ref=slots.at[slot],
            send_sem=sum_send.at[n], recv_sem=sum_recv.at[slot],
            device_id=(dp, mate), device_id_type=MESH,
        )

    for n in range(1, count):
        back(n, cls).start()
    slots[cls] = part(total_buf, cls)[...]
    for n in range(1, count):
        back(n, cls).wait_send()
        back(n, lax.rem(cls + n, count)).wait_recv()
    value = slots[0]
    for n in range(1, count):
        value = value + slots[n]
    grad_ref[...] = value


def classify(pooled, labels, head_low, cls_count, image_total):
    rows, width = pooled.shape
    images, classes = rows * cls_count, head_low.shape[1]
    wide = width + classes
    wide = wide + -wide % 128
    f32 = jnp.float32
    vmem = pl.BlockSpec(memory_space=pltpu.VMEM)
    return pl.pallas_call(
        functools.partial(head_kernel, image_total),
        out_shape=(
            jax.ShapeDtypeStruct((rows, width), f32),
            jax.ShapeDtypeStruct((images, wide), jnp.bfloat16),
            jax.ShapeDtypeStruct((8, 128), f32),
        ),
        in_specs=[vmem, vmem, pl.BlockSpec(memory_space=pltpu.HBM)],
        out_specs=(vmem, vmem, vmem),
        scratch_shapes=[
            pltpu.VMEM((width, classes), jnp.bfloat16),
            pltpu.VMEM((images, width), f32),
            pltpu.VMEM((images, width), f32),
            pltpu.VMEM((cls_count, rows, width), f32),
            pltpu.SemaphoreType.DMA,
        ]
        + [pltpu.SemaphoreType.DMA((cls_count,)) for _ in range(4)],
        compiler_params=pltpu.CompilerParams(
            collective_id=2, has_side_effects=True, vmem_limit_bytes=60 << 20
        ),
        name="classify",
    )(pooled, labels, head_low)


def gather_steps(own_ref, out_ref, send_sem, recv_sem, copy_sem):
    count, rows, width = own_ref.shape
    cols = width // 2
    z, y, x, core = torus_place()
    mate_core = torus_device(z, y, x, 1 - core)
    mate_x = torus_device(z, y, 1 - x, core)
    mate_y = torus_device(z, 1 - y, x, core)
    own_cols = pl.ds(pl.multiple_of(core * cols, 128), cols)
    other_cols = pl.ds(pl.multiple_of((1 - core) * cols, 128), cols)
    spare = rows - SPAN
    held = x * spare
    lone = (x * SPAN, (1 - x) * SPAN)

    def share(m, zz, yy, start, size):
        begin = (zz * 2 + yy) * rows + start
        return out_ref.at[m, pl.ds(pl.multiple_of(begin, 16), size), own_cols]

    def copy(slot, arrival, m, source, target, mate):
        return pltpu.make_async_remote_copy(
            src_ref=source, dst_ref=target,
            send_sem=send_sem.at[slot, m % 2], recv_sem=recv_sem.at[arrival, m],
            device_id=mate, device_id_type=MESH,
        )

    def local(m):
        return pltpu.make_async_copy(
            own_ref.at[m, :, own_cols], share(m, z, y, 0, rows), copy_sem.at[m % 2]
        )

    def along(m, n, outgoing):
        other = lax.rem(z + n, 4)
        origin = z if outgoing else other
        source = own_ref.at[m, pl.ds(pl.multiple_of(held, 16), SPAN), own_cols]
        mate = torus_device(other, y, x, core)
        return copy(n - 1, origin, m, source, share(m, origin, y, held, SPAN), mate)

    def cross(m, n, outgoing):
        block = share(m, n, y if outgoing else 1 - y, held, SPAN)
        return copy(3 + n, 4 + n, m, block, block, mate_y)

    def patch(m, n, outgoing):
        index = lax.rem(z * 2 + y + n, SHARES)
        block = share(m, index // 2, lax.rem(index, 2), lone[0 if outgoing else 1], spare)
        return copy(6 + n, 7 + n, m, block, block, mate_x)

    def swap(m, columns):
        block = out_ref.at[m, :, columns]
        return copy(14, 15, m, block, block, mate_core)

    def finish(copies):
        for outgoing, incoming in copies:
            outgoing.wait_send()
            incoming.wait_recv()

    def step(t):
        @pl.when(t < count)
        def _():
            local(t).start()
            for n in range(1, 4):
                along(t, n, True).start()

        @pl.when((t >= 1) & (t < count + 1))
        def _():
            m = t - 1
            local(m).wait()
            finish([(along(m, n, True), along(m, n, False)) for n in range(1, 4)])
            for n in range(4):
                cross(m, n, True).start()

        @pl.when((t >= 2) & (t < count + 2))
        def _():
            m = t - 2
            finish([(cross(m, n, True), cross(m, n, False)) for n in range(4)])
            for n in range(1, SHARES):
                patch(m, n, True).start()

        @pl.when((t >= 3) & (t < count + 3))
        def _():
            m = t - 3
            finish([(patch(m, n, True), patch(m, n, False)) for n in range(1, SHARES)])
            swap(m, own_cols).start()

        @pl.when((t >= 4) & (t < count + 4))
        def _():
            m = t - 4
            swap(m, own_cols).wait_send()
            swap(m, other_cols).wait_recv()

    return step, count + GATHER_DEPTH


def column_mate(n):
    z, y, x, core = torus_place()
    other = lax.rem(z * 2 + y + n, SHARES)
    return torus_device(other // 2, lax.rem(other, 2), x, core)


def gather_barrier():
    z, y, x, core = torus_place()
    barrier = pltpu.get_barrier_semaphore()
    mates = [torus_device(z, y, x, 1 - core), torus_device(z, y, 1 - x, core)]
    for mate in mates + [column_mate(n) for n in range(1, SHARES)]:
        pl.semaphore_signal(barrier, inc=1, device_id=mate, device_id_type=MESH)
    pl.semaphore_wait(barrier, SHARES + 1)


def gather_kernel(
    own_ref, vec_ref, out_ref, vec_out_ref, send_sem, recv_sem, copy_sem, vec_send, vec_recv
):
    z, y, _, _ = torus_place()
    me = z * 2 + y
    gather_barrier()

    def vec_copy(n, slot):
        return pltpu.make_async_remote_copy(
            src_ref=vec_ref, dst_ref=vec_out_ref.at[slot],
            send_sem=vec_send.at[n], recv_sem=vec_recv.at[slot],
            device_id=column_mate(n), device_id_type=MESH,
        )

    for n in range(1, SHARES):
        vec_copy(n, me).start()
    vec_out_ref[me] = vec_ref[...]
    gather_step, turns = gather_steps(own_ref, out_ref, send_sem, recv_sem, copy_sem)

    def step(t, carry):
        gather_step(t)
        return carry

    lax.fori_loop(0, turns, step, 0)
    for n in range(1, SHARES):
        vec_copy(n, me).wait_send()
        vec_copy(n, lax.rem(me + n, SHARES)).wait_recv()


def gather_semaphores(count):
    return [
        pltpu.SemaphoreType.DMA((15, 2)),
        pltpu.SemaphoreType.DMA((16, count)),
        pltpu.SemaphoreType.DMA((2,)),
    ]


def attention_gather_kernel(
    qids_ref, kcodes_ref, q_ref, k_ref, v_ref, own_ref, out_ref, blocks_ref,
    bias_ref, send_sem, recv_sem, copy_sem
):
    pair, tiles = pl.program_id(0), q_ref.shape[0] // QTILE
    slots = pl.num_programs(0) * tiles

    @pl.when(pair == 0)
    def _():
        gather_barrier()

    gather_step, turns = gather_steps(own_ref, blocks_ref, send_sem, recv_sem, copy_sem)
    attention_bias(qids_ref, kcodes_ref, bias_ref)
    for tile in range(tiles):
        slot = pair * tiles + tile
        begin, end = slot * turns // slots, (slot + 1) * turns // slots

        @pl.when(begin < end)
        def _(begin=begin):
            gather_step(begin)

        attention_tile(tile, q_ref, k_ref, v_ref, out_ref, bias_ref)


def attention_forward_gathering(qkv_rows, pack_ids, key_codes, own):
    _, length, width = qkv_rows.shape
    count, rows, _ = own.shape
    tiles = length // QTILE
    assert count + GATHER_DEPTH <= tiles * (width // PAIR)
    return pl.pallas_call(
        attention_gather_kernel,
        grid=(width // PAIR,),
        out_shape=(
            jax.ShapeDtypeStruct((length, width), jnp.bfloat16),
            jax.ShapeDtypeStruct((count, SHARES * rows, width), own.dtype),
        ),
        in_specs=[whole_spec((length, 1)), whole_spec((1, length))]
        + [pair_spec(length, part) for part in range(3)]
        + [whole_spec(own.shape)],
        out_specs=(pair_spec(length), pl.BlockSpec(memory_space=pl.ANY)),
        scratch_shapes=[pltpu.VMEM(bias_shape(length), jnp.float32)] + gather_semaphores(count),
        compiler_params=pltpu.CompilerParams(
            collective_id=4, has_side_effects=True, vmem_limit_bytes=40 << 20
        ),
        name="attention_forward",
    )(pack_ids[:, None], key_codes[None, :], qkv_rows, qkv_rows, qkv_rows, own)


def gather_weights(own, vec):
    count, rows, width = own.shape
    hbm = pl.BlockSpec(memory_space=pl.ANY)
    vmem = pl.BlockSpec(memory_space=pltpu.VMEM)
    return pl.pallas_call(
        gather_kernel,
        out_shape=(
            jax.ShapeDtypeStruct((count, SHARES * rows, width), own.dtype),
            jax.ShapeDtypeStruct((SHARES,) + vec.shape, vec.dtype),
        ),
        in_specs=[vmem, vmem],
        out_specs=(hbm, vmem),
        scratch_shapes=gather_semaphores(count)
        + [pltpu.SemaphoreType.DMA((SHARES,)), pltpu.SemaphoreType.DMA((SHARES,))],
        compiler_params=pltpu.CompilerParams(
            collective_id=3, has_side_effects=True, vmem_limit_bytes=32 << 20
        ),
        name="gather_weights",
    )(own, vec)


def adam_step(weight, grad, first, second, count):
    first = BETA_FIRST * first + (1.0 - BETA_FIRST) * grad
    second = BETA_SECOND * second + (1.0 - BETA_SECOND) * grad * grad
    fix_first = 1.0 - jnp.power(BETA_FIRST, count)
    fix_second = 1.0 - jnp.power(BETA_SECOND, count)
    update = first / fix_first / (jnp.sqrt(second / fix_second) + ADAM_EPS) + WEIGHT_DECAY * weight
    return (weight - ADAM_RATE * update, first, second)


def split_halves(values, half_size):
    block_count, row_count, feature_dim = values.shape
    return values.reshape(block_count, row_count, 2, half_size)


def reduced_half(values, half_groups):
    part = lax.psum_scatter(values, ("dp", "cls"), scatter_dimension=1, tiled=True)
    return lax.all_gather(part, ("dp", "cls"), axis=1, tiled=True, axis_index_groups=half_groups)


def preconditioned_rows(grad_half, root_left, right_half, own_start):
    count, row_count, width = root_left.shape
    half_size = width // 2
    block_rows = lax.dynamic_slice_in_dim(grad_half, own_start, row_count, 1)
    grad_quads = split_halves(grad_half, half_size)
    rows_quads = split_halves(block_rows, half_size)
    cols_quads = lax.dynamic_slice_in_dim(grad_quads, own_start, row_count, 3)
    precise = FULL_PRECISION
    left_add = jnp.einsum("brjk,bljk->brjl", rows_quads, grad_quads, precision=precise)
    right_add = jnp.einsum("bkja,bkjm->bajm", cols_quads, grad_quads, precision=precise)
    direction = jnp.einsum(
        "brjk,bkjm->brjm", split_halves(root_left, half_size), grad_quads, precision=precise
    )
    direction = jnp.einsum(
        "brjk,bkjm->brjm", direction, split_halves(right_half, half_size), precision=precise
    )
    flat = (count, row_count, width)
    return left_add.reshape(flat), right_add.reshape(flat), direction.reshape(flat), block_rows


def on_device(
    patches,
    image_ids,
    keep,
    labels,
    owner,
    step,
    enc_weights,
    stats_left,
    stats_right,
    root_left,
    root_right,
    head_weights,
    head_m,
    head_v,
    vectors,
    vec_m,
    vec_v,
):
    dp_count = lax.axis_size("dp")
    cls_count = lax.axis_size("cls")
    dp_index = lax.axis_index("dp")
    cls_index = lax.axis_index("cls")
    block_count, row_count, feature_dim = enc_weights.shape
    up_count = (block_count - 5) // 2
    half_size = feature_dim // 2
    part_rows = row_count // cls_count
    half_dp = dp_count // 2
    half_group = half_dp * cls_count
    half_groups = [
        list(range(half_group)),
        list(range(half_group, 2 * half_group)),
    ]

    def my_part(values):
        return lax.dynamic_slice_in_dim(values, cls_index * part_rows, part_rows, 1)

    on_torus = dp_count == 8 and cls_count == 4
    if on_torus:
        vec_block = jnp.pad(vectors, ((0, -vectors.shape[0] % 8), (0, -row_count % 128)))
        own_low = enc_weights.astype(jnp.bfloat16)
        blocks, vec_blocks = gather_weights(own_low[:5], vec_block)
        right_part, vec_blocks = lax.optimization_barrier((my_part(root_right), vec_blocks))
        vec_low = jnp.transpose(vec_blocks[:, : vectors.shape[0], :row_count], (1, 0, 2))
        vec_all = lax.reduce_precision(vec_low.reshape(vectors.shape[0], feature_dim), 8, 7)
    else:
        right_part = my_part(root_right)
        all_blocks = lax.all_gather(
            my_part(enc_weights.astype(jnp.bfloat16)), ("dp", "cls"), axis=1, tiled=True
        )
        blocks = all_blocks[:5]
        vec_low = lax.all_gather(vectors.astype(jnp.bfloat16), "dp", axis=1, tiled=True)
        vec_all = vec_low.astype(jnp.float32)
    head_low = lax.all_gather(head_weights.astype(jnp.bfloat16), "dp", axis=0, tiled=True)
    final_gain = vec_all[9 + up_count]
    final_shift = vec_all[10 + up_count]
    pack_ids, pack_keep = image_ids[0], keep[0]
    key_codes = jnp.where(pack_keep == 1, pack_ids, -1)

    def attend(qkv_rows):
        if on_torus:
            return attention_forward_gathering(qkv_rows, pack_ids, key_codes, own_low[5:])
        return attention_forward(qkv_rows, pack_ids, key_codes), all_blocks[5:]

    output, mlp_blocks, saved = layer_forward(blocks, vec_all, patches, attend)
    if on_torus:
        right_codes = lax.all_gather(
            encode_roots(right_part), ("dp", "cls"), axis=0, axis_index_groups=half_groups
        )
    else:
        right_half = lax.all_gather(
            right_part, ("dp", "cls"), axis=1, tiled=True, axis_index_groups=half_groups
        )
    pooled = pool_rows(output, final_gain, final_shift, pack_ids, pack_keep)
    class_dev = head_low.shape[1]
    image_total = labels.shape[0] * dp_count
    if on_torus:
        grad_pooled, own_rows, loss_rows = classify(
            lax.reduce_precision(pooled, 8, 7), labels, head_low, cls_count, image_total
        )
        loss_part = loss_rows[0, 0]
    else:
        group = lax.all_gather(pooled.astype(jnp.bfloat16), "cls", axis=0, tiled=True)
        logits = jnp.dot(group, head_low, preferred_element_type=jnp.float32)
        class_ids = cls_index * class_dev + jnp.arange(class_dev)
        valid = class_ids[None, :] < LABELS_REAL
        target = jnp.any(labels[:, :, None] == class_ids[None, None, :], 1).astype(jnp.float32)
        terms = jax.nn.softplus(logits) - target * logits
        loss_part = jnp.sum(jnp.where(valid, terms, 0.0)) / image_total
        grad_logits = jnp.where(valid, jax.nn.sigmoid(logits) - target, 0.0) / image_total
        grad_logits = grad_logits.astype(jnp.bfloat16)
        group_grad = jnp.einsum(
            "gc,dc->gd", grad_logits, head_low, preferred_element_type=jnp.float32
        )
        grad_pooled = lax.psum_scatter(group_grad, "cls", scatter_dimension=0, tiled=True)
        own_rows = jnp.concatenate([group, grad_logits], 1)

    def pool_local(rows_in, gain, shift):
        return pool_rows(rows_in, gain, shift, pack_ids, pack_keep)

    pool_back = jax.vjp(pool_local, output, final_gain, final_shift)[1]
    grad_output, grad_gain, grad_shift = pool_back(grad_pooled)
    lefts, rights, mlp_grads, grad_vectors, (own_rows, roots) = layer_backward(
        blocks,
        mlp_blocks,
        vec_all,
        patches,
        saved,
        pack_ids,
        key_codes,
        grad_output,
        grad_gain,
        grad_shift,
        (own_rows, right_codes if on_torus else right_half),
    )
    head_rows = lax.all_gather(own_rows, "dp", axis=0, tiled=True)
    pooled_all = head_rows[:, :feature_dim]
    grad_logits_all = head_rows[:, feature_dim : feature_dim + class_dev]
    pooled_mine = lax.dynamic_slice_in_dim(pooled_all, dp_index * row_count, row_count, 1)
    head_grad = jnp.einsum(
        "gr,gc->rc", pooled_mine, grad_logits_all, preferred_element_type=jnp.float32
    )

    head_squares = jnp.sum(head_grad * head_grad)
    if on_torus:
        padded = jnp.pad(grad_vectors, ((0, -grad_vectors.shape[0] % 8), (0, 0)))
        tail = jnp.pad(jnp.stack([head_squares, loss_part])[:, None], ((0, 6), (0, 127)))
        block_rows, left_add, right_add, direction, wide_scale, facts, vector_sum = (
            reduce_gradients(
                mlp_grads, lefts, rights, padded, tail, root_left, roots,
                dp_count, cls_count,
            )
        )
        vector_sum = vector_sum[: grad_vectors.shape[0]]
        loss, grad_norm, factor = facts[0, 0], facts[1, 0], facts[2, 0]
    else:
        over_rows = "td,te->de"
        first_grads = [
            jnp.einsum(over_rows, left, right, preferred_element_type=jnp.float32)[None]
            for left, right in (
                (lefts[0], rights[0]),
                (lefts[1], rights[1][0]),
                (lefts[1], rights[1][1]),
                (lefts[1], rights[1][2]),
                (lefts[2], rights[2]),
            )
        ]
        grad_half = reduced_half(jnp.concatenate(first_grads + list(mlp_grads), 0), half_groups)
        vector_sum = lax.psum(grad_vectors, ("dp", "cls"))
        left_add, right_add, direction, block_rows = preconditioned_rows(
            grad_half, root_left, roots, (dp_index % half_dp) * row_count
        )
        squares = jnp.sum(split_halves(direction * direction, half_size), (1, 3))
        in_top = (dp_index < half_dp).astype(jnp.float32)
        once = (cls_index == 0).astype(jnp.float32)
        all_squares = head_squares + once * jnp.sum(block_rows * block_rows)
        packed = jnp.concatenate(
            [
                (once * in_top * squares).reshape(-1),
                (once * (1.0 - in_top) * squares).reshape(-1),
                jnp.stack([all_squares, loss_part]),
            ]
        )
        packed = lax.psum(packed, ("dp", "cls"))
        loss = packed[4 * block_count + 1]
        all_squares = packed[4 * block_count]
        sums = packed[: 4 * block_count].reshape(2, block_count, 2)
        block_squares = jnp.where(dp_index < half_dp, sums[0], sums[1])
        grad_norm = jnp.sqrt(all_squares + jnp.sum(vector_sum * vector_sum))
        factor = CLIP_NORM / jnp.maximum(grad_norm, CLIP_NORM)
        mean_squares = block_squares / (half_size * half_size) * factor * factor
        scale = SHAMPOO_RATE * factor * lax.rsqrt(mean_squares + ROOT_EPS)
        wide_scale = jnp.repeat(scale, half_size, axis=1)[:, None, :]
    vector_rows = lax.dynamic_slice_in_dim(vector_sum, dp_index * row_count, row_count, 1)
    new_blocks = enc_weights - direction * wide_scale
    square_factor = 0.5 * factor * factor
    new_left = 0.5 * stats_left + square_factor * left_add
    new_right = 0.5 * stats_right + square_factor * right_add
    count = step.astype(jnp.float32)
    new_vec, new_vec_m, new_vec_v = adam_step(vectors, vector_rows * factor, vec_m, vec_v, count)
    new_head, new_head_m, new_head_v = adam_step(
        head_weights, head_grad * factor, head_m, head_v, count
    )
    return (
        loss,
        grad_norm,
        new_blocks,
        block_rows * factor,
        new_left,
        new_right,
        new_vec,
        new_vec_m,
        new_vec_v,
        new_head,
        new_head_m,
        new_head_v,
    )


def solution(mesh):
    return jax.shard_map(
        on_device,
        mesh=mesh,
        in_specs=(
            P(("dp", "cls"), None),
            P(("dp", "cls"), None),
            P(("dp", "cls"), None),
            P("dp", None),
            P(),
            P(),
            P(None, "dp", None),
            P(None, "dp", None),
            P(None, "dp", None),
            P(None, "dp", None),
            P(None, "dp", None),
            P("dp", "cls"),
            P("dp", "cls"),
            P("dp", "cls"),
            P(None, "dp"),
            P(None, "dp"),
            P(None, "dp"),
        ),
        out_specs=(
            P(),
            P(),
            P(None, "dp", None),
            P(None, "dp", None),
            P(None, "dp", None),
            P(None, "dp", None),
            P(None, "dp"),
            P(None, "dp"),
            P(None, "dp"),
            P("dp", "cls"),
            P("dp", "cls"),
            P("dp", "cls"),
        ),
        check_vma=False,
    )
```

```python
import functools

import jax
import jax.numpy as jnp
from jax import lax
from jax.experimental import pallas as pl
from jax.experimental.pallas import tpu as pltpu
from jax.sharding import PartitionSpec as P

HEADS = 12
HEAD = 64
LABELS_REAL = 21843
IMAGE_MAX = 196
QTILE = 512
PAIR = 2 * HEAD
ROWS = 256
HIDDEN_TILE = 768
MESH = pl.DeviceIdType.MESH
CODE_TOP = 32766.0
CODE_FLOOR = 1e-33
PIECE = 48
FEATURE_TILE = 128
SPAN = 48
SHARES = 8
GATHER_DEPTH = 4
CLASS_TILE = 512
IMG_PACK = 8


FULL_PRECISION = lax.Precision.HIGHEST
NORM_EPS = 1e-06
CLIP_NORM = 1.0
ADAM_RATE = 0.02
SHAMPOO_RATE = 0.01
BETA_FIRST = 0.9
BETA_SECOND = 0.999
ADAM_EPS = 1e-08
WEIGHT_DECAY = 0.1
ROOT_EPS = 1e-06


def norm_rows(values, gain, shift):
    centred = values - jnp.mean(values, -1, keepdims=True)
    spread = jnp.mean(centred * centred, -1, keepdims=True)
    return centred * lax.rsqrt(spread + NORM_EPS) * gain + shift


def pool_rows(output, gain, shift, pack_ids, pack_keep):
    final = norm_rows(output, gain, shift)
    member = (
        (pack_ids[None, :] == jnp.arange(IMG_PACK)[:, None]) & (pack_keep[None, :] == 1)
    ).astype(jnp.float32)
    counted = jnp.maximum(jnp.sum(member, 1), 1.0)
    return jnp.dot(member, final, precision=FULL_PRECISION) / counted[:, None]


def key_window(tile, length):
    reach = -(-(IMAGE_MAX - 1) // 128) * 128
    low = max(0, tile * QTILE - reach)
    high = min(length, (tile + 1) * QTILE + reach)
    return low, high


def attention_bias(qids_ref, kcodes_ref, bias_ref):
    length = qids_ref.shape[0]

    @pl.when(pl.program_id(0) == 0)
    def _():
        for tile in range(length // QTILE):
            low, high = key_window(tile, length)
            shape = (QTILE, high - low)
            rows = lax.broadcasted_iota(jnp.int32, shape, 0) + tile * QTILE
            cols = lax.broadcasted_iota(jnp.int32, shape, 1) + low
            same = qids_ref[tile * QTILE : (tile + 1) * QTILE, :] == kcodes_ref[:, low:high]
            bias_ref[tile, :, : high - low] = jnp.where(same | (rows == cols), 0.0, -1e30)


def attention_tile(tile, q_ref, k_ref, v_ref, out_ref, bias_ref):
    lane = lax.broadcasted_iota(jnp.int32, (QTILE, PAIR), 1)
    low, high = key_window(tile, q_ref.shape[0])
    rows = pl.ds(tile * QTILE, QTILE)
    queries = q_ref[rows, :] * jnp.bfloat16(HEAD ** (-0.5))
    keys = k_ref[low:high, :]
    values = v_ref[low:high, :]
    halves = []
    for head in range(2):
        mine = (lane >= head * HEAD) & (lane < (head + 1) * HEAD)
        picked = jnp.where(mine, queries, jnp.zeros_like(queries))
        scores = lax.dot_general(
            picked, keys, (((1,), (1,)), ((), ())), preferred_element_type=jnp.float32
        )
        scores = scores + bias_ref[tile, :, : high - low]
        top = jnp.max(scores, -1, keepdims=True)
        weights = jnp.exp(scores - top)
        probs = weights * (1.0 / jnp.sum(weights, -1, keepdims=True))
        halves.append(
            jnp.dot(probs.astype(jnp.bfloat16), values, preferred_element_type=jnp.float32)
        )
    out_ref[rows, :] = jnp.where(lane < HEAD, halves[0], halves[1]).astype(jnp.bfloat16)


def attention_forward_kernel(qids_ref, kcodes_ref, q_ref, k_ref, v_ref, out_ref, bias_ref):
    attention_bias(qids_ref, kcodes_ref, bias_ref)
    for tile in range(q_ref.shape[0] // QTILE):
        attention_tile(tile, q_ref, k_ref, v_ref, out_ref, bias_ref)


def attention_back_bias(qids_ref, kcodes_ref, bias_ref):
    length = kcodes_ref.shape[0]

    @pl.when(pl.program_id(0) == 0)
    def _():
        for tile in range(length // QTILE):
            low, high = key_window(tile, length)
            shape = (high - low, QTILE)
            rows = lax.broadcasted_iota(jnp.int32, shape, 0) + low
            cols = lax.broadcasted_iota(jnp.int32, shape, 1) + tile * QTILE
            same = kcodes_ref[low:high, :] == qids_ref[:, tile * QTILE : (tile + 1) * QTILE]
            bias_ref[tile, : high - low, :] = jnp.where(same | (rows == cols), 0.0, -1e30)


def attention_back_tile(tile, q_ref, k_ref, v_ref, do_ref, out_ref, bias_ref, dk_ref, dv_ref):
    length = q_ref.shape[0]
    lane = lax.broadcasted_iota(jnp.int32, (QTILE, PAIR), 1)
    scale = jnp.bfloat16(HEAD ** (-0.5))
    low, high = key_window(tile, length)
    rows = pl.ds(tile * QTILE, QTILE)
    window = pl.ds(low, high - low)
    queries = q_ref[rows, :] * scale
    keys = k_ref[window, :]
    values = v_ref[window, :]
    grads = do_ref[rows, :]
    halves = []
    for head in range(2):
        mine = (lane >= head * HEAD) & (lane < (head + 1) * HEAD)
        picked = jnp.where(mine, queries, jnp.zeros_like(queries))
        picked_grads = jnp.where(mine, grads, jnp.zeros_like(grads))
        scores = lax.dot_general(
            keys, picked, (((1,), (1,)), ((), ())), preferred_element_type=jnp.float32
        )
        scores = scores + bias_ref[tile, : high - low, :]
        top = jnp.max(scores, 0, keepdims=True)
        weights = jnp.exp(scores - top)
        probs = weights * (1.0 / jnp.sum(weights, 0, keepdims=True))
        grad_probs = lax.dot_general(
            values, picked_grads, (((1,), (1,)), ((), ())), preferred_element_type=jnp.float32
        )
        inner = jnp.sum(probs * grad_probs, 0, keepdims=True)
        grad_scores = (probs * (grad_probs - inner)).astype(jnp.bfloat16)
        dv_ref[window, :] += jnp.dot(
            probs.astype(jnp.bfloat16), picked_grads, preferred_element_type=jnp.float32
        )
        dk_ref[window, :] += jnp.dot(
            grad_scores, picked, preferred_element_type=jnp.float32
        )
        halves.append(
            lax.dot_general(
                grad_scores,
                keys,
                (((0,), (0,)), ((), ())),
                preferred_element_type=jnp.float32,
            )
        )
    grad_queries = jnp.where(lane < HEAD, halves[0], halves[1]) * HEAD ** (-0.5)
    out_ref[0, rows, :] = grad_queries.astype(jnp.bfloat16)


def attention_backward_kernel(
    qids_ref, kcodes_ref, q_ref, k_ref, v_ref, do_ref, out_ref, bias_ref, dk_ref, dv_ref
):
    attention_back_bias(qids_ref, kcodes_ref, bias_ref)
    dk_ref[...] = jnp.zeros_like(dk_ref)
    dv_ref[...] = jnp.zeros_like(dv_ref)
    for tile in range(q_ref.shape[0] // QTILE):
        attention_back_tile(tile, q_ref, k_ref, v_ref, do_ref, out_ref, bias_ref, dk_ref, dv_ref)
    out_ref[1] = dk_ref[...].astype(jnp.bfloat16)
    out_ref[2] = dv_ref[...].astype(jnp.bfloat16)


def pair_spec(length, part=None):
    if part is None:
        return pl.BlockSpec((length, PAIR), lambda pair: (0, pair))
    return pl.BlockSpec((None, length, PAIR), lambda pair: (part, 0, pair))


def whole_spec(shape):
    return pl.BlockSpec(shape, lambda pair: (0,) * len(shape))


def bias_shape(length):
    tiles = length // QTILE
    window = max(high - low for low, high in (key_window(t, length) for t in range(tiles)))
    return tiles, QTILE, window


def attention_forward(qkv_rows, pack_ids, key_codes):
    _, length, width = qkv_rows.shape
    return pl.pallas_call(
        attention_forward_kernel,
        grid=(width // PAIR,),
        out_shape=jax.ShapeDtypeStruct((length, width), jnp.bfloat16),
        in_specs=[whole_spec((length, 1)), whole_spec((1, length))]
        + [pair_spec(length, part) for part in range(3)],
        out_specs=pair_spec(length),
        scratch_shapes=[pltpu.VMEM(bias_shape(length), jnp.float32)],
        compiler_params=pltpu.CompilerParams(vmem_limit_bytes=40 << 20),
        name="attention_forward",
    )(pack_ids[:, None], key_codes[None, :], qkv_rows, qkv_rows, qkv_rows)


def attention_backward(qkv_rows, pack_ids, key_codes, grad_attended):
    _, length, width = qkv_rows.shape
    tiles = length // QTILE
    window = max(high - low for low, high in (key_window(t, length) for t in range(tiles)))
    return pl.pallas_call(
        attention_backward_kernel,
        grid=(width // PAIR,),
        out_shape=jax.ShapeDtypeStruct((3, length, width), jnp.bfloat16),
        in_specs=[whole_spec((1, length)), whole_spec((length, 1))]
        + [pair_spec(length, part) for part in range(3)]
        + [pair_spec(length)],
        out_specs=pl.BlockSpec((3, length, PAIR), lambda pair: (0, 0, pair)),
        scratch_shapes=[
            pltpu.VMEM((tiles, window, QTILE), jnp.float32),
            pltpu.VMEM((length, PAIR), jnp.float32),
            pltpu.VMEM((length, PAIR), jnp.float32),
        ],
        compiler_params=pltpu.CompilerParams(vmem_limit_bytes=40 << 20),
        name="attention_backward",
    )(pack_ids[None, :], key_codes[:, None], qkv_rows, qkv_rows, qkv_rows, grad_attended)


def mlp_forward_kernel(x_ref, up_ref, bias_ref, down_ref, units_ref, slope_ref, out_ref):
    first = pl.program_id(0) == 0

    @pl.when(first)
    def _():
        out_ref[...] = jnp.zeros_like(out_ref)

    for start in range(0, x_ref.shape[0], ROWS):
        rows = pl.ds(start, ROWS)
        pre = jnp.dot(x_ref[rows, :], up_ref[...], preferred_element_type=jnp.float32)
        pre = pre + bias_ref[...]
        half = 0.5 + 0.5 * lax.erf(pre * 0.7071067811865476)
        bell = jnp.exp(-0.5 * pre * pre) * 0.3989422804014327
        units = (pre * half).astype(jnp.bfloat16)
        units_ref[rows, :] = units
        slope_ref[rows, :] = half + pre * bell
        out_ref[rows, :] += jnp.dot(units, down_ref[...], preferred_element_type=jnp.float32)


def mlp_backward_kernel(
    x_ref, dm_ref, up_ref, down_ref, units_ref, slope_ref,
    grad_up_ref, grad_down_ref, bias_ref, dx_ref, dpre_ref
):
    @pl.when(pl.program_id(0) == 0)
    def _():
        dx_ref[...] = jnp.zeros_like(dx_ref)

    total = jnp.zeros((1, HIDDEN_TILE), jnp.float32)
    for start in range(0, x_ref.shape[0], ROWS):
        rows = pl.ds(start, ROWS)
        units_back = lax.dot_general(
            dm_ref[rows, :], down_ref[...], (((1,), (1,)), ((), ())),
            preferred_element_type=jnp.float32,
        )
        grad_pre = (units_back * slope_ref[rows, :]).astype(jnp.bfloat16)
        dpre_ref[rows, :] = grad_pre
        total = total + jnp.sum(grad_pre.astype(jnp.float32), 0, keepdims=True)
        dx_ref[rows, :] += lax.dot_general(
            grad_pre, up_ref[...], (((1,), (1,)), ((), ())), preferred_element_type=jnp.float32
        )
    bias_ref[...] = total
    over_rows = (((0,), (0,)), ((), ()))
    grad_down_ref[...] = lax.dot_general(
        units_ref[...], dm_ref[...], over_rows, preferred_element_type=jnp.float32
    )
    grad_up_ref[...] = lax.dot_general(
        x_ref[...], dpre_ref[...], over_rows, preferred_element_type=jnp.float32
    )


def mlp_specs(length, width, up_count):
    split = width // HIDDEN_TILE
    resident = pl.BlockSpec((length, width), lambda t: (0, 0))
    up = pl.BlockSpec((None, width, HIDDEN_TILE), lambda t: (t // split, 0, t % split))
    down = pl.BlockSpec(
        (None, HIDDEN_TILE, width), lambda t: (up_count + t // split, t % split, 0)
    )
    hidden = pl.BlockSpec((length, HIDDEN_TILE), lambda t: (0, t))
    bias = pl.BlockSpec((1, HIDDEN_TILE), lambda t: (0, t))
    return split, resident, up, down, hidden, bias


def mlp_forward(rows, blocks, up_bias):
    length, width = rows.shape
    up_count = blocks.shape[0] // 2
    split, resident, up, down, hidden, bias = mlp_specs(length, width, up_count)
    hidden_size = up_count * width
    return pl.pallas_call(
        mlp_forward_kernel,
        grid=(up_count * split,),
        out_shape=(
            jax.ShapeDtypeStruct((length, hidden_size), jnp.bfloat16),
            jax.ShapeDtypeStruct((length, hidden_size), jnp.float32),
            jax.ShapeDtypeStruct((length, width), jnp.float32),
        ),
        in_specs=[resident, up, bias, down],
        out_specs=(hidden, hidden, resident),
        compiler_params=pltpu.CompilerParams(vmem_limit_bytes=48 << 20),
        name="mlp_forward",
    )(rows, blocks, up_bias.reshape(1, hidden_size), blocks)


def mlp_backward(rows, grad_branch, blocks, units, slopes):
    length, width = rows.shape
    up_count = blocks.shape[0] // 2
    split, resident, up, down, hidden, bias = mlp_specs(length, width, up_count)
    hidden_size = up_count * width
    return pl.pallas_call(
        mlp_backward_kernel,
        grid=(up_count * split,),
        out_shape=(
            jax.ShapeDtypeStruct((up_count, width, width), jnp.float32),
            jax.ShapeDtypeStruct((up_count, width, width), jnp.float32),
            jax.ShapeDtypeStruct((1, hidden_size), jnp.float32),
            jax.ShapeDtypeStruct((length, width), jnp.float32),
        ),
        in_specs=[resident, resident, up, down, hidden, hidden],
        out_specs=(
            pl.BlockSpec((None, width, HIDDEN_TILE), lambda t: (t // split, 0, t % split)),
            pl.BlockSpec((None, HIDDEN_TILE, width), lambda t: (t // split, t % split, 0)),
            bias,
            resident,
        ),
        scratch_shapes=[pltpu.VMEM((length, HIDDEN_TILE), jnp.bfloat16)],
        compiler_params=pltpu.CompilerParams(vmem_limit_bytes=48 << 20),
        name="mlp_backward",
    )(rows, grad_branch, blocks, blocks, units, slopes)


def layer_forward(blocks, vec_all, patch, attend):
    embedded = jnp.dot(patch, blocks[0], preferred_element_type=jnp.float32) + vec_all[0]
    normed_one = norm_rows(embedded, vec_all[1], vec_all[2]).astype(jnp.bfloat16)
    qkv_rows = jnp.einsum(
        "td,kde->kte", normed_one, blocks[1:4], preferred_element_type=jnp.float32
    )
    qkv_bias = jnp.stack([vec_all[3], jnp.zeros_like(vec_all[3]), vec_all[4]])
    qkv_rows = (qkv_rows + qkv_bias[:, None, :]).astype(jnp.bfloat16)
    attended, mlp_blocks = attend(qkv_rows)
    up_count = mlp_blocks.shape[0] // 2
    hidden = (
        embedded + jnp.dot(attended, blocks[4], preferred_element_type=jnp.float32) + vec_all[5]
    )
    normed_two = norm_rows(hidden, vec_all[6], vec_all[7]).astype(jnp.bfloat16)
    units, slopes, branch = mlp_forward(normed_two, mlp_blocks, vec_all[8 : 8 + up_count])
    output = hidden + branch + vec_all[8 + up_count]
    return (
        output,
        mlp_blocks,
        (embedded, normed_one, qkv_rows, attended, hidden, normed_two, slopes, units),
    )


def layer_backward(
    blocks,
    mlp_blocks,
    vec_all,
    patch,
    saved,
    pack_ids,
    key_codes,
    grad_output,
    grad_gain,
    grad_shift,
    released,
):
    embedded, normed_one, qkv_rows, attended, hidden, normed_two, slopes, units = saved
    feature_dim = patch.shape[1]
    up_count = mlp_blocks.shape[0] // 2
    grad_branch = grad_output.astype(jnp.bfloat16)
    grad_up, grad_down, up_sums, grad_normed_two = mlp_backward(
        normed_two, grad_branch, mlp_blocks, units, slopes
    )
    up_sums, released = lax.optimization_barrier((up_sums, released))
    norm_two_back = jax.vjp(norm_rows, hidden, vec_all[6], vec_all[7])[1]
    grad_hidden_norm, grad_gain_two, grad_shift_two = norm_two_back(grad_normed_two)
    grad_hidden = grad_output + grad_hidden_norm
    grad_attn_out = grad_hidden.astype(jnp.bfloat16)
    grad_attended = jnp.einsum(
        "td,ed->te", grad_attn_out, blocks[4], preferred_element_type=jnp.float32
    ).astype(jnp.bfloat16)
    grad_qkv = attention_backward(qkv_rows, pack_ids, key_codes, grad_attended)
    grad_normed_one = jnp.einsum(
        "kte,kde->td", grad_qkv, blocks[1:4], preferred_element_type=jnp.float32
    )
    norm_one_back = jax.vjp(norm_rows, embedded, vec_all[1], vec_all[2])[1]
    grad_embed_norm, grad_gain_one, grad_shift_one = norm_one_back(grad_normed_one)
    grad_embedded = (grad_hidden + grad_embed_norm).astype(jnp.bfloat16)
    lefts = (patch, normed_one, attended)
    rights = (grad_embedded, grad_qkv, grad_attn_out)
    bias_sums = jnp.stack(
        [
            jnp.sum(grad_embedded.astype(jnp.float32), 0),
            grad_gain_one,
            grad_shift_one,
            jnp.sum(grad_qkv[0].astype(jnp.float32), 0),
            jnp.sum(grad_qkv[2].astype(jnp.float32), 0),
            jnp.sum(grad_attn_out.astype(jnp.float32), 0),
            grad_gain_two,
            grad_shift_two,
        ]
    )
    up_sums = up_sums.reshape(up_count, feature_dim)
    tail_sums = jnp.stack([jnp.sum(grad_branch.astype(jnp.float32), 0), grad_gain, grad_shift])
    grad_vectors = jnp.concatenate([bias_sums, up_sums, tail_sums], 0)
    return (lefts, rights, (grad_up, grad_down), grad_vectors, released)


def torus_place():
    dp, cls = lax.axis_index("dp"), lax.axis_index("cls")
    return dp // 2, dp % 2, cls // 2, cls % 2


def torus_device(z, y, x, core):
    return (z * 2 + y, x * 2 + core)


def encode(pieces, code_refs, scale_ref):
    top = None
    for piece in pieces:
        peak = jnp.max(jnp.abs(piece()), 0, keepdims=True)
        top = peak if top is None else jnp.maximum(top, peak)
    top = jnp.maximum(top, CODE_FLOOR)
    inverse = CODE_TOP / top
    for piece, code_ref in zip(pieces, code_refs):
        code_ref[...] = jnp.round(piece() * inverse).astype(jnp.int32).astype(jnp.int16)
    scale_ref[...] = top * (1.0 / CODE_TOP)


def decode(code, scale):
    return code.astype(jnp.int32).astype(jnp.float32) * scale


def reduce_kernel(counts, *refs):
    sources, refs = refs[: len(counts)], refs[len(counts) :]
    (patch_hbm, first_hbm, mid_hbm, dpatch_hbm, dfirst_hbm, dmid_hbm,
     vec_ref, tail_ref, left_hbm, right_hbm,
     own_hbm, left_out_hbm, right_out_hbm, step_hbm, wide_ref, facts_ref, vec_out_ref,
     left_buf, right_buf, right_full, outs_buf, squares, high_buf, low_buf, sum_slots, tail_slots,
     lhs_buf, rhs_buf, pair_sem,
     in_sem, sum_send, sum_recv, tail_send, tail_recv,
     acc, spare, kept, sent0, got0, sent1, got1, sent2, got2, sent3, got3, sent4, got4,
     ss0, gs0, ss1, gs1, ss2, gs2, ss3, gs3, ss4, gs4, codes, scales, vec_got,
     load_sem, out_sem, send_sem, recv_sem, send_scale_sem, recv_scale_sem,
     vec_send_sem, vec_recv_sem) = refs
    stored = sum(counts)
    paired = dfirst_hbm.shape[0] + 2
    total = stored + paired
    half, width = codes.shape[1], codes.shape[2]
    cols = width // 2
    z, y, x, core = torus_place()
    upper = z // 2
    inner = (z % 2) != upper
    mate_core = torus_device(z, y, x, 1 - core)
    mate_x = torus_device(z, y, 1 - x, core)
    mate_y = torus_device(z, 1 - y, x, core)
    mate_z = torus_device(z + 1 - 2 * (z % 2), y, x, core)
    mate_mid = torus_device(3 - z, y, x, core)
    mate_far = torus_device((z + 2) % 4, y, x, core)

    barrier = pltpu.get_barrier_semaphore()
    dp, cls = lax.axis_index("dp"), lax.axis_index("cls")
    everyone = tail_slots.shape[0]
    quarter = sum_slots.shape[0]
    me = dp * 4 + cls

    def any_mate(n):
        other = lax.rem(me + n, everyone)
        return (other // 4, lax.rem(other, 4))

    def half_mate(n):
        return (upper * quarter + lax.rem(dp + n, quarter), cls)

    for n in range(1, everyone):
        pl.semaphore_signal(barrier, inc=1, device_id=any_mate(n), device_id_type=MESH)
    pl.semaphore_wait(barrier, everyone - 1)
    own = lax.rem(dp, quarter) * left_buf.shape[1]

    own_cols = pl.ds(pl.multiple_of(core * cols, 128), cols)
    other_cols = pl.ds(pl.multiple_of((1 - core) * cols, 128), cols)

    def rows_at(start, size):
        return pl.ds(pl.multiple_of(start, PIECE), size)

    def loads(m, body):
        start = 0
        for source, count in zip(sources, counts):
            def one(source=source, start=start):
                pair = (
                    pltpu.make_async_copy(
                        source.at[m - start, :, own_cols], acc.at[m % 5], load_sem.at[m % 2, 0]
                    ),
                    pltpu.make_async_copy(
                        source.at[m - start, :, other_cols], spare.at[m % 2], load_sem.at[m % 2, 1]
                    ),
                )
                for copy in pair:
                    body(copy)

            pl.when((m >= start) & (m < start + count))(one)
            start += count

    def block_of(m):
        return lax.rem(m + paired, total)

    def pair_loads(m, body):
        index = m - stored
        last = paired - 1

        def run(left, right):
            body(pltpu.make_async_copy(left, lhs_buf.at[m % 2], pair_sem.at[m % 2, 0]))
            body(pltpu.make_async_copy(right, rhs_buf.at[m % 2], pair_sem.at[m % 2, 1]))

        pl.when(index == 0)(lambda: run(patch_hbm, dpatch_hbm))
        pl.when((index > 0) & (index < last))(
            lambda: run(first_hbm, dfirst_hbm.at[jnp.clip(index - 1, 0, last - 2)])
        )
        pl.when(index == last)(lambda: run(mid_hbm, dmid_hbm))

    def pair_product(m):
        chunk = 2 * FEATURE_TILE
        for r in range(0, width, chunk):
            left = lhs_buf[m % 2, :, r : r + chunk].T
            for target, columns in ((acc.at[m % 5], own_cols), (spare.at[m % 2], other_cols)):
                target[r : r + chunk, :] = jnp.dot(
                    left, rhs_buf[m % 2, :, columns], preferred_element_type=jnp.float32
                )

    def message(stage, m, source, scale_source, target, scale_target, mate):
        return (
            pltpu.make_async_remote_copy(
                src_ref=source, dst_ref=target,
                send_sem=send_sem.at[stage, m % 2], recv_sem=recv_sem.at[stage, m],
                device_id=mate, device_id_type=MESH,
            ),
            pltpu.make_async_remote_copy(
                src_ref=scale_source, dst_ref=scale_target,
                send_sem=send_scale_sem.at[stage, m % 2], recv_sem=recv_scale_sem.at[stage, m],
                device_id=mate, device_id_type=MESH,
            ),
        )

    def first(m):
        return message(0, m, sent0.at[m % 2], ss0.at[m % 2], got0.at[m], gs0.at[m], mate_core)

    def second(m, b):
        return message(
            1 + b, m, sent1.at[m % 2, b], ss1.at[m % 2, b], got1.at[m, b], gs1.at[m, b],
            mate_y if b else mate_x,
        )

    def third(m, b):
        return message(
            3 + b, m, sent2.at[m % 2, b], ss2.at[m % 2, b], got2.at[m, b], gs2.at[m, b],
            mate_x if b else mate_y,
        )

    def fourth(m):
        return message(5, m, sent3.at[m % 2], ss3.at[m % 2], got3.at[m], gs3.at[m], mate_z)

    def fifth(m):
        return message(6, m, sent4.at[m % 2], ss4.at[m % 2], got4.at[m], gs4.at[m], mate_mid)

    piece_a = 2 * x + y
    piece_b = 4 + 2 * y + x

    def spread(stage, m, piece, count, mate, columns=own_cols):
        rows = pl.ds(pl.multiple_of(piece * PIECE, PIECE), count * PIECE)
        block = codes.at[m, rows, columns]
        scale = scales.at[m, pl.ds(piece, count), :, columns]
        return message(stage, m, block, scale, block, scale, mate)

    def start(copies):
        for copy in copies:
            copy.start()

    def wait_send(copies):
        for copy in copies:
            copy.wait_send()

    def wait_recv(copies):
        for copy in copies:
            copy.wait_recv()

    def vec_copy(step, mate):
        return pltpu.make_async_remote_copy(
            src_ref=vec_got.at[step, 0], dst_ref=vec_got.at[step, 1],
            send_sem=vec_send_sem.at[step], recv_sem=vec_recv_sem.at[step],
            device_id=mate, device_id_type=MESH,
        )

    vec_mates = (mate_core, mate_x, mate_y, mate_z, mate_far)

    loads(jnp.int32(0), lambda copy: copy.start())
    vec_got[0, 0] = vec_ref[...]
    vec_copy(0, vec_mates[0]).start()

    def step(t, carry):
        for n in range(1, 6):
            @pl.when(t == n)
            def _(n=n):
                vec_copy(n - 1, vec_mates[n - 1]).wait()
                value = vec_got[n - 1, 0] + vec_got[n - 1, 1]
                if n < 5:
                    vec_got[n, 0] = value
                    vec_copy(n, vec_mates[n]).start()
                else:
                    vec_out_ref[...] = value

        @pl.when(t < total)
        def _():
            m = t

            @pl.when(m < stored)
            def _():
                loads(m, lambda copy: copy.wait())

            @pl.when(m + 1 < stored)
            def _():
                loads(m + 1, lambda copy: copy.start())

            @pl.when((m + 1 >= stored) & (m + 1 < total))
            def _():
                pair_loads(m + 1, lambda copy: copy.start())

            @pl.when(m >= stored)
            def _():
                pair_loads(m, lambda copy: copy.wait())
                pair_product(m)

            span = 2 * PIECE
            encode(
                [lambda r=r: spare[m % 2, r : r + span, :] for r in range(0, 2 * half, span)],
                [sent0.at[m % 2, r : r + span, :] for r in range(0, 2 * half, span)],
                ss0.at[m % 2],
            )
            start(first(m))

        @pl.when((t >= 1) & (t < total + 1))
        def _():
            m = t - 1
            copies = first(m)
            wait_send(copies)
            wait_recv(copies)
            slot = m % 5
            span = 2 * PIECE
            for r in range(0, 2 * half, span):
                acc[slot, r : r + span, :] += decode(got0[m, r : r + span, :], gs0[m])
            for b in range(2):
                other = (1 - y) if b else (1 - x)
                begins = [h * half + b * 4 * PIECE + other * span for h in range(2)]
                encode(
                    [lambda s=s: acc[slot, rows_at(s, span), :] for s in begins],
                    [sent1.at[m % 2, b, h] for h in range(2)],
                    ss1.at[m % 2, b],
                )
                start(second(m, b))

        @pl.when((t >= 2) & (t < total + 2))
        def _():
            m = t - 2
            slot = m % 5
            span = 2 * PIECE
            for b in range(2):
                copies = second(m, b)
                wait_send(copies)
                wait_recv(copies)
                mine = y if b else x
                other = (1 - x) if b else (1 - y)
                begins = [h * half + b * 4 * PIECE + mine * span for h in range(2)]
                for h, s in enumerate(begins):
                    acc[slot, rows_at(s, span), :] += decode(got1[m, b, h], gs1[m, b])
                encode(
                    [lambda s=s: acc[slot, rows_at(s + other * PIECE, PIECE), :] for s in begins],
                    [sent2.at[m % 2, b, h] for h in range(2)],
                    ss2.at[m % 2, b],
                )
                start(third(m, b))

        @pl.when((t >= 3) & (t < total + 3))
        def _():
            m = t - 3
            slot = m % 5
            for b in range(2):
                copies = third(m, b)
                wait_send(copies)
                wait_recv(copies)
                place = piece_b if b else piece_a
                for h in range(2):
                    kept[m % 3, h, b] = acc[
                        slot, rows_at(h * half + place * PIECE, PIECE), :
                    ] + decode(got2[m, b, h], gs2[m, b])

            @pl.when(jnp.logical_not(inner))
            def _():
                pairs = [(h, b) for h in range(2) for b in range(2)]
                encode(
                    [lambda h=h, b=b: kept[m % 3, h, b] for h, b in pairs],
                    [sent3.at[m % 2, h, b] for h, b in pairs],
                    ss3.at[m % 2],
                )
                start(fourth(m))

        @pl.when((t >= 4) & (t < total + 4))
        def _():
            m = t - 4
            copies = fourth(m)

            @pl.when(jnp.logical_not(inner))
            def _():
                wait_send(copies)

            @pl.when(inner)
            def _():
                wait_recv(copies)
                for h in range(2):
                    for b in range(2):
                        kept[m % 3, h, b] += decode(got3[m, h, b], gs3[m])
                encode(
                    [lambda b=b: kept[m % 3, 1 - upper, b] for b in range(2)],
                    [sent4.at[m % 2, b] for b in range(2)],
                    ss4.at[m % 2],
                )
                start(fifth(m))

        @pl.when((t >= 5) & (t < total + 5))
        def _():
            m = t - 5

            @pl.when(inner)
            def _():
                copies = fifth(m)
                wait_send(copies)
                wait_recv(copies)
                for b in range(2):
                    place = piece_b if b else piece_a
                    value = kept[m % 3, upper, b] + decode(got4[m, b], gs4[m])
                    encode(
                        [lambda value=value: value],
                        [codes.at[m, rows_at(place * PIECE, PIECE), own_cols]],
                        scales.at[m, place, :, own_cols],
                    )
                    start(spread(7 + b, m, place, 1, mate_z))

        @pl.when((t >= 6) & (t < total + 6))
        def _():
            m = t - 6
            for b in range(2):
                place = piece_b if b else piece_a
                copies = spread(7 + b, m, place, 1, mate_z)

                @pl.when(inner)
                def _(copies=copies):
                    wait_send(copies)

                @pl.when(jnp.logical_not(inner))
                def _(copies=copies):
                    wait_recv(copies)

                start(spread(9 + b, m, place, 1, mate_x if b else mate_y))

        @pl.when((t >= 7) & (t < total + 7))
        def _():
            m = t - 7
            for b in range(2):
                place = piece_b if b else piece_a
                theirs = (4 + 2 * y + 1 - x) if b else (2 * x + 1 - y)
                wait_send(spread(9 + b, m, place, 1, mate_x if b else mate_y))
                wait_recv(spread(9 + b, m, theirs, 1, mate_x if b else mate_y))
                begin = (4 + 2 * y) if b else 2 * x
                start(spread(11 + b, m, begin, 2, mate_y if b else mate_x))

        @pl.when((t >= 8) & (t < total + 8))
        def _():
            m = t - 8
            for b in range(2):
                begin = (4 + 2 * y) if b else 2 * x
                theirs = (4 + 2 * (1 - y)) if b else 2 * (1 - x)
                wait_send(spread(11 + b, m, begin, 2, mate_y if b else mate_x))
                wait_recv(spread(11 + b, m, theirs, 2, mate_y if b else mate_x))
            start(spread(13, m, 0, 8, mate_core))

        def ins(m):
            return (
                pltpu.make_async_copy(
                    left_hbm.at[block_of(m)], left_buf.at[m % 2], in_sem.at[m % 2, 0]
                ),
                pltpu.make_async_copy(
                    right_hbm.at[:, block_of(m)], right_buf.at[m % 2], in_sem.at[m % 2, 1]
                ),
            )

        def outs(m):
            targets = (own_hbm, left_out_hbm, right_out_hbm, step_hbm)
            return [
                pltpu.make_async_copy(
                    outs_buf.at[m % 2, n], target.at[block_of(m)], out_sem.at[m % 2, n]
                )
                for n, target in enumerate(targets)
            ]

        @pl.when((t >= 8) & (t < total + 8))
        def _():
            start(ins(t - 8))

        @pl.when((t >= 11) & (t < total + 11))
        def _():
            for copy in outs(t - 11):
                copy.wait()

        @pl.when((t >= 9) & (t < total + 9))
        def _():
            m = t - 9
            wait_send(spread(13, m, 0, 8, mate_core))
            wait_recv(spread(13, m, 0, 8, mate_core, other_cols))
            for copy in ins(m):
                copy.wait()
            precondition_block(
                own, codes.at[m], scales.at[m], left_buf.at[m % 2], right_buf.at[m % 2],
                outs_buf.at[m % 2], squares.at[m], high_buf, low_buf, right_full,
            )
            start(outs(m))

        return carry

    lax.fori_loop(0, total + 11, step, 0)

    def folded(row):
        return sum(row[:, n * 128 : (n + 1) * 128] for n in range(row.shape[1] // 128))

    layer = jnp.zeros((1, 128), jnp.float32)
    mine = lax.rem(dp, quarter)
    sum_slots[mine] = jnp.zeros(sum_slots.shape[1:], jnp.float32)
    for m in range(total):
        layer = layer + folded(squares[m, 0:1, :])
        for quad in range(2):
            part = squares[m, 1:2, quad * cols : (quad + 1) * cols]
            row = 2 * ((m + paired) % total) + quad
            sum_slots[mine, row : row + 1, :] = folded(part)
    once = (cls == 0).astype(jnp.float32)
    first_row = lax.broadcasted_iota(jnp.int32, tail_ref.shape, 0) == 0
    tail_slots[me] = tail_ref[...] + jnp.where(first_row, once * layer, 0.0)

    def sum_copy(n, slot):
        return pltpu.make_async_remote_copy(
            src_ref=sum_slots.at[slot], dst_ref=sum_slots.at[slot],
            send_sem=sum_send.at[n], recv_sem=sum_recv.at[slot],
            device_id=half_mate(n), device_id_type=MESH,
        )

    def tail_copy(n, slot):
        return pltpu.make_async_remote_copy(
            src_ref=tail_slots.at[slot], dst_ref=tail_slots.at[slot],
            send_sem=tail_send.at[n], recv_sem=tail_recv.at[slot],
            device_id=any_mate(n), device_id_type=MESH,
        )

    for n in range(1, quarter):
        sum_copy(n, lax.rem(dp, quarter)).start()
    for n in range(1, everyone):
        tail_copy(n, me).start()
    for n in range(1, quarter):
        sum_copy(n, lax.rem(dp, quarter)).wait_send()
        sum_copy(n, lax.rem(dp + n, quarter)).wait_recv()
    for n in range(1, everyone):
        tail_copy(n, me).wait_send()
        tail_copy(n, lax.rem(me + n, everyone)).wait_recv()
    value = sum_slots[0]
    for n in range(1, quarter):
        value = value + sum_slots[n]
    tail = tail_slots[0]
    for n in range(1, everyone):
        tail = tail + tail_slots[n]
    vec = vec_out_ref[...]
    vec_squares = jnp.sum(jnp.sum(vec * vec, 0, keepdims=True), 1, keepdims=True)
    norm = jnp.sqrt(jnp.sum(tail[0:1], 1, keepdims=True) + vec_squares)
    factor = CLIP_NORM / jnp.maximum(norm, CLIP_NORM)
    mean_squares = jnp.sum(value, 1, keepdims=True) / (half * cols) * factor * factor
    scale = SHAMPOO_RATE * factor * lax.rsqrt(mean_squares + ROOT_EPS)
    for b in range(total):
        for quad in range(2):
            row = 2 * b + quad
            wide_ref[b, :, quad * cols : (quad + 1) * cols] = jnp.broadcast_to(
                scale[row : row + 1], (1, cols)
            )
    rows = lax.broadcasted_iota(jnp.int32, facts_ref.shape, 0)
    loss = jnp.sum(tail[1:2], 1, keepdims=True)
    facts_ref[...] = jnp.where(rows == 0, loss, jnp.where(rows == 1, norm, factor))


def reduce_gradients(
    arrays, lefts, rights, vec_sums, tail, root_left, right_codes, dp_count, cls_count
):
    counts = tuple(array.shape[0] for array in arrays)
    total, rows, width = root_left.shape
    length = lefts[0].shape[0]
    parts, coded_rows = right_codes.shape[0], right_codes.shape[2]
    half, cols = width // 2, width // 2
    sum_rows = 2 * total + -2 * total % 8
    f32, i16 = jnp.float32, jnp.int16

    def pair(*shape):
        return [pltpu.VMEM((2,) + shape, i16), pltpu.VMEM((total,) + shape, i16)]

    def scale_pair(*shape):
        return [
            pltpu.VMEM((2,) + shape + (1, cols), f32),
            pltpu.VMEM((total,) + shape + (1, cols), f32),
        ]

    hbm = pl.BlockSpec(memory_space=pl.ANY)
    vmem = pl.BlockSpec(memory_space=pltpu.VMEM)
    return pl.pallas_call(
        functools.partial(reduce_kernel, counts),
        out_shape=(jax.ShapeDtypeStruct((total, rows, width), f32),) * 4
        + (
            jax.ShapeDtypeStruct((total, 1, width), f32),
            jax.ShapeDtypeStruct(tail.shape, f32),
            jax.ShapeDtypeStruct(vec_sums.shape, f32),
        ),
        in_specs=[hbm] * (len(arrays) + 6) + [vmem, vmem, hbm, hbm],
        out_specs=(hbm,) * 4 + (vmem,) * 3,
        scratch_shapes=[
            pltpu.VMEM((2, rows, width), f32),
            pltpu.VMEM((2, parts, coded_rows, width), jnp.int32),
            pltpu.VMEM((half, width), f32),
            pltpu.VMEM((2, 4, rows, width), f32),
            pltpu.VMEM((total, 2, width), f32),
            pltpu.VMEM((half, width), jnp.bfloat16),
            pltpu.VMEM((half, width), jnp.bfloat16),
            pltpu.VMEM((dp_count // 2, sum_rows, 128), f32),
            pltpu.VMEM((dp_count * cls_count,) + tail.shape, f32),
            pltpu.VMEM((2, length, width), jnp.bfloat16),
            pltpu.VMEM((2, length, width), jnp.bfloat16),
            pltpu.SemaphoreType.DMA((2, 2)),
            pltpu.SemaphoreType.DMA((2, 2)),
            pltpu.SemaphoreType.DMA((dp_count // 2,)),
            pltpu.SemaphoreType.DMA((dp_count // 2,)),
            pltpu.SemaphoreType.DMA((dp_count * cls_count,)),
            pltpu.SemaphoreType.DMA((dp_count * cls_count,)),
            pltpu.VMEM((5, width, cols), f32),
            pltpu.VMEM((2, width, cols), f32),
            pltpu.VMEM((3, 2, 2, PIECE, cols), f32),
        ]
        + pair(width, cols)
        + pair(2, 2, 2 * PIECE, cols)
        + pair(2, 2, PIECE, cols)
        + pair(2, 2, PIECE, cols)
        + pair(2, PIECE, cols)
        + scale_pair()
        + scale_pair(2)
        + scale_pair(2)
        + scale_pair()
        + scale_pair()
        + [
            pltpu.VMEM((total, half, width), i16),
            pltpu.VMEM((total, half // PIECE, 1, width), f32),
            pltpu.VMEM((5, 2) + vec_sums.shape, f32),
            pltpu.SemaphoreType.DMA((2, 2)),
            pltpu.SemaphoreType.DMA((2, 4)),
            pltpu.SemaphoreType.DMA((14, 2)),
            pltpu.SemaphoreType.DMA((14, total)),
            pltpu.SemaphoreType.DMA((14, 2)),
            pltpu.SemaphoreType.DMA((14, total)),
            pltpu.SemaphoreType.DMA((5,)),
            pltpu.SemaphoreType.DMA((5,)),
        ],
        compiler_params=pltpu.CompilerParams(
            collective_id=1, has_side_effects=True, vmem_limit_bytes=60 << 20
        ),
        name="reduce_gradients",
    )(*arrays, *lefts, *rights, vec_sums, tail, root_left, right_codes)


def split_float(values):
    high = values.astype(jnp.bfloat16)
    return high, (values - high.astype(jnp.float32)).astype(jnp.bfloat16)


def stacked_dot(lefts, right, contract_last):
    rows = lefts[0].shape[0]
    left = jnp.concatenate(lefts, 0) if len(lefts) > 1 else lefts[0]
    dims = (((1,), (1 if contract_last else 0,)), ((), ()))
    out = lax.dot_general(left, right, dims, preferred_element_type=jnp.float32)
    return [out[n * rows : (n + 1) * rows] for n in range(len(lefts))]


def encode_roots(part):
    top = jnp.max(jnp.abs(part), 1, keepdims=True)
    level = jnp.ceil(jnp.log2(jnp.maximum(top, 1e-30)))
    codes = jnp.round(part * jnp.exp2(15.0 - level))
    codes = jnp.clip(codes, -32767.0, 32767.0).astype(jnp.int32)
    levels = jnp.broadcast_to(level.astype(jnp.int32), (part.shape[0], 8, part.shape[2]))
    upper = jnp.concatenate([codes[:, 0:8], codes[:, 16:24]], 1)
    lower = jnp.concatenate([codes[:, 8:16], levels], 1)
    return upper * 65536 + (lower + 32768)


def precondition_block(
    own, codes_ref, scales_ref, left_ref, right_codes, outs_ref, squares_ref, high_ref, low_ref,
    right_ref
):
    half, width = codes_ref.shape
    rows = left_ref.shape[0]
    own_rows = pl.ds(pl.multiple_of(own, PIECE), rows)
    parts = right_codes.shape[0]
    size = half // parts
    for n in range(parts):
        packed = right_codes[n]
        upper = lax.shift_right_arithmetic(packed, jnp.full_like(packed, 16)).astype(jnp.float32)
        lower = ((packed & 65535) - 32768).astype(jnp.float32)
        scale = jnp.exp2(lower[8:9] - 15.0)
        right_ref[n * size : n * size + 8, :] = upper[0:8] * scale
        right_ref[n * size + 8 : n * size + 16, :] = lower[0:8] * scale
        right_ref[n * size + 16 : n * size + 24, :] = upper[8:16] * scale
    for piece in range(half // PIECE):
        part = slice(piece * PIECE, (piece + 1) * PIECE)
        high_ref[part, :], low_ref[part, :] = split_float(
            decode(codes_ref[part, :], scales_ref[piece])
        )
    own_value = high_ref[own_rows, :].astype(jnp.float32) + low_ref[own_rows, :].astype(jnp.float32)
    outs_ref[0] = own_value
    squares_ref[0:1, :] = jnp.sum(own_value * own_value, 0, keepdims=True)
    picks = (
        lax.broadcasted_iota(jnp.int32, (rows, half), 1)
        == lax.broadcasted_iota(jnp.int32, (rows, half), 0) + own
    ).astype(jnp.float32).astype(jnp.bfloat16)
    for quad in range(2):
        cols = slice(quad * half, (quad + 1) * half)
        high, low = high_ref[:, cols], low_ref[:, cols]
        mine_high, mine_low = high_ref[own_rows, cols], low_ref[own_rows, cols]
        hh, lh, turned_high = stacked_dot([mine_high, mine_low, picks], high, True)
        hl, turned_low = stacked_dot([mine_high, picks], low, True)
        outs_ref[1, :, cols] = hh + (lh + hl)
        turned_high = turned_high.astype(jnp.bfloat16)
        turned_low = turned_low.astype(jnp.bfloat16)
        root_high, root_low = split_float(left_ref[:, cols])
        thh, tlh, rhh, rlh = stacked_dot([turned_high, turned_low, root_high, root_low], high, False)
        thl, rhl = stacked_dot([turned_high, root_high], low, False)
        outs_ref[2, :, cols] = thh + (tlh + thl)
        half_step = rhh + (rlh + rhl)
        step_high, step_low = split_float(half_step)
        right_high, right_low = split_float(right_ref[:, cols])
        shh, slh = stacked_dot([step_high, step_low], right_high, False)
        (shl,) = stacked_dot([step_high], right_low, False)
        direction = shh + (slh + shl)
        outs_ref[3, :, cols] = direction
        squares_ref[1:2, cols] = jnp.sum(direction * direction, 0, keepdims=True)


def head_kernel(
    image_total, pooled_ref, labels_ref, head_hbm,
    grad_ref, rows_ref, loss_ref,
    head_buf, group_buf, total_buf, slots, load_sem, send_sem, recv_sem, sum_send, sum_recv
):
    dp, cls = lax.axis_index("dp"), lax.axis_index("cls")
    count, rows, width = slots.shape
    images = count * rows
    classes = head_buf.shape[1]
    load = pltpu.make_async_copy(head_hbm, head_buf, load_sem)
    load.start()
    barrier = pltpu.get_barrier_semaphore()
    for n in range(1, count):
        pl.semaphore_signal(
            barrier, inc=1, device_id=(dp, lax.rem(cls + n, count)), device_id_type=MESH
        )
    pl.semaphore_wait(barrier, count - 1)

    def part(ref, index):
        return ref.at[pl.ds(pl.multiple_of(index * rows, 8), rows)]

    def share(n, slot):
        return pltpu.make_async_remote_copy(
            src_ref=pooled_ref, dst_ref=part(group_buf, slot),
            send_sem=send_sem.at[n], recv_sem=recv_sem.at[slot],
            device_id=(dp, lax.rem(cls + n, count)), device_id_type=MESH,
        )

    for n in range(1, count):
        share(n, cls).start()
    part(group_buf, cls)[...] = pooled_ref[...]
    rows_ref[:, width + classes :] = jnp.zeros(
        (images, rows_ref.shape[1] - width - classes), rows_ref.dtype
    )
    for n in range(1, count):
        share(n, cls).wait_send()
        share(n, lax.rem(cls + n, count)).wait_recv()
    load.wait()
    group = group_buf[...].astype(jnp.bfloat16)
    rows_ref[:, :width] = group
    loss = jnp.zeros((1, 1), jnp.float32)
    total = jnp.zeros((images, width), jnp.float32)
    for start in range(0, classes, CLASS_TILE):
        stop = min(classes, start + CLASS_TILE)
        weights = head_buf[:, start:stop]
        logits = jnp.dot(group, weights, preferred_element_type=jnp.float32)
        ids = lax.broadcasted_iota(jnp.int32, logits.shape, 1) + (cls * classes + start)
        target = ids == labels_ref[:, 0:1]
        for n in range(1, labels_ref.shape[1]):
            target = target | (ids == labels_ref[:, n : n + 1])
        target = target.astype(jnp.float32)
        valid = ids < LABELS_REAL
        shrunk = jnp.exp(-jnp.abs(logits))
        terms = jnp.maximum(logits, 0.0) + jnp.log1p(shrunk) - target * logits
        terms = jnp.where(valid, terms, 0.0)
        loss = loss + jnp.sum(jnp.sum(terms, 0, keepdims=True), 1, keepdims=True)
        chance = jnp.where(logits >= 0.0, 1.0, shrunk) / (1.0 + shrunk)
        grads = jnp.where(valid, chance - target, 0.0) / image_total
        grads = grads.astype(jnp.bfloat16)
        rows_ref[:, width + start : width + stop] = grads
        total = total + lax.dot_general(
            grads, weights, (((1,), (1,)), ((), ())), preferred_element_type=jnp.float32
        )
    loss_ref[...] = jnp.broadcast_to(loss / image_total, loss_ref.shape)
    total_buf[...] = total

    def back(n, slot):
        mate = lax.rem(cls + n, count)
        return pltpu.make_async_remote_copy(
            src_ref=part(total_buf, mate), dst_ref=slots.at[slot],
            send_sem=sum_send.at[n], recv_sem=sum_recv.at[slot],
            device_id=(dp, mate), device_id_type=MESH,
        )

    for n in range(1, count):
        back(n, cls).start()
    slots[cls] = part(total_buf, cls)[...]
    for n in range(1, count):
        back(n, cls).wait_send()
        back(n, lax.rem(cls + n, count)).wait_recv()
    value = slots[0]
    for n in range(1, count):
        value = value + slots[n]
    grad_ref[...] = value


def classify(pooled, labels, head_low, cls_count, image_total):
    rows, width = pooled.shape
    images, classes = rows * cls_count, head_low.shape[1]
    wide = width + classes
    wide = wide + -wide % 128
    f32 = jnp.float32
    vmem = pl.BlockSpec(memory_space=pltpu.VMEM)
    return pl.pallas_call(
        functools.partial(head_kernel, image_total),
        out_shape=(
            jax.ShapeDtypeStruct((rows, width), f32),
            jax.ShapeDtypeStruct((images, wide), jnp.bfloat16),
            jax.ShapeDtypeStruct((8, 128), f32),
        ),
        in_specs=[vmem, vmem, pl.BlockSpec(memory_space=pltpu.HBM)],
        out_specs=(vmem, vmem, vmem),
        scratch_shapes=[
            pltpu.VMEM((width, classes), jnp.bfloat16),
            pltpu.VMEM((images, width), f32),
            pltpu.VMEM((images, width), f32),
            pltpu.VMEM((cls_count, rows, width), f32),
            pltpu.SemaphoreType.DMA,
        ]
        + [pltpu.SemaphoreType.DMA((cls_count,)) for _ in range(4)],
        compiler_params=pltpu.CompilerParams(
            collective_id=2, has_side_effects=True, vmem_limit_bytes=60 << 20
        ),
        name="classify",
    )(pooled, labels, head_low)


def gather_steps(own_ref, out_ref, send_sem, recv_sem, copy_sem):
    count, rows, width = own_ref.shape
    cols = width // 2
    z, y, x, core = torus_place()
    mate_core = torus_device(z, y, x, 1 - core)
    mate_x = torus_device(z, y, 1 - x, core)
    mate_y = torus_device(z, 1 - y, x, core)
    own_cols = pl.ds(pl.multiple_of(core * cols, 128), cols)
    other_cols = pl.ds(pl.multiple_of((1 - core) * cols, 128), cols)
    spare = rows - SPAN
    held = x * spare
    lone = (x * SPAN, (1 - x) * SPAN)

    def share(m, zz, yy, start, size):
        begin = (zz * 2 + yy) * rows + start
        return out_ref.at[m, pl.ds(pl.multiple_of(begin, 16), size), own_cols]

    def copy(slot, arrival, m, source, target, mate):
        return pltpu.make_async_remote_copy(
            src_ref=source, dst_ref=target,
            send_sem=send_sem.at[slot, m % 2], recv_sem=recv_sem.at[arrival, m],
            device_id=mate, device_id_type=MESH,
        )

    def local(m):
        return pltpu.make_async_copy(
            own_ref.at[m, :, own_cols], share(m, z, y, 0, rows), copy_sem.at[m % 2]
        )

    def along(m, n, outgoing):
        other = lax.rem(z + n, 4)
        origin = z if outgoing else other
        source = own_ref.at[m, pl.ds(pl.multiple_of(held, 16), SPAN), own_cols]
        mate = torus_device(other, y, x, core)
        return copy(n - 1, origin, m, source, share(m, origin, y, held, SPAN), mate)

    def cross(m, n, outgoing):
        block = share(m, n, y if outgoing else 1 - y, held, SPAN)
        return copy(3 + n, 4 + n, m, block, block, mate_y)

    def patch(m, n, outgoing):
        index = lax.rem(z * 2 + y + n, SHARES)
        block = share(m, index // 2, lax.rem(index, 2), lone[0 if outgoing else 1], spare)
        return copy(6 + n, 7 + n, m, block, block, mate_x)

    def swap(m, columns):
        block = out_ref.at[m, :, columns]
        return copy(14, 15, m, block, block, mate_core)

    def finish(copies):
        for outgoing, incoming in copies:
            outgoing.wait_send()
            incoming.wait_recv()

    def step(t):
        @pl.when(t < count)
        def _():
            local(t).start()
            for n in range(1, 4):
                along(t, n, True).start()

        @pl.when((t >= 1) & (t < count + 1))
        def _():
            m = t - 1
            local(m).wait()
            finish([(along(m, n, True), along(m, n, False)) for n in range(1, 4)])
            for n in range(4):
                cross(m, n, True).start()

        @pl.when((t >= 2) & (t < count + 2))
        def _():
            m = t - 2
            finish([(cross(m, n, True), cross(m, n, False)) for n in range(4)])
            for n in range(1, SHARES):
                patch(m, n, True).start()

        @pl.when((t >= 3) & (t < count + 3))
        def _():
            m = t - 3
            finish([(patch(m, n, True), patch(m, n, False)) for n in range(1, SHARES)])
            swap(m, own_cols).start()

        @pl.when((t >= 4) & (t < count + 4))
        def _():
            m = t - 4
            swap(m, own_cols).wait_send()
            swap(m, other_cols).wait_recv()

    return step, count + GATHER_DEPTH


def column_mate(n):
    z, y, x, core = torus_place()
    other = lax.rem(z * 2 + y + n, SHARES)
    return torus_device(other // 2, lax.rem(other, 2), x, core)


def gather_barrier():
    z, y, x, core = torus_place()
    barrier = pltpu.get_barrier_semaphore()
    mates = [torus_device(z, y, x, 1 - core), torus_device(z, y, 1 - x, core)]
    for mate in mates + [column_mate(n) for n in range(1, SHARES)]:
        pl.semaphore_signal(barrier, inc=1, device_id=mate, device_id_type=MESH)
    pl.semaphore_wait(barrier, SHARES + 1)


def gather_kernel(
    own_ref, vec_ref, out_ref, vec_out_ref, send_sem, recv_sem, copy_sem, vec_send, vec_recv
):
    z, y, _, _ = torus_place()
    me = z * 2 + y
    gather_barrier()

    def vec_copy(n, slot):
        return pltpu.make_async_remote_copy(
            src_ref=vec_ref, dst_ref=vec_out_ref.at[slot],
            send_sem=vec_send.at[n], recv_sem=vec_recv.at[slot],
            device_id=column_mate(n), device_id_type=MESH,
        )

    for n in range(1, SHARES):
        vec_copy(n, me).start()
    vec_out_ref[me] = vec_ref[...]
    gather_step, turns = gather_steps(own_ref, out_ref, send_sem, recv_sem, copy_sem)

    def step(t, carry):
        gather_step(t)
        return carry

    lax.fori_loop(0, turns, step, 0)
    for n in range(1, SHARES):
        vec_copy(n, me).wait_send()
        vec_copy(n, lax.rem(me + n, SHARES)).wait_recv()


def gather_semaphores(count):
    return [
        pltpu.SemaphoreType.DMA((15, 2)),
        pltpu.SemaphoreType.DMA((16, count)),
        pltpu.SemaphoreType.DMA((2,)),
    ]


def attention_gather_kernel(
    qids_ref, kcodes_ref, q_ref, k_ref, v_ref, own_ref, out_ref, blocks_ref,
    bias_ref, send_sem, recv_sem, copy_sem
):
    pair, tiles = pl.program_id(0), q_ref.shape[0] // QTILE
    slots = pl.num_programs(0) * tiles

    @pl.when(pair == 0)
    def _():
        gather_barrier()

    gather_step, turns = gather_steps(own_ref, blocks_ref, send_sem, recv_sem, copy_sem)
    attention_bias(qids_ref, kcodes_ref, bias_ref)
    for tile in range(tiles):
        slot = pair * tiles + tile
        begin, end = slot * turns // slots, (slot + 1) * turns // slots

        @pl.when(begin < end)
        def _(begin=begin):
            gather_step(begin)

        attention_tile(tile, q_ref, k_ref, v_ref, out_ref, bias_ref)


def attention_forward_gathering(qkv_rows, pack_ids, key_codes, own):
    _, length, width = qkv_rows.shape
    count, rows, _ = own.shape
    tiles = length // QTILE
    assert count + GATHER_DEPTH <= tiles * (width // PAIR)
    return pl.pallas_call(
        attention_gather_kernel,
        grid=(width // PAIR,),
        out_shape=(
            jax.ShapeDtypeStruct((length, width), jnp.bfloat16),
            jax.ShapeDtypeStruct((count, SHARES * rows, width), own.dtype),
        ),
        in_specs=[whole_spec((length, 1)), whole_spec((1, length))]
        + [pair_spec(length, part) for part in range(3)]
        + [whole_spec(own.shape)],
        out_specs=(pair_spec(length), pl.BlockSpec(memory_space=pl.ANY)),
        scratch_shapes=[pltpu.VMEM(bias_shape(length), jnp.float32)] + gather_semaphores(count),
        compiler_params=pltpu.CompilerParams(
            collective_id=4, has_side_effects=True, vmem_limit_bytes=40 << 20
        ),
        name="attention_forward",
    )(pack_ids[:, None], key_codes[None, :], qkv_rows, qkv_rows, qkv_rows, own)


def gather_weights(own, vec):
    count, rows, width = own.shape
    hbm = pl.BlockSpec(memory_space=pl.ANY)
    vmem = pl.BlockSpec(memory_space=pltpu.VMEM)
    return pl.pallas_call(
        gather_kernel,
        out_shape=(
            jax.ShapeDtypeStruct((count, SHARES * rows, width), own.dtype),
            jax.ShapeDtypeStruct((SHARES,) + vec.shape, vec.dtype),
        ),
        in_specs=[vmem, vmem],
        out_specs=(hbm, vmem),
        scratch_shapes=gather_semaphores(count)
        + [pltpu.SemaphoreType.DMA((SHARES,)), pltpu.SemaphoreType.DMA((SHARES,))],
        compiler_params=pltpu.CompilerParams(
            collective_id=3, has_side_effects=True, vmem_limit_bytes=32 << 20
        ),
        name="gather_weights",
    )(own, vec)


def adam_step(weight, grad, first, second, count):
    first = BETA_FIRST * first + (1.0 - BETA_FIRST) * grad
    second = BETA_SECOND * second + (1.0 - BETA_SECOND) * grad * grad
    fix_first = 1.0 - jnp.power(BETA_FIRST, count)
    fix_second = 1.0 - jnp.power(BETA_SECOND, count)
    update = first / fix_first / (jnp.sqrt(second / fix_second) + ADAM_EPS) + WEIGHT_DECAY * weight
    return (weight - ADAM_RATE * update, first, second)


def split_halves(values, half_size):
    block_count, row_count, feature_dim = values.shape
    return values.reshape(block_count, row_count, 2, half_size)


def reduced_half(values, half_groups):
    part = lax.psum_scatter(values, ("dp", "cls"), scatter_dimension=1, tiled=True)
    return lax.all_gather(part, ("dp", "cls"), axis=1, tiled=True, axis_index_groups=half_groups)


def preconditioned_rows(grad_half, root_left, right_half, own_start):
    count, row_count, width = root_left.shape
    half_size = width // 2
    block_rows = lax.dynamic_slice_in_dim(grad_half, own_start, row_count, 1)
    grad_quads = split_halves(grad_half, half_size)
    rows_quads = split_halves(block_rows, half_size)
    cols_quads = lax.dynamic_slice_in_dim(grad_quads, own_start, row_count, 3)
    precise = FULL_PRECISION
    left_add = jnp.einsum("brjk,bljk->brjl", rows_quads, grad_quads, precision=precise)
    right_add = jnp.einsum("bkja,bkjm->bajm", cols_quads, grad_quads, precision=precise)
    direction = jnp.einsum(
        "brjk,bkjm->brjm", split_halves(root_left, half_size), grad_quads, precision=precise
    )
    direction = jnp.einsum(
        "brjk,bkjm->brjm", direction, split_halves(right_half, half_size), precision=precise
    )
    flat = (count, row_count, width)
    return left_add.reshape(flat), right_add.reshape(flat), direction.reshape(flat), block_rows


def on_device(
    patches,
    image_ids,
    keep,
    labels,
    owner,
    step,
    enc_weights,
    stats_left,
    stats_right,
    root_left,
    root_right,
    head_weights,
    head_m,
    head_v,
    vectors,
    vec_m,
    vec_v,
):
    dp_count = lax.axis_size("dp")
    cls_count = lax.axis_size("cls")
    dp_index = lax.axis_index("dp")
    cls_index = lax.axis_index("cls")
    block_count, row_count, feature_dim = enc_weights.shape
    up_count = (block_count - 5) // 2
    half_size = feature_dim // 2
    part_rows = row_count // cls_count
    half_dp = dp_count // 2
    half_group = half_dp * cls_count
    half_groups = [
        list(range(half_group)),
        list(range(half_group, 2 * half_group)),
    ]

    def my_part(values):
        return lax.dynamic_slice_in_dim(values, cls_index * part_rows, part_rows, 1)

    on_torus = dp_count == 8 and cls_count == 4
    if on_torus:
        vec_block = jnp.pad(vectors, ((0, -vectors.shape[0] % 8), (0, -row_count % 128)))
        own_low = enc_weights.astype(jnp.bfloat16)
        blocks, vec_blocks = gather_weights(own_low[:5], vec_block)
        right_part, vec_blocks = lax.optimization_barrier((my_part(root_right), vec_blocks))
        vec_low = jnp.transpose(vec_blocks[:, : vectors.shape[0], :row_count], (1, 0, 2))
        vec_all = lax.reduce_precision(vec_low.reshape(vectors.shape[0], feature_dim), 8, 7)
    else:
        right_part = my_part(root_right)
        all_blocks = lax.all_gather(
            my_part(enc_weights.astype(jnp.bfloat16)), ("dp", "cls"), axis=1, tiled=True
        )
        blocks = all_blocks[:5]
        vec_low = lax.all_gather(vectors.astype(jnp.bfloat16), "dp", axis=1, tiled=True)
        vec_all = vec_low.astype(jnp.float32)
    head_low = lax.all_gather(head_weights.astype(jnp.bfloat16), "dp", axis=0, tiled=True)
    final_gain = vec_all[9 + up_count]
    final_shift = vec_all[10 + up_count]
    pack_ids, pack_keep = image_ids[0], keep[0]
    key_codes = jnp.where(pack_keep == 1, pack_ids, -1)

    def attend(qkv_rows):
        if on_torus:
            return attention_forward_gathering(qkv_rows, pack_ids, key_codes, own_low[5:])
        return attention_forward(qkv_rows, pack_ids, key_codes), all_blocks[5:]

    output, mlp_blocks, saved = layer_forward(blocks, vec_all, patches, attend)
    if on_torus:
        right_codes = lax.all_gather(
            encode_roots(right_part), ("dp", "cls"), axis=0, axis_index_groups=half_groups
        )
    else:
        right_half = lax.all_gather(
            right_part, ("dp", "cls"), axis=1, tiled=True, axis_index_groups=half_groups
        )
    pooled = pool_rows(output, final_gain, final_shift, pack_ids, pack_keep)
    class_dev = head_low.shape[1]
    image_total = labels.shape[0] * dp_count
    if on_torus:
        grad_pooled, own_rows, loss_rows = classify(
            lax.reduce_precision(pooled, 8, 7), labels, head_low, cls_count, image_total
        )
        loss_part = loss_rows[0, 0]
    else:
        group = lax.all_gather(pooled.astype(jnp.bfloat16), "cls", axis=0, tiled=True)
        logits = jnp.dot(group, head_low, preferred_element_type=jnp.float32)
        class_ids = cls_index * class_dev + jnp.arange(class_dev)
        valid = class_ids[None, :] < LABELS_REAL
        target = jnp.any(labels[:, :, None] == class_ids[None, None, :], 1).astype(jnp.float32)
        terms = jax.nn.softplus(logits) - target * logits
        loss_part = jnp.sum(jnp.where(valid, terms, 0.0)) / image_total
        grad_logits = jnp.where(valid, jax.nn.sigmoid(logits) - target, 0.0) / image_total
        grad_logits = grad_logits.astype(jnp.bfloat16)
        group_grad = jnp.einsum(
            "gc,dc->gd", grad_logits, head_low, preferred_element_type=jnp.float32
        )
        grad_pooled = lax.psum_scatter(group_grad, "cls", scatter_dimension=0, tiled=True)
        own_rows = jnp.concatenate([group, grad_logits], 1)

    def pool_local(rows_in, gain, shift):
        return pool_rows(rows_in, gain, shift, pack_ids, pack_keep)

    pool_back = jax.vjp(pool_local, output, final_gain, final_shift)[1]
    grad_output, grad_gain, grad_shift = pool_back(grad_pooled)
    lefts, rights, mlp_grads, grad_vectors, (own_rows, roots) = layer_backward(
        blocks,
        mlp_blocks,
        vec_all,
        patches,
        saved,
        pack_ids,
        key_codes,
        grad_output,
        grad_gain,
        grad_shift,
        (own_rows, right_codes if on_torus else right_half),
    )
    head_rows = lax.all_gather(own_rows, "dp", axis=0, tiled=True)
    pooled_all = head_rows[:, :feature_dim]
    grad_logits_all = head_rows[:, feature_dim : feature_dim + class_dev]
    pooled_mine = lax.dynamic_slice_in_dim(pooled_all, dp_index * row_count, row_count, 1)
    head_grad = jnp.einsum(
        "gr,gc->rc", pooled_mine, grad_logits_all, preferred_element_type=jnp.float32
    )

    head_squares = jnp.sum(head_grad * head_grad)
    if on_torus:
        padded = jnp.pad(grad_vectors, ((0, -grad_vectors.shape[0] % 8), (0, 0)))
        tail = jnp.pad(jnp.stack([head_squares, loss_part])[:, None], ((0, 6), (0, 127)))
        block_rows, left_add, right_add, direction, wide_scale, facts, vector_sum = (
            reduce_gradients(
                mlp_grads, lefts, rights, padded, tail, root_left, roots,
                dp_count, cls_count,
            )
        )
        vector_sum = vector_sum[: grad_vectors.shape[0]]
        loss, grad_norm, factor = facts[0, 0], facts[1, 0], facts[2, 0]
    else:
        over_rows = "td,te->de"
        first_grads = [
            jnp.einsum(over_rows, left, right, preferred_element_type=jnp.float32)[None]
            for left, right in (
                (lefts[0], rights[0]),
                (lefts[1], rights[1][0]),
                (lefts[1], rights[1][1]),
                (lefts[1], rights[1][2]),
                (lefts[2], rights[2]),
            )
        ]
        grad_half = reduced_half(jnp.concatenate(first_grads + list(mlp_grads), 0), half_groups)
        vector_sum = lax.psum(grad_vectors, ("dp", "cls"))
        left_add, right_add, direction, block_rows = preconditioned_rows(
            grad_half, root_left, roots, (dp_index % half_dp) * row_count
        )
        squares = jnp.sum(split_halves(direction * direction, half_size), (1, 3))
        in_top = (dp_index < half_dp).astype(jnp.float32)
        once = (cls_index == 0).astype(jnp.float32)
        all_squares = head_squares + once * jnp.sum(block_rows * block_rows)
        packed = jnp.concatenate(
            [
                (once * in_top * squares).reshape(-1),
                (once * (1.0 - in_top) * squares).reshape(-1),
                jnp.stack([all_squares, loss_part]),
            ]
        )
        packed = lax.psum(packed, ("dp", "cls"))
        loss = packed[4 * block_count + 1]
        all_squares = packed[4 * block_count]
        sums = packed[: 4 * block_count].reshape(2, block_count, 2)
        block_squares = jnp.where(dp_index < half_dp, sums[0], sums[1])
        grad_norm = jnp.sqrt(all_squares + jnp.sum(vector_sum * vector_sum))
        factor = CLIP_NORM / jnp.maximum(grad_norm, CLIP_NORM)
        mean_squares = block_squares / (half_size * half_size) * factor * factor
        scale = SHAMPOO_RATE * factor * lax.rsqrt(mean_squares + ROOT_EPS)
        wide_scale = jnp.repeat(scale, half_size, axis=1)[:, None, :]
    vector_rows = lax.dynamic_slice_in_dim(vector_sum, dp_index * row_count, row_count, 1)
    new_blocks = enc_weights - direction * wide_scale
    square_factor = 0.5 * factor * factor
    new_left = 0.5 * stats_left + square_factor * left_add
    new_right = 0.5 * stats_right + square_factor * right_add
    count = step.astype(jnp.float32)
    new_vec, new_vec_m, new_vec_v = adam_step(vectors, vector_rows * factor, vec_m, vec_v, count)
    new_head, new_head_m, new_head_v = adam_step(
        head_weights, head_grad * factor, head_m, head_v, count
    )
    return (
        loss,
        grad_norm,
        new_blocks,
        block_rows * factor,
        new_left,
        new_right,
        new_vec,
        new_vec_m,
        new_vec_v,
        new_head,
        new_head_m,
        new_head_v,
    )


def solution(mesh):
    return jax.shard_map(
        on_device,
        mesh=mesh,
        in_specs=(
            P(("dp", "cls"), None),
            P(("dp", "cls"), None),
            P(("dp", "cls"), None),
            P("dp", None),
            P(),
            P(),
            P(None, "dp", None),
            P(None, "dp", None),
            P(None, "dp", None),
            P(None, "dp", None),
            P(None, "dp", None),
            P("dp", "cls"),
            P("dp", "cls"),
            P("dp", "cls"),
            P(None, "dp"),
            P(None, "dp"),
            P(None, "dp"),
        ),
        out_specs=(
            P(),
            P(),
            P(None, "dp", None),
            P(None, "dp", None),
            P(None, "dp", None),
            P(None, "dp", None),
            P(None, "dp"),
            P(None, "dp"),
            P(None, "dp"),
            P("dp", "cls"),
            P("dp", "cls"),
            P("dp", "cls"),
        ),
        check_vma=False,
    )
```
